32 devices in a mesh: tp: 2 (over y), dp: 4 (over z), rep: 4 (over x, core).
Axes of the slice: x: 2, y: 2, z: 4, core: 2. Of those that a mesh axis runs over, the one named last changes fastest.
Arguments:
- layer_input: bfloat16 [16, 1024, 768], P(('dp', 'rep'), 'tp'), may hold values from -6 to 6
- history: bfloat16 [4, 16, 1024, 768], P(None, ('dp', 'rep'), 'tp'), may hold values from -6 to 6
- cotangent: bfloat16 [16, 1024, 768], P(('dp', 'rep'), 'tp'), may hold values from -6 to 6
- lengths: int32 [16, 3], P(('dp', 'rep')), may hold values from 1 to 512, 1024 in all within a row
- dwa_weights: float32 [5], replicated, may hold values from 0.2 to 1
- gain_one: float32 [768], replicated, may hold values from 0.1 to 1.9
- bias_one: float32 [768], replicated, may hold values from -3 to 3
- w_qkv: bfloat16 [3, 768, 768], P(None, None, 'tp'), may hold values from -0.21875 to 0.21875
- w_out: bfloat16 [768, 768], P('tp'), may hold values from -1.75 to 1.75
- gain_two: float32 [768], replicated, may hold values from 0.1 to 1.9
- bias_two: float32 [768], replicated, may hold values from -3 to 3
- w_up: bfloat16 [768, 3072], P(None, 'tp'), may hold values from -0.21875 to 0.21875
- w_down: bfloat16 [3072, 768], P('tp'), may hold values from -0.109375 to 0.109375
Outputs:
- output: bfloat16 [16, 1024, 768], P(('dp', 'rep'), 'tp')
- grad_input: bfloat16 [16, 1024, 768], P(('dp', 'rep'), 'tp')
- grad_history: bfloat16 [4, 16, 1024, 768], P(None, ('dp', 'rep'), 'tp')
- grad_dwa: float32 [5], replicated
- grad_gain_one: float32 [768], replicated
- grad_bias_one: float32 [768], replicated
- grad_w_qkv: float32 [3, 768, 768], P(None, 'dp', 'tp')
- grad_w_out: float32 [768, 768], P('tp', 'dp')
- grad_gain_two: float32 [768], replicated
- grad_bias_two: float32 [768], replicated
- grad_w_up: float32 [768, 3072], P('dp', 'tp')
- grad_w_down: float32 [3072, 768], P('tp', 'dp')
The draws below stay inside these ranges and needn't reach their ends.
Inputs may be any that keep to these rules, and one draw needn't show every extreme that they name: Row g lists in order the lengths of the 3 sequences packed into group g; they sum to 1024 and the largest of each row is 512.
All inputs are finite; a program needn't handle non-finite values.
Results may differ from the reference program's by a relative error of at most 0.02.
Values may be sent and summed in bfloat16 or wider, within the bound.
No kernel may reach another device: no remote copies, remote signals or barrier semaphores. Data moves between devices by JAX's collectives and lax.ppermute only.
A program may use at most 128 MiB of HBM per device.

```python
import math
import jax
import jax.numpy as jnp
import numpy as np
from jax import lax

D = 768
HEADS = 12
HEAD_DIM = 64
FF = 3072
TOK_DEV = 1024
NSEQ = 3
HIST = 4
SEQ_LEN = 512
GROUPS = 16


def steps_of(stream_key, extent, pieces, least, largest):
    factor_of = 1.0
    for dim, parts in pieces:
        heights = jax.random.uniform(jax.random.fold_in(jax.random.fold_in(stream_key, 6), dim), (parts,), jnp.float32, least / len(pieces), largest / len(pieces))
        factor_of = factor_of * jnp.repeat(jnp.exp(heights), extent[dim] // parts).reshape((-1,) + (1,) * (len(extent) - 1 - dim))
    return factor_of


def profile(amount, total, most, lean):
    weights = [(1 << 20) // math.isqrt(rank ** lean) + 1 for rank in range(2, amount + 1)]
    surplus, given = total - most - (amount - 1), [1] * (amount - 1)
    while surplus > 0:
        movable = [i for i in range(amount - 1) if given[i] < most]
        pool, remaining = sum([weights[i] for i in movable]), surplus
        for i in movable:
            more = min(most - given[i], max(1, remaining * weights[i] // pool), surplus)
            given[i] = given[i] + more
            surplus = surplus - more
    return np.array([most] + given)


def uneven(stream_key, amount, total, limit, lean):
    if amount == 2:
        one = jax.random.randint(stream_key, (), max(1, total - limit), min(limit, total - 1) + 1)
        return jnp.stack([one, total - one])
    tallies = jnp.asarray(profile(amount, total, limit, lean), jnp.int32)
    pairs = (amount - 1) // 2
    donor, sink = tallies[1:1 + 2 * pairs:2], tallies[2:2 + 2 * pairs:2]
    margin = jnp.minimum(donor - 1, limit - sink)
    passed = jax.random.randint(jax.random.fold_in(stream_key, 1), (pairs,), 0, 1 << 20) % (margin + 1)
    tallies = tallies.at[1:1 + 2 * pairs:2].set(donor - passed).at[2:2 + 2 * pairs:2].set(sink + passed)
    return tallies[jax.random.permutation(jax.random.fold_in(stream_key, 2), amount)]


def noise(rng, extent, deviation, bound, shards=(), held_as=jnp.bfloat16):
    drawn = jax.random.normal(rng, extent, jnp.float32) * deviation
    if len(shards) > 0:
        drawn = steps_of(rng, extent, shards, -0.22, 0.18) * drawn
    return jnp.clip(drawn, min=-bound, max=bound).astype(held_as)


def setup_inputs(seed: int = 0) -> dict:
    seeds = jax.random.split(jax.random.key(seed), 14)
    layer_input = noise(seeds[0], (GROUPS, TOK_DEV, D), 1.0, 6.0, ((0, 16), (1, 2)))
    history = noise(seeds[1], (HIST, GROUPS, TOK_DEV, D), 1.0, 6.0, ((1, 16), (2, 2)))
    cotangent = noise(seeds[2], (GROUPS, TOK_DEV, D), 1.0, 6.0, ((0, 16), (1, 2)))
    lengths = jax.vmap(lambda own: uneven(own, NSEQ, TOK_DEV, SEQ_LEN, 1))(jax.random.split(seeds[3], GROUPS)).reshape((GROUPS, NSEQ)).astype(jnp.int32)
    dwa_weights = jnp.clip(jax.random.uniform(seeds[4], (HIST + 1,), jnp.float32, 0.2, 1.0), 0.2, 1.0)
    gain_one = jnp.clip(1.0 + 0.18 * jax.random.normal(seeds[5], (D,), jnp.float32), 0.1, 1.9)
    bias_one = noise(seeds[6], (D,), 0.3, 3.0, (), jnp.float32)
    w_qkv = noise(seeds[7], (3, D, D), D ** -0.5, 0.21875, ((2, 2),))
    w_out = noise(seeds[8], (D, D), (D // 64) ** -0.5, 1.75, ((0, 2),))
    gain_two = jnp.clip(1.0 + 0.18 * jax.random.normal(seeds[9], (D,), jnp.float32), 0.1, 1.9)
    bias_two = noise(seeds[10], (D,), 0.3, 3.0, (), jnp.float32)
    w_up = noise(seeds[11], (D, FF), D ** -0.5, 0.21875, ((1, 2),))
    w_down = noise(seeds[12], (FF, D), FF ** -0.5, 0.109375, ((0, 2),))
    return {"layer_input": layer_input, "history": history, "cotangent": cotangent, "lengths": lengths, "dwa_weights": dwa_weights, "gain_one": gain_one, "bias_one": bias_one, "w_qkv": w_qkv, "w_out": w_out, "gain_two": gain_two, "bias_two": bias_two, "w_up": w_up, "w_down": w_down}


@jax.custom_vjp
def low(v):
    return lax.optimization_barrier(v.astype(jnp.bfloat16)).astype(jnp.float32)

@jax.custom_vjp
def low_back(v):
    return v

def low_keep(v):
    return (low(v), None)

def low_pass(kept, grad):
    return (grad,)

def back_keep(v):
    return (v, None)

def back_low(kept, grad):
    return (low(grad),)
low.defvjp(low_keep, low_pass)
low_back.defvjp(back_keep, back_low)
NEG_FILL = -1e+30
NORM_EPS = 1e-05
HIGH = lax.Precision.HIGHEST

def layer_norm(field, gain, shift):
    row_mean = lax.optimization_barrier(jnp.mean(field, axis=-1, keepdims=True))
    centered = field - row_mean
    variance = lax.optimization_barrier(jnp.mean(centered * centered, axis=-1, keepdims=True))
    return centered * lax.rsqrt(variance + NORM_EPS) * gain + shift

def positions(seq_lengths, token_count):
    seq_ends = jnp.cumsum(seq_lengths).astype(jnp.int32)
    seq_starts = seq_ends - seq_lengths
    token_index = jnp.arange(token_count, dtype=jnp.int32)
    seq_owner = lax.optimization_barrier(jnp.sum((token_index[:, None] >= seq_ends[None, :]).astype(jnp.int32), axis=1))
    picked = (seq_owner[:, None] == jnp.arange(seq_lengths.shape[0], dtype=jnp.int32)[None, :]).astype(jnp.int32)
    seq_begin = lax.optimization_barrier(jnp.sum(picked * seq_starts[None, :], axis=1))
    return (seq_owner, token_index - seq_begin)

def rotary(token_place, head_size):
    half_dim = head_size // 2
    frequency = jnp.exp(jnp.arange(half_dim, dtype=jnp.float32) * (-math.log(10000.0) / half_dim))
    angles = token_place.astype(jnp.float32)[:, None] * frequency[None, :]
    return (jnp.cos(angles), jnp.sin(angles))

def rotate(field, cos_table, sin_table):
    half_dim = field.shape[-1] // 2
    first_half = field[..., :half_dim]
    second_half = field[..., half_dim:]
    cos_rows = cos_table[:, None, :]
    sin_rows = sin_table[:, None, :]
    return jnp.concatenate([first_half * cos_rows - second_half * sin_rows, second_half * cos_rows + first_half * sin_rows], axis=-1)

def group_forward(seq_owner, token_place, layer_rows, hist_rows, params):
    dwa_weights, gain_one, bias_one, w_qkv, w_out, gain_two, bias_two, w_up, w_down = params
    token_count = layer_rows.shape[0]
    norm_one = low(layer_norm(layer_rows, gain_one, bias_one))
    qkv = low_back(jnp.einsum('td,cde->cte', norm_one, w_qkv, precision=HIGH))
    cos_table, sin_table = rotary(token_place, HEAD_DIM)
    shaped = qkv.reshape(3, token_count, HEADS, HEAD_DIM)
    queries = low(rotate(shaped[0], cos_table, sin_table))
    keys_rot = low(rotate(shaped[1], cos_table, sin_table))
    values = low(shaped[2])
    block_rows = min(512, token_count)
    key_index = jnp.arange(token_count, dtype=jnp.int32)
    score_scale = HEAD_DIM ** (-0.5)

    @jax.checkpoint
    def attend(row_start):
        query_block = lax.dynamic_slice_in_dim(queries, row_start, block_rows, 0)
        rows_here = row_start + jnp.arange(block_rows, dtype=jnp.int32)
        owner_rows = lax.dynamic_slice_in_dim(seq_owner, row_start, block_rows, 0)
        allowed = (owner_rows[:, None] == seq_owner[None, :]) & (key_index[None, :] <= rows_here[:, None])
        scores = low_back(score_scale * jnp.einsum('qhe,khe->hqk', query_block, keys_rot, precision=HIGH))
        scores = jnp.where(allowed[None], scores, NEG_FILL)
        row_max = lax.optimization_barrier(jnp.max(scores, axis=-1, keepdims=True))
        exponent = jnp.exp(scores - row_max)
        probabilities = low(exponent / lax.optimization_barrier(jnp.sum(exponent, axis=-1, keepdims=True)))
        return jnp.einsum('hqk,khe->qhe', probabilities, values, precision=HIGH)
    block_starts = jnp.arange(token_count // block_rows, dtype=jnp.int32) * block_rows
    mixed = lax.map(attend, block_starts).reshape(token_count, HEADS * HEAD_DIM)
    mixed = low(low_back(mixed))
    attn = low_back(jnp.dot(mixed, w_out, precision=HIGH))
    resid = layer_rows + attn
    norm_two = low(layer_norm(resid, gain_two, bias_two))
    up_rows = low_back(jnp.dot(norm_two, w_up, precision=HIGH))
    act = low(jax.nn.gelu(up_rows, approximate=True))
    down = low_back(jnp.dot(act, w_down, precision=HIGH))
    block_out = resid + down
    hist_count = hist_rows.shape[0]
    return lax.optimization_barrier(jnp.sum(dwa_weights[:hist_count, None, None] * hist_rows, axis=0)) + dwa_weights[hist_count] * block_out

def reference(layer_input, history, cotangent, lengths, dwa_weights, gain_one, bias_one, w_qkv, w_out, gain_two, bias_two, w_up, w_down):
    params = (dwa_weights, gain_one, bias_one, w_qkv.astype(jnp.float32), w_out.astype(jnp.float32), gain_two, bias_two, w_up.astype(jnp.float32), w_down.astype(jnp.float32))

    def one_group(running, item):
        layer_rows, hist_rows, cot_rows, seq_lengths = item
        seq_owner, token_place = positions(seq_lengths, layer_rows.shape[0])

        def forward(rows_in, hist_in, params_in):
            return group_forward(seq_owner, token_place, rows_in, hist_in, params_in)
        result, pull = jax.vjp(forward, layer_rows.astype(jnp.float32), hist_rows.astype(jnp.float32), params)
        grad_rows, grad_hist, grad_params = pull(cot_rows.astype(jnp.float32))
        running = jax.tree.map(jnp.add, running, grad_params)
        return (running, (result.astype(jnp.bfloat16), grad_rows.astype(jnp.bfloat16), grad_hist.astype(jnp.bfloat16)))
    zero_grads = jax.tree.map(jnp.zeros_like, params)
    summed, (outputs, grad_input, grad_hist) = lax.scan(one_group, zero_grads, (layer_input, jnp.moveaxis(history, 1, 0), cotangent, lengths))
    grad_history = jnp.moveaxis(grad_hist, 0, 1)
    return (outputs, grad_input, grad_history, summed[0], summed[1], summed[2], summed[3], summed[4], summed[5], summed[6], summed[7], summed[8])
```

```python
from functools import partial
import math

import jax
import jax.numpy as jnp
from jax import lax
from jax.sharding import PartitionSpec as P

HEAD_DIM = 64


NEG_FILL = -1e30
NORM_EPS = 1e-05


def layer_norm(field, gain, shift):
    row_mean = jnp.mean(field, axis=-1, keepdims=True)
    centered = field - row_mean
    variance = jnp.mean(centered * centered, axis=-1, keepdims=True)
    return centered * lax.rsqrt(variance + NORM_EPS) * gain + shift


def positions(seq_lengths, token_count):
    seq_ends = jnp.cumsum(seq_lengths)
    seq_starts = seq_ends - seq_lengths
    token_index = jnp.arange(token_count, dtype=jnp.int32)
    seq_owner = jnp.sum((token_index[:, None] >= seq_ends[None, :]).astype(jnp.int32), axis=1)
    picked = (
        seq_owner[:, None] == jnp.arange(seq_lengths.shape[0], dtype=jnp.int32)[None, :]
    ).astype(jnp.int32)
    seq_begin = jnp.sum(picked * seq_starts[None, :], axis=1)
    return (seq_owner, token_index - seq_begin)


def rotary(token_place, head_size):
    half_dim = head_size // 2
    frequency = jnp.exp(jnp.arange(half_dim, dtype=jnp.float32) * (-math.log(10000.0) / half_dim))
    angles = token_place.astype(jnp.float32)[:, None] * frequency[None, :]
    return (jnp.cos(angles), jnp.sin(angles))


def rotate(field, cos_table, sin_table):
    half_dim = field.shape[-1] // 2
    first_half = field[..., :half_dim]
    second_half = field[..., half_dim:]
    cos_rows = cos_table[:, None, :]
    sin_rows = sin_table[:, None, :]
    return jnp.concatenate(
        [
            first_half * cos_rows - second_half * sin_rows,
            second_half * cos_rows + first_half * sin_rows,
        ],
        axis=-1,
    )


def rotate_back(field, cos_table, sin_table):
    half_dim = field.shape[-1] // 2
    first_half = field[..., :half_dim]
    second_half = field[..., half_dim:]
    cos_rows = cos_table[:, None, :]
    sin_rows = sin_table[:, None, :]
    return jnp.concatenate(
        [
            first_half * cos_rows + second_half * sin_rows,
            second_half * cos_rows - first_half * sin_rows,
        ],
        axis=-1,
    )


AXES = ("tp", "dp", "rep")


def pairs_of(move):
    tps, dps, reps = (lax.axis_size(name) for name in AXES)
    return [
        ((t * dps + d) * reps + r, (a * dps + b) * reps + e)
        for t in range(tps)
        for d in range(dps)
        for r in range(reps)
        for a, b, e in [move(t, d, r)]
    ]


def swap_diagonal(field):
    return lax.ppermute(field, AXES, pairs_of(lambda t, d, r: (r % 2, d, r - r % 2 + t)))


def swap_near(field):
    return lax.ppermute(field, "rep", [(r, r ^ 1) for r in range(lax.axis_size("rep"))])


def swap_far(field):
    return lax.ppermute(field, "rep", [(r, r ^ 2) for r in range(lax.axis_size("rep"))])


def ordered(own, other, first):
    return jnp.where(
        first, jnp.concatenate([own, other], axis=0), jnp.concatenate([other, own], axis=0)
    )


def reduce_pieces(pieces, near, far):
    dps = lax.axis_size("dp")
    mine = lax.dynamic_slice_in_dim(pieces, 2 * far, 2, 0)
    theirs = lax.dynamic_slice_in_dim(pieces, 2 - 2 * far, 2, 0)
    pair = mine.astype(jnp.float32) + swap_far(theirs).astype(jnp.float32)
    pair = swap_diagonal(pair.astype(jnp.bfloat16))
    mine = lax.dynamic_index_in_dim(pair, near, 0, keepdims=False)
    theirs = lax.dynamic_index_in_dim(pair, 1 - near, 0, keepdims=False)
    one = mine.astype(jnp.float32) + swap_near(theirs).astype(jnp.float32)
    rows = one.shape[0] // dps
    if dps <= 8:
        place = lax.axis_index("dp")
        total = lax.dynamic_slice_in_dim(one, place * rows, rows, 0)
        low = one.astype(jnp.bfloat16)
        for step in range(1, dps):
            target = lax.rem(place + step, dps)
            sent = lax.dynamic_slice_in_dim(low, target * rows, rows, 0)
            total = total + lax.ppermute(
                sent, "dp", [(d, (d + step) % dps) for d in range(dps)]
            ).astype(jnp.float32)
    else:
        total = lax.psum_scatter(one.astype(jnp.bfloat16), "dp", scatter_dimension=0, tiled=True)
    total = total.astype(jnp.bfloat16)[None]
    total = ordered(total, swap_near(total), near == 0)
    total = ordered(total, swap_far(total), far == 0)
    return total.astype(jnp.float32)


def local(
    layer_input,
    history,
    cotangent,
    lengths,
    dwa_weights,
    gain_one,
    bias_one,
    w_qkv,
    w_out,
    gain_two,
    bias_two,
    w_up,
    w_down,
):
    rows = layer_input.shape[1]
    whole = rows * lax.axis_size("tp")
    heads_here = w_qkv.shape[2] // HEAD_DIM
    hist_count = history.shape[0]
    part, slot = lax.axis_index("tp"), lax.axis_index("rep")
    near, far = slot % 2, slot // 2
    input_half = swap_diagonal(layer_input[0])
    w_qkv = swap_diagonal(w_qkv)
    cot_half = swap_diagonal(cotangent[0])
    w_out = swap_diagonal(w_out)
    w_up = swap_diagonal(w_up)
    w_down = swap_diagonal(w_down)
    own_lengths = jnp.where(near == part, lengths, swap_near(lengths))
    seq_owner, token_place = positions(own_lengths[0], whole)
    cos_table, sin_table = rotary(token_place, HEAD_DIM)
    block_rows = min(512, whole)
    block_starts = jnp.arange(whole // block_rows, dtype=jnp.int32) * block_rows
    key_index = jnp.arange(whole, dtype=jnp.int32)
    score_scale = HEAD_DIM ** (-0.5)
    layer_rows = ordered(input_half, swap_near(input_half), near == 0).astype(jnp.float32)
    norm_one = layer_norm(layer_rows, gain_one, bias_one).astype(jnp.bfloat16)
    qkv = jnp.einsum("td,cde->cte", norm_one, w_qkv, preferred_element_type=jnp.float32)
    shaped = qkv.reshape(3, whole, heads_here, HEAD_DIM)
    queries = rotate(shaped[0], cos_table, sin_table).astype(jnp.bfloat16)
    keys_rot = rotate(shaped[1], cos_table, sin_table).astype(jnp.bfloat16)
    values = shaped[2].astype(jnp.bfloat16)

    def scores_for(row_start):
        query_block = lax.dynamic_slice_in_dim(queries, row_start, block_rows, 0)
        rows_here = row_start + jnp.arange(block_rows, dtype=jnp.int32)
        owner_rows = lax.dynamic_slice_in_dim(seq_owner, row_start, block_rows, 0)
        allowed = (owner_rows[:, None] == seq_owner[None, :]) & (
            key_index[None, :] <= rows_here[:, None]
        )
        raw_scores = score_scale * jnp.einsum(
            "qhe,khe->hqk", query_block, keys_rot, preferred_element_type=jnp.float32
        )
        return (query_block, jnp.where(allowed[None], raw_scores, NEG_FILL))

    def attend(row_start):
        query_block, scores = scores_for(row_start)
        row_max = jnp.max(scores, axis=-1, keepdims=True)
        exponent = jnp.exp(scores - row_max)
        row_sum = jnp.sum(exponent, axis=-1, keepdims=True)
        probabilities = (exponent / row_sum).astype(jnp.bfloat16)
        mixed_block = jnp.einsum(
            "hqk,khe->qhe", probabilities, values, preferred_element_type=jnp.float32
        )
        return (
            mixed_block.reshape(block_rows, -1).astype(jnp.bfloat16),
            (row_max + jnp.log(row_sum))[..., 0],
        )

    mixed_blocks, log_sums = lax.map(attend, block_starts)
    mixed = mixed_blocks.reshape(whole, -1)
    attn = jnp.dot(mixed, w_out, preferred_element_type=jnp.float32).astype(jnp.bfloat16)
    attn = attn.astype(jnp.float32) + swap_near(attn).astype(jnp.float32)
    resid = layer_rows + attn
    norm_two = layer_norm(resid, gain_two, bias_two).astype(jnp.bfloat16)
    up_rows = jnp.dot(norm_two, w_up, preferred_element_type=jnp.float32)
    act = jax.nn.gelu(up_rows, approximate=True).astype(jnp.bfloat16)
    cot_rows = ordered(cot_half, swap_near(cot_half), near == 0)
    grad_block = dwa_weights[hist_count] * cot_rows.astype(jnp.float32)
    grad_down = grad_block.astype(jnp.bfloat16)
    grad_act = jnp.einsum("td,fd->tf", grad_down, w_down, preferred_element_type=jnp.float32)
    unused_gelu, gelu_pull = jax.vjp(partial(jax.nn.gelu, approximate=True), up_rows)
    grad_up = gelu_pull(grad_act)[0].astype(jnp.bfloat16)
    grad_norm_two = jnp.einsum("tf,df->td", grad_up, w_up, preferred_element_type=jnp.float32)
    grad_norm_two = grad_norm_two.astype(jnp.bfloat16)
    grad_norm_two = grad_norm_two.astype(jnp.float32) + swap_near(grad_norm_two).astype(jnp.float32)

    quarter = w_up.shape[1] // 4
    grad_w_down = jnp.einsum("td,tf->df", grad_down, act, preferred_element_type=jnp.float32)
    grad_w_down = grad_w_down.astype(jnp.bfloat16).reshape(-1, 4, quarter).transpose(1, 0, 2)
    grad_w_up = jnp.einsum("td,tf->df", norm_two, grad_up, preferred_element_type=jnp.float32)
    grad_w_up = grad_w_up.astype(jnp.bfloat16).reshape(-1, 4, quarter).transpose(1, 0, 2)
    grad_w_down = reduce_pieces(grad_w_down, near, far)
    grad_w_up = reduce_pieces(grad_w_up, near, far)

    down = jnp.dot(act, w_down, preferred_element_type=jnp.float32)
    down_mine = lax.dynamic_slice_in_dim(down, near * rows, rows, 0)
    down_theirs = lax.dynamic_slice_in_dim(down, (1 - near) * rows, rows, 0).astype(jnp.bfloat16)
    block_half = (
        lax.dynamic_slice_in_dim(resid, near * rows, rows, 0)
        + down_mine
        + swap_near(down_theirs).astype(jnp.float32)
    )
    block_out = swap_diagonal(block_half.astype(jnp.bfloat16)).astype(jnp.float32)
    hist_rows = history[:, 0].astype(jnp.float32)
    output = (
        jnp.sum(dwa_weights[:hist_count, None, None] * hist_rows, axis=0)
        + dwa_weights[hist_count] * block_out
    )
    grad_out = cotangent[0].astype(jnp.float32)
    grad_history = (dwa_weights[:hist_count, None, None] * grad_out[None]).astype(jnp.bfloat16)[
        :, None
    ]
    dwa_terms = jnp.concatenate(
        [jnp.sum(hist_rows * grad_out[None], axis=(1, 2)), jnp.sum(block_out * grad_out)[None]]
    )

    def layer_norm_back(field, gain, shift, grad, row_start):
        centered = field - jnp.mean(field, axis=-1, keepdims=True)
        scale = lax.rsqrt(jnp.mean(centered * centered, axis=-1, keepdims=True) + NORM_EPS)
        unit = centered * scale
        inner = grad * gain
        back = scale * (
            inner
            - jnp.mean(inner, axis=-1, keepdims=True)
            - unit * jnp.mean(inner * unit, axis=-1, keepdims=True)
        )
        half_grad = lax.dynamic_slice_in_dim(grad, row_start, rows, 0)
        half_unit = lax.dynamic_slice_in_dim(unit, row_start, rows, 0)
        return back, jnp.sum(half_grad * half_unit, axis=0), jnp.sum(half_grad, axis=0)

    grad_resid_norm, grad_gain_two, grad_bias_two = layer_norm_back(
        resid, gain_two, bias_two, grad_norm_two, near * rows
    )
    grad_resid = grad_block + grad_resid_norm
    grad_attn = grad_resid.astype(jnp.bfloat16)
    grad_w_out = jnp.einsum("td,te->de", grad_attn, mixed, preferred_element_type=jnp.float32)
    grad_mixed = jnp.einsum("td,ed->te", grad_attn, w_out, preferred_element_type=jnp.float32).astype(
        jnp.bfloat16
    )
    grad_mixed = grad_mixed.reshape(whole, heads_here, HEAD_DIM)

    def attend_back(carry, item):
        grad_keys, grad_values = carry
        row_start, log_sum = item
        query_block, scores = scores_for(row_start)
        probabilities = jnp.exp(scores - log_sum[..., None])
        probs_low = probabilities.astype(jnp.bfloat16)
        grad_block_rows = lax.dynamic_slice_in_dim(grad_mixed, row_start, block_rows, 0)
        grad_values = grad_values + jnp.einsum(
            "hqk,qhe->khe", probs_low, grad_block_rows, preferred_element_type=jnp.float32
        )
        grad_probs = jnp.einsum(
            "qhe,khe->hqk", grad_block_rows, values, preferred_element_type=jnp.float32
        )
        row_dot = jnp.sum(probabilities * grad_probs, axis=-1, keepdims=True)
        grad_scores = (probabilities * (grad_probs - row_dot)).astype(jnp.bfloat16)
        grad_queries = score_scale * jnp.einsum(
            "hqk,khe->qhe", grad_scores, keys_rot, preferred_element_type=jnp.float32
        )
        grad_keys = grad_keys + score_scale * jnp.einsum(
            "hqk,qhe->khe", grad_scores, query_block, preferred_element_type=jnp.float32
        )
        return ((grad_keys, grad_values), grad_queries)

    zero_heads = jnp.zeros((whole, heads_here, HEAD_DIM), jnp.float32)
    (grad_keys, grad_values), grad_query_blocks = lax.scan(
        attend_back, (zero_heads, zero_heads), (block_starts, log_sums)
    )
    grad_queries = grad_query_blocks.reshape(whole, heads_here, HEAD_DIM)
    grad_qkv = jnp.stack(
        [
            rotate_back(grad_queries, cos_table, sin_table),
            rotate_back(grad_keys, cos_table, sin_table),
            grad_values,
        ]
    )
    grad_qkv = grad_qkv.reshape(3, whole, heads_here * HEAD_DIM).astype(jnp.bfloat16)
    grad_w_qkv = jnp.einsum("td,cte->cde", norm_one, grad_qkv, preferred_element_type=jnp.float32)
    grad_w_attn = reduce_pieces(
        jnp.concatenate([grad_w_qkv, grad_w_out[None]], axis=0).astype(jnp.bfloat16), near, far
    )
    grad_norm_one = jnp.einsum("cte,cde->td", grad_qkv, w_qkv, preferred_element_type=jnp.float32)
    one_mine = lax.dynamic_slice_in_dim(grad_norm_one, near * rows, rows, 0)
    one_theirs = lax.dynamic_slice_in_dim(grad_norm_one, (1 - near) * rows, rows, 0)
    grad_norm_half = one_mine + swap_near(one_theirs.astype(jnp.bfloat16)).astype(jnp.float32)
    grad_rows_norm, grad_gain_one, grad_bias_one = layer_norm_back(
        input_half.astype(jnp.float32), gain_one, bias_one, grad_norm_half, 0
    )
    grad_resid_half = lax.dynamic_slice_in_dim(grad_resid, near * rows, rows, 0)
    grad_input = swap_diagonal((grad_resid_half + grad_rows_norm).astype(jnp.bfloat16))
    small_sums = lax.psum(
        (grad_gain_one, grad_bias_one, grad_gain_two, grad_bias_two, dwa_terms), AXES
    )
    return (
        output.astype(jnp.bfloat16)[None],
        grad_input[None],
        grad_history,
        small_sums[4],
        small_sums[0],
        small_sums[1],
        grad_w_attn[:3],
        grad_w_attn[3].T,
        small_sums[2],
        small_sums[3],
        grad_w_up.transpose(1, 0, 2).reshape(grad_w_up.shape[1], -1),
        grad_w_down.transpose(1, 0, 2).reshape(grad_w_down.shape[1], -1).T,
    )


def solution(mesh):
    in_specs = (
        P(("dp", "rep"), "tp", None),
        P(None, ("dp", "rep"), "tp", None),
        P(("dp", "rep"), "tp", None),
        P(("dp", "rep"), None),
        P(),
        P(),
        P(),
        P(None, None, "tp"),
        P("tp", None),
        P(),
        P(),
        P(None, "tp"),
        P("tp", None),
    )
    out_specs = (
        P(("dp", "rep"), "tp", None),
        P(("dp", "rep"), "tp", None),
        P(None, ("dp", "rep"), "tp", None),
        P(),
        P(),
        P(),
        P(None, "dp", "tp"),
        P("tp", "dp"),
        P(),
        P(),
        P("dp", "tp"),
        P("tp", "dp"),
    )
    return jax.shard_map(local, mesh=mesh, in_specs=in_specs, out_specs=out_specs, check_vma=False)
```

```python
import functools
import math

import jax
import jax.numpy as jnp
from jax import lax
from jax.experimental import pallas as pl
from jax.experimental.pallas import tpu as pltpu
from jax.sharding import PartitionSpec as P

HEAD_DIM = 64
LONGEST = 512
NEG_FILL = -1e30
NORM_EPS = 1e-05
BLOCK = 256
LANES = 128
NT = (((1,), (1,)), ((), ()))


def dot(a, b, dims=(((1,), (0,)), ((), ()))):
    return lax.dot_general(a, b, dims, preferred_element_type=jnp.float32)


def spans(whole, reach):
    back = -(-(reach - 1) // BLOCK)
    runs = []
    for i in range(whole // BLOCK):
        count = min(i, back) + 1
        if runs and runs[-1][2] == count:
            runs[-1][1] = i + 1
        else:
            runs.append([i, i + 1, count])
    return runs


def each_block(whole, reach, body):
    for first, last, count in spans(whole, reach):
        def step(at, carry, first=first, count=count):
            i = first + at // 2
            body(i, i + 1 - count, count * BLOCK, at % 2)
            return carry
        lax.fori_loop(0, 2 * (last - first), step, 0)


def attend_kernel(reach, start_ref, q_ref, k_ref, v_ref, out_ref, acc_ref):
    whole = q_ref.shape[0]
    lane = lax.broadcasted_iota(jnp.int32, (BLOCK, LANES), 1) // HEAD_DIM

    def body(i, first, count, head):
        at = pl.ds(pl.multiple_of(i * BLOCK, BLOCK), BLOCK)
        keys = pl.ds(pl.multiple_of(first * BLOCK, BLOCK), count)
        query = q_ref[at, :] * (HEAD_DIM**-0.5)
        query = jnp.where(lane == head, query, jnp.zeros_like(query))
        scores = dot(query, k_ref[keys, :], NT)
        key_at = first * BLOCK + lax.broadcasted_iota(jnp.int32, scores.shape, 1)
        query_at = i * BLOCK + lax.broadcasted_iota(jnp.int32, scores.shape, 0)
        allowed = (key_at >= start_ref[at, :1]) & (key_at <= query_at)
        scores = jnp.where(allowed, scores, NEG_FILL)
        exponent = jnp.exp(scores - jnp.max(scores, axis=1, keepdims=True))
        row_sum = jnp.sum(exponent, axis=1, keepdims=True)
        probs = (exponent * (1.0 / row_sum)).astype(jnp.bfloat16)
        mixed = dot(probs, v_ref[keys, :])

        @pl.when(head == 0)
        def _():
            acc_ref[...] = mixed

        @pl.when(head == 1)
        def _():
            out_ref[at, :] = jnp.where(lane == 0, acc_ref[...], mixed).astype(out_ref.dtype)

    each_block(whole, reach, body)


def attend(start_column, queries, keys, values, reach):
    whole, width = queries.shape
    block = pl.BlockSpec((whole, LANES), lambda p: (0, p))
    return pl.pallas_call(
        functools.partial(attend_kernel, reach),
        grid=(width // LANES,),
        in_specs=[pl.BlockSpec((whole, LANES), lambda p: (0, 0)), block, block, block],
        out_specs=block,
        out_shape=jax.ShapeDtypeStruct((whole, width), jnp.bfloat16),
        scratch_shapes=[pltpu.VMEM((BLOCK, LANES), jnp.float32)],
        compiler_params=pltpu.CompilerParams(vmem_limit_bytes=40 << 20),
        cost_estimate=pl.CostEstimate(
            flops=4 * whole * width * 640, transcendentals=whole * 640 * 6, bytes_accessed=8 * whole * width
        ),
    )(start_column, queries, keys, values)


def turn_back(field, cos, sin):
    half = HEAD_DIM // 2
    lane = lax.broadcasted_iota(jnp.int32, field.shape, 1) % HEAD_DIM
    crossed = jnp.where(lane < half, pltpu.roll(field, LANES - half, 1), pltpu.roll(field, half, 1))
    return field * cos - crossed * sin


def attend_back_kernel(
    reach, start_ref, cos_ref, sin_ref, q_ref, k_ref, v_ref, g_ref, dq_ref, dk_ref, dv_ref,
    key_acc, value_acc, query_acc,
):
    whole = q_ref.shape[0]
    lane = lax.broadcasted_iota(jnp.int32, (BLOCK, LANES), 1) // HEAD_DIM
    key_acc[...] = jnp.zeros_like(key_acc)
    value_acc[...] = jnp.zeros_like(value_acc)

    def body(i, first, count, head):
        at = pl.ds(pl.multiple_of(i * BLOCK, BLOCK), BLOCK)
        span = pl.ds(pl.multiple_of(first * BLOCK, BLOCK), count)
        query = q_ref[at, :] * (HEAD_DIM**-0.5)
        query = jnp.where(lane == head, query, jnp.zeros_like(query))
        grad = g_ref[at, :]
        grad = jnp.where(lane == head, grad, jnp.zeros_like(grad))
        keys = k_ref[span, :]
        scores = dot(keys, query, NT)
        key_at = first * BLOCK + lax.broadcasted_iota(jnp.int32, scores.shape, 0)
        query_at = i * BLOCK + lax.broadcasted_iota(jnp.int32, scores.shape, 1)
        allowed = (key_at >= start_ref[:1, at]) & (key_at <= query_at)
        scores = jnp.where(allowed, scores, NEG_FILL)
        exponent = jnp.exp(scores - jnp.max(scores, axis=0, keepdims=True))
        probs = exponent * (1.0 / jnp.sum(exponent, axis=0, keepdims=True))
        value_acc[span, :] += dot(probs.astype(jnp.bfloat16), grad)
        grad_probs = dot(v_ref[span, :], grad, NT)
        weighted = probs * grad_probs
        grad_scores = (weighted - probs * jnp.sum(weighted, axis=0, keepdims=True)).astype(jnp.bfloat16)
        key_acc[span, :] += dot(grad_scores, query)
        here = dot(grad_scores, keys, (((0,), (0,)), ((), ())))

        @pl.when(head == 0)
        def _():
            query_acc[...] = here

        @pl.when(head == 1)
        def _():
            both = jnp.where(lane == 0, query_acc[...], here) * (HEAD_DIM**-0.5)
            dq_ref[at, :] = turn_back(both, cos_ref[at, :], sin_ref[at, :]).astype(dq_ref.dtype)

    each_block(whole, reach, body)

    def finish(i, carry):
        at = pl.ds(pl.multiple_of(i * BLOCK, BLOCK), BLOCK)
        dk_ref[at, :] = turn_back(key_acc[at, :], cos_ref[at, :], sin_ref[at, :]).astype(dk_ref.dtype)
        dv_ref[at, :] = value_acc[at, :].astype(dv_ref.dtype)
        return carry

    lax.fori_loop(0, whole // BLOCK, finish, 0)


def attend_back(start_row, cos, sin, queries, keys, values, grad_mixed, reach):
    whole, width = queries.shape
    block = pl.BlockSpec((whole, LANES), lambda p: (0, p))
    table = pl.BlockSpec((whole, LANES), lambda p: (0, 0))
    return pl.pallas_call(
        functools.partial(attend_back_kernel, reach),
        grid=(width // LANES,),
        in_specs=[pl.BlockSpec((8, whole), lambda p: (0, 0)), table, table, block, block, block, block],
        out_specs=[block] * 3,
        out_shape=[jax.ShapeDtypeStruct((whole, width), jnp.bfloat16)] * 3,
        scratch_shapes=[
            pltpu.VMEM((whole, LANES), jnp.float32),
            pltpu.VMEM((whole, LANES), jnp.float32),
            pltpu.VMEM((BLOCK, LANES), jnp.float32),
        ],
        compiler_params=pltpu.CompilerParams(vmem_limit_bytes=40 << 20),
        cost_estimate=pl.CostEstimate(
            flops=10 * whole * width * 640, transcendentals=whole * 640 * 6, bytes_accessed=14 * whole * width
        ),
    )(start_row, cos, sin, queries, keys, values, grad_mixed)


ROWS = 256


def norm_parts(field):
    centered = field - jnp.mean(field, axis=-1, keepdims=True)
    scale = lax.rsqrt(jnp.mean(centered * centered, axis=-1, keepdims=True) + NORM_EPS)
    return centered * scale, scale


def wide(ref, at):
    return ref[at, :].astype(jnp.float32)


def row_blocks(count, body):
    def step(i, carry):
        body(i, pl.ds(pl.multiple_of(i * ROWS, ROWS), ROWS))
        return carry

    lax.fori_loop(0, count // ROWS, step, 0)


def whole_spec(shape):
    return pl.BlockSpec(shape, lambda *at: (0,) * len(shape))


def turn(field, cos, sin):
    half = HEAD_DIM // 2
    lane = lax.broadcasted_iota(jnp.int32, field.shape, 1) % HEAD_DIM
    crossed = jnp.where(lane < half, pltpu.roll(field, LANES - half, 1), pltpu.roll(field, half, 1))
    return field * cos + crossed * sin


def project_kernel(
    flags, rows_ref, gain_ref, shift_ref, cos_ref, sin_ref, w_own, w_got, out_ref, turned_ref, norm_ref
):
    whole = rows_ref.shape[0]
    step = pl.program_id(0)

    @pl.when(step == 0)
    def _():
        def body(i, at):
            unit, unused = norm_parts(wide(rows_ref, at))
            norm = unit * gain_ref[...] + shift_ref[...]
            norm_ref[at, :] = norm.astype(jnp.bfloat16)
            turned_ref[:, at] = norm.T.astype(jnp.bfloat16)

        row_blocks(whole, body)

    weight = jnp.where(flags[0] == 1, w_own[0], w_got[0])

    def body(i, at):
        field = dot(norm_ref[at, :], weight)

        @pl.when(step < 2)
        def _():
            for p in range(field.shape[1] // LANES):
                lanes = slice(p * LANES, (p + 1) * LANES)
                out_ref[0, at, lanes] = turn(field[:, lanes], cos_ref[at, :], sin_ref[at, :]).astype(
                    jnp.bfloat16
                )

        @pl.when(step == 2)
        def _():
            out_ref[0, at, :] = field.astype(jnp.bfloat16)

    row_blocks(whole, body)


def project(flags, rows, gain, shift, cos, sin, w_own, w_got):
    whole, width = rows.shape
    count, unused, columns = w_own.shape
    weight = pl.BlockSpec((1, width, columns), lambda c, flags: (c, 0, 0))
    return pl.pallas_call(
        project_kernel,
        grid_spec=pltpu.PrefetchScalarGridSpec(
            num_scalar_prefetch=1,
            grid=(count,),
            in_specs=[
                whole_spec((whole, width)),
                whole_spec((1, width)),
                whole_spec((1, width)),
                whole_spec((whole, LANES)),
                whole_spec((whole, LANES)),
                weight,
                weight,
            ],
            out_specs=[
                pl.BlockSpec((1, whole, columns), lambda c, flags: (c, 0, 0)),
                whole_spec((width, whole)),
            ],
            scratch_shapes=[pltpu.VMEM((whole, width), jnp.bfloat16)],
        ),
        out_shape=[
            jax.ShapeDtypeStruct((count, whole, columns), jnp.bfloat16),
            jax.ShapeDtypeStruct((width, whole), jnp.bfloat16),
        ],
        compiler_params=pltpu.CompilerParams(vmem_limit_bytes=40 << 20),
        cost_estimate=pl.CostEstimate(
            flops=2 * whole * width * columns * count,
            transcendentals=0,
            bytes_accessed=12 * whole * width,
        ),
    )(flags, rows, gain, shift, cos, sin, w_own, w_got)


HIDDEN = 256


def gelu_both(up):
    root = math.sqrt(2.0 / math.pi)
    square = up * up
    bent = jnp.tanh(root * up * (1.0 + 0.044715 * square))
    half = 0.5 * (1.0 + bent)
    slope = half + 0.5 * up * (1.0 - bent * bent) * (root * (1.0 + 3.0 * 0.044715 * square))
    return up * half, slope


def feed_kernel(
    flags, weight_ref, rows_ref, own_ref, got_ref, cot_ref, gain_ref, shift_ref, up_own, up_got,
    down_own, down_got, down_ref, back_ref, gup_ref, gdown_ref,
    norm, norm_t, grad, grad_t, act, slope, up_w, down_w,
):
    whole, width = rows_ref.shape
    step = pl.program_id(0)
    last = pl.num_programs(0) - 1

    @pl.when(step == 0)
    def _():
        def body(i, at):
            unit, unused = norm_parts(wide(rows_ref, at) + wide(own_ref, at) + wide(got_ref, at))
            field = unit * gain_ref[...] + shift_ref[...]
            norm[at, :] = field.astype(jnp.bfloat16)
            norm_t[:, at] = field.T.astype(jnp.bfloat16)
            field = wide(cot_ref, at) * weight_ref[0]
            grad[at, :] = field.astype(jnp.bfloat16)
            grad_t[:, at] = field.T.astype(jnp.bfloat16)

        row_blocks(whole, body)

    same = flags[0] == 1
    hidden = pl.ds(pl.multiple_of(step * HIDDEN, HIDDEN), HIDDEN)
    up_block = jnp.where(same, up_own[...], up_got[...])
    down_block = jnp.where(same, down_own[...], down_got[...])
    up_w[:, hidden] = up_block
    down_w[hidden, :] = down_block

    def body(i, at):
        value, rise = gelu_both(dot(norm[at, :], up_block))
        act[at, hidden] = value.astype(jnp.bfloat16)
        slope[at, hidden] = (dot(grad[at, :], down_block, NT) * rise).astype(jnp.bfloat16)

    row_blocks(whole, body)

    def grads(i, at):
        gdown_ref[0, at, :] = dot(grad_t[at, :], act[:, hidden]).astype(jnp.bfloat16)
        gup_ref[0, at, :] = dot(norm_t[at, :], slope[:, hidden]).astype(jnp.bfloat16)

    row_blocks(width, grads)

    @pl.when(step == last)
    def _():
        def body(i, at):
            back_ref[at, :] = dot(slope[at, :], up_w[...], NT).astype(jnp.bfloat16)
            down_ref[at, :] = dot(act[at, :], down_w[...]).astype(jnp.bfloat16)

        row_blocks(whole, body)


def feed(flags, weight, rows, own, got, cot, gain, shift, up_own, up_got, down_own, down_got):
    whole, width = rows.shape
    hidden = up_own.shape[1]
    steps = hidden // HIDDEN
    half = steps // 2
    tokens = whole_spec((whole, width))
    vector = whole_spec((1, width))

    def at(j, flags):
        return lax.rem(flags[2] * half + j, steps)

    up_spec = pl.BlockSpec((width, HIDDEN), lambda j, flags: (0, at(j, flags)))
    down_spec = pl.BlockSpec((HIDDEN, width), lambda j, flags: (at(j, flags), 0))
    piece = pl.BlockSpec((1, width, HIDDEN), lambda j, flags: (j // half, 0, j % half))
    wide_bf16 = jax.ShapeDtypeStruct((whole, width), jnp.bfloat16)
    pieces = jax.ShapeDtypeStruct((2, width, hidden // 2), jnp.bfloat16)
    return pl.pallas_call(
        feed_kernel,
        grid_spec=pltpu.PrefetchScalarGridSpec(
            num_scalar_prefetch=1,
            grid=(steps,),
            in_specs=[
                pl.BlockSpec(memory_space=pltpu.SMEM),
                tokens,
                tokens,
                tokens,
                tokens,
                vector,
                vector,
                up_spec,
                up_spec,
                down_spec,
                down_spec,
            ],
            out_specs=[tokens, tokens, piece, piece],
            scratch_shapes=[
                pltpu.VMEM((whole, width), jnp.bfloat16),
                pltpu.VMEM((width, whole), jnp.bfloat16),
                pltpu.VMEM((whole, width), jnp.bfloat16),
                pltpu.VMEM((width, whole), jnp.bfloat16),
                pltpu.VMEM((whole, hidden), jnp.bfloat16),
                pltpu.VMEM((whole, hidden), jnp.bfloat16),
                pltpu.VMEM((width, hidden), jnp.bfloat16),
                pltpu.VMEM((hidden, width), jnp.bfloat16),
            ],
        ),
        out_shape=[wide_bf16, wide_bf16, pieces, pieces],
        compiler_params=pltpu.CompilerParams(vmem_limit_bytes=56 << 20),
        cost_estimate=pl.CostEstimate(
            flops=12 * whole * width * hidden, transcendentals=whole * hidden, bytes_accessed=32 * whole * width
        ),
    )(flags, weight, rows, own, got, cot, gain, shift, up_own, up_got, down_own, down_got)


def middle_kernel(
    flags, weight_ref, rows_ref, own_ref, got_ref, cot_ref, back_own, back_got, gain_ref, mixed_ref,
    w_own, w_got, grad_ref, gmixed_ref, gout_ref, sums_ref, turned,
):
    whole, width = rows_ref.shape
    weight = jnp.where(flags[0] == 1, w_own[...], w_got[...])
    gain = gain_ref[...]
    sums_ref[...] = jnp.zeros_like(sums_ref)

    def body(i, at):
        unit, scale = norm_parts(wide(rows_ref, at) + wide(own_ref, at) + wide(got_ref, at))
        back = wide(back_own, at) + wide(back_got, at)
        inner = back * gain
        mean = jnp.mean(inner, axis=-1, keepdims=True)
        slant = jnp.mean(inner * unit, axis=-1, keepdims=True)
        grad = wide(cot_ref, at) * weight_ref[0] + scale * (inner - mean - unit * slant)
        low = grad.astype(jnp.bfloat16)
        grad_ref[at, :] = low
        turned[:, at] = grad.T.astype(jnp.bfloat16)
        gmixed_ref[at, :] = dot(low, weight, NT).astype(jnp.bfloat16)

        @pl.when((i * ROWS) // (whole // 2) == flags[1])
        def _():
            sums_ref[0:1, :] += jnp.sum(back * unit, axis=0, keepdims=True)
            sums_ref[1:2, :] += jnp.sum(back, axis=0, keepdims=True)

    row_blocks(whole, body)

    def grads(i, at):
        gout_ref[at, :] = dot(turned[at, :], mixed_ref[...]).astype(jnp.bfloat16)

    row_blocks(width, grads)


def middle(flags, weight, rows, own, got, cot, back_own, back_got, gain, mixed, w_own, w_got):
    whole, width = rows.shape
    columns = mixed.shape[1]
    tokens = whole_spec((whole, width))
    narrow = whole_spec((whole, columns))
    projection = whole_spec((columns, width))
    return pl.pallas_call(
        middle_kernel,
        grid_spec=pltpu.PrefetchScalarGridSpec(
            num_scalar_prefetch=1,
            grid=(1,),
            in_specs=[pl.BlockSpec(memory_space=pltpu.SMEM)]
            + [tokens] * 6
            + [whole_spec((1, width)), narrow, projection, projection],
            out_specs=[tokens, narrow, whole_spec((width, columns)), whole_spec((8, width))],
            scratch_shapes=[pltpu.VMEM((width, whole), jnp.bfloat16)],
        ),
        out_shape=[
            jax.ShapeDtypeStruct((whole, width), jnp.bfloat16),
            jax.ShapeDtypeStruct((whole, columns), jnp.bfloat16),
            jax.ShapeDtypeStruct((width, columns), jnp.bfloat16),
            jax.ShapeDtypeStruct((8, width), jnp.float32),
        ],
        compiler_params=pltpu.CompilerParams(vmem_limit_bytes=56 << 20),
        cost_estimate=pl.CostEstimate(
            flops=4 * whole * width * columns, transcendentals=0, bytes_accessed=18 * whole * width
        ),
    )(flags, weight, rows, own, got, cot, back_own, back_got, gain, mixed, w_own, w_got)


def unproject_kernel(flags, gq_ref, gk_ref, gv_ref, turned_ref, w_own, w_got, keep_ref, send_ref, gw_ref, weight):
    whole = gq_ref.shape[0]
    width = turned_ref.shape[0]
    weight[...] = jnp.where(flags[0] == 1, w_own[...], w_got[...])
    half = whole // 2

    def side(near, out_ref):
        def body(i, at):
            from_rows = pl.ds(pl.multiple_of(near * half + i * ROWS, ROWS), ROWS)
            total = dot(gq_ref[from_rows, :], weight[0], NT)
            total = total + dot(gk_ref[from_rows, :], weight[1], NT)
            total = total + dot(gv_ref[from_rows, :], weight[2], NT)
            out_ref[at, :] = total.astype(out_ref.dtype)

        row_blocks(half, body)

    side(1 - flags[1], send_ref)
    side(flags[1], keep_ref)

    def grads(i, at):
        for c, ref in enumerate((gq_ref, gk_ref, gv_ref)):
            gw_ref[c, at, :] = dot(turned_ref[at, :], ref[...]).astype(jnp.bfloat16)

    row_blocks(width, grads)


def unproject(flags, gq, gk, gv, turned, w_own, w_got):
    whole, columns = gq.shape
    width = turned.shape[0]
    narrow = whole_spec((whole, columns))
    weights = whole_spec((3, width, columns))
    half = whole_spec((whole // 2, width))
    return pl.pallas_call(
        unproject_kernel,
        grid_spec=pltpu.PrefetchScalarGridSpec(
            num_scalar_prefetch=1,
            grid=(1,),
            in_specs=[narrow, narrow, narrow, whole_spec((width, whole)), weights, weights],
            out_specs=[half, half, weights],
            scratch_shapes=[pltpu.VMEM((3, width, columns), jnp.bfloat16)],
        ),
        out_shape=[
            jax.ShapeDtypeStruct((whole // 2, width), jnp.float32),
            jax.ShapeDtypeStruct((whole // 2, width), jnp.bfloat16),
            jax.ShapeDtypeStruct((3, width, columns), jnp.bfloat16),
        ],
        compiler_params=pltpu.CompilerParams(vmem_limit_bytes=56 << 20),
        cost_estimate=pl.CostEstimate(
            flops=12 * whole * width * columns, transcendentals=0, bytes_accessed=12 * whole * width
        ),
    )(flags, gq, gk, gv, turned, w_own, w_got)


def first_norm_kernel(flags, rows_ref, keep_ref, got_ref, resid_ref, gain_ref, out_ref, sums_ref):
    sums_ref[...] = jnp.zeros_like(sums_ref)

    def body(i, at):
        unit, scale = norm_parts(wide(rows_ref, at))
        back = keep_ref[at, :] + wide(got_ref, at)
        inner = back * gain_ref[...]
        mean = jnp.mean(inner, axis=-1, keepdims=True)
        slant = jnp.mean(inner * unit, axis=-1, keepdims=True)
        grad = wide(resid_ref, at) + scale * (inner - mean - unit * slant)
        out_ref[at, :] = grad.astype(jnp.bfloat16)
        sums_ref[0:1, :] += jnp.sum(back * unit, axis=0, keepdims=True)
        sums_ref[1:2, :] += jnp.sum(back, axis=0, keepdims=True)

    row_blocks(rows_ref.shape[0], body)


def first_norm_back(flags, rows, keep, got, resid, gain):
    half, width = keep.shape
    mine = pl.BlockSpec((half, width), lambda i, flags: (flags[1], 0))
    tokens = whole_spec((half, width))
    return pl.pallas_call(
        first_norm_kernel,
        grid_spec=pltpu.PrefetchScalarGridSpec(
            num_scalar_prefetch=1,
            grid=(1,),
            in_specs=[mine, tokens, tokens, mine, whole_spec((1, width))],
            out_specs=[tokens, whole_spec((8, width))],
        ),
        out_shape=[
            jax.ShapeDtypeStruct((half, width), jnp.bfloat16),
            jax.ShapeDtypeStruct((8, width), jnp.float32),
        ],
        compiler_params=pltpu.CompilerParams(vmem_limit_bytes=40 << 20),
        cost_estimate=pl.CostEstimate(flops=20 * half * width, transcendentals=0, bytes_accessed=12 * half * width),
    )(flags, rows, keep, got, resid, gain)


AXES = ("tp", "dp", "rep")


def pairs_of(move):
    tps, dps, reps = (lax.axis_size(name) for name in AXES)
    index = lambda t, d, r: (t * dps + d) * reps + r
    every = [(t, d, r) for t in range(tps) for d in range(dps) for r in range(reps)]
    return [(index(*at), index(*move(*at))) for at in every if move(*at) != at]


def swap_diagonal(field):
    return lax.ppermute(field, AXES, pairs_of(lambda t, d, r: (r % 2, d, r - r % 2 + t)))


def swap_near(field):
    return lax.ppermute(field, "rep", [(r, r ^ 1) for r in range(lax.axis_size("rep"))])


def swap_far(field):
    return lax.ppermute(field, "rep", [(r, r ^ 2) for r in range(lax.axis_size("rep"))])


def ordered(own, other, first):
    return jnp.where(
        first, jnp.concatenate([own, other], axis=0), jnp.concatenate([other, own], axis=0)
    )


def take(field, index):
    return lax.dynamic_index_in_dim(field, index, 0, keepdims=False)


def half_columns(field, index):
    size = field.shape[-1] // 2
    return lax.dynamic_slice_in_dim(field, index * size, size, field.ndim - 1)


def sum_rows(block):
    dps = lax.axis_size("dp")
    rows = block.shape[0] // dps
    low = block.astype(jnp.bfloat16)
    if dps <= 8:
        place = lax.axis_index("dp")
        total = lax.dynamic_slice_in_dim(block, place * rows, rows, 0)
        for step in range(1, dps):
            sent = lax.dynamic_slice_in_dim(low, lax.rem(place + step, dps) * rows, rows, 0)
            total = total + lax.ppermute(
                sent, "dp", [(d, (d + step) % dps) for d in range(dps)]
            ).astype(jnp.float32)
    else:
        total = lax.psum_scatter(low, "dp", scatter_dimension=0, tiled=True)
    return lax.all_gather(total.astype(jnp.bfloat16), "rep", axis=0).astype(jnp.float32)


def sum_far_first(mine, theirs, same, near):
    pair = (mine.astype(jnp.float32) + swap_far(theirs).astype(jnp.float32)).astype(jnp.bfloat16)
    pair = jnp.where(same, pair, swap_diagonal(pair))
    keep, send = half_columns(pair, near), half_columns(pair, 1 - near)
    return sum_rows(keep.astype(jnp.float32) + swap_near(send).astype(jnp.float32))


def sum_diagonal_first(pieces, same, near):
    pieces = jnp.where(same, pieces, swap_diagonal(pieces))
    keep, send = half_columns(pieces, near), half_columns(pieces, 1 - near)
    pair = keep.astype(jnp.float32) + swap_near(send).astype(jnp.float32)
    return sum_rows(pair[0] + swap_far(pair[1].astype(jnp.bfloat16)).astype(jnp.float32))


def local(
    layer_input,
    history,
    cotangent,
    lengths,
    dwa_weights,
    gain_one,
    bias_one,
    w_qkv,
    w_out,
    gain_two,
    bias_two,
    w_up,
    w_down,
):
    rows = layer_input.shape[1]
    whole = rows * lax.axis_size("tp")
    hist_count = history.shape[0]
    part, slot = lax.axis_index("tp"), lax.axis_index("rep")
    near, far = slot % 2, slot // 2
    same = near == part
    flags = jnp.stack([same.astype(jnp.int32), near, far])
    own_weight = dwa_weights[hist_count:]

    input_half = jnp.where(same, layer_input[0], swap_diagonal(layer_input[0]))
    got_qkv = swap_diagonal(w_qkv)
    got_out = swap_diagonal(w_out)
    got_up = swap_diagonal(w_up)
    cot_half = jnp.where(same, cotangent[0], swap_diagonal(cotangent[0]))
    got_down = swap_diagonal(w_down)
    own_lengths = jnp.where(same, lengths, swap_near(lengths))[0]
    seq_owner, token_place = positions(own_lengths, whole)
    seq_begin = jnp.arange(whole, dtype=jnp.int32) - token_place
    start_column = jnp.broadcast_to(seq_begin[:, None], (whole, LANES))
    start_row = jnp.broadcast_to(seq_begin[None, :], (8, whole))
    half_dim = HEAD_DIM // 2
    lane = jnp.arange(LANES, dtype=jnp.int32)
    frequency = jnp.exp((lane % half_dim).astype(jnp.float32) * (-math.log(10000.0) / half_dim))
    angles = token_place.astype(jnp.float32)[:, None] * frequency[None, :]
    cos_table = jnp.cos(angles)
    sin_table = jnp.sin(angles) * jnp.where(lane % HEAD_DIM < half_dim, -1.0, 1.0)[None, :]
    layer_rows = ordered(input_half, swap_near(input_half), near == 0)
    cot_rows = ordered(cot_half, swap_near(cot_half), near == 0)
    gain_one, bias_one = gain_one[None], bias_one[None]
    gain_two, bias_two = gain_two[None], bias_two[None]

    projected, norm_one_t = project(
        flags, layer_rows, gain_one, bias_one, cos_table, sin_table, w_qkv, got_qkv
    )
    queries, keys, values = projected[0], projected[1], projected[2]
    mixed = attend(start_column, queries, keys, values, LONGEST)
    attn = jnp.dot(
        mixed, jnp.where(same, w_out, got_out), preferred_element_type=jnp.float32
    ).astype(jnp.bfloat16)
    attn_got = swap_near(attn)
    down, back, grad_up, grad_down = feed(
        flags,
        own_weight,
        layer_rows,
        attn,
        attn_got,
        cot_rows,
        gain_two,
        bias_two,
        w_up,
        got_up,
        w_down,
        got_down,
    )
    back_got = swap_near(back)
    grad_attn, grad_mixed, grad_out, sums_two = middle(
        flags,
        own_weight,
        layer_rows,
        attn,
        attn_got,
        cot_rows,
        back,
        back_got,
        gain_two,
        mixed,
        w_out,
        got_out,
    )
    grad_w_up = sum_far_first(grad_up[0], grad_up[1], same, near)
    grad_w_down = sum_diagonal_first(grad_down, same, near)

    def half_of(field, index):
        return lax.dynamic_slice_in_dim(field, index * rows, rows, 0)

    block_half = sum(
        half_of(field, near).astype(jnp.float32) for field in (layer_rows, attn, attn_got, down)
    ) + swap_near(half_of(down, 1 - near)).astype(jnp.float32)
    block_half = block_half.astype(jnp.bfloat16)
    block_out = jnp.where(same, block_half, swap_diagonal(block_half)).astype(jnp.float32)
    hist_rows = history[:, 0].astype(jnp.float32)
    output = (
        jnp.sum(dwa_weights[:hist_count, None, None] * hist_rows, axis=0)
        + dwa_weights[hist_count] * block_out
    )
    grad_block = cotangent[0].astype(jnp.float32)
    grad_history = (dwa_weights[:hist_count, None, None] * grad_block[None]).astype(jnp.bfloat16)[
        :, None
    ]
    dwa_terms = jnp.concatenate(
        [jnp.sum(hist_rows * grad_block[None], axis=(1, 2)), jnp.sum(block_out * grad_block)[None]]
    )

    grad_queries, grad_keys, grad_values = attend_back(
        start_row, cos_table, sin_table, queries, keys, values, grad_mixed, LONGEST
    )
    keep, send, grad_qkv = unproject(
        flags, grad_queries, grad_keys, grad_values, norm_one_t, w_qkv, got_qkv
    )
    input_grad, sums_one = first_norm_back(flags, layer_rows, keep, swap_near(send), grad_attn, gain_one)
    grad_input = jnp.where(same, input_grad, swap_diagonal(input_grad))
    attn_pieces = jnp.concatenate([grad_qkv, grad_out[None]], axis=0)
    mine = lax.dynamic_slice_in_dim(attn_pieces, 2 * far, 2, 0)
    theirs = lax.dynamic_slice_in_dim(attn_pieces, 2 - 2 * far, 2, 0)
    pair = (mine.astype(jnp.float32) + swap_far(theirs).astype(jnp.float32)).astype(jnp.bfloat16)
    pair = jnp.where(same, pair, swap_diagonal(pair))
    grad_w_attn = sum_rows(
        take(pair, near).astype(jnp.float32) + swap_near(take(pair, 1 - near)).astype(jnp.float32)
    )

    small = jnp.concatenate(
        [sums_one[:2], sums_two[:2], jnp.pad(dwa_terms, (0, gain_one.shape[1] - hist_count - 1))[None]]
    )
    small = jnp.sum(lax.all_gather(small, AXES, axis=0), axis=0)

    def columns_of(pieces):
        return pieces.transpose(1, 0, 2).reshape(pieces.shape[1], -1)

    return (
        output.astype(jnp.bfloat16)[None],
        grad_input[None],
        grad_history,
        small[4, : hist_count + 1],
        small[0],
        small[1],
        grad_w_attn[:3],
        grad_w_attn[3].T,
        small[2],
        small[3],
        columns_of(grad_w_up),
        columns_of(grad_w_down).T,
    )


def positions(seq_lengths, token_count):
    seq_ends = jnp.cumsum(seq_lengths)
    seq_starts = seq_ends - seq_lengths
    token_index = jnp.arange(token_count, dtype=jnp.int32)
    seq_owner = jnp.sum((token_index[:, None] >= seq_ends[None, :]).astype(jnp.int32), axis=1)
    picked = (
        seq_owner[:, None] == jnp.arange(seq_lengths.shape[0], dtype=jnp.int32)[None, :]
    ).astype(jnp.int32)
    seq_begin = jnp.sum(picked * seq_starts[None, :], axis=1)
    return (seq_owner, token_index - seq_begin)


def solution(mesh):
    in_specs = (
        P(("dp", "rep"), "tp", None),
        P(None, ("dp", "rep"), "tp", None),
        P(("dp", "rep"), "tp", None),
        P(("dp", "rep"), None),
        P(),
        P(),
        P(),
        P(None, None, "tp"),
        P("tp", None),
        P(),
        P(),
        P(None, "tp"),
        P("tp", None),
    )
    out_specs = (
        P(("dp", "rep"), "tp", None),
        P(("dp", "rep"), "tp", None),
        P(None, ("dp", "rep"), "tp", None),
        P(),
        P(),
        P(),
        P(None, "dp", "tp"),
        P("tp", "dp"),
        P(),
        P(),
        P("dp", "tp"),
        P("tp", "dp"),
    )
    return jax.shard_map(local, mesh=mesh, in_specs=in_specs, out_specs=out_specs, check_vma=False)
```

```python
import functools
import math

import jax
import jax.numpy as jnp
from jax import lax
from jax.experimental import pallas as pl
from jax.experimental.pallas import tpu as pltpu
from jax.sharding import PartitionSpec as P

HEAD_DIM = 64
LONGEST = 512
NEG_FILL = -1e30
NORM_EPS = 1e-05
BLOCK = 256
LANES = 128
NT = (((1,), (1,)), ((), ()))


def dot(a, b, dims=(((1,), (0,)), ((), ()))):
    return lax.dot_general(a, b, dims, preferred_element_type=jnp.float32)


def spans(whole, reach):
    back = -(-(reach - 1) // BLOCK)
    runs = []
    for i in range(whole // BLOCK):
        count = min(i, back) + 1
        if runs and runs[-1][2] == count:
            runs[-1][1] = i + 1
        else:
            runs.append([i, i + 1, count])
    return runs


def each_block(whole, reach, body):
    for first, last, count in spans(whole, reach):
        def step(at, carry, first=first, count=count):
            i = first + at // 2
            body(i, i + 1 - count, count * BLOCK, at % 2)
            return carry
        lax.fori_loop(0, 2 * (last - first), step, 0)


def attend_kernel(reach, start_ref, q_ref, k_ref, v_ref, out_ref, acc_ref):
    whole = q_ref.shape[0]
    lane = lax.broadcasted_iota(jnp.int32, (BLOCK, LANES), 1) // HEAD_DIM

    def body(i, first, count, head):
        at = pl.ds(pl.multiple_of(i * BLOCK, BLOCK), BLOCK)
        keys = pl.ds(pl.multiple_of(first * BLOCK, BLOCK), count)
        query = q_ref[at, :] * (HEAD_DIM**-0.5)
        query = jnp.where(lane == head, query, jnp.zeros_like(query))
        scores = dot(query, k_ref[keys, :], NT)
        key_at = first * BLOCK + lax.broadcasted_iota(jnp.int32, scores.shape, 1)
        query_at = i * BLOCK + lax.broadcasted_iota(jnp.int32, scores.shape, 0)
        allowed = (key_at >= start_ref[at, :1]) & (key_at <= query_at)
        scores = jnp.where(allowed, scores, NEG_FILL)
        exponent = jnp.exp(scores - jnp.max(scores, axis=1, keepdims=True))
        row_sum = jnp.sum(exponent, axis=1, keepdims=True)
        probs = (exponent * (1.0 / row_sum)).astype(jnp.bfloat16)
        mixed = dot(probs, v_ref[keys, :])

        @pl.when(head == 0)
        def _():
            acc_ref[...] = mixed

        @pl.when(head == 1)
        def _():
            out_ref[at, :] = jnp.where(lane == 0, acc_ref[...], mixed).astype(out_ref.dtype)

    each_block(whole, reach, body)


def attend(start_column, queries, keys, values, reach):
    whole, width = queries.shape
    block = pl.BlockSpec((whole, LANES), lambda p: (0, p))
    return pl.pallas_call(
        functools.partial(attend_kernel, reach),
        grid=(width // LANES,),
        in_specs=[pl.BlockSpec((whole, LANES), lambda p: (0, 0)), block, block, block],
        out_specs=block,
        out_shape=jax.ShapeDtypeStruct((whole, width), jnp.bfloat16),
        scratch_shapes=[pltpu.VMEM((BLOCK, LANES), jnp.float32)],
        compiler_params=pltpu.CompilerParams(vmem_limit_bytes=40 << 20),
        cost_estimate=pl.CostEstimate(
            flops=4 * whole * width * 640, transcendentals=whole * 640 * 6, bytes_accessed=8 * whole * width
        ),
    )(start_column, queries, keys, values)


def turn_back(field, cos, sin):
    half = HEAD_DIM // 2
    lane = lax.broadcasted_iota(jnp.int32, field.shape, 1) % HEAD_DIM
    crossed = jnp.where(lane < half, pltpu.roll(field, LANES - half, 1), pltpu.roll(field, half, 1))
    return field * cos - crossed * sin


def attend_back_kernel(
    reach, start_ref, cos_ref, sin_ref, q_ref, k_ref, v_ref, g_ref, dq_ref, dk_ref, dv_ref,
    key_acc, value_acc, query_acc,
):
    whole = q_ref.shape[0]
    lane = lax.broadcasted_iota(jnp.int32, (BLOCK, LANES), 1) // HEAD_DIM
    key_acc[...] = jnp.zeros_like(key_acc)
    value_acc[...] = jnp.zeros_like(value_acc)

    def body(i, first, count, head):
        at = pl.ds(pl.multiple_of(i * BLOCK, BLOCK), BLOCK)
        span = pl.ds(pl.multiple_of(first * BLOCK, BLOCK), count)
        query = q_ref[at, :] * (HEAD_DIM**-0.5)
        query = jnp.where(lane == head, query, jnp.zeros_like(query))
        grad = g_ref[at, :]
        grad = jnp.where(lane == head, grad, jnp.zeros_like(grad))
        keys = k_ref[span, :]
        scores = dot(keys, query, NT)
        key_at = first * BLOCK + lax.broadcasted_iota(jnp.int32, scores.shape, 0)
        query_at = i * BLOCK + lax.broadcasted_iota(jnp.int32, scores.shape, 1)
        allowed = (key_at >= start_ref[:1, at]) & (key_at <= query_at)
        scores = jnp.where(allowed, scores, NEG_FILL)
        exponent = jnp.exp(scores - jnp.max(scores, axis=0, keepdims=True))
        probs = exponent * (1.0 / jnp.sum(exponent, axis=0, keepdims=True))
        value_acc[span, :] += dot(probs.astype(jnp.bfloat16), grad)
        grad_probs = dot(v_ref[span, :], grad, NT)
        weighted = probs * grad_probs
        grad_scores = (weighted - probs * jnp.sum(weighted, axis=0, keepdims=True)).astype(jnp.bfloat16)
        key_acc[span, :] += dot(grad_scores, query)
        here = dot(grad_scores, keys, (((0,), (0,)), ((), ())))

        @pl.when(head == 0)
        def _():
            query_acc[...] = here

        @pl.when(head == 1)
        def _():
            both = jnp.where(lane == 0, query_acc[...], here) * (HEAD_DIM**-0.5)
            dq_ref[at, :] = turn_back(both, cos_ref[at, :], sin_ref[at, :]).astype(dq_ref.dtype)

    each_block(whole, reach, body)

    def finish(i, carry):
        at = pl.ds(pl.multiple_of(i * BLOCK, BLOCK), BLOCK)
        dk_ref[at, :] = turn_back(key_acc[at, :], cos_ref[at, :], sin_ref[at, :]).astype(dk_ref.dtype)
        dv_ref[at, :] = value_acc[at, :].astype(dv_ref.dtype)
        return carry

    lax.fori_loop(0, whole // BLOCK, finish, 0)


def attend_back(start_row, cos, sin, queries, keys, values, grad_mixed, reach):
    whole, width = queries.shape
    block = pl.BlockSpec((whole, LANES), lambda p: (0, p))
    table = pl.BlockSpec((whole, LANES), lambda p: (0, 0))
    return pl.pallas_call(
        functools.partial(attend_back_kernel, reach),
        grid=(width // LANES,),
        in_specs=[pl.BlockSpec((8, whole), lambda p: (0, 0)), table, table, block, block, block, block],
        out_specs=[block] * 3,
        out_shape=[jax.ShapeDtypeStruct((whole, width), jnp.bfloat16)] * 3,
        scratch_shapes=[
            pltpu.VMEM((whole, LANES), jnp.float32),
            pltpu.VMEM((whole, LANES), jnp.float32),
            pltpu.VMEM((BLOCK, LANES), jnp.float32),
        ],
        compiler_params=pltpu.CompilerParams(vmem_limit_bytes=40 << 20),
        cost_estimate=pl.CostEstimate(
            flops=10 * whole * width * 640, transcendentals=whole * 640 * 6, bytes_accessed=14 * whole * width
        ),
    )(start_row, cos, sin, queries, keys, values, grad_mixed)


ROWS = 256


def norm_parts(field):
    centered = field - jnp.mean(field, axis=-1, keepdims=True)
    scale = lax.rsqrt(jnp.mean(centered * centered, axis=-1, keepdims=True) + NORM_EPS)
    return centered * scale, scale


def wide(ref, at):
    return ref[at, :].astype(jnp.float32)


def row_blocks(count, body):
    def step(i, carry):
        body(i, pl.ds(pl.multiple_of(i * ROWS, ROWS), ROWS))
        return carry

    lax.fori_loop(0, count // ROWS, step, 0)


def whole_spec(shape):
    return pl.BlockSpec(shape, lambda *at: (0,) * len(shape))


def join_rows(flags, own, near, far, out):
    half = near.shape[0]
    for index, got in ((flags[2], near), (1 - flags[2], far)):
        at = pl.ds(pl.multiple_of(index * half, half), half)
        out[at, :] = jnp.where(flags[0] == 1, own[at, :], got[...])


def turn(field, cos, sin):
    half = HEAD_DIM // 2
    lane = lax.broadcasted_iota(jnp.int32, field.shape, 1) % HEAD_DIM
    crossed = jnp.where(lane < half, pltpu.roll(field, LANES - half, 1), pltpu.roll(field, half, 1))
    return field * cos + crossed * sin


def project_kernel(
    flags, rows_ref, gain_ref, shift_ref, cos_ref, sin_ref, w_own, w_near, w_far, out_ref, turned_ref,
    weight_ref, norm_ref,
):
    whole = rows_ref.shape[0]
    step = pl.program_id(0)

    @pl.when(step == 0)
    def _():
        def body(i, at):
            unit, unused = norm_parts(wide(rows_ref, at))
            norm = unit * gain_ref[...] + shift_ref[...]
            norm_ref[at, :] = norm.astype(jnp.bfloat16)
            turned_ref[:, at] = norm.T.astype(jnp.bfloat16)

        row_blocks(whole, body)

    join_rows(flags, w_own.at[0], w_near.at[0], w_far.at[0], weight_ref.at[0])

    def body(i, at):
        field = dot(norm_ref[at, :], weight_ref[0])

        @pl.when(step < 2)
        def _():
            for p in range(field.shape[1] // LANES):
                lanes = slice(p * LANES, (p + 1) * LANES)
                out_ref[0, at, lanes] = turn(field[:, lanes], cos_ref[at, :], sin_ref[at, :]).astype(
                    jnp.bfloat16
                )

        @pl.when(step == 2)
        def _():
            out_ref[0, at, :] = field.astype(jnp.bfloat16)

    row_blocks(whole, body)


def project(flags, rows, gain, shift, cos, sin, w_own, w_near, w_far):
    whole, width = rows.shape
    count, unused, columns = w_own.shape
    weight = pl.BlockSpec((1, width, columns), lambda c, flags: (c, 0, 0))
    part = pl.BlockSpec((1, width // 2, columns), lambda c, flags: (c, 0, 0))
    return pl.pallas_call(
        project_kernel,
        grid_spec=pltpu.PrefetchScalarGridSpec(
            num_scalar_prefetch=1,
            grid=(count,),
            in_specs=[
                whole_spec((whole, width)),
                whole_spec((1, width)),
                whole_spec((1, width)),
                whole_spec((whole, LANES)),
                whole_spec((whole, LANES)),
                weight,
                part,
                part,
            ],
            out_specs=[
                pl.BlockSpec((1, whole, columns), lambda c, flags: (c, 0, 0)),
                whole_spec((width, whole)),
                weight,
            ],
            scratch_shapes=[pltpu.VMEM((whole, width), jnp.bfloat16)],
        ),
        out_shape=[
            jax.ShapeDtypeStruct((count, whole, columns), jnp.bfloat16),
            jax.ShapeDtypeStruct((width, whole), jnp.bfloat16),
            jax.ShapeDtypeStruct(w_own.shape, jnp.bfloat16),
        ],
        compiler_params=pltpu.CompilerParams(vmem_limit_bytes=40 << 20),
        cost_estimate=pl.CostEstimate(
            flops=2 * whole * width * columns * count,
            transcendentals=0,
            bytes_accessed=12 * whole * width,
        ),
    )(flags, rows, gain, shift, cos, sin, w_own, w_near, w_far)


HIDDEN = 256


def gelu_both(up):
    root = math.sqrt(2.0 / math.pi)
    square = up * up
    bent = jnp.tanh(root * up * (1.0 + 0.044715 * square))
    half = 0.5 * (1.0 + bent)
    slope = half + 0.5 * up * (1.0 - bent * bent) * (root * (1.0 + 3.0 * 0.044715 * square))
    return up * half, slope


def feed_kernel(
    flags, weight_ref, rows_ref, own_ref, got_ref, cot_ref, gain_ref, shift_ref, up_own, up_near,
    up_far, down_own, down_near, down_far, down_ref, back_ref, keep_ref, send_ref, gdown_ref, norm, norm_t, grad, grad_t, act, slope, up_w, down_w,
):
    whole, width = rows_ref.shape
    step = pl.program_id(0)
    last = pl.num_programs(0) - 1

    @pl.when(step == 0)
    def _():
        def body(i, at):
            unit, unused = norm_parts(wide(rows_ref, at) + wide(own_ref, at) + wide(got_ref, at))
            field = unit * gain_ref[...] + shift_ref[...]
            norm[at, :] = field.astype(jnp.bfloat16)
            norm_t[:, at] = field.T.astype(jnp.bfloat16)
            field = wide(cot_ref, at) * weight_ref[0]
            grad[at, :] = field.astype(jnp.bfloat16)
            grad_t[:, at] = field.T.astype(jnp.bfloat16)

        row_blocks(whole, body)

    hidden = pl.ds(pl.multiple_of(step * HIDDEN, HIDDEN), HIDDEN)
    first = step < pl.num_programs(0) // 2
    join_rows(flags, up_own, up_near, up_far, up_w.at[:, hidden])
    down_w[hidden, :] = jnp.where(
        flags[0] == 1, down_own[...], jnp.where(first, down_near[...], down_far[...])
    )
    up_block = up_w[:, hidden]
    down_block = down_w[hidden, :]

    def body(i, at):
        value, rise = gelu_both(dot(norm[at, :], up_block))
        act[at, hidden] = value.astype(jnp.bfloat16)
        slope[at, hidden] = (dot(grad[at, :], down_block, NT) * rise).astype(jnp.bfloat16)

    row_blocks(whole, body)

    def grads(i, at):
        gdown_ref[0, at, :] = dot(grad_t[at, :], act[:, hidden]).astype(jnp.bfloat16)
        grad_up = dot(norm_t[at, :], slope[:, hidden]).astype(jnp.bfloat16)

        @pl.when(first)
        def _():
            keep_ref[at, :] = grad_up

        @pl.when(jnp.logical_not(first))
        def _():
            send_ref[at, :] = grad_up

    row_blocks(width, grads)

    @pl.when(step == last)
    def _():
        def body(i, at):
            back_ref[at, :] = dot(slope[at, :], up_w[...], NT).astype(jnp.bfloat16)
            down_ref[at, :] = dot(act[at, :], down_w[...]).astype(jnp.bfloat16)

        row_blocks(whole, body)


def feed(flags, weight, rows, own, got, cot, gain, shift, up_own, up_near, up_far, down_own, down_near, down_far):
    whole, width = rows.shape
    hidden = up_own.shape[1]
    steps = hidden // HIDDEN
    half = steps // 2
    tokens = whole_spec((whole, width))
    vector = whole_spec((1, width))

    def at(j, flags):
        return lax.rem(flags[2] * half + j, steps)

    def early(j):
        return jnp.minimum(j, half - 1)

    def late(j):
        return jnp.maximum(j - half, 0)

    up_spec = pl.BlockSpec((width, HIDDEN), lambda j, flags: (0, at(j, flags)))
    up_part = pl.BlockSpec((width // 2, HIDDEN), lambda j, flags: (0, at(j, flags)))
    down_spec = pl.BlockSpec((HIDDEN, width), lambda j, flags: (at(j, flags), 0))
    piece = pl.BlockSpec(
        (1, width, HIDDEN), lambda j, flags: (at(j, flags) // half, 0, lax.rem(at(j, flags), half))
    )
    wide_bf16 = jax.ShapeDtypeStruct((whole, width), jnp.bfloat16)
    part = jax.ShapeDtypeStruct((width, hidden // 2), jnp.bfloat16)
    pieces = jax.ShapeDtypeStruct((2, width, hidden // 2), jnp.bfloat16)
    return pl.pallas_call(
        feed_kernel,
        grid_spec=pltpu.PrefetchScalarGridSpec(
            num_scalar_prefetch=1,
            grid=(steps,),
            in_specs=[
                pl.BlockSpec(memory_space=pltpu.SMEM),
                tokens,
                tokens,
                tokens,
                tokens,
                vector,
                vector,
                up_spec,
                up_part,
                up_part,
                down_spec,
                pl.BlockSpec((HIDDEN, width), lambda j, flags: (early(j), 0)),
                pl.BlockSpec((HIDDEN, width), lambda j, flags: (late(j), 0)),
            ],
            out_specs=[
                tokens,
                tokens,
                pl.BlockSpec((width, HIDDEN), lambda j, flags: (0, early(j))),
                pl.BlockSpec((width, HIDDEN), lambda j, flags: (0, late(j))),
                piece,
            ],
            scratch_shapes=[
                pltpu.VMEM((whole, width), jnp.bfloat16),
                pltpu.VMEM((width, whole), jnp.bfloat16),
                pltpu.VMEM((whole, width), jnp.bfloat16),
                pltpu.VMEM((width, whole), jnp.bfloat16),
                pltpu.VMEM((whole, hidden), jnp.bfloat16),
                pltpu.VMEM((whole, hidden), jnp.bfloat16),
                pltpu.VMEM((width, hidden), jnp.bfloat16),
                pltpu.VMEM((hidden, width), jnp.bfloat16),
            ],
        ),
        out_shape=[wide_bf16, wide_bf16, part, part, pieces],
        compiler_params=pltpu.CompilerParams(vmem_limit_bytes=56 << 20),
        cost_estimate=pl.CostEstimate(
            flops=12 * whole * width * hidden, transcendentals=whole * hidden, bytes_accessed=32 * whole * width
        ),
    )(flags, weight, rows, own, got, cot, gain, shift, up_own, up_near, up_far, down_own, down_near, down_far)


def middle_kernel(
    flags, weight_ref, rows_ref, own_ref, got_ref, cot_ref, back_own, back_got, gain_ref, mixed_ref,
    w_ref, grad_ref, gmixed_ref, gout_ref, sums_ref, turned,
):
    whole, width = rows_ref.shape
    weight = w_ref[...]
    gain = gain_ref[...]
    sums_ref[...] = jnp.zeros_like(sums_ref)

    def body(i, at):
        unit, scale = norm_parts(wide(rows_ref, at) + wide(own_ref, at) + wide(got_ref, at))
        back = wide(back_own, at) + wide(back_got, at)
        inner = back * gain
        mean = jnp.mean(inner, axis=-1, keepdims=True)
        slant = jnp.mean(inner * unit, axis=-1, keepdims=True)
        grad = wide(cot_ref, at) * weight_ref[0] + scale * (inner - mean - unit * slant)
        low = grad.astype(jnp.bfloat16)
        grad_ref[at, :] = low
        turned[:, at] = grad.T.astype(jnp.bfloat16)
        gmixed_ref[at, :] = dot(low, weight, NT).astype(jnp.bfloat16)

        @pl.when((i * ROWS) // (whole // 2) == flags[1])
        def _():
            sums_ref[0:1, :] += jnp.sum(back * unit, axis=0, keepdims=True)
            sums_ref[1:2, :] += jnp.sum(back, axis=0, keepdims=True)

    row_blocks(whole, body)

    def grads(i, at):
        gout_ref[at, :] = dot(turned[at, :], mixed_ref[...]).astype(jnp.bfloat16)

    row_blocks(width, grads)


def middle(flags, weight, rows, own, got, cot, back_own, back_got, gain, mixed, w_out):
    whole, width = rows.shape
    columns = mixed.shape[1]
    tokens = whole_spec((whole, width))
    narrow = whole_spec((whole, columns))
    projection = whole_spec((columns, width))
    return pl.pallas_call(
        middle_kernel,
        grid_spec=pltpu.PrefetchScalarGridSpec(
            num_scalar_prefetch=1,
            grid=(1,),
            in_specs=[pl.BlockSpec(memory_space=pltpu.SMEM)]
            + [tokens] * 6
            + [whole_spec((1, width)), narrow, projection],
            out_specs=[tokens, narrow, whole_spec((width, columns)), whole_spec((8, width))],
            scratch_shapes=[pltpu.VMEM((width, whole), jnp.bfloat16)],
        ),
        out_shape=[
            jax.ShapeDtypeStruct((whole, width), jnp.bfloat16),
            jax.ShapeDtypeStruct((whole, columns), jnp.bfloat16),
            jax.ShapeDtypeStruct((width, columns), jnp.bfloat16),
            jax.ShapeDtypeStruct((8, width), jnp.float32),
        ],
        compiler_params=pltpu.CompilerParams(vmem_limit_bytes=56 << 20),
        cost_estimate=pl.CostEstimate(
            flops=4 * whole * width * columns, transcendentals=0, bytes_accessed=18 * whole * width
        ),
    )(flags, weight, rows, own, got, cot, back_own, back_got, gain, mixed, w_out)


def weigh_kernel(turned_ref, gq_ref, gk_ref, gv_ref, out_ref):
    def grads(i, at):
        for c, ref in enumerate((gq_ref, gk_ref, gv_ref)):
            out_ref[c, at, :] = dot(turned_ref[at, :], ref[...]).astype(jnp.bfloat16)

    row_blocks(turned_ref.shape[0], grads)


def weigh(turned, gq, gk, gv):
    width, whole = turned.shape
    columns = gq.shape[1]
    return pl.pallas_call(
        weigh_kernel,
        out_shape=jax.ShapeDtypeStruct((3, width, columns), jnp.bfloat16),
        compiler_params=pltpu.CompilerParams(vmem_limit_bytes=40 << 20),
        cost_estimate=pl.CostEstimate(
            flops=6 * whole * width * columns, transcendentals=0, bytes_accessed=6 * whole * width
        ),
    )(turned, gq, gk, gv)


def unproject_kernel(flags, gq_ref, gk_ref, gv_ref, weight, keep_ref, send_ref):
    half = keep_ref.shape[0]

    def side(near, out_ref):
        def body(i, at):
            from_rows = pl.ds(pl.multiple_of(near * half + i * ROWS, ROWS), ROWS)
            total = dot(gq_ref[from_rows, :], weight[0], NT)
            total = total + dot(gk_ref[from_rows, :], weight[1], NT)
            total = total + dot(gv_ref[from_rows, :], weight[2], NT)
            out_ref[at, :] = total.astype(out_ref.dtype)

        row_blocks(half, body)

    side(1 - flags[1], send_ref)
    side(flags[1], keep_ref)


def unproject(flags, gq, gk, gv, weight):
    whole, columns = gq.shape
    width = weight.shape[1]
    narrow = whole_spec((whole, columns))
    half = whole_spec((whole // 2, width))
    return pl.pallas_call(
        unproject_kernel,
        grid_spec=pltpu.PrefetchScalarGridSpec(
            num_scalar_prefetch=1,
            grid=(1,),
            in_specs=[narrow, narrow, narrow, whole_spec((3, width, columns))],
            out_specs=[half, half],
        ),
        out_shape=[
            jax.ShapeDtypeStruct((whole // 2, width), jnp.float32),
            jax.ShapeDtypeStruct((whole // 2, width), jnp.bfloat16),
        ],
        compiler_params=pltpu.CompilerParams(vmem_limit_bytes=40 << 20),
        cost_estimate=pl.CostEstimate(
            flops=6 * whole * width * columns, transcendentals=0, bytes_accessed=8 * whole * width
        ),
    )(flags, gq, gk, gv, weight)


def first_norm_kernel(flags, rows_ref, keep_ref, got_ref, resid_ref, gain_ref, out_ref, sums_ref):
    sums_ref[...] = jnp.zeros_like(sums_ref)

    def body(i, at):
        unit, scale = norm_parts(wide(rows_ref, at))
        back = keep_ref[at, :] + wide(got_ref, at)
        inner = back * gain_ref[...]
        mean = jnp.mean(inner, axis=-1, keepdims=True)
        slant = jnp.mean(inner * unit, axis=-1, keepdims=True)
        grad = wide(resid_ref, at) + scale * (inner - mean - unit * slant)
        out_ref[at, :] = grad.astype(jnp.bfloat16)
        sums_ref[0:1, :] += jnp.sum(back * unit, axis=0, keepdims=True)
        sums_ref[1:2, :] += jnp.sum(back, axis=0, keepdims=True)

    row_blocks(rows_ref.shape[0], body)


def first_norm_back(flags, rows, keep, got, resid, gain):
    half, width = keep.shape
    mine = pl.BlockSpec((half, width), lambda i, flags: (flags[1], 0))
    tokens = whole_spec((half, width))
    return pl.pallas_call(
        first_norm_kernel,
        grid_spec=pltpu.PrefetchScalarGridSpec(
            num_scalar_prefetch=1,
            grid=(1,),
            in_specs=[mine, tokens, tokens, mine, whole_spec((1, width))],
            out_specs=[tokens, whole_spec((8, width))],
        ),
        out_shape=[
            jax.ShapeDtypeStruct((half, width), jnp.bfloat16),
            jax.ShapeDtypeStruct((8, width), jnp.float32),
        ],
        compiler_params=pltpu.CompilerParams(vmem_limit_bytes=40 << 20),
        cost_estimate=pl.CostEstimate(flops=20 * half * width, transcendentals=0, bytes_accessed=12 * half * width),
    )(flags, rows, keep, got, resid, gain)


def past_kernel(dwa_ref, hist_ref, cot_ref, grad_ref, part_ref, sums_ref):
    @pl.when(pl.program_id(0) == 0)
    def _():
        sums_ref[...] = jnp.zeros_like(sums_ref)

    grad = cot_ref[...].astype(jnp.float32)
    total = jnp.zeros_like(grad)
    for j in range(hist_ref.shape[0]):
        field = hist_ref[j].astype(jnp.float32)
        total += dwa_ref[j] * field
        grad_ref[j] = (dwa_ref[j] * grad).astype(jnp.bfloat16)
        sums_ref[j : j + 1, :] += jnp.sum(field * grad, axis=0, keepdims=True)
    part_ref[...] = total


def past(dwa, history, cot):
    count, rows, width = history.shape
    layers = pl.BlockSpec((count, ROWS, width), lambda i: (0, i, 0))
    tokens = pl.BlockSpec((ROWS, width), lambda i: (i, 0))
    return pl.pallas_call(
        past_kernel,
        grid=(rows // ROWS,),
        in_specs=[pl.BlockSpec(memory_space=pltpu.SMEM), layers, tokens],
        out_specs=[layers, tokens, whole_spec((8, width))],
        out_shape=[
            jax.ShapeDtypeStruct(history.shape, jnp.bfloat16),
            jax.ShapeDtypeStruct((rows, width), jnp.float32),
            jax.ShapeDtypeStruct((8, width), jnp.float32),
        ],
        compiler_params=pltpu.CompilerParams(vmem_limit_bytes=40 << 20),
        cost_estimate=pl.CostEstimate(
            flops=20 * rows * width, transcendentals=0, bytes_accessed=22 * rows * width
        ),
    )(dwa, history, cot)


def present_kernel(flags, weight_ref, part_ref, cot_ref, own_ref, got_ref, out_ref, sums_ref):
    field = jnp.where(flags[0] == 1, own_ref[...], got_ref[...]).astype(jnp.float32)
    out_ref[...] = (part_ref[...] + weight_ref[0] * field).astype(jnp.bfloat16)
    total = jnp.sum(field * cot_ref[...].astype(jnp.float32), axis=0, keepdims=True)
    sums_ref[...] = jnp.broadcast_to(total, sums_ref.shape)


def present(flags, weight, part, cot, own, got):
    rows, width = part.shape
    scalars = pl.BlockSpec(memory_space=pltpu.SMEM)
    tokens = whole_spec((rows, width))
    return pl.pallas_call(
        present_kernel,
        grid=(1,),
        in_specs=[scalars, scalars] + [tokens] * 4,
        out_specs=[tokens, whole_spec((8, width))],
        out_shape=[
            jax.ShapeDtypeStruct((rows, width), jnp.bfloat16),
            jax.ShapeDtypeStruct((8, width), jnp.float32),
        ],
        compiler_params=pltpu.CompilerParams(vmem_limit_bytes=40 << 20),
        cost_estimate=pl.CostEstimate(
            flops=4 * rows * width, transcendentals=0, bytes_accessed=12 * rows * width
        ),
    )(flags, weight, part, cot, own, got)


AXES = ("tp", "dp", "rep")


def crossing(move):
    tps, dps, reps = (lax.axis_size(name) for name in AXES)
    index = lambda t, d, r: (t * dps + d) * reps + r
    every = [(t, d, r) for t in range(tps) for d in range(dps) for r in range(reps)]
    return [(index(*at), index(*move(*at))) for at in every if at[0] != at[2] % 2]


def swap_diagonal(field):
    return lax.ppermute(field, AXES, crossing(lambda t, d, r: (r % 2, d, r - r % 2 + t)))


def swap_far_crossing(field):
    return lax.ppermute(field, AXES, crossing(lambda t, d, r: (t, d, r ^ 2)))


def swap_near(field):
    return lax.ppermute(field, "rep", [(r, r ^ 1) for r in range(lax.axis_size("rep"))])


def swap_far(field):
    return lax.ppermute(field, "rep", [(r, r ^ 2) for r in range(lax.axis_size("rep"))])


def after(field, *others):
    return lax.optimization_barrier((field, *others))[0]


def ordered(own, other, first, axis=0):
    return jnp.where(
        first, jnp.concatenate([own, other], axis=axis), jnp.concatenate([other, own], axis=axis)
    )


def take(field, index, axis=0):
    return lax.dynamic_index_in_dim(field, index, axis, keepdims=False)


def part_of(field, index, axis):
    size = field.shape[axis] // 2
    return lax.dynamic_slice_in_dim(field, index * size, size, axis)


def add(*fields):
    return sum(field.astype(jnp.float32) for field in fields).astype(jnp.bfloat16)


def move_rows(block):
    dps = lax.axis_size("dp")
    if dps > 8:
        flat = block.reshape(-1, block.shape[2])
        return [lax.psum_scatter(flat, "dp", scatter_dimension=0, tiled=True)]
    place = lax.axis_index("dp")
    moved = [take(block, place)]
    for step in range(1, dps):
        sent = take(block, lax.rem(place + step, dps))
        moved.append(lax.ppermute(sent, "dp", [(d, (d + step) % dps) for d in range(dps)]))
    return moved


def sum_everywhere(field):
    for name in ("rep", "tp", "dp"):
        size = lax.axis_size(name)
        bit = 1
        while bit < size:
            field = field + lax.ppermute(field, name, [(d, d ^ bit) for d in range(size)])
            bit *= 2
    return field


def local(
    layer_input,
    history,
    cotangent,
    lengths,
    dwa_weights,
    gain_one,
    bias_one,
    w_qkv,
    w_out,
    gain_two,
    bias_two,
    w_up,
    w_down,
):
    rows = layer_input.shape[1]
    whole = rows * lax.axis_size("tp")
    hist_count = history.shape[0]
    part, slot = lax.axis_index("tp"), lax.axis_index("rep")
    near, far = slot % 2, slot // 2
    same = near == part
    flags = jnp.stack([same.astype(jnp.int32), near, far])
    own_weight = dwa_weights[hist_count:]

    dps = lax.axis_size("dp")
    input_got = swap_diagonal(layer_input[0])
    qkv_near = swap_diagonal(part_of(w_qkv, far, 1))
    out_near = swap_diagonal(part_of(w_out, far, 0))
    up_near = swap_diagonal(part_of(w_up, far, 0))
    cot_got = swap_diagonal(cotangent[0])
    down_near = swap_diagonal(part_of(w_down, far, 0))
    qkv_far = swap_far_crossing(qkv_near)
    out_far = swap_far_crossing(out_near)
    up_far = swap_far_crossing(up_near)
    down_far = swap_far_crossing(down_near)

    own_lengths = jnp.where(same, lengths, swap_near(lengths))[0]
    seq_owner, token_place = positions(own_lengths, whole)
    seq_begin = jnp.arange(whole, dtype=jnp.int32) - token_place
    start_column = jnp.broadcast_to(seq_begin[:, None], (whole, LANES))
    start_row = jnp.broadcast_to(seq_begin[None, :], (8, whole))
    half_dim = HEAD_DIM // 2
    lane = jnp.arange(LANES, dtype=jnp.int32)
    frequency = jnp.exp((lane % half_dim).astype(jnp.float32) * (-math.log(10000.0) / half_dim))
    angles = token_place.astype(jnp.float32)[:, None] * frequency[None, :]
    cos_table = jnp.cos(angles)
    sin_table = jnp.sin(angles) * jnp.where(lane % HEAD_DIM < half_dim, -1.0, 1.0)[None, :]
    grad_history, past_sum, sums_past = past(dwa_weights, history[:, 0], cotangent[0])

    input_half = jnp.where(same, layer_input[0], input_got)
    layer_rows = ordered(input_half, swap_near(input_half), near == 0)
    layer_rows = after(layer_rows, past_sum, cos_table, sin_table, start_column, start_row)
    gain_one, bias_one = gain_one[None], bias_one[None]
    gain_two, bias_two = gain_two[None], bias_two[None]

    projected, norm_one_t, weight_qkv = project(
        flags, layer_rows, gain_one, bias_one, cos_table, sin_table, w_qkv, qkv_near, qkv_far
    )
    queries, keys, values = projected[0], projected[1], projected[2]
    mixed = attend(start_column, queries, keys, values, LONGEST)
    weight_out = jnp.where(same, w_out, ordered(out_near, out_far, far == 0))
    attn = jnp.dot(mixed, weight_out, preferred_element_type=jnp.float32).astype(jnp.bfloat16)
    attn_got = swap_near(attn)
    cot_half = jnp.where(same, cotangent[0], after(cot_got, mixed))
    cot_rows = ordered(cot_half, swap_near(cot_half), near == 0)
    down, back, up_keep, up_send, grad_down = feed(
        flags,
        own_weight,
        layer_rows,
        attn,
        attn_got,
        cot_rows,
        gain_two,
        bias_two,
        w_up,
        up_near,
        up_far,
        w_down,
        down_near,
        down_far,
    )
    back_got = swap_near(back)
    up_got = swap_far(up_send)
    down_got = swap_diagonal(grad_down)
    grad_attn, grad_mixed, grad_out, sums_two = middle(
        flags,
        own_weight,
        layer_rows,
        attn,
        attn_got,
        cot_rows,
        back,
        back_got,
        gain_two,
        mixed,
        weight_out,
    )
    grad_queries, grad_keys, grad_values = attend_back(
        start_row, cos_table, sin_table, queries, keys, values, grad_mixed, LONGEST
    )

    def columns_of(pieces):
        return pieces.transpose(1, 0, 2).reshape(pieces.shape[1], -1)

    def by_dp(block):
        return block.reshape(dps, block.shape[0] // dps, block.shape[1])

    up_pair = add(up_keep, after(up_got, grad_keys))
    up_moved = swap_diagonal(up_pair)
    down_pair = jnp.where(same, grad_down, after(down_got, grad_keys))
    down_other = swap_near(take(down_pair, 1 - near))
    grad_qkv = weigh(norm_one_t, grad_queries, grad_keys, grad_values)
    mine = take(grad_qkv, far)
    attn_got_far = swap_far(take(grad_qkv, 1 - far))
    late_pieces = jnp.stack([grad_qkv[2], grad_out])
    late_got = swap_diagonal(late_pieces)
    keep, send = unproject(flags, grad_queries, grad_keys, grad_values, weight_qkv)
    send_got = swap_near(send)
    down_one = add(take(down_pair, near), after(down_other, grad_qkv))
    down_blocks = move_rows(by_dp(down_one))
    input_grad, sums_one = first_norm_back(flags, layer_rows, keep, send_got, grad_attn, gain_one)
    grad_input = swap_diagonal(input_grad)
    up_pair = jnp.where(same, up_pair, after(up_moved, grad_qkv))
    up_one = add(part_of(up_pair, near, 1), swap_near(part_of(up_pair, 1 - near, 1)))
    up_blocks = move_rows(by_dp(up_one))

    def half_of(field, index):
        return lax.dynamic_slice_in_dim(field, index * rows, rows, 0)

    down_half = after(half_of(down, 1 - near), input_grad)
    block_half = add(
        *[half_of(field, near) for field in (layer_rows, attn, attn_got, down)], swap_near(down_half)
    )
    output, sums_now = present(
        flags, own_weight, past_sum, cotangent[0], block_half, swap_diagonal(block_half)
    )
    small = jnp.concatenate(
        [sums_one[:2], sums_two[:2], sums_past[:hist_count], sums_now[:1]], axis=0
    )
    small = sum_everywhere(small)

    key_pair = add(mine, attn_got_far)
    key_pair = by_dp(jnp.where(same, key_pair, swap_diagonal(key_pair)))
    key_one = add(part_of(key_pair, near, 1), swap_near(part_of(key_pair, 1 - near, 1)))
    late_pair = jnp.where(same, late_pieces, late_got)
    late_one = add(take(late_pair, near), swap_near(take(late_pair, 1 - near)))
    late_sum = add(*move_rows(by_dp(late_one)))
    key_sum = add(*move_rows(key_one))
    late_sum = add(late_sum, swap_far(late_sum))
    grad_value_out = ordered(late_sum[None], swap_near(late_sum)[None], near == 0)
    key_half = ordered(key_sum, swap_near(key_sum), near == 0)
    grad_query_key = ordered(key_half[None], swap_far(key_half)[None], far == 0)

    down_sum = add(*down_blocks)
    down_sum = add(down_sum, swap_far(down_sum))
    grad_w_down = ordered(down_sum[None], swap_near(down_sum)[None], near == 0)
    up_sum = add(*up_blocks)
    up_half = ordered(up_sum, swap_near(up_sum), near == 0, axis=1)
    grad_w_up = ordered(up_half[None], swap_far(up_half)[None], far == 0)
    grad_w_qkv = jnp.concatenate([grad_query_key, grad_value_out[:1]], axis=0)

    return (
        output[None],
        jnp.where(same, input_grad, grad_input)[None],
        grad_history[:, None],
        jnp.sum(small[4:], axis=1),
        small[0],
        small[1],
        grad_w_qkv.astype(jnp.float32),
        grad_value_out[1].astype(jnp.float32).T,
        small[2],
        small[3],
        columns_of(grad_w_up).astype(jnp.float32),
        columns_of(grad_w_down).astype(jnp.float32).T,
    )


def positions(seq_lengths, token_count):
    seq_ends = jnp.cumsum(seq_lengths)
    seq_starts = seq_ends - seq_lengths
    token_index = jnp.arange(token_count, dtype=jnp.int32)
    seq_owner = jnp.sum((token_index[:, None] >= seq_ends[None, :]).astype(jnp.int32), axis=1)
    picked = (
        seq_owner[:, None] == jnp.arange(seq_lengths.shape[0], dtype=jnp.int32)[None, :]
    ).astype(jnp.int32)
    seq_begin = jnp.sum(picked * seq_starts[None, :], axis=1)
    return (seq_owner, token_index - seq_begin)


def solution(mesh):
    in_specs = (
        P(("dp", "rep"), "tp", None),
        P(None, ("dp", "rep"), "tp", None),
        P(("dp", "rep"), "tp", None),
        P(("dp", "rep"), None),
        P(),
        P(),
        P(),
        P(None, None, "tp"),
        P("tp", None),
        P(),
        P(),
        P(None, "tp"),
        P("tp", None),
    )
    out_specs = (
        P(("dp", "rep"), "tp", None),
        P(("dp", "rep"), "tp", None),
        P(None, ("dp", "rep"), "tp", None),
        P(),
        P(),
        P(),
        P(None, "dp", "tp"),
        P("tp", "dp"),
        P(),
        P(),
        P("dp", "tp"),
        P("tp", "dp"),
    )
    return jax.shard_map(local, mesh=mesh, in_specs=in_specs, out_specs=out_specs, check_vma=False)
```

```python
import functools
import math

import jax
import jax.numpy as jnp
from jax import lax
from jax.experimental import pallas as pl
from jax.experimental.pallas import tpu as pltpu
from jax.sharding import PartitionSpec as P

HEAD_DIM = 64
LONGEST = 512
NEG_FILL = -1e30
NORM_EPS = 1e-05
BLOCK = 256
LANES = 128
NT = (((1,), (1,)), ((), ()))


def dot(a, b, dims=(((1,), (0,)), ((), ()))):
    return lax.dot_general(a, b, dims, preferred_element_type=jnp.float32)


def spans(whole, reach):
    back = -(-(reach - 1) // BLOCK)
    runs = []
    for i in range(whole // BLOCK):
        count = min(i, back) + 1
        if runs and runs[-1][2] == count:
            runs[-1][1] = i + 1
        else:
            runs.append([i, i + 1, count])
    return runs


def each_block(whole, reach, body):
    for first, last, count in spans(whole, reach):
        def step(at, carry, first=first, count=count):
            i = first + at // 2
            body(i, i + 1 - count, count * BLOCK, at % 2)
            return carry
        lax.fori_loop(0, 2 * (last - first), step, 0)


def attend_kernel(reach, start_ref, q_ref, k_ref, v_ref, out_ref, acc_ref):
    whole = q_ref.shape[0]
    lane = lax.broadcasted_iota(jnp.int32, (BLOCK, LANES), 1) // HEAD_DIM

    def body(i, first, count, head):
        at = pl.ds(pl.multiple_of(i * BLOCK, BLOCK), BLOCK)
        keys = pl.ds(pl.multiple_of(first * BLOCK, BLOCK), count)
        query = q_ref[at, :] * (HEAD_DIM**-0.5)
        query = jnp.where(lane == head, query, jnp.zeros_like(query))
        scores = dot(query, k_ref[keys, :], NT)
        key_at = first * BLOCK + lax.broadcasted_iota(jnp.int32, scores.shape, 1)
        query_at = i * BLOCK + lax.broadcasted_iota(jnp.int32, scores.shape, 0)
        allowed = (key_at >= start_ref[at, :1]) & (key_at <= query_at)
        scores = jnp.where(allowed, scores, NEG_FILL)
        exponent = jnp.exp(scores - jnp.max(scores, axis=1, keepdims=True))
        row_sum = jnp.sum(exponent, axis=1, keepdims=True)
        probs = (exponent * (1.0 / row_sum)).astype(jnp.bfloat16)
        mixed = dot(probs, v_ref[keys, :])

        @pl.when(head == 0)
        def _():
            acc_ref[...] = mixed

        @pl.when(head == 1)
        def _():
            out_ref[at, :] = jnp.where(lane == 0, acc_ref[...], mixed).astype(out_ref.dtype)

    each_block(whole, reach, body)


def attend(pair, start_column, projected, so_far, reach):
    count, whole, width = projected.shape

    def block(c):
        return pl.BlockSpec((None, whole, LANES), lambda i: (c, 0, pair))

    begun = [] if so_far is None else [so_far]
    kernel = attend_kernel if so_far is None else lambda reach, unused, *refs: attend_kernel(reach, *refs)
    return pl.pallas_call(
        functools.partial(kernel, reach),
        grid=(1,),
        in_specs=[pl.BlockSpec(memory_space=pl.ANY)] * len(begun)
        + [pl.BlockSpec((whole, LANES), lambda i: (0, 0)), block(0), block(1), block(2)],
        out_specs=pl.BlockSpec((whole, LANES), lambda i: (0, pair)),
        out_shape=jax.ShapeDtypeStruct((whole, width), jnp.bfloat16),
        scratch_shapes=[pltpu.VMEM((BLOCK, LANES), jnp.float32)],
        input_output_aliases={0: 0} if begun else {},
        compiler_params=pltpu.CompilerParams(vmem_limit_bytes=40 << 20),
        cost_estimate=pl.CostEstimate(
            flops=4 * whole * LANES * 640, transcendentals=whole * 640 * 2, bytes_accessed=8 * whole * LANES
        ),
    )(*begun, start_column, projected, projected, projected)


def turn_back(field, cos, sin):
    half = HEAD_DIM // 2
    lane = lax.broadcasted_iota(jnp.int32, field.shape, 1) % HEAD_DIM
    crossed = jnp.where(lane < half, pltpu.roll(field, LANES - half, 1), pltpu.roll(field, half, 1))
    return field * cos - crossed * sin


def attend_back_kernel(
    reach, start_ref, cos_ref, sin_ref, q_ref, k_ref, v_ref, g_ref, out_ref,
    key_acc, value_acc, query_acc,
):
    whole = q_ref.shape[0]
    lane = lax.broadcasted_iota(jnp.int32, (BLOCK, LANES), 1) // HEAD_DIM
    key_acc[...] = jnp.zeros_like(key_acc)
    value_acc[...] = jnp.zeros_like(value_acc)

    def body(i, first, count, head):
        at = pl.ds(pl.multiple_of(i * BLOCK, BLOCK), BLOCK)
        span = pl.ds(pl.multiple_of(first * BLOCK, BLOCK), count)
        query = q_ref[at, :] * (HEAD_DIM**-0.5)
        query = jnp.where(lane == head, query, jnp.zeros_like(query))
        grad = g_ref[at, :]
        grad = jnp.where(lane == head, grad, jnp.zeros_like(grad))
        keys = k_ref[span, :]
        scores = dot(keys, query, NT)
        key_at = first * BLOCK + lax.broadcasted_iota(jnp.int32, scores.shape, 0)
        query_at = i * BLOCK + lax.broadcasted_iota(jnp.int32, scores.shape, 1)
        allowed = (key_at >= start_ref[:1, at]) & (key_at <= query_at)
        scores = jnp.where(allowed, scores, NEG_FILL)
        exponent = jnp.exp(scores - jnp.max(scores, axis=0, keepdims=True))
        probs = exponent * (1.0 / jnp.sum(exponent, axis=0, keepdims=True))
        value_acc[span, :] += dot(probs.astype(jnp.bfloat16), grad)
        grad_probs = dot(v_ref[span, :], grad, NT)
        weighted = probs * grad_probs
        grad_scores = (weighted - probs * jnp.sum(weighted, axis=0, keepdims=True)).astype(jnp.bfloat16)
        key_acc[span, :] += dot(grad_scores, query)
        here = dot(grad_scores, keys, (((0,), (0,)), ((), ())))

        @pl.when(head == 0)
        def _():
            query_acc[...] = here

        @pl.when(head == 1)
        def _():
            both = jnp.where(lane == 0, query_acc[...], here) * (HEAD_DIM**-0.5)
            out_ref[0, at, :] = turn_back(both, cos_ref[at, :], sin_ref[at, :]).astype(out_ref.dtype)

    each_block(whole, reach, body)

    def finish(i, carry):
        at = pl.ds(pl.multiple_of(i * BLOCK, BLOCK), BLOCK)
        out_ref[1, at, :] = turn_back(key_acc[at, :], cos_ref[at, :], sin_ref[at, :]).astype(out_ref.dtype)
        out_ref[2, at, :] = value_acc[at, :].astype(out_ref.dtype)
        return carry

    lax.fori_loop(0, whole // BLOCK, finish, 0)


def attend_back(pair, start_row, cos, sin, projected, grad_mixed, so_far, reach):
    count, whole, width = projected.shape

    def block(c):
        return pl.BlockSpec((None, whole, LANES), lambda i: (c, 0, pair))

    table = pl.BlockSpec((whole, LANES), lambda i: (0, 0))
    begun = [] if so_far is None else [so_far]
    kernel = attend_back_kernel if so_far is None else lambda reach, unused, *refs: attend_back_kernel(reach, *refs)
    return pl.pallas_call(
        functools.partial(kernel, reach),
        grid=(1,),
        in_specs=[pl.BlockSpec(memory_space=pl.ANY)] * len(begun)
        + [
            pl.BlockSpec((8, whole), lambda i: (0, 0)),
            table,
            table,
            block(0),
            block(1),
            block(2),
            pl.BlockSpec((whole, LANES), lambda i: (0, pair)),
        ],
        out_specs=pl.BlockSpec((count, whole, LANES), lambda i: (0, 0, pair)),
        out_shape=jax.ShapeDtypeStruct((count, whole, width), jnp.bfloat16),
        scratch_shapes=[
            pltpu.VMEM((whole, LANES), jnp.float32),
            pltpu.VMEM((whole, LANES), jnp.float32),
            pltpu.VMEM((BLOCK, LANES), jnp.float32),
        ],
        input_output_aliases={0: 0} if begun else {},
        compiler_params=pltpu.CompilerParams(vmem_limit_bytes=40 << 20),
        cost_estimate=pl.CostEstimate(
            flops=10 * whole * LANES * 640, transcendentals=whole * 640 * 2, bytes_accessed=14 * whole * LANES
        ),
    )(*begun, start_row, cos, sin, projected, projected, projected, grad_mixed)


ROWS = 256


def norm_parts(field):
    centered = field - jnp.mean(field, axis=-1, keepdims=True)
    scale = lax.rsqrt(jnp.mean(centered * centered, axis=-1, keepdims=True) + NORM_EPS)
    return centered * scale, scale


def wide(ref, at):
    return ref[at, :].astype(jnp.float32)


def row_blocks(count, body):
    def step(i, carry):
        body(i, pl.ds(pl.multiple_of(i * ROWS, ROWS), ROWS))
        return carry

    lax.fori_loop(0, count // ROWS, step, 0)


def whole_spec(shape):
    return pl.BlockSpec(shape, lambda *at: (0,) * len(shape))


def turn(field, cos, sin):
    half = HEAD_DIM // 2
    lane = lax.broadcasted_iota(jnp.int32, field.shape, 1) % HEAD_DIM
    crossed = jnp.where(lane < half, pltpu.roll(field, LANES - half, 1), pltpu.roll(field, half, 1))
    return field * cos + crossed * sin


def project_kernel(
    flags, rows_ref, gain_ref, shift_ref, cos_ref, sin_ref, w_own, w_got, out_ref, turned_ref,
    weight_ref, norm_ref,
):
    whole = rows_ref.shape[0]
    step = pl.program_id(0)

    @pl.when(step == 0)
    def _():
        def body(i, at):
            unit, unused = norm_parts(wide(rows_ref, at))
            norm = unit * gain_ref[...] + shift_ref[...]
            norm_ref[at, :] = norm.astype(jnp.bfloat16)
            turned_ref[:, at] = norm.T.astype(jnp.bfloat16)

        row_blocks(whole, body)

    weight_ref[0] = jnp.where(flags[0] == 1, w_own[0], w_got[0])

    def body(i, at):
        field = dot(norm_ref[at, :], weight_ref[0])

        @pl.when(step < 2)
        def _():
            for p in range(field.shape[1] // LANES):
                lanes = slice(p * LANES, (p + 1) * LANES)
                out_ref[0, at, lanes] = turn(field[:, lanes], cos_ref[at, :], sin_ref[at, :]).astype(
                    jnp.bfloat16
                )

        @pl.when(step == 2)
        def _():
            out_ref[0, at, :] = field.astype(jnp.bfloat16)

    row_blocks(whole, body)


def project(flags, rows, gain, shift, cos, sin, w_own, w_got):
    whole, width = rows.shape
    count, unused, columns = w_own.shape
    weight = pl.BlockSpec((1, width, columns), lambda c, flags: (c, 0, 0))
    return pl.pallas_call(
        project_kernel,
        grid_spec=pltpu.PrefetchScalarGridSpec(
            num_scalar_prefetch=1,
            grid=(count,),
            in_specs=[
                whole_spec((whole, width)),
                whole_spec((1, width)),
                whole_spec((1, width)),
                whole_spec((whole, LANES)),
                whole_spec((whole, LANES)),
                weight,
                weight,
            ],
            out_specs=[
                pl.BlockSpec((1, whole, columns), lambda c, flags: (c, 0, 0)),
                whole_spec((width, whole)),
                weight,
            ],
            scratch_shapes=[pltpu.VMEM((whole, width), jnp.bfloat16)],
        ),
        out_shape=[
            jax.ShapeDtypeStruct((count, whole, columns), jnp.bfloat16),
            jax.ShapeDtypeStruct((width, whole), jnp.bfloat16),
            jax.ShapeDtypeStruct(w_own.shape, jnp.bfloat16),
        ],
        compiler_params=pltpu.CompilerParams(vmem_limit_bytes=40 << 20),
        cost_estimate=pl.CostEstimate(
            flops=2 * whole * width * columns * count,
            transcendentals=0,
            bytes_accessed=12 * whole * width,
        ),
    )(flags, rows, gain, shift, cos, sin, w_own, w_got)


HIDDEN = 256


def gelu_both(up):
    root = math.sqrt(2.0 / math.pi)
    square = up * up
    bent = jnp.tanh(root * up * (1.0 + 0.044715 * square))
    half = 0.5 * (1.0 + bent)
    slope = half + 0.5 * up * (1.0 - bent * bent) * (root * (1.0 + 3.0 * 0.044715 * square))
    return up * half, slope


def feed_kernel(early, flags, *refs):
    if early:
        weight_ref, rows_ref, own_ref, got_ref, cot_ref, gain_ref, shift_ref = refs[:7]
        refs = refs[7:]
        up_own, up_got, down_own, down_got, norm, norm_t, grad, grad_t = refs[:8]
    else:
        norm, norm_t, grad, grad_t, back_early, up_own, up_got, down_own, down_got = refs[:9]
    back_ref, act_ref, gup_ref, gdown_ref, slope, up_w = refs[-6:]
    whole, width = norm.shape
    step = pl.program_id(0)

    if early:

        @pl.when(step == 0)
        def _():
            def body(i, at):
                unit, unused = norm_parts(wide(rows_ref, at) + wide(own_ref, at) + wide(got_ref, at))
                field = unit * gain_ref[...] + shift_ref[...]
                norm[at, :] = field.astype(jnp.bfloat16)
                norm_t[:, at] = field.T.astype(jnp.bfloat16)
                field = wide(cot_ref, at) * weight_ref[0]
                grad[at, :] = field.astype(jnp.bfloat16)
                grad_t[:, at] = field.T.astype(jnp.bfloat16)

            row_blocks(whole, body)

    hidden = pl.ds(pl.multiple_of(step * HIDDEN, HIDDEN), HIDDEN)
    up_w[:, hidden] = jnp.where(flags[0] == 1, up_own[...], up_got[...])
    up_block = up_w[:, hidden]
    down_block = jnp.where(flags[0] == 1, down_own[...], down_got[...])

    def body(i, at):
        value, rise = gelu_both(dot(norm[at, :], up_block))
        act_ref[at, :] = value.astype(jnp.bfloat16)
        slope[at, hidden] = (dot(grad[at, :], down_block, NT) * rise).astype(jnp.bfloat16)

    row_blocks(whole, body)

    def grads(i, at):
        gdown_ref[at, :] = dot(grad_t[at, :], act_ref[...]).astype(jnp.bfloat16)
        gup_ref[at, :] = dot(norm_t[at, :], slope[:, hidden]).astype(jnp.bfloat16)

    row_blocks(width, grads)

    @pl.when(step == pl.num_programs(0) - 1)
    def _():
        def body(i, at):
            back = dot(slope[at, :], up_w[...], NT)
            if not early:
                back = back + back_early[at, :]
            back_ref[at, :] = back.astype(back_ref.dtype)

        row_blocks(whole, body)


def feed(early, flags, head, up_own, up_got, down_own, down_got):
    whole, width = head[1].shape if early else head[0].shape
    hidden = up_got.shape[1]
    steps = hidden // HIDDEN
    tokens = whole_spec((whole, width))
    turned = whole_spec((width, whole))
    vector = whole_spec((1, width))

    def at(j, flags):
        return ((1 - flags[2]) if early else flags[2]) * steps + j

    low = jax.ShapeDtypeStruct((whole, width), jnp.bfloat16)
    low_turned = jax.ShapeDtypeStruct((width, whole), jnp.bfloat16)
    full = jax.ShapeDtypeStruct((whole, width), jnp.float32)
    piece = jax.ShapeDtypeStruct((width, hidden), jnp.bfloat16)
    if early:
        head_specs = [pl.BlockSpec(memory_space=pltpu.SMEM)] + [tokens] * 4 + [vector] * 2
    else:
        head_specs = [tokens, turned, tokens, turned, tokens]
    block = pl.BlockSpec((width, HIDDEN), lambda j, flags: (0, j))
    return pl.pallas_call(
        functools.partial(feed_kernel, early),
        grid_spec=pltpu.PrefetchScalarGridSpec(
            num_scalar_prefetch=1,
            grid=(steps,),
            in_specs=head_specs
            + [
                pl.BlockSpec((width, HIDDEN), lambda j, flags: (0, at(j, flags))),
                block,
                pl.BlockSpec((HIDDEN, width), lambda j, flags: (at(j, flags), 0)),
                pl.BlockSpec((HIDDEN, width), lambda j, flags: (j, 0)),
            ],
            out_specs=([tokens, turned, tokens, turned] if early else [])
            + [tokens, pl.BlockSpec((whole, HIDDEN), lambda j, flags: (0, j)), block, block],
            scratch_shapes=[
                pltpu.VMEM((whole, hidden), jnp.bfloat16),
                pltpu.VMEM((width, hidden), jnp.bfloat16),
            ],
        ),
        out_shape=([low, low_turned, low, low_turned, full] if early else [low])
        + [jax.ShapeDtypeStruct((whole, hidden), jnp.bfloat16), piece, piece],
        compiler_params=pltpu.CompilerParams(vmem_limit_bytes=56 << 20),
        cost_estimate=pl.CostEstimate(
            flops=10 * whole * width * hidden,
            transcendentals=whole * hidden,
            bytes_accessed=24 * whole * width,
        ),
    )(flags, *head, up_own, up_got, down_own, down_got)


def lower_kernel(flags, act_early, act_late, own_early, got_early, own_late, got_late, rows_ref, own_ref, got_ref, keep_ref, send_ref):
    half = keep_ref.shape[0]
    same = flags[0] == 1
    first = jnp.where(same, own_early[...], got_early[...])
    second = jnp.where(same, own_late[...], got_late[...])

    def at_rows(near, i):
        return pl.ds(pl.multiple_of(near * half + i * ROWS, ROWS), ROWS)

    def send(i, at):
        here = at_rows(1 - flags[1], i)
        total = dot(act_early[here, :], first) + dot(act_late[here, :], second)
        send_ref[at, :] = total.astype(jnp.bfloat16)

    def keep(i, at):
        here = at_rows(flags[1], i)
        total = dot(act_early[here, :], first) + dot(act_late[here, :], second)
        keep_ref[at, :] = total + wide(rows_ref, here) + wide(own_ref, here) + wide(got_ref, here)

    row_blocks(half, send)
    row_blocks(half, keep)


def lower(flags, act_early, act_late, down_own, got_early, got_late, rows, own, got):
    whole, hidden = act_early.shape
    width = rows.shape[1]
    tokens = whole_spec((whole, width))
    half = whole_spec((whole // 2, width))
    piece = whole_spec((hidden, width))
    return pl.pallas_call(
        lower_kernel,
        grid_spec=pltpu.PrefetchScalarGridSpec(
            num_scalar_prefetch=1,
            grid=(1,),
            in_specs=[
                whole_spec((whole, hidden)),
                whole_spec((whole, hidden)),
                pl.BlockSpec((hidden, width), lambda i, flags: (1 - flags[2], 0)),
                piece,
                pl.BlockSpec((hidden, width), lambda i, flags: (flags[2], 0)),
                piece,
                tokens,
                tokens,
                tokens,
            ],
            out_specs=[half, half],
        ),
        out_shape=[
            jax.ShapeDtypeStruct((whole // 2, width), jnp.float32),
            jax.ShapeDtypeStruct((whole // 2, width), jnp.bfloat16),
        ],
        compiler_params=pltpu.CompilerParams(vmem_limit_bytes=56 << 20),
        cost_estimate=pl.CostEstimate(
            flops=4 * whole * width * hidden, transcendentals=0, bytes_accessed=18 * whole * width
        ),
    )(flags, act_early, act_late, down_own, got_early, down_own, got_late, rows, own, got)


def middle_kernel(
    flags, weight_ref, rows_ref, own_ref, got_ref, cot_ref, back_own, back_got, gain_ref, mixed_ref,
    w_ref, grad_ref, gmixed_ref, gout_ref, sums_ref, turned,
):
    whole, width = rows_ref.shape
    weight = w_ref[...]
    gain = gain_ref[...]
    sums_ref[...] = jnp.zeros_like(sums_ref)

    def body(i, at):
        unit, scale = norm_parts(wide(rows_ref, at) + wide(own_ref, at) + wide(got_ref, at))
        back = wide(back_own, at) + wide(back_got, at)
        inner = back * gain
        mean = jnp.mean(inner, axis=-1, keepdims=True)
        slant = jnp.mean(inner * unit, axis=-1, keepdims=True)
        grad = wide(cot_ref, at) * weight_ref[0] + scale * (inner - mean - unit * slant)
        low = grad.astype(jnp.bfloat16)
        grad_ref[at, :] = low
        turned[:, at] = grad.T.astype(jnp.bfloat16)
        gmixed_ref[at, :] = dot(low, weight, NT).astype(jnp.bfloat16)

        @pl.when((i * ROWS) // (whole // 2) == flags[1])
        def _():
            sums_ref[0:1, :] += jnp.sum(back * unit, axis=0, keepdims=True)
            sums_ref[1:2, :] += jnp.sum(back, axis=0, keepdims=True)

    row_blocks(whole, body)

    def grads(i, at):
        gout_ref[at, :] = dot(turned[at, :], mixed_ref[...]).astype(jnp.bfloat16)

    row_blocks(width, grads)


def middle(flags, weight, rows, own, got, cot, back_own, back_got, gain, mixed, w_out):
    whole, width = rows.shape
    columns = mixed.shape[1]
    tokens = whole_spec((whole, width))
    narrow = whole_spec((whole, columns))
    projection = whole_spec((columns, width))
    return pl.pallas_call(
        middle_kernel,
        grid_spec=pltpu.PrefetchScalarGridSpec(
            num_scalar_prefetch=1,
            grid=(1,),
            in_specs=[pl.BlockSpec(memory_space=pltpu.SMEM)]
            + [tokens] * 6
            + [whole_spec((1, width)), narrow, projection],
            out_specs=[tokens, narrow, whole_spec((width, columns)), whole_spec((8, width))],
            scratch_shapes=[pltpu.VMEM((width, whole), jnp.bfloat16)],
        ),
        out_shape=[
            jax.ShapeDtypeStruct((whole, width), jnp.bfloat16),
            jax.ShapeDtypeStruct((whole, columns), jnp.bfloat16),
            jax.ShapeDtypeStruct((width, columns), jnp.bfloat16),
            jax.ShapeDtypeStruct((8, width), jnp.float32),
        ],
        compiler_params=pltpu.CompilerParams(vmem_limit_bytes=56 << 20),
        cost_estimate=pl.CostEstimate(
            flops=4 * whole * width * columns, transcendentals=0, bytes_accessed=18 * whole * width
        ),
    )(flags, weight, rows, own, got, cot, back_own, back_got, gain, mixed, w_out)


def weigh_kernel(turned_ref, grad_ref, out_ref):
    def grads(i, at):
        for c in range(grad_ref.shape[0]):
            out_ref[c, at, :] = dot(turned_ref[at, :], grad_ref[c]).astype(jnp.bfloat16)

    row_blocks(turned_ref.shape[0], grads)


def weigh(turned, grad):
    width, whole = turned.shape
    columns = grad.shape[2]
    return pl.pallas_call(
        weigh_kernel,
        out_shape=jax.ShapeDtypeStruct((3, width, columns), jnp.bfloat16),
        compiler_params=pltpu.CompilerParams(vmem_limit_bytes=40 << 20),
        cost_estimate=pl.CostEstimate(
            flops=6 * whole * width * columns, transcendentals=0, bytes_accessed=6 * whole * width
        ),
    )(turned, grad)


def unproject_kernel(flags, grad_ref, weight, keep_ref, send_ref):
    half = keep_ref.shape[0]

    def side(near, out_ref):
        def body(i, at):
            from_rows = pl.ds(pl.multiple_of(near * half + i * ROWS, ROWS), ROWS)
            total = dot(grad_ref[0, from_rows, :], weight[0], NT)
            for c in range(1, grad_ref.shape[0]):
                total = total + dot(grad_ref[c, from_rows, :], weight[c], NT)
            out_ref[at, :] = total.astype(out_ref.dtype)

        row_blocks(half, body)

    side(1 - flags[1], send_ref)
    side(flags[1], keep_ref)


def unproject(flags, grad, weight):
    count, whole, columns = grad.shape
    width = weight.shape[1]
    half = whole_spec((whole // 2, width))
    return pl.pallas_call(
        unproject_kernel,
        grid_spec=pltpu.PrefetchScalarGridSpec(
            num_scalar_prefetch=1,
            grid=(1,),
            in_specs=[whole_spec(grad.shape), whole_spec((count, width, columns))],
            out_specs=[half, half],
        ),
        out_shape=[
            jax.ShapeDtypeStruct((whole // 2, width), jnp.float32),
            jax.ShapeDtypeStruct((whole // 2, width), jnp.bfloat16),
        ],
        compiler_params=pltpu.CompilerParams(vmem_limit_bytes=40 << 20),
        cost_estimate=pl.CostEstimate(
            flops=6 * whole * width * columns, transcendentals=0, bytes_accessed=8 * whole * width
        ),
    )(flags, grad, weight)


def first_norm_kernel(flags, rows_ref, keep_ref, got_ref, resid_ref, gain_ref, out_ref, sums_ref):
    sums_ref[...] = jnp.zeros_like(sums_ref)

    def body(i, at):
        unit, scale = norm_parts(wide(rows_ref, at))
        back = keep_ref[at, :] + wide(got_ref, at)
        inner = back * gain_ref[...]
        mean = jnp.mean(inner, axis=-1, keepdims=True)
        slant = jnp.mean(inner * unit, axis=-1, keepdims=True)
        grad = wide(resid_ref, at) + scale * (inner - mean - unit * slant)
        out_ref[at, :] = grad.astype(jnp.bfloat16)
        sums_ref[0:1, :] += jnp.sum(back * unit, axis=0, keepdims=True)
        sums_ref[1:2, :] += jnp.sum(back, axis=0, keepdims=True)

    row_blocks(rows_ref.shape[0], body)


def first_norm_back(flags, rows, keep, got, resid, gain):
    half, width = keep.shape
    mine = pl.BlockSpec((half, width), lambda i, flags: (flags[1], 0))
    tokens = whole_spec((half, width))
    return pl.pallas_call(
        first_norm_kernel,
        grid_spec=pltpu.PrefetchScalarGridSpec(
            num_scalar_prefetch=1,
            grid=(1,),
            in_specs=[mine, tokens, tokens, mine, whole_spec((1, width))],
            out_specs=[tokens, whole_spec((8, width))],
        ),
        out_shape=[
            jax.ShapeDtypeStruct((half, width), jnp.bfloat16),
            jax.ShapeDtypeStruct((8, width), jnp.float32),
        ],
        compiler_params=pltpu.CompilerParams(vmem_limit_bytes=40 << 20),
        cost_estimate=pl.CostEstimate(flops=20 * half * width, transcendentals=0, bytes_accessed=12 * half * width),
    )(flags, rows, keep, got, resid, gain)


def past_kernel(dwa_ref, hist_ref, cot_ref, grad_ref, part_ref, sums_ref):
    @pl.when(pl.program_id(0) == 0)
    def _():
        sums_ref[...] = jnp.zeros_like(sums_ref)

    grad = cot_ref[...].astype(jnp.float32)
    total = jnp.zeros_like(grad)
    for j in range(hist_ref.shape[0]):
        field = hist_ref[j].astype(jnp.float32)
        total += dwa_ref[j] * field
        grad_ref[j] = (dwa_ref[j] * grad).astype(jnp.bfloat16)
        sums_ref[j : j + 1, :] += jnp.sum(field * grad, axis=0, keepdims=True)
    part_ref[...] = total


def past(dwa, history, cot):
    count, rows, width = history.shape
    layers = pl.BlockSpec((count, ROWS, width), lambda i: (0, i, 0))
    tokens = pl.BlockSpec((ROWS, width), lambda i: (i, 0))
    return pl.pallas_call(
        past_kernel,
        grid=(rows // ROWS,),
        in_specs=[pl.BlockSpec(memory_space=pltpu.SMEM), layers, tokens],
        out_specs=[layers, tokens, whole_spec((8, width))],
        out_shape=[
            jax.ShapeDtypeStruct(history.shape, jnp.bfloat16),
            jax.ShapeDtypeStruct((rows, width), jnp.float32),
            jax.ShapeDtypeStruct((8, width), jnp.float32),
        ],
        compiler_params=pltpu.CompilerParams(vmem_limit_bytes=40 << 20),
        cost_estimate=pl.CostEstimate(
            flops=20 * rows * width, transcendentals=0, bytes_accessed=22 * rows * width
        ),
    )(dwa, history, cot)


def present_kernel(flags, weight_ref, part_ref, cot_ref, own_ref, got_ref, out_ref, sums_ref):
    field = jnp.where(flags[0] == 1, own_ref[...], got_ref[...]).astype(jnp.float32)
    out_ref[...] = (part_ref[...] + weight_ref[0] * field).astype(jnp.bfloat16)
    total = jnp.sum(field * cot_ref[...].astype(jnp.float32), axis=0, keepdims=True)
    sums_ref[...] = jnp.broadcast_to(total, sums_ref.shape)


def present(flags, weight, part, cot, own, got):
    rows, width = part.shape
    scalars = pl.BlockSpec(memory_space=pltpu.SMEM)
    tokens = whole_spec((rows, width))
    return pl.pallas_call(
        present_kernel,
        grid=(1,),
        in_specs=[scalars, scalars] + [tokens] * 4,
        out_specs=[tokens, whole_spec((8, width))],
        out_shape=[
            jax.ShapeDtypeStruct((rows, width), jnp.bfloat16),
            jax.ShapeDtypeStruct((8, width), jnp.float32),
        ],
        compiler_params=pltpu.CompilerParams(vmem_limit_bytes=40 << 20),
        cost_estimate=pl.CostEstimate(
            flops=4 * rows * width, transcendentals=0, bytes_accessed=12 * rows * width
        ),
    )(flags, weight, part, cot, own, got)


AXES = ("tp", "dp", "rep")


def crossing(move):
    tps, dps, reps = (lax.axis_size(name) for name in AXES)
    index = lambda t, d, r: (t * dps + d) * reps + r
    every = [(t, d, r) for t in range(tps) for d in range(dps) for r in range(reps)]
    return [(index(*at), index(*move(*at))) for at in every if at[0] != at[2] % 2]


def swap_diagonal(field):
    return lax.ppermute(field, AXES, crossing(lambda t, d, r: (r % 2, d, r - r % 2 + t)))


def swap_far_crossing(field):
    return lax.ppermute(field, AXES, crossing(lambda t, d, r: (t, d, r ^ 2)))


def swap_near(field):
    return lax.ppermute(field, "rep", [(r, r ^ 1) for r in range(lax.axis_size("rep"))])


def swap_far(field):
    return lax.ppermute(field, "rep", [(r, r ^ 2) for r in range(lax.axis_size("rep"))])


def after(field, *others):
    return lax.optimization_barrier((field, *others))[0]


def ordered(own, other, first, axis=0):
    return jnp.where(
        first, jnp.concatenate([own, other], axis=axis), jnp.concatenate([other, own], axis=axis)
    )


def take(field, index, axis=0):
    return lax.dynamic_index_in_dim(field, index, axis, keepdims=False)


def part_of(field, index, axis):
    size = field.shape[axis] // 2
    return lax.dynamic_slice_in_dim(field, index * size, size, axis)


def add(*fields):
    return sum(field.astype(jnp.float32) for field in fields).astype(jnp.bfloat16)


def move_rows(block):
    dps = lax.axis_size("dp")
    if dps > 8:
        flat = block.reshape(-1, block.shape[2])
        return [lax.psum_scatter(flat, "dp", scatter_dimension=0, tiled=True)]
    place = lax.axis_index("dp")
    moved = [take(block, place)]
    for step in range(1, dps):
        sent = take(block, lax.rem(place + step, dps))
        moved.append(lax.ppermute(sent, "dp", [(d, (d + step) % dps) for d in range(dps)]))
    return moved


def sum_everywhere(field):
    for name in ("rep", "tp", "dp"):
        size = lax.axis_size(name)
        bit = 1
        while bit < size:
            field = field + lax.ppermute(field, name, [(d, d ^ bit) for d in range(size)])
            bit *= 2
    return field


def local(
    layer_input,
    history,
    cotangent,
    lengths,
    dwa_weights,
    gain_one,
    bias_one,
    w_qkv,
    w_out,
    gain_two,
    bias_two,
    w_up,
    w_down,
):
    rows = layer_input.shape[1]
    whole = rows * lax.axis_size("tp")
    hist_count = history.shape[0]
    part, slot = lax.axis_index("tp"), lax.axis_index("rep")
    near, far = slot % 2, slot // 2
    same = near == part
    flags = jnp.stack([same.astype(jnp.int32), near, far])
    own_weight = dwa_weights[hist_count:]

    dps = lax.axis_size("dp")
    input_got = swap_diagonal(layer_input[0])
    qkv_got = swap_diagonal(w_qkv)
    up_early = swap_diagonal(after(part_of(w_up, 1 - far, 1), input_got))
    down_early = swap_diagonal(after(part_of(w_down, 1 - far, 0), qkv_got))
    out_got = swap_diagonal(after(w_out, qkv_got))
    cot_got = swap_diagonal(after(cotangent[0], qkv_got))

    own_lengths = jnp.where(same, lengths, swap_near(lengths))[0]
    seq_owner, token_place = positions(own_lengths, whole)
    seq_begin = jnp.arange(whole, dtype=jnp.int32) - token_place
    start_column = jnp.broadcast_to(seq_begin[:, None], (whole, LANES))
    start_row = jnp.broadcast_to(seq_begin[None, :], (8, whole))
    half_dim = HEAD_DIM // 2
    lane = jnp.arange(LANES, dtype=jnp.int32)
    frequency = jnp.exp((lane % half_dim).astype(jnp.float32) * (-math.log(10000.0) / half_dim))
    angles = token_place.astype(jnp.float32)[:, None] * frequency[None, :]
    cos_table = jnp.cos(angles)
    sin_table = jnp.sin(angles) * jnp.where(lane % HEAD_DIM < half_dim, -1.0, 1.0)[None, :]
    grad_history, past_sum, sums_past = past(dwa_weights, history[:, 0], cotangent[0])

    input_half = jnp.where(same, layer_input[0], input_got)
    layer_rows = ordered(input_half, swap_near(input_half), near == 0)
    layer_rows = after(layer_rows, past_sum, cos_table, sin_table, start_column, start_row)
    gain_one, bias_one = gain_one[None], bias_one[None]
    gain_two, bias_two = gain_two[None], bias_two[None]

    projected, norm_one_t, weight_qkv = project(
        flags, layer_rows, gain_one, bias_one, cos_table, sin_table, w_qkv, qkv_got
    )
    pairs = projected.shape[2] // LANES
    mixed = attend(0, start_column, projected, None, LONGEST)
    for pair in range(1, pairs):
        if pair == 1:
            up_late = swap_far_crossing(after(up_early, mixed))
        mixed = attend(pair, start_column, projected, mixed, LONGEST)
    down_late = swap_far_crossing(after(down_early, mixed))
    weight_out = jnp.where(same, w_out, after(out_got, mixed))
    attn = jnp.dot(mixed, weight_out, preferred_element_type=jnp.float32).astype(jnp.bfloat16)
    attn_got = swap_near(attn)
    cot_half = jnp.where(same, cotangent[0], after(cot_got, mixed))
    cot_rows = ordered(cot_half, swap_near(cot_half), near == 0)
    head = (own_weight, layer_rows, attn, attn_got, cot_rows, gain_two, bias_two)
    *kept, act_early, up_send, down_first = feed(
        True, flags, head, w_up, up_early, w_down, down_early
    )
    up_got = swap_far(up_send)
    first_got = swap_diagonal(down_first)
    back, act_late, up_keep, down_second = feed(
        False, flags, kept, w_up, up_late, w_down, down_late
    )
    back_got = swap_near(back)
    second_got = swap_diagonal(down_second)
    block_keep, block_send = lower(
        flags, act_early, act_late, w_down, down_early, down_late, layer_rows, attn, attn_got
    )
    block_got = swap_near(block_send)
    grad_attn, grad_mixed, grad_out, sums_two = middle(
        flags,
        own_weight,
        layer_rows,
        attn,
        attn_got,
        cot_rows,
        after(back, block_send),
        back_got,
        gain_two,
        mixed,
        weight_out,
    )

    def columns_of(pieces):
        return pieces.transpose(1, 0, 2).reshape(pieces.shape[1], -1)

    def by_dp(block):
        return block.reshape(dps, block.shape[0] // dps, block.shape[1])

    grad_qkv = attend_back(0, start_row, cos_table, sin_table, projected, grad_mixed, None, LONGEST)
    up_pair = add(up_keep, after(up_got, grad_qkv))
    up_moved = swap_diagonal(up_pair)
    first_sum = jnp.where(same, down_first, after(first_got, grad_qkv))
    second_sum = jnp.where(same, down_second, after(second_got, grad_qkv))
    down_keep = jnp.where(near == far, second_sum, first_sum)
    down_other = swap_near(jnp.where(near == far, first_sum, second_sum))
    block_half = add(block_keep, after(block_got, grad_qkv))
    block_moved = swap_diagonal(block_half)
    grad_qkv = after(grad_qkv, up_pair, down_keep, block_half)
    for pair in range(1, pairs):
        grad_qkv = attend_back(
            pair, start_row, cos_table, sin_table, projected, grad_mixed, grad_qkv, LONGEST
        )
        if pair == 1:
            down_one = add(down_keep, after(down_other, grad_qkv))
            down_blocks = move_rows(by_dp(down_one))
            up_pair = jnp.where(same, up_pair, after(up_moved, grad_qkv))
            up_other = swap_near(part_of(up_pair, 1 - near, 1))
            grad_qkv = after(grad_qkv, down_one, up_pair)
    up_one = add(part_of(up_pair, near, 1), after(up_other, grad_qkv))
    up_blocks = move_rows(by_dp(up_one))
    grad_weights = weigh(norm_one_t, grad_qkv)
    mine = take(grad_weights, far)
    key_got = swap_far(take(grad_weights, 1 - far))
    late_pieces = jnp.stack([grad_weights[2], grad_out])
    late_got = swap_diagonal(late_pieces)
    keep, send = unproject(flags, after(grad_qkv, grad_weights), weight_qkv)
    send_got = swap_near(send)
    output, sums_now = present(
        flags, own_weight, past_sum, cotangent[0], block_half, after(block_moved, send)
    )
    input_grad, sums_one = first_norm_back(flags, layer_rows, keep, send_got, grad_attn, gain_one)
    grad_input = swap_diagonal(input_grad)
    down_sum = add(*[after(block, input_grad) for block in down_blocks])
    down_far = swap_far(down_sum)
    small = jnp.concatenate(
        [sums_one[:2], sums_two[:2], sums_past[:hist_count], sums_now[:1]], axis=0
    )
    small = sum_everywhere(small)

    key_pair = add(mine, after(key_got, input_grad))
    key_moved = swap_diagonal(key_pair)
    late_pair = jnp.where(same, late_pieces, after(late_got, key_pair))
    late_one = add(take(late_pair, near), swap_near(take(late_pair, 1 - near)))
    late_blocks = move_rows(by_dp(late_one))
    key_pair = by_dp(jnp.where(same, key_pair, key_moved))
    key_one = add(part_of(key_pair, near, 1), swap_near(part_of(key_pair, 1 - near, 1)))
    key_blocks = move_rows(key_one)
    up_sum = add(*[after(block, key_one) for block in up_blocks])
    up_half = ordered(up_sum, swap_near(up_sum), near == 0, axis=1)
    up_far = swap_far(up_half)
    down_sum = add(down_sum, down_far)
    grad_w_down = ordered(down_sum[None], swap_near(down_sum)[None], near == 0)
    late_sum = add(*late_blocks)
    late_sum = add(late_sum, swap_far(late_sum))
    grad_value_out = ordered(late_sum[None], swap_near(late_sum)[None], near == 0)
    key_sum = add(*key_blocks)
    key_half = ordered(key_sum, swap_near(key_sum), near == 0)
    grad_query_key = ordered(key_half[None], swap_far(key_half)[None], far == 0)
    grad_w_up = ordered(up_half[None], up_far[None], far == 0)
    grad_w_qkv = jnp.concatenate([grad_query_key, grad_value_out[:1]], axis=0)

    return (
        output[None],
        jnp.where(same, input_grad, grad_input)[None],
        grad_history[:, None],
        jnp.sum(small[4:], axis=1),
        small[0],
        small[1],
        grad_w_qkv.astype(jnp.float32),
        grad_value_out[1].astype(jnp.float32).T,
        small[2],
        small[3],
        columns_of(grad_w_up).astype(jnp.float32),
        columns_of(grad_w_down).astype(jnp.float32).T,
    )


def positions(seq_lengths, token_count):
    seq_ends = jnp.cumsum(seq_lengths)
    seq_starts = seq_ends - seq_lengths
    token_index = jnp.arange(token_count, dtype=jnp.int32)
    seq_owner = jnp.sum((token_index[:, None] >= seq_ends[None, :]).astype(jnp.int32), axis=1)
    picked = (
        seq_owner[:, None] == jnp.arange(seq_lengths.shape[0], dtype=jnp.int32)[None, :]
    ).astype(jnp.int32)
    seq_begin = jnp.sum(picked * seq_starts[None, :], axis=1)
    return (seq_owner, token_index - seq_begin)


def solution(mesh):
    in_specs = (
        P(("dp", "rep"), "tp", None),
        P(None, ("dp", "rep"), "tp", None),
        P(("dp", "rep"), "tp", None),
        P(("dp", "rep"), None),
        P(),
        P(),
        P(),
        P(None, None, "tp"),
        P("tp", None),
        P(),
        P(),
        P(None, "tp"),
        P("tp", None),
    )
    out_specs = (
        P(("dp", "rep"), "tp", None),
        P(("dp", "rep"), "tp", None),
        P(None, ("dp", "rep"), "tp", None),
        P(),
        P(),
        P(),
        P(None, "dp", "tp"),
        P("tp", "dp"),
        P(),
        P(),
        P("dp", "tp"),
        P("tp", "dp"),
    )
    return jax.shard_map(local, mesh=mesh, in_specs=in_specs, out_specs=out_specs, check_vma=False)
```

```python
import functools
import itertools
import math

import jax
import jax.numpy as jnp
from jax import lax
from jax.experimental import pallas as pl
from jax.experimental.pallas import tpu as pltpu
from jax.sharding import Mesh, PartitionSpec as P

HEAD_DIM = 64
LONGEST = 512
NEG_FILL = -1e30
NORM_EPS = 1e-05
RATE = 3e6


def lasting(microseconds):
    return pl.CostEstimate(flops=0, transcendentals=0, bytes_accessed=int(microseconds * RATE))


BLOCK = 256
LANES = 128
NT = (((1,), (1,)), ((), ()))


def dot(a, b, dims=(((1,), (0,)), ((), ()))):
    return lax.dot_general(a, b, dims, preferred_element_type=jnp.float32)


def spans(whole, reach):
    back = -(-(reach - 1) // BLOCK)
    runs = []
    for i in range(whole // BLOCK):
        count = min(i, back) + 1
        if runs and runs[-1][2] == count:
            runs[-1][1] = i + 1
        else:
            runs.append([i, i + 1, count])
    return runs


def each_block(whole, reach, body):
    for first, last, count in spans(whole, reach):
        def step(at, carry, first=first, count=count):
            i = first + at // 2
            body(i, i + 1 - count, count * BLOCK, at % 2)
            return carry
        lax.fori_loop(0, 2 * (last - first), step, 0)


def attend_kernel(reach, start_ref, q_ref, k_ref, v_ref, out_ref, acc_ref):
    whole = q_ref.shape[0]
    lane = lax.broadcasted_iota(jnp.int32, (BLOCK, LANES), 1) // HEAD_DIM

    def body(i, first, count, head):
        at = pl.ds(pl.multiple_of(i * BLOCK, BLOCK), BLOCK)
        keys = pl.ds(pl.multiple_of(first * BLOCK, BLOCK), count)
        query = q_ref[at, :] * (HEAD_DIM**-0.5)
        query = jnp.where(lane == head, query, jnp.zeros_like(query))
        scores = dot(query, k_ref[keys, :], NT)
        key_at = first * BLOCK + lax.broadcasted_iota(jnp.int32, scores.shape, 1)
        query_at = i * BLOCK + lax.broadcasted_iota(jnp.int32, scores.shape, 0)
        allowed = (key_at >= start_ref[at, :1]) & (key_at <= query_at)
        scores = jnp.where(allowed, scores, NEG_FILL)
        exponent = jnp.exp(scores - jnp.max(scores, axis=1, keepdims=True))
        row_sum = jnp.sum(exponent, axis=1, keepdims=True)
        probs = (exponent * (1.0 / row_sum)).astype(jnp.bfloat16)
        mixed = dot(probs, v_ref[keys, :])

        @pl.when(head == 0)
        def _():
            acc_ref[...] = mixed

        @pl.when(head == 1)
        def _():
            out_ref[at, :] = jnp.where(lane == 0, acc_ref[...], mixed).astype(out_ref.dtype)

    each_block(whole, reach, body)


def attend(pair, start_column, projected, so_far, reach):
    count, whole, width = projected.shape

    def block(c):
        return pl.BlockSpec((None, whole, LANES), lambda i: (c, 0, pair))

    begun = [] if so_far is None else [so_far]
    kernel = attend_kernel if so_far is None else lambda reach, unused, *refs: attend_kernel(reach, *refs)
    return pl.pallas_call(
        functools.partial(kernel, reach),
        grid=(1,),
        in_specs=[pl.BlockSpec(memory_space=pl.ANY)] * len(begun)
        + [pl.BlockSpec((whole, LANES), lambda i: (0, 0)), block(0), block(1), block(2)],
        out_specs=pl.BlockSpec((whole, LANES), lambda i: (0, pair)),
        out_shape=jax.ShapeDtypeStruct((whole, width), jnp.bfloat16),
        scratch_shapes=[pltpu.VMEM((BLOCK, LANES), jnp.float32)],
        input_output_aliases={0: 0} if begun else {},
        compiler_params=pltpu.CompilerParams(vmem_limit_bytes=40 << 20),
        cost_estimate=lasting(5),
    )(*begun, start_column, projected, projected, projected)


def turn_back(field, cos, sin):
    half = HEAD_DIM // 2
    lane = lax.broadcasted_iota(jnp.int32, field.shape, 1) % HEAD_DIM
    crossed = jnp.where(lane < half, pltpu.roll(field, LANES - half, 1), pltpu.roll(field, half, 1))
    return field * cos - crossed * sin


def attend_back_kernel(
    reach, start_ref, cos_ref, sin_ref, q_ref, k_ref, v_ref, g_ref, out_ref,
    key_acc, value_acc, query_acc,
):
    whole = q_ref.shape[0]
    lane = lax.broadcasted_iota(jnp.int32, (BLOCK, LANES), 1) // HEAD_DIM
    key_acc[...] = jnp.zeros_like(key_acc)
    value_acc[...] = jnp.zeros_like(value_acc)

    def body(i, first, count, head):
        at = pl.ds(pl.multiple_of(i * BLOCK, BLOCK), BLOCK)
        span = pl.ds(pl.multiple_of(first * BLOCK, BLOCK), count)
        query = q_ref[at, :] * (HEAD_DIM**-0.5)
        query = jnp.where(lane == head, query, jnp.zeros_like(query))
        grad = g_ref[at, :]
        grad = jnp.where(lane == head, grad, jnp.zeros_like(grad))
        keys = k_ref[span, :]
        scores = dot(keys, query, NT)
        key_at = first * BLOCK + lax.broadcasted_iota(jnp.int32, scores.shape, 0)
        query_at = i * BLOCK + lax.broadcasted_iota(jnp.int32, scores.shape, 1)
        allowed = (key_at >= start_ref[:1, at]) & (key_at <= query_at)
        scores = jnp.where(allowed, scores, NEG_FILL)
        exponent = jnp.exp(scores - jnp.max(scores, axis=0, keepdims=True))
        probs = exponent * (1.0 / jnp.sum(exponent, axis=0, keepdims=True))
        value_acc[span, :] += dot(probs.astype(jnp.bfloat16), grad)
        grad_probs = dot(v_ref[span, :], grad, NT)
        weighted = probs * grad_probs
        grad_scores = (weighted - probs * jnp.sum(weighted, axis=0, keepdims=True)).astype(jnp.bfloat16)
        key_acc[span, :] += dot(grad_scores, query)
        here = dot(grad_scores, keys, (((0,), (0,)), ((), ())))

        @pl.when(head == 0)
        def _():
            query_acc[...] = here

        @pl.when(head == 1)
        def _():
            both = jnp.where(lane == 0, query_acc[...], here) * (HEAD_DIM**-0.5)
            out_ref[0, at, :] = turn_back(both, cos_ref[at, :], sin_ref[at, :]).astype(out_ref.dtype)

    each_block(whole, reach, body)

    def finish(i, carry):
        at = pl.ds(pl.multiple_of(i * BLOCK, BLOCK), BLOCK)
        out_ref[1, at, :] = turn_back(key_acc[at, :], cos_ref[at, :], sin_ref[at, :]).astype(out_ref.dtype)
        out_ref[2, at, :] = value_acc[at, :].astype(out_ref.dtype)
        return carry

    lax.fori_loop(0, whole // BLOCK, finish, 0)


def attend_back(pair, start_row, cos, sin, projected, grad_mixed, so_far, reach):
    count, whole, width = projected.shape

    def block(c):
        return pl.BlockSpec((None, whole, LANES), lambda i: (c, 0, pair))

    table = pl.BlockSpec((whole, LANES), lambda i: (0, 0))
    begun = [] if so_far is None else [so_far]
    kernel = attend_back_kernel if so_far is None else lambda reach, unused, *refs: attend_back_kernel(reach, *refs)
    return pl.pallas_call(
        functools.partial(kernel, reach),
        grid=(1,),
        in_specs=[pl.BlockSpec(memory_space=pl.ANY)] * len(begun)
        + [
            pl.BlockSpec((8, whole), lambda i: (0, 0)),
            table,
            table,
            block(0),
            block(1),
            block(2),
            pl.BlockSpec((whole, LANES), lambda i: (0, pair)),
        ],
        out_specs=pl.BlockSpec((count, whole, LANES), lambda i: (0, 0, pair)),
        out_shape=jax.ShapeDtypeStruct((count, whole, width), jnp.bfloat16),
        scratch_shapes=[
            pltpu.VMEM((whole, LANES), jnp.float32),
            pltpu.VMEM((whole, LANES), jnp.float32),
            pltpu.VMEM((BLOCK, LANES), jnp.float32),
        ],
        input_output_aliases={0: 0} if begun else {},
        compiler_params=pltpu.CompilerParams(vmem_limit_bytes=40 << 20),
        cost_estimate=lasting(9),
    )(*begun, start_row, cos, sin, projected, projected, projected, grad_mixed)


ROWS = 256


def norm_parts(field):
    centered = field - jnp.mean(field, axis=-1, keepdims=True)
    scale = lax.rsqrt(jnp.mean(centered * centered, axis=-1, keepdims=True) + NORM_EPS)
    return centered * scale, scale


def wide(ref, at):
    return ref[at, :].astype(jnp.float32)


def row_blocks(count, body):
    def step(i, carry):
        body(i, pl.ds(pl.multiple_of(i * ROWS, ROWS), ROWS))
        return carry

    lax.fori_loop(0, count // ROWS, step, 0)


def whole_spec(shape):
    return pl.BlockSpec(shape, lambda *at: (0,) * len(shape))


def turn(field, cos, sin):
    half = HEAD_DIM // 2
    lane = lax.broadcasted_iota(jnp.int32, field.shape, 1) % HEAD_DIM
    crossed = jnp.where(lane < half, pltpu.roll(field, LANES - half, 1), pltpu.roll(field, half, 1))
    return field * cos + crossed * sin


def project_kernel(
    flags, rows_ref, gain_ref, shift_ref, cos_ref, sin_ref, w_own, w_got, out_ref, turned_ref,
    weight_ref, norm_ref,
):
    whole = rows_ref.shape[0]
    step = pl.program_id(0)

    @pl.when(step == 0)
    def _():
        def body(i, at):
            unit, unused = norm_parts(wide(rows_ref, at))
            norm = unit * gain_ref[...] + shift_ref[...]
            norm_ref[at, :] = norm.astype(jnp.bfloat16)
            turned_ref[:, at] = norm.T.astype(jnp.bfloat16)

        row_blocks(whole, body)

    weight_ref[0] = jnp.where(flags[0] == 1, w_own[0], w_got[0])

    def body(i, at):
        field = dot(norm_ref[at, :], weight_ref[0])

        @pl.when(step < 2)
        def _():
            for p in range(field.shape[1] // LANES):
                lanes = slice(p * LANES, (p + 1) * LANES)
                out_ref[0, at, lanes] = turn(field[:, lanes], cos_ref[at, :], sin_ref[at, :]).astype(
                    jnp.bfloat16
                )

        @pl.when(step == 2)
        def _():
            out_ref[0, at, :] = field.astype(jnp.bfloat16)

    row_blocks(whole, body)


def project(flags, rows, gain, shift, cos, sin, w_own, w_got):
    whole, width = rows.shape
    count, unused, columns = w_own.shape
    weight = pl.BlockSpec((1, width, columns), lambda c, flags: (c, 0, 0))
    return pl.pallas_call(
        project_kernel,
        grid_spec=pltpu.PrefetchScalarGridSpec(
            num_scalar_prefetch=1,
            grid=(count,),
            in_specs=[
                whole_spec((whole, width)),
                whole_spec((1, width)),
                whole_spec((1, width)),
                whole_spec((whole, LANES)),
                whole_spec((whole, LANES)),
                weight,
                weight,
            ],
            out_specs=[
                pl.BlockSpec((1, whole, columns), lambda c, flags: (c, 0, 0)),
                whole_spec((width, whole)),
                weight,
            ],
            scratch_shapes=[pltpu.VMEM((whole, width), jnp.bfloat16)],
        ),
        out_shape=[
            jax.ShapeDtypeStruct((count, whole, columns), jnp.bfloat16),
            jax.ShapeDtypeStruct((width, whole), jnp.bfloat16),
            jax.ShapeDtypeStruct(w_own.shape, jnp.bfloat16),
        ],
        compiler_params=pltpu.CompilerParams(vmem_limit_bytes=40 << 20),
        cost_estimate=lasting(9),
    )(flags, rows, gain, shift, cos, sin, w_own, w_got)


HIDDEN = 256


def gelu_both(up):
    root = math.sqrt(2.0 / math.pi)
    square = up * up
    bent = jnp.tanh(root * up * (1.0 + 0.044715 * square))
    half = 0.5 * (1.0 + bent)
    slope = half + 0.5 * up * (1.0 - bent * bent) * (root * (1.0 + 3.0 * 0.044715 * square))
    return up * half, slope


def join_rows(flags, own, near, far, out):
    half = near.shape[0]
    for index, got in ((flags[2], near), (1 - flags[2], far)):
        at = pl.ds(pl.multiple_of(index * half, half), half)
        out[at, :] = jnp.where(flags[0] == 1, own[at, :], got[...])


def feed_kernel(early, flags, *refs):
    if early:
        weight_ref, rows_ref, own_ref, got_ref, cot_ref, gain_ref, shift_ref = refs[:7]
        refs = refs[7:]
        up_own, down_own, near, far, norm, norm_t, grad, grad_t = refs[:8]
    else:
        norm, norm_t, grad, grad_t, back_early, up_own, down_own, whole_got = refs[:8]
    back_ref, act_ref, pieces_ref, down_ref, slope, up_w = refs[-6:]
    whole, width = norm.shape
    part = pieces_ref.shape[2]
    step = pl.program_id(0)

    @pl.when(step == 0)
    def _():
        if not early:
            half = whole_got.shape[0] // 2
            up_w[...] = jnp.where(flags[0] == 1, up_own[...], whole_got[:half])
            down_ref[...] = jnp.where(flags[0] == 1, down_own[...], whole_got[half:])
        else:
            half = near.shape[0] // 2
            join_rows(flags, up_own, near.at[:half], far.at[:half], up_w)
            join_rows(flags, down_own, near.at[half:], far.at[half:], down_ref)

            def body(i, at):
                unit, unused = norm_parts(wide(rows_ref, at) + wide(own_ref, at) + wide(got_ref, at))
                field = unit * gain_ref[...] + shift_ref[...]
                norm[at, :] = field.astype(jnp.bfloat16)
                norm_t[:, at] = field.T.astype(jnp.bfloat16)
                field = wide(cot_ref, at) * weight_ref[0]
                grad[at, :] = field.astype(jnp.bfloat16)
                grad_t[:, at] = field.T.astype(jnp.bfloat16)

            row_blocks(whole, body)

    hidden = pl.ds(pl.multiple_of(step * HIDDEN, HIDDEN), HIDDEN)
    up_block = up_w[:, hidden]
    down_block = down_ref[hidden, :]

    def body(i, at):
        value, rise = gelu_both(dot(norm[at, :], up_block))
        act_ref[at, :] = value.astype(jnp.bfloat16)
        slope[at, hidden] = (dot(grad[at, :], down_block, NT) * rise).astype(jnp.bfloat16)

    row_blocks(whole, body)

    def grads(i, at):
        fields = (dot(norm_t[at, :], slope[:, hidden]), dot(grad_t[at, :], act_ref[...]))
        for k, field in enumerate(fields):
            field = field.astype(jnp.bfloat16)
            for j in range(2 * part // HIDDEN):

                @pl.when(step == j)
                def _():
                    for p in range(2):
                        first, last = max(p * part, j * HIDDEN), min((p + 1) * part, (j + 1) * HIDDEN)
                        if first < last:
                            pieces_ref[2 * k + p, at, first - p * part : last - p * part] = field[
                                :, first - j * HIDDEN : last - j * HIDDEN
                            ]

    row_blocks(width, grads)

    @pl.when(step == pl.num_programs(0) - 1)
    def _():
        def body(i, at):
            back = dot(slope[at, :], up_w[...], NT)
            if not early:
                back = back + back_early[at, :]
            back_ref[at, :] = back.astype(back_ref.dtype)

        row_blocks(whole, body)


def feed(early, flags, head, w_up, w_down, *got):
    whole, width = head[1].shape if early else head[0].shape
    hidden = w_up.shape[1] // 2
    steps = hidden // HIDDEN
    tokens = whole_spec((whole, width))
    turned = whole_spec((width, whole))
    vector = whole_spec((1, width))
    index = 0 if early else 1
    low = jax.ShapeDtypeStruct((whole, width), jnp.bfloat16)
    low_turned = jax.ShapeDtypeStruct((width, whole), jnp.bfloat16)
    full = jax.ShapeDtypeStruct((whole, width), jnp.float32)
    if early:
        head_specs = [pl.BlockSpec(memory_space=pltpu.SMEM)] + [tokens] * 4 + [vector] * 2
    else:
        head_specs = [tokens, turned, tokens, turned, tokens]
    return pl.pallas_call(
        functools.partial(feed_kernel, early),
        grid_spec=pltpu.PrefetchScalarGridSpec(
            num_scalar_prefetch=1,
            grid=(steps,),
            in_specs=head_specs
            + [
                pl.BlockSpec((width, hidden), lambda j, flags: (0, index)),
                pl.BlockSpec((hidden, width), lambda j, flags: (index, 0)),
            ]
            + [whole_spec(field.shape) for field in got],
            out_specs=([tokens, turned, tokens, turned] if early else [])
            + [
                tokens,
                pl.BlockSpec((whole, HIDDEN), lambda j, flags: (0, j)),
                whole_spec((4, width, hidden // 2)),
                whole_spec((hidden, width)),
            ],
            scratch_shapes=[
                pltpu.VMEM((whole, hidden), jnp.bfloat16),
                pltpu.VMEM((width, hidden), jnp.bfloat16),
            ],
        ),
        out_shape=([low, low_turned, low, low_turned, full] if early else [low])
        + [
            jax.ShapeDtypeStruct((whole, hidden), jnp.bfloat16),
            jax.ShapeDtypeStruct((4, width, hidden // 2), jnp.bfloat16),
            jax.ShapeDtypeStruct((hidden, width), jnp.bfloat16),
        ],
        compiler_params=pltpu.CompilerParams(vmem_limit_bytes=58 << 20),
        cost_estimate=lasting(20),
    )(flags, *head, w_up, w_down, *got)


def lower_kernel(flags, act_early, act_late, early_ref, late_ref, rows_ref, own_ref, got_ref, keep_ref, send_ref):
    half = keep_ref.shape[0]
    first, second = early_ref[...], late_ref[...]

    def at_rows(near, i):
        return pl.ds(pl.multiple_of(near * half + i * ROWS, ROWS), ROWS)

    def send(i, at):
        here = at_rows(1 - flags[1], i)
        total = dot(act_early[here, :], first) + dot(act_late[here, :], second)
        send_ref[at, :] = total.astype(jnp.bfloat16)

    def keep(i, at):
        here = at_rows(flags[1], i)
        total = dot(act_early[here, :], first) + dot(act_late[here, :], second)
        keep_ref[at, :] = total + wide(rows_ref, here) + wide(own_ref, here) + wide(got_ref, here)

    row_blocks(half, send)
    row_blocks(half, keep)


def lower(flags, act_early, act_late, down_early, down_late, rows, own, got):
    whole, hidden = act_early.shape
    width = rows.shape[1]
    half = whole_spec((whole // 2, width))
    return pl.pallas_call(
        lower_kernel,
        grid_spec=pltpu.PrefetchScalarGridSpec(
            num_scalar_prefetch=1,
            grid=(1,),
            in_specs=[whole_spec((whole, hidden))] * 2
            + [whole_spec((hidden, width))] * 2
            + [whole_spec((whole, width))] * 3,
            out_specs=[half, half],
        ),
        out_shape=[
            jax.ShapeDtypeStruct((whole // 2, width), jnp.float32),
            jax.ShapeDtypeStruct((whole // 2, width), jnp.bfloat16),
        ],
        compiler_params=pltpu.CompilerParams(vmem_limit_bytes=56 << 20),
        cost_estimate=lasting(7),
    )(flags, act_early, act_late, down_early, down_late, rows, own, got)


def middle_kernel(
    flags, weight_ref, rows_ref, own_ref, got_ref, cot_ref, back_own, back_got, gain_ref, mixed_ref,
    w_ref, grad_ref, gmixed_ref, gout_ref, sums_ref, turned,
):
    whole, width = rows_ref.shape
    weight = w_ref[...]
    gain = gain_ref[...]
    sums_ref[...] = jnp.zeros_like(sums_ref)

    def body(i, at):
        unit, scale = norm_parts(wide(rows_ref, at) + wide(own_ref, at) + wide(got_ref, at))
        back = wide(back_own, at) + wide(back_got, at)
        inner = back * gain
        mean = jnp.mean(inner, axis=-1, keepdims=True)
        slant = jnp.mean(inner * unit, axis=-1, keepdims=True)
        grad = wide(cot_ref, at) * weight_ref[0] + scale * (inner - mean - unit * slant)
        low = grad.astype(jnp.bfloat16)
        grad_ref[at, :] = low
        turned[:, at] = grad.T.astype(jnp.bfloat16)
        gmixed_ref[at, :] = dot(low, weight, NT).astype(jnp.bfloat16)

        @pl.when((i * ROWS) // (whole // 2) == flags[1])
        def _():
            sums_ref[0:1, :] += jnp.sum(back * unit, axis=0, keepdims=True)
            sums_ref[1:2, :] += jnp.sum(back, axis=0, keepdims=True)

    row_blocks(whole, body)

    def grads(i, at):
        gout_ref[at, :] = dot(turned[at, :], mixed_ref[...]).astype(jnp.bfloat16)

    row_blocks(width, grads)


def middle(flags, weight, rows, own, got, cot, back_own, back_got, gain, mixed, w_out):
    whole, width = rows.shape
    columns = mixed.shape[1]
    tokens = whole_spec((whole, width))
    narrow = whole_spec((whole, columns))
    projection = whole_spec((columns, width))
    return pl.pallas_call(
        middle_kernel,
        grid_spec=pltpu.PrefetchScalarGridSpec(
            num_scalar_prefetch=1,
            grid=(1,),
            in_specs=[pl.BlockSpec(memory_space=pltpu.SMEM)]
            + [tokens] * 6
            + [whole_spec((1, width)), narrow, projection],
            out_specs=[tokens, narrow, whole_spec((width, columns)), whole_spec((8, width))],
            scratch_shapes=[pltpu.VMEM((width, whole), jnp.bfloat16)],
        ),
        out_shape=[
            jax.ShapeDtypeStruct((whole, width), jnp.bfloat16),
            jax.ShapeDtypeStruct((whole, columns), jnp.bfloat16),
            jax.ShapeDtypeStruct((width, columns), jnp.bfloat16),
            jax.ShapeDtypeStruct((8, width), jnp.float32),
        ],
        compiler_params=pltpu.CompilerParams(vmem_limit_bytes=56 << 20),
        cost_estimate=lasting(12),
    )(flags, weight, rows, own, got, cot, back_own, back_got, gain, mixed, w_out)


def weigh_kernel(flags, turned_ref, grad_ref, out_grad_ref, keep_ref, send_ref, late_ref):
    far = flags[2]

    def grads(i, at):
        rows = turned_ref[at, :]
        send_ref[at, :] = dot(rows, grad_ref[1 - far]).astype(jnp.bfloat16)
        late_ref[0, at, :] = dot(rows, grad_ref[2]).astype(jnp.bfloat16)
        late_ref[1, at, :] = out_grad_ref[at, :]
        keep_ref[at, :] = dot(rows, grad_ref[far]).astype(jnp.bfloat16)

    row_blocks(turned_ref.shape[0], grads)


def weigh(flags, turned, grad, out_grad):
    width, whole = turned.shape
    columns = grad.shape[2]
    piece = whole_spec((width, columns))
    return pl.pallas_call(
        weigh_kernel,
        grid_spec=pltpu.PrefetchScalarGridSpec(
            num_scalar_prefetch=1,
            grid=(1,),
            in_specs=[whole_spec((width, whole)), whole_spec(grad.shape), piece],
            out_specs=[piece, piece, whole_spec((2, width, columns))],
        ),
        out_shape=[jax.ShapeDtypeStruct((width, columns), jnp.bfloat16)] * 2
        + [jax.ShapeDtypeStruct((2, width, columns), jnp.bfloat16)],
        compiler_params=pltpu.CompilerParams(vmem_limit_bytes=40 << 20),
        cost_estimate=lasting(3),
    )(flags, turned, grad, out_grad)


def unproject_kernel(flags, grad_ref, weight, keep_ref, send_ref):
    half = keep_ref.shape[0]

    def side(near, out_ref):
        def body(i, at):
            from_rows = pl.ds(pl.multiple_of(near * half + i * ROWS, ROWS), ROWS)
            total = dot(grad_ref[0, from_rows, :], weight[0], NT)
            for c in range(1, grad_ref.shape[0]):
                total = total + dot(grad_ref[c, from_rows, :], weight[c], NT)
            out_ref[at, :] = total.astype(out_ref.dtype)

        row_blocks(half, body)

    side(1 - flags[1], send_ref)
    side(flags[1], keep_ref)


def unproject(flags, grad, weight):
    count, whole, columns = grad.shape
    width = weight.shape[1]
    half = whole_spec((whole // 2, width))
    return pl.pallas_call(
        unproject_kernel,
        grid_spec=pltpu.PrefetchScalarGridSpec(
            num_scalar_prefetch=1,
            grid=(1,),
            in_specs=[whole_spec(grad.shape), whole_spec((count, width, columns))],
            out_specs=[half, half],
        ),
        out_shape=[
            jax.ShapeDtypeStruct((whole // 2, width), jnp.float32),
            jax.ShapeDtypeStruct((whole // 2, width), jnp.bfloat16),
        ],
        compiler_params=pltpu.CompilerParams(vmem_limit_bytes=40 << 20),
        cost_estimate=lasting(4),
    )(flags, grad, weight)


def first_norm_kernel(flags, rows_ref, keep_ref, got_ref, resid_ref, gain_ref, out_ref, sums_ref):
    sums_ref[...] = jnp.zeros_like(sums_ref)

    def body(i, at):
        unit, scale = norm_parts(wide(rows_ref, at))
        back = keep_ref[at, :] + wide(got_ref, at)
        inner = back * gain_ref[...]
        mean = jnp.mean(inner, axis=-1, keepdims=True)
        slant = jnp.mean(inner * unit, axis=-1, keepdims=True)
        grad = wide(resid_ref, at) + scale * (inner - mean - unit * slant)
        out_ref[at, :] = grad.astype(jnp.bfloat16)
        sums_ref[0:1, :] += jnp.sum(back * unit, axis=0, keepdims=True)
        sums_ref[1:2, :] += jnp.sum(back, axis=0, keepdims=True)

    row_blocks(rows_ref.shape[0], body)


def first_norm_back(flags, rows, keep, got, resid, gain):
    half, width = keep.shape
    mine = pl.BlockSpec((half, width), lambda i, flags: (flags[1], 0))
    tokens = whole_spec((half, width))
    return pl.pallas_call(
        first_norm_kernel,
        grid_spec=pltpu.PrefetchScalarGridSpec(
            num_scalar_prefetch=1,
            grid=(1,),
            in_specs=[mine, tokens, tokens, mine, whole_spec((1, width))],
            out_specs=[tokens, whole_spec((8, width))],
        ),
        out_shape=[
            jax.ShapeDtypeStruct((half, width), jnp.bfloat16),
            jax.ShapeDtypeStruct((8, width), jnp.float32),
        ],
        compiler_params=pltpu.CompilerParams(vmem_limit_bytes=40 << 20),
        cost_estimate=lasting(2),
    )(flags, rows, keep, got, resid, gain)


def past_kernel(dwa_ref, hist_ref, cot_ref, grad_ref, part_ref, sums_ref):
    @pl.when(pl.program_id(0) == 0)
    def _():
        sums_ref[...] = jnp.zeros_like(sums_ref)

    grad = cot_ref[...].astype(jnp.float32)
    total = jnp.zeros_like(grad)
    for j in range(hist_ref.shape[0]):
        field = hist_ref[j].astype(jnp.float32)
        total += dwa_ref[j] * field
        grad_ref[j] = (dwa_ref[j] * grad).astype(jnp.bfloat16)
        sums_ref[j : j + 1, :] += jnp.sum(field * grad, axis=0, keepdims=True)
    part_ref[...] = total


def past(dwa, history, cot):
    count, rows, width = history.shape
    layers = pl.BlockSpec((count, ROWS, width), lambda i: (0, i, 0))
    tokens = pl.BlockSpec((ROWS, width), lambda i: (i, 0))
    return pl.pallas_call(
        past_kernel,
        grid=(rows // ROWS,),
        in_specs=[pl.BlockSpec(memory_space=pltpu.SMEM), layers, tokens],
        out_specs=[layers, tokens, whole_spec((8, width))],
        out_shape=[
            jax.ShapeDtypeStruct(history.shape, jnp.bfloat16),
            jax.ShapeDtypeStruct((rows, width), jnp.float32),
            jax.ShapeDtypeStruct((8, width), jnp.float32),
        ],
        compiler_params=pltpu.CompilerParams(vmem_limit_bytes=40 << 20),
        cost_estimate=lasting(3),
    )(dwa, history, cot)


def present_kernel(flags, weight_ref, part_ref, cot_ref, own_ref, got_ref, out_ref, sums_ref):
    field = jnp.where(flags[0] == 1, own_ref[...], got_ref[...]).astype(jnp.float32)
    out_ref[...] = (part_ref[...] + weight_ref[0] * field).astype(jnp.bfloat16)
    total = jnp.sum(field * cot_ref[...].astype(jnp.float32), axis=0, keepdims=True)
    sums_ref[...] = jnp.broadcast_to(total, sums_ref.shape)


def present(flags, weight, part, cot, own, got):
    rows, width = part.shape
    scalars = pl.BlockSpec(memory_space=pltpu.SMEM)
    tokens = whole_spec((rows, width))
    return pl.pallas_call(
        present_kernel,
        grid=(1,),
        in_specs=[scalars, scalars] + [tokens] * 4,
        out_specs=[tokens, whole_spec((8, width))],
        out_shape=[
            jax.ShapeDtypeStruct((rows, width), jnp.bfloat16),
            jax.ShapeDtypeStruct((8, width), jnp.float32),
        ],
        compiler_params=pltpu.CompilerParams(vmem_limit_bytes=40 << 20),
        cost_estimate=lasting(2),
    )(flags, weight, part, cot, own, got)


AXES = ("tp", "dp", "far", "near")


def moves(chosen, move):
    sizes = [lax.axis_size(name) for name in AXES]
    places = [place for place in itertools.product(*map(range, sizes)) if chosen(*place)]
    index = lambda place: functools.reduce(lambda at, step: at * step[0] + step[1], zip(sizes, place), 0)
    return [(index(place), index(move(*place))) for place in places]


def away(t, d, k, c):
    return t != c


def home(t, d, k, c):
    return t == c


def swap_diagonal(field):
    return lax.ppermute(field, AXES, moves(away, lambda t, d, k, c: (c, d, k, t)))


def swap_far_away(field):
    return lax.ppermute(field, AXES, moves(away, lambda t, d, k, c: (t, d, 1 - k, c)))


def bring_home(field):
    return lax.ppermute(field, AXES, moves(away, lambda t, d, k, c: (c, d, k, c)))


def swap_far_home(field):
    return lax.ppermute(field, AXES, moves(home, lambda t, d, k, c: (t, d, 1 - k, c)))


def swap_far(field):
    return lax.ppermute(field, "far", [(0, 1), (1, 0)])


def swap_near(field):
    return lax.ppermute(field, "near", [(0, 1), (1, 0)])


def after(field, *others):
    return lax.optimization_barrier((field, *others))[0]


def ordered(own, other, first, axis=0):
    return jnp.where(
        first, jnp.concatenate([own, other], axis=axis), jnp.concatenate([other, own], axis=axis)
    )


def take(field, index):
    return lax.dynamic_index_in_dim(field, index, 0, keepdims=False)


def part_of(field, index, axis):
    size = field.shape[axis] // 2
    return lax.dynamic_slice_in_dim(field, index * size, size, axis)


def add(*fields):
    return sum(field.astype(jnp.float32) for field in fields).astype(jnp.bfloat16)


def scatter_plane(pieces):
    return lax.psum_scatter(pieces, ("tp", "far"), scatter_dimension=0, tiled=True)[0]


def scatter_rows(piece):
    return lax.psum_scatter(piece, "dp", scatter_dimension=0, tiled=True)


def gather(piece, part, far, same):
    pair = ordered(piece[None], bring_home(piece)[None], part == 0)
    pairs = ordered(pair[None], swap_far_home(pair)[None], far == 0)
    return jnp.where(same, pairs, swap_near(pairs))


def sum_everywhere(field):
    for name in ("near", "far", "tp", "dp"):
        size = lax.axis_size(name)
        bit = 1
        while bit < size:
            field = field + lax.ppermute(field, name, [(d, d ^ bit) for d in range(size)])
            bit *= 2
    return field


def local(
    layer_input,
    history,
    cotangent,
    lengths,
    dwa_weights,
    gain_one,
    bias_one,
    w_qkv,
    w_out,
    gain_two,
    bias_two,
    w_up,
    w_down,
):
    rows = layer_input.shape[1]
    whole = rows * lax.axis_size("tp")
    hist_count = history.shape[0]
    part, far, near = lax.axis_index("tp"), lax.axis_index("far"), lax.axis_index("near")
    same = near == part
    flags = jnp.stack([same.astype(jnp.int32), near, far])
    own_weight = dwa_weights[hist_count:]

    input_got = swap_diagonal(layer_input[0])
    qkv_got = swap_diagonal(w_qkv)

    up_part, down_part = part_of(w_up, 0, 1), part_of(w_down, 0, 0)
    early_near = jnp.concatenate([part_of(up_part, far, 0), part_of(down_part, far, 0)], axis=0)
    late_got = jnp.concatenate([part_of(w_up, 1, 1), part_of(w_down, 1, 0)], axis=0)
    last_near = jnp.concatenate([w_out, cotangent[0]], axis=0)
    gain_one, bias_one = gain_one[None], bias_one[None]
    gain_two, bias_two = gain_two[None], bias_two[None]

    own_lengths = jnp.where(same, lengths, swap_near(lengths))[0]
    seq_owner, token_place = positions(own_lengths, whole)
    seq_begin = jnp.arange(whole, dtype=jnp.int32) - token_place
    start_column = jnp.broadcast_to(seq_begin[:, None], (whole, LANES))
    start_row = jnp.broadcast_to(seq_begin[None, :], (8, whole))
    half_dim = HEAD_DIM // 2
    lane = jnp.arange(LANES, dtype=jnp.int32)
    frequency = jnp.exp((lane % half_dim).astype(jnp.float32) * (-math.log(10000.0) / half_dim))
    angles = token_place.astype(jnp.float32)[:, None] * frequency[None, :]
    cos_table = jnp.cos(angles)
    sin_table = jnp.sin(angles) * jnp.where(lane % HEAD_DIM < half_dim, -1.0, 1.0)[None, :]
    grad_history, past_sum, sums_past = past(dwa_weights, history[:, 0], cotangent[0])

    input_half = jnp.where(same, layer_input[0], input_got)
    layer_rows = ordered(input_half, swap_near(input_half), near == 0)
    early_near = swap_diagonal(early_near)
    layer_rows, *ready = lax.optimization_barrier(
        (layer_rows, late_got, last_near, gain_one, bias_one, gain_two, bias_two, own_weight)
        + (past_sum, cos_table, sin_table, start_column, start_row)
    )
    late_got, last_near, gain_one, bias_one, gain_two, bias_two, own_weight = ready[:7]
    past_sum, cos_table, sin_table, start_column, start_row = ready[7:]

    projected, norm_one_t, weight_qkv = project(
        flags, layer_rows, gain_one, bias_one, cos_table, sin_table, w_qkv, qkv_got
    )
    pairs = projected.shape[2] // LANES
    mixed = attend(0, start_column, projected, None, LONGEST)
    last_got = swap_diagonal(last_near)
    early_far = swap_far_away(early_near)
    for pair in range(1, pairs):
        mixed = attend(pair, start_column, projected, mixed, LONGEST)
    late_got = swap_diagonal(after(late_got, mixed))
    last_got = jnp.where(same, last_near, last_got)
    weight_out = last_got[: w_out.shape[0]]
    attn = jnp.dot(mixed, weight_out, preferred_element_type=jnp.float32).astype(jnp.bfloat16)
    attn_got = swap_near(attn)
    cot_half = last_got[w_out.shape[0] :]
    cot_rows = ordered(cot_half, swap_near(cot_half), near == 0)
    head = (own_weight, layer_rows, attn, attn_got, cot_rows, gain_two, bias_two)
    *kept, act_early, early_pieces, down_early = feed(
        True, flags, head, w_up, w_down, early_near, early_far
    )
    back, act_late, late_pieces, down_late = feed(False, flags, kept, w_up, w_down, late_got)
    early_sum = scatter_plane(after(early_pieces, late_got))
    late_sum = scatter_plane(late_pieces)
    back_got = swap_near(back)
    grad_attn, grad_mixed, grad_out, sums_two = middle(
        flags,
        own_weight,
        layer_rows,
        attn,
        attn_got,
        cot_rows,
        back,
        back_got,
        gain_two,
        mixed,
        weight_out,
    )

    grad_qkv = attend_back(0, start_row, cos_table, sin_table, projected, grad_mixed, None, LONGEST)
    for pair in range(1, pairs):
        grad_qkv = attend_back(
            pair, start_row, cos_table, sin_table, projected, grad_mixed, grad_qkv, LONGEST
        )
    key_keep, key_send, late_pieces = weigh(flags, norm_one_t, grad_qkv, grad_out)
    key_got = swap_far(key_send)
    late_got = swap_diagonal(late_pieces)
    keep, send = unproject(flags, after(grad_qkv, key_keep), weight_qkv)
    send_got = swap_near(send)
    block_keep, block_send = lower(
        flags, after(act_early, send), act_late, down_early, down_late, layer_rows, attn, attn_got
    )
    block_got = swap_near(block_send)
    key_pair = add(key_keep, after(key_got, block_send))
    key_moved = swap_diagonal(key_pair)
    late_pair = jnp.where(same, late_pieces, late_got)
    late_other = swap_near(take(late_pair, 1 - near))
    input_grad, sums_one = first_norm_back(
        flags, layer_rows, after(keep, key_pair), send_got, grad_attn, gain_one
    )
    grad_input = swap_diagonal(input_grad)
    block_half = add(block_keep, after(block_got, input_grad))
    block_moved = swap_diagonal(block_half)
    feed_sum = scatter_rows(jnp.concatenate([after(early_sum, input_grad), late_sum], axis=1))
    late_one = scatter_rows(add(take(late_pair, near), after(late_other, input_grad)))
    dps = lax.axis_size("dp")
    key_pair = jnp.where(same, key_pair, key_moved)
    key_pair = key_pair.reshape(dps, key_pair.shape[0] // dps, key_pair.shape[1])
    key_one = add(part_of(key_pair, near, 1), swap_near(part_of(key_pair, 1 - near, 1)))
    key_one = scatter_rows(key_one.reshape(-1, key_one.shape[2]))
    output, sums_now = present(
        flags, own_weight, past_sum, cotangent[0], block_half, after(block_moved, key_pair)
    )
    small = jnp.concatenate(
        [sums_one[:2], sums_two[:2], sums_past[:hist_count], sums_now[:1]], axis=0
    )
    small = sum_everywhere(small)
    feed_sum = after(feed_sum, small).reshape(feed_sum.shape[0], 2, -1).transpose(1, 0, 2)
    feed_all = gather(feed_sum, part, far, same)
    late_one = add(late_one, swap_far(late_one))
    grad_value_out = ordered(late_one[None], swap_near(late_one)[None], near == 0)
    key_half = ordered(key_one, swap_near(key_one), near == 0)
    grad_query_key = ordered(key_half[None], swap_far(key_half)[None], far == 0)

    def columns_of(pieces):
        return pieces.transpose(2, 1, 0, 3).reshape(pieces.shape[2], -1).astype(jnp.float32)

    return (
        output[None],
        jnp.where(same, input_grad, grad_input)[None],
        grad_history[:, None],
        jnp.sum(small[4:], axis=1),
        small[0],
        small[1],
        jnp.concatenate([grad_query_key, grad_value_out[:1]], axis=0).astype(jnp.float32),
        grad_value_out[1].astype(jnp.float32).T,
        small[2],
        small[3],
        columns_of(feed_all[:, 0]),
        columns_of(feed_all[:, 1]).T,
    )


def positions(seq_lengths, token_count):
    seq_ends = jnp.cumsum(seq_lengths)
    seq_starts = seq_ends - seq_lengths
    token_index = jnp.arange(token_count, dtype=jnp.int32)
    seq_owner = jnp.sum((token_index[:, None] >= seq_ends[None, :]).astype(jnp.int32), axis=1)
    picked = (
        seq_owner[:, None] == jnp.arange(seq_lengths.shape[0], dtype=jnp.int32)[None, :]
    ).astype(jnp.int32)
    seq_begin = jnp.sum(picked * seq_starts[None, :], axis=1)
    return (seq_owner, token_index - seq_begin)


def solution(mesh):
    tps, dps, reps = (mesh.shape[name] for name in ("tp", "dp", "rep"))
    split = Mesh(mesh.devices.reshape(tps, dps, reps // 2, 2), AXES)
    in_specs = (
        P(("dp", "far", "near"), "tp", None),
        P(None, ("dp", "far", "near"), "tp", None),
        P(("dp", "far", "near"), "tp", None),
        P(("dp", "far", "near"), None),
        P(),
        P(),
        P(),
        P(None, None, "tp"),
        P("tp", None),
        P(),
        P(),
        P(None, "tp"),
        P("tp", None),
    )
    out_specs = (
        P(("dp", "far", "near"), "tp", None),
        P(("dp", "far", "near"), "tp", None),
        P(None, ("dp", "far", "near"), "tp", None),
        P(),
        P(),
        P(),
        P(None, "dp", "tp"),
        P("tp", "dp"),
        P(),
        P(),
        P("dp", "tp"),
        P("tp", "dp"),
    )
    return jax.shard_map(local, mesh=split, in_specs=in_specs, out_specs=out_specs, check_vma=False)
```

```python
import functools
import itertools
import math

import jax
import jax.numpy as jnp
from jax import lax
from jax.experimental import pallas as pl
from jax.experimental.pallas import tpu as pltpu
from jax.sharding import Mesh, PartitionSpec as P

HEAD_DIM = 64
LONGEST = 512
NEG_FILL = -1e30
NORM_EPS = 1e-05
RATE = 3e6
ROOM = 60 << 20


def lasting(microseconds):
    return pl.CostEstimate(flops=0, transcendentals=0, bytes_accessed=int(microseconds * RATE))


BLOCK = 256
LANES = 128
NT = (((1,), (1,)), ((), ()))


def dot(a, b, dims=(((1,), (0,)), ((), ()))):
    return lax.dot_general(a, b, dims, preferred_element_type=jnp.float32)


def spans(whole, reach):
    back = -(-(reach - 1) // BLOCK)
    runs = []
    for i in range(whole // BLOCK):
        count = min(i, back) + 1
        if runs and runs[-1][2] == count:
            runs[-1][1] = i + 1
        else:
            runs.append([i, i + 1, count])
    return runs


def each_block(whole, reach, body):
    for first, last, count in spans(whole, reach):
        def step(at, carry, first=first, count=count):
            i = first + at // 2
            body(i, i + 1 - count, count * BLOCK, at % 2)
            return carry
        lax.fori_loop(0, 2 * (last - first), step, 0)


def attend_kernel(reach, start_ref, q_ref, k_ref, v_ref, out_ref, acc_ref):
    whole = q_ref.shape[0]
    lane = lax.broadcasted_iota(jnp.int32, (BLOCK, LANES), 1) // HEAD_DIM

    def body(i, first, count, head):
        at = pl.ds(pl.multiple_of(i * BLOCK, BLOCK), BLOCK)
        keys = pl.ds(pl.multiple_of(first * BLOCK, BLOCK), count)
        query = q_ref[at, :] * (HEAD_DIM**-0.5)
        query = jnp.where(lane == head, query, jnp.zeros_like(query))
        scores = dot(query, k_ref[keys, :], NT)
        key_at = first * BLOCK + lax.broadcasted_iota(jnp.int32, scores.shape, 1)
        query_at = i * BLOCK + lax.broadcasted_iota(jnp.int32, scores.shape, 0)
        allowed = (key_at >= start_ref[at, :1]) & (key_at <= query_at)
        scores = jnp.where(allowed, scores, NEG_FILL)
        exponent = jnp.exp(scores - jnp.max(scores, axis=1, keepdims=True))
        row_sum = jnp.sum(exponent, axis=1, keepdims=True)
        probs = (exponent * (1.0 / row_sum)).astype(jnp.bfloat16)
        mixed = dot(probs, v_ref[keys, :])

        @pl.when(head == 0)
        def _():
            acc_ref[...] = mixed

        @pl.when(head == 1)
        def _():
            out_ref[at, :] = jnp.where(lane == 0, acc_ref[...], mixed).astype(out_ref.dtype)

    each_block(whole, reach, body)


def attend(pair, start_column, projected, so_far, reach):
    count, whole, width = projected.shape

    def block(c):
        return pl.BlockSpec((None, whole, LANES), lambda i: (c, 0, pair))

    begun = [] if so_far is None else [so_far]
    kernel = attend_kernel if so_far is None else lambda reach, unused, *refs: attend_kernel(reach, *refs)
    return pl.pallas_call(
        functools.partial(kernel, reach),
        grid=(1,),
        in_specs=[pl.BlockSpec(memory_space=pl.ANY)] * len(begun)
        + [pl.BlockSpec((whole, LANES), lambda i: (0, 0)), block(0), block(1), block(2)],
        out_specs=pl.BlockSpec((whole, LANES), lambda i: (0, pair)),
        out_shape=jax.ShapeDtypeStruct((whole, width), jnp.bfloat16),
        scratch_shapes=[pltpu.VMEM((BLOCK, LANES), jnp.float32)],
        input_output_aliases={0: 0} if begun else {},
        compiler_params=pltpu.CompilerParams(vmem_limit_bytes=ROOM),
        cost_estimate=lasting(5),
    )(*begun, start_column, projected, projected, projected)


def turn_back(field, cos, sin):
    half = HEAD_DIM // 2
    lane = lax.broadcasted_iota(jnp.int32, field.shape, 1) % HEAD_DIM
    crossed = jnp.where(lane < half, pltpu.roll(field, LANES - half, 1), pltpu.roll(field, half, 1))
    return field * cos - crossed * sin


def attend_back_kernel(
    reach, start_ref, cos_ref, sin_ref, q_ref, k_ref, v_ref, g_ref, out_ref,
    key_acc, value_acc, query_acc,
):
    whole = q_ref.shape[0]
    lane = lax.broadcasted_iota(jnp.int32, (BLOCK, LANES), 1) // HEAD_DIM
    key_acc[...] = jnp.zeros_like(key_acc)
    value_acc[...] = jnp.zeros_like(value_acc)

    def body(i, first, count, head):
        at = pl.ds(pl.multiple_of(i * BLOCK, BLOCK), BLOCK)
        span = pl.ds(pl.multiple_of(first * BLOCK, BLOCK), count)
        query = q_ref[at, :] * (HEAD_DIM**-0.5)
        query = jnp.where(lane == head, query, jnp.zeros_like(query))
        grad = g_ref[at, :]
        grad = jnp.where(lane == head, grad, jnp.zeros_like(grad))
        keys = k_ref[span, :]
        scores = dot(keys, query, NT)
        key_at = first * BLOCK + lax.broadcasted_iota(jnp.int32, scores.shape, 0)
        query_at = i * BLOCK + lax.broadcasted_iota(jnp.int32, scores.shape, 1)
        allowed = (key_at >= start_ref[:1, at]) & (key_at <= query_at)
        scores = jnp.where(allowed, scores, NEG_FILL)
        exponent = jnp.exp(scores - jnp.max(scores, axis=0, keepdims=True))
        probs = exponent * (1.0 / jnp.sum(exponent, axis=0, keepdims=True))
        value_acc[span, :] += dot(probs.astype(jnp.bfloat16), grad)
        grad_probs = dot(v_ref[span, :], grad, NT)
        weighted = probs * grad_probs
        grad_scores = (weighted - probs * jnp.sum(weighted, axis=0, keepdims=True)).astype(jnp.bfloat16)
        key_acc[span, :] += dot(grad_scores, query)
        here = dot(grad_scores, keys, (((0,), (0,)), ((), ())))

        @pl.when(head == 0)
        def _():
            query_acc[...] = here

        @pl.when(head == 1)
        def _():
            both = jnp.where(lane == 0, query_acc[...], here) * (HEAD_DIM**-0.5)
            out_ref[0, at, :] = turn_back(both, cos_ref[at, :], sin_ref[at, :]).astype(out_ref.dtype)

    each_block(whole, reach, body)

    def finish(i, carry):
        at = pl.ds(pl.multiple_of(i * BLOCK, BLOCK), BLOCK)
        out_ref[1, at, :] = turn_back(key_acc[at, :], cos_ref[at, :], sin_ref[at, :]).astype(out_ref.dtype)
        out_ref[2, at, :] = value_acc[at, :].astype(out_ref.dtype)
        return carry

    lax.fori_loop(0, whole // BLOCK, finish, 0)


def attend_back(pair, start_row, cos, sin, projected, grad_mixed, so_far, reach):
    count, whole, width = projected.shape

    def block(c):
        return pl.BlockSpec((None, whole, LANES), lambda i: (c, 0, pair))

    table = pl.BlockSpec((whole, LANES), lambda i: (0, 0))
    begun = [] if so_far is None else [so_far]
    kernel = attend_back_kernel if so_far is None else lambda reach, unused, *refs: attend_back_kernel(reach, *refs)
    return pl.pallas_call(
        functools.partial(kernel, reach),
        grid=(1,),
        in_specs=[pl.BlockSpec(memory_space=pl.ANY)] * len(begun)
        + [
            pl.BlockSpec((8, whole), lambda i: (0, 0)),
            table,
            table,
            block(0),
            block(1),
            block(2),
            pl.BlockSpec((whole, LANES), lambda i: (0, pair)),
        ],
        out_specs=pl.BlockSpec((count, whole, LANES), lambda i: (0, 0, pair)),
        out_shape=jax.ShapeDtypeStruct((count, whole, width), jnp.bfloat16),
        scratch_shapes=[
            pltpu.VMEM((whole, LANES), jnp.float32),
            pltpu.VMEM((whole, LANES), jnp.float32),
            pltpu.VMEM((BLOCK, LANES), jnp.float32),
        ],
        input_output_aliases={0: 0} if begun else {},
        compiler_params=pltpu.CompilerParams(vmem_limit_bytes=ROOM),
        cost_estimate=lasting(9),
    )(*begun, start_row, cos, sin, projected, projected, projected, grad_mixed)


ROWS = 256


def norm_parts(field):
    centered = field - jnp.mean(field, axis=-1, keepdims=True)
    scale = lax.rsqrt(jnp.mean(centered * centered, axis=-1, keepdims=True) + NORM_EPS)
    return centered * scale, scale


def wide(ref, at):
    return ref[at, :].astype(jnp.float32)


def row_blocks(count, body):
    def step(i, carry):
        body(i, pl.ds(pl.multiple_of(i * ROWS, ROWS), ROWS))
        return carry

    lax.fori_loop(0, count // ROWS, step, 0)


def whole_spec(shape):
    return pl.BlockSpec(shape, lambda *at: (0,) * len(shape))


def turn(field, cos, sin):
    half = HEAD_DIM // 2
    lane = lax.broadcasted_iota(jnp.int32, field.shape, 1) % HEAD_DIM
    crossed = jnp.where(lane < half, pltpu.roll(field, LANES - half, 1), pltpu.roll(field, half, 1))
    return field * cos + crossed * sin


def project_kernel(
    flags, rows_ref, vectors, cos_ref, sin_ref, w_own, w_got, out_ref, turned_ref,
    weight_ref, norm_ref,
):
    whole = rows_ref.shape[0]
    step = pl.program_id(0)

    @pl.when(step == 0)
    def _():
        def body(i, at):
            unit, unused = norm_parts(wide(rows_ref, at))
            norm = unit * vectors[0:1, :] + vectors[1:2, :]
            norm_ref[at, :] = norm.astype(jnp.bfloat16)
            turned_ref[:, at] = norm.T.astype(jnp.bfloat16)

        row_blocks(whole, body)

    weight_ref[0] = jnp.where(flags[0] == 1, w_own[0], w_got[0])

    def body(i, at):
        field = dot(norm_ref[at, :], weight_ref[0])

        @pl.when(step < 2)
        def _():
            for p in range(field.shape[1] // LANES):
                lanes = slice(p * LANES, (p + 1) * LANES)
                out_ref[0, at, lanes] = turn(field[:, lanes], cos_ref[at, :], sin_ref[at, :]).astype(
                    jnp.bfloat16
                )

        @pl.when(step == 2)
        def _():
            out_ref[0, at, :] = field.astype(jnp.bfloat16)

    row_blocks(whole, body)


def project(flags, rows, vectors, cos, sin, w_own, w_got):
    whole, width = rows.shape
    count, unused, columns = w_own.shape
    weight = pl.BlockSpec((1, width, columns), lambda c, flags: (c, 0, 0))
    return pl.pallas_call(
        project_kernel,
        grid_spec=pltpu.PrefetchScalarGridSpec(
            num_scalar_prefetch=1,
            grid=(count,),
            in_specs=[
                whole_spec((whole, width)),
                whole_spec(vectors.shape),
                whole_spec((whole, LANES)),
                whole_spec((whole, LANES)),
                weight,
                weight,
            ],
            out_specs=[
                pl.BlockSpec((1, whole, columns), lambda c, flags: (c, 0, 0)),
                whole_spec((width, whole)),
                weight,
            ],
            scratch_shapes=[pltpu.VMEM((whole, width), jnp.bfloat16)],
        ),
        out_shape=[
            jax.ShapeDtypeStruct((count, whole, columns), jnp.bfloat16),
            jax.ShapeDtypeStruct((width, whole), jnp.bfloat16),
            jax.ShapeDtypeStruct(w_own.shape, jnp.bfloat16),
        ],
        compiler_params=pltpu.CompilerParams(vmem_limit_bytes=ROOM),
        cost_estimate=lasting(9),
    )(flags, rows, vectors, cos, sin, w_own, w_got)


HIDDEN = 256


def gelu_both(up):
    root = math.sqrt(2.0 / math.pi)
    square = up * up
    bent = jnp.tanh(root * up * (1.0 + 0.044715 * square))
    half = 0.5 * (1.0 + bent)
    slope = half + 0.5 * up * (1.0 - bent * bent) * (root * (1.0 + 3.0 * 0.044715 * square))
    return up * half, slope


def feed_kernel(early, flags, *refs):
    if early:
        weight_ref, rows_ref, own_ref, got_ref, cot_ref, vectors = refs[:6]
        up_own, down_own, got, norm, norm_t, grad, grad_t = refs[6:13]
    else:
        norm, norm_t, grad, grad_t, back_early, up_own, down_own, got = refs[:8]
    back_ref, act_ref, pieces_ref, down_ref, slope, up_w = refs[-6:]
    whole, width = norm.shape
    part = pieces_ref.shape[2]
    step = pl.program_id(0)

    @pl.when(step == 0)
    def _():
        up_w[...] = jnp.where(flags[0] == 1, up_own[...], got[:width])
        down_ref[...] = jnp.where(flags[0] == 1, down_own[...], got[width:])
        if early:

            def body(i, at):
                unit, unused = norm_parts(wide(rows_ref, at) + wide(own_ref, at) + wide(got_ref, at))
                field = unit * vectors[2:3, :] + vectors[3:4, :]
                norm[at, :] = field.astype(jnp.bfloat16)
                norm_t[:, at] = field.T.astype(jnp.bfloat16)
                field = wide(cot_ref, at) * weight_ref[weight_ref.shape[0] - 1]
                grad[at, :] = field.astype(jnp.bfloat16)
                grad_t[:, at] = field.T.astype(jnp.bfloat16)

            row_blocks(whole, body)

    hidden = pl.ds(pl.multiple_of(step * HIDDEN, HIDDEN), HIDDEN)
    up_block = up_w[:, hidden]
    down_block = down_ref[hidden, :]

    def body(i, at):
        value, rise = gelu_both(dot(norm[at, :], up_block))
        act_ref[at, :] = value.astype(jnp.bfloat16)
        slope[at, hidden] = (dot(grad[at, :], down_block, NT) * rise).astype(jnp.bfloat16)

    row_blocks(whole, body)

    def grads(i, at):
        fields = (dot(norm_t[at, :], slope[:, hidden]), dot(grad_t[at, :], act_ref[...]))
        for k, field in enumerate(fields):
            field = field.astype(jnp.bfloat16)
            for j in range(2 * part // HIDDEN):

                @pl.when(step == j)
                def _():
                    for p in range(2):
                        first, last = max(p * part, j * HIDDEN), min((p + 1) * part, (j + 1) * HIDDEN)
                        if first < last:
                            pieces_ref[2 * k + p, at, first - p * part : last - p * part] = field[
                                :, first - j * HIDDEN : last - j * HIDDEN
                            ]

    row_blocks(width, grads)

    @pl.when(step == pl.num_programs(0) - 1)
    def _():
        def body(i, at):
            back = dot(slope[at, :], up_w[...], NT)
            if not early:
                back = back + back_early[at, :]
            back_ref[at, :] = back.astype(back_ref.dtype)

        row_blocks(whole, body)


def feed(early, flags, head, w_up, w_down, got):
    whole, width = head[1].shape if early else head[0].shape
    hidden = w_up.shape[1] // 2
    steps = hidden // HIDDEN
    tokens = whole_spec((whole, width))
    turned = whole_spec((width, whole))
    index = 0 if early else 1
    low = jax.ShapeDtypeStruct((whole, width), jnp.bfloat16)
    low_turned = jax.ShapeDtypeStruct((width, whole), jnp.bfloat16)
    full = jax.ShapeDtypeStruct((whole, width), jnp.float32)
    if early:
        head_specs = [pl.BlockSpec(memory_space=pltpu.SMEM)] + [tokens] * 4
        head_specs = head_specs + [whole_spec(head[-1].shape)]
    else:
        head_specs = [tokens, turned, tokens, turned, tokens]
    return pl.pallas_call(
        functools.partial(feed_kernel, early),
        grid_spec=pltpu.PrefetchScalarGridSpec(
            num_scalar_prefetch=1,
            grid=(steps,),
            in_specs=head_specs
            + [
                pl.BlockSpec((width, hidden), lambda j, flags: (0, index)),
                pl.BlockSpec((hidden, width), lambda j, flags: (index, 0)),
                whole_spec(got.shape),
            ],
            out_specs=([tokens, turned, tokens, turned] if early else [])
            + [
                tokens,
                pl.BlockSpec((whole, HIDDEN), lambda j, flags: (0, j)),
                whole_spec((4, width, hidden // 2)),
                whole_spec((hidden, width)),
            ],
            scratch_shapes=[
                pltpu.VMEM((whole, hidden), jnp.bfloat16),
                pltpu.VMEM((width, hidden), jnp.bfloat16),
            ],
        ),
        out_shape=([low, low_turned, low, low_turned, full] if early else [low])
        + [
            jax.ShapeDtypeStruct((whole, hidden), jnp.bfloat16),
            jax.ShapeDtypeStruct((4, width, hidden // 2), jnp.bfloat16),
            jax.ShapeDtypeStruct((hidden, width), jnp.bfloat16),
        ],
        compiler_params=pltpu.CompilerParams(vmem_limit_bytes=ROOM),
        cost_estimate=lasting(20),
    )(flags, *head, w_up, w_down, got)


def lower_kernel(flags, act_early, act_late, early_ref, late_ref, rows_ref, own_ref, got_ref, keep_ref, send_ref):
    half = keep_ref.shape[0]
    first, second = early_ref[...], late_ref[...]

    def at_rows(near, i):
        return pl.ds(pl.multiple_of(near * half + i * ROWS, ROWS), ROWS)

    def send(i, at):
        here = at_rows(1 - flags[1], i)
        total = dot(act_early[here, :], first) + dot(act_late[here, :], second)
        send_ref[at, :] = total.astype(jnp.bfloat16)

    def keep(i, at):
        here = at_rows(flags[1], i)
        total = dot(act_early[here, :], first) + dot(act_late[here, :], second)
        keep_ref[at, :] = total + wide(rows_ref, here) + wide(own_ref, here) + wide(got_ref, here)

    row_blocks(half, send)
    row_blocks(half, keep)


def lower(flags, act_early, act_late, down_early, down_late, rows, own, got):
    whole, hidden = act_early.shape
    width = rows.shape[1]
    half = whole_spec((whole // 2, width))
    return pl.pallas_call(
        lower_kernel,
        grid_spec=pltpu.PrefetchScalarGridSpec(
            num_scalar_prefetch=1,
            grid=(1,),
            in_specs=[whole_spec((whole, hidden))] * 2
            + [whole_spec((hidden, width))] * 2
            + [whole_spec((whole, width))] * 3,
            out_specs=[half, half],
        ),
        out_shape=[
            jax.ShapeDtypeStruct((whole // 2, width), jnp.float32),
            jax.ShapeDtypeStruct((whole // 2, width), jnp.bfloat16),
        ],
        compiler_params=pltpu.CompilerParams(vmem_limit_bytes=ROOM),
        cost_estimate=lasting(7),
    )(flags, act_early, act_late, down_early, down_late, rows, own, got)


def middle_kernel(
    flags, weight_ref, rows_ref, own_ref, got_ref, cot_ref, back_own, back_got, vectors, mixed_ref,
    w_ref, grad_ref, gmixed_ref, gout_ref, sums_ref, turned,
):
    whole, width = rows_ref.shape
    weight = w_ref[...]
    gain = vectors[2:3, :]
    sums_ref[...] = jnp.zeros_like(sums_ref)

    def body(i, at):
        unit, scale = norm_parts(wide(rows_ref, at) + wide(own_ref, at) + wide(got_ref, at))
        back = wide(back_own, at) + wide(back_got, at)
        inner = back * gain
        mean = jnp.mean(inner, axis=-1, keepdims=True)
        slant = jnp.mean(inner * unit, axis=-1, keepdims=True)
        grad = wide(cot_ref, at) * weight_ref[weight_ref.shape[0] - 1] + scale * (inner - mean - unit * slant)
        low = grad.astype(jnp.bfloat16)
        grad_ref[at, :] = low
        turned[:, at] = grad.T.astype(jnp.bfloat16)
        gmixed_ref[at, :] = dot(low, weight, NT).astype(jnp.bfloat16)

        @pl.when((i * ROWS) // (whole // 2) == flags[1])
        def _():
            sums_ref[0:1, :] += jnp.sum(back * unit, axis=0, keepdims=True)
            sums_ref[1:2, :] += jnp.sum(back, axis=0, keepdims=True)

    row_blocks(whole, body)

    def grads(i, at):
        gout_ref[at, :] = dot(turned[at, :], mixed_ref[...]).astype(jnp.bfloat16)

    row_blocks(width, grads)


def middle(flags, weight, rows, own, got, cot, back_own, back_got, vectors, mixed, w_out):
    whole, width = rows.shape
    columns = mixed.shape[1]
    tokens = whole_spec((whole, width))
    narrow = whole_spec((whole, columns))
    projection = whole_spec((columns, width))
    return pl.pallas_call(
        middle_kernel,
        grid_spec=pltpu.PrefetchScalarGridSpec(
            num_scalar_prefetch=1,
            grid=(1,),
            in_specs=[pl.BlockSpec(memory_space=pltpu.SMEM)]
            + [tokens] * 6
            + [whole_spec(vectors.shape), narrow, projection],
            out_specs=[tokens, narrow, whole_spec((width, columns)), whole_spec((8, width))],
            scratch_shapes=[pltpu.VMEM((width, whole), jnp.bfloat16)],
        ),
        out_shape=[
            jax.ShapeDtypeStruct((whole, width), jnp.bfloat16),
            jax.ShapeDtypeStruct((whole, columns), jnp.bfloat16),
            jax.ShapeDtypeStruct((width, columns), jnp.bfloat16),
            jax.ShapeDtypeStruct((8, width), jnp.float32),
        ],
        compiler_params=pltpu.CompilerParams(vmem_limit_bytes=ROOM),
        cost_estimate=lasting(12),
    )(flags, weight, rows, own, got, cot, back_own, back_got, vectors, mixed, w_out)


def weigh_kernel(flags, turned_ref, grad_ref, out_grad_ref, *out_refs):
    last = grad_ref.shape[0]

    def grads(i, at):
        for j, out_ref in enumerate(out_refs):
            piece = flags[3 + j]

            @pl.when(piece < last)
            def _():
                out_ref[at, :] = dot(turned_ref[at, :], grad_ref[jnp.minimum(piece, last - 1)]).astype(
                    jnp.bfloat16
                )

            @pl.when(piece == last)
            def _():
                out_ref[at, :] = out_grad_ref[at, :]

    row_blocks(turned_ref.shape[0], grads)


def weigh(flags, turned, grad, out_grad):
    width, whole = turned.shape
    columns = grad.shape[2]
    piece = whole_spec((width, columns))
    return pl.pallas_call(
        weigh_kernel,
        grid_spec=pltpu.PrefetchScalarGridSpec(
            num_scalar_prefetch=1,
            grid=(1,),
            in_specs=[whole_spec((width, whole)), whole_spec(grad.shape), piece],
            out_specs=[piece] * 4,
        ),
        out_shape=[jax.ShapeDtypeStruct((width, columns), jnp.bfloat16)] * 4,
        compiler_params=pltpu.CompilerParams(vmem_limit_bytes=ROOM),
        cost_estimate=lasting(3),
    )(flags, turned, grad, out_grad)


def unproject_kernel(flags, grad_ref, weight, keep_ref, send_ref):
    half = keep_ref.shape[0]

    def side(near, out_ref):
        def body(i, at):
            from_rows = pl.ds(pl.multiple_of(near * half + i * ROWS, ROWS), ROWS)
            total = dot(grad_ref[0, from_rows, :], weight[0], NT)
            for c in range(1, grad_ref.shape[0]):
                total = total + dot(grad_ref[c, from_rows, :], weight[c], NT)
            out_ref[at, :] = total.astype(out_ref.dtype)

        row_blocks(half, body)

    side(1 - flags[1], send_ref)
    side(flags[1], keep_ref)


def unproject(flags, grad, weight):
    count, whole, columns = grad.shape
    width = weight.shape[1]
    half = whole_spec((whole // 2, width))
    return pl.pallas_call(
        unproject_kernel,
        grid_spec=pltpu.PrefetchScalarGridSpec(
            num_scalar_prefetch=1,
            grid=(1,),
            in_specs=[whole_spec(grad.shape), whole_spec((count, width, columns))],
            out_specs=[half, half],
        ),
        out_shape=[
            jax.ShapeDtypeStruct((whole // 2, width), jnp.float32),
            jax.ShapeDtypeStruct((whole // 2, width), jnp.bfloat16),
        ],
        compiler_params=pltpu.CompilerParams(vmem_limit_bytes=ROOM),
        cost_estimate=lasting(4),
    )(flags, grad, weight)


def last_kernel(
    flags, rows_ref, keep_ref, got_ref, resid_ref, vectors, block_keep, block_got, cot_ref, out_ref, sums_ref
):
    sums_ref[...] = jnp.zeros_like(sums_ref)

    def body(i, at):
        unit, scale = norm_parts(wide(rows_ref, at))
        back = keep_ref[at, :] + wide(got_ref, at)
        inner = back * vectors[0:1, :]
        mean = jnp.mean(inner, axis=-1, keepdims=True)
        slant = jnp.mean(inner * unit, axis=-1, keepdims=True)
        grad = wide(resid_ref, at) + scale * (inner - mean - unit * slant)
        out_ref[0, at, :] = grad.astype(jnp.bfloat16)
        block = block_keep[at, :] + wide(block_got, at)
        out_ref[1, at, :] = block.astype(jnp.bfloat16)
        sums_ref[0:1, :] += jnp.sum(back * unit, axis=0, keepdims=True)
        sums_ref[1:2, :] += jnp.sum(back, axis=0, keepdims=True)
        sums_ref[2:3, :] += jnp.sum(block * wide(cot_ref, at), axis=0, keepdims=True)

    row_blocks(rows_ref.shape[0], body)


def last(flags, rows, keep, got, resid, vectors, block_keep, block_got, cot):
    half, width = keep.shape
    mine = pl.BlockSpec((half, width), lambda i, flags: (flags[1], 0))
    tokens = whole_spec((half, width))
    return pl.pallas_call(
        last_kernel,
        grid_spec=pltpu.PrefetchScalarGridSpec(
            num_scalar_prefetch=1,
            grid=(1,),
            in_specs=[mine, tokens, tokens, mine, whole_spec(vectors.shape), tokens, tokens, mine],
            out_specs=[whole_spec((2, half, width)), whole_spec((8, width))],
        ),
        out_shape=[
            jax.ShapeDtypeStruct((2, half, width), jnp.bfloat16),
            jax.ShapeDtypeStruct((8, width), jnp.float32),
        ],
        compiler_params=pltpu.CompilerParams(vmem_limit_bytes=ROOM),
        cost_estimate=lasting(3),
    )(flags, rows, keep, got, resid, vectors, block_keep, block_got, cot)


def past_kernel(dwa_ref, hist_ref, cot_ref, grad_ref, part_ref, sums_ref):
    @pl.when(pl.program_id(0) == 0)
    def _():
        sums_ref[...] = jnp.zeros_like(sums_ref)

    grad = cot_ref[...].astype(jnp.float32)
    total = jnp.zeros_like(grad)
    for j in range(hist_ref.shape[0]):
        field = hist_ref[j].astype(jnp.float32)
        total += dwa_ref[j] * field
        grad_ref[j] = (dwa_ref[j] * grad).astype(jnp.bfloat16)
        sums_ref[j : j + 1, :] += jnp.sum(field * grad, axis=0, keepdims=True)
    part_ref[...] = total


def past(dwa, history, cot):
    count, rows, width = history.shape
    layers = pl.BlockSpec((count, ROWS, width), lambda i: (0, i, 0))
    tokens = pl.BlockSpec((ROWS, width), lambda i: (i, 0))
    return pl.pallas_call(
        past_kernel,
        grid=(rows // ROWS,),
        in_specs=[pl.BlockSpec(memory_space=pltpu.SMEM), layers, tokens],
        out_specs=[layers, tokens, whole_spec((8, width))],
        out_shape=[
            jax.ShapeDtypeStruct(history.shape, jnp.bfloat16),
            jax.ShapeDtypeStruct((rows, width), jnp.float32),
            jax.ShapeDtypeStruct((8, width), jnp.float32),
        ],
        compiler_params=pltpu.CompilerParams(vmem_limit_bytes=ROOM),
        cost_estimate=lasting(3),
    )(dwa, history, cot)


def present_kernel(flags, weight_ref, part_ref, own_ref, got_ref, out_ref, grad_ref):
    here = jnp.where(flags[0] == 1, own_ref[1], got_ref[1]).astype(jnp.float32)
    out_ref[...] = (part_ref[...] + weight_ref[weight_ref.shape[0] - 1] * here).astype(jnp.bfloat16)
    grad_ref[...] = jnp.where(flags[0] == 1, own_ref[0], got_ref[0])


def present(flags, weight, part, own, got):
    rows, width = part.shape
    scalars = pl.BlockSpec(memory_space=pltpu.SMEM)
    tokens = pl.BlockSpec((ROWS, width), lambda i: (i, 0))
    both = pl.BlockSpec((2, ROWS, width), lambda i: (0, i, 0))
    return pl.pallas_call(
        present_kernel,
        grid=(rows // ROWS,),
        in_specs=[scalars, scalars, tokens, both, both],
        out_specs=[tokens, tokens],
        out_shape=[jax.ShapeDtypeStruct((rows, width), jnp.bfloat16)] * 2,
        compiler_params=pltpu.CompilerParams(vmem_limit_bytes=ROOM),
        cost_estimate=lasting(2),
    )(flags, weight, part, own, got)


AXES = ("tp", "dp", "far", "near")


def moves(chosen, move):
    sizes = [lax.axis_size(name) for name in AXES]
    places = [place for place in itertools.product(*map(range, sizes)) if chosen(*place)]
    index = lambda place: functools.reduce(lambda at, step: at * step[0] + step[1], zip(sizes, place), 0)
    return [(index(place), index(move(*place))) for place in places]


def away(t, d, k, c):
    return t != c


def anyone(t, d, k, c):
    return True


def home(t, d, k, c):
    return t == c


def swap_diagonal(field):
    return lax.ppermute(field, AXES, moves(away, lambda t, d, k, c: (c, d, k, t)))


def send_to_owner(field, other_far, other_tp):
    return lax.ppermute(
        field,
        AXES,
        moves(
            away if not other_far and not other_tp else anyone,
            lambda t, d, k, c: (c, d, k ^ other_far, t ^ other_tp),
        ),
    )


def bring_home(field):
    return lax.ppermute(field, AXES, moves(away, lambda t, d, k, c: (c, d, k, c)))


def swap_far_home(field):
    return lax.ppermute(field, AXES, moves(home, lambda t, d, k, c: (t, d, 1 - k, c)))


def swap_far(field):
    return lax.ppermute(field, "far", [(0, 1), (1, 0)])


def swap_near(field):
    return lax.ppermute(field, "near", [(0, 1), (1, 0)])


def after(field, *others):
    return lax.optimization_barrier((field, *others))[0]


def ordered(own, other, first, axis=0):
    return jnp.where(
        first, jnp.concatenate([own, other], axis=axis), jnp.concatenate([other, own], axis=axis)
    )


def part_of(field, index, axis):
    size = field.shape[axis] // 2
    return lax.dynamic_slice_in_dim(field, index * size, size, axis)


def add(*fields):
    return sum(field.astype(jnp.float32) for field in fields).astype(jnp.bfloat16)


def scatter_plane(pieces):
    return lax.psum_scatter(pieces, ("tp", "far"), scatter_dimension=0, tiled=True)[0]


def scatter_rows(piece):
    return lax.psum_scatter(piece, "dp", scatter_dimension=0, tiled=True)


def gather(piece, part, far, same):
    pair = ordered(piece[None], bring_home(piece)[None], part == 0)
    pairs = ordered(pair[None], swap_far_home(pair)[None], far == 0)
    return jnp.where(same, pairs, swap_near(pairs))


def sum_everywhere(field):
    for name in ("near", "far", "tp", "dp"):
        size = lax.axis_size(name)
        bit = 1
        while bit < size:
            field = field + lax.ppermute(field, name, [(d, d ^ bit) for d in range(size)])
            bit *= 2
    return field


def local(
    layer_input,
    history,
    cotangent,
    lengths,
    dwa_weights,
    gain_one,
    bias_one,
    w_qkv,
    w_out,
    gain_two,
    bias_two,
    w_up,
    w_down,
):
    rows = layer_input.shape[1]
    whole = rows * lax.axis_size("tp")
    hist_count = history.shape[0]
    part, far, near = lax.axis_index("tp"), lax.axis_index("far"), lax.axis_index("near")
    same = near == part
    pieces = [2 * (far ^ a) + (part ^ b) for a in range(2) for b in range(2)]
    flags = jnp.stack([same.astype(jnp.int32), near, far, *pieces])

    input_got = swap_diagonal(layer_input[0])
    qkv_got = swap_diagonal(w_qkv)
    early_got = jnp.concatenate([part_of(w_up, 0, 1), part_of(w_down, 0, 0)], axis=0)
    late_got = jnp.concatenate([part_of(w_up, 1, 1), part_of(w_down, 1, 0)], axis=0)
    last_own = jnp.concatenate([w_out, cotangent[0]], axis=0)
    vectors = jnp.stack([gain_one, bias_one, gain_two, bias_two])

    own_lengths = jnp.where(same, lengths, swap_near(lengths))[0]
    seq_owner, token_place = positions(own_lengths, whole)
    seq_begin = jnp.arange(whole, dtype=jnp.int32) - token_place
    start_column = jnp.broadcast_to(seq_begin[:, None], (whole, LANES))
    start_row = jnp.broadcast_to(seq_begin[None, :], (8, whole))
    half_dim = HEAD_DIM // 2
    lane = jnp.arange(LANES, dtype=jnp.int32)
    frequency = jnp.exp((lane % half_dim).astype(jnp.float32) * (-math.log(10000.0) / half_dim))
    angles = token_place.astype(jnp.float32)[:, None] * frequency[None, :]
    cos_table = jnp.cos(angles)
    sin_table = jnp.sin(angles) * jnp.where(lane % HEAD_DIM < half_dim, -1.0, 1.0)[None, :]
    grad_history, past_sum, sums_past = past(dwa_weights, history[:, 0], cotangent[0])

    input_half = jnp.where(same, layer_input[0], input_got)
    layer_rows = ordered(input_half, swap_near(input_half), near == 0)
    layer_rows, last_own, early_got, late_got, vectors, past_sum, *tables = lax.optimization_barrier(
        (layer_rows, last_own, early_got, late_got, vectors, past_sum)
        + (cos_table, sin_table, start_column, start_row)
    )
    cos_table, sin_table, start_column, start_row = tables
    early_got = swap_diagonal(early_got)
    last_got = swap_diagonal(last_own)
    projected, norm_one_t, weight_qkv = project(
        flags, layer_rows, vectors, cos_table, sin_table, w_qkv, qkv_got
    )
    pairs = projected.shape[2] // LANES
    mixed = attend(0, start_column, projected, None, LONGEST)
    for pair in range(1, pairs):
        mixed = attend(pair, start_column, projected, mixed, LONGEST)
    late_got = swap_diagonal(after(late_got, mixed))
    last_got = jnp.where(same, last_own, last_got)
    weight_out = last_got[: w_out.shape[0]]
    attn = jnp.dot(mixed, weight_out, preferred_element_type=jnp.float32).astype(jnp.bfloat16)
    attn_got = swap_near(attn)
    cot_half = last_got[w_out.shape[0] :]
    cot_rows = ordered(cot_half, swap_near(cot_half), near == 0)
    head = (dwa_weights, layer_rows, attn, attn_got, cot_rows, vectors)
    *kept, act_early, early_pieces, down_early = feed(True, flags, head, w_up, w_down, early_got)
    early_sum = scatter_plane(after(early_pieces, late_got))
    back, act_late, late_pieces, down_late = feed(False, flags, kept, w_up, w_down, late_got)
    late_sum = scatter_plane(late_pieces)
    back_got = swap_near(back)
    grad_attn, grad_mixed, grad_out, sums_two = middle(
        flags,
        dwa_weights,
        layer_rows,
        attn,
        attn_got,
        cot_rows,
        back,
        back_got,
        vectors,
        mixed,
        weight_out,
    )

    grad_qkv = attend_back(0, start_row, cos_table, sin_table, projected, grad_mixed, None, LONGEST)
    for pair in range(1, pairs):
        grad_qkv = attend_back(
            pair, start_row, cos_table, sin_table, projected, grad_mixed, grad_qkv, LONGEST
        )
    owned = weigh(flags, norm_one_t, grad_qkv, grad_out)
    moved = [send_to_owner(owned[j], j // 2, j % 2) for j in range(4)]
    keep, send = unproject(flags, after(grad_qkv, owned[0]), weight_qkv)
    block_keep, block_send = lower(
        flags, after(act_early, send), act_late, down_early, down_late, layer_rows, attn, attn_got
    )
    feed_sum = scatter_rows(jnp.concatenate([after(early_sum, owned[0]), late_sum], axis=1))
    keep, send, block_keep, block_send, *moved = lax.optimization_barrier(
        (keep, send, block_keep, block_send, *moved)
    )
    ours, sums_one = last(
        flags,
        layer_rows,
        keep,
        swap_near(send),
        grad_attn,
        vectors,
        block_keep,
        swap_near(block_send),
        cot_rows,
    )
    attn_sum = scatter_rows(add(jnp.where(same, owned[0], moved[0]), *moved[1:]))
    theirs = swap_diagonal(ours)
    small = jnp.concatenate([sums_one[:3], sums_two[:2], sums_past[:hist_count]], axis=0)
    small = sum_everywhere(small)
    output, grad_input = present(flags, dwa_weights, past_sum, ours, after(theirs, small))
    feed_sum = after(feed_sum, output).reshape(feed_sum.shape[0], 2, -1).transpose(1, 0, 2)
    feed_all = gather(feed_sum, part, far, same)
    attn_sum = after(attn_sum, output)
    attn_pair = ordered(attn_sum[None], swap_near(attn_sum)[None], near == 0)
    attn_all = ordered(attn_pair, swap_far(attn_pair), far == 0)

    def columns_of(pieces):
        return pieces.transpose(2, 1, 0, 3).reshape(pieces.shape[2], -1).astype(jnp.float32)

    return (
        output[None],
        grad_input[None],
        grad_history[:, None],
        jnp.sum(jnp.concatenate([small[5:], small[2:3]], axis=0), axis=1),
        small[0],
        small[1],
        attn_all[:3].astype(jnp.float32),
        attn_all[3].astype(jnp.float32).T,
        small[3],
        small[4],
        columns_of(feed_all[:, 0]),
        columns_of(feed_all[:, 1]).T,
    )


def positions(seq_lengths, token_count):
    seq_ends = jnp.cumsum(seq_lengths)
    seq_starts = seq_ends - seq_lengths
    token_index = jnp.arange(token_count, dtype=jnp.int32)
    seq_owner = jnp.sum((token_index[:, None] >= seq_ends[None, :]).astype(jnp.int32), axis=1)
    picked = (
        seq_owner[:, None] == jnp.arange(seq_lengths.shape[0], dtype=jnp.int32)[None, :]
    ).astype(jnp.int32)
    seq_begin = jnp.sum(picked * seq_starts[None, :], axis=1)
    return (seq_owner, token_index - seq_begin)


def solution(mesh):
    tps, dps, reps = (mesh.shape[name] for name in ("tp", "dp", "rep"))
    split = Mesh(mesh.devices.reshape(tps, dps, reps // 2, 2), AXES)
    in_specs = (
        P(("dp", "far", "near"), "tp", None),
        P(None, ("dp", "far", "near"), "tp", None),
        P(("dp", "far", "near"), "tp", None),
        P(("dp", "far", "near"), None),
        P(),
        P(),
        P(),
        P(None, None, "tp"),
        P("tp", None),
        P(),
        P(),
        P(None, "tp"),
        P("tp", None),
    )
    out_specs = (
        P(("dp", "far", "near"), "tp", None),
        P(("dp", "far", "near"), "tp", None),
        P(None, ("dp", "far", "near"), "tp", None),
        P(),
        P(),
        P(),
        P(None, "dp", "tp"),
        P("tp", "dp"),
        P(),
        P(),
        P("dp", "tp"),
        P("tp", "dp"),
    )
    return jax.shard_map(local, mesh=split, in_specs=in_specs, out_specs=out_specs, check_vma=False)
```

```python
import functools
import itertools
import math

import jax
import jax.numpy as jnp
from jax import lax
from jax.experimental import pallas as pl
from jax.experimental.pallas import tpu as pltpu
from jax.sharding import Mesh, PartitionSpec as P

HEAD_DIM = 64
LONGEST = 512
NEG_FILL = -1e30
NORM_EPS = 1e-05
RATE = 3e6
MIB = 1 << 20


def lasting(microseconds):
    return pl.CostEstimate(flops=0, transcendentals=0, bytes_accessed=int(microseconds * RATE))


BLOCK = 256
LANES = 128
NT = (((1,), (1,)), ((), ()))


def dot(a, b, dims=(((1,), (0,)), ((), ()))):
    return lax.dot_general(a, b, dims, preferred_element_type=jnp.float32)


def spans(whole, reach):
    back = -(-(reach - 1) // BLOCK)
    runs = []
    for i in range(whole // BLOCK):
        count = min(i, back) + 1
        if runs and runs[-1][2] == count:
            runs[-1][1] = i + 1
        else:
            runs.append([i, i + 1, count])
    return runs


def each_block(whole, reach, body):
    for first, last, count in spans(whole, reach):
        def step(at, carry, first=first, count=count):
            i = first + at // 2
            body(i, i + 1 - count, count * BLOCK, at % 2)
            return carry
        lax.fori_loop(0, 2 * (last - first), step, 0)


def attend_kernel(reach, start_ref, q_ref, k_ref, v_ref, out_ref, acc_ref):
    whole = q_ref.shape[0]
    lane = lax.broadcasted_iota(jnp.int32, (BLOCK, LANES), 1) // HEAD_DIM

    def body(i, first, count, head):
        at = pl.ds(pl.multiple_of(i * BLOCK, BLOCK), BLOCK)
        keys = pl.ds(pl.multiple_of(first * BLOCK, BLOCK), count)
        query = q_ref[at, :] * (HEAD_DIM**-0.5)
        query = jnp.where(lane == head, query, jnp.zeros_like(query))
        scores = dot(query, k_ref[keys, :], NT)
        key_at = first * BLOCK + lax.broadcasted_iota(jnp.int32, scores.shape, 1)
        query_at = i * BLOCK + lax.broadcasted_iota(jnp.int32, scores.shape, 0)
        allowed = (key_at >= start_ref[at, :1]) & (key_at <= query_at)
        scores = jnp.where(allowed, scores, NEG_FILL)
        exponent = jnp.exp(scores - jnp.max(scores, axis=1, keepdims=True))
        row_sum = jnp.sum(exponent, axis=1, keepdims=True)
        probs = (exponent * (1.0 / row_sum)).astype(jnp.bfloat16)
        mixed = dot(probs, v_ref[keys, :])

        @pl.when(head == 0)
        def _():
            acc_ref[...] = mixed

        @pl.when(head == 1)
        def _():
            out_ref[at, :] = jnp.where(lane == 0, acc_ref[...], mixed).astype(out_ref.dtype)

    each_block(whole, reach, body)


def attend(start_column, projected, reach):
    count, whole, width = projected.shape

    def block(c):
        return pl.BlockSpec((None, whole, LANES), lambda p: (c, 0, p))

    return pl.pallas_call(
        functools.partial(attend_kernel, reach),
        grid=(width // LANES,),
        in_specs=[pl.BlockSpec((whole, LANES), lambda p: (0, 0)), block(0), block(1), block(2)],
        out_specs=pl.BlockSpec((whole, LANES), lambda p: (0, p)),
        out_shape=jax.ShapeDtypeStruct((whole, width), jnp.bfloat16),
        scratch_shapes=[pltpu.VMEM((BLOCK, LANES), jnp.float32)],
        compiler_params=pltpu.CompilerParams(vmem_limit_bytes=16 * MIB),
        cost_estimate=lasting(17),
    )(start_column, projected, projected, projected)


def turn_back(field, cos, sin):
    half = HEAD_DIM // 2
    lane = lax.broadcasted_iota(jnp.int32, field.shape, 1) % HEAD_DIM
    crossed = jnp.where(lane < half, pltpu.roll(field, LANES - half, 1), pltpu.roll(field, half, 1))
    return field * cos - crossed * sin


def attend_back_kernel(
    reach, start_ref, cos_ref, sin_ref, q_ref, k_ref, v_ref, g_ref, out_ref,
    key_acc, value_acc, query_acc,
):
    whole = q_ref.shape[0]
    lane = lax.broadcasted_iota(jnp.int32, (BLOCK, LANES), 1) // HEAD_DIM
    key_acc[...] = jnp.zeros_like(key_acc)
    value_acc[...] = jnp.zeros_like(value_acc)

    def body(i, first, count, head):
        at = pl.ds(pl.multiple_of(i * BLOCK, BLOCK), BLOCK)
        span = pl.ds(pl.multiple_of(first * BLOCK, BLOCK), count)
        query = q_ref[at, :] * (HEAD_DIM**-0.5)
        query = jnp.where(lane == head, query, jnp.zeros_like(query))
        grad = g_ref[at, :]
        grad = jnp.where(lane == head, grad, jnp.zeros_like(grad))
        keys = k_ref[span, :]
        scores = dot(keys, query, NT)
        key_at = first * BLOCK + lax.broadcasted_iota(jnp.int32, scores.shape, 0)
        query_at = i * BLOCK + lax.broadcasted_iota(jnp.int32, scores.shape, 1)
        allowed = (key_at >= start_ref[:1, at]) & (key_at <= query_at)
        scores = jnp.where(allowed, scores, NEG_FILL)
        exponent = jnp.exp(scores - jnp.max(scores, axis=0, keepdims=True))
        probs = exponent * (1.0 / jnp.sum(exponent, axis=0, keepdims=True))
        value_acc[span, :] += dot(probs.astype(jnp.bfloat16), grad)
        grad_probs = dot(v_ref[span, :], grad, NT)
        weighted = probs * grad_probs
        grad_scores = (weighted - probs * jnp.sum(weighted, axis=0, keepdims=True)).astype(jnp.bfloat16)
        key_acc[span, :] += dot(grad_scores, query)
        here = dot(grad_scores, keys, (((0,), (0,)), ((), ())))

        @pl.when(head == 0)
        def _():
            query_acc[...] = here

        @pl.when(head == 1)
        def _():
            both = jnp.where(lane == 0, query_acc[...], here) * (HEAD_DIM**-0.5)
            out_ref[0, at, :] = turn_back(both, cos_ref[at, :], sin_ref[at, :]).astype(out_ref.dtype)

    each_block(whole, reach, body)

    def finish(i, carry):
        at = pl.ds(pl.multiple_of(i * BLOCK, BLOCK), BLOCK)
        out_ref[1, at, :] = turn_back(key_acc[at, :], cos_ref[at, :], sin_ref[at, :]).astype(out_ref.dtype)
        out_ref[2, at, :] = value_acc[at, :].astype(out_ref.dtype)
        return carry

    lax.fori_loop(0, whole // BLOCK, finish, 0)


def attend_back(start_row, cos, sin, projected, grad_mixed, reach):
    count, whole, width = projected.shape

    def block(c):
        return pl.BlockSpec((None, whole, LANES), lambda p: (c, 0, p))

    table = pl.BlockSpec((whole, LANES), lambda p: (0, 0))
    return pl.pallas_call(
        functools.partial(attend_back_kernel, reach),
        grid=(width // LANES,),
        in_specs=[
            pl.BlockSpec((8, whole), lambda p: (0, 0)),
            table,
            table,
            block(0),
            block(1),
            block(2),
            pl.BlockSpec((whole, LANES), lambda p: (0, p)),
        ],
        out_specs=pl.BlockSpec((count, whole, LANES), lambda p: (0, 0, p)),
        out_shape=jax.ShapeDtypeStruct((count, whole, width), jnp.bfloat16),
        scratch_shapes=[
            pltpu.VMEM((whole, LANES), jnp.float32),
            pltpu.VMEM((whole, LANES), jnp.float32),
            pltpu.VMEM((BLOCK, LANES), jnp.float32),
        ],
        compiler_params=pltpu.CompilerParams(vmem_limit_bytes=20 * MIB),
        cost_estimate=lasting(28),
    )(start_row, cos, sin, projected, projected, projected, grad_mixed)


ROWS = 256


def norm_parts(field):
    centered = field - jnp.mean(field, axis=-1, keepdims=True)
    scale = lax.rsqrt(jnp.mean(centered * centered, axis=-1, keepdims=True) + NORM_EPS)
    return centered * scale, scale


def wide(ref, at):
    return ref[at, :].astype(jnp.float32)


def row_blocks(count, body):
    def step(i, carry):
        body(i, pl.ds(pl.multiple_of(i * ROWS, ROWS), ROWS))
        return carry

    lax.fori_loop(0, count // ROWS, step, 0)


def whole_spec(shape):
    return pl.BlockSpec(shape, lambda *at: (0,) * len(shape))


def turn(field, cos, sin):
    half = HEAD_DIM // 2
    lane = lax.broadcasted_iota(jnp.int32, field.shape, 1) % HEAD_DIM
    crossed = jnp.where(lane < half, pltpu.roll(field, LANES - half, 1), pltpu.roll(field, half, 1))
    return field * cos + crossed * sin


def project_kernel(
    flags, rows_ref, vectors, cos_ref, sin_ref, w_own, w_got, out_ref, turned_ref,
    weight_ref, norm_ref,
):
    whole = rows_ref.shape[0]
    step = pl.program_id(0)

    @pl.when(step == 0)
    def _():
        def body(i, at):
            unit, unused = norm_parts(wide(rows_ref, at))
            norm = unit * vectors[0:1, :] + vectors[1:2, :]
            norm_ref[at, :] = norm.astype(jnp.bfloat16)
            turned_ref[:, at] = norm.T.astype(jnp.bfloat16)

        row_blocks(whole, body)

    weight_ref[0] = jnp.where(flags[0] == 1, w_own[0], w_got[0])

    def body(i, at):
        field = dot(norm_ref[at, :], weight_ref[0])

        @pl.when(step < 2)
        def _():
            for p in range(field.shape[1] // LANES):
                lanes = slice(p * LANES, (p + 1) * LANES)
                out_ref[0, at, lanes] = turn(field[:, lanes], cos_ref[at, :], sin_ref[at, :]).astype(
                    jnp.bfloat16
                )

        @pl.when(step == 2)
        def _():
            out_ref[0, at, :] = field.astype(jnp.bfloat16)

    row_blocks(whole, body)


def project(flags, rows, vectors, cos, sin, w_own, w_got):
    whole, width = rows.shape
    count, unused, columns = w_own.shape
    weight = pl.BlockSpec((1, width, columns), lambda c, flags: (c, 0, 0))
    return pl.pallas_call(
        project_kernel,
        grid_spec=pltpu.PrefetchScalarGridSpec(
            num_scalar_prefetch=1,
            grid=(count,),
            in_specs=[
                whole_spec((whole, width)),
                whole_spec(vectors.shape),
                whole_spec((whole, LANES)),
                whole_spec((whole, LANES)),
                weight,
                weight,
            ],
            out_specs=[
                pl.BlockSpec((1, whole, columns), lambda c, flags: (c, 0, 0)),
                whole_spec((width, whole)),
                weight,
            ],
            scratch_shapes=[pltpu.VMEM((whole, width), jnp.bfloat16)],
        ),
        out_shape=[
            jax.ShapeDtypeStruct((count, whole, columns), jnp.bfloat16),
            jax.ShapeDtypeStruct((width, whole), jnp.bfloat16),
            jax.ShapeDtypeStruct(w_own.shape, jnp.bfloat16),
        ],
        compiler_params=pltpu.CompilerParams(vmem_limit_bytes=24 * MIB),
        cost_estimate=lasting(9),
    )(flags, rows, vectors, cos, sin, w_own, w_got)


HIDDEN = 256


def gelu_both(up):
    root = math.sqrt(2.0 / math.pi)
    square = up * up
    bent = jnp.tanh(root * up * (1.0 + 0.044715 * square))
    half = 0.5 * (1.0 + bent)
    slope = half + 0.5 * up * (1.0 - bent * bent) * (root * (1.0 + 3.0 * 0.044715 * square))
    return up * half, slope


def feed_kernel(early, flags, *refs):
    if early:
        weight_ref, rows_ref, own_ref, got_ref, cot_ref, vectors = refs[:6]
        up_own, down_own, got, norm, norm_t, grad, grad_t = refs[6:13]
        up_got, down_got = got.at[: norm.shape[1]], got.at[norm.shape[1] :]
    else:
        norm, norm_t, grad, grad_t, back_early, up_own, down_own, up_got, down_got = refs[:9]
    back_ref, act_ref, pieces_ref, down_ref, slope, up_w = refs[-6:]
    whole, width = norm.shape
    part = pieces_ref.shape[2]
    step = pl.program_id(0)

    @pl.when(step == 0)
    def _():
        up_w[...] = jnp.where(flags[0] == 1, up_own[...], up_got[...])
        down_ref[...] = jnp.where(flags[0] == 1, down_own[...], down_got[...])
        if early:

            def body(i, at):
                unit, unused = norm_parts(wide(rows_ref, at) + wide(own_ref, at) + wide(got_ref, at))
                field = unit * vectors[2:3, :] + vectors[3:4, :]
                norm[at, :] = field.astype(jnp.bfloat16)
                norm_t[:, at] = field.T.astype(jnp.bfloat16)
                field = wide(cot_ref, at) * weight_ref[weight_ref.shape[0] - 1]
                grad[at, :] = field.astype(jnp.bfloat16)
                grad_t[:, at] = field.T.astype(jnp.bfloat16)

            row_blocks(whole, body)

    hidden = pl.ds(pl.multiple_of(step * HIDDEN, HIDDEN), HIDDEN)
    up_block = up_w[:, hidden]
    down_block = down_ref[hidden, :]

    def body(i, at):
        value, rise = gelu_both(dot(norm[at, :], up_block))
        act_ref[at, :] = value.astype(jnp.bfloat16)
        slope[at, hidden] = (dot(grad[at, :], down_block, NT) * rise).astype(jnp.bfloat16)

    row_blocks(whole, body)

    def grads(i, at):
        fields = (dot(norm_t[at, :], slope[:, hidden]), dot(grad_t[at, :], act_ref[...]))
        for k, field in enumerate(fields):
            field = field.astype(jnp.bfloat16)
            for j in range(2 * part // HIDDEN):

                @pl.when(step == j)
                def _():
                    for p in range(2):
                        first, last = max(p * part, j * HIDDEN), min((p + 1) * part, (j + 1) * HIDDEN)
                        if first < last:
                            pieces_ref[2 * k + p, at, first - p * part : last - p * part] = field[
                                :, first - j * HIDDEN : last - j * HIDDEN
                            ]

    row_blocks(width, grads)

    @pl.when(step == pl.num_programs(0) - 1)
    def _():
        def body(i, at):
            back = dot(slope[at, :], up_w[...], NT)
            if not early:
                back = back + back_early[at, :]
            back_ref[at, :] = back.astype(back_ref.dtype)

        row_blocks(whole, body)


def feed(early, flags, head, w_up, w_down, *got):
    whole, width = head[1].shape if early else head[0].shape
    hidden = w_up.shape[1] // 2
    steps = hidden // HIDDEN
    tokens = whole_spec((whole, width))
    turned = whole_spec((width, whole))
    index = 0 if early else 1
    low = jax.ShapeDtypeStruct((whole, width), jnp.bfloat16)
    low_turned = jax.ShapeDtypeStruct((width, whole), jnp.bfloat16)
    full = jax.ShapeDtypeStruct((whole, width), jnp.float32)
    if early:
        head_specs = [pl.BlockSpec(memory_space=pltpu.SMEM)] + [tokens] * 4
        head_specs = head_specs + [whole_spec(head[-1].shape)]
    else:
        head_specs = [tokens, turned, tokens, turned, tokens]
    return pl.pallas_call(
        functools.partial(feed_kernel, early),
        grid_spec=pltpu.PrefetchScalarGridSpec(
            num_scalar_prefetch=1,
            grid=(steps,),
            in_specs=head_specs
            + [
                pl.BlockSpec((width, hidden), lambda j, flags: (0, index)),
                pl.BlockSpec((hidden, width), lambda j, flags: (index, 0)),
            ]
            + [whole_spec(field.shape) for field in got],
            out_specs=([tokens, turned, tokens, turned] if early else [])
            + [
                tokens,
                pl.BlockSpec((whole, HIDDEN), lambda j, flags: (0, j)),
                whole_spec((4, width, hidden // 2)),
                whole_spec((hidden, width)),
            ],
            scratch_shapes=[
                pltpu.VMEM((whole, hidden), jnp.bfloat16),
                pltpu.VMEM((width, hidden), jnp.bfloat16),
            ],
        ),
        out_shape=([low, low_turned, low, low_turned, full] if early else [low])
        + [
            jax.ShapeDtypeStruct((whole, hidden), jnp.bfloat16),
            jax.ShapeDtypeStruct((4, width, hidden // 2), jnp.bfloat16),
            jax.ShapeDtypeStruct((hidden, width), jnp.bfloat16),
        ],
        compiler_params=pltpu.CompilerParams(vmem_limit_bytes=52 * MIB),
        cost_estimate=lasting(20),
    )(flags, *head, w_up, w_down, *got)


def lower_kernel(
    flags, act_early, act_late, early_ref, late_ref, rows_ref, own_ref, got_ref, cot_ref, keep_ref, send_ref, sums_ref
):
    half = keep_ref.shape[0]
    first, second = early_ref[...], late_ref[...]
    sums_ref[...] = jnp.zeros_like(sums_ref)

    def at_rows(near, i):
        return pl.ds(pl.multiple_of(near * half + i * ROWS, ROWS), ROWS)

    def send(i, at):
        here = at_rows(1 - flags[1], i)
        total = dot(act_early[here, :], first) + dot(act_late[here, :], second)
        send_ref[at, :] = total.astype(jnp.bfloat16)
        sums_ref[0:1, :] += jnp.sum(total * wide(cot_ref, here), axis=0, keepdims=True)

    def keep(i, at):
        here = at_rows(flags[1], i)
        total = dot(act_early[here, :], first) + dot(act_late[here, :], second)
        total = total + wide(rows_ref, here) + wide(own_ref, here) + wide(got_ref, here)
        keep_ref[at, :] = total
        sums_ref[0:1, :] += jnp.sum(total * wide(cot_ref, here), axis=0, keepdims=True)

    row_blocks(half, send)
    row_blocks(half, keep)


def lower(flags, act_early, act_late, down_early, down_late, rows, own, got, cot):
    whole, hidden = act_early.shape
    width = rows.shape[1]
    half = whole_spec((whole // 2, width))
    return pl.pallas_call(
        lower_kernel,
        grid_spec=pltpu.PrefetchScalarGridSpec(
            num_scalar_prefetch=1,
            grid=(1,),
            in_specs=[whole_spec((whole, hidden))] * 2
            + [whole_spec((hidden, width))] * 2
            + [whole_spec((whole, width))] * 4,
            out_specs=[half, half, whole_spec((8, width))],
        ),
        out_shape=[
            jax.ShapeDtypeStruct((whole // 2, width), jnp.float32),
            jax.ShapeDtypeStruct((whole // 2, width), jnp.bfloat16),
            jax.ShapeDtypeStruct((8, width), jnp.float32),
        ],
        compiler_params=pltpu.CompilerParams(vmem_limit_bytes=28 * MIB),
        cost_estimate=lasting(8),
    )(flags, act_early, act_late, down_early, down_late, rows, own, got, cot)


def middle_kernel(
    flags, weight_ref, rows_ref, own_ref, got_ref, cot_ref, back_own, back_got, vectors, mixed_ref,
    w_ref, grad_ref, gmixed_ref, gout_ref, sums_ref, turned,
):
    whole, width = rows_ref.shape
    weight = w_ref[...]
    gain = vectors[2:3, :]
    sums_ref[...] = jnp.zeros_like(sums_ref)

    def body(i, at):
        unit, scale = norm_parts(wide(rows_ref, at) + wide(own_ref, at) + wide(got_ref, at))
        back = wide(back_own, at) + wide(back_got, at)
        inner = back * gain
        mean = jnp.mean(inner, axis=-1, keepdims=True)
        slant = jnp.mean(inner * unit, axis=-1, keepdims=True)
        grad = wide(cot_ref, at) * weight_ref[weight_ref.shape[0] - 1] + scale * (inner - mean - unit * slant)
        low = grad.astype(jnp.bfloat16)
        grad_ref[at, :] = low
        turned[:, at] = grad.T.astype(jnp.bfloat16)
        gmixed_ref[at, :] = dot(low, weight, NT).astype(jnp.bfloat16)

        @pl.when((i * ROWS) // (whole // 2) == flags[1])
        def _():
            sums_ref[0:1, :] += jnp.sum(back * unit, axis=0, keepdims=True)
            sums_ref[1:2, :] += jnp.sum(back, axis=0, keepdims=True)

    row_blocks(whole, body)

    def grads(i, at):
        gout_ref[at, :] = dot(turned[at, :], mixed_ref[...]).astype(jnp.bfloat16)

    row_blocks(width, grads)


def middle(flags, weight, rows, own, got, cot, back_own, back_got, vectors, mixed, w_out):
    whole, width = rows.shape
    columns = mixed.shape[1]
    tokens = whole_spec((whole, width))
    narrow = whole_spec((whole, columns))
    projection = whole_spec((columns, width))
    return pl.pallas_call(
        middle_kernel,
        grid_spec=pltpu.PrefetchScalarGridSpec(
            num_scalar_prefetch=1,
            grid=(1,),
            in_specs=[pl.BlockSpec(memory_space=pltpu.SMEM)]
            + [tokens] * 6
            + [whole_spec(vectors.shape), narrow, projection],
            out_specs=[tokens, narrow, whole_spec((width, columns)), whole_spec((8, width))],
            scratch_shapes=[pltpu.VMEM((width, whole), jnp.bfloat16)],
        ),
        out_shape=[
            jax.ShapeDtypeStruct((whole, width), jnp.bfloat16),
            jax.ShapeDtypeStruct((whole, columns), jnp.bfloat16),
            jax.ShapeDtypeStruct((width, columns), jnp.bfloat16),
            jax.ShapeDtypeStruct((8, width), jnp.float32),
        ],
        compiler_params=pltpu.CompilerParams(vmem_limit_bytes=36 * MIB),
        cost_estimate=lasting(12),
    )(flags, weight, rows, own, got, cot, back_own, back_got, vectors, mixed, w_out)


def weigh_kernel(flags, turned_ref, grad_ref, out_grad_ref, *out_refs):
    last = grad_ref.shape[0]

    def grads(i, at):
        for j, out_ref in enumerate(out_refs):
            piece = flags[3 + j]

            @pl.when(piece < last)
            def _():
                out_ref[at, :] = dot(turned_ref[at, :], grad_ref[jnp.minimum(piece, last - 1)]).astype(
                    jnp.bfloat16
                )

            @pl.when(piece == last)
            def _():
                out_ref[at, :] = out_grad_ref[at, :]

    row_blocks(turned_ref.shape[0], grads)


def weigh(flags, turned, grad, out_grad):
    width, whole = turned.shape
    columns = grad.shape[2]
    piece = whole_spec((width, columns))
    return pl.pallas_call(
        weigh_kernel,
        grid_spec=pltpu.PrefetchScalarGridSpec(
            num_scalar_prefetch=1,
            grid=(1,),
            in_specs=[whole_spec((width, whole)), whole_spec(grad.shape), piece],
            out_specs=[piece] * 4,
        ),
        out_shape=[jax.ShapeDtypeStruct((width, columns), jnp.bfloat16)] * 4,
        compiler_params=pltpu.CompilerParams(vmem_limit_bytes=16 * MIB),
        cost_estimate=lasting(3),
    )(flags, turned, grad, out_grad)


def unproject_kernel(flags, grad_ref, weight, rows_ref, keep_ref, send_ref, sums_ref):
    half = keep_ref.shape[0]
    sums_ref[...] = jnp.zeros_like(sums_ref)

    def side(near, out_ref):
        def body(i, at):
            from_rows = pl.ds(pl.multiple_of(near * half + i * ROWS, ROWS), ROWS)
            total = dot(grad_ref[0, from_rows, :], weight[0], NT)
            for c in range(1, grad_ref.shape[0]):
                total = total + dot(grad_ref[c, from_rows, :], weight[c], NT)
            out_ref[at, :] = total.astype(out_ref.dtype)
            unit, unused = norm_parts(wide(rows_ref, from_rows))
            sums_ref[0:1, :] += jnp.sum(total * unit, axis=0, keepdims=True)
            sums_ref[1:2, :] += jnp.sum(total, axis=0, keepdims=True)

        row_blocks(half, body)

    side(1 - flags[1], send_ref)
    side(flags[1], keep_ref)


def unproject(flags, grad, weight, rows):
    count, whole, columns = grad.shape
    width = weight.shape[1]
    half = whole_spec((whole // 2, width))
    return pl.pallas_call(
        unproject_kernel,
        grid_spec=pltpu.PrefetchScalarGridSpec(
            num_scalar_prefetch=1,
            grid=(1,),
            in_specs=[whole_spec(grad.shape), whole_spec((count, width, columns)), whole_spec(rows.shape)],
            out_specs=[half, half, whole_spec((8, width))],
        ),
        out_shape=[
            jax.ShapeDtypeStruct((whole // 2, width), jnp.float32),
            jax.ShapeDtypeStruct((whole // 2, width), jnp.bfloat16),
            jax.ShapeDtypeStruct((8, width), jnp.float32),
        ],
        compiler_params=pltpu.CompilerParams(vmem_limit_bytes=20 * MIB),
        cost_estimate=lasting(4),
    )(flags, grad, weight, rows)


def last_kernel(flags, rows_ref, keep_ref, got_ref, resid_ref, vectors, block_keep, block_got, grad_ref, block_ref):
    def body(i, at):
        unit, scale = norm_parts(wide(rows_ref, at))
        inner = (keep_ref[at, :] + wide(got_ref, at)) * vectors[0:1, :]
        mean = jnp.mean(inner, axis=-1, keepdims=True)
        slant = jnp.mean(inner * unit, axis=-1, keepdims=True)
        grad = wide(resid_ref, at) + scale * (inner - mean - unit * slant)
        grad_ref[at, :] = grad.astype(jnp.bfloat16)
        block_ref[at, :] = (block_keep[at, :] + wide(block_got, at)).astype(jnp.bfloat16)

    row_blocks(rows_ref.shape[0], body)


def last(flags, rows, keep, got, resid, vectors, block_keep, block_got):
    half, width = keep.shape
    mine = pl.BlockSpec((half, width), lambda i, flags: (flags[1], 0))
    tokens = whole_spec((half, width))
    return pl.pallas_call(
        last_kernel,
        grid_spec=pltpu.PrefetchScalarGridSpec(
            num_scalar_prefetch=1,
            grid=(1,),
            in_specs=[mine, tokens, tokens, mine, whole_spec(vectors.shape), tokens, tokens],
            out_specs=[tokens, tokens],
        ),
        out_shape=[jax.ShapeDtypeStruct((half, width), jnp.bfloat16)] * 2,
        compiler_params=pltpu.CompilerParams(vmem_limit_bytes=16 * MIB),
        cost_estimate=lasting(3),
    )(flags, rows, keep, got, resid, vectors, block_keep, block_got)


def past_kernel(dwa_ref, hist_ref, cot_ref, grad_ref, part_ref, sums_ref):
    @pl.when(pl.program_id(0) == 0)
    def _():
        sums_ref[...] = jnp.zeros_like(sums_ref)

    grad = cot_ref[...].astype(jnp.float32)
    total = jnp.zeros_like(grad)
    for j in range(hist_ref.shape[0]):
        field = hist_ref[j].astype(jnp.float32)
        total += dwa_ref[j] * field
        grad_ref[j] = (dwa_ref[j] * grad).astype(jnp.bfloat16)
        sums_ref[j : j + 1, :] += jnp.sum(field * grad, axis=0, keepdims=True)
    part_ref[...] = total


def past(dwa, history, cot):
    count, rows, width = history.shape
    layers = pl.BlockSpec((count, ROWS, width), lambda i: (0, i, 0))
    tokens = pl.BlockSpec((ROWS, width), lambda i: (i, 0))
    return pl.pallas_call(
        past_kernel,
        grid=(rows // ROWS,),
        in_specs=[pl.BlockSpec(memory_space=pltpu.SMEM), layers, tokens],
        out_specs=[layers, tokens, whole_spec((8, width))],
        out_shape=[
            jax.ShapeDtypeStruct(history.shape, jnp.bfloat16),
            jax.ShapeDtypeStruct((rows, width), jnp.float32),
            jax.ShapeDtypeStruct((8, width), jnp.float32),
        ],
        compiler_params=pltpu.CompilerParams(vmem_limit_bytes=16 * MIB),
        cost_estimate=lasting(3),
    )(dwa, history, cot)


def present_kernel(flags, weight_ref, part_ref, grad_own, grad_got, block_own, block_got, out_ref, grad_ref):
    here = jnp.where(flags[0] == 1, block_own[...], block_got[...]).astype(jnp.float32)
    out_ref[...] = (part_ref[...] + weight_ref[weight_ref.shape[0] - 1] * here).astype(jnp.bfloat16)
    grad_ref[...] = jnp.where(flags[0] == 1, grad_own[...], grad_got[...])


def present(flags, weight, part, grad_own, grad_got, block_own, block_got):
    rows, width = part.shape
    scalars = pl.BlockSpec(memory_space=pltpu.SMEM)
    tokens = pl.BlockSpec((ROWS, width), lambda i: (i, 0))
    return pl.pallas_call(
        present_kernel,
        grid=(rows // ROWS,),
        in_specs=[scalars, scalars] + [tokens] * 5,
        out_specs=[tokens, tokens],
        out_shape=[jax.ShapeDtypeStruct((rows, width), jnp.bfloat16)] * 2,
        compiler_params=pltpu.CompilerParams(vmem_limit_bytes=12 * MIB),
        cost_estimate=lasting(2),
    )(flags, weight, part, grad_own, grad_got, block_own, block_got)


def place_feed_kernel(flags, own_ref, got_ref, up_ref, down_ref):
    part = own_ref.shape[-1]
    far, tp = flags[2], flags[7]
    for k in range(2):
        for t, out_ref in enumerate((up_ref, down_ref)):
            for half in range(2):
                at = (2 * half + k) * part
                here = [ref[k ^ far, t ^ tp, half].astype(jnp.float32) for ref in (own_ref, got_ref)]
                out_ref[:, at : at + part] = jnp.where(flags[0] == 1, *here)


def place_feed(flags, own, got):
    rows, part = own.shape[-2:]
    both = whole_spec(own.shape)
    block = whole_spec((rows, 4 * part))
    return pl.pallas_call(
        place_feed_kernel,
        grid_spec=pltpu.PrefetchScalarGridSpec(
            num_scalar_prefetch=1, grid=(1,), in_specs=[both, both], out_specs=[block, block]
        ),
        out_shape=[jax.ShapeDtypeStruct((rows, 4 * part), jnp.float32)] * 2,
        compiler_params=pltpu.CompilerParams(vmem_limit_bytes=16 * MIB),
        cost_estimate=lasting(2),
    )(flags, own, got)


def place_attention_kernel(flags, own_ref, got_ref, qkv_ref, out_ref):
    near, far = flags[1], flags[2]
    for k in range(2):
        for c in range(2):
            here = [ref[c ^ near].astype(jnp.float32) for ref in (own_ref, got_ref)]
            field = jnp.where(far == k, *here)
            if 2 * k + c < 3:
                qkv_ref[2 * k + c] = field
            else:
                out_ref[...] = field


def place_attention(flags, own, got):
    rows, part = own.shape[-2:]
    both = whole_spec(own.shape)
    return pl.pallas_call(
        place_attention_kernel,
        grid_spec=pltpu.PrefetchScalarGridSpec(
            num_scalar_prefetch=1,
            grid=(1,),
            in_specs=[both, both],
            out_specs=[whole_spec((3, rows, part)), whole_spec((rows, part))],
        ),
        out_shape=[
            jax.ShapeDtypeStruct((3, rows, part), jnp.float32),
            jax.ShapeDtypeStruct((rows, part), jnp.float32),
        ],
        compiler_params=pltpu.CompilerParams(vmem_limit_bytes=16 * MIB),
        cost_estimate=lasting(1),
    )(flags, own, got)


AXES = ("tp", "dp", "far", "near")


def moves(chosen, move):
    sizes = [lax.axis_size(name) for name in AXES]
    places = [place for place in itertools.product(*map(range, sizes)) if chosen(*place)]
    index = lambda place: functools.reduce(lambda at, step: at * step[0] + step[1], zip(sizes, place), 0)
    return [(index(place), index(move(*place))) for place in places]


def away(t, d, k, c):
    return t != c


def anyone(t, d, k, c):
    return True


def home(t, d, k, c):
    return t == c


def swap_diagonal(field):
    return lax.ppermute(field, AXES, moves(away, lambda t, d, k, c: (c, d, k, t)))


def send_to_owner(field, other_far, other_tp):
    return lax.ppermute(
        field,
        AXES,
        moves(
            away if not other_far and not other_tp else anyone,
            lambda t, d, k, c: (c, d, k ^ other_far, t ^ other_tp),
        ),
    )


def bring_home(field):
    return lax.ppermute(field, AXES, moves(away, lambda t, d, k, c: (c, d, k, c)))


def swap_far_home(field):
    return lax.ppermute(field, AXES, moves(home, lambda t, d, k, c: (t, d, 1 - k, c)))


def swap_far(field):
    return lax.ppermute(field, "far", [(0, 1), (1, 0)])


def swap_near(field):
    return lax.ppermute(field, "near", [(0, 1), (1, 0)])


def after(field, *others):
    return lax.optimization_barrier((field, *others))[0]


def ordered(own, other, first, axis=0):
    return jnp.where(
        first, jnp.concatenate([own, other], axis=axis), jnp.concatenate([other, own], axis=axis)
    )


def part_of(field, index, axis):
    size = field.shape[axis] // 2
    return lax.dynamic_slice_in_dim(field, index * size, size, axis)


def add(*fields):
    return sum(field.astype(jnp.float32) for field in fields).astype(jnp.bfloat16)


def scatter_plane(pieces):
    return lax.psum_scatter(pieces, ("tp", "far"), scatter_dimension=0, tiled=True)[0]


def scatter_rows(piece):
    return lax.psum_scatter(piece, "dp", scatter_dimension=0, tiled=True)


def move_rows(block):
    dps = lax.axis_size("dp")
    if dps > 8:
        return [scatter_rows(block)]
    block = block.reshape(dps, block.shape[0] // dps, block.shape[1])
    place = lax.axis_index("dp")
    moved = [lax.dynamic_index_in_dim(block, place, 0, keepdims=False)]
    for step in range(1, dps):
        sent = lax.dynamic_index_in_dim(block, lax.rem(place + step, dps), 0, keepdims=False)
        moved.append(lax.ppermute(sent, "dp", [(d, (d + step) % dps) for d in range(dps)]))
    return moved


def sum_over(field, name):
    size = lax.axis_size(name)
    bit = 1
    while bit < size:
        field = field + lax.ppermute(field, name, [(d, d ^ bit) for d in range(size)])
        bit *= 2
    return field


def local(
    layer_input,
    history,
    cotangent,
    lengths,
    dwa_weights,
    gain_one,
    bias_one,
    w_qkv,
    w_out,
    gain_two,
    bias_two,
    w_up,
    w_down,
):
    rows = layer_input.shape[1]
    whole = rows * lax.axis_size("tp")
    hist_count = history.shape[0]
    part, far, near = lax.axis_index("tp"), lax.axis_index("far"), lax.axis_index("near")
    same = near == part
    pieces = [2 * (far ^ a) + (part ^ b) for a in range(2) for b in range(2)]
    flags = jnp.stack([same.astype(jnp.int32), near, far, *pieces, part])

    input_got = swap_diagonal(layer_input[0])
    qkv_got = swap_diagonal(w_qkv)
    early_got = jnp.concatenate([part_of(w_up, 0, 1), part_of(w_down, 0, 0)], axis=0)
    late_up, late_down = part_of(w_up, 1, 1), part_of(w_down, 1, 0)
    last_own = jnp.concatenate([w_out, cotangent[0]], axis=0)
    vectors = jnp.stack([gain_one, bias_one, gain_two, bias_two])

    own_lengths = jnp.where(same, lengths, swap_near(lengths))[0]
    seq_owner, token_place = positions(own_lengths, whole)
    seq_begin = jnp.arange(whole, dtype=jnp.int32) - token_place
    start_column = jnp.broadcast_to(seq_begin[:, None], (whole, LANES))
    start_row = jnp.broadcast_to(seq_begin[None, :], (8, whole))
    half_dim = HEAD_DIM // 2
    lane = jnp.arange(LANES, dtype=jnp.int32)
    frequency = jnp.exp((lane % half_dim).astype(jnp.float32) * (-math.log(10000.0) / half_dim))
    angles = token_place.astype(jnp.float32)[:, None] * frequency[None, :]
    cos_table = jnp.cos(angles)
    sin_table = jnp.sin(angles) * jnp.where(lane % HEAD_DIM < half_dim, -1.0, 1.0)[None, :]
    grad_history, past_sum, sums_past = past(dwa_weights, history[:, 0], cotangent[0])

    input_half = jnp.where(same, layer_input[0], input_got)
    layer_rows = ordered(input_half, swap_near(input_half), near == 0)
    layer_rows, last_own, early_got, late_up, vectors, past_sum, *tables = lax.optimization_barrier(
        (layer_rows, last_own, early_got, late_up, vectors, past_sum)
        + (cos_table, sin_table, start_column, start_row)
    )
    cos_table, sin_table, start_column, start_row = tables
    early_got = swap_diagonal(early_got)
    last_got = swap_diagonal(last_own)
    projected, norm_one_t, weight_qkv = project(
        flags, layer_rows, vectors, cos_table, sin_table, w_qkv, qkv_got
    )
    mixed = attend(start_column, projected, LONGEST)
    late_up = swap_diagonal(after(late_up, mixed))
    late_down = swap_diagonal(after(late_down, mixed))
    last_got = jnp.where(same, last_own, last_got)
    weight_out = last_got[: w_out.shape[0]]
    attn = jnp.dot(mixed, weight_out, preferred_element_type=jnp.float32).astype(jnp.bfloat16)
    attn_got = swap_near(attn)
    cot_half = last_got[w_out.shape[0] :]
    cot_rows = ordered(cot_half, swap_near(cot_half), near == 0)
    head = (dwa_weights, layer_rows, attn, attn_got, cot_rows, vectors)
    *kept, act_early, early_pieces, down_early = feed(True, flags, head, w_up, w_down, early_got)
    early_sum = scatter_plane(after(early_pieces, late_up, late_down))
    back, act_late, late_pieces, down_late = feed(False, flags, kept, w_up, w_down, late_up, late_down)
    late_sum = scatter_plane(late_pieces)
    back_got = swap_near(back)
    grad_attn, grad_mixed, grad_out, sums_two = middle(
        flags,
        dwa_weights,
        layer_rows,
        attn,
        attn_got,
        cot_rows,
        back,
        back_got,
        vectors,
        mixed,
        weight_out,
    )

    grad_qkv = attend_back(start_row, cos_table, sin_table, projected, grad_mixed, LONGEST)
    owned = weigh(flags, norm_one_t, grad_qkv, grad_out)
    moved = [send_to_owner(owned[j], j // 2, j % 2) for j in range(4)]
    keep, send, sums_one = unproject(flags, after(grad_qkv, owned[0]), weight_qkv, layer_rows)
    block_keep, block_send, sums_now = lower(
        flags, act_early, act_late, down_early, down_late, layer_rows, attn, attn_got, after(cot_rows, send)
    )
    small = jnp.concatenate([sums_one[:2], sums_two[:2], sums_now[:1], sums_past[:hist_count]], axis=0)
    early_sum = scatter_rows(after(early_sum, owned[0]))
    for name in ("near", "dp", "tp", "far"):
        small = sum_over(small, name)
    small, keep, send, block_keep, block_send, *moved = lax.optimization_barrier(
        (small, keep, send, block_keep, block_send, *moved)
    )
    attn_one = add(jnp.where(same, owned[0], moved[0]), *moved[1:])
    attn_moved = move_rows(attn_one)
    input_grad, block_half = last(
        flags, layer_rows, after(keep, attn_one), swap_near(send), grad_attn, vectors, block_keep, swap_near(block_send)
    )
    input_moved = swap_diagonal(input_grad)
    late_sum = scatter_rows(after(late_sum, attn_one))
    input_grad, input_moved, block_half, *attn_moved = lax.optimization_barrier(
        (input_grad, input_moved, block_half, *attn_moved)
    )
    block_moved = swap_diagonal(block_half)
    attn_sum = add(*attn_moved)
    attn_own = jnp.stack([attn_sum, swap_near(attn_sum)])
    attn_got = swap_far(attn_own)
    feed_sum = jnp.stack([after(early_sum, attn_sum), late_sum])
    feed_home = bring_home(feed_sum)
    block_moved, attn_own, attn_got, feed_sum, feed_home = lax.optimization_barrier(
        (block_moved, attn_own, attn_got, feed_sum, feed_home)
    )
    feed_own = jnp.stack([feed_sum, feed_home])
    feed_both = jnp.stack([feed_own, swap_far_home(feed_own)])
    feed_got = swap_near(feed_both)
    grad_w_qkv, grad_w_out = place_attention(flags, attn_own, attn_got)
    grad_w_up, grad_w_down = place_feed(flags, feed_both, feed_got)
    output, grad_input = present(
        flags, dwa_weights, past_sum, input_grad, input_moved, block_half, block_moved
    )

    return (
        output[None],
        grad_input[None],
        grad_history[:, None],
        jnp.sum(jnp.concatenate([small[5:], small[4:5]], axis=0), axis=1),
        small[0],
        small[1],
        grad_w_qkv,
        grad_w_out.T,
        small[2],
        small[3],
        grad_w_up,
        grad_w_down.T,
    )


def positions(seq_lengths, token_count):
    seq_ends = jnp.cumsum(seq_lengths)
    seq_starts = seq_ends - seq_lengths
    token_index = jnp.arange(token_count, dtype=jnp.int32)
    seq_owner = jnp.sum((token_index[:, None] >= seq_ends[None, :]).astype(jnp.int32), axis=1)
    picked = (
        seq_owner[:, None] == jnp.arange(seq_lengths.shape[0], dtype=jnp.int32)[None, :]
    ).astype(jnp.int32)
    seq_begin = jnp.sum(picked * seq_starts[None, :], axis=1)
    return (seq_owner, token_index - seq_begin)


def solution(mesh):
    tps, dps, reps = (mesh.shape[name] for name in ("tp", "dp", "rep"))
    split = Mesh(mesh.devices.reshape(tps, dps, reps // 2, 2), AXES)
    in_specs = (
        P(("dp", "far", "near"), "tp", None),
        P(None, ("dp", "far", "near"), "tp", None),
        P(("dp", "far", "near"), "tp", None),
        P(("dp", "far", "near"), None),
        P(),
        P(),
        P(),
        P(None, None, "tp"),
        P("tp", None),
        P(),
        P(),
        P(None, "tp"),
        P("tp", None),
    )
    out_specs = (
        P(("dp", "far", "near"), "tp", None),
        P(("dp", "far", "near"), "tp", None),
        P(None, ("dp", "far", "near"), "tp", None),
        P(),
        P(),
        P(),
        P(None, "dp", "tp"),
        P("tp", "dp"),
        P(),
        P(),
        P("dp", "tp"),
        P("tp", "dp"),
    )
    return jax.shard_map(local, mesh=split, in_specs=in_specs, out_specs=out_specs, check_vma=False)
```

```python
import functools
import itertools
import math

import jax
import jax.numpy as jnp
from jax import lax
from jax.experimental import pallas as pl
from jax.experimental.pallas import tpu as pltpu
from jax.sharding import Mesh, PartitionSpec as P

HEAD_DIM = 64
LONGEST = 512
NEG_FILL = -1e30
NORM_EPS = 1e-05
RATE = 3e6
ROOM = 60 << 20


def lasting(microseconds):
    return pl.CostEstimate(flops=0, transcendentals=0, bytes_accessed=int(microseconds * RATE))


BLOCK = 256
LANES = 128
NT = (((1,), (1,)), ((), ()))


def dot(a, b, dims=(((1,), (0,)), ((), ()))):
    return lax.dot_general(a, b, dims, preferred_element_type=jnp.float32)


def spans(whole, reach):
    back = -(-(reach - 1) // BLOCK)
    runs = []
    for i in range(whole // BLOCK):
        count = min(i, back) + 1
        if runs and runs[-1][2] == count:
            runs[-1][1] = i + 1
        else:
            runs.append([i, i + 1, count])
    return runs


def each_block(whole, reach, body):
    for first, last, count in spans(whole, reach):

        def step(i, carry, count=count):
            body(i, i + 1 - count, count)
            return carry

        lax.fori_loop(first, last, step, 0)


def block_at(i, count=1):
    return pl.ds(pl.multiple_of(i * BLOCK, BLOCK), count * BLOCK)


def head_query(q_ref, apart_ref, i, head):
    lane = lax.broadcasted_iota(jnp.int32, (BLOCK, LANES), 1) // HEAD_DIM
    query = q_ref[block_at(i), :] * (HEAD_DIM**-0.5)
    query = jnp.where(lane == head, query, jnp.zeros_like(query))
    return query, jnp.concatenate([query, apart_ref[block_at(i), :]], axis=1)


def attend_kernel(reach, apart_ref, member_ref, q_ref, k_ref, v_ref, out_ref, keys):
    whole = q_ref.shape[0]
    lane = lax.broadcasted_iota(jnp.int32, (BLOCK, LANES), 1) // HEAD_DIM
    keys[:, :LANES] = k_ref[...]
    keys[:, LANES:] = member_ref[...]

    def one(i, first, count, head):
        unused, query = head_query(q_ref, apart_ref, i, head)
        own = dot(query, keys[block_at(i), :], NT)
        key_at = lax.broadcasted_iota(jnp.int32, own.shape, 1)
        query_at = lax.broadcasted_iota(jnp.int32, own.shape, 0)
        scores = jnp.where(key_at <= query_at, own, NEG_FILL)
        if count > 1:
            scores = jnp.concatenate([dot(query, keys[block_at(first, count - 1), :], NT), scores], axis=1)
        exponent = jnp.exp(scores - jnp.max(scores, axis=1, keepdims=True))
        row_sum = jnp.sum(exponent, axis=1, keepdims=True)
        return dot(exponent.astype(jnp.bfloat16), v_ref[block_at(first, count), :]) * (1.0 / row_sum)

    def body(i, first, count):
        mixed = [one(i, first, count, head) for head in range(2)]
        out_ref[block_at(i), :] = jnp.where(lane == 0, *mixed).astype(out_ref.dtype)

    each_block(whole, reach, body)


def attend(apart, member, projected, reach):
    count, whole, width = projected.shape

    def block(c):
        return pl.BlockSpec((None, whole, LANES), lambda p: (c, 0, p))

    table = pl.BlockSpec((whole, LANES), lambda p: (0, 0))
    return pl.pallas_call(
        functools.partial(attend_kernel, reach),
        grid=(width // LANES,),
        in_specs=[table, table, block(0), block(1), block(2)],
        out_specs=pl.BlockSpec((whole, LANES), lambda p: (0, p)),
        out_shape=jax.ShapeDtypeStruct((whole, width), jnp.bfloat16),
        scratch_shapes=[pltpu.VMEM((whole, 2 * LANES), jnp.bfloat16)],
        compiler_params=pltpu.CompilerParams(vmem_limit_bytes=ROOM),
        cost_estimate=lasting(12),
    )(apart, member, projected, projected, projected)


def turn_back(field, cos, sin):
    half = HEAD_DIM // 2
    lane = lax.broadcasted_iota(jnp.int32, field.shape, 1) % HEAD_DIM
    crossed = jnp.where(lane < half, pltpu.roll(field, LANES - half, 1), pltpu.roll(field, half, 1))
    return field * cos - crossed * sin


def attend_back_kernel(
    reach, apart_ref, member_ref, cos_ref, sin_ref, q_ref, k_ref, v_ref, g_ref, out_ref, keys, keys_t, key_acc, value_acc
):
    whole = q_ref.shape[0]
    lane = lax.broadcasted_iota(jnp.int32, (BLOCK, LANES), 1) // HEAD_DIM
    keys[:, :LANES] = k_ref[...]
    keys[:, LANES:] = member_ref[...]
    keys_t[...] = k_ref[...].astype(jnp.float32).T.astype(jnp.bfloat16)
    key_acc[...] = jnp.zeros_like(key_acc)
    value_acc[...] = jnp.zeros_like(value_acc)

    def one(i, first, count, head):
        span = block_at(first, count)
        plain, query = head_query(q_ref, apart_ref, i, head)
        grad = g_ref[block_at(i), :]
        grad = jnp.where(lane == head, grad, jnp.zeros_like(grad))
        own = dot(keys[block_at(i), :], query, NT)
        key_at = lax.broadcasted_iota(jnp.int32, own.shape, 0)
        query_at = lax.broadcasted_iota(jnp.int32, own.shape, 1)
        scores = jnp.where(key_at <= query_at, own, NEG_FILL)
        if count > 1:
            scores = jnp.concatenate([dot(keys[block_at(first, count - 1), :], query, NT), scores], axis=0)
        exponent = jnp.exp(scores - jnp.max(scores, axis=0, keepdims=True))
        probs = exponent * (1.0 / jnp.sum(exponent, axis=0, keepdims=True))
        grad_values = dot(probs.astype(jnp.bfloat16), grad)
        weighted = probs * dot(v_ref[span, :], grad, NT)
        grad_scores = (weighted - probs * jnp.sum(weighted, axis=0, keepdims=True)).astype(jnp.bfloat16)
        here = dot(keys_t[:, span], grad_scores)
        return grad_values, dot(grad_scores, plain), here

    def body(i, first, count):
        span, at = block_at(first, count), block_at(i)
        values, keys_, queries = zip(*[one(i, first, count, head) for head in range(2)])
        value_acc[span, :] += values[0] + values[1]
        key_acc[span, :] += keys_[0] + keys_[1]
        row = lax.broadcasted_iota(jnp.int32, queries[0].shape, 0) // HEAD_DIM
        both = jnp.where(row == 0, *queries).T * (HEAD_DIM**-0.5)
        out_ref[0, at, :] = turn_back(both, cos_ref[at, :], sin_ref[at, :]).astype(out_ref.dtype)

    each_block(whole, reach, body)

    def finish(i, carry):
        at = block_at(i)
        out_ref[1, at, :] = turn_back(key_acc[at, :], cos_ref[at, :], sin_ref[at, :]).astype(out_ref.dtype)
        out_ref[2, at, :] = value_acc[at, :].astype(out_ref.dtype)
        return carry

    lax.fori_loop(0, whole // BLOCK, finish, 0)


def attend_back(apart, member, cos, sin, projected, grad_mixed, reach):
    count, whole, width = projected.shape

    def block(c):
        return pl.BlockSpec((None, whole, LANES), lambda p: (c, 0, p))

    table = pl.BlockSpec((whole, LANES), lambda p: (0, 0))
    return pl.pallas_call(
        functools.partial(attend_back_kernel, reach),
        grid=(width // LANES,),
        in_specs=[table] * 4 + [block(0), block(1), block(2), pl.BlockSpec((whole, LANES), lambda p: (0, p))],
        out_specs=pl.BlockSpec((count, whole, LANES), lambda p: (0, 0, p)),
        out_shape=jax.ShapeDtypeStruct((count, whole, width), jnp.bfloat16),
        scratch_shapes=[
            pltpu.VMEM((whole, 2 * LANES), jnp.bfloat16),
            pltpu.VMEM((LANES, whole), jnp.bfloat16),
            pltpu.VMEM((whole, LANES), jnp.float32),
            pltpu.VMEM((whole, LANES), jnp.float32),
        ],
        compiler_params=pltpu.CompilerParams(vmem_limit_bytes=ROOM),
        cost_estimate=lasting(22),
    )(apart, member, cos, sin, projected, projected, projected, grad_mixed)


ROWS = 256


def norm_parts(field):
    centered = field - jnp.mean(field, axis=-1, keepdims=True)
    scale = lax.rsqrt(jnp.mean(centered * centered, axis=-1, keepdims=True) + NORM_EPS)
    return centered * scale, scale


def wide(ref, at):
    return ref[at, :].astype(jnp.float32)


def row_blocks(count, body):
    def step(i, carry):
        body(i, pl.ds(pl.multiple_of(i * ROWS, ROWS), ROWS))
        return carry

    lax.fori_loop(0, count // ROWS, step, 0)


TALL = 512


def streamed(kernel, steps, scalars, fields, outs, scratch, microseconds):
    def spec(shape, block=None, at=None):
        if block is None:
            return pl.BlockSpec(shape, lambda i, *scalars: (0,) * len(shape))
        return pl.BlockSpec(block, at)

    fields = [field if isinstance(field, tuple) else (field,) for field in fields]
    return pl.pallas_call(
        kernel,
        grid_spec=pltpu.PrefetchScalarGridSpec(
            num_scalar_prefetch=len(scalars),
            grid=(steps,),
            in_specs=[spec(field[0].shape, *field[1:]) for field in fields],
            out_specs=[spec(out[0], *out[2:]) for out in outs],
            scratch_shapes=[pltpu.VMEM(shape, dtype) for shape, dtype in scratch],
        ),
        out_shape=[jax.ShapeDtypeStruct(*out[:2]) for out in outs],
        compiler_params=pltpu.CompilerParams(vmem_limit_bytes=ROOM),
        cost_estimate=lasting(microseconds),
    )(*scalars, *[field[0] for field in fields])


def by_rows(field, rows, shift=None):
    if shift is None:
        return field, (rows, field.shape[1]), lambda i, *scalars: (i, 0)
    return field, (rows, field.shape[1]), lambda i, *scalars: (shift(i, *scalars), 0)


def whole_spec(shape):
    return pl.BlockSpec(shape, lambda *at: (0,) * len(shape))


def turn(field, cos, sin):
    half = HEAD_DIM // 2
    lane = lax.broadcasted_iota(jnp.int32, field.shape, 1) % HEAD_DIM
    crossed = jnp.where(lane < half, pltpu.roll(field, LANES - half, 1), pltpu.roll(field, half, 1))
    return field * cos + crossed * sin


def project_kernel(flags, rows_ref, cos_ref, sin_ref, vectors, w_own, w_got, out_ref, turned_ref, weight_ref):
    @pl.when(pl.program_id(0) == 0)
    def _():
        weight_ref[...] = jnp.where(flags[0] == 1, w_own[...], w_got[...])

    unit, unused = norm_parts(rows_ref[...].astype(jnp.float32))
    norm = unit * vectors[0:1, :] + vectors[1:2, :]
    turned_ref[...] = norm.T.astype(jnp.bfloat16)
    norm = norm.astype(jnp.bfloat16)
    for c in range(weight_ref.shape[0]):
        field = dot(norm, weight_ref[c])
        if c == 2:
            out_ref[c] = field.astype(jnp.bfloat16)
        else:
            for p in range(field.shape[1] // LANES):
                lanes = slice(p * LANES, (p + 1) * LANES)
                out_ref[c, :, lanes] = turn(field[:, lanes], cos_ref[...], sin_ref[...]).astype(jnp.bfloat16)


def project(flags, rows, vectors, cos, sin, w_own, w_got):
    whole, width = rows.shape
    count, unused, columns = w_own.shape
    low = jnp.bfloat16
    return streamed(
        project_kernel,
        whole // ROWS,
        [flags],
        [by_rows(rows, ROWS), by_rows(cos, ROWS), by_rows(sin, ROWS), vectors, w_own, w_got],
        [
            ((count, whole, columns), low, (count, ROWS, columns), lambda i, flags: (0, i, 0)),
            ((width, whole), low, (width, ROWS), lambda i, flags: (0, i)),
            (w_own.shape, low),
        ],
        [],
        8,
    )


def gelu_both(up):
    root = math.sqrt(2.0 / math.pi)
    square = up * up
    bent = jnp.tanh(root * up * (1.0 + 0.044715 * square))
    half = 0.5 * (1.0 + bent)
    slope = half + 0.5 * up * (1.0 - bent * bent) * (root * (1.0 + 3.0 * 0.044715 * square))
    return up * half, slope


def feed_kernel(early, *refs):
    if early:
        flags, weight_ref, rows_ref, own_ref, got_ref, cot_ref, vectors, up_own, down_own, got = refs[:10]
        norm, norm_t, grad, grad_t = refs[10:14]
        up_got, down_got = got.at[: norm.shape[1]], got.at[norm.shape[1] :]
    else:
        flags, norm, norm_t, grad, grad_t, up_own, down_own, up_got, down_got = refs[:9]
    back_ref, act_ref, pieces_ref, down_ref, up_w, up_sum, down_sum = refs[-7:]
    part = pieces_ref.shape[2]
    step, last = pl.program_id(0), pl.num_programs(0) - 1

    @pl.when(step == 0)
    def _():
        up_w[...] = jnp.where(flags[0] == 1, up_own[...], up_got[...])
        down_ref[...] = jnp.where(flags[0] == 1, down_own[...], down_got[...])

    if early:

        def head(i, at):
            unit, unused = norm_parts(wide(rows_ref, at) + wide(own_ref, at) + wide(got_ref, at))
            field = unit * vectors[2:3, :] + vectors[3:4, :]
            norm[at, :] = field.astype(jnp.bfloat16)
            norm_t[:, at] = field.T.astype(jnp.bfloat16)
            field = wide(cot_ref, at) * weight_ref[weight_ref.shape[0] - 1]
            grad[at, :] = field.astype(jnp.bfloat16)
            grad_t[:, at] = field.T.astype(jnp.bfloat16)

        row_blocks(norm.shape[0], head)
    value, rise = gelu_both(dot(norm[...], up_w[...]))
    act_ref[...] = value.astype(jnp.bfloat16)
    slope = (dot(grad[...], down_ref[...], NT) * rise).astype(jnp.bfloat16)
    back_ref[...] = dot(slope, up_w[...], NT).astype(jnp.bfloat16)

    def grads(i, at):
        fields = (dot(norm_t[at, :], slope), dot(grad_t[at, :], act_ref[...]))
        for k, (field, total) in enumerate(zip(fields, (up_sum, down_sum))):

            @pl.when(step == 0)
            def _():
                total[at, :] = field

            @pl.when(step == last)
            def _():
                low = (total[at, :] + field).astype(jnp.bfloat16)
                for p in range(2):
                    pieces_ref[2 * k + p, at, :] = low[:, p * part : (p + 1) * part]

    row_blocks(norm_t.shape[0], grads)


def feed(early, scalars, fields, w_up, w_down, *got):
    whole, width = fields[0].shape
    hidden = w_up.shape[1] // 2
    rows = whole // 2
    half = 0 if early else 1
    low = jnp.bfloat16

    def across(i, *scalars):
        return (0, i)

    tokens = ((whole, width), low, (rows, width), lambda i, *scalars: (i, 0))
    turned = ((width, whole), low, (width, rows), across)
    if early:
        operands = [by_rows(field, rows) for field in fields[:4]] + [fields[4]]
        outs = [tokens, turned, tokens, turned]
    else:
        operands = [by_rows(fields[0], rows), (fields[1], (width, rows), across)]
        operands += [by_rows(fields[2], rows), (fields[3], (width, rows), across)]
        outs = []
    operands += [
        (w_up, (width, hidden), lambda i, *scalars: (0, half)),
        (w_down, (hidden, width), lambda i, *scalars: (half, 0)),
        *got,
    ]
    outs += [
        tokens,
        ((whole, hidden), low, (rows, hidden), lambda i, *scalars: (i, 0)),
        ((4, width, hidden // 2), low),
        ((hidden, width), low),
    ]
    sums = ((width, hidden), jnp.float32)
    return streamed(
        functools.partial(feed_kernel, early), 2, scalars, operands, outs, [((width, hidden), low), sums, sums], 17
    )


def lower_kernel(flags, act_early, act_late, rows_ref, own_ref, got_ref, cot_ref, early_ref, late_ref, keep_ref, send_ref, sums_ref):
    step, half = pl.program_id(0), pl.num_programs(0) // 2

    @pl.when(step == 0)
    def _():
        sums_ref[...] = jnp.zeros_like(sums_ref)

    total = dot(act_early[...], early_ref[...]) + dot(act_late[...], late_ref[...])
    cot = cot_ref[...].astype(jnp.float32)

    @pl.when(step < half)
    def _():
        send_ref[...] = total.astype(jnp.bfloat16)
        sums_ref[0:1, :] += jnp.sum(total * cot, axis=0, keepdims=True)

    @pl.when(step >= half)
    def _():
        parts = [ref[...].astype(jnp.float32) for ref in (rows_ref, own_ref, got_ref)]
        block = total + parts[0] + parts[1] + parts[2]
        keep_ref[...] = block
        sums_ref[0:1, :] += jnp.sum(block * cot, axis=0, keepdims=True)


def theirs_first(steps):
    return lambda i, flags, *more: lax.rem((1 - flags[1]) * (steps // 2) + i, steps)


def halves(steps, rows, width):
    keep = (rows, width), lambda i, *scalars: (jnp.maximum(i - steps // 2, 0), 0)
    send = (rows, width), lambda i, *scalars: (jnp.minimum(i, steps // 2 - 1), 0)
    return keep, send


def lower(flags, act_early, act_late, down_early, down_late, rows, own, got, cot):
    whole, width = rows.shape
    steps = whole // ROWS
    order = theirs_first(steps)
    keep, send = halves(steps, ROWS, width)
    shape = (whole // 2, width)
    return streamed(
        lower_kernel,
        steps,
        [flags],
        [by_rows(field, ROWS, order) for field in (act_early, act_late, rows, own, got, cot)] + [down_early, down_late],
        [(shape, jnp.float32, *keep), (shape, jnp.bfloat16, *send), ((8, width), jnp.float32)],
        [],
        6,
    )


def middle_kernel(
    flags, weight_ref, rows_ref, own_ref, got_ref, cot_ref, early_own, early_got, late_own, late_got, mixed_ref,
    vectors, w_ref, grad_ref, gmixed_ref, gout_ref, sums_ref, gout,
):
    step, last = pl.program_id(0), pl.num_programs(0) - 1
    unit, scale = norm_parts(sum(ref[...].astype(jnp.float32) for ref in (rows_ref, own_ref, got_ref)))
    back = sum(ref[...].astype(jnp.float32) for ref in (early_own, early_got, late_own, late_got))
    inner = back * vectors[2:3, :]
    mean = jnp.mean(inner, axis=-1, keepdims=True)
    slant = jnp.mean(inner * unit, axis=-1, keepdims=True)
    cot = cot_ref[...].astype(jnp.float32) * weight_ref[weight_ref.shape[0] - 1]
    grad = cot + scale * (inner - mean - unit * slant)
    low = grad.astype(jnp.bfloat16)
    grad_ref[...] = low
    gmixed_ref[...] = dot(low, w_ref[...], NT).astype(jnp.bfloat16)
    part = dot(grad.T.astype(jnp.bfloat16), mixed_ref[...])

    @pl.when(step == 0)
    def _():
        gout[...] = part
        sums_ref[...] = jnp.zeros_like(sums_ref)

    @pl.when(step > 0)
    def _():
        gout[...] += part

    @pl.when(step == last)
    def _():
        gout_ref[...] = gout[...].astype(jnp.bfloat16)

    @pl.when(step // ((last + 1) // 2) == flags[1])
    def _():
        sums_ref[0:1, :] += jnp.sum(back * unit, axis=0, keepdims=True)
        sums_ref[1:2, :] += jnp.sum(back, axis=0, keepdims=True)


def middle(flags, weight, fields, mixed, vectors, w_out):
    whole, width = fields[0].shape
    columns = mixed.shape[1]
    low = jnp.bfloat16
    in_order = lambda i, *scalars: (i, 0)
    return streamed(
        middle_kernel,
        whole // ROWS,
        [flags, weight],
        [by_rows(field, ROWS) for field in (*fields, mixed)] + [vectors, w_out],
        [
            ((whole, width), low, (ROWS, width), in_order),
            ((whole, columns), low, (ROWS, columns), in_order),
            ((width, columns), low),
            ((8, width), jnp.float32),
        ],
        [((width, columns), jnp.float32)],
        8,
    )


def weigh_kernel(flags, turned_ref, out_grad_ref, grad_ref, *out_refs):
    last = grad_ref.shape[0]
    for j, out_ref in enumerate(out_refs):
        piece = flags[3 + j]

        @pl.when(piece < last)
        def _():
            out_ref[...] = dot(turned_ref[...], grad_ref[jnp.minimum(piece, last - 1)]).astype(jnp.bfloat16)

        @pl.when(piece == last)
        def _():
            out_ref[...] = out_grad_ref[...]


def weigh(flags, turned, grad, out_grad):
    width, columns = turned.shape[0], grad.shape[2]
    piece = ((width, columns), jnp.bfloat16, (ROWS, columns), lambda i, flags: (i, 0))
    return streamed(
        weigh_kernel, width // ROWS, [flags], [by_rows(turned, ROWS), by_rows(out_grad, ROWS), grad], [piece] * 4, [], 4
    )


def unproject_kernel(flags, grad_ref, rows_ref, weight, keep_ref, send_ref, sums_ref):
    step, half = pl.program_id(0), pl.num_programs(0) // 2
    total = dot(grad_ref[0], weight[0], NT)
    for c in range(1, grad_ref.shape[0]):
        total = total + dot(grad_ref[c], weight[c], NT)
    unit, unused = norm_parts(rows_ref[...].astype(jnp.float32))

    @pl.when(step == 0)
    def _():
        sums_ref[...] = jnp.zeros_like(sums_ref)

    sums_ref[0:1, :] += jnp.sum(total * unit, axis=0, keepdims=True)
    sums_ref[1:2, :] += jnp.sum(total, axis=0, keepdims=True)

    @pl.when(step < half)
    def _():
        send_ref[...] = total.astype(jnp.bfloat16)

    @pl.when(step >= half)
    def _():
        keep_ref[...] = total


def unproject(flags, grad, weight, rows):
    whole, width = rows.shape
    count, unused, columns = grad.shape
    steps = whole // ROWS
    order = theirs_first(steps)
    keep, send = halves(steps, ROWS, width)
    shape = (whole // 2, width)
    return streamed(
        unproject_kernel,
        steps,
        [flags],
        [(grad, (count, ROWS, columns), lambda i, flags: (0, order(i, flags), 0)), by_rows(rows, ROWS, order), weight],
        [(shape, jnp.float32, *keep), (shape, jnp.bfloat16, *send), ((8, width), jnp.float32)],
        [],
        5,
    )


def last_kernel(flags, rows_ref, resid_ref, keep_ref, got_ref, block_keep, block_got, vectors, grad_ref, block_ref):
    unit, scale = norm_parts(rows_ref[...].astype(jnp.float32))
    inner = (keep_ref[...] + got_ref[...].astype(jnp.float32)) * vectors[0:1, :]
    mean = jnp.mean(inner, axis=-1, keepdims=True)
    slant = jnp.mean(inner * unit, axis=-1, keepdims=True)
    grad = resid_ref[...].astype(jnp.float32) + scale * (inner - mean - unit * slant)
    grad_ref[...] = grad.astype(jnp.bfloat16)
    block_ref[...] = (block_keep[...] + block_got[...].astype(jnp.float32)).astype(jnp.bfloat16)


def last(flags, rows, resid, keep, got, block_keep, block_got, vectors):
    half, width = keep.shape
    steps = half // ROWS

    def mine(i, flags):
        return flags[1] * steps + i

    out = ((half, width), jnp.bfloat16, (ROWS, width), lambda i, flags: (i, 0))
    fields = [by_rows(rows, ROWS, mine), by_rows(resid, ROWS, mine)]
    fields += [by_rows(field, ROWS) for field in (keep, got, block_keep, block_got)]
    return streamed(last_kernel, steps, [flags], fields + [vectors], [out] * 2, [], 3)


def past_kernel(dwa_ref, hist_ref, cot_ref, grad_ref, part_ref, sums_ref):
    @pl.when(pl.program_id(0) == 0)
    def _():
        sums_ref[...] = jnp.zeros_like(sums_ref)

    grad = cot_ref[...].astype(jnp.float32)
    total = jnp.zeros_like(grad)
    for j in range(hist_ref.shape[0]):
        field = hist_ref[j].astype(jnp.float32)
        total += dwa_ref[j] * field
        grad_ref[j] = (dwa_ref[j] * grad).astype(jnp.bfloat16)
        sums_ref[j : j + 1, :] += jnp.sum(field * grad, axis=0, keepdims=True)
    part_ref[...] = total


def past(dwa, history, cot):
    count, rows, width = history.shape
    layers = pl.BlockSpec((count, ROWS, width), lambda i: (0, i, 0))
    tokens = pl.BlockSpec((ROWS, width), lambda i: (i, 0))
    return pl.pallas_call(
        past_kernel,
        grid=(rows // ROWS,),
        in_specs=[pl.BlockSpec(memory_space=pltpu.SMEM), layers, tokens],
        out_specs=[layers, tokens, whole_spec((8, width))],
        out_shape=[
            jax.ShapeDtypeStruct(history.shape, jnp.bfloat16),
            jax.ShapeDtypeStruct((rows, width), jnp.float32),
            jax.ShapeDtypeStruct((8, width), jnp.float32),
        ],
        compiler_params=pltpu.CompilerParams(vmem_limit_bytes=ROOM),
        cost_estimate=lasting(3),
    )(dwa, history, cot)


def present_kernel(flags, weight_ref, part_ref, grad_own, grad_got, block_own, block_got, out_ref, grad_ref):
    here = jnp.where(flags[0] == 1, block_own[...], block_got[...]).astype(jnp.float32)
    out_ref[...] = (part_ref[...] + weight_ref[weight_ref.shape[0] - 1] * here).astype(jnp.bfloat16)
    grad_ref[...] = jnp.where(flags[0] == 1, grad_own[...], grad_got[...])


def present(flags, weight, part, grad_own, grad_got, block_own, block_got):
    rows, width = part.shape
    scalars = pl.BlockSpec(memory_space=pltpu.SMEM)
    tokens = pl.BlockSpec((ROWS, width), lambda i: (i, 0))
    return pl.pallas_call(
        present_kernel,
        grid=(rows // ROWS,),
        in_specs=[scalars, scalars] + [tokens] * 5,
        out_specs=[tokens, tokens],
        out_shape=[jax.ShapeDtypeStruct((rows, width), jnp.bfloat16)] * 2,
        compiler_params=pltpu.CompilerParams(vmem_limit_bytes=ROOM),
        cost_estimate=lasting(2),
    )(flags, weight, part, grad_own, grad_got, block_own, block_got)


def place_feed_kernel(flags, own_ref, got_ref, up_ref, down_ref):
    part = own_ref.shape[-1]
    far, tp = flags[2], flags[7]
    for k in range(2):
        for t, out_ref in enumerate((up_ref, down_ref)):
            for half in range(2):
                at = (2 * half + k) * part
                here = [ref[k ^ far, t ^ tp, half].astype(jnp.float32) for ref in (own_ref, got_ref)]
                out_ref[:, at : at + part] = jnp.where(flags[0] == 1, *here)


def place_feed(flags, own, got):
    rows, part = own.shape[-2:]
    both = whole_spec(own.shape)
    block = whole_spec((rows, 4 * part))
    return pl.pallas_call(
        place_feed_kernel,
        grid_spec=pltpu.PrefetchScalarGridSpec(
            num_scalar_prefetch=1, grid=(1,), in_specs=[both, both], out_specs=[block, block]
        ),
        out_shape=[jax.ShapeDtypeStruct((rows, 4 * part), jnp.float32)] * 2,
        compiler_params=pltpu.CompilerParams(vmem_limit_bytes=ROOM),
        cost_estimate=lasting(2),
    )(flags, own, got)


def place_attention_kernel(flags, own_ref, got_ref, qkv_ref, out_ref):
    near, far = flags[1], flags[2]
    for k in range(2):
        for c in range(2):
            here = [ref[c ^ near].astype(jnp.float32) for ref in (own_ref, got_ref)]
            field = jnp.where(far == k, *here)
            if 2 * k + c < 3:
                qkv_ref[2 * k + c] = field
            else:
                out_ref[...] = field


def place_attention(flags, own, got):
    rows, part = own.shape[-2:]
    both = whole_spec(own.shape)
    return pl.pallas_call(
        place_attention_kernel,
        grid_spec=pltpu.PrefetchScalarGridSpec(
            num_scalar_prefetch=1,
            grid=(1,),
            in_specs=[both, both],
            out_specs=[whole_spec((3, rows, part)), whole_spec((rows, part))],
        ),
        out_shape=[
            jax.ShapeDtypeStruct((3, rows, part), jnp.float32),
            jax.ShapeDtypeStruct((rows, part), jnp.float32),
        ],
        compiler_params=pltpu.CompilerParams(vmem_limit_bytes=ROOM),
        cost_estimate=lasting(1),
    )(flags, own, got)


AXES = ("tp", "dp", "far", "near")


def moves(chosen, move):
    sizes = [lax.axis_size(name) for name in AXES]
    places = [place for place in itertools.product(*map(range, sizes)) if chosen(*place)]
    index = lambda place: functools.reduce(lambda at, step: at * step[0] + step[1], zip(sizes, place), 0)
    return [(index(place), index(move(*place))) for place in places]


def away(t, d, k, c):
    return t != c


def anyone(t, d, k, c):
    return True


def home(t, d, k, c):
    return t == c


def swap_diagonal(field):
    return lax.ppermute(field, AXES, moves(away, lambda t, d, k, c: (c, d, k, t)))


def send_to_owner(field, other_far, other_tp):
    return lax.ppermute(
        field,
        AXES,
        moves(
            away if not other_far and not other_tp else anyone,
            lambda t, d, k, c: (c, d, k ^ other_far, t ^ other_tp),
        ),
    )


def bring_home(field):
    return lax.ppermute(field, AXES, moves(away, lambda t, d, k, c: (c, d, k, c)))


def swap_far_home(field):
    return lax.ppermute(field, AXES, moves(home, lambda t, d, k, c: (t, d, 1 - k, c)))


def swap_far(field):
    return lax.ppermute(field, "far", [(0, 1), (1, 0)])


def swap_near(field):
    return lax.ppermute(field, "near", [(0, 1), (1, 0)])


def after(field, *others):
    return lax.optimization_barrier((field, *others))[0]


def ordered(own, other, first, axis=0):
    return jnp.where(
        first, jnp.concatenate([own, other], axis=axis), jnp.concatenate([other, own], axis=axis)
    )


def part_of(field, index, axis):
    size = field.shape[axis] // 2
    return lax.dynamic_slice_in_dim(field, index * size, size, axis)


def add(*fields):
    return sum(field.astype(jnp.float32) for field in fields).astype(jnp.bfloat16)


def scatter_plane(pieces):
    return lax.psum_scatter(pieces, ("tp", "far"), scatter_dimension=0, tiled=True)[0]


def scatter_rows(piece):
    return lax.psum_scatter(piece, "dp", scatter_dimension=0, tiled=True)


def move_rows(block):
    dps = lax.axis_size("dp")
    if dps > 8:
        return [scatter_rows(block)]
    block = block.reshape(dps, block.shape[0] // dps, block.shape[1])
    place = lax.axis_index("dp")
    moved = [lax.dynamic_index_in_dim(block, place, 0, keepdims=False)]
    for step in range(1, dps):
        sent = lax.dynamic_index_in_dim(block, lax.rem(place + step, dps), 0, keepdims=False)
        moved.append(lax.ppermute(sent, "dp", [(d, (d + step) % dps) for d in range(dps)]))
    return moved


def sum_over(field, name):
    size = lax.axis_size(name)
    bit = 1
    while bit < size:
        field = field + lax.ppermute(field, name, [(d, d ^ bit) for d in range(size)])
        bit *= 2
    return field


def local(
    layer_input,
    history,
    cotangent,
    lengths,
    dwa_weights,
    gain_one,
    bias_one,
    w_qkv,
    w_out,
    gain_two,
    bias_two,
    w_up,
    w_down,
):
    rows = layer_input.shape[1]
    whole = rows * lax.axis_size("tp")
    hist_count = history.shape[0]
    part, far, near = lax.axis_index("tp"), lax.axis_index("far"), lax.axis_index("near")
    same = near == part
    pieces = [2 * (far ^ a) + (part ^ b) for a in range(2) for b in range(2)]
    flags = jnp.stack([same.astype(jnp.int32), near, far, *pieces, part])

    input_got = swap_diagonal(layer_input[0])
    qkv_got = swap_diagonal(w_qkv)
    early_got = jnp.concatenate([part_of(w_up, 0, 1), part_of(w_down, 0, 0)], axis=0)
    late_up, late_down = part_of(w_up, 1, 1), part_of(w_down, 1, 0)
    last_own = jnp.concatenate([w_out, cotangent[0]], axis=0)
    vectors = jnp.stack([gain_one, bias_one, gain_two, bias_two])

    own_lengths = jnp.where(same, lengths, swap_near(lengths))[0]
    seq_owner, token_place = positions(own_lengths, whole)
    lane = jnp.arange(LANES, dtype=jnp.int32)
    member = seq_owner[:, None] == lane[None, :]
    apart = jnp.where(member | (lane >= lengths.shape[1])[None, :], 0.0, NEG_FILL).astype(jnp.bfloat16)
    member = member.astype(jnp.bfloat16)
    half_dim = HEAD_DIM // 2
    frequency = jnp.exp((lane % half_dim).astype(jnp.float32) * (-math.log(10000.0) / half_dim))
    angles = token_place.astype(jnp.float32)[:, None] * frequency[None, :]
    cos_table = jnp.cos(angles)
    sin_table = jnp.sin(angles) * jnp.where(lane % HEAD_DIM < half_dim, -1.0, 1.0)[None, :]
    grad_history, past_sum, sums_past = past(dwa_weights, history[:, 0], cotangent[0])

    input_half = jnp.where(same, layer_input[0], input_got)
    layer_rows = ordered(input_half, swap_near(input_half), near == 0)
    layer_rows, last_own, early_got, late_up, vectors, past_sum, *tables = lax.optimization_barrier(
        (layer_rows, last_own, early_got, late_up, vectors, past_sum)
        + (cos_table, sin_table, apart, member)
    )
    cos_table, sin_table, apart, member = tables
    early_got = swap_diagonal(early_got)
    last_got = swap_diagonal(last_own)
    projected, norm_one_t, weight_qkv = project(
        flags, layer_rows, vectors, cos_table, sin_table, w_qkv, qkv_got
    )
    mixed = attend(apart, member, projected, LONGEST)
    late_up = swap_diagonal(after(late_up, mixed))
    late_down = swap_diagonal(after(late_down, mixed))
    last_got = jnp.where(same, last_own, last_got)
    weight_out = last_got[: w_out.shape[0]]
    attn = jnp.dot(mixed, weight_out, preferred_element_type=jnp.float32).astype(jnp.bfloat16)
    attn_got = swap_near(attn)
    cot_half = last_got[w_out.shape[0] :]
    cot_rows = ordered(cot_half, swap_near(cot_half), near == 0)
    scalars = [flags, dwa_weights]
    fields = [layer_rows, attn, attn_got, cot_rows, vectors]
    *kept, back_early, act_early, early_pieces, down_early = feed(True, scalars, fields, w_up, w_down, early_got)
    early_sum = scatter_plane(after(early_pieces, late_up, late_down))
    back_late, act_late, late_pieces, down_late = feed(False, [flags], kept, w_up, w_down, late_up, late_down)
    late_sum = scatter_plane(late_pieces)
    fields = [layer_rows, attn, attn_got, cot_rows, back_early, swap_near(back_early), back_late, swap_near(back_late)]
    grad_attn, grad_mixed, grad_out, sums_two = middle(flags, dwa_weights, fields, mixed, vectors, weight_out)
    grad_qkv = attend_back(apart, member, cos_table, sin_table, projected, grad_mixed, LONGEST)
    owned = weigh(flags, norm_one_t, grad_qkv, grad_out)
    moved = [send_to_owner(owned[j], j // 2, j % 2) for j in range(4)]
    keep, send, sums_one = unproject(flags, after(grad_qkv, owned[0]), weight_qkv, layer_rows)
    block_keep, block_send, sums_now = lower(
        flags, act_early, act_late, down_early, down_late, layer_rows, attn, attn_got, after(cot_rows, send)
    )
    small = jnp.concatenate([sums_one[:2], sums_two[:2], sums_now[:1], sums_past[:hist_count]], axis=0)
    early_sum = scatter_rows(after(early_sum, owned[0]))
    for name in ("near", "dp", "tp", "far"):
        small = sum_over(small, name)
    small, keep, send, block_keep, block_send, *moved = lax.optimization_barrier(
        (small, keep, send, block_keep, block_send, *moved)
    )
    attn_one = add(jnp.where(same, owned[0], moved[0]), *moved[1:])
    attn_moved = move_rows(attn_one)
    input_grad, block_half = last(
        flags, layer_rows, grad_attn, after(keep, attn_one), swap_near(send), block_keep, swap_near(block_send), vectors
    )
    input_moved = swap_diagonal(input_grad)
    late_sum = scatter_rows(after(late_sum, attn_one))
    input_grad, input_moved, block_half, *attn_moved = lax.optimization_barrier(
        (input_grad, input_moved, block_half, *attn_moved)
    )
    block_moved = swap_diagonal(block_half)
    attn_sum = add(*attn_moved)
    attn_own = jnp.stack([attn_sum, swap_near(attn_sum)])
    attn_got = swap_far(attn_own)
    feed_sum = jnp.stack([after(early_sum, attn_sum), late_sum])
    feed_home = bring_home(feed_sum)
    block_moved, attn_own, attn_got, feed_sum, feed_home = lax.optimization_barrier(
        (block_moved, attn_own, attn_got, feed_sum, feed_home)
    )
    feed_own = jnp.stack([feed_sum, feed_home])
    feed_both = jnp.stack([feed_own, swap_far_home(feed_own)])
    feed_got = swap_near(feed_both)
    grad_w_qkv, grad_w_out = place_attention(flags, attn_own, attn_got)
    grad_w_up, grad_w_down = place_feed(flags, feed_both, feed_got)
    output, grad_input = present(
        flags, dwa_weights, past_sum, input_grad, input_moved, block_half, block_moved
    )

    return (
        output[None],
        grad_input[None],
        grad_history[:, None],
        jnp.sum(jnp.concatenate([small[5:], small[4:5]], axis=0), axis=1),
        small[0],
        small[1],
        grad_w_qkv,
        grad_w_out.T,
        small[2],
        small[3],
        grad_w_up,
        grad_w_down.T,
    )


def positions(seq_lengths, token_count):
    seq_ends = jnp.cumsum(seq_lengths)
    seq_starts = seq_ends - seq_lengths
    token_index = jnp.arange(token_count, dtype=jnp.int32)
    seq_owner = jnp.sum((token_index[:, None] >= seq_ends[None, :]).astype(jnp.int32), axis=1)
    picked = (
        seq_owner[:, None] == jnp.arange(seq_lengths.shape[0], dtype=jnp.int32)[None, :]
    ).astype(jnp.int32)
    seq_begin = jnp.sum(picked * seq_starts[None, :], axis=1)
    return (seq_owner, token_index - seq_begin)


def solution(mesh):
    tps, dps, reps = (mesh.shape[name] for name in ("tp", "dp", "rep"))
    split = Mesh(mesh.devices.reshape(tps, dps, reps // 2, 2), AXES)
    in_specs = (
        P(("dp", "far", "near"), "tp", None),
        P(None, ("dp", "far", "near"), "tp", None),
        P(("dp", "far", "near"), "tp", None),
        P(("dp", "far", "near"), None),
        P(),
        P(),
        P(),
        P(None, None, "tp"),
        P("tp", None),
        P(),
        P(),
        P(None, "tp"),
        P("tp", None),
    )
    out_specs = (
        P(("dp", "far", "near"), "tp", None),
        P(("dp", "far", "near"), "tp", None),
        P(None, ("dp", "far", "near"), "tp", None),
        P(),
        P(),
        P(),
        P(None, "dp", "tp"),
        P("tp", "dp"),
        P(),
        P(),
        P("dp", "tp"),
        P("tp", "dp"),
    )
    return jax.shard_map(local, mesh=split, in_specs=in_specs, out_specs=out_specs, check_vma=False)
```

```python
import functools
import itertools
import math

import jax
import jax.numpy as jnp
from jax import lax
from jax.experimental import pallas as pl
from jax.experimental.pallas import tpu as pltpu
from jax.sharding import Mesh, PartitionSpec as P

HEAD_DIM = 64
LONGEST = 512
NEG_FILL = -1e30
NORM_EPS = 1e-05
RATE = 3e6
ROOM = 60 << 20
SNUG = 18 << 20


def lasting(microseconds):
    return pl.CostEstimate(flops=0, transcendentals=0, bytes_accessed=int(microseconds * RATE))


BLOCK = 256
LANES = 128
NT = (((1,), (1,)), ((), ()))


def dot(a, b, dims=(((1,), (0,)), ((), ()))):
    return lax.dot_general(a, b, dims, preferred_element_type=jnp.float32)


def spans(whole, reach):
    back = -(-(reach - 1) // BLOCK)
    runs = []
    for i in range(whole // BLOCK):
        count = min(i, back) + 1
        if runs and runs[-1][2] == count:
            runs[-1][1] = i + 1
        else:
            runs.append([i, i + 1, count])
    return runs


def each_block(whole, reach, body):
    for first, last, count in spans(whole, reach):

        def step(i, carry, count=count):
            body(i, i + 1 - count, count)
            return carry

        lax.fori_loop(first, last, step, 0)


def block_at(i, count=1):
    return pl.ds(pl.multiple_of(i * BLOCK, BLOCK), count * BLOCK)


def head_query(q_ref, apart_ref, i, head):
    lane = lax.broadcasted_iota(jnp.int32, (BLOCK, LANES), 1) // HEAD_DIM
    query = q_ref[block_at(i), :] * (HEAD_DIM**-0.5)
    query = jnp.where(lane == head, query, jnp.zeros_like(query))
    return query, jnp.concatenate([query, apart_ref[block_at(i), :]], axis=1)


def attend_kernel(reach, apart_ref, member_ref, q_ref, k_ref, v_ref, out_ref, keys):
    whole = q_ref.shape[0]
    lane = lax.broadcasted_iota(jnp.int32, (BLOCK, LANES), 1) // HEAD_DIM
    keys[:, :LANES] = k_ref[...]
    keys[:, LANES:] = member_ref[...]

    def one(i, first, count, head):
        unused, query = head_query(q_ref, apart_ref, i, head)
        own = dot(query, keys[block_at(i), :], NT)
        key_at = lax.broadcasted_iota(jnp.int32, own.shape, 1)
        query_at = lax.broadcasted_iota(jnp.int32, own.shape, 0)
        scores = jnp.where(key_at <= query_at, own, NEG_FILL)
        if count > 1:
            scores = jnp.concatenate([dot(query, keys[block_at(first, count - 1), :], NT), scores], axis=1)
        exponent = jnp.exp(scores - jnp.max(scores, axis=1, keepdims=True))
        row_sum = jnp.sum(exponent, axis=1, keepdims=True)
        return dot(exponent.astype(jnp.bfloat16), v_ref[block_at(first, count), :]) * (1.0 / row_sum)

    def body(i, first, count):
        mixed = [one(i, first, count, head) for head in range(2)]
        out_ref[block_at(i), :] = jnp.where(lane == 0, *mixed).astype(out_ref.dtype)

    each_block(whole, reach, body)


def attend(apart, member, projected, reach):
    count, whole, width = projected.shape

    def block(c):
        return pl.BlockSpec((None, whole, LANES), lambda p: (c, 0, p))

    table = pl.BlockSpec((whole, LANES), lambda p: (0, 0))
    return pl.pallas_call(
        functools.partial(attend_kernel, reach),
        grid=(width // LANES,),
        in_specs=[table, table, block(0), block(1), block(2)],
        out_specs=pl.BlockSpec((whole, LANES), lambda p: (0, p)),
        out_shape=jax.ShapeDtypeStruct((whole, width), jnp.bfloat16),
        scratch_shapes=[pltpu.VMEM((whole, 2 * LANES), jnp.bfloat16)],
        compiler_params=pltpu.CompilerParams(vmem_limit_bytes=ROOM),
        cost_estimate=lasting(12),
    )(apart, member, projected, projected, projected)


def turn_back(field, cos, sin):
    half = HEAD_DIM // 2
    lane = lax.broadcasted_iota(jnp.int32, field.shape, 1) % HEAD_DIM
    crossed = jnp.where(lane < half, pltpu.roll(field, LANES - half, 1), pltpu.roll(field, half, 1))
    return field * cos - crossed * sin


def attend_back_kernel(
    reach, apart_ref, member_ref, cos_ref, sin_ref, q_ref, k_ref, v_ref, g_ref, out_ref, keys, keys_t, key_acc, value_acc
):
    whole = q_ref.shape[0]
    lane = lax.broadcasted_iota(jnp.int32, (BLOCK, LANES), 1) // HEAD_DIM
    keys[:, :LANES] = k_ref[...]
    keys[:, LANES:] = member_ref[...]
    keys_t[...] = k_ref[...].astype(jnp.float32).T.astype(jnp.bfloat16)
    key_acc[...] = jnp.zeros_like(key_acc)
    value_acc[...] = jnp.zeros_like(value_acc)

    def one(i, first, count, head):
        span = block_at(first, count)
        plain, query = head_query(q_ref, apart_ref, i, head)
        grad = g_ref[block_at(i), :]
        grad = jnp.where(lane == head, grad, jnp.zeros_like(grad))
        own = dot(keys[block_at(i), :], query, NT)
        key_at = lax.broadcasted_iota(jnp.int32, own.shape, 0)
        query_at = lax.broadcasted_iota(jnp.int32, own.shape, 1)
        scores = jnp.where(key_at <= query_at, own, NEG_FILL)
        if count > 1:
            scores = jnp.concatenate([dot(keys[block_at(first, count - 1), :], query, NT), scores], axis=0)
        exponent = jnp.exp(scores - jnp.max(scores, axis=0, keepdims=True))
        probs = exponent * (1.0 / jnp.sum(exponent, axis=0, keepdims=True))
        grad_values = dot(probs.astype(jnp.bfloat16), grad)
        weighted = probs * dot(v_ref[span, :], grad, NT)
        grad_scores = (weighted - probs * jnp.sum(weighted, axis=0, keepdims=True)).astype(jnp.bfloat16)
        here = dot(keys_t[:, span], grad_scores)
        return grad_values, dot(grad_scores, plain), here

    def body(i, first, count):
        span, at = block_at(first, count), block_at(i)
        values, keys_, queries = zip(*[one(i, first, count, head) for head in range(2)])
        value_acc[span, :] += values[0] + values[1]
        key_acc[span, :] += keys_[0] + keys_[1]
        row = lax.broadcasted_iota(jnp.int32, queries[0].shape, 0) // HEAD_DIM
        both = jnp.where(row == 0, *queries).T * (HEAD_DIM**-0.5)
        out_ref[0, at, :] = turn_back(both, cos_ref[at, :], sin_ref[at, :]).astype(out_ref.dtype)

    each_block(whole, reach, body)

    def finish(i, carry):
        at = block_at(i)
        out_ref[1, at, :] = turn_back(key_acc[at, :], cos_ref[at, :], sin_ref[at, :]).astype(out_ref.dtype)
        out_ref[2, at, :] = value_acc[at, :].astype(out_ref.dtype)
        return carry

    lax.fori_loop(0, whole // BLOCK, finish, 0)


def attend_back(apart, member, cos, sin, projected, grad_mixed, reach):
    count, whole, width = projected.shape

    def block(c):
        return pl.BlockSpec((None, whole, LANES), lambda p: (c, 0, p))

    table = pl.BlockSpec((whole, LANES), lambda p: (0, 0))
    return pl.pallas_call(
        functools.partial(attend_back_kernel, reach),
        grid=(width // LANES,),
        in_specs=[table] * 4 + [block(0), block(1), block(2), pl.BlockSpec((whole, LANES), lambda p: (0, p))],
        out_specs=pl.BlockSpec((count, whole, LANES), lambda p: (0, 0, p)),
        out_shape=jax.ShapeDtypeStruct((count, whole, width), jnp.bfloat16),
        scratch_shapes=[
            pltpu.VMEM((whole, 2 * LANES), jnp.bfloat16),
            pltpu.VMEM((LANES, whole), jnp.bfloat16),
            pltpu.VMEM((whole, LANES), jnp.float32),
            pltpu.VMEM((whole, LANES), jnp.float32),
        ],
        compiler_params=pltpu.CompilerParams(vmem_limit_bytes=ROOM),
        cost_estimate=lasting(22),
    )(apart, member, cos, sin, projected, projected, projected, grad_mixed)


ROWS = 256


def norm_parts(field):
    centered = field - jnp.mean(field, axis=-1, keepdims=True)
    scale = lax.rsqrt(jnp.mean(centered * centered, axis=-1, keepdims=True) + NORM_EPS)
    return centered * scale, scale


def wide(ref, at):
    return ref[at, :].astype(jnp.float32)


def row_blocks(count, body):
    def step(i, carry):
        body(i, pl.ds(pl.multiple_of(i * ROWS, ROWS), ROWS))
        return carry

    lax.fori_loop(0, count // ROWS, step, 0)


TALL = 512


def streamed(kernel, steps, scalars, fields, outs, scratch, microseconds, room=ROOM):
    def spec(shape, block=None, at=None):
        if block is None:
            return pl.BlockSpec(shape, lambda i, *scalars: (0,) * len(shape))
        return pl.BlockSpec(block, at)

    fields = [field if isinstance(field, tuple) else (field,) for field in fields]
    return pl.pallas_call(
        kernel,
        grid_spec=pltpu.PrefetchScalarGridSpec(
            num_scalar_prefetch=len(scalars),
            grid=(steps,),
            in_specs=[spec(field[0].shape, *field[1:]) for field in fields],
            out_specs=[spec(out[0], *out[2:]) for out in outs],
            scratch_shapes=[pltpu.VMEM(shape, dtype) for shape, dtype in scratch],
        ),
        out_shape=[jax.ShapeDtypeStruct(*out[:2]) for out in outs],
        compiler_params=pltpu.CompilerParams(vmem_limit_bytes=room),
        cost_estimate=lasting(microseconds),
    )(*scalars, *[field[0] for field in fields])


def by_rows(field, rows, shift=None):
    if shift is None:
        return field, (rows, field.shape[1]), lambda i, *scalars: (i, 0)
    return field, (rows, field.shape[1]), lambda i, *scalars: (shift(i, *scalars), 0)


def whole_spec(shape):
    return pl.BlockSpec(shape, lambda *at: (0,) * len(shape))


def turn(field, cos, sin):
    half = HEAD_DIM // 2
    lane = lax.broadcasted_iota(jnp.int32, field.shape, 1) % HEAD_DIM
    crossed = jnp.where(lane < half, pltpu.roll(field, LANES - half, 1), pltpu.roll(field, half, 1))
    return field * cos + crossed * sin


def project_kernel(flags, rows_ref, cos_ref, sin_ref, vectors, w_own, w_got, out_ref, turned_ref, weight_ref):
    @pl.when(pl.program_id(0) == 0)
    def _():
        weight_ref[...] = jnp.where(flags[0] == 1, w_own[...], w_got[...])

    unit, unused = norm_parts(rows_ref[...].astype(jnp.float32))
    norm = unit * vectors[0:1, :] + vectors[1:2, :]
    turned_ref[...] = norm.T.astype(jnp.bfloat16)
    norm = norm.astype(jnp.bfloat16)
    for c in range(weight_ref.shape[0]):
        field = dot(norm, weight_ref[c])
        if c == 2:
            out_ref[c] = field.astype(jnp.bfloat16)
        else:
            for p in range(field.shape[1] // LANES):
                lanes = slice(p * LANES, (p + 1) * LANES)
                out_ref[c, :, lanes] = turn(field[:, lanes], cos_ref[...], sin_ref[...]).astype(jnp.bfloat16)


def project(flags, rows, vectors, cos, sin, w_own, w_got):
    whole, width = rows.shape
    count, unused, columns = w_own.shape
    low = jnp.bfloat16
    return streamed(
        project_kernel,
        whole // ROWS,
        [flags],
        [by_rows(rows, ROWS), by_rows(cos, ROWS), by_rows(sin, ROWS), vectors, w_own, w_got],
        [
            ((count, whole, columns), low, (count, ROWS, columns), lambda i, flags: (0, i, 0)),
            ((width, whole), low, (width, ROWS), lambda i, flags: (0, i)),
            (w_own.shape, low),
        ],
        [],
        8,
    )


def gelu_both(up):
    root = math.sqrt(2.0 / math.pi)
    square = up * up
    bent = jnp.tanh(root * up * (1.0 + 0.044715 * square))
    half = 0.5 * (1.0 + bent)
    slope = half + 0.5 * up * (1.0 - bent * bent) * (root * (1.0 + 3.0 * 0.044715 * square))
    return up * half, slope


def feed_kernel(early, *refs):
    if early:
        flags, weight_ref, rows_ref, own_ref, got_ref, cot_ref, vectors, up_own, down_own, got = refs[:10]
        norm, norm_t, grad, grad_t = refs[10:14]
        up_got, down_got = got.at[: norm.shape[1]], got.at[norm.shape[1] :]
    else:
        flags, norm, norm_t, grad, grad_t, up_own, down_own, up_got, down_got = refs[:9]
    back_ref, act_ref, pieces_ref, down_ref, up_w, up_sum, down_sum = refs[-7:]
    part = pieces_ref.shape[2]
    step, last = pl.program_id(0), pl.num_programs(0) - 1

    @pl.when(step == 0)
    def _():
        up_w[...] = jnp.where(flags[0] == 1, up_own[...], up_got[...])
        down_ref[...] = jnp.where(flags[0] == 1, down_own[...], down_got[...])

    if early:

        def head(i, at):
            unit, unused = norm_parts(wide(rows_ref, at) + wide(own_ref, at) + wide(got_ref, at))
            field = unit * vectors[2:3, :] + vectors[3:4, :]
            norm[at, :] = field.astype(jnp.bfloat16)
            norm_t[:, at] = field.T.astype(jnp.bfloat16)
            field = wide(cot_ref, at) * weight_ref[weight_ref.shape[0] - 1]
            grad[at, :] = field.astype(jnp.bfloat16)
            grad_t[:, at] = field.T.astype(jnp.bfloat16)

        row_blocks(norm.shape[0], head)
    value, rise = gelu_both(dot(norm[...], up_w[...]))
    act_ref[...] = value.astype(jnp.bfloat16)
    slope = (dot(grad[...], down_ref[...], NT) * rise).astype(jnp.bfloat16)
    back_ref[...] = dot(slope, up_w[...], NT).astype(jnp.bfloat16)

    def grads(i, at):
        fields = (dot(norm_t[at, :], slope), dot(grad_t[at, :], act_ref[...]))
        for k, (field, total) in enumerate(zip(fields, (up_sum, down_sum))):

            @pl.when(step == 0)
            def _():
                total[at, :] = field

            @pl.when(step == last)
            def _():
                low = (total[at, :] + field).astype(jnp.bfloat16)
                for p in range(2):
                    pieces_ref[2 * k + p, at, :] = low[:, p * part : (p + 1) * part]

    row_blocks(norm_t.shape[0], grads)


def feed(early, scalars, fields, w_up, w_down, *got):
    whole, width = fields[0].shape
    hidden = w_up.shape[1] // 2
    rows = whole // 2
    half = 0 if early else 1
    low = jnp.bfloat16

    def across(i, *scalars):
        return (0, i)

    tokens = ((whole, width), low, (rows, width), lambda i, *scalars: (i, 0))
    turned = ((width, whole), low, (width, rows), across)
    if early:
        operands = [by_rows(field, rows) for field in fields[:4]] + [fields[4]]
        outs = [tokens, turned, tokens, turned]
    else:
        operands = [by_rows(fields[0], rows), (fields[1], (width, rows), across)]
        operands += [by_rows(fields[2], rows), (fields[3], (width, rows), across)]
        outs = []
    operands += [
        (w_up, (width, hidden), lambda i, *scalars: (0, half)),
        (w_down, (hidden, width), lambda i, *scalars: (half, 0)),
        *got,
    ]
    outs += [
        tokens,
        ((whole, hidden), low, (rows, hidden), lambda i, *scalars: (i, 0)),
        ((4, width, hidden // 2), low),
        ((hidden, width), low),
    ]
    sums = ((width, hidden), jnp.float32)
    return streamed(
        functools.partial(feed_kernel, early), 2, scalars, operands, outs, [((width, hidden), low), sums, sums], 17
    )


def lower_kernel(flags, act_early, act_late, rows_ref, own_ref, got_ref, cot_ref, early_ref, late_ref, keep_ref, send_ref, sums_ref):
    step, half = pl.program_id(0), pl.num_programs(0) // 2

    @pl.when(step == 0)
    def _():
        sums_ref[...] = jnp.zeros_like(sums_ref)

    total = dot(act_early[...], early_ref[...]) + dot(act_late[...], late_ref[...])
    cot = cot_ref[...].astype(jnp.float32)

    @pl.when(step < half)
    def _():
        send_ref[...] = total.astype(jnp.bfloat16)
        sums_ref[0:1, :] += jnp.sum(total * cot, axis=0, keepdims=True)

    @pl.when(step >= half)
    def _():
        parts = [ref[...].astype(jnp.float32) for ref in (rows_ref, own_ref, got_ref)]
        block = total + parts[0] + parts[1] + parts[2]
        keep_ref[...] = block
        sums_ref[0:1, :] += jnp.sum(block * cot, axis=0, keepdims=True)


def theirs_first(steps):
    return lambda i, flags, *more: lax.rem((1 - flags[1]) * (steps // 2) + i, steps)


def halves(steps, rows, width):
    keep = (rows, width), lambda i, *scalars: (jnp.maximum(i - steps // 2, 0), 0)
    send = (rows, width), lambda i, *scalars: (jnp.minimum(i, steps // 2 - 1), 0)
    return keep, send


def lower(flags, act_early, act_late, down_early, down_late, rows, own, got, cot):
    whole, width = rows.shape
    steps = whole // ROWS
    order = theirs_first(steps)
    keep, send = halves(steps, ROWS, width)
    shape = (whole // 2, width)
    return streamed(
        lower_kernel,
        steps,
        [flags],
        [by_rows(field, ROWS, order) for field in (act_early, act_late, rows, own, got, cot)] + [down_early, down_late],
        [(shape, jnp.float32, *keep), (shape, jnp.bfloat16, *send), ((8, width), jnp.float32)],
        [],
        6,
        SNUG,
    )


def middle_kernel(
    flags, weight_ref, rows_ref, own_ref, got_ref, cot_ref, early_own, early_got, late_own, late_got, mixed_ref,
    vectors, w_ref, grad_ref, gmixed_ref, gout_ref, sums_ref, gout,
):
    step, last = pl.program_id(0), pl.num_programs(0) - 1
    unit, scale = norm_parts(sum(ref[...].astype(jnp.float32) for ref in (rows_ref, own_ref, got_ref)))
    back = sum(ref[...].astype(jnp.float32) for ref in (early_own, early_got, late_own, late_got))
    inner = back * vectors[2:3, :]
    mean = jnp.mean(inner, axis=-1, keepdims=True)
    slant = jnp.mean(inner * unit, axis=-1, keepdims=True)
    cot = cot_ref[...].astype(jnp.float32) * weight_ref[weight_ref.shape[0] - 1]
    grad = cot + scale * (inner - mean - unit * slant)
    low = grad.astype(jnp.bfloat16)
    grad_ref[...] = low
    gmixed_ref[...] = dot(low, w_ref[...], NT).astype(jnp.bfloat16)
    part = dot(grad.T.astype(jnp.bfloat16), mixed_ref[...])

    @pl.when(step == 0)
    def _():
        gout[...] = part
        sums_ref[...] = jnp.zeros_like(sums_ref)

    @pl.when(step > 0)
    def _():
        gout[...] += part

    @pl.when(step == last)
    def _():
        gout_ref[...] = gout[...].astype(jnp.bfloat16)

    @pl.when(step // ((last + 1) // 2) == flags[1])
    def _():
        sums_ref[0:1, :] += jnp.sum(back * unit, axis=0, keepdims=True)
        sums_ref[1:2, :] += jnp.sum(back, axis=0, keepdims=True)


def middle(flags, weight, fields, mixed, vectors, w_out):
    whole, width = fields[0].shape
    columns = mixed.shape[1]
    low = jnp.bfloat16
    in_order = lambda i, *scalars: (i, 0)
    return streamed(
        middle_kernel,
        whole // ROWS,
        [flags, weight],
        [by_rows(field, ROWS) for field in (*fields, mixed)] + [vectors, w_out],
        [
            ((whole, width), low, (ROWS, width), in_order),
            ((whole, columns), low, (ROWS, columns), in_order),
            ((width, columns), low),
            ((8, width), jnp.float32),
        ],
        [((width, columns), jnp.float32)],
        8,
    )


def weigh_kernel(flags, turned_ref, out_grad_ref, grad_ref, *out_refs):
    last = grad_ref.shape[0]
    for j, out_ref in enumerate(out_refs):
        piece = flags[3 + j]

        @pl.when(piece < last)
        def _():
            out_ref[...] = dot(turned_ref[...], grad_ref[jnp.minimum(piece, last - 1)]).astype(jnp.bfloat16)

        @pl.when(piece == last)
        def _():
            out_ref[...] = out_grad_ref[...]


def weigh(flags, turned, grad, out_grad):
    width, columns = turned.shape[0], grad.shape[2]
    piece = ((width, columns), jnp.bfloat16, (ROWS, columns), lambda i, flags: (i, 0))
    return streamed(
        weigh_kernel, width // ROWS, [flags], [by_rows(turned, ROWS), by_rows(out_grad, ROWS), grad], [piece] * 4, [], 4
    )


def unproject_kernel(flags, grad_ref, rows_ref, weight, keep_ref, send_ref, sums_ref):
    step, half = pl.program_id(0), pl.num_programs(0) // 2
    total = dot(grad_ref[0], weight[0], NT)
    for c in range(1, grad_ref.shape[0]):
        total = total + dot(grad_ref[c], weight[c], NT)
    unit, unused = norm_parts(rows_ref[...].astype(jnp.float32))

    @pl.when(step == 0)
    def _():
        sums_ref[...] = jnp.zeros_like(sums_ref)

    sums_ref[0:1, :] += jnp.sum(total * unit, axis=0, keepdims=True)
    sums_ref[1:2, :] += jnp.sum(total, axis=0, keepdims=True)

    @pl.when(step < half)
    def _():
        send_ref[...] = total.astype(jnp.bfloat16)

    @pl.when(step >= half)
    def _():
        keep_ref[...] = total


def unproject(flags, grad, weight, rows):
    whole, width = rows.shape
    count, unused, columns = grad.shape
    steps = whole // ROWS
    order = theirs_first(steps)
    keep, send = halves(steps, ROWS, width)
    shape = (whole // 2, width)
    return streamed(
        unproject_kernel,
        steps,
        [flags],
        [(grad, (count, ROWS, columns), lambda i, flags: (0, order(i, flags), 0)), by_rows(rows, ROWS, order), weight],
        [(shape, jnp.float32, *keep), (shape, jnp.bfloat16, *send), ((8, width), jnp.float32)],
        [],
        5,
        SNUG,
    )


def last_kernel(flags, rows_ref, resid_ref, keep_ref, got_ref, block_keep, block_got, vectors, out_ref):
    unit, scale = norm_parts(rows_ref[...].astype(jnp.float32))
    inner = (keep_ref[...] + got_ref[...].astype(jnp.float32)) * vectors[0:1, :]
    mean = jnp.mean(inner, axis=-1, keepdims=True)
    slant = jnp.mean(inner * unit, axis=-1, keepdims=True)
    grad = resid_ref[...].astype(jnp.float32) + scale * (inner - mean - unit * slant)
    out_ref[0] = grad.astype(jnp.bfloat16)
    out_ref[1] = (block_keep[...] + block_got[...].astype(jnp.float32)).astype(jnp.bfloat16)


def last(flags, rows, resid, keep, got, block_keep, block_got, vectors):
    half, width = keep.shape
    steps = half // ROWS

    def mine(i, flags):
        return flags[1] * steps + i

    out = ((2, half, width), jnp.bfloat16, (2, ROWS, width), lambda i, flags: (0, i, 0))
    fields = [by_rows(rows, ROWS, mine), by_rows(resid, ROWS, mine)]
    fields += [by_rows(field, ROWS) for field in (keep, got, block_keep, block_got)]
    return streamed(last_kernel, steps, [flags], fields + [vectors], [out], [], 3, SNUG)[0]


def past_kernel(dwa_ref, hist_ref, cot_ref, grad_ref, part_ref, sums_ref):
    @pl.when(pl.program_id(0) == 0)
    def _():
        sums_ref[...] = jnp.zeros_like(sums_ref)

    grad = cot_ref[...].astype(jnp.float32)
    total = jnp.zeros_like(grad)
    for j in range(hist_ref.shape[0]):
        field = hist_ref[j].astype(jnp.float32)
        total += dwa_ref[j] * field
        grad_ref[j] = (dwa_ref[j] * grad).astype(jnp.bfloat16)
        sums_ref[j : j + 1, :] += jnp.sum(field * grad, axis=0, keepdims=True)
    part_ref[...] = total


def past(dwa, history, cot):
    count, rows, width = history.shape
    layers = pl.BlockSpec((count, ROWS, width), lambda i: (0, i, 0))
    tokens = pl.BlockSpec((ROWS, width), lambda i: (i, 0))
    return pl.pallas_call(
        past_kernel,
        grid=(rows // ROWS,),
        in_specs=[pl.BlockSpec(memory_space=pltpu.SMEM), layers, tokens],
        out_specs=[layers, tokens, whole_spec((8, width))],
        out_shape=[
            jax.ShapeDtypeStruct(history.shape, jnp.bfloat16),
            jax.ShapeDtypeStruct((rows, width), jnp.float32),
            jax.ShapeDtypeStruct((8, width), jnp.float32),
        ],
        compiler_params=pltpu.CompilerParams(vmem_limit_bytes=ROOM),
        cost_estimate=lasting(3),
    )(dwa, history, cot)


def present_kernel(flags, weight_ref, part_ref, own_ref, got_ref, out_ref, grad_ref):
    here = jnp.where(flags[0] == 1, own_ref[1], got_ref[1]).astype(jnp.float32)
    out_ref[...] = (part_ref[...] + weight_ref[weight_ref.shape[0] - 1] * here).astype(jnp.bfloat16)
    grad_ref[...] = jnp.where(flags[0] == 1, own_ref[0], got_ref[0])


def present(flags, weight, part, own, got):
    rows, width = part.shape
    both = (2, ROWS, width), lambda i, *scalars: (0, i, 0)
    out = ((rows, width), jnp.bfloat16, (ROWS, width), lambda i, *scalars: (i, 0))
    fields = [by_rows(part, ROWS), (own, *both), (got, *both)]
    return streamed(present_kernel, rows // ROWS, [flags, weight], fields, [out] * 2, [], 2, SNUG)


def place_kernel(flags, here_ref, there_ref, qkv_ref, out_ref, up_ref, down_ref):
    near, far = flags[1], flags[2]
    part = out_ref.shape[1]
    for k in range(2):
        for c in range(2):
            field = jnp.where(near == c, here_ref[k ^ far], there_ref[k ^ far]).astype(jnp.float32)
            if 2 * k + c < 3:
                qkv_ref[2 * k + c] = field[:, :part]
            else:
                out_ref[...] = field[:, :part]
            for half in range(2):
                at = (2 * half + k) * part
                (up_ref, down_ref)[c][:, at : at + part] = field[:, (1 + half) * part : (2 + half) * part]


def place(flags, here, there):
    rows, part = here.shape[1], here.shape[2] // 3
    outs = [((3, rows, part), jnp.float32), ((rows, part), jnp.float32)]
    outs += [((rows, 4 * part), jnp.float32)] * 2
    return streamed(place_kernel, 1, [flags], [here, there], outs, [], 3, SNUG)


AXES = ("tp", "dp", "far", "near")


def moves(chosen, move):
    sizes = [lax.axis_size(name) for name in AXES]
    places = [place for place in itertools.product(*map(range, sizes)) if chosen(*place)]
    index = lambda place: functools.reduce(lambda at, step: at * step[0] + step[1], zip(sizes, place), 0)
    return [(index(place), index(move(*place))) for place in places]


def away(t, d, k, c):
    return t != c


def anyone(t, d, k, c):
    return True


def swap_diagonal(field):
    return lax.ppermute(field, AXES, moves(away, lambda t, d, k, c: (c, d, k, t)))


def send_to_owner(field, other_far, other_tp):
    return lax.ppermute(
        field,
        AXES,
        moves(
            away if not other_far and not other_tp else anyone,
            lambda t, d, k, c: (c, d, k ^ other_far, t ^ other_tp),
        ),
    )


def swap_far(field):
    return lax.ppermute(field, "far", [(0, 1), (1, 0)])


def swap_near(field):
    return lax.ppermute(field, "near", [(0, 1), (1, 0)])


def after(field, *others):
    return lax.optimization_barrier((field, *others))[0]


def ordered(own, other, first, axis=0):
    return jnp.where(
        first, jnp.concatenate([own, other], axis=axis), jnp.concatenate([other, own], axis=axis)
    )


def part_of(field, index, axis):
    size = field.shape[axis] // 2
    return lax.dynamic_slice_in_dim(field, index * size, size, axis)


def add(*fields):
    return sum(field.astype(jnp.float32) for field in fields).astype(jnp.bfloat16)


def scatter_plane(pieces):
    return lax.psum_scatter(pieces, ("tp", "far"), scatter_dimension=0, tiled=True)[0]


def scatter_rows(piece):
    return lax.psum_scatter(piece, "dp", scatter_dimension=0, tiled=True)


def move_rows(block):
    dps = lax.axis_size("dp")
    if dps > 8:
        return [scatter_rows(block)]
    block = block.reshape(dps, block.shape[0] // dps, block.shape[1])
    place = lax.axis_index("dp")
    moved = [lax.dynamic_index_in_dim(block, place, 0, keepdims=False)]
    for step in range(1, dps):
        sent = lax.dynamic_index_in_dim(block, lax.rem(place + step, dps), 0, keepdims=False)
        moved.append(lax.ppermute(sent, "dp", [(d, (d + step) % dps) for d in range(dps)]))
    return moved


def sum_over(field, name):
    size = lax.axis_size(name)
    bit = 1
    while bit < size:
        field = field + lax.ppermute(field, name, [(d, d ^ bit) for d in range(size)])
        bit *= 2
    return field


def local(
    layer_input,
    history,
    cotangent,
    lengths,
    dwa_weights,
    gain_one,
    bias_one,
    w_qkv,
    w_out,
    gain_two,
    bias_two,
    w_up,
    w_down,
):
    rows = layer_input.shape[1]
    whole = rows * lax.axis_size("tp")
    hist_count = history.shape[0]
    part, far, near = lax.axis_index("tp"), lax.axis_index("far"), lax.axis_index("near")
    same = near == part
    pieces = [2 * (far ^ a) + (part ^ b) for a in range(2) for b in range(2)]
    flags = jnp.stack([same.astype(jnp.int32), near, far, *pieces, part])

    input_got = swap_diagonal(layer_input[0])
    qkv_got = swap_diagonal(w_qkv)
    early_got = jnp.concatenate([part_of(w_up, 0, 1), part_of(w_down, 0, 0)], axis=0)
    late_up, late_down = part_of(w_up, 1, 1), part_of(w_down, 1, 0)
    last_own = jnp.concatenate([w_out, cotangent[0]], axis=0)
    vectors = jnp.stack([gain_one, bias_one, gain_two, bias_two])

    own_lengths = jnp.where(same, lengths, swap_near(lengths))[0]
    seq_owner, token_place = positions(own_lengths, whole)
    lane = jnp.arange(LANES, dtype=jnp.int32)
    member = seq_owner[:, None] == lane[None, :]
    apart = jnp.where(member | (lane >= lengths.shape[1])[None, :], 0.0, NEG_FILL).astype(jnp.bfloat16)
    member = member.astype(jnp.bfloat16)
    half_dim = HEAD_DIM // 2
    frequency = jnp.exp((lane % half_dim).astype(jnp.float32) * (-math.log(10000.0) / half_dim))
    angles = token_place.astype(jnp.float32)[:, None] * frequency[None, :]
    cos_table = jnp.cos(angles)
    sin_table = jnp.sin(angles) * jnp.where(lane % HEAD_DIM < half_dim, -1.0, 1.0)[None, :]
    grad_history, past_sum, sums_past = past(dwa_weights, history[:, 0], cotangent[0])

    input_half = jnp.where(same, layer_input[0], input_got)
    layer_rows = ordered(input_half, swap_near(input_half), near == 0)
    layer_rows, last_own, early_got, late_up, vectors, past_sum, *tables = lax.optimization_barrier(
        (layer_rows, last_own, early_got, late_up, vectors, past_sum)
        + (cos_table, sin_table, apart, member)
    )
    cos_table, sin_table, apart, member = tables
    early_got = swap_diagonal(early_got)
    last_got = swap_diagonal(last_own)
    projected, norm_one_t, weight_qkv = project(
        flags, layer_rows, vectors, cos_table, sin_table, w_qkv, qkv_got
    )
    mixed = attend(apart, member, projected, LONGEST)
    late_up = swap_diagonal(after(late_up, mixed))
    late_down = swap_diagonal(after(late_down, mixed))
    last_got = jnp.where(same, last_own, last_got)
    weight_out = last_got[: w_out.shape[0]]
    attn = jnp.dot(mixed, weight_out, preferred_element_type=jnp.float32).astype(jnp.bfloat16)
    attn_got = swap_near(attn)
    cot_half = last_got[w_out.shape[0] :]
    cot_rows = ordered(cot_half, swap_near(cot_half), near == 0)
    scalars = [flags, dwa_weights]
    fields = [layer_rows, attn, attn_got, cot_rows, vectors]
    *kept, back_early, act_early, early_pieces, down_early = feed(True, scalars, fields, w_up, w_down, early_got)
    early_sum = scatter_plane(after(early_pieces, late_up, late_down))
    back_late, act_late, late_pieces, down_late = feed(False, [flags], kept, w_up, w_down, late_up, late_down)
    late_sum = scatter_plane(late_pieces)
    fields = [layer_rows, attn, attn_got, cot_rows, back_early, swap_near(back_early), back_late, swap_near(back_late)]
    grad_attn, grad_mixed, grad_out, sums_two = middle(flags, dwa_weights, fields, mixed, vectors, weight_out)
    grad_qkv = attend_back(apart, member, cos_table, sin_table, projected, grad_mixed, LONGEST)
    owned = weigh(flags, norm_one_t, grad_qkv, grad_out)
    moved = [send_to_owner(owned[j], j // 2, j % 2) for j in range(4)]
    keep, send, sums_one = unproject(flags, after(grad_qkv, owned[0]), weight_qkv, layer_rows)
    block_keep, block_send, sums_now = lower(
        flags, act_early, act_late, down_early, down_late, layer_rows, attn, attn_got, after(cot_rows, send)
    )
    small = jnp.concatenate([sums_one[:2], sums_two[:2], sums_now[:1], sums_past[:hist_count]], axis=0)
    for name in ("near", "dp"):
        small = sum_over(small, name)
    small, keep, send, block_keep, block_send, *moved = lax.optimization_barrier(
        (small, keep, send, block_keep, block_send, *moved)
    )
    attn_one = add(jnp.where(same, owned[0], moved[0]), *moved[1:])
    attn_moved = move_rows(attn_one)
    feed_sum = scatter_rows(jnp.concatenate([after(early_sum, attn_one), late_sum], axis=1))
    ours = last(
        flags, layer_rows, grad_attn, keep, swap_near(send), block_keep, swap_near(block_send), vectors
    )
    for name in ("tp", "far"):
        small = sum_over(small, name)
    small, ours, *attn_moved = lax.optimization_barrier((small, ours, *attn_moved))
    theirs = swap_diagonal(ours)
    feed_sum = after(feed_sum, small)
    feed_got = swap_diagonal(feed_sum)
    attn_sum = add(*attn_moved)
    blocks = jnp.concatenate([attn_sum, jnp.where(same, feed_sum, feed_got)], axis=1)
    here = jnp.stack([blocks, swap_far(blocks)])
    output, grad_input = present(flags, dwa_weights, past_sum, ours, theirs)
    here = after(here, output)
    grad_w_qkv, grad_w_out, grad_w_up, grad_w_down = place(flags, here, swap_near(here))

    return (
        output[None],
        grad_input[None],
        grad_history[:, None],
        jnp.sum(jnp.concatenate([small[5:], small[4:5]], axis=0), axis=1),
        small[0],
        small[1],
        grad_w_qkv,
        grad_w_out.T,
        small[2],
        small[3],
        grad_w_up,
        grad_w_down.T,
    )


def positions(seq_lengths, token_count):
    seq_ends = jnp.cumsum(seq_lengths)
    seq_starts = seq_ends - seq_lengths
    token_index = jnp.arange(token_count, dtype=jnp.int32)
    seq_owner = jnp.sum((token_index[:, None] >= seq_ends[None, :]).astype(jnp.int32), axis=1)
    picked = (
        seq_owner[:, None] == jnp.arange(seq_lengths.shape[0], dtype=jnp.int32)[None, :]
    ).astype(jnp.int32)
    seq_begin = jnp.sum(picked * seq_starts[None, :], axis=1)
    return (seq_owner, token_index - seq_begin)


def solution(mesh):
    tps, dps, reps = (mesh.shape[name] for name in ("tp", "dp", "rep"))
    split = Mesh(mesh.devices.reshape(tps, dps, reps // 2, 2), AXES)
    in_specs = (
        P(("dp", "far", "near"), "tp", None),
        P(None, ("dp", "far", "near"), "tp", None),
        P(("dp", "far", "near"), "tp", None),
        P(("dp", "far", "near"), None),
        P(),
        P(),
        P(),
        P(None, None, "tp"),
        P("tp", None),
        P(),
        P(),
        P(None, "tp"),
        P("tp", None),
    )
    out_specs = (
        P(("dp", "far", "near"), "tp", None),
        P(("dp", "far", "near"), "tp", None),
        P(None, ("dp", "far", "near"), "tp", None),
        P(),
        P(),
        P(),
        P(None, "dp", "tp"),
        P("tp", "dp"),
        P(),
        P(),
        P("dp", "tp"),
        P("tp", "dp"),
    )
    return jax.shard_map(local, mesh=split, in_specs=in_specs, out_specs=out_specs, check_vma=False)
```

```python
import functools
import itertools
import math

import jax
import jax.numpy as jnp
from jax import lax
from jax.experimental import pallas as pl
from jax.experimental.pallas import tpu as pltpu
from jax.sharding import Mesh, PartitionSpec as P

HEAD_DIM = 64
LONGEST = 512
NEG_FILL = -1e30
NORM_EPS = 1e-05
RATE = 3e6
ROOM = 60 << 20
SNUG = 18 << 20


def lasting(microseconds):
    return pl.CostEstimate(flops=0, transcendentals=0, bytes_accessed=int(microseconds * RATE))


BLOCK = 256
LANES = 128
NT = (((1,), (1,)), ((), ()))


def dot(a, b, dims=(((1,), (0,)), ((), ()))):
    return lax.dot_general(a, b, dims, preferred_element_type=jnp.float32)


def spans(whole, reach):
    back = -(-(reach - 1) // BLOCK)
    runs = []
    for i in range(whole // BLOCK):
        count = min(i, back) + 1
        if runs and runs[-1][2] == count:
            runs[-1][1] = i + 1
        else:
            runs.append([i, i + 1, count])
    return runs


def each_block(whole, reach, body):
    for first, last, count in spans(whole, reach):

        def step(i, carry, count=count):
            body(i, i + 1 - count, count)
            return carry

        lax.fori_loop(first, last, step, 0)


def block_at(i, count=1):
    return pl.ds(pl.multiple_of(i * BLOCK, BLOCK), count * BLOCK)


def head_query(q_ref, apart_ref, i, head):
    lane = lax.broadcasted_iota(jnp.int32, (BLOCK, LANES), 1) // HEAD_DIM
    query = q_ref[block_at(i), :] * (HEAD_DIM**-0.5)
    query = jnp.where(lane == head, query, jnp.zeros_like(query))
    return query, jnp.concatenate([query, apart_ref[block_at(i), :]], axis=1)


def attend_kernel(reach, apart_ref, member_ref, q_ref, k_ref, v_ref, out_ref, keys):
    whole = q_ref.shape[0]
    lane = lax.broadcasted_iota(jnp.int32, (BLOCK, LANES), 1) // HEAD_DIM
    keys[:, :LANES] = k_ref[...]
    keys[:, LANES:] = member_ref[...]

    def one(i, first, count, head):
        unused, query = head_query(q_ref, apart_ref, i, head)
        own = dot(query, keys[block_at(i), :], NT)
        key_at = lax.broadcasted_iota(jnp.int32, own.shape, 1)
        query_at = lax.broadcasted_iota(jnp.int32, own.shape, 0)
        scores = jnp.where(key_at <= query_at, own, NEG_FILL)
        if count > 1:
            scores = jnp.concatenate([dot(query, keys[block_at(first, count - 1), :], NT), scores], axis=1)
        exponent = jnp.exp(scores - jnp.max(scores, axis=1, keepdims=True))
        row_sum = jnp.sum(exponent, axis=1, keepdims=True)
        return dot(exponent.astype(jnp.bfloat16), v_ref[block_at(first, count), :]) * (1.0 / row_sum)

    def body(i, first, count):
        mixed = [one(i, first, count, head) for head in range(2)]
        out_ref[block_at(i), :] = jnp.where(lane == 0, *mixed).astype(out_ref.dtype)

    each_block(whole, reach, body)


def attend(apart, member, projected, reach):
    count, whole, width = projected.shape

    def block(c):
        return pl.BlockSpec((None, whole, LANES), lambda p: (c, 0, p))

    table = pl.BlockSpec((whole, LANES), lambda p: (0, 0))
    return pl.pallas_call(
        functools.partial(attend_kernel, reach),
        grid=(width // LANES,),
        in_specs=[table, table, block(0), block(1), block(2)],
        out_specs=pl.BlockSpec((whole, LANES), lambda p: (0, p)),
        out_shape=jax.ShapeDtypeStruct((whole, width), jnp.bfloat16),
        scratch_shapes=[pltpu.VMEM((whole, 2 * LANES), jnp.bfloat16)],
        compiler_params=pltpu.CompilerParams(vmem_limit_bytes=ROOM),
        cost_estimate=lasting(12),
    )(apart, member, projected, projected, projected)


def turn_back(field, cos, sin):
    half = HEAD_DIM // 2
    lane = lax.broadcasted_iota(jnp.int32, field.shape, 1) % HEAD_DIM
    crossed = jnp.where(lane < half, pltpu.roll(field, LANES - half, 1), pltpu.roll(field, half, 1))
    return field * cos - crossed * sin


def attend_back_kernel(
    reach, apart_ref, member_ref, cos_ref, sin_ref, q_ref, k_ref, v_ref, g_ref, out_ref, keys, keys_t, key_acc, value_acc
):
    whole = q_ref.shape[0]
    lane = lax.broadcasted_iota(jnp.int32, (BLOCK, LANES), 1) // HEAD_DIM
    keys[:, :LANES] = k_ref[...]
    keys[:, LANES:] = member_ref[...]
    keys_t[...] = k_ref[...].astype(jnp.float32).T.astype(jnp.bfloat16)
    key_acc[...] = jnp.zeros_like(key_acc)
    value_acc[...] = jnp.zeros_like(value_acc)

    def one(i, first, count, head):
        span = block_at(first, count)
        plain, query = head_query(q_ref, apart_ref, i, head)
        grad = g_ref[block_at(i), :]
        grad = jnp.where(lane == head, grad, jnp.zeros_like(grad))
        own = dot(keys[block_at(i), :], query, NT)
        key_at = lax.broadcasted_iota(jnp.int32, own.shape, 0)
        query_at = lax.broadcasted_iota(jnp.int32, own.shape, 1)
        scores = jnp.where(key_at <= query_at, own, NEG_FILL)
        if count > 1:
            scores = jnp.concatenate([dot(keys[block_at(first, count - 1), :], query, NT), scores], axis=0)
        exponent = jnp.exp(scores - jnp.max(scores, axis=0, keepdims=True))
        probs = exponent * (1.0 / jnp.sum(exponent, axis=0, keepdims=True))
        grad_values = dot(probs.astype(jnp.bfloat16), grad)
        weighted = probs * dot(v_ref[span, :], grad, NT)
        grad_scores = (weighted - probs * jnp.sum(weighted, axis=0, keepdims=True)).astype(jnp.bfloat16)
        here = dot(keys_t[:, span], grad_scores)
        return grad_values, dot(grad_scores, plain), here

    def body(i, first, count):
        span, at = block_at(first, count), block_at(i)
        values, keys_, queries = zip(*[one(i, first, count, head) for head in range(2)])
        value_acc[span, :] += values[0] + values[1]
        key_acc[span, :] += keys_[0] + keys_[1]
        row = lax.broadcasted_iota(jnp.int32, queries[0].shape, 0) // HEAD_DIM
        both = jnp.where(row == 0, *queries).T * (HEAD_DIM**-0.5)
        out_ref[0, at, :] = turn_back(both, cos_ref[at, :], sin_ref[at, :]).astype(out_ref.dtype)

    each_block(whole, reach, body)

    def finish(i, carry):
        at = block_at(i)
        out_ref[1, at, :] = turn_back(key_acc[at, :], cos_ref[at, :], sin_ref[at, :]).astype(out_ref.dtype)
        out_ref[2, at, :] = value_acc[at, :].astype(out_ref.dtype)
        return carry

    lax.fori_loop(0, whole // BLOCK, finish, 0)


def attend_back(apart, member, cos, sin, projected, grad_mixed, reach):
    count, whole, width = projected.shape

    def block(c):
        return pl.BlockSpec((None, whole, LANES), lambda p: (c, 0, p))

    table = pl.BlockSpec((whole, LANES), lambda p: (0, 0))
    return pl.pallas_call(
        functools.partial(attend_back_kernel, reach),
        grid=(width // LANES,),
        in_specs=[table] * 4 + [block(0), block(1), block(2), pl.BlockSpec((whole, LANES), lambda p: (0, p))],
        out_specs=pl.BlockSpec((count, whole, LANES), lambda p: (0, 0, p)),
        out_shape=jax.ShapeDtypeStruct((count, whole, width), jnp.bfloat16),
        scratch_shapes=[
            pltpu.VMEM((whole, 2 * LANES), jnp.bfloat16),
            pltpu.VMEM((LANES, whole), jnp.bfloat16),
            pltpu.VMEM((whole, LANES), jnp.float32),
            pltpu.VMEM((whole, LANES), jnp.float32),
        ],
        compiler_params=pltpu.CompilerParams(vmem_limit_bytes=ROOM),
        cost_estimate=lasting(22),
    )(apart, member, cos, sin, projected, projected, projected, grad_mixed)


ROWS = 256


def norm_parts(field):
    centered = field - jnp.mean(field, axis=-1, keepdims=True)
    scale = lax.rsqrt(jnp.mean(centered * centered, axis=-1, keepdims=True) + NORM_EPS)
    return centered * scale, scale


def wide(ref, at):
    return ref[at, :].astype(jnp.float32)


def row_blocks(count, body):
    def step(i, carry):
        body(i, pl.ds(pl.multiple_of(i * ROWS, ROWS), ROWS))
        return carry

    lax.fori_loop(0, count // ROWS, step, 0)


TALL = 512


def streamed(kernel, steps, scalars, fields, outs, scratch, microseconds, room=ROOM):
    def spec(shape, block=None, at=None):
        if block is None:
            return pl.BlockSpec(shape, lambda i, *scalars: (0,) * len(shape))
        return pl.BlockSpec(block, at)

    fields = [field if isinstance(field, tuple) else (field,) for field in fields]
    return pl.pallas_call(
        kernel,
        grid_spec=pltpu.PrefetchScalarGridSpec(
            num_scalar_prefetch=len(scalars),
            grid=(steps,),
            in_specs=[spec(field[0].shape, *field[1:]) for field in fields],
            out_specs=[spec(out[0], *out[2:]) for out in outs],
            scratch_shapes=[pltpu.VMEM(shape, dtype) for shape, dtype in scratch],
        ),
        out_shape=[jax.ShapeDtypeStruct(*out[:2]) for out in outs],
        compiler_params=pltpu.CompilerParams(vmem_limit_bytes=room),
        cost_estimate=lasting(microseconds),
    )(*scalars, *[field[0] for field in fields])


def by_rows(field, rows, shift=None):
    if shift is None:
        return field, (rows, field.shape[1]), lambda i, *scalars: (i, 0)
    return field, (rows, field.shape[1]), lambda i, *scalars: (shift(i, *scalars), 0)


def whole_spec(shape):
    return pl.BlockSpec(shape, lambda *at: (0,) * len(shape))


def turn(field, cos, sin):
    half = HEAD_DIM // 2
    lane = lax.broadcasted_iota(jnp.int32, field.shape, 1) % HEAD_DIM
    crossed = jnp.where(lane < half, pltpu.roll(field, LANES - half, 1), pltpu.roll(field, half, 1))
    return field * cos + crossed * sin


def project_kernel(flags, rows_ref, cos_ref, sin_ref, vectors, w_own, w_got, out_ref, turned_ref, weight_ref):
    @pl.when(pl.program_id(0) == 0)
    def _():
        weight_ref[...] = jnp.where(flags[0] == 1, w_own[...], w_got[...])

    unit, unused = norm_parts(rows_ref[...].astype(jnp.float32))
    norm = unit * vectors[0:1, :] + vectors[1:2, :]
    turned_ref[...] = norm.T.astype(jnp.bfloat16)
    norm = norm.astype(jnp.bfloat16)
    for c in range(weight_ref.shape[0]):
        field = dot(norm, weight_ref[c])
        if c == 2:
            out_ref[c] = field.astype(jnp.bfloat16)
        else:
            for p in range(field.shape[1] // LANES):
                lanes = slice(p * LANES, (p + 1) * LANES)
                out_ref[c, :, lanes] = turn(field[:, lanes], cos_ref[...], sin_ref[...]).astype(jnp.bfloat16)


def project(flags, rows, vectors, cos, sin, w_own, w_got):
    whole, width = rows.shape
    count, unused, columns = w_own.shape
    low = jnp.bfloat16
    return streamed(
        project_kernel,
        whole // ROWS,
        [flags],
        [by_rows(rows, ROWS), by_rows(cos, ROWS), by_rows(sin, ROWS), vectors, w_own, w_got],
        [
            ((count, whole, columns), low, (count, ROWS, columns), lambda i, flags: (0, i, 0)),
            ((width, whole), low, (width, ROWS), lambda i, flags: (0, i)),
            (w_own.shape, low),
        ],
        [],
        8,
    )


def gelu_both(up):
    root = math.sqrt(2.0 / math.pi)
    square = up * up
    bent = jnp.tanh(root * up * (1.0 + 0.044715 * square))
    half = 0.5 * (1.0 + bent)
    slope = half + 0.5 * up * (1.0 - bent * bent) * (root * (1.0 + 3.0 * 0.044715 * square))
    return up * half, slope


def feed_kernel(early, *refs):
    if early:
        flags, weight_ref, rows_ref, own_ref, got_ref, cot_ref, vectors, up_own, down_own, got = refs[:10]
        norm, norm_t, grad, grad_t = refs[10:14]
        up_got, down_got = got.at[: norm.shape[1]], got.at[norm.shape[1] :]
    else:
        flags, norm, norm_t, grad, grad_t, up_own, down_own, up_got, down_got = refs[:9]
    back_ref, act_ref, pieces_ref, down_ref, up_w, up_sum, down_sum = refs[-7:]
    part = pieces_ref.shape[2]
    step, last = pl.program_id(0), pl.num_programs(0) - 1

    @pl.when(step == 0)
    def _():
        up_w[...] = jnp.where(flags[0] == 1, up_own[...], up_got[...])
        down_ref[...] = jnp.where(flags[0] == 1, down_own[...], down_got[...])

    if early:

        def head(i, at):
            unit, unused = norm_parts(wide(rows_ref, at) + wide(own_ref, at) + wide(got_ref, at))
            field = unit * vectors[2:3, :] + vectors[3:4, :]
            norm[at, :] = field.astype(jnp.bfloat16)
            norm_t[:, at] = field.T.astype(jnp.bfloat16)
            field = wide(cot_ref, at) * weight_ref[weight_ref.shape[0] - 1]
            grad[at, :] = field.astype(jnp.bfloat16)
            grad_t[:, at] = field.T.astype(jnp.bfloat16)

        row_blocks(norm.shape[0], head)
    value, rise = gelu_both(dot(norm[...], up_w[...]))
    act_ref[...] = value.astype(jnp.bfloat16)
    slope = (dot(grad[...], down_ref[...], NT) * rise).astype(jnp.bfloat16)
    back_ref[...] = dot(slope, up_w[...], NT).astype(jnp.bfloat16)

    def grads(i, at):
        fields = (dot(norm_t[at, :], slope), dot(grad_t[at, :], act_ref[...]))
        for k, (field, total) in enumerate(zip(fields, (up_sum, down_sum))):

            @pl.when(step == 0)
            def _():
                total[at, :] = field

            @pl.when(step == last)
            def _():
                low = (total[at, :] + field).astype(jnp.bfloat16)
                for p in range(2):
                    pieces_ref[2 * k + p, at, :] = low[:, p * part : (p + 1) * part]

    row_blocks(norm_t.shape[0], grads)


def feed(early, scalars, fields, w_up, w_down, *got):
    whole, width = fields[0].shape
    hidden = w_up.shape[1] // 2
    rows = whole // 2
    half = 0 if early else 1
    low = jnp.bfloat16

    def across(i, *scalars):
        return (0, i)

    tokens = ((whole, width), low, (rows, width), lambda i, *scalars: (i, 0))
    turned = ((width, whole), low, (width, rows), across)
    if early:
        operands = [by_rows(field, rows) for field in fields[:4]] + [fields[4]]
        outs = [tokens, turned, tokens, turned]
    else:
        operands = [by_rows(fields[0], rows), (fields[1], (width, rows), across)]
        operands += [by_rows(fields[2], rows), (fields[3], (width, rows), across)]
        outs = []
    operands += [
        (w_up, (width, hidden), lambda i, *scalars: (0, half)),
        (w_down, (hidden, width), lambda i, *scalars: (half, 0)),
        *got,
    ]
    outs += [
        tokens,
        ((whole, hidden), low, (rows, hidden), lambda i, *scalars: (i, 0)),
        ((4, width, hidden // 2), low),
        ((hidden, width), low),
    ]
    sums = ((width, hidden), jnp.float32)
    return streamed(
        functools.partial(feed_kernel, early), 2, scalars, operands, outs, [((width, hidden), low), sums, sums], 17
    )


def lower_kernel(flags, act_early, act_late, rows_ref, own_ref, got_ref, cot_ref, early_ref, late_ref, keep_ref, send_ref, sums_ref):
    step, half = pl.program_id(0), pl.num_programs(0) // 2

    @pl.when(step == 0)
    def _():
        sums_ref[...] = jnp.zeros_like(sums_ref)

    total = dot(act_early[...], early_ref[...]) + dot(act_late[...], late_ref[...])
    cot = cot_ref[...].astype(jnp.float32)

    @pl.when(step < half)
    def _():
        send_ref[...] = total.astype(jnp.bfloat16)
        sums_ref[0:1, :] += jnp.sum(total * cot, axis=0, keepdims=True)

    @pl.when(step >= half)
    def _():
        parts = [ref[...].astype(jnp.float32) for ref in (rows_ref, own_ref, got_ref)]
        block = total + parts[0] + parts[1] + parts[2]
        keep_ref[...] = block
        sums_ref[0:1, :] += jnp.sum(block * cot, axis=0, keepdims=True)


def theirs_first(steps):
    return lambda i, flags, *more: lax.rem((1 - flags[1]) * (steps // 2) + i, steps)


def halves(steps, rows, width):
    keep = (rows, width), lambda i, *scalars: (jnp.maximum(i - steps // 2, 0), 0)
    send = (rows, width), lambda i, *scalars: (jnp.minimum(i, steps // 2 - 1), 0)
    return keep, send


def lower(flags, act_early, act_late, down_early, down_late, rows, own, got, cot):
    whole, width = rows.shape
    steps = whole // ROWS
    order = theirs_first(steps)
    keep, send = halves(steps, ROWS, width)
    shape = (whole // 2, width)
    return streamed(
        lower_kernel,
        steps,
        [flags],
        [by_rows(field, ROWS, order) for field in (act_early, act_late, rows, own, got, cot)] + [down_early, down_late],
        [(shape, jnp.float32, *keep), (shape, jnp.bfloat16, *send), ((8, width), jnp.float32)],
        [],
        6,
        SNUG,
    )


def middle_kernel(
    flags, weight_ref, rows_ref, own_ref, got_ref, cot_ref, early_own, early_got, late_own, late_got, mixed_ref,
    vectors, w_ref, grad_ref, gmixed_ref, gout_ref, sums_ref, gout,
):
    step, last = pl.program_id(0), pl.num_programs(0) - 1
    unit, scale = norm_parts(sum(ref[...].astype(jnp.float32) for ref in (rows_ref, own_ref, got_ref)))
    back = sum(ref[...].astype(jnp.float32) for ref in (early_own, early_got, late_own, late_got))
    inner = back * vectors[2:3, :]
    mean = jnp.mean(inner, axis=-1, keepdims=True)
    slant = jnp.mean(inner * unit, axis=-1, keepdims=True)
    cot = cot_ref[...].astype(jnp.float32) * weight_ref[weight_ref.shape[0] - 1]
    grad = cot + scale * (inner - mean - unit * slant)
    low = grad.astype(jnp.bfloat16)
    grad_ref[...] = low
    gmixed_ref[...] = dot(low, w_ref[...], NT).astype(jnp.bfloat16)
    part = dot(grad.T.astype(jnp.bfloat16), mixed_ref[...])

    @pl.when(step == 0)
    def _():
        gout[...] = part
        sums_ref[...] = jnp.zeros_like(sums_ref)

    @pl.when(step > 0)
    def _():
        gout[...] += part

    @pl.when(step == last)
    def _():
        gout_ref[...] = gout[...].astype(jnp.bfloat16)

    @pl.when(step // ((last + 1) // 2) == flags[1])
    def _():
        sums_ref[0:1, :] += jnp.sum(back * unit, axis=0, keepdims=True)
        sums_ref[1:2, :] += jnp.sum(back, axis=0, keepdims=True)


def middle(flags, weight, fields, mixed, vectors, w_out):
    whole, width = fields[0].shape
    columns = mixed.shape[1]
    low = jnp.bfloat16
    in_order = lambda i, *scalars: (i, 0)
    return streamed(
        middle_kernel,
        whole // ROWS,
        [flags, weight],
        [by_rows(field, ROWS) for field in (*fields, mixed)] + [vectors, w_out],
        [
            ((whole, width), low, (ROWS, width), in_order),
            ((whole, columns), low, (ROWS, columns), in_order),
            ((width, columns), low),
            ((8, width), jnp.float32),
        ],
        [((width, columns), jnp.float32)],
        8,
    )


def weigh_kernel(flags, turned_ref, out_grad_ref, grad_ref, *out_refs):
    last = grad_ref.shape[0]
    for j, out_ref in enumerate(out_refs):
        piece = flags[3 + j]

        @pl.when(piece < last)
        def _():
            out_ref[...] = dot(turned_ref[...], grad_ref[jnp.minimum(piece, last - 1)]).astype(jnp.bfloat16)

        @pl.when(piece == last)
        def _():
            out_ref[...] = out_grad_ref[...]


def weigh(flags, turned, grad, out_grad):
    width, columns = turned.shape[0], grad.shape[2]
    piece = ((width, columns), jnp.bfloat16, (ROWS, columns), lambda i, flags: (i, 0))
    return streamed(
        weigh_kernel, width // ROWS, [flags], [by_rows(turned, ROWS), by_rows(out_grad, ROWS), grad], [piece] * 4, [], 4
    )


def unproject_kernel(flags, grad_ref, rows_ref, weight, keep_ref, send_ref, sums_ref):
    step, half = pl.program_id(0), pl.num_programs(0) // 2
    total = dot(grad_ref[0], weight[0], NT)
    for c in range(1, grad_ref.shape[0]):
        total = total + dot(grad_ref[c], weight[c], NT)
    unit, unused = norm_parts(rows_ref[...].astype(jnp.float32))

    @pl.when(step == 0)
    def _():
        sums_ref[...] = jnp.zeros_like(sums_ref)

    sums_ref[0:1, :] += jnp.sum(total * unit, axis=0, keepdims=True)
    sums_ref[1:2, :] += jnp.sum(total, axis=0, keepdims=True)

    @pl.when(step < half)
    def _():
        send_ref[...] = total.astype(jnp.bfloat16)

    @pl.when(step >= half)
    def _():
        keep_ref[...] = total


def unproject(flags, grad, weight, rows):
    whole, width = rows.shape
    count, unused, columns = grad.shape
    steps = whole // ROWS
    order = theirs_first(steps)
    keep, send = halves(steps, ROWS, width)
    shape = (whole // 2, width)
    return streamed(
        unproject_kernel,
        steps,
        [flags],
        [(grad, (count, ROWS, columns), lambda i, flags: (0, order(i, flags), 0)), by_rows(rows, ROWS, order), weight],
        [(shape, jnp.float32, *keep), (shape, jnp.bfloat16, *send), ((8, width), jnp.float32)],
        [],
        5,
        SNUG,
    )


def last_kernel(flags, rows_ref, resid_ref, keep_ref, got_ref, block_keep, block_got, vectors, out_ref):
    unit, scale = norm_parts(rows_ref[...].astype(jnp.float32))
    inner = (keep_ref[...] + got_ref[...].astype(jnp.float32)) * vectors[0:1, :]
    mean = jnp.mean(inner, axis=-1, keepdims=True)
    slant = jnp.mean(inner * unit, axis=-1, keepdims=True)
    grad = resid_ref[...].astype(jnp.float32) + scale * (inner - mean - unit * slant)
    out_ref[0] = grad.astype(jnp.bfloat16)
    out_ref[1] = (block_keep[...] + block_got[...].astype(jnp.float32)).astype(jnp.bfloat16)


def last(flags, rows, resid, keep, got, block_keep, block_got, vectors):
    half, width = keep.shape
    steps = half // ROWS

    def mine(i, flags):
        return flags[1] * steps + i

    out = ((2, half, width), jnp.bfloat16, (2, ROWS, width), lambda i, flags: (0, i, 0))
    fields = [by_rows(rows, ROWS, mine), by_rows(resid, ROWS, mine)]
    fields += [by_rows(field, ROWS) for field in (keep, got, block_keep, block_got)]
    return streamed(last_kernel, steps, [flags], fields + [vectors], [out], [], 3, SNUG)[0]


def past_kernel(dwa_ref, hist_ref, cot_ref, grad_ref, part_ref, sums_ref):
    @pl.when(pl.program_id(0) == 0)
    def _():
        sums_ref[...] = jnp.zeros_like(sums_ref)

    grad = cot_ref[...].astype(jnp.float32)
    total = jnp.zeros_like(grad)
    for j in range(hist_ref.shape[0]):
        field = hist_ref[j].astype(jnp.float32)
        total += dwa_ref[j] * field
        grad_ref[j] = (dwa_ref[j] * grad).astype(jnp.bfloat16)
        sums_ref[j : j + 1, :] += jnp.sum(field * grad, axis=0, keepdims=True)
    part_ref[...] = total


def past(dwa, history, cot):
    count, rows, width = history.shape
    layers = pl.BlockSpec((count, ROWS, width), lambda i: (0, i, 0))
    tokens = pl.BlockSpec((ROWS, width), lambda i: (i, 0))
    return pl.pallas_call(
        past_kernel,
        grid=(rows // ROWS,),
        in_specs=[pl.BlockSpec(memory_space=pltpu.SMEM), layers, tokens],
        out_specs=[layers, tokens, whole_spec((8, width))],
        out_shape=[
            jax.ShapeDtypeStruct(history.shape, jnp.bfloat16),
            jax.ShapeDtypeStruct((rows, width), jnp.float32),
            jax.ShapeDtypeStruct((8, width), jnp.float32),
        ],
        compiler_params=pltpu.CompilerParams(vmem_limit_bytes=ROOM),
        cost_estimate=lasting(3),
    )(dwa, history, cot)


def present_kernel(flags, weight_ref, part_ref, own_ref, got_ref, out_ref, grad_ref):
    here = jnp.where(flags[0] == 1, own_ref[1], got_ref[1]).astype(jnp.float32)
    out_ref[...] = (part_ref[...] + weight_ref[weight_ref.shape[0] - 1] * here).astype(jnp.bfloat16)
    grad_ref[...] = jnp.where(flags[0] == 1, own_ref[0], got_ref[0])


def present(flags, weight, part, own, got):
    rows, width = part.shape
    both = (2, ROWS, width), lambda i, *scalars: (0, i, 0)
    out = ((rows, width), jnp.bfloat16, (ROWS, width), lambda i, *scalars: (i, 0))
    fields = [by_rows(part, ROWS), (own, *both), (got, *both)]
    return streamed(present_kernel, rows // ROWS, [flags, weight], fields, [out] * 2, [], 2, SNUG)


def place_kernel(flags, here_ref, there_ref, qkv_ref, out_ref, up_ref, down_ref):
    near, far = flags[1], flags[2]
    part = out_ref.shape[1]
    for k in range(2):
        for c in range(2):
            field = jnp.where(near == c, here_ref[k ^ far], there_ref[k ^ far]).astype(jnp.float32)
            if 2 * k + c < 3:
                qkv_ref[2 * k + c] = field[:, :part]
            else:
                out_ref[...] = field[:, :part]
            for half in range(2):
                at = (2 * half + k) * part
                (up_ref, down_ref)[c][:, at : at + part] = field[:, (1 + half) * part : (2 + half) * part]


def place(flags, here, there):
    rows, part = here.shape[1], here.shape[2] // 3
    outs = [((3, rows, part), jnp.float32), ((rows, part), jnp.float32)]
    outs += [((rows, 4 * part), jnp.float32)] * 2
    return streamed(place_kernel, 1, [flags], [here, there], outs, [], 3, SNUG)


AXES = ("tp", "dp", "far", "near")


def moves(chosen, move):
    sizes = [lax.axis_size(name) for name in AXES]
    places = [place for place in itertools.product(*map(range, sizes)) if chosen(*place)]
    index = lambda place: functools.reduce(lambda at, step: at * step[0] + step[1], zip(sizes, place), 0)
    return [(index(place), index(move(*place))) for place in places]


def away(t, d, k, c):
    return t != c


def anyone(t, d, k, c):
    return True


def swap_diagonal(field):
    return lax.ppermute(field, AXES, moves(away, lambda t, d, k, c: (c, d, k, t)))


def send_to_owner(field, other_far, other_tp):
    return lax.ppermute(
        field,
        AXES,
        moves(
            away if not other_far and not other_tp else anyone,
            lambda t, d, k, c: (c, d, k ^ other_far, t ^ other_tp),
        ),
    )


def swap_far(field):
    return lax.ppermute(field, "far", [(0, 1), (1, 0)])


def swap_near(field):
    return lax.ppermute(field, "near", [(0, 1), (1, 0)])


def after(field, *others):
    return lax.optimization_barrier((field, *others))[0]


def ordered(own, other, first, axis=0):
    return jnp.where(
        first, jnp.concatenate([own, other], axis=axis), jnp.concatenate([other, own], axis=axis)
    )


def part_of(field, index, axis):
    size = field.shape[axis] // 2
    return lax.dynamic_slice_in_dim(field, index * size, size, axis)


def add(*fields):
    return sum(field.astype(jnp.float32) for field in fields).astype(jnp.bfloat16)


def scatter_plane(pieces):
    return lax.psum_scatter(pieces, ("tp", "far"), scatter_dimension=0, tiled=True)[0]


def scatter_rows(piece):
    return lax.psum_scatter(piece, "dp", scatter_dimension=0, tiled=True)


def move_rows(block):
    dps = lax.axis_size("dp")
    if dps > 8:
        return [scatter_rows(block)]
    block = block.reshape(dps, block.shape[0] // dps, block.shape[1])
    place = lax.axis_index("dp")
    moved = [lax.dynamic_index_in_dim(block, place, 0, keepdims=False)]
    for step in range(1, dps):
        sent = lax.dynamic_index_in_dim(block, lax.rem(place + step, dps), 0, keepdims=False)
        moved.append(lax.ppermute(sent, "dp", [(d, (d + step) % dps) for d in range(dps)]))
    return moved


def sum_over(field, name):
    size = lax.axis_size(name)
    bit = 1
    while bit < size:
        field = field + lax.ppermute(field, name, [(d, d ^ bit) for d in range(size)])
        bit *= 2
    return field


def local(
    layer_input,
    history,
    cotangent,
    lengths,
    dwa_weights,
    gain_one,
    bias_one,
    w_qkv,
    w_out,
    gain_two,
    bias_two,
    w_up,
    w_down,
):
    rows = layer_input.shape[1]
    whole = rows * lax.axis_size("tp")
    hist_count = history.shape[0]
    part, far, near = lax.axis_index("tp"), lax.axis_index("far"), lax.axis_index("near")
    same = near == part
    pieces = [2 * (far ^ a) + (part ^ b) for a in range(2) for b in range(2)]
    flags = jnp.stack([same.astype(jnp.int32), near, far, *pieces, part])

    input_got = swap_diagonal(layer_input[0])
    qkv_got = swap_diagonal(w_qkv)
    early_got = jnp.concatenate([part_of(w_up, 0, 1), part_of(w_down, 0, 0)], axis=0)
    late_up, late_down = part_of(w_up, 1, 1), part_of(w_down, 1, 0)
    last_own = jnp.concatenate([w_out, cotangent[0]], axis=0)
    vectors = jnp.stack([gain_one, bias_one, gain_two, bias_two])

    own_lengths = jnp.where(same, lengths, swap_near(lengths))[0]
    seq_owner, token_place = positions(own_lengths, whole)
    lane = jnp.arange(LANES, dtype=jnp.int32)
    member = seq_owner[:, None] == lane[None, :]
    apart = jnp.where(member | (lane >= lengths.shape[1])[None, :], 0.0, NEG_FILL).astype(jnp.bfloat16)
    member = member.astype(jnp.bfloat16)
    half_dim = HEAD_DIM // 2
    frequency = jnp.exp((lane % half_dim).astype(jnp.float32) * (-math.log(10000.0) / half_dim))
    angles = token_place.astype(jnp.float32)[:, None] * frequency[None, :]
    cos_table = jnp.cos(angles)
    sin_table = jnp.sin(angles) * jnp.where(lane % HEAD_DIM < half_dim, -1.0, 1.0)[None, :]
    grad_history, past_sum, sums_past = past(dwa_weights, history[:, 0], cotangent[0])

    input_half = jnp.where(same, layer_input[0], input_got)
    layer_rows = ordered(input_half, swap_near(input_half), near == 0)
    layer_rows, last_own, early_got, late_up, vectors, past_sum, *tables = lax.optimization_barrier(
        (layer_rows, last_own, early_got, late_up, vectors, past_sum)
        + (cos_table, sin_table, apart, member)
    )
    cos_table, sin_table, apart, member = tables
    early_got = swap_diagonal(early_got)
    last_got = swap_diagonal(last_own)
    projected, norm_one_t, weight_qkv = project(
        flags, layer_rows, vectors, cos_table, sin_table, w_qkv, qkv_got
    )
    mixed = attend(apart, member, projected, LONGEST)
    late_up = swap_diagonal(after(late_up, mixed))
    late_down = swap_diagonal(after(late_down, mixed))
    last_got = jnp.where(same, last_own, last_got)
    weight_out = last_got[: w_out.shape[0]]
    attn = jnp.dot(mixed, weight_out, preferred_element_type=jnp.float32).astype(jnp.bfloat16)
    attn_got = swap_near(attn)
    cot_half = last_got[w_out.shape[0] :]
    cot_rows = ordered(cot_half, swap_near(cot_half), near == 0)
    scalars = [flags, dwa_weights]
    fields = [layer_rows, attn, attn_got, cot_rows, vectors]
    *kept, back_early, act_early, early_pieces, down_early = feed(True, scalars, fields, w_up, w_down, early_got)
    early_sum = scatter_plane(after(early_pieces, late_up, late_down))
    back_late, act_late, late_pieces, down_late = feed(False, [flags], kept, w_up, w_down, late_up, late_down)
    late_sum = scatter_plane(late_pieces)
    fields = [layer_rows, attn, attn_got, cot_rows, back_early, swap_near(back_early), back_late, swap_near(back_late)]
    grad_attn, grad_mixed, grad_out, sums_two = middle(flags, dwa_weights, fields, mixed, vectors, weight_out)
    grad_qkv = attend_back(apart, member, cos_table, sin_table, projected, grad_mixed, LONGEST)
    owned = weigh(flags, norm_one_t, grad_qkv, grad_out)
    moved = [send_to_owner(owned[j], j // 2, j % 2) for j in range(4)]
    keep, send, sums_one = unproject(flags, after(grad_qkv, owned[0]), weight_qkv, layer_rows)
    block_keep, block_send, sums_now = lower(
        flags, act_early, act_late, down_early, down_late, layer_rows, attn, attn_got, after(cot_rows, send)
    )
    early_sum = scatter_rows(after(early_sum, owned[0]))
    keep, send, block_keep, block_send, *moved = lax.optimization_barrier(
        (keep, send, block_keep, block_send, *moved)
    )
    attn_one = add(jnp.where(same, owned[0], moved[0]), *moved[1:])
    attn_moved = move_rows(attn_one)
    late_sum = scatter_rows(after(late_sum, attn_one))
    ours = last(
        flags, layer_rows, grad_attn, keep, swap_near(send), block_keep, swap_near(block_send), vectors
    )
    small = jnp.concatenate([sums_one[:2], sums_two[:2], sums_now[:1], sums_past[:hist_count]], axis=0)
    small = after(small, attn_one)
    for name in ("near", "tp", "far"):
        small = sum_over(small, name)
    small, ours, *attn_moved = lax.optimization_barrier((small, ours, *attn_moved))
    feed_sum = jnp.concatenate([after(early_sum, small), late_sum], axis=1)
    feed_got = swap_diagonal(feed_sum)
    theirs = swap_diagonal(after(ours, feed_got))
    small = sum_over(small, "dp")
    attn_sum = add(*attn_moved)
    blocks = jnp.concatenate([attn_sum, jnp.where(same, feed_sum, feed_got)], axis=1)
    here = jnp.stack([blocks, swap_far(blocks)])
    output, grad_input = present(flags, dwa_weights, past_sum, ours, theirs)
    grad_w_qkv, grad_w_out, grad_w_up, grad_w_down = place(flags, here, swap_near(here))

    return (
        output[None],
        grad_input[None],
        grad_history[:, None],
        jnp.sum(jnp.concatenate([small[5:], small[4:5]], axis=0), axis=1),
        small[0],
        small[1],
        grad_w_qkv,
        grad_w_out.T,
        small[2],
        small[3],
        grad_w_up,
        grad_w_down.T,
    )


def positions(seq_lengths, token_count):
    seq_ends = jnp.cumsum(seq_lengths)
    seq_starts = seq_ends - seq_lengths
    token_index = jnp.arange(token_count, dtype=jnp.int32)
    seq_owner = jnp.sum((token_index[:, None] >= seq_ends[None, :]).astype(jnp.int32), axis=1)
    picked = (
        seq_owner[:, None] == jnp.arange(seq_lengths.shape[0], dtype=jnp.int32)[None, :]
    ).astype(jnp.int32)
    seq_begin = jnp.sum(picked * seq_starts[None, :], axis=1)
    return (seq_owner, token_index - seq_begin)


def solution(mesh):
    tps, dps, reps = (mesh.shape[name] for name in ("tp", "dp", "rep"))
    split = Mesh(mesh.devices.reshape(tps, dps, reps // 2, 2), AXES)
    in_specs = (
        P(("dp", "far", "near"), "tp", None),
        P(None, ("dp", "far", "near"), "tp", None),
        P(("dp", "far", "near"), "tp", None),
        P(("dp", "far", "near"), None),
        P(),
        P(),
        P(),
        P(None, None, "tp"),
        P("tp", None),
        P(),
        P(),
        P(None, "tp"),
        P("tp", None),
    )
    out_specs = (
        P(("dp", "far", "near"), "tp", None),
        P(("dp", "far", "near"), "tp", None),
        P(None, ("dp", "far", "near"), "tp", None),
        P(),
        P(),
        P(),
        P(None, "dp", "tp"),
        P("tp", "dp"),
        P(),
        P(),
        P("dp", "tp"),
        P("tp", "dp"),
    )
    return jax.shard_map(local, mesh=split, in_specs=in_specs, out_specs=out_specs, check_vma=False)
```

```python
import functools
import itertools
import math

import jax
import jax.numpy as jnp
from jax import lax
from jax.experimental import pallas as pl
from jax.experimental.pallas import tpu as pltpu
from jax.sharding import Mesh, PartitionSpec as P

HEAD_DIM = 64
LONGEST = 512
NEG_FILL = -1e30
NORM_EPS = 1e-05
RATE = 3e6
ROOM = 60 << 20
SNUG = 18 << 20


def lasting(microseconds):
    return pl.CostEstimate(flops=0, transcendentals=0, bytes_accessed=int(microseconds * RATE))


BLOCK = 256
LANES = 128
NT = (((1,), (1,)), ((), ()))


def dot(a, b, dims=(((1,), (0,)), ((), ()))):
    return lax.dot_general(a, b, dims, preferred_element_type=jnp.float32)


def spans(whole, reach):
    back = -(-(reach - 1) // BLOCK)
    runs = []
    for i in range(whole // BLOCK):
        count = min(i, back) + 1
        if runs and runs[-1][2] == count:
            runs[-1][1] = i + 1
        else:
            runs.append([i, i + 1, count])
    return runs


def each_block(whole, reach, body):
    for first, last, count in spans(whole, reach):

        def step(i, carry, count=count):
            body(i, i + 1 - count, count)
            return carry

        lax.fori_loop(first, last, step, 0)


def block_at(i, count=1):
    return pl.ds(pl.multiple_of(i * BLOCK, BLOCK), count * BLOCK)


def head_query(q_ref, apart_ref, i, head):
    lane = lax.broadcasted_iota(jnp.int32, (BLOCK, LANES), 1) // HEAD_DIM
    query = q_ref[block_at(i), :] * (HEAD_DIM**-0.5)
    query = jnp.where(lane == head, query, jnp.zeros_like(query))
    return query, jnp.concatenate([query, apart_ref[block_at(i), :]], axis=1)


def attend_kernel(reach, apart_ref, member_ref, q_ref, k_ref, v_ref, out_ref, keys):
    whole = q_ref.shape[0]
    lane = lax.broadcasted_iota(jnp.int32, (BLOCK, LANES), 1) // HEAD_DIM
    keys[:, :LANES] = k_ref[...]
    keys[:, LANES:] = member_ref[...]

    def one(i, first, count, head):
        unused, query = head_query(q_ref, apart_ref, i, head)
        own = dot(query, keys[block_at(i), :], NT)
        key_at = lax.broadcasted_iota(jnp.int32, own.shape, 1)
        query_at = lax.broadcasted_iota(jnp.int32, own.shape, 0)
        scores = jnp.where(key_at <= query_at, own, NEG_FILL)
        if count > 1:
            scores = jnp.concatenate([dot(query, keys[block_at(first, count - 1), :], NT), scores], axis=1)
        exponent = jnp.exp(scores - jnp.max(scores, axis=1, keepdims=True))
        row_sum = jnp.sum(exponent, axis=1, keepdims=True)
        return dot(exponent.astype(jnp.bfloat16), v_ref[block_at(first, count), :]) * (1.0 / row_sum)

    def body(i, first, count):
        mixed = [one(i, first, count, head) for head in range(2)]
        out_ref[block_at(i), :] = jnp.where(lane == 0, *mixed).astype(out_ref.dtype)

    each_block(whole, reach, body)


def attend(apart, member, projected, reach):
    count, whole, width = projected.shape

    def block(c):
        return pl.BlockSpec((None, whole, LANES), lambda p: (c, 0, p))

    table = pl.BlockSpec((whole, LANES), lambda p: (0, 0))
    return pl.pallas_call(
        functools.partial(attend_kernel, reach),
        grid=(width // LANES,),
        in_specs=[table, table, block(0), block(1), block(2)],
        out_specs=pl.BlockSpec((whole, LANES), lambda p: (0, p)),
        out_shape=jax.ShapeDtypeStruct((whole, width), jnp.bfloat16),
        scratch_shapes=[pltpu.VMEM((whole, 2 * LANES), jnp.bfloat16)],
        compiler_params=pltpu.CompilerParams(vmem_limit_bytes=ROOM),
        cost_estimate=lasting(12),
    )(apart, member, projected, projected, projected)


def turn_back(field, cos, sin):
    half = HEAD_DIM // 2
    lane = lax.broadcasted_iota(jnp.int32, field.shape, 1) % HEAD_DIM
    crossed = jnp.where(lane < half, pltpu.roll(field, LANES - half, 1), pltpu.roll(field, half, 1))
    return field * cos - crossed * sin


def attend_back_kernel(
    reach, apart_ref, member_ref, cos_ref, sin_ref, q_ref, k_ref, v_ref, g_ref, out_ref, keys, keys_t, key_acc, value_acc
):
    whole = q_ref.shape[0]
    lane = lax.broadcasted_iota(jnp.int32, (BLOCK, LANES), 1) // HEAD_DIM
    keys[:, :LANES] = k_ref[...]
    keys[:, LANES:] = member_ref[...]
    keys_t[...] = k_ref[...].astype(jnp.float32).T.astype(jnp.bfloat16)
    key_acc[...] = jnp.zeros_like(key_acc)
    value_acc[...] = jnp.zeros_like(value_acc)

    def one(i, first, count, head):
        span = block_at(first, count)
        plain, query = head_query(q_ref, apart_ref, i, head)
        grad = g_ref[block_at(i), :]
        grad = jnp.where(lane == head, grad, jnp.zeros_like(grad))
        own = dot(keys[block_at(i), :], query, NT)
        key_at = lax.broadcasted_iota(jnp.int32, own.shape, 0)
        query_at = lax.broadcasted_iota(jnp.int32, own.shape, 1)
        scores = jnp.where(key_at <= query_at, own, NEG_FILL)
        if count > 1:
            scores = jnp.concatenate([dot(keys[block_at(first, count - 1), :], query, NT), scores], axis=0)
        exponent = jnp.exp(scores - jnp.max(scores, axis=0, keepdims=True))
        probs = exponent * (1.0 / jnp.sum(exponent, axis=0, keepdims=True))
        grad_values = dot(probs.astype(jnp.bfloat16), grad)
        weighted = probs * dot(v_ref[span, :], grad, NT)
        grad_scores = (weighted - probs * jnp.sum(weighted, axis=0, keepdims=True)).astype(jnp.bfloat16)
        here = dot(keys_t[:, span], grad_scores)
        return grad_values, dot(grad_scores, plain), here

    def body(i, first, count):
        span, at = block_at(first, count), block_at(i)
        values, keys_, queries = zip(*[one(i, first, count, head) for head in range(2)])
        value_acc[span, :] += values[0] + values[1]
        key_acc[span, :] += keys_[0] + keys_[1]
        row = lax.broadcasted_iota(jnp.int32, queries[0].shape, 0) // HEAD_DIM
        both = jnp.where(row == 0, *queries).T * (HEAD_DIM**-0.5)
        out_ref[0, at, :] = turn_back(both, cos_ref[at, :], sin_ref[at, :]).astype(out_ref.dtype)

    each_block(whole, reach, body)

    def finish(i, carry):
        at = block_at(i)
        out_ref[1, at, :] = turn_back(key_acc[at, :], cos_ref[at, :], sin_ref[at, :]).astype(out_ref.dtype)
        out_ref[2, at, :] = value_acc[at, :].astype(out_ref.dtype)
        return carry

    lax.fori_loop(0, whole // BLOCK, finish, 0)


def attend_back(apart, member, cos, sin, projected, grad_mixed, reach):
    count, whole, width = projected.shape

    def block(c):
        return pl.BlockSpec((None, whole, LANES), lambda p: (c, 0, p))

    table = pl.BlockSpec((whole, LANES), lambda p: (0, 0))
    return pl.pallas_call(
        functools.partial(attend_back_kernel, reach),
        grid=(width // LANES,),
        in_specs=[table] * 4 + [block(0), block(1), block(2), pl.BlockSpec((whole, LANES), lambda p: (0, p))],
        out_specs=pl.BlockSpec((count, whole, LANES), lambda p: (0, 0, p)),
        out_shape=jax.ShapeDtypeStruct((count, whole, width), jnp.bfloat16),
        scratch_shapes=[
            pltpu.VMEM((whole, 2 * LANES), jnp.bfloat16),
            pltpu.VMEM((LANES, whole), jnp.bfloat16),
            pltpu.VMEM((whole, LANES), jnp.float32),
            pltpu.VMEM((whole, LANES), jnp.float32),
        ],
        compiler_params=pltpu.CompilerParams(vmem_limit_bytes=ROOM),
        cost_estimate=lasting(22),
    )(apart, member, cos, sin, projected, projected, projected, grad_mixed)


ROWS = 256


def norm_parts(field):
    centered = field - jnp.mean(field, axis=-1, keepdims=True)
    scale = lax.rsqrt(jnp.mean(centered * centered, axis=-1, keepdims=True) + NORM_EPS)
    return centered * scale, scale


def wide(ref, at):
    return ref[at, :].astype(jnp.float32)


def row_blocks(count, body):
    def step(i, carry):
        body(i, pl.ds(pl.multiple_of(i * ROWS, ROWS), ROWS))
        return carry

    lax.fori_loop(0, count // ROWS, step, 0)


TALL = 512


def streamed(kernel, steps, scalars, fields, outs, scratch, microseconds, room=ROOM):
    def spec(shape, block=None, at=None):
        if block is None:
            return pl.BlockSpec(shape, lambda i, *scalars: (0,) * len(shape))
        return pl.BlockSpec(block, at)

    fields = [field if isinstance(field, tuple) else (field,) for field in fields]
    return pl.pallas_call(
        kernel,
        grid_spec=pltpu.PrefetchScalarGridSpec(
            num_scalar_prefetch=len(scalars),
            grid=(steps,),
            in_specs=[spec(field[0].shape, *field[1:]) for field in fields],
            out_specs=[spec(out[0], *out[2:]) for out in outs],
            scratch_shapes=[pltpu.VMEM(shape, dtype) for shape, dtype in scratch],
        ),
        out_shape=[jax.ShapeDtypeStruct(*out[:2]) for out in outs],
        compiler_params=pltpu.CompilerParams(vmem_limit_bytes=room),
        cost_estimate=lasting(microseconds),
    )(*scalars, *[field[0] for field in fields])


def by_rows(field, rows, shift=None):
    if shift is None:
        return field, (rows, field.shape[1]), lambda i, *scalars: (i, 0)
    return field, (rows, field.shape[1]), lambda i, *scalars: (shift(i, *scalars), 0)


def whole_spec(shape):
    return pl.BlockSpec(shape, lambda *at: (0,) * len(shape))


def turn(field, cos, sin):
    half = HEAD_DIM // 2
    lane = lax.broadcasted_iota(jnp.int32, field.shape, 1) % HEAD_DIM
    crossed = jnp.where(lane < half, pltpu.roll(field, LANES - half, 1), pltpu.roll(field, half, 1))
    return field * cos + crossed * sin


def project_kernel(flags, rows_ref, cos_ref, sin_ref, vectors, w_own, w_got, out_ref, turned_ref, weight_ref):
    @pl.when(pl.program_id(0) == 0)
    def _():
        weight_ref[...] = jnp.where(flags[0] == 1, w_own[...], w_got[...])

    unit, unused = norm_parts(rows_ref[...].astype(jnp.float32))
    norm = unit * vectors[0:1, :] + vectors[1:2, :]
    turned_ref[...] = norm.T.astype(jnp.bfloat16)
    norm = norm.astype(jnp.bfloat16)
    for c in range(weight_ref.shape[0]):
        field = dot(norm, weight_ref[c])
        if c == 2:
            out_ref[c] = field.astype(jnp.bfloat16)
        else:
            for p in range(field.shape[1] // LANES):
                lanes = slice(p * LANES, (p + 1) * LANES)
                out_ref[c, :, lanes] = turn(field[:, lanes], cos_ref[...], sin_ref[...]).astype(jnp.bfloat16)


def project(flags, rows, vectors, cos, sin, w_own, w_got):
    whole, width = rows.shape
    count, unused, columns = w_own.shape
    low = jnp.bfloat16
    return streamed(
        project_kernel,
        whole // ROWS,
        [flags],
        [by_rows(rows, ROWS), by_rows(cos, ROWS), by_rows(sin, ROWS), vectors, w_own, w_got],
        [
            ((count, whole, columns), low, (count, ROWS, columns), lambda i, flags: (0, i, 0)),
            ((width, whole), low, (width, ROWS), lambda i, flags: (0, i)),
            (w_own.shape, low),
        ],
        [],
        8,
    )


def gelu_both(up):
    root = math.sqrt(2.0 / math.pi)
    square = up * up
    bent = jnp.tanh(root * up * (1.0 + 0.044715 * square))
    half = 0.5 * (1.0 + bent)
    slope = half + 0.5 * up * (1.0 - bent * bent) * (root * (1.0 + 3.0 * 0.044715 * square))
    return up * half, slope


def feed_kernel(early, *refs):
    if early:
        flags, weight_ref, rows_ref, own_ref, got_ref, cot_ref, vectors, up_own, down_own, got = refs[:10]
        norm, norm_t, grad, grad_t, back_ref, act_ref, down_ref, pieces = refs[10:18]
        up_got, down_got = got.at[: norm.shape[1]], got.at[norm.shape[1] :]
    else:
        flags, norm, norm_t, grad, grad_t, back_early, up_own, down_own, up_got, down_got = refs[:10]
        back_ref, act_ref, down_ref, *pieces = refs[10:17]
    up_w, up_sum, down_sum = refs[-3:]
    part = up_w.shape[1] // 2
    step, last = pl.program_id(0), pl.num_programs(0) - 1

    @pl.when(step == 0)
    def _():
        up_w[...] = jnp.where(flags[0] == 1, up_own[...], up_got[...])
        down_ref[...] = jnp.where(flags[0] == 1, down_own[...], down_got[...])

    if early:

        def head(i, at):
            unit, unused = norm_parts(wide(rows_ref, at) + wide(own_ref, at) + wide(got_ref, at))
            field = unit * vectors[2:3, :] + vectors[3:4, :]
            norm[at, :] = field.astype(jnp.bfloat16)
            norm_t[:, at] = field.T.astype(jnp.bfloat16)
            field = wide(cot_ref, at) * weight_ref[weight_ref.shape[0] - 1]
            grad[at, :] = field.astype(jnp.bfloat16)
            grad_t[:, at] = field.T.astype(jnp.bfloat16)

        row_blocks(norm.shape[0], head)
    value, rise = gelu_both(dot(norm[...], up_w[...]))
    act_ref[...] = value.astype(jnp.bfloat16)
    slope = (dot(grad[...], down_ref[...], NT) * rise).astype(jnp.bfloat16)
    back = dot(slope, up_w[...], NT)
    if not early:
        back = back + back_early[...].astype(jnp.float32)
    back_ref[...] = back.astype(jnp.bfloat16)

    def store(p, at, low):
        if early:
            pieces[p, at, :] = low
            return
        slot = 2 * (flags[2] ^ (p % 2)) + (flags[7] ^ (p // 2))
        for j, piece in enumerate(pieces):

            @pl.when(slot == j)
            def _():
                piece[at, :] = low

    def grads(i, at):
        fields = (dot(norm_t[at, :], slope), dot(grad_t[at, :], act_ref[...]))
        for k, (field, total) in enumerate(zip(fields, (up_sum, down_sum))):

            @pl.when(step == 0)
            def _():
                total[at, :] = field

            @pl.when(step == last)
            def _():
                low = (total[at, :] + field).astype(jnp.bfloat16)
                for p in range(2):
                    store(2 * k + p, at, low[:, p * part : (p + 1) * part])

    row_blocks(norm_t.shape[0], grads)


def feed(early, scalars, fields, w_up, w_down, *got):
    whole, width = fields[0].shape
    hidden = w_up.shape[1] // 2
    rows = whole // 2
    half = 0 if early else 1
    low = jnp.bfloat16

    def across(i, *scalars):
        return (0, i)

    tokens = ((whole, width), low, (rows, width), lambda i, *scalars: (i, 0))
    turned = ((width, whole), low, (width, rows), across)
    if early:
        operands = [by_rows(field, rows) for field in fields[:4]] + [fields[4]]
        outs = [tokens, turned, tokens, turned]
        pieces = [((4, width, hidden // 2), low)]
    else:
        operands = [by_rows(fields[0], rows), (fields[1], (width, rows), across)]
        operands += [by_rows(fields[2], rows), (fields[3], (width, rows), across), by_rows(fields[4], rows)]
        outs = []
        pieces = [((width, hidden // 2), low)] * 4
    operands += [
        (w_up, (width, hidden), lambda i, *scalars: (0, half)),
        (w_down, (hidden, width), lambda i, *scalars: (half, 0)),
        *got,
    ]
    outs += [tokens, ((whole, hidden), low, (rows, hidden), lambda i, *scalars: (i, 0)), ((hidden, width), low)]
    sums = ((width, hidden), jnp.float32)
    return streamed(
        functools.partial(feed_kernel, early), 2, scalars, operands, outs + pieces, [((width, hidden), low), sums, sums], 17
    )


def lower_kernel(
    flags, act_early, act_late, rows_ref, own_ref, got_ref, cot_ref, early_ref, late_ref, keep_ref, first, second, sums_ref
):
    step = pl.program_id(0)
    total = dot(act_early[...], early_ref[...]) + dot(act_late[...], late_ref[...])
    cot = cot_ref[...].astype(jnp.float32)

    @pl.when(step == 0)
    def _():
        sums_ref[...] = jnp.zeros_like(sums_ref)

    send_or_keep(
        total,
        total + sum(ref[...].astype(jnp.float32) for ref in (rows_ref, own_ref, got_ref)),
        first,
        second,
        keep_ref,
    )
    mine = jnp.where(step < pl.num_programs(0) // 2, 0.0, 1.0)
    block = total + mine * sum(ref[...].astype(jnp.float32) for ref in (rows_ref, own_ref, got_ref))
    sums_ref[0:1, :] += jnp.sum(block * cot, axis=0, keepdims=True)


def send_or_keep(sent, kept, first, second, keep_ref):
    step = pl.program_id(0)
    for j, ref in enumerate((first, second)):

        @pl.when(step == j)
        def _():
            ref[...] = sent.astype(ref.dtype)

    @pl.when(step >= 2)
    def _():
        keep_ref[...] = kept


def theirs_first(i, flags, *more):
    return lax.rem((1 - flags[1]) * 2 + i, 4)


def sent_and_kept(whole, width):
    rows = whole // 4
    keep = ((2 * rows, width), jnp.float32, (rows, width), lambda i, *scalars: (jnp.maximum(i - 2, 0), 0))
    send = ((rows, width), jnp.bfloat16)
    return [keep, send, send, ((8, width), jnp.float32)]


def lower(flags, act_early, act_late, down_early, down_late, rows, own, got, cot):
    whole, width = rows.shape
    fields = [by_rows(field, whole // 4, theirs_first) for field in (act_early, act_late, rows, own, got, cot)]
    return streamed(
        lower_kernel, 4, [flags], fields + [down_early, down_late], sent_and_kept(whole, width), [], 6, SNUG
    )


def middle_kernel(
    flags, weight_ref, rows_ref, own_ref, got_ref, cot_ref, back_own, back_got, mixed_ref,
    vectors, w_ref, grad_ref, gmixed_ref, gout_ref, sums_ref, gout,
):
    step, last = pl.program_id(0), pl.num_programs(0) - 1
    unit, scale = norm_parts(sum(ref[...].astype(jnp.float32) for ref in (rows_ref, own_ref, got_ref)))
    back = sum(ref[...].astype(jnp.float32) for ref in (back_own, back_got))
    inner = back * vectors[2:3, :]
    mean = jnp.mean(inner, axis=-1, keepdims=True)
    slant = jnp.mean(inner * unit, axis=-1, keepdims=True)
    cot = cot_ref[...].astype(jnp.float32) * weight_ref[weight_ref.shape[0] - 1]
    grad = cot + scale * (inner - mean - unit * slant)
    low = grad.astype(jnp.bfloat16)
    grad_ref[...] = low
    gmixed_ref[...] = dot(low, w_ref[...], NT).astype(jnp.bfloat16)
    part = dot(grad.T.astype(jnp.bfloat16), mixed_ref[...])

    @pl.when(step == 0)
    def _():
        gout[...] = part
        sums_ref[...] = jnp.zeros_like(sums_ref)

    @pl.when(step > 0)
    def _():
        gout[...] += part

    @pl.when(step == last)
    def _():
        gout_ref[...] = gout[...].astype(jnp.bfloat16)

    @pl.when(step // ((last + 1) // 2) == flags[1])
    def _():
        sums_ref[0:1, :] += jnp.sum(back * unit, axis=0, keepdims=True)
        sums_ref[1:2, :] += jnp.sum(back, axis=0, keepdims=True)


def middle(flags, weight, fields, mixed, vectors, w_out):
    whole, width = fields[0].shape
    columns = mixed.shape[1]
    low = jnp.bfloat16
    in_order = lambda i, *scalars: (i, 0)
    return streamed(
        middle_kernel,
        whole // ROWS,
        [flags, weight],
        [by_rows(field, ROWS) for field in (*fields, mixed)] + [vectors, w_out],
        [
            ((whole, width), low, (ROWS, width), in_order),
            ((whole, columns), low, (ROWS, columns), in_order),
            ((width, columns), low),
            ((8, width), jnp.float32),
        ],
        [((width, columns), jnp.float32)],
        8,
    )


def weigh_kernel(flags, turned_ref, out_grad_ref, grad_ref, *out_refs):
    last = grad_ref.shape[0]
    for j, out_ref in enumerate(out_refs):
        piece = flags[3 + j]

        @pl.when(piece < last)
        def _():
            out_ref[...] = dot(turned_ref[...], grad_ref[jnp.minimum(piece, last - 1)]).astype(jnp.bfloat16)

        @pl.when(piece == last)
        def _():
            out_ref[...] = out_grad_ref[...]


def weigh(flags, turned, grad, out_grad):
    width, columns = turned.shape[0], grad.shape[2]
    piece = ((width, columns), jnp.bfloat16, (ROWS, columns), lambda i, flags: (i, 0))
    return streamed(
        weigh_kernel, width // ROWS, [flags], [by_rows(turned, ROWS), by_rows(out_grad, ROWS), grad], [piece] * 4, [], 4
    )


def unproject_kernel(flags, grad_ref, rows_ref, weight, keep_ref, first, second, sums_ref):
    total = dot(grad_ref[0], weight[0], NT)
    for c in range(1, grad_ref.shape[0]):
        total = total + dot(grad_ref[c], weight[c], NT)
    unit, unused = norm_parts(rows_ref[...].astype(jnp.float32))

    @pl.when(pl.program_id(0) == 0)
    def _():
        sums_ref[...] = jnp.zeros_like(sums_ref)

    sums_ref[0:1, :] += jnp.sum(total * unit, axis=0, keepdims=True)
    sums_ref[1:2, :] += jnp.sum(total, axis=0, keepdims=True)
    send_or_keep(total, total, first, second, keep_ref)


def unproject(flags, grad, weight, rows):
    whole, width = rows.shape
    count, unused, columns = grad.shape
    grads = (grad, (count, whole // 4, columns), lambda i, flags: (0, theirs_first(i, flags), 0))
    fields = [grads, by_rows(rows, whole // 4, theirs_first), weight]
    return streamed(unproject_kernel, 4, [flags], fields, sent_and_kept(whole, width), [], 5, SNUG)


def last_kernel(
    flags, rows_ref, resid_ref, keep_ref, block_keep, got_first, got_second, block_first, block_second, vectors, out_ref
):
    first = pl.program_id(0) == 0
    unit, scale = norm_parts(rows_ref[...].astype(jnp.float32))
    got = jnp.where(first, got_first[...], got_second[...]).astype(jnp.float32)
    inner = (keep_ref[...] + got) * vectors[0:1, :]
    mean = jnp.mean(inner, axis=-1, keepdims=True)
    slant = jnp.mean(inner * unit, axis=-1, keepdims=True)
    grad = resid_ref[...].astype(jnp.float32) + scale * (inner - mean - unit * slant)
    out_ref[0] = grad.astype(jnp.bfloat16)
    got = jnp.where(first, block_first[...], block_second[...]).astype(jnp.float32)
    out_ref[1] = (block_keep[...] + got).astype(jnp.bfloat16)


def last(flags, rows, resid, keep, block_keep, got, vectors):
    half, width = keep.shape
    size = half // 2

    def mine(i, flags):
        return flags[1] * 2 + i

    out = ((2, half, width), jnp.bfloat16, (2, size, width), lambda i, flags: (0, i, 0))
    fields = [by_rows(rows, size, mine), by_rows(resid, size, mine), by_rows(keep, size), by_rows(block_keep, size)]
    return streamed(last_kernel, 2, [flags], fields + [*got, vectors], [out], [], 3)[0]


def past_kernel(dwa_ref, hist_ref, cot_ref, grad_ref, part_ref, sums_ref):
    @pl.when(pl.program_id(0) == 0)
    def _():
        sums_ref[...] = jnp.zeros_like(sums_ref)

    grad = cot_ref[...].astype(jnp.float32)
    total = jnp.zeros_like(grad)
    for j in range(hist_ref.shape[0]):
        field = hist_ref[j].astype(jnp.float32)
        total += dwa_ref[j] * field
        grad_ref[j] = (dwa_ref[j] * grad).astype(jnp.bfloat16)
        sums_ref[j : j + 1, :] += jnp.sum(field * grad, axis=0, keepdims=True)
    part_ref[...] = total


def past(dwa, history, cot):
    count, rows, width = history.shape
    layers = pl.BlockSpec((count, ROWS, width), lambda i: (0, i, 0))
    tokens = pl.BlockSpec((ROWS, width), lambda i: (i, 0))
    return pl.pallas_call(
        past_kernel,
        grid=(rows // ROWS,),
        in_specs=[pl.BlockSpec(memory_space=pltpu.SMEM), layers, tokens],
        out_specs=[layers, tokens, whole_spec((8, width))],
        out_shape=[
            jax.ShapeDtypeStruct(history.shape, jnp.bfloat16),
            jax.ShapeDtypeStruct((rows, width), jnp.float32),
            jax.ShapeDtypeStruct((8, width), jnp.float32),
        ],
        compiler_params=pltpu.CompilerParams(vmem_limit_bytes=ROOM),
        cost_estimate=lasting(3),
    )(dwa, history, cot)


def present_kernel(flags, weight_ref, part_ref, own_ref, got_ref, out_ref, grad_ref):
    here = jnp.where(flags[0] == 1, own_ref[1], got_ref[1]).astype(jnp.float32)
    out_ref[...] = (part_ref[...] + weight_ref[weight_ref.shape[0] - 1] * here).astype(jnp.bfloat16)
    grad_ref[...] = jnp.where(flags[0] == 1, own_ref[0], got_ref[0])


def present(flags, weight, part, own, got):
    rows, width = part.shape
    both = (2, ROWS, width), lambda i, *scalars: (0, i, 0)
    out = ((rows, width), jnp.bfloat16, (ROWS, width), lambda i, *scalars: (i, 0))
    fields = [by_rows(part, ROWS), (own, *both), (got, *both)]
    return streamed(present_kernel, rows // ROWS, [flags, weight], fields, [out] * 2, [], 2, SNUG)


def place_kernel(flags, here_ref, there_ref, qkv_ref, out_ref, up_ref, down_ref):
    near, far = flags[1], flags[2]
    part = out_ref.shape[1]
    for k in range(2):
        for c in range(2):
            field = jnp.where(near == c, here_ref[k ^ far], there_ref[k ^ far]).astype(jnp.float32)
            if 2 * k + c < 3:
                qkv_ref[2 * k + c] = field[:, :part]
            else:
                out_ref[...] = field[:, :part]
            for half in range(2):
                at = (2 * half + k) * part
                (up_ref, down_ref)[c][:, at : at + part] = field[:, (1 + half) * part : (2 + half) * part]


def place(flags, here, there):
    rows, part = here.shape[1], here.shape[2] // 3
    outs = [((3, rows, part), jnp.float32), ((rows, part), jnp.float32)]
    outs += [((rows, 4 * part), jnp.float32)] * 2
    return streamed(place_kernel, 1, [flags], [here, there], outs, [], 3, SNUG)


AXES = ("tp", "dp", "far", "near")


def moves(chosen, move):
    sizes = [lax.axis_size(name) for name in AXES]
    places = [place for place in itertools.product(*map(range, sizes)) if chosen(*place)]
    index = lambda place: functools.reduce(lambda at, step: at * step[0] + step[1], zip(sizes, place), 0)
    return [(index(place), index(move(*place))) for place in places]


def away(t, d, k, c):
    return t != c


def anyone(t, d, k, c):
    return True


def swap_diagonal(field):
    return lax.ppermute(field, AXES, moves(away, lambda t, d, k, c: (c, d, k, t)))


def send_to_owner(field, other_far, other_tp):
    return lax.ppermute(
        field,
        AXES,
        moves(
            away if not other_far and not other_tp else anyone,
            lambda t, d, k, c: (c, d, k ^ other_far, t ^ other_tp),
        ),
    )


def swap_far(field):
    return lax.ppermute(field, "far", [(0, 1), (1, 0)])


def swap_near(field):
    return lax.ppermute(field, "near", [(0, 1), (1, 0)])


def after(field, *others):
    return lax.optimization_barrier((field, *others))[0]


def ordered(own, other, first, axis=0):
    return jnp.where(
        first, jnp.concatenate([own, other], axis=axis), jnp.concatenate([other, own], axis=axis)
    )


def part_of(field, index, axis):
    size = field.shape[axis] // 2
    return lax.dynamic_slice_in_dim(field, index * size, size, axis)


def add(*fields):
    return sum(field.astype(jnp.float32) for field in fields).astype(jnp.bfloat16)


def scatter_plane(pieces):
    return lax.psum_scatter(pieces, ("tp", "far"), scatter_dimension=0, tiled=True)[0]


def scatter_rows(piece):
    return lax.psum_scatter(piece, "dp", scatter_dimension=0, tiled=True)


def move_rows(block):
    dps = lax.axis_size("dp")
    if dps > 8:
        return [scatter_rows(block)]
    block = block.reshape(dps, block.shape[0] // dps, block.shape[1])
    place = lax.axis_index("dp")
    moved = [lax.dynamic_index_in_dim(block, place, 0, keepdims=False)]
    for step in range(1, dps):
        sent = lax.dynamic_index_in_dim(block, lax.rem(place + step, dps), 0, keepdims=False)
        moved.append(lax.ppermute(sent, "dp", [(d, (d + step) % dps) for d in range(dps)]))
    return moved


def sum_over(field, name):
    size = lax.axis_size(name)
    bit = 1
    while bit < size:
        field = field + lax.ppermute(field, name, [(d, d ^ bit) for d in range(size)])
        bit *= 2
    return field


def local(
    layer_input,
    history,
    cotangent,
    lengths,
    dwa_weights,
    gain_one,
    bias_one,
    w_qkv,
    w_out,
    gain_two,
    bias_two,
    w_up,
    w_down,
):
    rows = layer_input.shape[1]
    whole = rows * lax.axis_size("tp")
    hist_count = history.shape[0]
    part, far, near = lax.axis_index("tp"), lax.axis_index("far"), lax.axis_index("near")
    same = near == part
    pieces = [2 * (far ^ a) + (part ^ b) for a in range(2) for b in range(2)]
    flags = jnp.stack([same.astype(jnp.int32), near, far, *pieces, part])

    input_got = swap_diagonal(layer_input[0])
    qkv_got = swap_diagonal(w_qkv)
    early_got = jnp.concatenate([part_of(w_up, 0, 1), part_of(w_down, 0, 0)], axis=0)
    late_up, late_down = part_of(w_up, 1, 1), part_of(w_down, 1, 0)
    last_own = jnp.concatenate([w_out, cotangent[0]], axis=0)
    vectors = jnp.stack([gain_one, bias_one, gain_two, bias_two])

    own_lengths = jnp.where(same, lengths, swap_near(lengths))[0]
    seq_owner, token_place = positions(own_lengths, whole)
    lane = jnp.arange(LANES, dtype=jnp.int32)
    member = seq_owner[:, None] == lane[None, :]
    apart = jnp.where(member | (lane >= lengths.shape[1])[None, :], 0.0, NEG_FILL).astype(jnp.bfloat16)
    member = member.astype(jnp.bfloat16)
    half_dim = HEAD_DIM // 2
    frequency = jnp.exp((lane % half_dim).astype(jnp.float32) * (-math.log(10000.0) / half_dim))
    angles = token_place.astype(jnp.float32)[:, None] * frequency[None, :]
    cos_table = jnp.cos(angles)
    sin_table = jnp.sin(angles) * jnp.where(lane % HEAD_DIM < half_dim, -1.0, 1.0)[None, :]
    grad_history, past_sum, sums_past = past(dwa_weights, history[:, 0], cotangent[0])

    input_half = jnp.where(same, layer_input[0], input_got)
    layer_rows = ordered(input_half, swap_near(input_half), near == 0)
    layer_rows, last_own, early_got, late_up, vectors, past_sum, *tables = lax.optimization_barrier(
        (layer_rows, last_own, early_got, late_up, vectors, past_sum)
        + (cos_table, sin_table, apart, member)
    )
    cos_table, sin_table, apart, member = tables
    early_got = swap_diagonal(early_got)
    last_got = swap_diagonal(last_own)
    projected, norm_one_t, weight_qkv = project(
        flags, layer_rows, vectors, cos_table, sin_table, w_qkv, qkv_got
    )
    mixed = attend(apart, member, projected, LONGEST)
    late_up = swap_diagonal(after(late_up, mixed))
    late_down = swap_diagonal(after(late_down, mixed))
    last_got = jnp.where(same, last_own, last_got)
    weight_out = last_got[: w_out.shape[0]]
    attn = jnp.dot(mixed, weight_out, preferred_element_type=jnp.float32).astype(jnp.bfloat16)
    attn_got = swap_near(attn)
    cot_half = last_got[w_out.shape[0] :]
    cot_rows = ordered(cot_half, swap_near(cot_half), near == 0)
    scalars = [flags, dwa_weights]
    fields = [layer_rows, attn, attn_got, cot_rows, vectors]
    *kept, back, act_early, down_early, early_pieces = feed(True, scalars, fields, w_up, w_down, early_got)
    early_sum = scatter_plane(after(early_pieces, late_up, late_down))
    back, act_late, down_late, *late_owned = feed(
        False, [flags], [*kept, back], w_up, w_down, late_up, late_down
    )
    late_moved = [send_to_owner(late_owned[j], j // 2, j % 2) for j in range(4)]
    fields = [layer_rows, attn, attn_got, cot_rows, back, swap_near(back)]
    grad_attn, grad_mixed, grad_out, sums_two = middle(flags, dwa_weights, fields, mixed, vectors, weight_out)
    grad_qkv = attend_back(apart, member, cos_table, sin_table, projected, grad_mixed, LONGEST)
    grad_qkv, *late_moved = lax.optimization_barrier((grad_qkv, *late_moved))
    owned = weigh(flags, norm_one_t, grad_qkv, grad_out)
    moved = [send_to_owner(owned[j], j // 2, j % 2) for j in range(4)]
    late_sum = add(jnp.where(same, late_owned[0], after(late_moved[0], owned[0])), *late_moved[1:])
    feed_sum = scatter_rows(jnp.concatenate([early_sum, late_sum], axis=1))
    keep, *send, sums_one = unproject(flags, after(grad_qkv, owned[0]), weight_qkv, layer_rows)
    block_keep, *block_send, sums_now = lower(
        flags, act_early, act_late, down_early, down_late, layer_rows, attn, attn_got, after(cot_rows, keep)
    )
    sent = [*send, *block_send]
    keep, block_keep, *arrived = lax.optimization_barrier((keep, block_keep, *sent, *moved))
    sent, moved = arrived[:4], arrived[4:]
    attn_one = add(jnp.where(same, owned[0], moved[0]), *moved[1:])
    attn_moved = move_rows(attn_one)
    got = [swap_near(field) for field in sent]
    ours = last(flags, layer_rows, grad_attn, after(keep, attn_one), block_keep, got, vectors)
    early_sum, late_sum = jnp.split(after(feed_sum, attn_one), 2, axis=1)
    early_got = swap_diagonal(early_sum)
    small = jnp.concatenate([sums_one[:2], sums_two[:2], sums_now[:1], sums_past[:hist_count]], axis=0)
    small = after(small, ours)
    for name in ("near", "tp", "far"):
        small = sum_over(small, name)
    small, ours, late_sum, early_sum, early_got, *attn_moved = lax.optimization_barrier(
        (small, ours, late_sum, early_sum, early_got, *attn_moved)
    )
    theirs = swap_diagonal(ours)
    small = sum_over(small, "dp")
    attn_sum = add(*attn_moved)
    blocks = jnp.concatenate([attn_sum, jnp.where(same, early_sum, early_got), late_sum], axis=1)
    here = jnp.stack([blocks, swap_far(blocks)])
    output, grad_input = present(flags, dwa_weights, past_sum, ours, theirs)
    grad_w_qkv, grad_w_out, grad_w_up, grad_w_down = place(flags, here, swap_near(here))

    return (
        output[None],
        grad_input[None],
        grad_history[:, None],
        jnp.sum(jnp.concatenate([small[5:], small[4:5]], axis=0), axis=1),
        small[0],
        small[1],
        grad_w_qkv,
        grad_w_out.T,
        small[2],
        small[3],
        grad_w_up,
        grad_w_down.T,
    )


def positions(seq_lengths, token_count):
    seq_ends = jnp.cumsum(seq_lengths)
    seq_starts = seq_ends - seq_lengths
    token_index = jnp.arange(token_count, dtype=jnp.int32)
    seq_owner = jnp.sum((token_index[:, None] >= seq_ends[None, :]).astype(jnp.int32), axis=1)
    picked = (
        seq_owner[:, None] == jnp.arange(seq_lengths.shape[0], dtype=jnp.int32)[None, :]
    ).astype(jnp.int32)
    seq_begin = jnp.sum(picked * seq_starts[None, :], axis=1)
    return (seq_owner, token_index - seq_begin)


def solution(mesh):
    tps, dps, reps = (mesh.shape[name] for name in ("tp", "dp", "rep"))
    split = Mesh(mesh.devices.reshape(tps, dps, reps // 2, 2), AXES)
    in_specs = (
        P(("dp", "far", "near"), "tp", None),
        P(None, ("dp", "far", "near"), "tp", None),
        P(("dp", "far", "near"), "tp", None),
        P(("dp", "far", "near"), None),
        P(),
        P(),
        P(),
        P(None, None, "tp"),
        P("tp", None),
        P(),
        P(),
        P(None, "tp"),
        P("tp", None),
    )
    out_specs = (
        P(("dp", "far", "near"), "tp", None),
        P(("dp", "far", "near"), "tp", None),
        P(None, ("dp", "far", "near"), "tp", None),
        P(),
        P(),
        P(),
        P(None, "dp", "tp"),
        P("tp", "dp"),
        P(),
        P(),
        P("dp", "tp"),
        P("tp", "dp"),
    )
    return jax.shard_map(local, mesh=split, in_specs=in_specs, out_specs=out_specs, check_vma=False)
```

```python
import functools
import itertools
import math

import jax
import jax.numpy as jnp
from jax import lax
from jax.experimental import pallas as pl
from jax.experimental.pallas import tpu as pltpu
from jax.sharding import Mesh, PartitionSpec as P

HEAD_DIM = 64
LONGEST = 512
NEG_FILL = -1e30
NORM_EPS = 1e-05
RATE = 3e6
ROOM = 60 << 20
SNUG = 18 << 20


def lasting(microseconds):
    return pl.CostEstimate(flops=0, transcendentals=0, bytes_accessed=int(microseconds * RATE))


BLOCK = 256
LANES = 128
NT = (((1,), (1,)), ((), ()))


def dot(a, b, dims=(((1,), (0,)), ((), ()))):
    return lax.dot_general(a, b, dims, preferred_element_type=jnp.float32)


def spans(whole, reach):
    back = -(-(reach - 1) // BLOCK)
    runs = []
    for i in range(whole // BLOCK):
        count = min(i, back) + 1
        if runs and runs[-1][2] == count:
            runs[-1][1] = i + 1
        else:
            runs.append([i, i + 1, count])
    return runs


def each_block(whole, reach, body):
    for first, last, count in spans(whole, reach):

        def step(i, carry, count=count):
            body(i, i + 1 - count, count)
            return carry

        lax.fori_loop(first, last, step, 0)


def block_at(i, count=1):
    return pl.ds(pl.multiple_of(i * BLOCK, BLOCK), count * BLOCK)


def head_query(q_ref, apart_ref, i, head):
    lane = lax.broadcasted_iota(jnp.int32, (BLOCK, LANES), 1) // HEAD_DIM
    query = q_ref[block_at(i), :] * (HEAD_DIM**-0.5)
    query = jnp.where(lane == head, query, jnp.zeros_like(query))
    return query, jnp.concatenate([query, apart_ref[block_at(i), :]], axis=1)


def attend_kernel(reach, apart_ref, member_ref, q_ref, k_ref, v_ref, out_ref, keys):
    whole = q_ref.shape[0]
    lane = lax.broadcasted_iota(jnp.int32, (BLOCK, LANES), 1) // HEAD_DIM
    keys[:, :LANES] = k_ref[...]
    keys[:, LANES:] = member_ref[...]

    def one(i, first, count, head):
        unused, query = head_query(q_ref, apart_ref, i, head)
        own = dot(query, keys[block_at(i), :], NT)
        key_at = lax.broadcasted_iota(jnp.int32, own.shape, 1)
        query_at = lax.broadcasted_iota(jnp.int32, own.shape, 0)
        scores = jnp.where(key_at <= query_at, own, NEG_FILL)
        if count > 1:
            scores = jnp.concatenate([dot(query, keys[block_at(first, count - 1), :], NT), scores], axis=1)
        exponent = jnp.exp(scores - jnp.max(scores, axis=1, keepdims=True))
        row_sum = jnp.sum(exponent, axis=1, keepdims=True)
        return dot(exponent.astype(jnp.bfloat16), v_ref[block_at(first, count), :]) * (1.0 / row_sum)

    def body(i, first, count):
        mixed = [one(i, first, count, head) for head in range(2)]
        out_ref[block_at(i), :] = jnp.where(lane == 0, *mixed).astype(out_ref.dtype)

    each_block(whole, reach, body)


def attend(apart, member, projected, reach):
    count, whole, width = projected.shape

    def block(c):
        return pl.BlockSpec((None, whole, LANES), lambda p: (c, 0, p))

    table = pl.BlockSpec((whole, LANES), lambda p: (0, 0))
    return pl.pallas_call(
        functools.partial(attend_kernel, reach),
        grid=(width // LANES,),
        in_specs=[table, table, block(0), block(1), block(2)],
        out_specs=pl.BlockSpec((whole, LANES), lambda p: (0, p)),
        out_shape=jax.ShapeDtypeStruct((whole, width), jnp.bfloat16),
        scratch_shapes=[pltpu.VMEM((whole, 2 * LANES), jnp.bfloat16)],
        compiler_params=pltpu.CompilerParams(vmem_limit_bytes=ROOM),
        cost_estimate=lasting(12),
    )(apart, member, projected, projected, projected)


def turn_back(field, cos, sin):
    half = HEAD_DIM // 2
    lane = lax.broadcasted_iota(jnp.int32, field.shape, 1) % HEAD_DIM
    crossed = jnp.where(lane < half, pltpu.roll(field, LANES - half, 1), pltpu.roll(field, half, 1))
    return field * cos - crossed * sin


def attend_back_kernel(
    reach, flags, apart_ref, member_ref, cos_ref, sin_ref, q_ref, k_ref, v_ref, g_ref, turned_ref, out_grad_ref,
    out_ref, *refs,
):
    owned, (keys, keys_t, key_acc, value_acc) = refs[:4], refs[4:]
    whole = q_ref.shape[0]
    lane = lax.broadcasted_iota(jnp.int32, (BLOCK, LANES), 1) // HEAD_DIM
    keys[:, :LANES] = k_ref[...]
    keys[:, LANES:] = member_ref[...]
    keys_t[...] = k_ref[...].astype(jnp.float32).T.astype(jnp.bfloat16)
    key_acc[...] = jnp.zeros_like(key_acc)
    value_acc[...] = jnp.zeros_like(value_acc)

    def one(i, first, count, head):
        span = block_at(first, count)
        plain, query = head_query(q_ref, apart_ref, i, head)
        grad = g_ref[block_at(i), :]
        grad = jnp.where(lane == head, grad, jnp.zeros_like(grad))
        own = dot(keys[block_at(i), :], query, NT)
        key_at = lax.broadcasted_iota(jnp.int32, own.shape, 0)
        query_at = lax.broadcasted_iota(jnp.int32, own.shape, 1)
        scores = jnp.where(key_at <= query_at, own, NEG_FILL)
        if count > 1:
            scores = jnp.concatenate([dot(keys[block_at(first, count - 1), :], query, NT), scores], axis=0)
        exponent = jnp.exp(scores - jnp.max(scores, axis=0, keepdims=True))
        probs = exponent * (1.0 / jnp.sum(exponent, axis=0, keepdims=True))
        grad_values = dot(probs.astype(jnp.bfloat16), grad)
        weighted = probs * dot(v_ref[span, :], grad, NT)
        grad_scores = (weighted - probs * jnp.sum(weighted, axis=0, keepdims=True)).astype(jnp.bfloat16)
        here = dot(keys_t[:, span], grad_scores)
        return grad_values, dot(grad_scores, plain), here

    def body(i, first, count):
        span, at = block_at(first, count), block_at(i)
        values, keys_, queries = zip(*[one(i, first, count, head) for head in range(2)])
        value_acc[span, :] += values[0] + values[1]
        key_acc[span, :] += keys_[0] + keys_[1]
        row = lax.broadcasted_iota(jnp.int32, queries[0].shape, 0) // HEAD_DIM
        both = jnp.where(row == 0, *queries).T * (HEAD_DIM**-0.5)
        out_ref[0, at, :] = turn_back(both, cos_ref[at, :], sin_ref[at, :]).astype(out_ref.dtype)

    each_block(whole, reach, body)

    def finish(i, carry):
        at = block_at(i)
        out_ref[1, at, :] = turn_back(key_acc[at, :], cos_ref[at, :], sin_ref[at, :]).astype(out_ref.dtype)
        out_ref[2, at, :] = value_acc[at, :].astype(out_ref.dtype)
        return carry

    lax.fori_loop(0, whole // BLOCK, finish, 0)

    def store(piece, at, low):
        slot = 2 * (flags[2] ^ (piece // 2)) + (flags[3] ^ (piece % 2))
        for j, ref in enumerate(owned):

            @pl.when(slot == j)
            def _():
                ref[at, :] = low

    def weigh(i, carry):
        at = block_at(i)
        rows = turned_ref[at, :]
        both = dot(rows, jnp.concatenate([out_ref[0], out_ref[1]], axis=1)).astype(jnp.bfloat16)
        store(0, at, both[:, :LANES])
        store(1, at, both[:, LANES:])
        store(2, at, dot(rows, out_ref[2]).astype(jnp.bfloat16))
        store(3, at, out_grad_ref[at, :])
        return carry

    lax.fori_loop(0, turned_ref.shape[0] // BLOCK, weigh, 0)


def attend_back(flags, apart, member, cos, sin, projected, grad_mixed, turned, out_grad, reach):
    count, whole, width = projected.shape
    depth = turned.shape[0]

    def block(c):
        return projected, (None, whole, LANES), lambda p, flags: (c, 0, p)

    def columns(field):
        return field, (field.shape[0], LANES), lambda p, flags: (0, p)

    low = jnp.bfloat16
    piece = ((depth, width), low, (depth, LANES), lambda p, flags: (0, p))
    return streamed(
        functools.partial(attend_back_kernel, reach),
        width // LANES,
        [flags],
        [apart, member, cos, sin, block(0), block(1), block(2), columns(grad_mixed), turned, columns(out_grad)],
        [((count, whole, width), low, (count, whole, LANES), lambda p, flags: (0, 0, p))] + [piece] * 4,
        [
            ((whole, 2 * LANES), low),
            ((LANES, whole), low),
            ((whole, LANES), jnp.float32),
            ((whole, LANES), jnp.float32),
        ],
        28,
    )


ROWS = 256


def norm_parts(field):
    centered = field - jnp.mean(field, axis=-1, keepdims=True)
    scale = lax.rsqrt(jnp.mean(centered * centered, axis=-1, keepdims=True) + NORM_EPS)
    return centered * scale, scale


def wide(ref, at):
    return ref[at, :].astype(jnp.float32)


def row_blocks(count, body):
    def step(i, carry):
        body(i, pl.ds(pl.multiple_of(i * ROWS, ROWS), ROWS))
        return carry

    lax.fori_loop(0, count // ROWS, step, 0)


TALL = 512


def streamed(kernel, steps, scalars, fields, outs, scratch, microseconds, room=ROOM):
    def spec(shape, block=None, at=None):
        if block is None:
            return pl.BlockSpec(shape, lambda i, *scalars: (0,) * len(shape))
        return pl.BlockSpec(block, at)

    fields = [field if isinstance(field, tuple) else (field,) for field in fields]
    return pl.pallas_call(
        kernel,
        grid_spec=pltpu.PrefetchScalarGridSpec(
            num_scalar_prefetch=len(scalars),
            grid=(steps,),
            in_specs=[spec(field[0].shape, *field[1:]) for field in fields],
            out_specs=[spec(out[0], *out[2:]) for out in outs],
            scratch_shapes=[pltpu.VMEM(shape, dtype) for shape, dtype in scratch],
        ),
        out_shape=[jax.ShapeDtypeStruct(*out[:2]) for out in outs],
        compiler_params=pltpu.CompilerParams(vmem_limit_bytes=room),
        cost_estimate=lasting(microseconds),
    )(*scalars, *[field[0] for field in fields])


def by_rows(field, rows, shift=None):
    if shift is None:
        return field, (rows, field.shape[1]), lambda i, *scalars: (i, 0)
    return field, (rows, field.shape[1]), lambda i, *scalars: (shift(i, *scalars), 0)


def whole_spec(shape):
    return pl.BlockSpec(shape, lambda *at: (0,) * len(shape))


def turn(field, cos, sin):
    half = HEAD_DIM // 2
    lane = lax.broadcasted_iota(jnp.int32, field.shape, 1) % HEAD_DIM
    crossed = jnp.where(lane < half, pltpu.roll(field, LANES - half, 1), pltpu.roll(field, half, 1))
    return field * cos + crossed * sin


def project_kernel(flags, rows_ref, cos_ref, sin_ref, vectors, w_own, w_near, w_far, out_ref, turned_ref, weight_ref):
    @pl.when(pl.program_id(0) == 0)
    def _():
        half = w_near.shape[1]
        for index, got in ((flags[2], w_near), (1 - flags[2], w_far)):
            at = pl.ds(pl.multiple_of(index * half, half), half)
            weight_ref[:, at, :] = jnp.where(flags[0] == 1, w_own[:, at, :], got[...])

    unit, unused = norm_parts(rows_ref[...].astype(jnp.float32))
    norm = unit * vectors[0:1, :] + vectors[1:2, :]
    turned_ref[...] = norm.T.astype(jnp.bfloat16)
    norm = norm.astype(jnp.bfloat16)
    for c in range(weight_ref.shape[0]):
        field = dot(norm, weight_ref[c])
        if c == 2:
            out_ref[c] = field.astype(jnp.bfloat16)
        else:
            for p in range(field.shape[1] // LANES):
                lanes = slice(p * LANES, (p + 1) * LANES)
                out_ref[c, :, lanes] = turn(field[:, lanes], cos_ref[...], sin_ref[...]).astype(jnp.bfloat16)


def project(flags, rows, vectors, cos, sin, w_own, w_near, w_far):
    whole, width = rows.shape
    count, unused, columns = w_own.shape
    low = jnp.bfloat16
    return streamed(
        project_kernel,
        whole // ROWS,
        [flags],
        [by_rows(rows, ROWS), by_rows(cos, ROWS), by_rows(sin, ROWS), vectors, w_own, w_near, w_far],
        [
            ((count, whole, columns), low, (count, ROWS, columns), lambda i, flags: (0, i, 0)),
            ((width, whole), low, (width, ROWS), lambda i, flags: (0, i)),
            (w_own.shape, low),
        ],
        [],
        8,
    )


def gelu_both(up):
    root = math.sqrt(2.0 / math.pi)
    square = up * up
    bent = jnp.tanh(root * up * (1.0 + 0.044715 * square))
    half = 0.5 * (1.0 + bent)
    slope = half + 0.5 * up * (1.0 - bent * bent) * (root * (1.0 + 3.0 * 0.044715 * square))
    return up * half, slope


def feed_kernel(early, *refs):
    if early:
        flags, weight_ref, rows_ref, own_ref, got_ref, cot_ref, vectors, up_own, down_own, got = refs[:10]
        norm, norm_t, grad, grad_t, back_ref, act_ref, down_ref, pieces = refs[10:18]
        up_got, down_got = got.at[: norm.shape[1]], got.at[norm.shape[1] :]
    else:
        flags, norm, norm_t, grad, grad_t, back_early, up_own, down_own, up_got, down_got = refs[:10]
        back_ref, act_ref, down_ref, *pieces = refs[10:17]
    up_w, up_sum, down_sum = refs[-3:]
    part = up_w.shape[1] // 2
    step, last = pl.program_id(0), pl.num_programs(0) - 1

    @pl.when(step == 0)
    def _():
        up_w[...] = jnp.where(flags[0] == 1, up_own[...], up_got[...])
        down_ref[...] = jnp.where(flags[0] == 1, down_own[...], down_got[...])

    if early:

        def head(i, at):
            unit, unused = norm_parts(wide(rows_ref, at) + wide(own_ref, at) + wide(got_ref, at))
            field = unit * vectors[2:3, :] + vectors[3:4, :]
            norm[at, :] = field.astype(jnp.bfloat16)
            norm_t[:, at] = field.T.astype(jnp.bfloat16)
            field = wide(cot_ref, at) * weight_ref[weight_ref.shape[0] - 1]
            grad[at, :] = field.astype(jnp.bfloat16)
            grad_t[:, at] = field.T.astype(jnp.bfloat16)

        row_blocks(norm.shape[0], head)
    value, rise = gelu_both(dot(norm[...], up_w[...]))
    act_ref[...] = value.astype(jnp.bfloat16)
    slope = (dot(grad[...], down_ref[...], NT) * rise).astype(jnp.bfloat16)
    back = dot(slope, up_w[...], NT)
    if not early:
        back = back + back_early[...].astype(jnp.float32)
    back_ref[...] = back.astype(jnp.bfloat16)

    def store(p, at, low):
        if early:
            pieces[p, at, :] = low
            return
        slot = 2 * (flags[2] ^ (p % 2)) + (flags[3] ^ (p // 2))
        for j, piece in enumerate(pieces):

            @pl.when(slot == j)
            def _():
                piece[at, :] = low

    def grads(i, at):
        fields = (dot(norm_t[at, :], slope), dot(grad_t[at, :], act_ref[...]))
        for k, (field, total) in enumerate(zip(fields, (up_sum, down_sum))):

            @pl.when(step == 0)
            def _():
                total[at, :] = field

            @pl.when(step == last)
            def _():
                low = (total[at, :] + field).astype(jnp.bfloat16)
                for p in range(2):
                    store(2 * k + p, at, low[:, p * part : (p + 1) * part])

    row_blocks(norm_t.shape[0], grads)


def feed(early, scalars, fields, w_up, w_down, *got):
    whole, width = fields[0].shape
    hidden = w_up.shape[1] // 2
    rows = whole // 2
    half = 0 if early else 1
    low = jnp.bfloat16

    def across(i, *scalars):
        return (0, i)

    tokens = ((whole, width), low, (rows, width), lambda i, *scalars: (i, 0))
    turned = ((width, whole), low, (width, rows), across)
    if early:
        operands = [by_rows(field, rows) for field in fields[:4]] + [fields[4]]
        outs = [tokens, turned, tokens, turned]
        pieces = [((4, width, hidden // 2), low)]
    else:
        operands = [by_rows(fields[0], rows), (fields[1], (width, rows), across)]
        operands += [by_rows(fields[2], rows), (fields[3], (width, rows), across), by_rows(fields[4], rows)]
        outs = []
        pieces = [((width, hidden // 2), low)] * 4
    operands += [
        (w_up, (width, hidden), lambda i, *scalars: (0, half)),
        (w_down, (hidden, width), lambda i, *scalars: (half, 0)),
        *got,
    ]
    outs += [tokens, ((whole, hidden), low, (rows, hidden), lambda i, *scalars: (i, 0)), ((hidden, width), low)]
    sums = ((width, hidden), jnp.float32)
    return streamed(
        functools.partial(feed_kernel, early), 2, scalars, operands, outs + pieces, [((width, hidden), low), sums, sums], 17
    )


def lower_kernel(
    flags, act_early, act_late, rows_ref, own_ref, got_ref, cot_ref, early_ref, late_ref, keep_ref, first, second, sums_ref
):
    step = pl.program_id(0)
    total = dot(act_early[...], early_ref[...]) + dot(act_late[...], late_ref[...])
    cot = cot_ref[...].astype(jnp.float32)

    @pl.when(step == 0)
    def _():
        sums_ref[...] = jnp.zeros_like(sums_ref)

    send_or_keep(
        total,
        total + sum(ref[...].astype(jnp.float32) for ref in (rows_ref, own_ref, got_ref)),
        first,
        second,
        keep_ref,
    )
    mine = jnp.where(step < pl.num_programs(0) // 2, 0.0, 1.0)
    block = total + mine * sum(ref[...].astype(jnp.float32) for ref in (rows_ref, own_ref, got_ref))
    sums_ref[0:1, :] += jnp.sum(block * cot, axis=0, keepdims=True)


def send_or_keep(sent, kept, first, second, keep_ref):
    step = pl.program_id(0)
    for j, ref in enumerate((first, second)):

        @pl.when(step == j)
        def _():
            ref[...] = sent.astype(ref.dtype)

    @pl.when(step >= 2)
    def _():
        keep_ref[...] = kept


def theirs_first(i, flags, *more):
    return lax.rem((1 - flags[1]) * 2 + i, 4)


def sent_and_kept(whole, width):
    rows = whole // 4
    keep = ((2 * rows, width), jnp.float32, (rows, width), lambda i, *scalars: (jnp.maximum(i - 2, 0), 0))
    send = ((rows, width), jnp.bfloat16)
    return [keep, send, send, ((8, width), jnp.float32)]


def lower(flags, act_early, act_late, down_early, down_late, rows, own, got, cot):
    whole, width = rows.shape
    fields = [by_rows(field, whole // 4, theirs_first) for field in (act_early, act_late, rows, own, got, cot)]
    return streamed(
        lower_kernel, 4, [flags], fields + [down_early, down_late], sent_and_kept(whole, width), [], 6, SNUG
    )


def middle_kernel(
    flags, weight_ref, rows_ref, own_ref, got_ref, cot_ref, back_own, back_got, mixed_ref,
    vectors, w_ref, grad_ref, gmixed_ref, gout_ref, sums_ref, gout,
):
    step, last = pl.program_id(0), pl.num_programs(0) - 1
    unit, scale = norm_parts(sum(ref[...].astype(jnp.float32) for ref in (rows_ref, own_ref, got_ref)))
    back = sum(ref[...].astype(jnp.float32) for ref in (back_own, back_got))
    inner = back * vectors[2:3, :]
    mean = jnp.mean(inner, axis=-1, keepdims=True)
    slant = jnp.mean(inner * unit, axis=-1, keepdims=True)
    cot = cot_ref[...].astype(jnp.float32) * weight_ref[weight_ref.shape[0] - 1]
    grad = cot + scale * (inner - mean - unit * slant)
    low = grad.astype(jnp.bfloat16)
    grad_ref[...] = low
    gmixed_ref[...] = dot(low, w_ref[...], NT).astype(jnp.bfloat16)
    part = dot(grad.T.astype(jnp.bfloat16), mixed_ref[...])

    @pl.when(step == 0)
    def _():
        gout[...] = part
        sums_ref[...] = jnp.zeros_like(sums_ref)

    @pl.when(step > 0)
    def _():
        gout[...] += part

    @pl.when(step == last)
    def _():
        gout_ref[...] = gout[...].astype(jnp.bfloat16)

    @pl.when(step // ((last + 1) // 2) == flags[1])
    def _():
        sums_ref[0:1, :] += jnp.sum(back * unit, axis=0, keepdims=True)
        sums_ref[1:2, :] += jnp.sum(back, axis=0, keepdims=True)


def middle(flags, weight, fields, mixed, vectors, bundle):
    whole, width = fields[0].shape
    columns = mixed.shape[1]
    low = jnp.bfloat16
    in_order = lambda i, *scalars: (i, 0)
    return streamed(
        middle_kernel,
        whole // ROWS,
        [flags, weight],
        [by_rows(field, ROWS) for field in (*fields, mixed)]
        + [vectors, (bundle, (columns, width), lambda i, *scalars: (0, 0))],
        [
            ((whole, width), low, (ROWS, width), in_order),
            ((whole, columns), low, (ROWS, columns), in_order),
            ((width, columns), low),
            ((8, width), jnp.float32),
        ],
        [((width, columns), jnp.float32)],
        8,
    )


def unproject_kernel(flags, grad_ref, rows_ref, weight, keep_ref, first, second, sums_ref):
    total = dot(grad_ref[0], weight[0], NT)
    for c in range(1, grad_ref.shape[0]):
        total = total + dot(grad_ref[c], weight[c], NT)
    unit, unused = norm_parts(rows_ref[...].astype(jnp.float32))

    @pl.when(pl.program_id(0) == 0)
    def _():
        sums_ref[...] = jnp.zeros_like(sums_ref)

    sums_ref[0:1, :] += jnp.sum(total * unit, axis=0, keepdims=True)
    sums_ref[1:2, :] += jnp.sum(total, axis=0, keepdims=True)
    send_or_keep(total, total, first, second, keep_ref)


def unproject(flags, grad, weight, rows):
    whole, width = rows.shape
    count, unused, columns = grad.shape
    grads = (grad, (count, whole // 4, columns), lambda i, flags: (0, theirs_first(i, flags), 0))
    fields = [grads, by_rows(rows, whole // 4, theirs_first), weight]
    return streamed(unproject_kernel, 4, [flags], fields, sent_and_kept(whole, width), [], 5, SNUG)


def last_kernel(
    flags, rows_ref, resid_ref, keep_ref, block_keep, got_first, got_second, block_first, block_second, vectors, out_ref
):
    first = pl.program_id(0) == 0
    unit, scale = norm_parts(rows_ref[...].astype(jnp.float32))
    got = jnp.where(first, got_first[...], got_second[...]).astype(jnp.float32)
    inner = (keep_ref[...] + got) * vectors[0:1, :]
    mean = jnp.mean(inner, axis=-1, keepdims=True)
    slant = jnp.mean(inner * unit, axis=-1, keepdims=True)
    grad = resid_ref[...].astype(jnp.float32) + scale * (inner - mean - unit * slant)
    out_ref[0] = grad.astype(jnp.bfloat16)
    got = jnp.where(first, block_first[...], block_second[...]).astype(jnp.float32)
    out_ref[1] = (block_keep[...] + got).astype(jnp.bfloat16)


def last(flags, rows, resid, keep, block_keep, got, vectors):
    half, width = keep.shape
    size = half // 2

    def mine(i, flags):
        return flags[1] * 2 + i

    out = ((2, half, width), jnp.bfloat16, (2, size, width), lambda i, flags: (0, i, 0))
    fields = [by_rows(rows, size, mine), by_rows(resid, size, mine), by_rows(keep, size), by_rows(block_keep, size)]
    return streamed(last_kernel, 2, [flags], fields + [*got, vectors], [out], [], 3)[0]


def past_kernel(dwa_ref, hist_ref, cot_ref, grad_ref, part_ref, sums_ref):
    @pl.when(pl.program_id(0) == 0)
    def _():
        sums_ref[...] = jnp.zeros_like(sums_ref)

    grad = cot_ref[...].astype(jnp.float32)
    total = jnp.zeros_like(grad)
    for j in range(hist_ref.shape[0]):
        field = hist_ref[j].astype(jnp.float32)
        total += dwa_ref[j] * field
        grad_ref[j] = (dwa_ref[j] * grad).astype(jnp.bfloat16)
        sums_ref[j : j + 1, :] += jnp.sum(field * grad, axis=0, keepdims=True)
    part_ref[...] = total


def past(dwa, history, cot):
    count, rows, width = history.shape
    layers = pl.BlockSpec((count, ROWS, width), lambda i: (0, i, 0))
    tokens = pl.BlockSpec((ROWS, width), lambda i: (i, 0))
    return pl.pallas_call(
        past_kernel,
        grid=(rows // ROWS,),
        in_specs=[pl.BlockSpec(memory_space=pltpu.SMEM), layers, tokens],
        out_specs=[layers, tokens, whole_spec((8, width))],
        out_shape=[
            jax.ShapeDtypeStruct(history.shape, jnp.bfloat16),
            jax.ShapeDtypeStruct((rows, width), jnp.float32),
            jax.ShapeDtypeStruct((8, width), jnp.float32),
        ],
        compiler_params=pltpu.CompilerParams(vmem_limit_bytes=ROOM),
        cost_estimate=lasting(3),
    )(dwa, history, cot)


def present_kernel(flags, weight_ref, part_ref, own_ref, got_ref, out_ref, grad_ref):
    here = jnp.where(flags[0] == 1, own_ref[1], got_ref[1]).astype(jnp.float32)
    out_ref[...] = (part_ref[...] + weight_ref[weight_ref.shape[0] - 1] * here).astype(jnp.bfloat16)
    grad_ref[...] = jnp.where(flags[0] == 1, own_ref[0], got_ref[0])


def present(flags, weight, part, own, got):
    rows, width = part.shape
    both = (2, ROWS, width), lambda i, *scalars: (0, i, 0)
    out = ((rows, width), jnp.bfloat16, (ROWS, width), lambda i, *scalars: (i, 0))
    fields = [by_rows(part, ROWS), (own, *both), (got, *both)]
    return streamed(present_kernel, rows // ROWS, [flags, weight], fields, [out] * 2, [], 2, SNUG)


def place_kernel(flags, here_ref, there_ref, qkv_ref, out_ref, up_ref, down_ref):
    near, far = flags[1], flags[2]
    part = out_ref.shape[1]
    for k in range(2):
        for c in range(2):
            field = jnp.where(near == c, here_ref[k ^ far], there_ref[k ^ far]).astype(jnp.float32)
            if 2 * k + c < 3:
                qkv_ref[2 * k + c] = field[:, :part]
            else:
                out_ref[...] = field[:, :part]
            for half in range(2):
                at = (2 * half + k) * part
                (up_ref, down_ref)[c][:, at : at + part] = field[:, (1 + half) * part : (2 + half) * part]


def place(flags, here, there):
    rows, part = here.shape[1], here.shape[2] // 3
    outs = [((3, rows, part), jnp.float32), ((rows, part), jnp.float32)]
    outs += [((rows, 4 * part), jnp.float32)] * 2
    return streamed(place_kernel, 1, [flags], [here, there], outs, [], 3, SNUG)


AXES = ("tp", "dp", "far", "near")


def moves(chosen, move):
    sizes = [lax.axis_size(name) for name in AXES]
    places = [place for place in itertools.product(*map(range, sizes)) if chosen(*place)]
    index = lambda place: functools.reduce(lambda at, step: at * step[0] + step[1], zip(sizes, place), 0)
    return [(index(place), index(move(*place))) for place in places]


def away(t, d, k, c):
    return t != c


def anyone(t, d, k, c):
    return True


def swap_diagonal(field):
    return lax.ppermute(field, AXES, moves(away, lambda t, d, k, c: (c, d, k, t)))


def send_to_owner(field, other_far, other_tp):
    return lax.ppermute(
        field,
        AXES,
        moves(
            away if not other_far and not other_tp else anyone,
            lambda t, d, k, c: (c, d, k ^ other_far, t ^ other_tp),
        ),
    )


def swap_far_away(field):
    return lax.ppermute(field, AXES, moves(away, lambda t, d, k, c: (t, d, 1 - k, c)))


def swap_far(field):
    return lax.ppermute(field, "far", [(0, 1), (1, 0)])


def swap_near(field):
    return lax.ppermute(field, "near", [(0, 1), (1, 0)])


def after(field, *others):
    return lax.optimization_barrier((field, *others))[0]


def ordered(own, other, first, axis=0):
    return jnp.where(
        first, jnp.concatenate([own, other], axis=axis), jnp.concatenate([other, own], axis=axis)
    )


def part_of(field, index, axis):
    size = field.shape[axis] // 2
    return lax.dynamic_slice_in_dim(field, index * size, size, axis)


def add(*fields):
    return sum(field.astype(jnp.float32) for field in fields).astype(jnp.bfloat16)


def scatter_plane(pieces):
    return lax.psum_scatter(pieces, ("tp", "far"), scatter_dimension=0, tiled=True)[0]


def scatter_rows(piece):
    return lax.psum_scatter(piece, "dp", scatter_dimension=0, tiled=True)


def move_rows(block):
    dps = lax.axis_size("dp")
    if dps > 8:
        return [scatter_rows(block)]
    block = block.reshape(dps, block.shape[0] // dps, block.shape[1])
    place = lax.axis_index("dp")
    moved = [lax.dynamic_index_in_dim(block, place, 0, keepdims=False)]
    for step in range(1, dps):
        sent = lax.dynamic_index_in_dim(block, lax.rem(place + step, dps), 0, keepdims=False)
        moved.append(lax.ppermute(sent, "dp", [(d, (d + step) % dps) for d in range(dps)]))
    return moved


def sum_over(field, name):
    size = lax.axis_size(name)
    bit = 1
    while bit < size:
        field = field + lax.ppermute(field, name, [(d, d ^ bit) for d in range(size)])
        bit *= 2
    return field


def local(
    layer_input,
    history,
    cotangent,
    lengths,
    dwa_weights,
    gain_one,
    bias_one,
    w_qkv,
    w_out,
    gain_two,
    bias_two,
    w_up,
    w_down,
):
    rows = layer_input.shape[1]
    whole = rows * lax.axis_size("tp")
    hist_count = history.shape[0]
    part, far, near = lax.axis_index("tp"), lax.axis_index("far"), lax.axis_index("near")
    same = near == part
    flags = jnp.stack([same.astype(jnp.int32), near, far, part])

    input_got = swap_diagonal(layer_input[0])
    qkv_near = swap_diagonal(part_of(w_qkv, far, 1))
    qkv_far = swap_far_away(qkv_near)
    early_got = jnp.concatenate([part_of(w_up, 0, 1), part_of(w_down, 0, 0)], axis=0)
    late_up, late_down = part_of(w_up, 1, 1), part_of(w_down, 1, 0)
    last_own = jnp.concatenate([w_out, cotangent[0]], axis=0)
    vectors = jnp.stack([gain_one, bias_one, gain_two, bias_two])

    own_lengths = jnp.where(same, lengths, swap_near(lengths))[0]
    seq_owner, token_place = positions(own_lengths, whole)
    lane = jnp.arange(LANES, dtype=jnp.int32)
    member = seq_owner[:, None] == lane[None, :]
    apart = jnp.where(member | (lane >= lengths.shape[1])[None, :], 0.0, NEG_FILL).astype(jnp.bfloat16)
    member = member.astype(jnp.bfloat16)
    half_dim = HEAD_DIM // 2
    frequency = jnp.exp((lane % half_dim).astype(jnp.float32) * (-math.log(10000.0) / half_dim))
    angles = token_place.astype(jnp.float32)[:, None] * frequency[None, :]
    cos_table = jnp.cos(angles)
    sin_table = jnp.sin(angles) * jnp.where(lane % HEAD_DIM < half_dim, -1.0, 1.0)[None, :]
    grad_history, past_sum, sums_past = past(dwa_weights, history[:, 0], cotangent[0])

    input_half = jnp.where(same, layer_input[0], input_got)
    layer_rows = ordered(input_half, swap_near(input_half), near == 0)
    layer_rows, last_own, early_got, late_up, vectors, past_sum, *tables = lax.optimization_barrier(
        (layer_rows, last_own, early_got, late_up, vectors, past_sum)
        + (cos_table, sin_table, apart, member)
    )
    cos_table, sin_table, apart, member = tables
    early_got = swap_diagonal(early_got)
    last_got = swap_diagonal(last_own)
    projected, norm_one_t, weight_qkv = project(
        flags, layer_rows, vectors, cos_table, sin_table, w_qkv, qkv_near, qkv_far
    )
    mixed = attend(apart, member, projected, LONGEST)
    late_up = swap_diagonal(after(late_up, mixed))
    late_down = swap_diagonal(after(late_down, mixed))
    last_got = jnp.where(same, last_own, last_got)
    weight_out = last_got[: w_out.shape[0]]
    attn = jnp.dot(mixed, weight_out, preferred_element_type=jnp.float32).astype(jnp.bfloat16)
    attn_got = swap_near(attn)
    cot_half = last_got[w_out.shape[0] :]
    cot_rows = ordered(cot_half, swap_near(cot_half), near == 0)
    scalars = [flags, dwa_weights]
    fields = [layer_rows, attn, attn_got, cot_rows, vectors]
    *kept, back, act_early, down_early, early_pieces = feed(True, scalars, fields, w_up, w_down, early_got)
    early_sum = scatter_plane(after(early_pieces, late_up, late_down))
    back, act_late, down_late, *late_owned = feed(
        False, [flags], [*kept, back], w_up, w_down, late_up, late_down
    )
    late_moved = [send_to_owner(late_owned[j], j // 2, j % 2) for j in range(4)]
    fields = [layer_rows, attn, attn_got, cot_rows, back, swap_near(back)]
    grad_attn, grad_mixed, grad_out, sums_two = middle(flags, dwa_weights, fields, mixed, vectors, last_got)
    grad_qkv, *owned = attend_back(
        flags, apart, member, cos_table, sin_table, projected, grad_mixed, norm_one_t, grad_out, LONGEST
    )
    grad_qkv, *late_moved = lax.optimization_barrier((grad_qkv, *late_moved))
    moved = [send_to_owner(owned[j], j // 2, j % 2) for j in range(4)]
    early_sum = scatter_rows(after(early_sum, grad_qkv))
    late_sum = scatter_rows(add(jnp.where(same, late_owned[0], late_moved[0]), *late_moved[1:]))
    keep, *send, sums_one = unproject(flags, grad_qkv, weight_qkv, layer_rows)
    block_keep, *block_send, sums_now = lower(
        flags, act_early, act_late, down_early, down_late, layer_rows, attn, attn_got, after(cot_rows, keep)
    )
    sent = [*send, *block_send]
    keep, block_keep, *arrived = lax.optimization_barrier((keep, block_keep, *sent, *moved))
    sent, moved = arrived[:4], arrived[4:]
    attn_one = add(jnp.where(same, owned[0], moved[0]), *moved[1:])
    attn_moved = move_rows(attn_one)
    got = [swap_near(field) for field in sent]
    ours = last(flags, layer_rows, grad_attn, after(keep, attn_one), block_keep, got, vectors)
    early_sum = after(early_sum, attn_one)
    early_got = swap_diagonal(early_sum)
    small = jnp.concatenate([sums_one[:2], sums_two[:2], sums_now[:1], sums_past[:hist_count]], axis=0)
    small = after(small, ours)
    for name in ("near", "tp", "far"):
        small = sum_over(small, name)
    small, ours, late_sum, early_sum, early_got, *attn_moved = lax.optimization_barrier(
        (small, ours, late_sum, early_sum, early_got, *attn_moved)
    )
    theirs = swap_diagonal(ours)
    small = sum_over(small, "dp")
    attn_sum = add(*attn_moved)
    blocks = jnp.concatenate([attn_sum, jnp.where(same, early_sum, early_got), late_sum], axis=1)
    here = jnp.stack([blocks, swap_far(blocks)])
    output, grad_input = present(flags, dwa_weights, past_sum, ours, theirs)
    grad_w_qkv, grad_w_out, grad_w_up, grad_w_down = place(flags, here, swap_near(here))

    return (
        output[None],
        grad_input[None],
        grad_history[:, None],
        jnp.sum(jnp.concatenate([small[5:], small[4:5]], axis=0), axis=1),
        small[0],
        small[1],
        grad_w_qkv,
        grad_w_out.T,
        small[2],
        small[3],
        grad_w_up,
        grad_w_down.T,
    )


def positions(seq_lengths, token_count):
    seq_ends = jnp.cumsum(seq_lengths)
    seq_starts = seq_ends - seq_lengths
    token_index = jnp.arange(token_count, dtype=jnp.int32)
    seq_owner = jnp.sum((token_index[:, None] >= seq_ends[None, :]).astype(jnp.int32), axis=1)
    picked = (
        seq_owner[:, None] == jnp.arange(seq_lengths.shape[0], dtype=jnp.int32)[None, :]
    ).astype(jnp.int32)
    seq_begin = jnp.sum(picked * seq_starts[None, :], axis=1)
    return (seq_owner, token_index - seq_begin)


def solution(mesh):
    tps, dps, reps = (mesh.shape[name] for name in ("tp", "dp", "rep"))
    split = Mesh(mesh.devices.reshape(tps, dps, reps // 2, 2), AXES)
    in_specs = (
        P(("dp", "far", "near"), "tp", None),
        P(None, ("dp", "far", "near"), "tp", None),
        P(("dp", "far", "near"), "tp", None),
        P(("dp", "far", "near"), None),
        P(),
        P(),
        P(),
        P(None, None, "tp"),
        P("tp", None),
        P(),
        P(),
        P(None, "tp"),
        P("tp", None),
    )
    out_specs = (
        P(("dp", "far", "near"), "tp", None),
        P(("dp", "far", "near"), "tp", None),
        P(None, ("dp", "far", "near"), "tp", None),
        P(),
        P(),
        P(),
        P(None, "dp", "tp"),
        P("tp", "dp"),
        P(),
        P(),
        P("dp", "tp"),
        P("tp", "dp"),
    )
    return jax.shard_map(local, mesh=split, in_specs=in_specs, out_specs=out_specs, check_vma=False)
```

```python
import functools
import itertools
import math

import jax
import jax.numpy as jnp
from jax import lax
from jax.experimental import pallas as pl
from jax.experimental.pallas import tpu as pltpu
from jax.sharding import Mesh, PartitionSpec as P

HEAD_DIM = 64
LONGEST = 512
NEG_FILL = -1e30
NORM_EPS = 1e-05
RATE = 3e6
ROOM = 60 << 20
SNUG = 18 << 20


def lasting(microseconds):
    return pl.CostEstimate(flops=0, transcendentals=0, bytes_accessed=int(microseconds * RATE))


BLOCK = 256
LANES = 128
NT = (((1,), (1,)), ((), ()))


def dot(a, b, dims=(((1,), (0,)), ((), ()))):
    return lax.dot_general(a, b, dims, preferred_element_type=jnp.float32)


def spans(whole, reach):
    back = -(-(reach - 1) // BLOCK)
    runs = []
    for i in range(whole // BLOCK):
        count = min(i, back) + 1
        if runs and runs[-1][2] == count:
            runs[-1][1] = i + 1
        else:
            runs.append([i, i + 1, count])
    return runs


def each_block(whole, reach, body):
    for first, last, count in spans(whole, reach):

        def step(i, carry, count=count):
            body(i, i + 1 - count, count)
            return carry

        lax.fori_loop(first, last, step, 0)


def block_at(i, count=1):
    return pl.ds(pl.multiple_of(i * BLOCK, BLOCK), count * BLOCK)


def head_query(q_ref, apart_ref, i, head):
    lane = lax.broadcasted_iota(jnp.int32, (BLOCK, LANES), 1) // HEAD_DIM
    query = q_ref[block_at(i), :] * (HEAD_DIM**-0.5)
    query = jnp.where(lane == head, query, jnp.zeros_like(query))
    return query, jnp.concatenate([query, apart_ref[block_at(i), :]], axis=1)


def attend_kernel(reach, apart_ref, member_ref, q_ref, k_ref, v_ref, out_ref, keys):
    whole = q_ref.shape[0]
    lane = lax.broadcasted_iota(jnp.int32, (BLOCK, LANES), 1) // HEAD_DIM
    keys[:, :LANES] = k_ref[...]
    keys[:, LANES:] = member_ref[...]

    def one(i, first, count, head):
        unused, query = head_query(q_ref, apart_ref, i, head)
        own = dot(query, keys[block_at(i), :], NT)
        key_at = lax.broadcasted_iota(jnp.int32, own.shape, 1)
        query_at = lax.broadcasted_iota(jnp.int32, own.shape, 0)
        scores = jnp.where(key_at <= query_at, own, NEG_FILL)
        if count > 1:
            scores = jnp.concatenate([dot(query, keys[block_at(first, count - 1), :], NT), scores], axis=1)
        exponent = jnp.exp(scores - jnp.max(scores, axis=1, keepdims=True))
        row_sum = jnp.sum(exponent, axis=1, keepdims=True)
        return dot(exponent.astype(jnp.bfloat16), v_ref[block_at(first, count), :]) * (1.0 / row_sum)

    def body(i, first, count):
        mixed = [one(i, first, count, head) for head in range(2)]
        out_ref[block_at(i), :] = jnp.where(lane == 0, *mixed).astype(out_ref.dtype)

    each_block(whole, reach, body)


def attend(apart, member, projected, reach):
    count, whole, width = projected.shape

    def block(c):
        return pl.BlockSpec((None, whole, LANES), lambda p: (c, 0, p))

    table = pl.BlockSpec((whole, LANES), lambda p: (0, 0))
    return pl.pallas_call(
        functools.partial(attend_kernel, reach),
        grid=(width // LANES,),
        in_specs=[table, table, block(0), block(1), block(2)],
        out_specs=pl.BlockSpec((whole, LANES), lambda p: (0, p)),
        out_shape=jax.ShapeDtypeStruct((whole, width), jnp.bfloat16),
        scratch_shapes=[pltpu.VMEM((whole, 2 * LANES), jnp.bfloat16)],
        compiler_params=pltpu.CompilerParams(vmem_limit_bytes=ROOM),
        cost_estimate=lasting(12),
    )(apart, member, projected, projected, projected)


def turn_back(field, cos, sin):
    half = HEAD_DIM // 2
    lane = lax.broadcasted_iota(jnp.int32, field.shape, 1) % HEAD_DIM
    crossed = jnp.where(lane < half, pltpu.roll(field, LANES - half, 1), pltpu.roll(field, half, 1))
    return field * cos - crossed * sin


def attend_back_kernel(
    reach, apart_ref, member_ref, cos_ref, sin_ref, q_ref, k_ref, v_ref, g_ref, out_ref, keys, keys_t, key_acc, value_acc
):
    whole = q_ref.shape[0]
    lane = lax.broadcasted_iota(jnp.int32, (BLOCK, LANES), 1) // HEAD_DIM
    keys[:, :LANES] = k_ref[...]
    keys[:, LANES:] = member_ref[...]
    keys_t[...] = k_ref[...].astype(jnp.float32).T.astype(jnp.bfloat16)
    key_acc[...] = jnp.zeros_like(key_acc)
    value_acc[...] = jnp.zeros_like(value_acc)

    def one(i, first, count, head):
        span = block_at(first, count)
        plain, query = head_query(q_ref, apart_ref, i, head)
        grad = g_ref[block_at(i), :]
        grad = jnp.where(lane == head, grad, jnp.zeros_like(grad))
        own = dot(keys[block_at(i), :], query, NT)
        key_at = lax.broadcasted_iota(jnp.int32, own.shape, 0)
        query_at = lax.broadcasted_iota(jnp.int32, own.shape, 1)
        scores = jnp.where(key_at <= query_at, own, NEG_FILL)
        if count > 1:
            scores = jnp.concatenate([dot(keys[block_at(first, count - 1), :], query, NT), scores], axis=0)
        exponent = jnp.exp(scores - jnp.max(scores, axis=0, keepdims=True))
        probs = exponent * (1.0 / jnp.sum(exponent, axis=0, keepdims=True))
        grad_values = dot(probs.astype(jnp.bfloat16), grad)
        weighted = probs * dot(v_ref[span, :], grad, NT)
        grad_scores = (weighted - probs * jnp.sum(weighted, axis=0, keepdims=True)).astype(jnp.bfloat16)
        here = dot(keys_t[:, span], grad_scores)
        return grad_values, dot(grad_scores, plain), here

    def body(i, first, count):
        span, at = block_at(first, count), block_at(i)
        values, keys_, queries = zip(*[one(i, first, count, head) for head in range(2)])
        value_acc[span, :] += values[0] + values[1]
        key_acc[span, :] += keys_[0] + keys_[1]
        row = lax.broadcasted_iota(jnp.int32, queries[0].shape, 0) // HEAD_DIM
        both = jnp.where(row == 0, *queries).T * (HEAD_DIM**-0.5)
        out_ref[0, at, :] = turn_back(both, cos_ref[at, :], sin_ref[at, :]).astype(out_ref.dtype)

    each_block(whole, reach, body)

    def finish(i, carry):
        at = block_at(i)
        out_ref[1, at, :] = turn_back(key_acc[at, :], cos_ref[at, :], sin_ref[at, :]).astype(out_ref.dtype)
        out_ref[2, at, :] = value_acc[at, :].astype(out_ref.dtype)
        return carry

    lax.fori_loop(0, whole // BLOCK, finish, 0)


def attend_back(apart, member, cos, sin, projected, grad_mixed, reach):
    count, whole, width = projected.shape

    def block(c):
        return pl.BlockSpec((None, whole, LANES), lambda p: (c, 0, p))

    table = pl.BlockSpec((whole, LANES), lambda p: (0, 0))
    return pl.pallas_call(
        functools.partial(attend_back_kernel, reach),
        grid=(width // LANES,),
        in_specs=[table] * 4 + [block(0), block(1), block(2), pl.BlockSpec((whole, LANES), lambda p: (0, p))],
        out_specs=pl.BlockSpec((count, whole, LANES), lambda p: (0, 0, p)),
        out_shape=jax.ShapeDtypeStruct((count, whole, width), jnp.bfloat16),
        scratch_shapes=[
            pltpu.VMEM((whole, 2 * LANES), jnp.bfloat16),
            pltpu.VMEM((LANES, whole), jnp.bfloat16),
            pltpu.VMEM((whole, LANES), jnp.float32),
            pltpu.VMEM((whole, LANES), jnp.float32),
        ],
        compiler_params=pltpu.CompilerParams(vmem_limit_bytes=ROOM),
        cost_estimate=lasting(22),
    )(apart, member, cos, sin, projected, projected, projected, grad_mixed)


ROWS = 256


def norm_parts(field):
    centered = field - jnp.mean(field, axis=-1, keepdims=True)
    scale = lax.rsqrt(jnp.mean(centered * centered, axis=-1, keepdims=True) + NORM_EPS)
    return centered * scale, scale


def wide(ref, at):
    return ref[at, :].astype(jnp.float32)


def row_blocks(count, body):
    def step(i, carry):
        body(i, pl.ds(pl.multiple_of(i * ROWS, ROWS), ROWS))
        return carry

    lax.fori_loop(0, count // ROWS, step, 0)


TALL = 512


def streamed(kernel, steps, scalars, fields, outs, scratch, microseconds, room=ROOM):
    def spec(shape, block=None, at=None):
        if block is None:
            return pl.BlockSpec(shape, lambda i, *scalars: (0,) * len(shape))
        return pl.BlockSpec(block, at)

    fields = [field if isinstance(field, tuple) else (field,) for field in fields]
    return pl.pallas_call(
        kernel,
        grid_spec=pltpu.PrefetchScalarGridSpec(
            num_scalar_prefetch=len(scalars),
            grid=(steps,),
            in_specs=[spec(field[0].shape, *field[1:]) for field in fields],
            out_specs=[spec(out[0], *out[2:]) for out in outs],
            scratch_shapes=[pltpu.VMEM(shape, dtype) for shape, dtype in scratch],
        ),
        out_shape=[jax.ShapeDtypeStruct(*out[:2]) for out in outs],
        compiler_params=pltpu.CompilerParams(vmem_limit_bytes=room),
        cost_estimate=lasting(microseconds),
    )(*scalars, *[field[0] for field in fields])


def by_rows(field, rows, shift=None):
    if shift is None:
        return field, (rows, field.shape[1]), lambda i, *scalars: (i, 0)
    return field, (rows, field.shape[1]), lambda i, *scalars: (shift(i, *scalars), 0)


def whole_spec(shape):
    return pl.BlockSpec(shape, lambda *at: (0,) * len(shape))


def turn(field, cos, sin):
    half = HEAD_DIM // 2
    lane = lax.broadcasted_iota(jnp.int32, field.shape, 1) % HEAD_DIM
    crossed = jnp.where(lane < half, pltpu.roll(field, LANES - half, 1), pltpu.roll(field, half, 1))
    return field * cos + crossed * sin


def project_kernel(flags, rows_ref, cos_ref, sin_ref, vectors, w_own, w_near, w_far, out_ref, turned_ref, weight_ref):
    @pl.when(pl.program_id(0) == 0)
    def _():
        half = w_near.shape[1]
        for index, got in ((flags[2], w_near), (1 - flags[2], w_far)):
            at = pl.ds(pl.multiple_of(index * half, half), half)
            weight_ref[:, at, :] = jnp.where(flags[0] == 1, w_own[:, at, :], got[...])

    unit, unused = norm_parts(rows_ref[...].astype(jnp.float32))
    norm = unit * vectors[0:1, :] + vectors[1:2, :]
    turned_ref[...] = norm.T.astype(jnp.bfloat16)
    norm = norm.astype(jnp.bfloat16)
    for c in range(weight_ref.shape[0]):
        field = dot(norm, weight_ref[c])
        if c == 2:
            out_ref[c] = field.astype(jnp.bfloat16)
        else:
            for p in range(field.shape[1] // LANES):
                lanes = slice(p * LANES, (p + 1) * LANES)
                out_ref[c, :, lanes] = turn(field[:, lanes], cos_ref[...], sin_ref[...]).astype(jnp.bfloat16)


def project(flags, rows, vectors, cos, sin, w_own, w_near, w_far):
    whole, width = rows.shape
    count, unused, columns = w_own.shape
    low = jnp.bfloat16
    return streamed(
        project_kernel,
        whole // ROWS,
        [flags],
        [by_rows(rows, ROWS), by_rows(cos, ROWS), by_rows(sin, ROWS), vectors, w_own, w_near, w_far],
        [
            ((count, whole, columns), low, (count, ROWS, columns), lambda i, flags: (0, i, 0)),
            ((width, whole), low, (width, ROWS), lambda i, flags: (0, i)),
            (w_own.shape, low),
        ],
        [],
        8,
    )


def gelu_both(up):
    root = math.sqrt(2.0 / math.pi)
    square = up * up
    bent = jnp.tanh(root * up * (1.0 + 0.044715 * square))
    half = 0.5 * (1.0 + bent)
    slope = half + 0.5 * up * (1.0 - bent * bent) * (root * (1.0 + 3.0 * 0.044715 * square))
    return up * half, slope


def feed_kernel(early, *refs):
    if early:
        flags, weight_ref, rows_ref, own_ref, got_ref, cot_here, cot_there, vectors, up_own, down_own, got = refs[:11]
        norm, norm_t, grad, grad_t, back_ref, act_ref, down_ref, pieces = refs[11:19]
        up_got, down_got = got.at[: norm.shape[1]], got.at[norm.shape[1] :]
    else:
        flags, norm, norm_t, grad, grad_t, back_early, up_own, down_own, up_got, down_got = refs[:10]
        back_ref, act_ref, down_ref, *pieces = refs[10:17]
    up_w, up_sum, down_sum = refs[-3:]
    part = up_w.shape[1] // 2
    step, last = pl.program_id(0), pl.num_programs(0) - 1

    @pl.when(step == 0)
    def _():
        up_w[...] = jnp.where(flags[0] == 1, up_own[...], up_got[...])
        down_ref[...] = jnp.where(flags[0] == 1, down_own[...], down_got[...])

    if early:

        def head(i, at):
            unit, unused = norm_parts(wide(rows_ref, at) + wide(own_ref, at) + wide(got_ref, at))
            field = unit * vectors[2:3, :] + vectors[3:4, :]
            norm[at, :] = field.astype(jnp.bfloat16)
            norm_t[:, at] = field.T.astype(jnp.bfloat16)
            cot = jnp.where(flags[1] == step, cot_here[at, :], cot_there[at, :])
            field = cot.astype(jnp.float32) * weight_ref[weight_ref.shape[0] - 1]
            grad[at, :] = field.astype(jnp.bfloat16)
            grad_t[:, at] = field.T.astype(jnp.bfloat16)

        row_blocks(norm.shape[0], head)
    value, rise = gelu_both(dot(norm[...], up_w[...]))
    act_ref[...] = value.astype(jnp.bfloat16)
    slope = (dot(grad[...], down_ref[...], NT) * rise).astype(jnp.bfloat16)
    back = dot(slope, up_w[...], NT)
    if not early:
        back = back + back_early[...].astype(jnp.float32)
    back_ref[...] = back.astype(jnp.bfloat16)

    def store(p, at, low):
        if early:
            pieces[p, at, :] = low
            return
        slot = 2 * (flags[2] ^ (p % 2)) + (flags[3] ^ (p // 2))
        for j, piece in enumerate(pieces):

            @pl.when(slot == j)
            def _():
                piece[at, :] = low

    def grads(i, at):
        fields = (dot(norm_t[at, :], slope), dot(grad_t[at, :], act_ref[...]))
        for k, (field, total) in enumerate(zip(fields, (up_sum, down_sum))):

            @pl.when(step == 0)
            def _():
                total[at, :] = field

            @pl.when(step == last)
            def _():
                low = (total[at, :] + field).astype(jnp.bfloat16)
                for p in range(2):
                    store(2 * k + p, at, low[:, p * part : (p + 1) * part])

    row_blocks(norm_t.shape[0], grads)


def feed(early, scalars, fields, w_up, w_down, *got):
    whole, width = fields[0].shape
    hidden = w_up.shape[1] // 2
    rows = whole // 2
    half = 0 if early else 1
    low = jnp.bfloat16

    def across(i, *scalars):
        return (0, i)

    tokens = ((whole, width), low, (rows, width), lambda i, *scalars: (i, 0))
    turned = ((width, whole), low, (width, rows), across)
    if early:
        operands = [by_rows(field, rows) for field in fields[:3]] + [*fields[3:]]
        outs = [tokens, turned, tokens, turned]
        pieces = [((4, width, hidden // 2), low)]
    else:
        operands = [by_rows(fields[0], rows), (fields[1], (width, rows), across)]
        operands += [by_rows(fields[2], rows), (fields[3], (width, rows), across), by_rows(fields[4], rows)]
        outs = []
        pieces = [((width, hidden // 2), low)] * 4
    operands += [
        (w_up, (width, hidden), lambda i, *scalars: (0, half)),
        (w_down, (hidden, width), lambda i, *scalars: (half, 0)),
        *got,
    ]
    outs += [tokens, ((whole, hidden), low, (rows, hidden), lambda i, *scalars: (i, 0)), ((hidden, width), low)]
    sums = ((width, hidden), jnp.float32)
    return streamed(
        functools.partial(feed_kernel, early), 2, scalars, operands, outs + pieces, [((width, hidden), low), sums, sums], 17
    )


def lower_kernel(
    flags, act_early, act_late, rows_ref, own_ref, got_ref, cot_ref, early_ref, late_ref, keep_ref, first, second, sums_ref
):
    step = pl.program_id(0)
    total = dot(act_early[...], early_ref[...]) + dot(act_late[...], late_ref[...])
    cot = cot_ref[...].astype(jnp.float32)

    @pl.when(step == 0)
    def _():
        sums_ref[...] = jnp.zeros_like(sums_ref)

    send_or_keep(
        total,
        total + sum(ref[...].astype(jnp.float32) for ref in (rows_ref, own_ref, got_ref)),
        first,
        second,
        keep_ref,
    )
    mine = jnp.where(step < pl.num_programs(0) // 2, 0.0, 1.0)
    block = total + mine * sum(ref[...].astype(jnp.float32) for ref in (rows_ref, own_ref, got_ref))
    sums_ref[0:1, :] += jnp.sum(block * cot, axis=0, keepdims=True)


def send_or_keep(sent, kept, first, second, keep_ref):
    step = pl.program_id(0)
    for j, ref in enumerate((first, second)):

        @pl.when(step == j)
        def _():
            ref[...] = sent.astype(ref.dtype)

    @pl.when(step >= 2)
    def _():
        keep_ref[...] = kept


def theirs_first(i, flags, *more):
    return lax.rem((1 - flags[1]) * 2 + i, 4)


def sent_and_kept(whole, width):
    rows = whole // 4
    keep = ((2 * rows, width), jnp.float32, (rows, width), lambda i, *scalars: (jnp.maximum(i - 2, 0), 0))
    send = ((rows, width), jnp.bfloat16)
    return [keep, send, send, ((8, width), jnp.float32)]


def lower(flags, act_early, act_late, down_early, down_late, rows, own, got, cot):
    whole, width = rows.shape
    fields = [by_rows(field, whole // 4, theirs_first) for field in (act_early, act_late, rows, own, got, cot)]
    return streamed(
        lower_kernel, 4, [flags], fields + [down_early, down_late], sent_and_kept(whole, width), [], 6, SNUG
    )


def middle_kernel(
    flags, rows_ref, own_ref, got_ref, cot_ref, back_own, back_got, mixed_ref,
    vectors, w_ref, grad_ref, gmixed_ref, gout_ref, sums_ref, gout,
):
    step, last = pl.program_id(0), pl.num_programs(0) - 1
    unit, scale = norm_parts(sum(ref[...].astype(jnp.float32) for ref in (rows_ref, own_ref, got_ref)))
    back = sum(ref[...].astype(jnp.float32) for ref in (back_own, back_got))
    inner = back * vectors[2:3, :]
    mean = jnp.mean(inner, axis=-1, keepdims=True)
    slant = jnp.mean(inner * unit, axis=-1, keepdims=True)
    grad = cot_ref[...].astype(jnp.float32) + scale * (inner - mean - unit * slant)
    low = grad.astype(jnp.bfloat16)
    grad_ref[...] = low
    gmixed_ref[...] = dot(low, w_ref[...], NT).astype(jnp.bfloat16)
    part = dot(grad.T.astype(jnp.bfloat16), mixed_ref[...])

    @pl.when(step == 0)
    def _():
        gout[...] = part
        sums_ref[...] = jnp.zeros_like(sums_ref)

    @pl.when(step > 0)
    def _():
        gout[...] += part

    @pl.when(step == last)
    def _():
        gout_ref[...] = gout[...].astype(jnp.bfloat16)

    @pl.when(step // ((last + 1) // 2) == flags[1])
    def _():
        sums_ref[0:1, :] += jnp.sum(back * unit, axis=0, keepdims=True)
        sums_ref[1:2, :] += jnp.sum(back, axis=0, keepdims=True)


def middle(flags, fields, mixed, vectors, bundle):
    whole, width = fields[0].shape
    columns = mixed.shape[1]
    low = jnp.bfloat16
    in_order = lambda i, *scalars: (i, 0)
    return streamed(
        middle_kernel,
        whole // ROWS,
        [flags],
        [by_rows(field, ROWS) for field in (*fields, mixed)]
        + [vectors, (bundle, (columns, width), lambda i, *scalars: (0, 0))],
        [
            ((whole, width), low, (ROWS, width), in_order),
            ((whole, columns), low, (ROWS, columns), in_order),
            ((width, columns), low),
            ((8, width), jnp.float32),
        ],
        [((width, columns), jnp.float32)],
        8,
    )


def weigh_kernel(flags, turned_ref, out_grad_ref, grad_ref, *out_refs):
    last = grad_ref.shape[0]
    for j, out_ref in enumerate(out_refs):
        piece = 2 * (flags[2] ^ (j // 2)) + (flags[3] ^ (j % 2))

        @pl.when(piece < last)
        def _():
            out_ref[...] = dot(turned_ref[...], grad_ref[jnp.minimum(piece, last - 1)]).astype(jnp.bfloat16)

        @pl.when(piece == last)
        def _():
            out_ref[...] = out_grad_ref[...]


def weigh(flags, turned, grad, out_grad):
    width, columns = turned.shape[0], grad.shape[2]
    piece = ((width, columns), jnp.bfloat16, (ROWS, columns), lambda i, flags: (i, 0))
    return streamed(
        weigh_kernel, width // ROWS, [flags], [by_rows(turned, ROWS), by_rows(out_grad, ROWS), grad], [piece] * 4, [], 4
    )


def unproject_kernel(flags, grad_ref, rows_ref, weight, keep_ref, first, second, sums_ref):
    total = dot(grad_ref[0], weight[0], NT)
    for c in range(1, grad_ref.shape[0]):
        total = total + dot(grad_ref[c], weight[c], NT)
    unit, unused = norm_parts(rows_ref[...].astype(jnp.float32))

    @pl.when(pl.program_id(0) == 0)
    def _():
        sums_ref[...] = jnp.zeros_like(sums_ref)

    sums_ref[0:1, :] += jnp.sum(total * unit, axis=0, keepdims=True)
    sums_ref[1:2, :] += jnp.sum(total, axis=0, keepdims=True)
    send_or_keep(total, total, first, second, keep_ref)


def unproject(flags, grad, weight, rows):
    whole, width = rows.shape
    count, unused, columns = grad.shape
    grads = (grad, (count, whole // 4, columns), lambda i, flags: (0, theirs_first(i, flags), 0))
    fields = [grads, by_rows(rows, whole // 4, theirs_first), weight]
    return streamed(unproject_kernel, 4, [flags], fields, sent_and_kept(whole, width), [], 5, SNUG)


def last_kernel(flags, rows_ref, resid_ref, keep_ref, got_first, got_second, vectors, out_ref):
    unit, scale = norm_parts(rows_ref[...].astype(jnp.float32))
    got = jnp.where(pl.program_id(0) == 0, got_first[...], got_second[...]).astype(jnp.float32)
    inner = (keep_ref[...] + got) * vectors[0:1, :]
    mean = jnp.mean(inner, axis=-1, keepdims=True)
    slant = jnp.mean(inner * unit, axis=-1, keepdims=True)
    grad = resid_ref[...].astype(jnp.float32) + scale * (inner - mean - unit * slant)
    out_ref[...] = grad.astype(jnp.bfloat16)


def last(flags, rows, resid, keep, got, vectors):
    half, width = keep.shape
    size = half // 2

    def mine(i, flags):
        return flags[1] * 2 + i

    out = ((half, width), jnp.bfloat16, (size, width), lambda i, flags: (i, 0))
    fields = [by_rows(rows, size, mine), by_rows(resid, size, mine), by_rows(keep, size)]
    return streamed(last_kernel, 2, [flags], fields + [*got, vectors], [out], [], 3)[0]


def past_kernel(dwa_ref, hist_ref, cot_ref, grad_ref, part_ref, sums_ref):
    @pl.when(pl.program_id(0) == 0)
    def _():
        sums_ref[...] = jnp.zeros_like(sums_ref)

    grad = cot_ref[...].astype(jnp.float32)
    total = jnp.zeros_like(grad)
    for j in range(hist_ref.shape[0]):
        field = hist_ref[j].astype(jnp.float32)
        total += dwa_ref[j] * field
        grad_ref[j] = (dwa_ref[j] * grad).astype(jnp.bfloat16)
        sums_ref[j : j + 1, :] += jnp.sum(field * grad, axis=0, keepdims=True)
    part_ref[...] = total


def past(dwa, history, cot):
    count, rows, width = history.shape
    layers = pl.BlockSpec((count, ROWS, width), lambda i: (0, i, 0))
    tokens = pl.BlockSpec((ROWS, width), lambda i: (i, 0))
    return pl.pallas_call(
        past_kernel,
        grid=(rows // ROWS,),
        in_specs=[pl.BlockSpec(memory_space=pltpu.SMEM), layers, tokens],
        out_specs=[layers, tokens, whole_spec((8, width))],
        out_shape=[
            jax.ShapeDtypeStruct(history.shape, jnp.bfloat16),
            jax.ShapeDtypeStruct((rows, width), jnp.float32),
            jax.ShapeDtypeStruct((8, width), jnp.float32),
        ],
        compiler_params=pltpu.CompilerParams(vmem_limit_bytes=ROOM),
        cost_estimate=lasting(3),
    )(dwa, history, cot)


def present_kernel(flags, weight_ref, part_ref, grad_own, grad_got, block_own, block_got, out_ref, grad_ref):
    here = jnp.where(flags[0] == 1, block_own[...], block_got[...]).astype(jnp.float32)
    out_ref[...] = (part_ref[...] + weight_ref[weight_ref.shape[0] - 1] * here).astype(jnp.bfloat16)
    grad_ref[...] = jnp.where(flags[0] == 1, grad_own[...], grad_got[...])


def present(flags, weight, *fields):
    rows, width = fields[0].shape
    out = ((rows, width), jnp.bfloat16, (ROWS, width), lambda i, *scalars: (i, 0))
    fields = [by_rows(field, ROWS) for field in fields]
    return streamed(present_kernel, rows // ROWS, [flags, weight], fields, [out] * 2, [], 2, SNUG)


def place_kernel(flags, here_ref, there_ref, qkv_ref, out_ref, up_ref, down_ref):
    near, far = flags[1], flags[2]
    part = out_ref.shape[1]
    for k in range(2):
        for c in range(2):
            field = jnp.where(near == c, here_ref[k ^ far], there_ref[k ^ far]).astype(jnp.float32)
            if 2 * k + c < 3:
                qkv_ref[2 * k + c] = field[:, :part]
            else:
                out_ref[...] = field[:, :part]
            for half in range(2):
                at = (2 * half + k) * part
                (up_ref, down_ref)[c][:, at : at + part] = field[:, (1 + half) * part : (2 + half) * part]


def place(flags, here, there):
    rows, part = here.shape[1], here.shape[2] // 3
    outs = [((3, rows, part), jnp.float32), ((rows, part), jnp.float32)]
    outs += [((rows, 4 * part), jnp.float32)] * 2
    return streamed(place_kernel, 1, [flags], [here, there], outs, [], 3, SNUG)


AXES = ("tp", "dp", "far", "near")


def moves(chosen, move):
    sizes = [lax.axis_size(name) for name in AXES]
    places = [place for place in itertools.product(*map(range, sizes)) if chosen(*place)]
    index = lambda place: functools.reduce(lambda at, step: at * step[0] + step[1], zip(sizes, place), 0)
    return [(index(place), index(move(*place))) for place in places]


def away(t, d, k, c):
    return t != c


def anyone(t, d, k, c):
    return True


def swap_diagonal(field):
    return lax.ppermute(field, AXES, moves(away, lambda t, d, k, c: (c, d, k, t)))


def send_to_owner(field, other_far, other_tp):
    return lax.ppermute(
        field,
        AXES,
        moves(
            away if not other_far and not other_tp else anyone,
            lambda t, d, k, c: (c, d, k ^ other_far, t ^ other_tp),
        ),
    )


def swap_far_away(field):
    return lax.ppermute(field, AXES, moves(away, lambda t, d, k, c: (t, d, 1 - k, c)))


def swap_far(field):
    return lax.ppermute(field, "far", [(0, 1), (1, 0)])


def swap_near(field):
    return lax.ppermute(field, "near", [(0, 1), (1, 0)])


def after(field, *others):
    return lax.optimization_barrier((field, *others))[0]


def ordered(own, other, first, axis=0):
    return jnp.where(
        first, jnp.concatenate([own, other], axis=axis), jnp.concatenate([other, own], axis=axis)
    )


def part_of(field, index, axis):
    size = field.shape[axis] // 2
    return lax.dynamic_slice_in_dim(field, index * size, size, axis)


def add(*fields):
    return sum(field.astype(jnp.float32) for field in fields).astype(jnp.bfloat16)


def scatter_plane(pieces):
    return lax.psum_scatter(pieces, ("tp", "far"), scatter_dimension=0, tiled=True)[0]


def scatter_rows(piece):
    return lax.psum_scatter(piece, "dp", scatter_dimension=0, tiled=True)


def move_rows(block):
    dps = lax.axis_size("dp")
    if dps > 8:
        return [scatter_rows(block)]
    block = block.reshape(dps, block.shape[0] // dps, block.shape[1])
    place = lax.axis_index("dp")
    moved = [lax.dynamic_index_in_dim(block, place, 0, keepdims=False)]
    for step in range(1, dps):
        sent = lax.dynamic_index_in_dim(block, lax.rem(place + step, dps), 0, keepdims=False)
        moved.append(lax.ppermute(sent, "dp", [(d, (d + step) % dps) for d in range(dps)]))
    return moved


def sum_over(field, name):
    size = lax.axis_size(name)
    bit = 1
    while bit < size:
        field = field + lax.ppermute(field, name, [(d, d ^ bit) for d in range(size)])
        bit *= 2
    return field


def local(
    layer_input,
    history,
    cotangent,
    lengths,
    dwa_weights,
    gain_one,
    bias_one,
    w_qkv,
    w_out,
    gain_two,
    bias_two,
    w_up,
    w_down,
):
    rows = layer_input.shape[1]
    whole = rows * lax.axis_size("tp")
    hist_count = history.shape[0]
    part, far, near = lax.axis_index("tp"), lax.axis_index("far"), lax.axis_index("near")
    same = near == part
    flags = jnp.stack([same.astype(jnp.int32), near, far, part])

    input_got = swap_diagonal(layer_input[0])
    qkv_near = swap_diagonal(part_of(w_qkv, far, 1))
    qkv_far = swap_far_away(qkv_near)
    early_got = jnp.concatenate([part_of(w_up, 0, 1), part_of(w_down, 0, 0)], axis=0)
    late_up, late_down = part_of(w_up, 1, 1), part_of(w_down, 1, 0)
    last_own = jnp.concatenate([w_out, cotangent[0]], axis=0)
    vectors = jnp.stack([gain_one, bias_one, gain_two, bias_two])

    own_lengths = jnp.where(same, lengths, swap_near(lengths))[0]
    seq_owner, token_place = positions(own_lengths, whole)
    lane = jnp.arange(LANES, dtype=jnp.int32)
    member = seq_owner[:, None] == lane[None, :]
    apart = jnp.where(member | (lane >= lengths.shape[1])[None, :], 0.0, NEG_FILL).astype(jnp.bfloat16)
    member = member.astype(jnp.bfloat16)
    half_dim = HEAD_DIM // 2
    frequency = jnp.exp((lane % half_dim).astype(jnp.float32) * (-math.log(10000.0) / half_dim))
    angles = token_place.astype(jnp.float32)[:, None] * frequency[None, :]
    cos_table = jnp.cos(angles)
    sin_table = jnp.sin(angles) * jnp.where(lane % HEAD_DIM < half_dim, -1.0, 1.0)[None, :]
    grad_history, past_sum, sums_past = past(dwa_weights, history[:, 0], cotangent[0])

    input_half = jnp.where(same, layer_input[0], input_got)
    layer_rows = ordered(input_half, swap_near(input_half), near == 0)
    layer_rows, vectors, past_sum, cos_table, sin_table, apart, member = lax.optimization_barrier(
        (layer_rows, vectors, past_sum, cos_table, sin_table, apart, member)
    )
    early_got = swap_diagonal(after(early_got, input_got))
    last_got = swap_diagonal(after(last_own, input_got))
    projected, norm_one_t, weight_qkv = project(
        flags, layer_rows, vectors, cos_table, sin_table, w_qkv, qkv_near, qkv_far
    )
    mixed = attend(apart, member, projected, LONGEST)
    late_up = swap_diagonal(after(late_up, mixed))
    late_down = swap_diagonal(after(late_down, mixed))
    last_got = jnp.where(same, last_own, after(last_got, mixed))
    weight_out = last_got[: w_out.shape[0]]
    attn = jnp.dot(mixed, weight_out, preferred_element_type=jnp.float32).astype(jnp.bfloat16)
    attn_got = swap_near(attn)
    cot_half = last_got[w_out.shape[0] :]
    scalars = [flags, dwa_weights]
    fields = [layer_rows, attn, attn_got, cot_half, swap_near(cot_half), vectors]
    *kept, back, act_early, down_early, early_pieces = feed(True, scalars, fields, w_up, w_down, early_got)
    early_sum = scatter_plane(after(early_pieces, late_up, late_down))
    back, act_late, down_late, *late_owned = feed(
        False, [flags], [*kept, back], w_up, w_down, late_up, late_down
    )
    late_moved = [send_to_owner(late_owned[j], j // 2, j % 2) for j in range(4)]
    grad_down = kept[2]
    fields = [layer_rows, attn, attn_got, grad_down, back, swap_near(back)]
    grad_attn, grad_mixed, grad_out, sums_two = middle(flags, fields, mixed, vectors, last_got)
    grad_qkv = attend_back(apart, member, cos_table, sin_table, projected, grad_mixed, LONGEST)
    grad_qkv, *late_moved = lax.optimization_barrier((grad_qkv, *late_moved))
    owned = weigh(flags, norm_one_t, grad_qkv, grad_out)
    moved = [send_to_owner(owned[j], j // 2, j % 2) for j in range(4)]
    early_sum = scatter_rows(after(early_sum, grad_qkv))
    late_sum = scatter_rows(add(jnp.where(same, late_owned[0], after(late_moved[0], owned[0])), *late_moved[1:]))
    keep, *send, sums_one = unproject(flags, after(grad_qkv, owned[0]), weight_qkv, layer_rows)
    block_keep, *block_send, sums_now = lower(
        flags, act_early, act_late, down_early, down_late, layer_rows, attn, attn_got, after(grad_down, keep)
    )
    sent = [*send, *block_send]
    keep, block_keep, *arrived = lax.optimization_barrier((keep, block_keep, *sent, *moved))
    sent, moved = arrived[:4], arrived[4:]
    attn_one = add(jnp.where(same, owned[0], moved[0]), *moved[1:])
    attn_moved = move_rows(attn_one)
    got = [swap_near(field) for field in sent]
    block_half = add(block_keep, jnp.concatenate(got[2:], axis=0))
    block_moved = swap_diagonal(block_half)
    input_grad = last(flags, layer_rows, grad_attn, after(keep, attn_one), got[:2], vectors)
    early_sum = after(early_sum, attn_one)
    early_got = swap_diagonal(early_sum)
    small = jnp.concatenate([sums_one[:2], sums_two[:2], sums_now[:1], sums_past[:hist_count]], axis=0)
    small = after(small, input_grad)
    for name in ("tp", "far"):
        small = sum_over(small, name)
    small, input_grad, block_moved, late_sum, early_sum, early_got, *attn_moved = lax.optimization_barrier(
        (small, input_grad, block_moved, late_sum, early_sum, early_got, *attn_moved)
    )
    input_moved = swap_diagonal(input_grad)
    for name in ("near", "dp"):
        small = sum_over(small, name)
    attn_sum = add(*attn_moved)
    blocks = jnp.concatenate([attn_sum, jnp.where(same, early_sum, early_got), late_sum], axis=1)
    here = jnp.stack([blocks, swap_far(blocks)])
    output, grad_input = present(
        flags, dwa_weights, past_sum, input_grad, input_moved, block_half, block_moved
    )
    grad_w_qkv, grad_w_out, grad_w_up, grad_w_down = place(flags, here, swap_near(here))

    return (
        output[None],
        grad_input[None],
        grad_history[:, None],
        jnp.sum(jnp.concatenate([small[5:], small[4:5] / dwa_weights[hist_count]], axis=0), axis=1),
        small[0],
        small[1],
        grad_w_qkv,
        grad_w_out.T,
        small[2],
        small[3],
        grad_w_up,
        grad_w_down.T,
    )


def positions(seq_lengths, token_count):
    seq_ends = jnp.cumsum(seq_lengths)
    seq_starts = seq_ends - seq_lengths
    token_index = jnp.arange(token_count, dtype=jnp.int32)
    seq_owner = jnp.sum((token_index[:, None] >= seq_ends[None, :]).astype(jnp.int32), axis=1)
    picked = (
        seq_owner[:, None] == jnp.arange(seq_lengths.shape[0], dtype=jnp.int32)[None, :]
    ).astype(jnp.int32)
    seq_begin = jnp.sum(picked * seq_starts[None, :], axis=1)
    return (seq_owner, token_index - seq_begin)


def solution(mesh):
    tps, dps, reps = (mesh.shape[name] for name in ("tp", "dp", "rep"))
    split = Mesh(mesh.devices.reshape(tps, dps, reps // 2, 2), AXES)
    in_specs = (
        P(("dp", "far", "near"), "tp", None),
        P(None, ("dp", "far", "near"), "tp", None),
        P(("dp", "far", "near"), "tp", None),
        P(("dp", "far", "near"), None),
        P(),
        P(),
        P(),
        P(None, None, "tp"),
        P("tp", None),
        P(),
        P(),
        P(None, "tp"),
        P("tp", None),
    )
    out_specs = (
        P(("dp", "far", "near"), "tp", None),
        P(("dp", "far", "near"), "tp", None),
        P(None, ("dp", "far", "near"), "tp", None),
        P(),
        P(),
        P(),
        P(None, "dp", "tp"),
        P("tp", "dp"),
        P(),
        P(),
        P("dp", "tp"),
        P("tp", "dp"),
    )
    return jax.shard_map(local, mesh=split, in_specs=in_specs, out_specs=out_specs, check_vma=False)
```

```python
import functools
import itertools
import math

import jax
import jax.numpy as jnp
from jax import lax
from jax.experimental import pallas as pl
from jax.experimental.pallas import tpu as pltpu
from jax.sharding import Mesh, PartitionSpec as P

HEAD_DIM = 64
LONGEST = 512
NEG_FILL = -1e30
NORM_EPS = 1e-05
RATE = 3e6
ROOM = 60 << 20
SNUG = 18 << 20


def lasting(microseconds):
    return pl.CostEstimate(flops=0, transcendentals=0, bytes_accessed=int(microseconds * RATE))


BLOCK = 256
LANES = 128
NT = (((1,), (1,)), ((), ()))


def dot(a, b, dims=(((1,), (0,)), ((), ()))):
    return lax.dot_general(a, b, dims, preferred_element_type=jnp.float32)


def spans(whole, reach):
    back = -(-(reach - 1) // BLOCK)
    runs = []
    for i in range(whole // BLOCK):
        count = min(i, back) + 1
        if runs and runs[-1][2] == count:
            runs[-1][1] = i + 1
        else:
            runs.append([i, i + 1, count])
    return runs


def each_block(whole, reach, body):
    for first, last, count in spans(whole, reach):

        def step(i, carry, count=count):
            body(i, i + 1 - count, count)
            return carry

        lax.fori_loop(first, last, step, 0)


def block_at(i, count=1):
    return pl.ds(pl.multiple_of(i * BLOCK, BLOCK), count * BLOCK)


def head_query(q_ref, apart_ref, i, head):
    lane = lax.broadcasted_iota(jnp.int32, (BLOCK, LANES), 1) // HEAD_DIM
    query = q_ref[block_at(i), :] * (HEAD_DIM**-0.5)
    query = jnp.where(lane == head, query, jnp.zeros_like(query))
    return query, jnp.concatenate([query, apart_ref[block_at(i), :]], axis=1)


def attend_kernel(reach, apart_ref, member_ref, q_ref, k_ref, v_ref, out_ref, keys):
    whole = q_ref.shape[0]
    lane = lax.broadcasted_iota(jnp.int32, (BLOCK, LANES), 1) // HEAD_DIM
    keys[:, :LANES] = k_ref[...]
    keys[:, LANES:] = member_ref[...]

    def one(i, first, count, head):
        unused, query = head_query(q_ref, apart_ref, i, head)
        own = dot(query, keys[block_at(i), :], NT)
        key_at = lax.broadcasted_iota(jnp.int32, own.shape, 1)
        query_at = lax.broadcasted_iota(jnp.int32, own.shape, 0)
        scores = jnp.where(key_at <= query_at, own, NEG_FILL)
        if count > 1:
            scores = jnp.concatenate([dot(query, keys[block_at(first, count - 1), :], NT), scores], axis=1)
        exponent = jnp.exp(scores - jnp.max(scores, axis=1, keepdims=True))
        row_sum = jnp.sum(exponent, axis=1, keepdims=True)
        return dot(exponent.astype(jnp.bfloat16), v_ref[block_at(first, count), :]) * (1.0 / row_sum)

    def body(i, first, count):
        mixed = [one(i, first, count, head) for head in range(2)]
        out_ref[block_at(i), :] = jnp.where(lane == 0, *mixed).astype(out_ref.dtype)

    each_block(whole, reach, body)


def attend(apart, member, projected, reach):
    count, whole, width = projected.shape

    def block(c):
        return pl.BlockSpec((None, whole, LANES), lambda p: (c, 0, p))

    table = pl.BlockSpec((whole, LANES), lambda p: (0, 0))
    return pl.pallas_call(
        functools.partial(attend_kernel, reach),
        grid=(width // LANES,),
        in_specs=[table, table, block(0), block(1), block(2)],
        out_specs=pl.BlockSpec((whole, LANES), lambda p: (0, p)),
        out_shape=jax.ShapeDtypeStruct((whole, width), jnp.bfloat16),
        scratch_shapes=[pltpu.VMEM((whole, 2 * LANES), jnp.bfloat16)],
        compiler_params=pltpu.CompilerParams(vmem_limit_bytes=ROOM),
        cost_estimate=lasting(12),
    )(apart, member, projected, projected, projected)


def turn_back(field, cos, sin):
    half = HEAD_DIM // 2
    lane = lax.broadcasted_iota(jnp.int32, field.shape, 1) % HEAD_DIM
    crossed = jnp.where(lane < half, pltpu.roll(field, LANES - half, 1), pltpu.roll(field, half, 1))
    return field * cos - crossed * sin


def attend_back_kernel(
    reach, apart_ref, member_ref, cos_ref, sin_ref, q_ref, k_ref, v_ref, g_ref, out_ref, keys, keys_t, key_acc, value_acc
):
    whole = q_ref.shape[0]
    lane = lax.broadcasted_iota(jnp.int32, (BLOCK, LANES), 1) // HEAD_DIM
    keys[:, :LANES] = k_ref[...]
    keys[:, LANES:] = member_ref[...]
    keys_t[...] = k_ref[...].astype(jnp.float32).T.astype(jnp.bfloat16)
    key_acc[...] = jnp.zeros_like(key_acc)
    value_acc[...] = jnp.zeros_like(value_acc)

    def one(i, first, count, head):
        span = block_at(first, count)
        plain, query = head_query(q_ref, apart_ref, i, head)
        grad = g_ref[block_at(i), :]
        grad = jnp.where(lane == head, grad, jnp.zeros_like(grad))
        own = dot(keys[block_at(i), :], query, NT)
        key_at = lax.broadcasted_iota(jnp.int32, own.shape, 0)
        query_at = lax.broadcasted_iota(jnp.int32, own.shape, 1)
        scores = jnp.where(key_at <= query_at, own, NEG_FILL)
        if count > 1:
            scores = jnp.concatenate([dot(keys[block_at(first, count - 1), :], query, NT), scores], axis=0)
        exponent = jnp.exp(scores - jnp.max(scores, axis=0, keepdims=True))
        probs = exponent * (1.0 / jnp.sum(exponent, axis=0, keepdims=True))
        grad_values = dot(probs.astype(jnp.bfloat16), grad)
        weighted = probs * dot(v_ref[span, :], grad, NT)
        grad_scores = (weighted - probs * jnp.sum(weighted, axis=0, keepdims=True)).astype(jnp.bfloat16)
        here = dot(keys_t[:, span], grad_scores)
        return grad_values, dot(grad_scores, plain), here

    def body(i, first, count):
        span, at = block_at(first, count), block_at(i)
        values, keys_, queries = zip(*[one(i, first, count, head) for head in range(2)])
        value_acc[span, :] += values[0] + values[1]
        key_acc[span, :] += keys_[0] + keys_[1]
        row = lax.broadcasted_iota(jnp.int32, queries[0].shape, 0) // HEAD_DIM
        both = jnp.where(row == 0, *queries).T * (HEAD_DIM**-0.5)
        out_ref[0, at, :] = turn_back(both, cos_ref[at, :], sin_ref[at, :]).astype(out_ref.dtype)

    each_block(whole, reach, body)

    def finish(i, carry):
        at = block_at(i)
        out_ref[1, at, :] = turn_back(key_acc[at, :], cos_ref[at, :], sin_ref[at, :]).astype(out_ref.dtype)
        out_ref[2, at, :] = value_acc[at, :].astype(out_ref.dtype)
        return carry

    lax.fori_loop(0, whole // BLOCK, finish, 0)


def attend_back(apart, member, cos, sin, projected, grad_mixed, reach):
    count, whole, width = projected.shape

    def block(c):
        return pl.BlockSpec((None, whole, LANES), lambda p: (c, 0, p))

    table = pl.BlockSpec((whole, LANES), lambda p: (0, 0))
    return pl.pallas_call(
        functools.partial(attend_back_kernel, reach),
        grid=(width // LANES,),
        in_specs=[table] * 4 + [block(0), block(1), block(2), pl.BlockSpec((whole, LANES), lambda p: (0, p))],
        out_specs=pl.BlockSpec((count, whole, LANES), lambda p: (0, 0, p)),
        out_shape=jax.ShapeDtypeStruct((count, whole, width), jnp.bfloat16),
        scratch_shapes=[
            pltpu.VMEM((whole, 2 * LANES), jnp.bfloat16),
            pltpu.VMEM((LANES, whole), jnp.bfloat16),
            pltpu.VMEM((whole, LANES), jnp.float32),
            pltpu.VMEM((whole, LANES), jnp.float32),
        ],
        compiler_params=pltpu.CompilerParams(vmem_limit_bytes=ROOM),
        cost_estimate=lasting(22),
    )(apart, member, cos, sin, projected, projected, projected, grad_mixed)


ROWS = 256


def norm_parts(field):
    centered = field - jnp.mean(field, axis=-1, keepdims=True)
    scale = lax.rsqrt(jnp.mean(centered * centered, axis=-1, keepdims=True) + NORM_EPS)
    return centered * scale, scale


def wide(ref, at):
    return ref[at, :].astype(jnp.float32)


def row_blocks(count, body):
    def step(i, carry):
        body(i, pl.ds(pl.multiple_of(i * ROWS, ROWS), ROWS))
        return carry

    lax.fori_loop(0, count // ROWS, step, 0)


TALL = 512


def streamed(kernel, steps, scalars, fields, outs, scratch, microseconds, room=ROOM):
    def spec(shape, block=None, at=None):
        if block is None:
            return pl.BlockSpec(shape, lambda i, *scalars: (0,) * len(shape))
        return pl.BlockSpec(block, at)

    fields = [field if isinstance(field, tuple) else (field,) for field in fields]
    return pl.pallas_call(
        kernel,
        grid_spec=pltpu.PrefetchScalarGridSpec(
            num_scalar_prefetch=len(scalars),
            grid=(steps,),
            in_specs=[spec(field[0].shape, *field[1:]) for field in fields],
            out_specs=[spec(out[0], *out[2:]) for out in outs],
            scratch_shapes=[pltpu.VMEM(shape, dtype) for shape, dtype in scratch],
        ),
        out_shape=[jax.ShapeDtypeStruct(*out[:2]) for out in outs],
        compiler_params=pltpu.CompilerParams(vmem_limit_bytes=room),
        cost_estimate=lasting(microseconds),
    )(*scalars, *[field[0] for field in fields])


def by_rows(field, rows, shift=None):
    if shift is None:
        return field, (rows, field.shape[1]), lambda i, *scalars: (i, 0)
    return field, (rows, field.shape[1]), lambda i, *scalars: (shift(i, *scalars), 0)


def whole_spec(shape):
    return pl.BlockSpec(shape, lambda *at: (0,) * len(shape))


def turn(field, cos, sin):
    half = HEAD_DIM // 2
    lane = lax.broadcasted_iota(jnp.int32, field.shape, 1) % HEAD_DIM
    crossed = jnp.where(lane < half, pltpu.roll(field, LANES - half, 1), pltpu.roll(field, half, 1))
    return field * cos + crossed * sin


def project_kernel(flags, rows_ref, cos_ref, sin_ref, vectors, w_own, w_near, w_far, out_ref, turned_ref, weight_ref):
    @pl.when(pl.program_id(0) == 0)
    def _():
        half = w_near.shape[1]
        for index, got in ((flags[2], w_near), (1 - flags[2], w_far)):
            at = pl.ds(pl.multiple_of(index * half, half), half)
            weight_ref[:, at, :] = jnp.where(flags[0] == 1, w_own[:, at, :], got[...])

    unit, unused = norm_parts(rows_ref[...].astype(jnp.float32))
    norm = unit * vectors[0:1, :] + vectors[1:2, :]
    turned_ref[...] = norm.T.astype(jnp.bfloat16)
    norm = norm.astype(jnp.bfloat16)
    for c in range(weight_ref.shape[0]):
        field = dot(norm, weight_ref[c])
        if c == 2:
            out_ref[c] = field.astype(jnp.bfloat16)
        else:
            for p in range(field.shape[1] // LANES):
                lanes = slice(p * LANES, (p + 1) * LANES)
                out_ref[c, :, lanes] = turn(field[:, lanes], cos_ref[...], sin_ref[...]).astype(jnp.bfloat16)


def project(flags, rows, vectors, cos, sin, w_own, w_near, w_far):
    whole, width = rows.shape
    count, unused, columns = w_own.shape
    low = jnp.bfloat16
    return streamed(
        project_kernel,
        whole // ROWS,
        [flags],
        [by_rows(rows, ROWS), by_rows(cos, ROWS), by_rows(sin, ROWS), vectors, w_own, w_near, w_far],
        [
            ((count, whole, columns), low, (count, ROWS, columns), lambda i, flags: (0, i, 0)),
            ((width, whole), low, (width, ROWS), lambda i, flags: (0, i)),
            (w_own.shape, low),
        ],
        [],
        8,
    )


def gelu_both(up):
    root = math.sqrt(2.0 / math.pi)
    square = up * up
    bent = jnp.tanh(root * up * (1.0 + 0.044715 * square))
    half = 0.5 * (1.0 + bent)
    slope = half + 0.5 * up * (1.0 - bent * bent) * (root * (1.0 + 3.0 * 0.044715 * square))
    return up * half, slope


def feed_kernel(early, *refs):
    if early:
        flags, weight_ref, rows_ref, own_ref, got_ref, cot_here, cot_there, vectors, up_own, down_own, got = refs[:11]
        norm, norm_t, grad, grad_t, back_ref, act_ref, down_ref, pieces = refs[11:19]
        up_got, down_got = got.at[: norm.shape[1]], got.at[norm.shape[1] :]
    else:
        flags, norm, norm_t, grad, grad_t, back_early, up_own, down_own, up_got, down_got = refs[:10]
        back_ref, act_ref, down_ref, *pieces = refs[10:17]
    up_w, up_sum, down_sum = refs[-3:]
    part = up_w.shape[1] // 2
    step, last = pl.program_id(0), pl.num_programs(0) - 1

    @pl.when(step == 0)
    def _():
        up_w[...] = jnp.where(flags[0] == 1, up_own[...], up_got[...])
        down_ref[...] = jnp.where(flags[0] == 1, down_own[...], down_got[...])

    if early:

        def head(i, at):
            unit, unused = norm_parts(wide(rows_ref, at) + wide(own_ref, at) + wide(got_ref, at))
            field = unit * vectors[2:3, :] + vectors[3:4, :]
            norm[at, :] = field.astype(jnp.bfloat16)
            norm_t[:, at] = field.T.astype(jnp.bfloat16)
            cot = jnp.where(flags[1] == step, cot_here[at, :], cot_there[at, :])
            field = cot.astype(jnp.float32) * weight_ref[weight_ref.shape[0] - 1]
            grad[at, :] = field.astype(jnp.bfloat16)
            grad_t[:, at] = field.T.astype(jnp.bfloat16)

        row_blocks(norm.shape[0], head)
    value, rise = gelu_both(dot(norm[...], up_w[...]))
    act_ref[...] = value.astype(jnp.bfloat16)
    slope = (dot(grad[...], down_ref[...], NT) * rise).astype(jnp.bfloat16)
    back = dot(slope, up_w[...], NT)
    if not early:
        back = back + back_early[...].astype(jnp.float32)
    back_ref[...] = back.astype(jnp.bfloat16)

    def store(p, at, low):
        if early:
            pieces[p, at, :] = low
            return
        slot = 2 * (flags[2] ^ (p % 2)) + (flags[3] ^ (p // 2))
        for j, piece in enumerate(pieces):

            @pl.when(slot == j)
            def _():
                piece[at, :] = low

    def grads(i, at):
        fields = (dot(norm_t[at, :], slope), dot(grad_t[at, :], act_ref[...]))
        for k, (field, total) in enumerate(zip(fields, (up_sum, down_sum))):

            @pl.when(step == 0)
            def _():
                total[at, :] = field

            @pl.when(step == last)
            def _():
                low = (total[at, :] + field).astype(jnp.bfloat16)
                for p in range(2):
                    store(2 * k + p, at, low[:, p * part : (p + 1) * part])

    row_blocks(norm_t.shape[0], grads)


def feed(early, scalars, fields, w_up, w_down, *got):
    whole, width = fields[0].shape
    hidden = w_up.shape[1] // 2
    rows = whole // 2
    half = 0 if early else 1
    low = jnp.bfloat16

    def across(i, *scalars):
        return (0, i)

    tokens = ((whole, width), low, (rows, width), lambda i, *scalars: (i, 0))
    turned = ((width, whole), low, (width, rows), across)
    if early:
        operands = [by_rows(field, rows) for field in fields[:3]] + [*fields[3:]]
        outs = [tokens, turned, tokens, turned]
        pieces = [((4, width, hidden // 2), low)]
    else:
        operands = [by_rows(fields[0], rows), (fields[1], (width, rows), across)]
        operands += [by_rows(fields[2], rows), (fields[3], (width, rows), across), by_rows(fields[4], rows)]
        outs = []
        pieces = [((width, hidden // 2), low)] * 4
    operands += [
        (w_up, (width, hidden), lambda i, *scalars: (0, half)),
        (w_down, (hidden, width), lambda i, *scalars: (half, 0)),
        *got,
    ]
    outs += [tokens, ((whole, hidden), low, (rows, hidden), lambda i, *scalars: (i, 0)), ((hidden, width), low)]
    sums = ((width, hidden), jnp.float32)
    return streamed(
        functools.partial(feed_kernel, early), 2, scalars, operands, outs + pieces, [((width, hidden), low), sums, sums], 17
    )


def lower_kernel(
    flags, act_early, act_late, rows_ref, own_ref, got_ref, cot_ref, early_ref, late_ref, keep_ref, first, second, sums_ref
):
    step = pl.program_id(0)
    total = dot(act_early[...], early_ref[...]) + dot(act_late[...], late_ref[...])
    cot = cot_ref[...].astype(jnp.float32)

    @pl.when(step == 0)
    def _():
        sums_ref[...] = jnp.zeros_like(sums_ref)

    send_or_keep(
        total,
        total + sum(ref[...].astype(jnp.float32) for ref in (rows_ref, own_ref, got_ref)),
        first,
        second,
        keep_ref,
    )
    mine = jnp.where(step < pl.num_programs(0) // 2, 0.0, 1.0)
    block = total + mine * sum(ref[...].astype(jnp.float32) for ref in (rows_ref, own_ref, got_ref))
    sums_ref[0:1, :] += jnp.sum(block * cot, axis=0, keepdims=True)


def send_or_keep(sent, kept, first, second, keep_ref):
    step = pl.program_id(0)
    for j, ref in enumerate((first, second)):

        @pl.when(step == j)
        def _():
            ref[...] = sent.astype(ref.dtype)

    @pl.when(step >= 2)
    def _():
        keep_ref[...] = kept


def theirs_first(i, flags, *more):
    return lax.rem((1 - flags[1]) * 2 + i, 4)


def sent_and_kept(whole, width):
    rows = whole // 4
    keep = ((2 * rows, width), jnp.float32, (rows, width), lambda i, *scalars: (jnp.maximum(i - 2, 0), 0))
    send = ((rows, width), jnp.bfloat16)
    return [keep, send, send, ((8, width), jnp.float32)]


def lower(flags, act_early, act_late, down_early, down_late, rows, own, got, cot):
    whole, width = rows.shape
    fields = [by_rows(field, whole // 4, theirs_first) for field in (act_early, act_late, rows, own, got, cot)]
    return streamed(
        lower_kernel, 4, [flags], fields + [down_early, down_late], sent_and_kept(whole, width), [], 6, SNUG
    )


def middle_kernel(
    flags, rows_ref, own_ref, got_ref, cot_ref, back_own, back_got, mixed_ref,
    vectors, w_ref, grad_ref, gmixed_ref, gout_ref, sums_ref, gout,
):
    step, last = pl.program_id(0), pl.num_programs(0) - 1
    unit, scale = norm_parts(sum(ref[...].astype(jnp.float32) for ref in (rows_ref, own_ref, got_ref)))
    back = sum(ref[...].astype(jnp.float32) for ref in (back_own, back_got))
    inner = back * vectors[2:3, :]
    mean = jnp.mean(inner, axis=-1, keepdims=True)
    slant = jnp.mean(inner * unit, axis=-1, keepdims=True)
    grad = cot_ref[...].astype(jnp.float32) + scale * (inner - mean - unit * slant)
    low = grad.astype(jnp.bfloat16)
    grad_ref[...] = low
    gmixed_ref[...] = dot(low, w_ref[...], NT).astype(jnp.bfloat16)
    part = dot(grad.T.astype(jnp.bfloat16), mixed_ref[...])

    @pl.when(step == 0)
    def _():
        gout[...] = part
        sums_ref[...] = jnp.zeros_like(sums_ref)

    @pl.when(step > 0)
    def _():
        gout[...] += part

    @pl.when(step == last)
    def _():
        gout_ref[...] = gout[...].astype(jnp.bfloat16)

    @pl.when(step // ((last + 1) // 2) == flags[1])
    def _():
        sums_ref[0:1, :] += jnp.sum(back * unit, axis=0, keepdims=True)
        sums_ref[1:2, :] += jnp.sum(back, axis=0, keepdims=True)


def middle(flags, fields, mixed, vectors, bundle):
    whole, width = fields[0].shape
    columns = mixed.shape[1]
    low = jnp.bfloat16
    in_order = lambda i, *scalars: (i, 0)
    return streamed(
        middle_kernel,
        whole // ROWS,
        [flags],
        [by_rows(field, ROWS) for field in (*fields, mixed)]
        + [vectors, (bundle, (columns, width), lambda i, *scalars: (0, 0))],
        [
            ((whole, width), low, (ROWS, width), in_order),
            ((whole, columns), low, (ROWS, columns), in_order),
            ((width, columns), low),
            ((8, width), jnp.float32),
        ],
        [((width, columns), jnp.float32)],
        8,
    )


def weigh_kernel(flags, turned_ref, out_grad_ref, grad_ref, *out_refs):
    last = grad_ref.shape[0]
    for j, out_ref in enumerate(out_refs):
        piece = 2 * (flags[2] ^ (j // 2)) + (flags[3] ^ (j % 2))

        @pl.when(piece < last)
        def _():
            out_ref[...] = dot(turned_ref[...], grad_ref[jnp.minimum(piece, last - 1)]).astype(jnp.bfloat16)

        @pl.when(piece == last)
        def _():
            out_ref[...] = out_grad_ref[...]


def weigh(flags, turned, grad, out_grad):
    width, columns = turned.shape[0], grad.shape[2]
    piece = ((width, columns), jnp.bfloat16, (ROWS, columns), lambda i, flags: (i, 0))
    return streamed(
        weigh_kernel, width // ROWS, [flags], [by_rows(turned, ROWS), by_rows(out_grad, ROWS), grad], [piece] * 4, [], 4
    )


def unproject_kernel(flags, grad_ref, rows_ref, weight, keep_ref, first, second, sums_ref):
    total = dot(grad_ref[0], weight[0], NT)
    for c in range(1, grad_ref.shape[0]):
        total = total + dot(grad_ref[c], weight[c], NT)
    unit, unused = norm_parts(rows_ref[...].astype(jnp.float32))

    @pl.when(pl.program_id(0) == 0)
    def _():
        sums_ref[...] = jnp.zeros_like(sums_ref)

    sums_ref[0:1, :] += jnp.sum(total * unit, axis=0, keepdims=True)
    sums_ref[1:2, :] += jnp.sum(total, axis=0, keepdims=True)
    send_or_keep(total, total, first, second, keep_ref)


def unproject(flags, grad, weight, rows):
    whole, width = rows.shape
    count, unused, columns = grad.shape
    grads = (grad, (count, whole // 4, columns), lambda i, flags: (0, theirs_first(i, flags), 0))
    fields = [grads, by_rows(rows, whole // 4, theirs_first), weight]
    return streamed(unproject_kernel, 4, [flags], fields, sent_and_kept(whole, width), [], 5, SNUG)


def last_kernel(
    flags, rows_ref, resid_ref, keep_ref, block_keep, got_first, got_second, block_first, block_second, vectors, out_ref
):
    first = pl.program_id(0) == 0
    unit, scale = norm_parts(rows_ref[...].astype(jnp.float32))
    got = jnp.where(first, got_first[...], got_second[...]).astype(jnp.float32)
    inner = (keep_ref[...] + got) * vectors[0:1, :]
    mean = jnp.mean(inner, axis=-1, keepdims=True)
    slant = jnp.mean(inner * unit, axis=-1, keepdims=True)
    grad = resid_ref[...].astype(jnp.float32) + scale * (inner - mean - unit * slant)
    out_ref[0] = grad.astype(jnp.bfloat16)
    got = jnp.where(first, block_first[...], block_second[...]).astype(jnp.float32)
    out_ref[1] = (block_keep[...] + got).astype(jnp.bfloat16)


def last(flags, rows, resid, keep, block_keep, got, vectors):
    half, width = keep.shape
    size = half // 2

    def mine(i, flags):
        return flags[1] * 2 + i

    out = ((2, half, width), jnp.bfloat16, (2, size, width), lambda i, flags: (0, i, 0))
    fields = [by_rows(rows, size, mine), by_rows(resid, size, mine), by_rows(keep, size), by_rows(block_keep, size)]
    return streamed(last_kernel, 2, [flags], fields + [*got, vectors], [out], [], 3)[0]


def past_kernel(dwa_ref, hist_ref, cot_ref, grad_ref, part_ref, sums_ref):
    @pl.when(pl.program_id(0) == 0)
    def _():
        sums_ref[...] = jnp.zeros_like(sums_ref)

    grad = cot_ref[...].astype(jnp.float32)
    total = jnp.zeros_like(grad)
    for j in range(hist_ref.shape[0]):
        field = hist_ref[j].astype(jnp.float32)
        total += dwa_ref[j] * field
        grad_ref[j] = (dwa_ref[j] * grad).astype(jnp.bfloat16)
        sums_ref[j : j + 1, :] += jnp.sum(field * grad, axis=0, keepdims=True)
    part_ref[...] = total


def past(dwa, history, cot):
    count, rows, width = history.shape
    layers = pl.BlockSpec((count, ROWS, width), lambda i: (0, i, 0))
    tokens = pl.BlockSpec((ROWS, width), lambda i: (i, 0))
    return pl.pallas_call(
        past_kernel,
        grid=(rows // ROWS,),
        in_specs=[pl.BlockSpec(memory_space=pltpu.SMEM), layers, tokens],
        out_specs=[layers, tokens, whole_spec((8, width))],
        out_shape=[
            jax.ShapeDtypeStruct(history.shape, jnp.bfloat16),
            jax.ShapeDtypeStruct((rows, width), jnp.float32),
            jax.ShapeDtypeStruct((8, width), jnp.float32),
        ],
        compiler_params=pltpu.CompilerParams(vmem_limit_bytes=ROOM),
        cost_estimate=lasting(3),
    )(dwa, history, cot)


def present_kernel(flags, weight_ref, part_ref, own_ref, got_ref, out_ref, grad_ref):
    here = jnp.where(flags[0] == 1, own_ref[1], got_ref[1]).astype(jnp.float32)
    out_ref[...] = (part_ref[...] + weight_ref[weight_ref.shape[0] - 1] * here).astype(jnp.bfloat16)
    grad_ref[...] = jnp.where(flags[0] == 1, own_ref[0], got_ref[0])


def present(flags, weight, part, own, got):
    rows, width = part.shape
    both = (2, ROWS, width), lambda i, *scalars: (0, i, 0)
    out = ((rows, width), jnp.bfloat16, (ROWS, width), lambda i, *scalars: (i, 0))
    fields = [by_rows(part, ROWS), (own, *both), (got, *both)]
    return streamed(present_kernel, rows // ROWS, [flags, weight], fields, [out] * 2, [], 2, SNUG)


def place_kernel(flags, here_ref, there_ref, qkv_ref, out_ref, up_ref, down_ref):
    near, far = flags[1], flags[2]
    part = out_ref.shape[1]
    for k in range(2):
        for c in range(2):
            field = jnp.where(near == c, here_ref[k ^ far], there_ref[k ^ far]).astype(jnp.float32)
            if 2 * k + c < 3:
                qkv_ref[2 * k + c] = field[:, :part]
            else:
                out_ref[...] = field[:, :part]
            for half in range(2):
                at = (2 * half + k) * part
                (up_ref, down_ref)[c][:, at : at + part] = field[:, (1 + half) * part : (2 + half) * part]


def place(flags, here, there):
    rows, part = here.shape[1], here.shape[2] // 3
    outs = [((3, rows, part), jnp.float32), ((rows, part), jnp.float32)]
    outs += [((rows, 4 * part), jnp.float32)] * 2
    return streamed(place_kernel, 1, [flags], [here, there], outs, [], 3, SNUG)


AXES = ("tp", "dp", "far", "near")


def moves(chosen, move):
    sizes = [lax.axis_size(name) for name in AXES]
    places = [place for place in itertools.product(*map(range, sizes)) if chosen(*place)]
    index = lambda place: functools.reduce(lambda at, step: at * step[0] + step[1], zip(sizes, place), 0)
    return [(index(place), index(move(*place))) for place in places]


def away(t, d, k, c):
    return t != c


def anyone(t, d, k, c):
    return True


def swap_diagonal(field):
    return lax.ppermute(field, AXES, moves(away, lambda t, d, k, c: (c, d, k, t)))


def send_to_owner(field, other_far, other_tp):
    return lax.ppermute(
        field,
        AXES,
        moves(
            away if not other_far and not other_tp else anyone,
            lambda t, d, k, c: (c, d, k ^ other_far, t ^ other_tp),
        ),
    )


def swap_far_away(field):
    return lax.ppermute(field, AXES, moves(away, lambda t, d, k, c: (t, d, 1 - k, c)))


def swap_far(field):
    return lax.ppermute(field, "far", [(0, 1), (1, 0)])


def swap_near(field):
    return lax.ppermute(field, "near", [(0, 1), (1, 0)])


def after(field, *others):
    return lax.optimization_barrier((field, *others))[0]


def ordered(own, other, first, axis=0):
    return jnp.where(
        first, jnp.concatenate([own, other], axis=axis), jnp.concatenate([other, own], axis=axis)
    )


def part_of(field, index, axis):
    size = field.shape[axis] // 2
    return lax.dynamic_slice_in_dim(field, index * size, size, axis)


def add(*fields):
    return sum(field.astype(jnp.float32) for field in fields).astype(jnp.bfloat16)


def scatter_plane(pieces):
    return lax.psum_scatter(pieces, ("tp", "far"), scatter_dimension=0, tiled=True)[0]


def scatter_rows(piece):
    return lax.psum_scatter(piece, "dp", scatter_dimension=0, tiled=True)


def move_rows(block):
    dps = lax.axis_size("dp")
    if dps > 8:
        return [scatter_rows(block)]
    block = block.reshape(dps, block.shape[0] // dps, block.shape[1])
    place = lax.axis_index("dp")
    moved = [lax.dynamic_index_in_dim(block, place, 0, keepdims=False)]
    for step in range(1, dps):
        sent = lax.dynamic_index_in_dim(block, lax.rem(place + step, dps), 0, keepdims=False)
        moved.append(lax.ppermute(sent, "dp", [(d, (d + step) % dps) for d in range(dps)]))
    return moved


def sum_over(field, name):
    size = lax.axis_size(name)
    bit = 1
    while bit < size:
        field = field + lax.ppermute(field, name, [(d, d ^ bit) for d in range(size)])
        bit *= 2
    return field


def local(
    layer_input,
    history,
    cotangent,
    lengths,
    dwa_weights,
    gain_one,
    bias_one,
    w_qkv,
    w_out,
    gain_two,
    bias_two,
    w_up,
    w_down,
):
    rows = layer_input.shape[1]
    whole = rows * lax.axis_size("tp")
    hist_count = history.shape[0]
    part, far, near = lax.axis_index("tp"), lax.axis_index("far"), lax.axis_index("near")
    same = near == part
    flags = jnp.stack([same.astype(jnp.int32), near, far, part])

    input_got = swap_diagonal(layer_input[0])
    qkv_near = swap_diagonal(part_of(w_qkv, far, 1))
    qkv_far = swap_far_away(qkv_near)
    early_got = jnp.concatenate([part_of(w_up, 0, 1), part_of(w_down, 0, 0)], axis=0)
    late_up, late_down = part_of(w_up, 1, 1), part_of(w_down, 1, 0)
    last_own = jnp.concatenate([w_out, cotangent[0]], axis=0)
    vectors = jnp.stack([gain_one, bias_one, gain_two, bias_two])

    own_lengths = jnp.where(same, lengths, swap_near(lengths))[0]
    seq_owner, token_place = positions(own_lengths, whole)
    lane = jnp.arange(LANES, dtype=jnp.int32)
    member = seq_owner[:, None] == lane[None, :]
    apart = jnp.where(member | (lane >= lengths.shape[1])[None, :], 0.0, NEG_FILL).astype(jnp.bfloat16)
    member = member.astype(jnp.bfloat16)
    half_dim = HEAD_DIM // 2
    frequency = jnp.exp((lane % half_dim).astype(jnp.float32) * (-math.log(10000.0) / half_dim))
    angles = token_place.astype(jnp.float32)[:, None] * frequency[None, :]
    cos_table = jnp.cos(angles)
    sin_table = jnp.sin(angles) * jnp.where(lane % HEAD_DIM < half_dim, -1.0, 1.0)[None, :]
    grad_history, past_sum, sums_past = past(dwa_weights, history[:, 0], cotangent[0])

    input_half = jnp.where(same, layer_input[0], input_got)
    layer_rows = ordered(input_half, swap_near(input_half), near == 0)
    layer_rows, vectors, past_sum, cos_table, sin_table, apart, member = lax.optimization_barrier(
        (layer_rows, vectors, past_sum, cos_table, sin_table, apart, member)
    )
    early_got = swap_diagonal(after(early_got, input_got))
    last_got = swap_diagonal(after(last_own, input_got))
    projected, norm_one_t, weight_qkv = project(
        flags, layer_rows, vectors, cos_table, sin_table, w_qkv, qkv_near, qkv_far
    )
    mixed = attend(apart, member, projected, LONGEST)
    late_up = swap_diagonal(after(late_up, mixed))
    late_down = swap_diagonal(after(late_down, mixed))
    last_got = jnp.where(same, last_own, after(last_got, mixed))
    weight_out = last_got[: w_out.shape[0]]
    attn = jnp.dot(mixed, weight_out, preferred_element_type=jnp.float32).astype(jnp.bfloat16)
    attn_got = swap_near(attn)
    cot_half = last_got[w_out.shape[0] :]
    scalars = [flags, dwa_weights]
    fields = [layer_rows, attn, attn_got, cot_half, swap_near(cot_half), vectors]
    *kept, back, act_early, down_early, early_pieces = feed(True, scalars, fields, w_up, w_down, early_got)
    early_sum = scatter_plane(after(early_pieces, late_up, late_down))
    back, act_late, down_late, *late_owned = feed(
        False, [flags], [*kept, back], w_up, w_down, late_up, late_down
    )
    late_moved = [send_to_owner(late_owned[j], j // 2, j % 2) for j in range(4)]
    grad_down = kept[2]
    fields = [layer_rows, attn, attn_got, grad_down, back, swap_near(back)]
    grad_attn, grad_mixed, grad_out, sums_two = middle(flags, fields, mixed, vectors, last_got)
    grad_qkv = attend_back(apart, member, cos_table, sin_table, projected, grad_mixed, LONGEST)
    grad_qkv, *late_moved = lax.optimization_barrier((grad_qkv, *late_moved))
    owned = weigh(flags, norm_one_t, grad_qkv, grad_out)
    moved = [send_to_owner(owned[j], j // 2, j % 2) for j in range(4)]
    early_sum = scatter_rows(after(early_sum, grad_qkv))
    late_sum = scatter_rows(add(jnp.where(same, late_owned[0], after(late_moved[0], owned[0])), *late_moved[1:]))
    keep, *send, sums_one = unproject(flags, after(grad_qkv, owned[0]), weight_qkv, layer_rows)
    block_keep, *block_send, sums_now = lower(
        flags, act_early, act_late, down_early, down_late, layer_rows, attn, attn_got, after(grad_down, keep)
    )
    sent = [*send, *block_send]
    keep, block_keep, *arrived = lax.optimization_barrier((keep, block_keep, *sent, *moved))
    sent, moved = arrived[:4], arrived[4:]
    attn_one = add(jnp.where(same, owned[0], moved[0]), *moved[1:])
    attn_moved = move_rows(attn_one)
    got = [swap_near(field) for field in sent]
    ours = last(flags, layer_rows, grad_attn, after(keep, attn_one), block_keep, got, vectors)
    early_sum = after(early_sum, attn_one)
    early_got = swap_diagonal(early_sum)
    small = jnp.concatenate([sums_one[:2], sums_two[:2], sums_now[:1], sums_past[:hist_count]], axis=0)
    small = after(small, ours)
    for name in ("near", "tp", "far"):
        small = sum_over(small, name)
    small, ours, late_sum, early_sum, early_got, *attn_moved = lax.optimization_barrier(
        (small, ours, late_sum, early_sum, early_got, *attn_moved)
    )
    theirs = swap_diagonal(ours)
    small = sum_over(small, "dp")
    attn_sum = add(*attn_moved)
    blocks = jnp.concatenate([attn_sum, jnp.where(same, early_sum, early_got), late_sum], axis=1)
    here = jnp.stack([blocks, swap_far(blocks)])
    output, grad_input = present(flags, dwa_weights, past_sum, ours, theirs)
    grad_w_qkv, grad_w_out, grad_w_up, grad_w_down = place(flags, here, swap_near(here))

    return (
        output[None],
        grad_input[None],
        grad_history[:, None],
        jnp.sum(jnp.concatenate([small[5:], small[4:5] / dwa_weights[hist_count]], axis=0), axis=1),
        small[0],
        small[1],
        grad_w_qkv,
        grad_w_out.T,
        small[2],
        small[3],
        grad_w_up,
        grad_w_down.T,
    )


def positions(seq_lengths, token_count):
    seq_ends = jnp.cumsum(seq_lengths)
    seq_starts = seq_ends - seq_lengths
    token_index = jnp.arange(token_count, dtype=jnp.int32)
    seq_owner = jnp.sum((token_index[:, None] >= seq_ends[None, :]).astype(jnp.int32), axis=1)
    picked = (
        seq_owner[:, None] == jnp.arange(seq_lengths.shape[0], dtype=jnp.int32)[None, :]
    ).astype(jnp.int32)
    seq_begin = jnp.sum(picked * seq_starts[None, :], axis=1)
    return (seq_owner, token_index - seq_begin)


def solution(mesh):
    tps, dps, reps = (mesh.shape[name] for name in ("tp", "dp", "rep"))
    split = Mesh(mesh.devices.reshape(tps, dps, reps // 2, 2), AXES)
    in_specs = (
        P(("dp", "far", "near"), "tp", None),
        P(None, ("dp", "far", "near"), "tp", None),
        P(("dp", "far", "near"), "tp", None),
        P(("dp", "far", "near"), None),
        P(),
        P(),
        P(),
        P(None, None, "tp"),
        P("tp", None),
        P(),
        P(),
        P(None, "tp"),
        P("tp", None),
    )
    out_specs = (
        P(("dp", "far", "near"), "tp", None),
        P(("dp", "far", "near"), "tp", None),
        P(None, ("dp", "far", "near"), "tp", None),
        P(),
        P(),
        P(),
        P(None, "dp", "tp"),
        P("tp", "dp"),
        P(),
        P(),
        P("dp", "tp"),
        P("tp", "dp"),
    )
    return jax.shard_map(local, mesh=split, in_specs=in_specs, out_specs=out_specs, check_vma=False)
```

```python
import functools
import itertools
import math

import jax
import jax.numpy as jnp
from jax import lax
from jax.experimental import pallas as pl
from jax.experimental.pallas import tpu as pltpu
from jax.sharding import Mesh, PartitionSpec as P

HEAD_DIM = 64
LONGEST = 512
NEG_FILL = -1e30
NORM_EPS = 1e-05
RATE = 3e6
ROOM = 60 << 20
SNUG = 18 << 20


def lasting(microseconds):
    return pl.CostEstimate(flops=0, transcendentals=0, bytes_accessed=int(microseconds * RATE))


BLOCK = 256
LANES = 128
NT = (((1,), (1,)), ((), ()))


def dot(a, b, dims=(((1,), (0,)), ((), ()))):
    return lax.dot_general(a, b, dims, preferred_element_type=jnp.float32)


def spans(whole, reach):
    back = -(-(reach - 1) // BLOCK)
    runs = []
    for i in range(whole // BLOCK):
        count = min(i, back) + 1
        if runs and runs[-1][2] == count:
            runs[-1][1] = i + 1
        else:
            runs.append([i, i + 1, count])
    return runs


def each_block(whole, reach, body):
    for first, last, count in spans(whole, reach):

        def step(i, carry, count=count):
            body(i, i + 1 - count, count)
            return carry

        lax.fori_loop(first, last, step, 0)


def block_at(i, count=1):
    return pl.ds(pl.multiple_of(i * BLOCK, BLOCK), count * BLOCK)


def head_query(q_ref, apart_ref, i, head):
    lane = lax.broadcasted_iota(jnp.int32, (BLOCK, LANES), 1) // HEAD_DIM
    query = q_ref[block_at(i), :] * (HEAD_DIM**-0.5)
    query = jnp.where(lane == head, query, jnp.zeros_like(query))
    return query, jnp.concatenate([query, apart_ref[block_at(i), :]], axis=1)


def attend_kernel(reach, apart_ref, member_ref, q_ref, k_ref, v_ref, out_ref, logs_ref, keys):
    whole = q_ref.shape[0]
    lane = lax.broadcasted_iota(jnp.int32, (BLOCK, LANES), 1) // HEAD_DIM
    keys[:, :LANES] = k_ref[...]
    keys[:, LANES:] = member_ref[...]

    def one(i, first, count, head):
        unused, query = head_query(q_ref, apart_ref, i, head)
        own = dot(query, keys[block_at(i), :], NT)
        key_at = lax.broadcasted_iota(jnp.int32, own.shape, 1)
        query_at = lax.broadcasted_iota(jnp.int32, own.shape, 0)
        scores = jnp.where(key_at <= query_at, own, NEG_FILL)
        if count > 1:
            scores = jnp.concatenate([dot(query, keys[block_at(first, count - 1), :], NT), scores], axis=1)
        row_max = jnp.max(scores, axis=1, keepdims=True)
        exponent = jnp.exp(scores - row_max)
        row_sum = jnp.sum(exponent, axis=1, keepdims=True)
        mixed = dot(exponent.astype(jnp.bfloat16), v_ref[block_at(first, count), :]) * (1.0 / row_sum)
        return mixed, row_max + jnp.log(row_sum)

    def body(i, first, count):
        mixed, logs = zip(*[one(i, first, count, head) for head in range(2)])
        out_ref[block_at(i), :] = jnp.where(lane == 0, *mixed).astype(out_ref.dtype)
        turned = jnp.where(lane == 0, *logs).T
        for head in range(2):
            logs_ref[head : head + 1, block_at(i)] = turned[head * HEAD_DIM : head * HEAD_DIM + 1]

    each_block(whole, reach, body)


def attend(apart, member, projected, reach):
    count, whole, width = projected.shape

    def block(c):
        return pl.BlockSpec((None, whole, LANES), lambda p: (c, 0, p))

    table = pl.BlockSpec((whole, LANES), lambda p: (0, 0))
    return pl.pallas_call(
        functools.partial(attend_kernel, reach),
        grid=(width // LANES,),
        in_specs=[table, table, block(0), block(1), block(2)],
        out_specs=[
            pl.BlockSpec((whole, LANES), lambda p: (0, p)),
            pl.BlockSpec((None, 8, whole), lambda p: (p, 0, 0)),
        ],
        out_shape=[
            jax.ShapeDtypeStruct((whole, width), jnp.bfloat16),
            jax.ShapeDtypeStruct((width // LANES, 8, whole), jnp.float32),
        ],
        scratch_shapes=[pltpu.VMEM((whole, 2 * LANES), jnp.bfloat16)],
        compiler_params=pltpu.CompilerParams(vmem_limit_bytes=ROOM),
        cost_estimate=lasting(12),
    )(apart, member, projected, projected, projected)


def turn_back(field, cos, sin):
    half = HEAD_DIM // 2
    lane = lax.broadcasted_iota(jnp.int32, field.shape, 1) % HEAD_DIM
    crossed = jnp.where(lane < half, pltpu.roll(field, LANES - half, 1), pltpu.roll(field, half, 1))
    return field * cos - crossed * sin


def attend_back_kernel(
    reach, apart_ref, member_ref, cos_ref, sin_ref, q_ref, k_ref, v_ref, g_ref, mixed_ref, logs_ref, out_ref,
    keys, keys_t, key_acc, value_acc
):
    whole = q_ref.shape[0]
    lane = lax.broadcasted_iota(jnp.int32, (BLOCK, LANES), 1) // HEAD_DIM
    keys[:, :LANES] = k_ref[...]
    keys[:, LANES:] = member_ref[...]
    keys_t[...] = k_ref[...].astype(jnp.float32).T.astype(jnp.bfloat16)
    key_acc[...] = jnp.zeros_like(key_acc)
    value_acc[...] = jnp.zeros_like(value_acc)

    def one(i, first, count, head):
        span = block_at(first, count)
        plain, query = head_query(q_ref, apart_ref, i, head)
        grad = g_ref[block_at(i), :]
        grad = jnp.where(lane == head, grad, jnp.zeros_like(grad))
        own = dot(keys[block_at(i), :], query, NT)
        key_at = lax.broadcasted_iota(jnp.int32, own.shape, 0)
        query_at = lax.broadcasted_iota(jnp.int32, own.shape, 1)
        scores = jnp.where(key_at <= query_at, own, NEG_FILL)
        if count > 1:
            scores = jnp.concatenate([dot(keys[block_at(first, count - 1), :], query, NT), scores], axis=0)
        probs = jnp.exp(scores - logs_ref[head : head + 1, block_at(i)])
        grad_values = dot(probs.astype(jnp.bfloat16), grad)
        product = grad.astype(jnp.float32) * mixed_ref[block_at(i), :].astype(jnp.float32)
        high = product.astype(jnp.bfloat16)
        ones = jnp.ones((8, LANES), jnp.bfloat16)
        row_dot = dot(ones, high, NT) + dot(ones, (product - high.astype(jnp.float32)).astype(jnp.bfloat16), NT)
        grad_scores = (probs * (dot(v_ref[span, :], grad, NT) - row_dot[:1])).astype(jnp.bfloat16)
        here = dot(keys_t[:, span], grad_scores)
        return grad_values, dot(grad_scores, plain), here

    def body(i, first, count):
        span, at = block_at(first, count), block_at(i)
        values, keys_, queries = zip(*[one(i, first, count, head) for head in range(2)])
        value_acc[span, :] += values[0] + values[1]
        key_acc[span, :] += keys_[0] + keys_[1]
        row = lax.broadcasted_iota(jnp.int32, queries[0].shape, 0) // HEAD_DIM
        both = jnp.where(row == 0, *queries).T * (HEAD_DIM**-0.5)
        out_ref[0, at, :] = turn_back(both, cos_ref[at, :], sin_ref[at, :]).astype(out_ref.dtype)

    each_block(whole, reach, body)

    def finish(i, carry):
        at = block_at(i)
        out_ref[1, at, :] = turn_back(key_acc[at, :], cos_ref[at, :], sin_ref[at, :]).astype(out_ref.dtype)
        out_ref[2, at, :] = value_acc[at, :].astype(out_ref.dtype)
        return carry

    lax.fori_loop(0, whole // BLOCK, finish, 0)


def attend_back(apart, member, cos, sin, projected, grad_mixed, mixed, logs, reach):
    count, whole, width = projected.shape

    def block(c):
        return pl.BlockSpec((None, whole, LANES), lambda p: (c, 0, p))

    table = pl.BlockSpec((whole, LANES), lambda p: (0, 0))
    return pl.pallas_call(
        functools.partial(attend_back_kernel, reach),
        grid=(width // LANES,),
        in_specs=[table] * 4
        + [block(0), block(1), block(2)]
        + [pl.BlockSpec((whole, LANES), lambda p: (0, p))] * 2
        + [pl.BlockSpec((None, 8, whole), lambda p: (p, 0, 0))],
        out_specs=pl.BlockSpec((count, whole, LANES), lambda p: (0, 0, p)),
        out_shape=jax.ShapeDtypeStruct((count, whole, width), jnp.bfloat16),
        scratch_shapes=[
            pltpu.VMEM((whole, 2 * LANES), jnp.bfloat16),
            pltpu.VMEM((LANES, whole), jnp.bfloat16),
            pltpu.VMEM((whole, LANES), jnp.float32),
            pltpu.VMEM((whole, LANES), jnp.float32),
        ],
        compiler_params=pltpu.CompilerParams(vmem_limit_bytes=ROOM),
        cost_estimate=lasting(22),
    )(apart, member, cos, sin, projected, projected, projected, grad_mixed, mixed, logs)


ROWS = 256


def norm_parts(field):
    centered = field - jnp.mean(field, axis=-1, keepdims=True)
    scale = lax.rsqrt(jnp.mean(centered * centered, axis=-1, keepdims=True) + NORM_EPS)
    return centered * scale, scale


def wide(ref, at):
    return ref[at, :].astype(jnp.float32)


def row_blocks(count, body):
    def step(i, carry):
        body(i, pl.ds(pl.multiple_of(i * ROWS, ROWS), ROWS))
        return carry

    lax.fori_loop(0, count // ROWS, step, 0)


TALL = 512


def streamed(kernel, steps, scalars, fields, outs, scratch, microseconds, room=ROOM):
    def spec(shape, block=None, at=None):
        if block is None:
            return pl.BlockSpec(shape, lambda i, *scalars: (0,) * len(shape))
        return pl.BlockSpec(block, at)

    fields = [field if isinstance(field, tuple) else (field,) for field in fields]
    return pl.pallas_call(
        kernel,
        grid_spec=pltpu.PrefetchScalarGridSpec(
            num_scalar_prefetch=len(scalars),
            grid=(steps,),
            in_specs=[spec(field[0].shape, *field[1:]) for field in fields],
            out_specs=[spec(out[0], *out[2:]) for out in outs],
            scratch_shapes=[pltpu.VMEM(shape, dtype) for shape, dtype in scratch],
        ),
        out_shape=[jax.ShapeDtypeStruct(*out[:2]) for out in outs],
        compiler_params=pltpu.CompilerParams(vmem_limit_bytes=room),
        cost_estimate=lasting(microseconds),
    )(*scalars, *[field[0] for field in fields])


def by_rows(field, rows, shift=None):
    if shift is None:
        return field, (rows, field.shape[1]), lambda i, *scalars: (i, 0)
    return field, (rows, field.shape[1]), lambda i, *scalars: (shift(i, *scalars), 0)


def whole_spec(shape):
    return pl.BlockSpec(shape, lambda *at: (0,) * len(shape))


def turn(field, cos, sin):
    half = HEAD_DIM // 2
    lane = lax.broadcasted_iota(jnp.int32, field.shape, 1) % HEAD_DIM
    crossed = jnp.where(lane < half, pltpu.roll(field, LANES - half, 1), pltpu.roll(field, half, 1))
    return field * cos + crossed * sin


def join_rows(flags, own, near, far, out):
    half = near.shape[1]
    for index, got in ((flags[2], near), (1 - flags[2], far)):
        at = pl.ds(pl.multiple_of(index * half, half), half)
        out[:, at, :] = jnp.where(flags[0] == 1, own[:, at, :], got[...])


def project_kernel(flags, rows_ref, cos_ref, sin_ref, vectors, w_own, w_near, w_far, out_ref, turned_ref, weight_ref):
    @pl.when(pl.program_id(0) == 0)
    def _():
        join_rows(flags, w_own, w_near, w_far, weight_ref)

    unit, unused = norm_parts(rows_ref[...].astype(jnp.float32))
    norm = unit * vectors[0:1, :] + vectors[1:2, :]
    turned_ref[...] = norm.T.astype(jnp.bfloat16)
    norm = norm.astype(jnp.bfloat16)
    for c in range(weight_ref.shape[0]):
        field = dot(norm, weight_ref[c])
        if c == 2:
            out_ref[c] = field.astype(jnp.bfloat16)
        else:
            for p in range(field.shape[1] // LANES):
                lanes = slice(p * LANES, (p + 1) * LANES)
                out_ref[c, :, lanes] = turn(field[:, lanes], cos_ref[...], sin_ref[...]).astype(jnp.bfloat16)


def project(flags, rows, vectors, cos, sin, w_own, w_near, w_far):
    whole, width = rows.shape
    count, unused, columns = w_own.shape
    low = jnp.bfloat16
    return streamed(
        project_kernel,
        whole // ROWS,
        [flags],
        [by_rows(rows, ROWS), by_rows(cos, ROWS), by_rows(sin, ROWS), vectors, w_own, w_near, w_far],
        [
            ((count, whole, columns), low, (count, ROWS, columns), lambda i, flags: (0, i, 0)),
            ((width, whole), low, (width, ROWS), lambda i, flags: (0, i)),
        ],
        [(w_own.shape, low)],
        8,
    )


def gelu_both(up):
    root = math.sqrt(2.0 / math.pi)
    square = up * up
    bent = jnp.tanh(root * up * (1.0 + 0.044715 * square))
    half = 0.5 * (1.0 + bent)
    slope = half + 0.5 * up * (1.0 - bent * bent) * (root * (1.0 + 3.0 * 0.044715 * square))
    return up * half, slope


def feed_kernel(early, *refs):
    if early:
        flags, weight_ref, rows_ref, own_ref, got_ref, cot_here, cot_there, vectors, up_own, down_own, got = refs[:11]
        norm, norm_t, grad, grad_t, back_ref, act_ref, down_ref, pieces = refs[11:19]
        up_got, down_got = got.at[: norm.shape[1]], got.at[norm.shape[1] :]
    else:
        flags, norm, norm_t, grad, grad_t, back_early, up_own, down_own, up_got, down_got = refs[:10]
        back_ref, act_ref, down_ref, *pieces = refs[10:17]
    up_w, up_sum, down_sum = refs[-3:]
    part = up_w.shape[1] // 2
    step, last = pl.program_id(0), pl.num_programs(0) - 1

    @pl.when(step == 0)
    def _():
        up_w[...] = jnp.where(flags[0] == 1, up_own[...], up_got[...])
        down_ref[...] = jnp.where(flags[0] == 1, down_own[...], down_got[...])

    if early:

        def head(i, at):
            unit, unused = norm_parts(wide(rows_ref, at) + wide(own_ref, at) + wide(got_ref, at))
            field = unit * vectors[2:3, :] + vectors[3:4, :]
            norm[at, :] = field.astype(jnp.bfloat16)
            norm_t[:, at] = field.T.astype(jnp.bfloat16)
            cot = jnp.where(flags[1] == step, cot_here[at, :], cot_there[at, :])
            field = cot.astype(jnp.float32) * weight_ref[weight_ref.shape[0] - 1]
            grad[at, :] = field.astype(jnp.bfloat16)
            grad_t[:, at] = field.T.astype(jnp.bfloat16)

        row_blocks(norm.shape[0], head)
    value, rise = gelu_both(dot(norm[...], up_w[...]))
    act_ref[...] = value.astype(jnp.bfloat16)
    slope = (dot(grad[...], down_ref[...], NT) * rise).astype(jnp.bfloat16)
    back = dot(slope, up_w[...], NT)
    if not early:
        back = back + back_early[...].astype(jnp.float32)
    back_ref[...] = back.astype(jnp.bfloat16)

    def store(p, at, low):
        if early:
            pieces[p, at, :] = low
            return
        slot = 2 * (flags[2] ^ (p % 2)) + (flags[3] ^ (p // 2))
        for j, piece in enumerate(pieces):

            @pl.when(slot == j)
            def _():
                piece[at, :] = low

    def grads(i, at):
        fields = (dot(norm_t[at, :], slope), dot(grad_t[at, :], act_ref[...]))
        for k, (field, total) in enumerate(zip(fields, (up_sum, down_sum))):

            @pl.when(step == 0)
            def _():
                total[at, :] = field

            @pl.when(step == last)
            def _():
                low = (total[at, :] + field).astype(jnp.bfloat16)
                for p in range(2):
                    store(2 * k + p, at, low[:, p * part : (p + 1) * part])

    row_blocks(norm_t.shape[0], grads)


def feed(early, scalars, fields, w_up, w_down, *got):
    whole, width = fields[0].shape
    hidden = w_up.shape[1] // 2
    rows = whole // 2
    half = 0 if early else 1
    low = jnp.bfloat16

    def across(i, *scalars):
        return (0, i)

    tokens = ((whole, width), low, (rows, width), lambda i, *scalars: (i, 0))
    turned = ((width, whole), low, (width, rows), across)
    if early:
        operands = [by_rows(field, rows) for field in fields[:3]] + [*fields[3:]]
        outs = [tokens, turned, tokens, turned]
        pieces = [((4, width, hidden // 2), low)]
    else:
        operands = [by_rows(fields[0], rows), (fields[1], (width, rows), across)]
        operands += [by_rows(fields[2], rows), (fields[3], (width, rows), across), by_rows(fields[4], rows)]
        outs = []
        pieces = [((width, hidden // 2), low)] * 4
    operands += [
        (w_up, (width, hidden), lambda i, *scalars: (0, half)),
        (w_down, (hidden, width), lambda i, *scalars: (half, 0)),
        *got,
    ]
    outs += [tokens, ((whole, hidden), low, (rows, hidden), lambda i, *scalars: (i, 0)), ((hidden, width), low)]
    sums = ((width, hidden), jnp.float32)
    return streamed(
        functools.partial(feed_kernel, early), 2, scalars, operands, outs + pieces, [((width, hidden), low), sums, sums], 17
    )


def lower_kernel(
    flags, act_early, act_late, rows_ref, own_ref, got_ref, cot_ref, early_ref, late_ref, keep_ref, first, second, sums_ref
):
    step = pl.program_id(0)
    total = dot(act_early[...], early_ref[...]) + dot(act_late[...], late_ref[...])
    cot = cot_ref[...].astype(jnp.float32)

    @pl.when(step == 0)
    def _():
        sums_ref[...] = jnp.zeros_like(sums_ref)

    send_or_keep(
        total,
        total + sum(ref[...].astype(jnp.float32) for ref in (rows_ref, own_ref, got_ref)),
        first,
        second,
        keep_ref,
    )
    mine = jnp.where(step < pl.num_programs(0) // 2, 0.0, 1.0)
    block = total + mine * sum(ref[...].astype(jnp.float32) for ref in (rows_ref, own_ref, got_ref))
    sums_ref[0:1, :] += jnp.sum(block * cot, axis=0, keepdims=True)


def send_or_keep(sent, kept, first, second, keep_ref):
    step = pl.program_id(0)
    for j, ref in enumerate((first, second)):

        @pl.when(step == j)
        def _():
            ref[...] = sent.astype(ref.dtype)

    @pl.when(step >= 2)
    def _():
        keep_ref[...] = kept


def theirs_first(i, flags, *more):
    return lax.rem((1 - flags[1]) * 2 + i, 4)


def sent_and_kept(whole, width):
    rows = whole // 4
    keep = ((2 * rows, width), jnp.float32, (rows, width), lambda i, *scalars: (jnp.maximum(i - 2, 0), 0))
    send = ((rows, width), jnp.bfloat16)
    return [keep, send, send, ((8, width), jnp.float32)]


def lower(flags, act_early, act_late, down_early, down_late, rows, own, got, cot):
    whole, width = rows.shape
    fields = [by_rows(field, whole // 4, theirs_first) for field in (act_early, act_late, rows, own, got, cot)]
    return streamed(
        lower_kernel, 4, [flags], fields + [down_early, down_late], sent_and_kept(whole, width), [], 6, SNUG
    )


def middle_kernel(
    flags, rows_ref, own_ref, got_ref, cot_ref, back_own, back_got, mixed_ref,
    vectors, w_ref, grad_ref, gmixed_ref, gout_ref, sums_ref, gout,
):
    step, last = pl.program_id(0), pl.num_programs(0) - 1
    unit, scale = norm_parts(sum(ref[...].astype(jnp.float32) for ref in (rows_ref, own_ref, got_ref)))
    back = sum(ref[...].astype(jnp.float32) for ref in (back_own, back_got))
    inner = back * vectors[2:3, :]
    mean = jnp.mean(inner, axis=-1, keepdims=True)
    slant = jnp.mean(inner * unit, axis=-1, keepdims=True)
    grad = cot_ref[...].astype(jnp.float32) + scale * (inner - mean - unit * slant)
    low = grad.astype(jnp.bfloat16)
    grad_ref[...] = low
    gmixed_ref[...] = dot(low, w_ref[...], NT).astype(jnp.bfloat16)
    part = dot(grad.T.astype(jnp.bfloat16), mixed_ref[...])

    @pl.when(step == 0)
    def _():
        gout[...] = part
        sums_ref[...] = jnp.zeros_like(sums_ref)

    @pl.when(step > 0)
    def _():
        gout[...] += part

    @pl.when(step == last)
    def _():
        gout_ref[...] = gout[...].astype(jnp.bfloat16)

    @pl.when(step // ((last + 1) // 2) == flags[1])
    def _():
        sums_ref[0:1, :] += jnp.sum(back * unit, axis=0, keepdims=True)
        sums_ref[1:2, :] += jnp.sum(back, axis=0, keepdims=True)


def middle(flags, fields, mixed, vectors, bundle):
    whole, width = fields[0].shape
    columns = mixed.shape[1]
    low = jnp.bfloat16
    in_order = lambda i, *scalars: (i, 0)
    return streamed(
        middle_kernel,
        whole // ROWS,
        [flags],
        [by_rows(field, ROWS) for field in (*fields, mixed)]
        + [vectors, (bundle, (columns, width), lambda i, *scalars: (0, 0))],
        [
            ((whole, width), low, (ROWS, width), in_order),
            ((whole, columns), low, (ROWS, columns), in_order),
            ((width, columns), low),
            ((8, width), jnp.float32),
        ],
        [((width, columns), jnp.float32)],
        8,
    )


def weigh_kernel(flags, turned_ref, out_grad_ref, grad_ref, *out_refs):
    last = grad_ref.shape[0]
    for j, out_ref in enumerate(out_refs):
        piece = 2 * (flags[2] ^ (j // 2)) + (flags[3] ^ (j % 2))

        @pl.when(piece < last)
        def _():
            out_ref[...] = dot(turned_ref[...], grad_ref[jnp.minimum(piece, last - 1)]).astype(jnp.bfloat16)

        @pl.when(piece == last)
        def _():
            out_ref[...] = out_grad_ref[...]


def weigh(flags, turned, grad, out_grad):
    width, columns = turned.shape[0], grad.shape[2]
    piece = ((width, columns), jnp.bfloat16, (ROWS, columns), lambda i, flags: (i, 0))
    return streamed(
        weigh_kernel, width // ROWS, [flags], [by_rows(turned, ROWS), by_rows(out_grad, ROWS), grad], [piece] * 4, [], 4
    )


def unproject_kernel(flags, grad_ref, rows_ref, w_own, w_near, w_far, keep_ref, first, second, sums_ref, weight):
    @pl.when(pl.program_id(0) == 0)
    def _():
        join_rows(flags, w_own, w_near, w_far, weight)

    total = dot(grad_ref[0], weight[0], NT)
    for c in range(1, grad_ref.shape[0]):
        total = total + dot(grad_ref[c], weight[c], NT)
    unit, unused = norm_parts(rows_ref[...].astype(jnp.float32))

    @pl.when(pl.program_id(0) == 0)
    def _():
        sums_ref[...] = jnp.zeros_like(sums_ref)

    sums_ref[0:1, :] += jnp.sum(total * unit, axis=0, keepdims=True)
    sums_ref[1:2, :] += jnp.sum(total, axis=0, keepdims=True)
    send_or_keep(total, total, first, second, keep_ref)


def unproject(flags, grad, weights, rows):
    whole, width = rows.shape
    count, unused, columns = grad.shape
    grads = (grad, (count, whole // 4, columns), lambda i, flags: (0, theirs_first(i, flags), 0))
    fields = [grads, by_rows(rows, whole // 4, theirs_first), *weights]
    scratch = [((count, width, columns), jnp.bfloat16)]
    return streamed(unproject_kernel, 4, [flags], fields, sent_and_kept(whole, width), scratch, 5, SNUG + (4 << 20))


def last_kernel(
    flags, rows_ref, resid_ref, keep_ref, block_keep, got_first, got_second, block_first, block_second, vectors, out_ref
):
    first = pl.program_id(0) == 0
    unit, scale = norm_parts(rows_ref[...].astype(jnp.float32))
    got = jnp.where(first, got_first[...], got_second[...]).astype(jnp.float32)
    inner = (keep_ref[...] + got) * vectors[0:1, :]
    mean = jnp.mean(inner, axis=-1, keepdims=True)
    slant = jnp.mean(inner * unit, axis=-1, keepdims=True)
    grad = resid_ref[...].astype(jnp.float32) + scale * (inner - mean - unit * slant)
    out_ref[0] = grad.astype(jnp.bfloat16)
    got = jnp.where(first, block_first[...], block_second[...]).astype(jnp.float32)
    out_ref[1] = (block_keep[...] + got).astype(jnp.bfloat16)


def last(flags, rows, resid, keep, block_keep, got, vectors):
    half, width = keep.shape
    size = half // 2

    def mine(i, flags):
        return flags[1] * 2 + i

    out = ((2, half, width), jnp.bfloat16, (2, size, width), lambda i, flags: (0, i, 0))
    fields = [by_rows(rows, size, mine), by_rows(resid, size, mine), by_rows(keep, size), by_rows(block_keep, size)]
    return streamed(last_kernel, 2, [flags], fields + [*got, vectors], [out], [], 3)[0]


def past_kernel(dwa_ref, hist_ref, cot_ref, grad_ref, part_ref, sums_ref):
    @pl.when(pl.program_id(0) == 0)
    def _():
        sums_ref[...] = jnp.zeros_like(sums_ref)

    grad = cot_ref[...].astype(jnp.float32)
    total = jnp.zeros_like(grad)
    for j in range(hist_ref.shape[0]):
        field = hist_ref[j].astype(jnp.float32)
        total += dwa_ref[j] * field
        grad_ref[j] = (dwa_ref[j] * grad).astype(jnp.bfloat16)
        sums_ref[j : j + 1, :] += jnp.sum(field * grad, axis=0, keepdims=True)
    part_ref[...] = total


def past(dwa, history, cot):
    count, rows, width = history.shape
    layers = pl.BlockSpec((count, ROWS, width), lambda i: (0, i, 0))
    tokens = pl.BlockSpec((ROWS, width), lambda i: (i, 0))
    return pl.pallas_call(
        past_kernel,
        grid=(rows // ROWS,),
        in_specs=[pl.BlockSpec(memory_space=pltpu.SMEM), layers, tokens],
        out_specs=[layers, tokens, whole_spec((8, width))],
        out_shape=[
            jax.ShapeDtypeStruct(history.shape, jnp.bfloat16),
            jax.ShapeDtypeStruct((rows, width), jnp.float32),
            jax.ShapeDtypeStruct((8, width), jnp.float32),
        ],
        compiler_params=pltpu.CompilerParams(vmem_limit_bytes=ROOM),
        cost_estimate=lasting(3),
    )(dwa, history, cot)


def present_kernel(flags, weight_ref, part_ref, own_ref, got_ref, out_ref, grad_ref):
    here = jnp.where(flags[0] == 1, own_ref[1], got_ref[1]).astype(jnp.float32)
    out_ref[...] = (part_ref[...] + weight_ref[weight_ref.shape[0] - 1] * here).astype(jnp.bfloat16)
    grad_ref[...] = jnp.where(flags[0] == 1, own_ref[0], got_ref[0])


def present(flags, weight, part, own, got):
    rows, width = part.shape
    both = (2, ROWS, width), lambda i, *scalars: (0, i, 0)
    out = ((rows, width), jnp.bfloat16, (ROWS, width), lambda i, *scalars: (i, 0))
    fields = [by_rows(part, ROWS), (own, *both), (got, *both)]
    return streamed(present_kernel, rows // ROWS, [flags, weight], fields, [out] * 2, [], 2, SNUG)


def place_kernel(flags, here_ref, there_ref, qkv_ref, out_ref, up_ref, down_ref):
    near, far = flags[1], flags[2]
    part = out_ref.shape[1]
    for k in range(2):
        for c in range(2):
            field = jnp.where(near == c, here_ref[k ^ far], there_ref[k ^ far]).astype(jnp.float32)
            if 2 * k + c < 3:
                qkv_ref[2 * k + c] = field[:, :part]
            else:
                out_ref[...] = field[:, :part]
            for half in range(2):
                at = (2 * half + k) * part
                (up_ref, down_ref)[c][:, at : at + part] = field[:, (1 + half) * part : (2 + half) * part]


def place(flags, here, there):
    rows, part = here.shape[1], here.shape[2] // 3
    outs = [((3, rows, part), jnp.float32), ((rows, part), jnp.float32)]
    outs += [((rows, 4 * part), jnp.float32)] * 2
    return streamed(place_kernel, 1, [flags], [here, there], outs, [], 3, SNUG)


AXES = ("tp", "dp", "far", "near")


def moves(chosen, move):
    sizes = [lax.axis_size(name) for name in AXES]
    places = [place for place in itertools.product(*map(range, sizes)) if chosen(*place)]
    index = lambda place: functools.reduce(lambda at, step: at * step[0] + step[1], zip(sizes, place), 0)
    return [(index(place), index(move(*place))) for place in places]


def away(t, d, k, c):
    return t != c


def anyone(t, d, k, c):
    return True


def swap_diagonal(field):
    return lax.ppermute(field, AXES, moves(away, lambda t, d, k, c: (c, d, k, t)))


def send_to_owner(field, other_far, other_tp):
    return lax.ppermute(
        field,
        AXES,
        moves(
            away if not other_far and not other_tp else anyone,
            lambda t, d, k, c: (c, d, k ^ other_far, t ^ other_tp),
        ),
    )


def swap_far_away(field):
    return lax.ppermute(field, AXES, moves(away, lambda t, d, k, c: (t, d, 1 - k, c)))


def swap_far(field):
    return lax.ppermute(field, "far", [(0, 1), (1, 0)])


def swap_near(field):
    return lax.ppermute(field, "near", [(0, 1), (1, 0)])


def after(field, *others):
    return lax.optimization_barrier((field, *others))[0]


def ordered(own, other, first, axis=0):
    return jnp.where(
        first, jnp.concatenate([own, other], axis=axis), jnp.concatenate([other, own], axis=axis)
    )


def part_of(field, index, axis):
    size = field.shape[axis] // 2
    return lax.dynamic_slice_in_dim(field, index * size, size, axis)


def add(*fields):
    return sum(field.astype(jnp.float32) for field in fields).astype(jnp.bfloat16)


def scatter_plane(pieces):
    return lax.psum_scatter(pieces, ("tp", "far"), scatter_dimension=0, tiled=True)[0]


def scatter_rows(piece):
    return lax.psum_scatter(piece, "dp", scatter_dimension=0, tiled=True)


def move_rows(block):
    dps = lax.axis_size("dp")
    if dps > 8:
        return [scatter_rows(block)]
    block = block.reshape(dps, block.shape[0] // dps, block.shape[1])
    place = lax.axis_index("dp")
    moved = [lax.dynamic_index_in_dim(block, place, 0, keepdims=False)]
    for step in range(1, dps):
        sent = lax.dynamic_index_in_dim(block, lax.rem(place + step, dps), 0, keepdims=False)
        moved.append(lax.ppermute(sent, "dp", [(d, (d + step) % dps) for d in range(dps)]))
    return moved


def sum_over(field, name):
    size = lax.axis_size(name)
    bit = 1
    while bit < size:
        field = field + lax.ppermute(field, name, [(d, d ^ bit) for d in range(size)])
        bit *= 2
    return field


def local(
    layer_input,
    history,
    cotangent,
    lengths,
    dwa_weights,
    gain_one,
    bias_one,
    w_qkv,
    w_out,
    gain_two,
    bias_two,
    w_up,
    w_down,
):
    rows = layer_input.shape[1]
    whole = rows * lax.axis_size("tp")
    hist_count = history.shape[0]
    part, far, near = lax.axis_index("tp"), lax.axis_index("far"), lax.axis_index("near")
    same = near == part
    flags = jnp.stack([same.astype(jnp.int32), near, far, part])

    input_got = swap_diagonal(layer_input[0])
    qkv_near = swap_diagonal(part_of(w_qkv, far, 1))
    qkv_far = swap_far_away(qkv_near)
    early_got = jnp.concatenate([part_of(w_up, 0, 1), part_of(w_down, 0, 0)], axis=0)
    late_up, late_down = part_of(w_up, 1, 1), part_of(w_down, 1, 0)
    last_own = jnp.concatenate([w_out, cotangent[0]], axis=0)
    vectors = jnp.stack([gain_one, bias_one, gain_two, bias_two])

    own_lengths = jnp.where(same, lengths, swap_near(lengths))[0]
    seq_owner, token_place = positions(own_lengths, whole)
    lane = jnp.arange(LANES, dtype=jnp.int32)
    member = seq_owner[:, None] == lane[None, :]
    apart = jnp.where(member | (lane >= lengths.shape[1])[None, :], 0.0, NEG_FILL).astype(jnp.bfloat16)
    member = member.astype(jnp.bfloat16)
    half_dim = HEAD_DIM // 2
    frequency = jnp.exp((lane % half_dim).astype(jnp.float32) * (-math.log(10000.0) / half_dim))
    angles = token_place.astype(jnp.float32)[:, None] * frequency[None, :]
    cos_table = jnp.cos(angles)
    sin_table = jnp.sin(angles) * jnp.where(lane % HEAD_DIM < half_dim, -1.0, 1.0)[None, :]
    grad_history, past_sum, sums_past = past(dwa_weights, history[:, 0], cotangent[0])

    input_half = jnp.where(same, layer_input[0], input_got)
    layer_rows = ordered(input_half, swap_near(input_half), near == 0)
    layer_rows, vectors, past_sum, cos_table, sin_table, apart, member = lax.optimization_barrier(
        (layer_rows, vectors, past_sum, cos_table, sin_table, apart, member)
    )
    early_got = swap_diagonal(after(early_got, input_got))
    last_got = swap_diagonal(after(last_own, input_got))
    projected, norm_one_t = project(
        flags, layer_rows, vectors, cos_table, sin_table, w_qkv, qkv_near, qkv_far
    )
    mixed, logs = attend(apart, member, projected, LONGEST)
    late_up = swap_diagonal(after(late_up, mixed))
    late_down = swap_diagonal(after(late_down, mixed))
    last_got = jnp.where(same, last_own, after(last_got, mixed))
    weight_out = last_got[: w_out.shape[0]]
    attn = jnp.dot(mixed, weight_out, preferred_element_type=jnp.float32).astype(jnp.bfloat16)
    attn_got = swap_near(attn)
    cot_half = last_got[w_out.shape[0] :]
    scalars = [flags, dwa_weights]
    fields = [layer_rows, attn, attn_got, cot_half, swap_near(cot_half), vectors]
    *kept, back, act_early, down_early, early_pieces = feed(True, scalars, fields, w_up, w_down, early_got)
    early_sum = scatter_plane(after(early_pieces, late_up, late_down))
    back, act_late, down_late, *late_owned = feed(
        False, [flags], [*kept, back], w_up, w_down, late_up, late_down
    )
    late_moved = [send_to_owner(late_owned[j], j // 2, j % 2) for j in range(4)]
    grad_down = kept[2]
    fields = [layer_rows, attn, attn_got, grad_down, back, swap_near(back)]
    grad_attn, grad_mixed, grad_out, sums_two = middle(flags, fields, mixed, vectors, last_got)
    grad_qkv = attend_back(
        apart, member, cos_table, sin_table, projected, grad_mixed, mixed, logs, LONGEST
    )
    grad_qkv, *late_moved = lax.optimization_barrier((grad_qkv, *late_moved))
    owned = weigh(flags, norm_one_t, grad_qkv, grad_out)
    moved = [send_to_owner(owned[j], j // 2, j % 2) for j in range(4)]
    early_sum = scatter_rows(after(early_sum, grad_qkv))
    late_sum = scatter_rows(add(jnp.where(same, late_owned[0], after(late_moved[0], owned[0])), *late_moved[1:]))
    keep, *send, sums_one = unproject(
        flags, after(grad_qkv, owned[0]), (w_qkv, qkv_near, qkv_far), layer_rows
    )
    block_keep, *block_send, sums_now = lower(
        flags, act_early, act_late, down_early, down_late, layer_rows, attn, attn_got, after(grad_down, keep)
    )
    sent = [*send, *block_send]
    keep, block_keep, *arrived = lax.optimization_barrier((keep, block_keep, *sent, *moved))
    sent, moved = arrived[:4], arrived[4:]
    attn_one = add(jnp.where(same, owned[0], moved[0]), *moved[1:])
    attn_moved = move_rows(attn_one)
    got = [swap_near(field) for field in sent]
    ours = last(flags, layer_rows, grad_attn, after(keep, attn_one), block_keep, got, vectors)
    early_sum = after(early_sum, attn_one)
    early_got = swap_diagonal(early_sum)
    small = jnp.concatenate([sums_one[:2], sums_two[:2], sums_now[:1], sums_past[:hist_count]], axis=0)
    small = after(small, ours)
    for name in ("near", "tp", "far"):
        small = sum_over(small, name)
    small, ours, late_sum, early_sum, early_got, *attn_moved = lax.optimization_barrier(
        (small, ours, late_sum, early_sum, early_got, *attn_moved)
    )
    theirs = swap_diagonal(ours)
    small = sum_over(small, "dp")
    attn_sum = add(*attn_moved)
    blocks = jnp.concatenate([attn_sum, jnp.where(same, early_sum, early_got), late_sum], axis=1)
    here = jnp.stack([blocks, swap_far(blocks)])
    output, grad_input = present(flags, dwa_weights, past_sum, ours, theirs)
    grad_w_qkv, grad_w_out, grad_w_up, grad_w_down = place(flags, here, swap_near(here))

    return (
        output[None],
        grad_input[None],
        grad_history[:, None],
        jnp.sum(jnp.concatenate([small[5:], small[4:5] / dwa_weights[hist_count]], axis=0), axis=1),
        small[0],
        small[1],
        grad_w_qkv,
        grad_w_out.T,
        small[2],
        small[3],
        grad_w_up,
        grad_w_down.T,
    )


def positions(seq_lengths, token_count):
    seq_ends = jnp.cumsum(seq_lengths)
    seq_starts = seq_ends - seq_lengths
    token_index = jnp.arange(token_count, dtype=jnp.int32)
    seq_owner = jnp.sum((token_index[:, None] >= seq_ends[None, :]).astype(jnp.int32), axis=1)
    picked = (
        seq_owner[:, None] == jnp.arange(seq_lengths.shape[0], dtype=jnp.int32)[None, :]
    ).astype(jnp.int32)
    seq_begin = jnp.sum(picked * seq_starts[None, :], axis=1)
    return (seq_owner, token_index - seq_begin)


def solution(mesh):
    tps, dps, reps = (mesh.shape[name] for name in ("tp", "dp", "rep"))
    split = Mesh(mesh.devices.reshape(tps, dps, reps // 2, 2), AXES)
    in_specs = (
        P(("dp", "far", "near"), "tp", None),
        P(None, ("dp", "far", "near"), "tp", None),
        P(("dp", "far", "near"), "tp", None),
        P(("dp", "far", "near"), None),
        P(),
        P(),
        P(),
        P(None, None, "tp"),
        P("tp", None),
        P(),
        P(),
        P(None, "tp"),
        P("tp", None),
    )
    out_specs = (
        P(("dp", "far", "near"), "tp", None),
        P(("dp", "far", "near"), "tp", None),
        P(None, ("dp", "far", "near"), "tp", None),
        P(),
        P(),
        P(),
        P(None, "dp", "tp"),
        P("tp", "dp"),
        P(),
        P(),
        P("dp", "tp"),
        P("tp", "dp"),
    )
    return jax.shard_map(local, mesh=split, in_specs=in_specs, out_specs=out_specs, check_vma=False)
```

```python
import functools
import itertools
import math

import jax
import jax.numpy as jnp
from jax import lax
from jax.experimental import pallas as pl
from jax.experimental.pallas import tpu as pltpu
from jax.sharding import Mesh, PartitionSpec as P

HEAD_DIM = 64
LONGEST = 512
NEG_FILL = -1e30
NORM_EPS = 1e-05
RATE = 3e6
ROOM = 60 << 20
SNUG = 18 << 20


def lasting(microseconds):
    return pl.CostEstimate(flops=0, transcendentals=0, bytes_accessed=int(microseconds * RATE))


BLOCK = 256
LANES = 128
NT = (((1,), (1,)), ((), ()))


def dot(a, b, dims=(((1,), (0,)), ((), ()))):
    return lax.dot_general(a, b, dims, preferred_element_type=jnp.float32)


def spans(whole, reach):
    back = -(-(reach - 1) // BLOCK)
    runs = []
    for i in range(whole // BLOCK):
        count = min(i, back) + 1
        if runs and runs[-1][2] == count:
            runs[-1][1] = i + 1
        else:
            runs.append([i, i + 1, count])
    return runs


def each_block(whole, reach, body):
    for first, last, count in spans(whole, reach):

        def step(i, carry, count=count):
            body(i, i + 1 - count, count)
            return carry

        lax.fori_loop(first, last, step, 0)


def block_at(i, count=1):
    return pl.ds(pl.multiple_of(i * BLOCK, BLOCK), count * BLOCK)


def head_query(q_ref, apart_ref, i, head):
    lane = lax.broadcasted_iota(jnp.int32, (BLOCK, LANES), 1) // HEAD_DIM
    query = q_ref[block_at(i), :] * (HEAD_DIM**-0.5)
    query = jnp.where(lane == head, query, jnp.zeros_like(query))
    return query, jnp.concatenate([query, apart_ref[block_at(i), :]], axis=1)


def attend_kernel(reach, apart_ref, member_ref, q_ref, k_ref, v_ref, out_ref, logs_ref, keys):
    whole = q_ref.shape[0]
    lane = lax.broadcasted_iota(jnp.int32, (BLOCK, LANES), 1) // HEAD_DIM
    keys[:, :LANES] = k_ref[...]
    keys[:, LANES:] = member_ref[...]

    def one(i, first, count, head):
        unused, query = head_query(q_ref, apart_ref, i, head)
        own = dot(query, keys[block_at(i), :], NT)
        key_at = lax.broadcasted_iota(jnp.int32, own.shape, 1)
        query_at = lax.broadcasted_iota(jnp.int32, own.shape, 0)
        scores = jnp.where(key_at <= query_at, own, NEG_FILL)
        if count > 1:
            scores = jnp.concatenate([dot(query, keys[block_at(first, count - 1), :], NT), scores], axis=1)
        row_max = jnp.max(scores, axis=1, keepdims=True)
        exponent = jnp.exp(scores - row_max)
        row_sum = jnp.sum(exponent, axis=1, keepdims=True)
        mixed = dot(exponent.astype(jnp.bfloat16), v_ref[block_at(first, count), :]) * (1.0 / row_sum)
        return mixed, row_max + jnp.log(row_sum)

    def body(i, first, count):
        mixed, logs = zip(*[one(i, first, count, head) for head in range(2)])
        out_ref[block_at(i), :] = jnp.where(lane == 0, *mixed).astype(out_ref.dtype)
        turned = jnp.where(lane == 0, *logs).T
        for head in range(2):
            logs_ref[head : head + 1, block_at(i)] = turned[head * HEAD_DIM : head * HEAD_DIM + 1]

    each_block(whole, reach, body)


def attend(apart, member, projected, reach):
    count, whole, width = projected.shape

    def block(c):
        return pl.BlockSpec((None, whole, LANES), lambda p: (c, 0, p))

    table = pl.BlockSpec((whole, LANES), lambda p: (0, 0))
    return pl.pallas_call(
        functools.partial(attend_kernel, reach),
        grid=(width // LANES,),
        in_specs=[table, table, block(0), block(1), block(2)],
        out_specs=[
            pl.BlockSpec((whole, LANES), lambda p: (0, p)),
            pl.BlockSpec((None, 8, whole), lambda p: (p, 0, 0)),
        ],
        out_shape=[
            jax.ShapeDtypeStruct((whole, width), jnp.bfloat16),
            jax.ShapeDtypeStruct((width // LANES, 8, whole), jnp.float32),
        ],
        scratch_shapes=[pltpu.VMEM((whole, 2 * LANES), jnp.bfloat16)],
        compiler_params=pltpu.CompilerParams(vmem_limit_bytes=ROOM),
        cost_estimate=lasting(12),
    )(apart, member, projected, projected, projected)


def turn_back(field, cos, sin):
    half = HEAD_DIM // 2
    lane = lax.broadcasted_iota(jnp.int32, field.shape, 1) % HEAD_DIM
    crossed = jnp.where(lane < half, pltpu.roll(field, LANES - half, 1), pltpu.roll(field, half, 1))
    return field * cos - crossed * sin


def attend_back_kernel(
    reach, apart_ref, member_ref, cos_ref, sin_ref, q_ref, k_ref, v_ref, g_ref, mixed_ref, logs_ref, out_ref,
    keys, keys_t, key_acc, value_acc
):
    whole = q_ref.shape[0]
    lane = lax.broadcasted_iota(jnp.int32, (BLOCK, LANES), 1) // HEAD_DIM
    keys[:, :LANES] = k_ref[...]
    keys[:, LANES:] = member_ref[...]
    keys_t[...] = k_ref[...].astype(jnp.float32).T.astype(jnp.bfloat16)
    key_acc[...] = jnp.zeros_like(key_acc)
    value_acc[...] = jnp.zeros_like(value_acc)

    def one(i, first, count, head):
        span = block_at(first, count)
        plain, query = head_query(q_ref, apart_ref, i, head)
        grad = g_ref[block_at(i), :]
        grad = jnp.where(lane == head, grad, jnp.zeros_like(grad))
        own = dot(keys[block_at(i), :], query, NT)
        key_at = lax.broadcasted_iota(jnp.int32, own.shape, 0)
        query_at = lax.broadcasted_iota(jnp.int32, own.shape, 1)
        scores = jnp.where(key_at <= query_at, own, NEG_FILL)
        if count > 1:
            scores = jnp.concatenate([dot(keys[block_at(first, count - 1), :], query, NT), scores], axis=0)
        probs = jnp.exp(scores - logs_ref[head : head + 1, block_at(i)])
        grad_values = dot(probs.astype(jnp.bfloat16), grad)
        product = grad.astype(jnp.float32) * mixed_ref[block_at(i), :].astype(jnp.float32)
        high = product.astype(jnp.bfloat16)
        ones = jnp.ones((8, LANES), jnp.bfloat16)
        row_dot = dot(ones, high, NT) + dot(ones, (product - high.astype(jnp.float32)).astype(jnp.bfloat16), NT)
        grad_scores = (probs * (dot(v_ref[span, :], grad, NT) - row_dot[:1])).astype(jnp.bfloat16)
        here = dot(keys_t[:, span], grad_scores)
        return grad_values, dot(grad_scores, plain), here

    def body(i, first, count):
        span, at = block_at(first, count), block_at(i)
        values, keys_, queries = zip(*[one(i, first, count, head) for head in range(2)])
        value_acc[span, :] += values[0] + values[1]
        key_acc[span, :] += keys_[0] + keys_[1]
        row = lax.broadcasted_iota(jnp.int32, queries[0].shape, 0) // HEAD_DIM
        both = jnp.where(row == 0, *queries).T * (HEAD_DIM**-0.5)
        out_ref[0, at, :] = turn_back(both, cos_ref[at, :], sin_ref[at, :]).astype(out_ref.dtype)

    each_block(whole, reach, body)

    def finish(i, carry):
        at = block_at(i)
        out_ref[1, at, :] = turn_back(key_acc[at, :], cos_ref[at, :], sin_ref[at, :]).astype(out_ref.dtype)
        out_ref[2, at, :] = value_acc[at, :].astype(out_ref.dtype)
        return carry

    lax.fori_loop(0, whole // BLOCK, finish, 0)


def attend_back(apart, member, cos, sin, projected, grad_mixed, mixed, logs, reach):
    count, whole, width = projected.shape

    def block(c):
        return pl.BlockSpec((None, whole, LANES), lambda p: (c, 0, p))

    table = pl.BlockSpec((whole, LANES), lambda p: (0, 0))
    return pl.pallas_call(
        functools.partial(attend_back_kernel, reach),
        grid=(width // LANES,),
        in_specs=[table] * 4
        + [block(0), block(1), block(2)]
        + [pl.BlockSpec((whole, LANES), lambda p: (0, p))] * 2
        + [pl.BlockSpec((None, 8, whole), lambda p: (p, 0, 0))],
        out_specs=pl.BlockSpec((count, whole, LANES), lambda p: (0, 0, p)),
        out_shape=jax.ShapeDtypeStruct((count, whole, width), jnp.bfloat16),
        scratch_shapes=[
            pltpu.VMEM((whole, 2 * LANES), jnp.bfloat16),
            pltpu.VMEM((LANES, whole), jnp.bfloat16),
            pltpu.VMEM((whole, LANES), jnp.float32),
            pltpu.VMEM((whole, LANES), jnp.float32),
        ],
        compiler_params=pltpu.CompilerParams(vmem_limit_bytes=ROOM),
        cost_estimate=lasting(22),
    )(apart, member, cos, sin, projected, projected, projected, grad_mixed, mixed, logs)


ROWS = 256


def norm_parts(field):
    centered = field - jnp.mean(field, axis=-1, keepdims=True)
    scale = lax.rsqrt(jnp.mean(centered * centered, axis=-1, keepdims=True) + NORM_EPS)
    return centered * scale, scale


def wide(ref, at):
    return ref[at, :].astype(jnp.float32)


def row_blocks(count, body):
    def step(i, carry):
        body(i, pl.ds(pl.multiple_of(i * ROWS, ROWS), ROWS))
        return carry

    lax.fori_loop(0, count // ROWS, step, 0)


TALL = 512


def streamed(kernel, steps, scalars, fields, outs, scratch, microseconds, room=ROOM):
    def spec(shape, block=None, at=None):
        if block is None:
            return pl.BlockSpec(shape, lambda i, *scalars: (0,) * len(shape))
        return pl.BlockSpec(block, at)

    fields = [field if isinstance(field, tuple) else (field,) for field in fields]
    return pl.pallas_call(
        kernel,
        grid_spec=pltpu.PrefetchScalarGridSpec(
            num_scalar_prefetch=len(scalars),
            grid=(steps,),
            in_specs=[spec(field[0].shape, *field[1:]) for field in fields],
            out_specs=[spec(out[0], *out[2:]) for out in outs],
            scratch_shapes=[pltpu.VMEM(shape, dtype) for shape, dtype in scratch],
        ),
        out_shape=[jax.ShapeDtypeStruct(*out[:2]) for out in outs],
        compiler_params=pltpu.CompilerParams(vmem_limit_bytes=room),
        cost_estimate=lasting(microseconds),
    )(*scalars, *[field[0] for field in fields])


def by_rows(field, rows, shift=None):
    if shift is None:
        return field, (rows, field.shape[1]), lambda i, *scalars: (i, 0)
    return field, (rows, field.shape[1]), lambda i, *scalars: (shift(i, *scalars), 0)


def whole_spec(shape):
    return pl.BlockSpec(shape, lambda *at: (0,) * len(shape))


def turn(field, cos, sin):
    half = HEAD_DIM // 2
    lane = lax.broadcasted_iota(jnp.int32, field.shape, 1) % HEAD_DIM
    crossed = jnp.where(lane < half, pltpu.roll(field, LANES - half, 1), pltpu.roll(field, half, 1))
    return field * cos + crossed * sin


def join_rows(flags, own, near, far, out):
    half = near.shape[1]
    for index, got in ((flags[2], near), (1 - flags[2], far)):
        at = pl.ds(pl.multiple_of(index * half, half), half)
        out[:, at, :] = jnp.where(flags[0] == 1, own[:, at, :], got[...])


def project_kernel(flags, rows_ref, cos_ref, sin_ref, vectors, w_own, w_near, w_far, out_ref, turned_ref, weight_ref):
    @pl.when(pl.program_id(0) == 0)
    def _():
        join_rows(flags, w_own, w_near, w_far, weight_ref)

    unit, unused = norm_parts(rows_ref[...].astype(jnp.float32))
    norm = unit * vectors[0:1, :] + vectors[1:2, :]
    turned_ref[...] = norm.T.astype(jnp.bfloat16)
    norm = norm.astype(jnp.bfloat16)
    for c in range(weight_ref.shape[0]):
        field = dot(norm, weight_ref[c])
        if c == 2:
            out_ref[c] = field.astype(jnp.bfloat16)
        else:
            for p in range(field.shape[1] // LANES):
                lanes = slice(p * LANES, (p + 1) * LANES)
                out_ref[c, :, lanes] = turn(field[:, lanes], cos_ref[...], sin_ref[...]).astype(jnp.bfloat16)


def project(flags, rows, vectors, cos, sin, w_own, w_near, w_far):
    whole, width = rows.shape
    count, unused, columns = w_own.shape
    low = jnp.bfloat16
    return streamed(
        project_kernel,
        whole // ROWS,
        [flags],
        [by_rows(rows, ROWS), by_rows(cos, ROWS), by_rows(sin, ROWS), vectors, w_own, w_near, w_far],
        [
            ((count, whole, columns), low, (count, ROWS, columns), lambda i, flags: (0, i, 0)),
            ((width, whole), low, (width, ROWS), lambda i, flags: (0, i)),
        ],
        [(w_own.shape, low)],
        8,
    )


def gelu_both(up):
    root = math.sqrt(2.0 / math.pi)
    square = up * up
    bent = jnp.tanh(root * up * (1.0 + 0.044715 * square))
    half = 0.5 * (1.0 + bent)
    slope = half + 0.5 * up * (1.0 - bent * bent) * (root * (1.0 + 3.0 * 0.044715 * square))
    return up * half, slope


def feed_kernel(early, *refs):
    if early:
        flags, weight_ref, rows_ref, own_ref, got_ref, cot_here, cot_there, vectors, up_own, down_own, got = refs[:11]
        norm, norm_t, grad, grad_t, back_ref, act_ref, down_ref, pieces = refs[11:19]
    else:
        flags, norm, norm_t, grad, grad_t, back_early, up_own, down_own, got = refs[:9]
        back_ref, act_ref, down_ref, *pieces = refs[9:16]
    up_got, down_got = got.at[: norm.shape[1]], got.at[norm.shape[1] :]
    up_w, up_sum, down_sum = refs[-3:]
    part = up_w.shape[1] // 2
    step, last = pl.program_id(0), pl.num_programs(0) - 1

    @pl.when(step == 0)
    def _():
        up_w[...] = jnp.where(flags[0] == 1, up_own[...], up_got[...])
        down_ref[...] = jnp.where(flags[0] == 1, down_own[...], down_got[...])

    if early:

        def head(i, at):
            unit, unused = norm_parts(wide(rows_ref, at) + wide(own_ref, at) + wide(got_ref, at))
            field = unit * vectors[2:3, :] + vectors[3:4, :]
            norm[at, :] = field.astype(jnp.bfloat16)
            norm_t[:, at] = field.T.astype(jnp.bfloat16)
            cot = jnp.where(flags[1] == step, cot_here[at, :], cot_there[at, :])
            field = cot.astype(jnp.float32) * weight_ref[weight_ref.shape[0] - 1]
            grad[at, :] = field.astype(jnp.bfloat16)
            grad_t[:, at] = field.T.astype(jnp.bfloat16)

        row_blocks(norm.shape[0], head)
    value, rise = gelu_both(dot(norm[...], up_w[...]))
    act_ref[...] = value.astype(jnp.bfloat16)
    slope = (dot(grad[...], down_ref[...], NT) * rise).astype(jnp.bfloat16)
    back = dot(slope, up_w[...], NT)
    if not early:
        back = back + back_early[...].astype(jnp.float32)
    back_ref[...] = back.astype(jnp.bfloat16)

    def store(p, at, low):
        if early:
            pieces[p, at, :] = low
            return
        slot = 2 * (flags[2] ^ (p % 2)) + (flags[3] ^ (p // 2))
        for j, piece in enumerate(pieces):

            @pl.when(slot == j)
            def _():
                piece[at, :] = low

    def grads(i, at):
        fields = (dot(norm_t[at, :], slope), dot(grad_t[at, :], act_ref[...]))
        for k, (field, total) in enumerate(zip(fields, (up_sum, down_sum))):

            @pl.when(step == 0)
            def _():
                total[at, :] = field

            @pl.when(step == last)
            def _():
                low = (total[at, :] + field).astype(jnp.bfloat16)
                for p in range(2):
                    store(2 * k + p, at, low[:, p * part : (p + 1) * part])

    row_blocks(norm_t.shape[0], grads)


def feed(early, scalars, fields, w_up, w_down, got):
    whole, width = fields[0].shape
    hidden = w_up.shape[1] // 2
    rows = whole // 2
    half = 0 if early else 1
    low = jnp.bfloat16

    def across(i, *scalars):
        return (0, i)

    tokens = ((whole, width), low, (rows, width), lambda i, *scalars: (i, 0))
    turned = ((width, whole), low, (width, rows), across)
    if early:
        operands = [by_rows(field, rows) for field in fields[:3]] + [*fields[3:]]
        outs = [tokens, turned, tokens, turned]
        pieces = [((4, width, hidden // 2), low)]
    else:
        operands = [by_rows(fields[0], rows), (fields[1], (width, rows), across)]
        operands += [by_rows(fields[2], rows), (fields[3], (width, rows), across), by_rows(fields[4], rows)]
        outs = []
        pieces = [((width, hidden // 2), low)] * 4
    operands += [
        (w_up, (width, hidden), lambda i, *scalars: (0, half)),
        (w_down, (hidden, width), lambda i, *scalars: (half, 0)),
        got,
    ]
    outs += [tokens, ((whole, hidden), low, (rows, hidden), lambda i, *scalars: (i, 0)), ((hidden, width), low)]
    sums = ((width, hidden), jnp.float32)
    return streamed(
        functools.partial(feed_kernel, early), 2, scalars, operands, outs + pieces, [((width, hidden), low), sums, sums], 17
    )


def lower_kernel(
    flags, act_early, act_late, rows_ref, own_ref, got_ref, cot_ref, early_ref, late_ref, keep_ref, first, second, sums_ref
):
    step = pl.program_id(0)
    total = dot(act_early[...], early_ref[...]) + dot(act_late[...], late_ref[...])
    cot = cot_ref[...].astype(jnp.float32)

    @pl.when(step == 0)
    def _():
        sums_ref[...] = jnp.zeros_like(sums_ref)

    send_or_keep(
        total,
        total + sum(ref[...].astype(jnp.float32) for ref in (rows_ref, own_ref, got_ref)),
        first,
        second,
        keep_ref,
    )
    mine = jnp.where(step < pl.num_programs(0) // 2, 0.0, 1.0)
    block = total + mine * sum(ref[...].astype(jnp.float32) for ref in (rows_ref, own_ref, got_ref))
    sums_ref[0:1, :] += jnp.sum(block * cot, axis=0, keepdims=True)


def send_or_keep(sent, kept, first, second, keep_ref):
    step = pl.program_id(0)
    for j, ref in enumerate((first, second)):

        @pl.when(step == j)
        def _():
            ref[...] = sent.astype(ref.dtype)

    @pl.when(step >= 2)
    def _():
        keep_ref[...] = kept


def theirs_first(i, flags, *more):
    return lax.rem((1 - flags[1]) * 2 + i, 4)


def sent_and_kept(whole, width):
    rows = whole // 4
    keep = ((2 * rows, width), jnp.float32, (rows, width), lambda i, *scalars: (jnp.maximum(i - 2, 0), 0))
    send = ((rows, width), jnp.bfloat16)
    return [keep, send, send, ((8, width), jnp.float32)]


def lower(flags, act_early, act_late, down_early, down_late, rows, own, got, cot):
    whole, width = rows.shape
    fields = [by_rows(field, whole // 4, theirs_first) for field in (act_early, act_late, rows, own, got, cot)]
    return streamed(
        lower_kernel, 4, [flags], fields + [down_early, down_late], sent_and_kept(whole, width), [], 6, SNUG
    )


def middle_kernel(
    flags, rows_ref, own_ref, got_ref, cot_ref, back_own, back_got, mixed_ref,
    vectors, w_ref, grad_ref, gmixed_ref, gout_ref, sums_ref, gout,
):
    step, last = pl.program_id(0), pl.num_programs(0) - 1
    unit, scale = norm_parts(sum(ref[...].astype(jnp.float32) for ref in (rows_ref, own_ref, got_ref)))
    back = sum(ref[...].astype(jnp.float32) for ref in (back_own, back_got))
    inner = back * vectors[2:3, :]
    mean = jnp.mean(inner, axis=-1, keepdims=True)
    slant = jnp.mean(inner * unit, axis=-1, keepdims=True)
    grad = cot_ref[...].astype(jnp.float32) + scale * (inner - mean - unit * slant)
    low = grad.astype(jnp.bfloat16)
    grad_ref[...] = low
    gmixed_ref[...] = dot(low, w_ref[...], NT).astype(jnp.bfloat16)
    part = dot(grad.T.astype(jnp.bfloat16), mixed_ref[...])

    @pl.when(step == 0)
    def _():
        gout[...] = part
        sums_ref[...] = jnp.zeros_like(sums_ref)

    @pl.when(step > 0)
    def _():
        gout[...] += part

    @pl.when(step == last)
    def _():
        gout_ref[...] = gout[...].astype(jnp.bfloat16)

    @pl.when(step // ((last + 1) // 2) == flags[1])
    def _():
        sums_ref[0:1, :] += jnp.sum(back * unit, axis=0, keepdims=True)
        sums_ref[1:2, :] += jnp.sum(back, axis=0, keepdims=True)


def middle(flags, fields, mixed, vectors, bundle):
    whole, width = fields[0].shape
    columns = mixed.shape[1]
    low = jnp.bfloat16
    in_order = lambda i, *scalars: (i, 0)
    return streamed(
        middle_kernel,
        whole // ROWS,
        [flags],
        [by_rows(field, ROWS) for field in (*fields, mixed)]
        + [vectors, (bundle, (columns, width), lambda i, *scalars: (0, 0))],
        [
            ((whole, width), low, (ROWS, width), in_order),
            ((whole, columns), low, (ROWS, columns), in_order),
            ((width, columns), low),
            ((8, width), jnp.float32),
        ],
        [((width, columns), jnp.float32)],
        8,
    )


def weigh_kernel(flags, turned_ref, out_grad_ref, grad_ref, *out_refs):
    last = grad_ref.shape[0]
    for j, out_ref in enumerate(out_refs):
        piece = 2 * (flags[2] ^ (j // 2)) + (flags[3] ^ (j % 2))

        @pl.when(piece < last)
        def _():
            out_ref[...] = dot(turned_ref[...], grad_ref[jnp.minimum(piece, last - 1)]).astype(jnp.bfloat16)

        @pl.when(piece == last)
        def _():
            out_ref[...] = out_grad_ref[...]


def weigh(flags, turned, grad, out_grad):
    width, columns = turned.shape[0], grad.shape[2]
    piece = ((width, columns), jnp.bfloat16, (ROWS, columns), lambda i, flags: (i, 0))
    return streamed(
        weigh_kernel, width // ROWS, [flags], [by_rows(turned, ROWS), by_rows(out_grad, ROWS), grad], [piece] * 4, [], 4
    )


def unproject_kernel(flags, grad_ref, rows_ref, w_own, w_near, w_far, keep_ref, first, second, sums_ref, weight):
    @pl.when(pl.program_id(0) == 0)
    def _():
        join_rows(flags, w_own, w_near, w_far, weight)

    total = dot(grad_ref[0], weight[0], NT)
    for c in range(1, grad_ref.shape[0]):
        total = total + dot(grad_ref[c], weight[c], NT)
    unit, unused = norm_parts(rows_ref[...].astype(jnp.float32))

    @pl.when(pl.program_id(0) == 0)
    def _():
        sums_ref[...] = jnp.zeros_like(sums_ref)

    sums_ref[0:1, :] += jnp.sum(total * unit, axis=0, keepdims=True)
    sums_ref[1:2, :] += jnp.sum(total, axis=0, keepdims=True)
    send_or_keep(total, total, first, second, keep_ref)


def unproject(flags, grad, weights, rows):
    whole, width = rows.shape
    count, unused, columns = grad.shape
    grads = (grad, (count, whole // 4, columns), lambda i, flags: (0, theirs_first(i, flags), 0))
    fields = [grads, by_rows(rows, whole // 4, theirs_first), *weights]
    scratch = [((count, width, columns), jnp.bfloat16)]
    return streamed(unproject_kernel, 4, [flags], fields, sent_and_kept(whole, width), scratch, 5, SNUG + (4 << 20))


def last_kernel(
    flags, rows_ref, resid_ref, keep_ref, block_keep, got_first, got_second, block_first, block_second, vectors, out_ref
):
    first = pl.program_id(0) == 0
    unit, scale = norm_parts(rows_ref[...].astype(jnp.float32))
    got = jnp.where(first, got_first[...], got_second[...]).astype(jnp.float32)
    inner = (keep_ref[...] + got) * vectors[0:1, :]
    mean = jnp.mean(inner, axis=-1, keepdims=True)
    slant = jnp.mean(inner * unit, axis=-1, keepdims=True)
    grad = resid_ref[...].astype(jnp.float32) + scale * (inner - mean - unit * slant)
    out_ref[0] = grad.astype(jnp.bfloat16)
    got = jnp.where(first, block_first[...], block_second[...]).astype(jnp.float32)
    out_ref[1] = (block_keep[...] + got).astype(jnp.bfloat16)


def last(flags, rows, resid, keep, block_keep, got, vectors):
    half, width = keep.shape
    size = half // 2

    def mine(i, flags):
        return flags[1] * 2 + i

    out = ((2, half, width), jnp.bfloat16, (2, size, width), lambda i, flags: (0, i, 0))
    fields = [by_rows(rows, size, mine), by_rows(resid, size, mine), by_rows(keep, size), by_rows(block_keep, size)]
    return streamed(last_kernel, 2, [flags], fields + [*got, vectors], [out], [], 3)[0]


def past_kernel(dwa_ref, hist_ref, cot_ref, grad_ref, part_ref, sums_ref):
    @pl.when(pl.program_id(0) == 0)
    def _():
        sums_ref[...] = jnp.zeros_like(sums_ref)

    grad = cot_ref[...].astype(jnp.float32)
    total = jnp.zeros_like(grad)
    for j in range(hist_ref.shape[0]):
        field = hist_ref[j].astype(jnp.float32)
        total += dwa_ref[j] * field
        grad_ref[j] = (dwa_ref[j] * grad).astype(jnp.bfloat16)
        sums_ref[j : j + 1, :] += jnp.sum(field * grad, axis=0, keepdims=True)
    part_ref[...] = total


def past(dwa, history, cot):
    count, rows, width = history.shape
    layers = pl.BlockSpec((count, ROWS, width), lambda i: (0, i, 0))
    tokens = pl.BlockSpec((ROWS, width), lambda i: (i, 0))
    return pl.pallas_call(
        past_kernel,
        grid=(rows // ROWS,),
        in_specs=[pl.BlockSpec(memory_space=pltpu.SMEM), layers, tokens],
        out_specs=[layers, tokens, whole_spec((8, width))],
        out_shape=[
            jax.ShapeDtypeStruct(history.shape, jnp.bfloat16),
            jax.ShapeDtypeStruct((rows, width), jnp.float32),
            jax.ShapeDtypeStruct((8, width), jnp.float32),
        ],
        compiler_params=pltpu.CompilerParams(vmem_limit_bytes=ROOM),
        cost_estimate=lasting(3),
    )(dwa, history, cot)


def present_kernel(flags, weight_ref, part_ref, own_ref, got_ref, out_ref, grad_ref):
    here = jnp.where(flags[0] == 1, own_ref[1], got_ref[1]).astype(jnp.float32)
    out_ref[...] = (part_ref[...] + weight_ref[weight_ref.shape[0] - 1] * here).astype(jnp.bfloat16)
    grad_ref[...] = jnp.where(flags[0] == 1, own_ref[0], got_ref[0])


def present(flags, weight, part, own, got):
    rows, width = part.shape
    both = (2, ROWS, width), lambda i, *scalars: (0, i, 0)
    out = ((rows, width), jnp.bfloat16, (ROWS, width), lambda i, *scalars: (i, 0))
    fields = [by_rows(part, ROWS), (own, *both), (got, *both)]
    return streamed(present_kernel, rows // ROWS, [flags, weight], fields, [out] * 2, [], 2, SNUG)


def place_kernel(flags, here_ref, there_ref, qkv_ref, out_ref, up_ref, down_ref):
    near, far = flags[1], flags[2]
    part = out_ref.shape[1]
    for k in range(2):
        for c in range(2):
            field = jnp.where(near == c, here_ref[k ^ far], there_ref[k ^ far]).astype(jnp.float32)
            if 2 * k + c < 3:
                qkv_ref[2 * k + c] = field[:, :part]
            else:
                out_ref[...] = field[:, :part]
            for half in range(2):
                at = (2 * half + k) * part
                (up_ref, down_ref)[c][:, at : at + part] = field[:, (1 + half) * part : (2 + half) * part]


def place(flags, here, there):
    rows, part = here.shape[1], here.shape[2] // 3
    outs = [((3, rows, part), jnp.float32), ((rows, part), jnp.float32)]
    outs += [((rows, 4 * part), jnp.float32)] * 2
    return streamed(place_kernel, 1, [flags], [here, there], outs, [], 3, SNUG)


AXES = ("tp", "dp", "far", "near")


def moves(chosen, move):
    sizes = [lax.axis_size(name) for name in AXES]
    places = [place for place in itertools.product(*map(range, sizes)) if chosen(*place)]
    index = lambda place: functools.reduce(lambda at, step: at * step[0] + step[1], zip(sizes, place), 0)
    return [(index(place), index(move(*place))) for place in places]


def away(t, d, k, c):
    return t != c


def anyone(t, d, k, c):
    return True


def swap_diagonal(field):
    return lax.ppermute(field, AXES, moves(away, lambda t, d, k, c: (c, d, k, t)))


def send_to_owner(field, other_far, other_tp):
    return lax.ppermute(
        field,
        AXES,
        moves(
            away if not other_far and not other_tp else anyone,
            lambda t, d, k, c: (c, d, k ^ other_far, t ^ other_tp),
        ),
    )


def swap_far_away(field):
    return lax.ppermute(field, AXES, moves(away, lambda t, d, k, c: (t, d, 1 - k, c)))


def swap_far(field):
    return lax.ppermute(field, "far", [(0, 1), (1, 0)])


def swap_near(field):
    return lax.ppermute(field, "near", [(0, 1), (1, 0)])


def after(field, *others):
    return lax.optimization_barrier((field, *others))[0]


def ordered(own, other, first, axis=0):
    return jnp.where(
        first, jnp.concatenate([own, other], axis=axis), jnp.concatenate([other, own], axis=axis)
    )


def part_of(field, index, axis):
    size = field.shape[axis] // 2
    return lax.dynamic_slice_in_dim(field, index * size, size, axis)


def add(*fields):
    return sum(field.astype(jnp.float32) for field in fields).astype(jnp.bfloat16)


def scatter_plane(pieces):
    return lax.psum_scatter(pieces, ("tp", "far"), scatter_dimension=0, tiled=True)[0]


def scatter_rows(piece):
    return lax.psum_scatter(piece, "dp", scatter_dimension=0, tiled=True)


def move_rows(block):
    dps = lax.axis_size("dp")
    if dps > 8:
        return [scatter_rows(block)]
    block = block.reshape(dps, block.shape[0] // dps, block.shape[1])
    place = lax.axis_index("dp")
    moved = [lax.dynamic_index_in_dim(block, place, 0, keepdims=False)]
    for step in range(1, dps):
        sent = lax.dynamic_index_in_dim(block, lax.rem(place + step, dps), 0, keepdims=False)
        moved.append(lax.ppermute(sent, "dp", [(d, (d + step) % dps) for d in range(dps)]))
    return moved


def sum_over(field, name):
    size = lax.axis_size(name)
    bit = 1
    while bit < size:
        field = field + lax.ppermute(field, name, [(d, d ^ bit) for d in range(size)])
        bit *= 2
    return field


def local(
    layer_input,
    history,
    cotangent,
    lengths,
    dwa_weights,
    gain_one,
    bias_one,
    w_qkv,
    w_out,
    gain_two,
    bias_two,
    w_up,
    w_down,
):
    rows = layer_input.shape[1]
    whole = rows * lax.axis_size("tp")
    hist_count = history.shape[0]
    part, far, near = lax.axis_index("tp"), lax.axis_index("far"), lax.axis_index("near")
    same = near == part
    flags = jnp.stack([same.astype(jnp.int32), near, far, part])

    input_got = swap_diagonal(layer_input[0])
    qkv_near = swap_diagonal(part_of(w_qkv, far, 1))
    qkv_far = swap_far_away(qkv_near)
    early_got = jnp.concatenate([part_of(w_up, 0, 1), part_of(w_down, 0, 0)], axis=0)
    late_got = jnp.concatenate([part_of(w_up, 1, 1), part_of(w_down, 1, 0)], axis=0)
    last_own = jnp.concatenate([w_out, cotangent[0]], axis=0)
    vectors = jnp.stack([gain_one, bias_one, gain_two, bias_two])

    own_lengths = jnp.where(same, lengths, swap_near(lengths))[0]
    seq_owner, token_place = positions(own_lengths, whole)
    lane = jnp.arange(LANES, dtype=jnp.int32)
    member = seq_owner[:, None] == lane[None, :]
    apart = jnp.where(member | (lane >= lengths.shape[1])[None, :], 0.0, NEG_FILL).astype(jnp.bfloat16)
    member = member.astype(jnp.bfloat16)
    half_dim = HEAD_DIM // 2
    frequency = jnp.exp((lane % half_dim).astype(jnp.float32) * (-math.log(10000.0) / half_dim))
    angles = token_place.astype(jnp.float32)[:, None] * frequency[None, :]
    cos_table = jnp.cos(angles)
    sin_table = jnp.sin(angles) * jnp.where(lane % HEAD_DIM < half_dim, -1.0, 1.0)[None, :]
    grad_history, past_sum, sums_past = past(dwa_weights, history[:, 0], cotangent[0])

    input_half = jnp.where(same, layer_input[0], input_got)
    layer_rows = ordered(input_half, swap_near(input_half), near == 0)
    layer_rows, vectors, past_sum, cos_table, sin_table, apart, member = lax.optimization_barrier(
        (layer_rows, vectors, past_sum, cos_table, sin_table, apart, member)
    )
    early_got = swap_diagonal(after(early_got, input_got))
    last_got = swap_diagonal(after(last_own, input_got))
    projected, norm_one_t = project(
        flags, layer_rows, vectors, cos_table, sin_table, w_qkv, qkv_near, qkv_far
    )
    mixed, logs = attend(apart, member, projected, LONGEST)
    late_got = swap_diagonal(after(late_got, mixed))
    last_got = jnp.where(same, last_own, after(last_got, mixed))
    weight_out = last_got[: w_out.shape[0]]
    attn = jnp.dot(mixed, weight_out, preferred_element_type=jnp.float32).astype(jnp.bfloat16)
    attn_got = swap_near(attn)
    cot_half = last_got[w_out.shape[0] :]
    scalars = [flags, dwa_weights]
    fields = [layer_rows, attn, attn_got, cot_half, swap_near(cot_half), vectors]
    *kept, back, act_early, down_early, early_pieces = feed(True, scalars, fields, w_up, w_down, early_got)
    early_sum = scatter_plane(after(early_pieces, late_got))
    back, act_late, down_late, *late_owned = feed(
        False, [flags], [*kept, back], w_up, w_down, late_got
    )
    late_moved = [send_to_owner(late_owned[j], j // 2, j % 2) for j in range(4)]
    grad_down = kept[2]
    fields = [layer_rows, attn, attn_got, grad_down, back, swap_near(back)]
    grad_attn, grad_mixed, grad_out, sums_two = middle(flags, fields, mixed, vectors, last_got)
    grad_qkv = attend_back(
        apart, member, cos_table, sin_table, projected, grad_mixed, mixed, logs, LONGEST
    )
    grad_qkv, *late_moved = lax.optimization_barrier((grad_qkv, *late_moved))
    owned = weigh(flags, norm_one_t, grad_qkv, grad_out)
    moved = [send_to_owner(owned[j], j // 2, j % 2) for j in range(4)]
    early_sum = scatter_rows(after(early_sum, grad_qkv))
    late_sum = scatter_rows(add(jnp.where(same, late_owned[0], after(late_moved[0], owned[0])), *late_moved[1:]))
    keep, *send, sums_one = unproject(
        flags, after(grad_qkv, owned[0]), (w_qkv, qkv_near, qkv_far), layer_rows
    )
    block_keep, *block_send, sums_now = lower(
        flags, act_early, act_late, down_early, down_late, layer_rows, attn, attn_got, after(grad_down, keep)
    )
    sent = [*send, *block_send]
    keep, block_keep, *arrived = lax.optimization_barrier((keep, block_keep, *sent, *moved))
    sent, moved = arrived[:4], arrived[4:]
    attn_one = add(jnp.where(same, owned[0], moved[0]), *moved[1:])
    attn_moved = move_rows(attn_one)
    got = [swap_near(field) for field in sent]
    ours = last(flags, layer_rows, grad_attn, after(keep, attn_one), block_keep, got, vectors)
    early_sum = after(early_sum, attn_one)
    early_got = swap_diagonal(early_sum)
    small = jnp.concatenate([sums_one[:2], sums_two[:2], sums_now[:1], sums_past[:hist_count]], axis=0)
    small = after(small, ours)
    for name in ("tp", "far"):
        small = sum_over(small, name)
    theirs = swap_diagonal(ours)
    small, late_sum, early_sum, early_got, *attn_moved = lax.optimization_barrier(
        (small, late_sum, early_sum, early_got, *attn_moved)
    )
    for name in ("near", "dp"):
        small = sum_over(small, name)
    attn_sum = add(*attn_moved)
    blocks = jnp.concatenate([attn_sum, jnp.where(same, early_sum, early_got), late_sum], axis=1)
    here = jnp.stack([blocks, swap_far(blocks)])
    output, grad_input = present(flags, dwa_weights, past_sum, ours, theirs)
    grad_w_qkv, grad_w_out, grad_w_up, grad_w_down = place(flags, here, swap_near(here))

    return (
        output[None],
        grad_input[None],
        grad_history[:, None],
        jnp.sum(jnp.concatenate([small[5:], small[4:5] / dwa_weights[hist_count]], axis=0), axis=1),
        small[0],
        small[1],
        grad_w_qkv,
        grad_w_out.T,
        small[2],
        small[3],
        grad_w_up,
        grad_w_down.T,
    )


def positions(seq_lengths, token_count):
    seq_ends = jnp.cumsum(seq_lengths)
    seq_starts = seq_ends - seq_lengths
    token_index = jnp.arange(token_count, dtype=jnp.int32)
    seq_owner = jnp.sum((token_index[:, None] >= seq_ends[None, :]).astype(jnp.int32), axis=1)
    picked = (
        seq_owner[:, None] == jnp.arange(seq_lengths.shape[0], dtype=jnp.int32)[None, :]
    ).astype(jnp.int32)
    seq_begin = jnp.sum(picked * seq_starts[None, :], axis=1)
    return (seq_owner, token_index - seq_begin)


def solution(mesh):
    tps, dps, reps = (mesh.shape[name] for name in ("tp", "dp", "rep"))
    split = Mesh(mesh.devices.reshape(tps, dps, reps // 2, 2), AXES)
    in_specs = (
        P(("dp", "far", "near"), "tp", None),
        P(None, ("dp", "far", "near"), "tp", None),
        P(("dp", "far", "near"), "tp", None),
        P(("dp", "far", "near"), None),
        P(),
        P(),
        P(),
        P(None, None, "tp"),
        P("tp", None),
        P(),
        P(),
        P(None, "tp"),
        P("tp", None),
    )
    out_specs = (
        P(("dp", "far", "near"), "tp", None),
        P(("dp", "far", "near"), "tp", None),
        P(None, ("dp", "far", "near"), "tp", None),
        P(),
        P(),
        P(),
        P(None, "dp", "tp"),
        P("tp", "dp"),
        P(),
        P(),
        P("dp", "tp"),
        P("tp", "dp"),
    )
    return jax.shard_map(local, mesh=split, in_specs=in_specs, out_specs=out_specs, check_vma=False)
```

```python
import functools
import itertools
import math

import jax
import jax.numpy as jnp
from jax import lax
from jax.experimental import pallas as pl
from jax.experimental.pallas import tpu as pltpu
from jax.sharding import Mesh, PartitionSpec as P

HEAD_DIM = 64
LONGEST = 512
NEG_FILL = -1e30
NORM_EPS = 1e-05
RATE = 3e6
ROOM = 60 << 20
SNUG = 18 << 20


def lasting(microseconds):
    return pl.CostEstimate(flops=0, transcendentals=0, bytes_accessed=int(microseconds * RATE))


BLOCK = 256
LANES = 128
NT = (((1,), (1,)), ((), ()))


def dot(a, b, dims=(((1,), (0,)), ((), ()))):
    return lax.dot_general(a, b, dims, preferred_element_type=jnp.float32)


def spans(whole, reach):
    back = -(-(reach - 1) // BLOCK)
    runs = []
    for i in range(whole // BLOCK):
        count = min(i, back) + 1
        if runs and runs[-1][2] == count:
            runs[-1][1] = i + 1
        else:
            runs.append([i, i + 1, count])
    return runs


def each_block(whole, reach, body):
    for first, last, count in spans(whole, reach):

        def step(i, carry, count=count):
            body(i, i + 1 - count, count)
            return carry

        lax.fori_loop(first, last, step, 0)


def block_at(i, count=1):
    return pl.ds(pl.multiple_of(i * BLOCK, BLOCK), count * BLOCK)


def head_query(q_ref, apart_ref, i, head):
    lane = lax.broadcasted_iota(jnp.int32, (BLOCK, LANES), 1) // HEAD_DIM
    query = q_ref[block_at(i), :] * (HEAD_DIM**-0.5)
    query = jnp.where(lane == head, query, jnp.zeros_like(query))
    return query, jnp.concatenate([query, apart_ref[block_at(i), :]], axis=1)


def attend_kernel(reach, apart_ref, member_ref, q_ref, k_ref, v_ref, out_ref, logs_ref, keys):
    whole = q_ref.shape[0]
    lane = lax.broadcasted_iota(jnp.int32, (BLOCK, LANES), 1) // HEAD_DIM
    keys[:, :LANES] = k_ref[...]
    keys[:, LANES:] = member_ref[...]

    def one(i, first, count, head):
        unused, query = head_query(q_ref, apart_ref, i, head)
        own = dot(query, keys[block_at(i), :], NT)
        key_at = lax.broadcasted_iota(jnp.int32, own.shape, 1)
        query_at = lax.broadcasted_iota(jnp.int32, own.shape, 0)
        scores = jnp.where(key_at <= query_at, own, NEG_FILL)
        if count > 1:
            scores = jnp.concatenate([dot(query, keys[block_at(first, count - 1), :], NT), scores], axis=1)
        row_max = jnp.max(scores, axis=1, keepdims=True)
        exponent = jnp.exp(scores - row_max)
        row_sum = jnp.sum(exponent, axis=1, keepdims=True)
        mixed = dot(exponent.astype(jnp.bfloat16), v_ref[block_at(first, count), :]) * (1.0 / row_sum)
        return mixed, row_max + jnp.log(row_sum)

    def body(i, first, count):
        mixed, logs = zip(*[one(i, first, count, head) for head in range(2)])
        out_ref[block_at(i), :] = jnp.where(lane == 0, *mixed).astype(out_ref.dtype)
        turned = jnp.where(lane == 0, *logs).T
        for head in range(2):
            logs_ref[head : head + 1, block_at(i)] = turned[head * HEAD_DIM : head * HEAD_DIM + 1]

    each_block(whole, reach, body)


def attend(apart, member, projected, reach):
    count, whole, width = projected.shape

    def block(c):
        return pl.BlockSpec((None, whole, LANES), lambda p: (c, 0, p))

    table = pl.BlockSpec((whole, LANES), lambda p: (0, 0))
    return pl.pallas_call(
        functools.partial(attend_kernel, reach),
        grid=(width // LANES,),
        in_specs=[table, table, block(0), block(1), block(2)],
        out_specs=[
            pl.BlockSpec((whole, LANES), lambda p: (0, p)),
            pl.BlockSpec((None, 8, whole), lambda p: (p, 0, 0)),
        ],
        out_shape=[
            jax.ShapeDtypeStruct((whole, width), jnp.bfloat16),
            jax.ShapeDtypeStruct((width // LANES, 8, whole), jnp.float32),
        ],
        scratch_shapes=[pltpu.VMEM((whole, 2 * LANES), jnp.bfloat16)],
        compiler_params=pltpu.CompilerParams(vmem_limit_bytes=ROOM),
        cost_estimate=lasting(12),
    )(apart, member, projected, projected, projected)


def turn_back(field, cos, sin):
    half = HEAD_DIM // 2
    lane = lax.broadcasted_iota(jnp.int32, field.shape, 1) % HEAD_DIM
    crossed = jnp.where(lane < half, pltpu.roll(field, LANES - half, 1), pltpu.roll(field, half, 1))
    return field * cos - crossed * sin


def attend_back_kernel(
    reach, apart_ref, member_ref, cos_ref, sin_ref, q_ref, k_ref, v_ref, g_ref, mixed_ref, logs_ref, out_ref,
    keys, keys_t, key_acc, value_acc
):
    whole = q_ref.shape[0]
    lane = lax.broadcasted_iota(jnp.int32, (BLOCK, LANES), 1) // HEAD_DIM
    keys[:, :LANES] = k_ref[...]
    keys[:, LANES:] = member_ref[...]
    keys_t[...] = k_ref[...].astype(jnp.float32).T.astype(jnp.bfloat16)
    key_acc[...] = jnp.zeros_like(key_acc)
    value_acc[...] = jnp.zeros_like(value_acc)

    def one(i, first, count, head):
        span = block_at(first, count)
        plain, query = head_query(q_ref, apart_ref, i, head)
        grad = g_ref[block_at(i), :]
        grad = jnp.where(lane == head, grad, jnp.zeros_like(grad))
        own = dot(keys[block_at(i), :], query, NT)
        key_at = lax.broadcasted_iota(jnp.int32, own.shape, 0)
        query_at = lax.broadcasted_iota(jnp.int32, own.shape, 1)
        scores = jnp.where(key_at <= query_at, own, NEG_FILL)
        if count > 1:
            scores = jnp.concatenate([dot(keys[block_at(first, count - 1), :], query, NT), scores], axis=0)
        probs = jnp.exp(scores - logs_ref[head : head + 1, block_at(i)])
        grad_values = dot(probs.astype(jnp.bfloat16), grad)
        product = grad.astype(jnp.float32) * mixed_ref[block_at(i), :].astype(jnp.float32)
        high = product.astype(jnp.bfloat16)
        ones = jnp.ones((8, LANES), jnp.bfloat16)
        row_dot = dot(ones, high, NT) + dot(ones, (product - high.astype(jnp.float32)).astype(jnp.bfloat16), NT)
        grad_scores = (probs * (dot(v_ref[span, :], grad, NT) - row_dot[:1])).astype(jnp.bfloat16)
        here = dot(keys_t[:, span], grad_scores)
        return grad_values, dot(grad_scores, plain), here

    def body(i, first, count):
        span, at = block_at(first, count), block_at(i)
        values, keys_, queries = zip(*[one(i, first, count, head) for head in range(2)])
        value_acc[span, :] += values[0] + values[1]
        key_acc[span, :] += keys_[0] + keys_[1]
        row = lax.broadcasted_iota(jnp.int32, queries[0].shape, 0) // HEAD_DIM
        both = jnp.where(row == 0, *queries).T * (HEAD_DIM**-0.5)
        out_ref[0, at, :] = turn_back(both, cos_ref[at, :], sin_ref[at, :]).astype(out_ref.dtype)

    each_block(whole, reach, body)

    def finish(i, carry):
        at = block_at(i)
        out_ref[1, at, :] = turn_back(key_acc[at, :], cos_ref[at, :], sin_ref[at, :]).astype(out_ref.dtype)
        out_ref[2, at, :] = value_acc[at, :].astype(out_ref.dtype)
        return carry

    lax.fori_loop(0, whole // BLOCK, finish, 0)


def attend_back(apart, member, cos, sin, projected, grad_mixed, mixed, logs, reach):
    count, whole, width = projected.shape

    def block(c):
        return pl.BlockSpec((None, whole, LANES), lambda p: (c, 0, p))

    table = pl.BlockSpec((whole, LANES), lambda p: (0, 0))
    return pl.pallas_call(
        functools.partial(attend_back_kernel, reach),
        grid=(width // LANES,),
        in_specs=[table] * 4
        + [block(0), block(1), block(2)]
        + [pl.BlockSpec((whole, LANES), lambda p: (0, p))] * 2
        + [pl.BlockSpec((None, 8, whole), lambda p: (p, 0, 0))],
        out_specs=pl.BlockSpec((count, whole, LANES), lambda p: (0, 0, p)),
        out_shape=jax.ShapeDtypeStruct((count, whole, width), jnp.bfloat16),
        scratch_shapes=[
            pltpu.VMEM((whole, 2 * LANES), jnp.bfloat16),
            pltpu.VMEM((LANES, whole), jnp.bfloat16),
            pltpu.VMEM((whole, LANES), jnp.float32),
            pltpu.VMEM((whole, LANES), jnp.float32),
        ],
        compiler_params=pltpu.CompilerParams(vmem_limit_bytes=ROOM),
        cost_estimate=lasting(22),
    )(apart, member, cos, sin, projected, projected, projected, grad_mixed, mixed, logs)


ROWS = 256


def norm_parts(field):
    centered = field - jnp.mean(field, axis=-1, keepdims=True)
    scale = lax.rsqrt(jnp.mean(centered * centered, axis=-1, keepdims=True) + NORM_EPS)
    return centered * scale, scale


def wide(ref, at):
    return ref[at, :].astype(jnp.float32)


def row_blocks(count, body):
    def step(i, carry):
        body(i, pl.ds(pl.multiple_of(i * ROWS, ROWS), ROWS))
        return carry

    lax.fori_loop(0, count // ROWS, step, 0)


TALL = 512


def streamed(kernel, steps, scalars, fields, outs, scratch, microseconds, room=ROOM):
    def spec(shape, block=None, at=None):
        if block is None:
            return pl.BlockSpec(shape, lambda i, *scalars: (0,) * len(shape))
        return pl.BlockSpec(block, at)

    fields = [field if isinstance(field, tuple) else (field,) for field in fields]
    return pl.pallas_call(
        kernel,
        grid_spec=pltpu.PrefetchScalarGridSpec(
            num_scalar_prefetch=len(scalars),
            grid=(steps,),
            in_specs=[spec(field[0].shape, *field[1:]) for field in fields],
            out_specs=[spec(out[0], *out[2:]) for out in outs],
            scratch_shapes=[pltpu.VMEM(shape, dtype) for shape, dtype in scratch],
        ),
        out_shape=[jax.ShapeDtypeStruct(*out[:2]) for out in outs],
        compiler_params=pltpu.CompilerParams(vmem_limit_bytes=room),
        cost_estimate=lasting(microseconds),
    )(*scalars, *[field[0] for field in fields])


def by_rows(field, rows, shift=None):
    if shift is None:
        return field, (rows, field.shape[1]), lambda i, *scalars: (i, 0)
    return field, (rows, field.shape[1]), lambda i, *scalars: (shift(i, *scalars), 0)


def whole_spec(shape):
    return pl.BlockSpec(shape, lambda *at: (0,) * len(shape))


def turn(field, cos, sin):
    half = HEAD_DIM // 2
    lane = lax.broadcasted_iota(jnp.int32, field.shape, 1) % HEAD_DIM
    crossed = jnp.where(lane < half, pltpu.roll(field, LANES - half, 1), pltpu.roll(field, half, 1))
    return field * cos + crossed * sin


def join_rows(flags, own, near, far, out):
    half = near.shape[1]
    for index, got in ((flags[2], near), (1 - flags[2], far)):
        at = pl.ds(pl.multiple_of(index * half, half), half)
        out[:, at, :] = jnp.where(flags[0] == 1, own[:, at, :], got[...])


def project_kernel(flags, rows_ref, cos_ref, sin_ref, vectors, w_own, w_near, w_far, out_ref, turned_ref, weight_ref):
    @pl.when(pl.program_id(0) == 0)
    def _():
        join_rows(flags, w_own, w_near, w_far, weight_ref)

    unit, unused = norm_parts(rows_ref[...].astype(jnp.float32))
    norm = unit * vectors[0:1, :] + vectors[1:2, :]
    turned_ref[...] = norm.T.astype(jnp.bfloat16)
    norm = norm.astype(jnp.bfloat16)
    for c in range(weight_ref.shape[0]):
        field = dot(norm, weight_ref[c])
        if c == 2:
            out_ref[c] = field.astype(jnp.bfloat16)
        else:
            for p in range(field.shape[1] // LANES):
                lanes = slice(p * LANES, (p + 1) * LANES)
                out_ref[c, :, lanes] = turn(field[:, lanes], cos_ref[...], sin_ref[...]).astype(jnp.bfloat16)


def project(flags, rows, vectors, cos, sin, w_own, w_near, w_far):
    whole, width = rows.shape
    count, unused, columns = w_own.shape
    low = jnp.bfloat16
    return streamed(
        project_kernel,
        whole // ROWS,
        [flags],
        [by_rows(rows, ROWS), by_rows(cos, ROWS), by_rows(sin, ROWS), vectors, w_own, w_near, w_far],
        [
            ((count, whole, columns), low, (count, ROWS, columns), lambda i, flags: (0, i, 0)),
            ((width, whole), low, (width, ROWS), lambda i, flags: (0, i)),
        ],
        [(w_own.shape, low)],
        8,
    )


def gelu_both(up):
    root = math.sqrt(2.0 / math.pi)
    square = up * up
    bent = jnp.tanh(root * up * (1.0 + 0.044715 * square))
    half = 0.5 * (1.0 + bent)
    slope = half + 0.5 * up * (1.0 - bent * bent) * (root * (1.0 + 3.0 * 0.044715 * square))
    return up * half, slope


def feed_kernel(early, *refs):
    if early:
        flags, weight_ref, rows_ref, own_ref, got_ref, cot_here, cot_there, vectors, up_own, down_own, got = refs[:11]
        norm, norm_t, grad, grad_t, back_ref, act_ref, down_ref, pieces = refs[11:19]
    else:
        flags, norm, norm_t, grad, grad_t, back_early, up_own, down_own, got = refs[:9]
        back_ref, act_ref, down_ref, *pieces = refs[9:16]
    up_got, down_got = got.at[: norm.shape[1]], got.at[norm.shape[1] :]
    up_w, up_sum, down_sum = refs[-3:]
    part = up_w.shape[1] // 2
    step, last = pl.program_id(0), pl.num_programs(0) - 1

    @pl.when(step == 0)
    def _():
        up_w[...] = jnp.where(flags[0] == 1, up_own[...], up_got[...])
        down_ref[...] = jnp.where(flags[0] == 1, down_own[...], down_got[...])

    if early:

        def head(i, at):
            unit, unused = norm_parts(wide(rows_ref, at) + wide(own_ref, at) + wide(got_ref, at))
            field = unit * vectors[2:3, :] + vectors[3:4, :]
            norm[at, :] = field.astype(jnp.bfloat16)
            norm_t[:, at] = field.T.astype(jnp.bfloat16)
            cot = jnp.where(flags[1] == step, cot_here[at, :], cot_there[at, :])
            field = cot.astype(jnp.float32) * weight_ref[weight_ref.shape[0] - 1]
            grad[at, :] = field.astype(jnp.bfloat16)
            grad_t[:, at] = field.T.astype(jnp.bfloat16)

        row_blocks(norm.shape[0], head)
    value, rise = gelu_both(dot(norm[...], up_w[...]))
    act_ref[...] = value.astype(jnp.bfloat16)
    slope = (dot(grad[...], down_ref[...], NT) * rise).astype(jnp.bfloat16)
    back = dot(slope, up_w[...], NT)
    if not early:
        back = back + back_early[...].astype(jnp.float32)
    back_ref[...] = back.astype(jnp.bfloat16)

    def store(p, at, low):
        if early:
            pieces[p, at, :] = low
            return
        slot = 2 * (flags[2] ^ (p % 2)) + (flags[3] ^ (p // 2))
        for j, piece in enumerate(pieces):

            @pl.when(slot == j)
            def _():
                piece[at, :] = low

    def grads(i, at):
        fields = (dot(norm_t[at, :], slope), dot(grad_t[at, :], act_ref[...]))
        for k, (field, total) in enumerate(zip(fields, (up_sum, down_sum))):

            @pl.when(step == 0)
            def _():
                total[at, :] = field

            @pl.when(step == last)
            def _():
                low = (total[at, :] + field).astype(jnp.bfloat16)
                for p in range(2):
                    store(2 * k + p, at, low[:, p * part : (p + 1) * part])

    row_blocks(norm_t.shape[0], grads)


def feed(early, scalars, fields, w_up, w_down, got):
    whole, width = fields[0].shape
    hidden = w_up.shape[1] // 2
    rows = whole // 2
    half = 0 if early else 1
    low = jnp.bfloat16

    def across(i, *scalars):
        return (0, i)

    tokens = ((whole, width), low, (rows, width), lambda i, *scalars: (i, 0))
    turned = ((width, whole), low, (width, rows), across)
    if early:
        operands = [by_rows(field, rows) for field in fields[:3]] + [*fields[3:]]
        outs = [tokens, turned, tokens, turned]
        pieces = [((4, width, hidden // 2), low)]
    else:
        operands = [by_rows(fields[0], rows), (fields[1], (width, rows), across)]
        operands += [by_rows(fields[2], rows), (fields[3], (width, rows), across), by_rows(fields[4], rows)]
        outs = []
        pieces = [((width, hidden // 2), low)] * 4
    operands += [
        (w_up, (width, hidden), lambda i, *scalars: (0, half)),
        (w_down, (hidden, width), lambda i, *scalars: (half, 0)),
        got,
    ]
    outs += [tokens, ((whole, hidden), low, (rows, hidden), lambda i, *scalars: (i, 0)), ((hidden, width), low)]
    sums = ((width, hidden), jnp.float32)
    return streamed(
        functools.partial(feed_kernel, early), 2, scalars, operands, outs + pieces, [((width, hidden), low), sums, sums], 17
    )


def lower_kernel(
    flags, act_early, act_late, rows_ref, own_ref, got_ref, cot_ref, early_ref, late_ref, keep_ref, first, second, sums_ref
):
    step = pl.program_id(0)
    total = dot(act_early[...], early_ref[...]) + dot(act_late[...], late_ref[...])
    cot = cot_ref[...].astype(jnp.float32)

    @pl.when(step == 0)
    def _():
        sums_ref[...] = jnp.zeros_like(sums_ref)

    send_or_keep(
        total,
        total + sum(ref[...].astype(jnp.float32) for ref in (rows_ref, own_ref, got_ref)),
        first,
        second,
        keep_ref,
    )
    mine = jnp.where(step < pl.num_programs(0) // 2, 0.0, 1.0)
    block = total + mine * sum(ref[...].astype(jnp.float32) for ref in (rows_ref, own_ref, got_ref))
    sums_ref[0:1, :] += jnp.sum(block * cot, axis=0, keepdims=True)


def send_or_keep(sent, kept, first, second, keep_ref):
    step = pl.program_id(0)
    for j, ref in enumerate((first, second)):

        @pl.when(step == j)
        def _():
            ref[...] = sent.astype(ref.dtype)

    @pl.when(step >= 2)
    def _():
        keep_ref[...] = kept


def theirs_first(i, flags, *more):
    return lax.rem((1 - flags[1]) * 2 + i, 4)


def sent_and_kept(whole, width):
    rows = whole // 4
    keep = ((2 * rows, width), jnp.float32, (rows, width), lambda i, *scalars: (jnp.maximum(i - 2, 0), 0))
    send = ((rows, width), jnp.bfloat16)
    return [keep, send, send, ((8, width), jnp.float32)]


def lower(flags, act_early, act_late, down_early, down_late, rows, own, got, cot):
    whole, width = rows.shape
    fields = [by_rows(field, whole // 4, theirs_first) for field in (act_early, act_late, rows, own, got, cot)]
    return streamed(
        lower_kernel, 4, [flags], fields + [down_early, down_late], sent_and_kept(whole, width), [], 6, SNUG
    )


def middle_kernel(
    flags, rows_ref, own_ref, got_ref, cot_ref, back_own, back_got, mixed_ref,
    vectors, w_ref, grad_ref, gmixed_ref, gout_ref, sums_ref, gout,
):
    step, last = pl.program_id(0), pl.num_programs(0) - 1
    unit, scale = norm_parts(sum(ref[...].astype(jnp.float32) for ref in (rows_ref, own_ref, got_ref)))
    back = sum(ref[...].astype(jnp.float32) for ref in (back_own, back_got))
    inner = back * vectors[2:3, :]
    mean = jnp.mean(inner, axis=-1, keepdims=True)
    slant = jnp.mean(inner * unit, axis=-1, keepdims=True)
    grad = cot_ref[...].astype(jnp.float32) + scale * (inner - mean - unit * slant)
    low = grad.astype(jnp.bfloat16)
    grad_ref[...] = low
    gmixed_ref[...] = dot(low, w_ref[...], NT).astype(jnp.bfloat16)
    part = dot(grad.T.astype(jnp.bfloat16), mixed_ref[...])

    @pl.when(step == 0)
    def _():
        gout[...] = part
        sums_ref[...] = jnp.zeros_like(sums_ref)

    @pl.when(step > 0)
    def _():
        gout[...] += part

    @pl.when(step == last)
    def _():
        gout_ref[...] = gout[...].astype(jnp.bfloat16)

    @pl.when(step // ((last + 1) // 2) == flags[1])
    def _():
        sums_ref[0:1, :] += jnp.sum(back * unit, axis=0, keepdims=True)
        sums_ref[1:2, :] += jnp.sum(back, axis=0, keepdims=True)


def middle(flags, fields, mixed, vectors, bundle):
    whole, width = fields[0].shape
    columns = mixed.shape[1]
    low = jnp.bfloat16
    in_order = lambda i, *scalars: (i, 0)
    return streamed(
        middle_kernel,
        whole // ROWS,
        [flags],
        [by_rows(field, ROWS) for field in (*fields, mixed)]
        + [vectors, (bundle, (columns, width), lambda i, *scalars: (0, 0))],
        [
            ((whole, width), low, (ROWS, width), in_order),
            ((whole, columns), low, (ROWS, columns), in_order),
            ((width, columns), low),
            ((8, width), jnp.float32),
        ],
        [((width, columns), jnp.float32)],
        8,
    )


def weigh_kernel(flags, turned_ref, out_grad_ref, query_ref, key_ref, value_ref, *out_refs):
    rows = turned_ref[...]
    fields = [dot(rows, ref[...]).astype(jnp.bfloat16) for ref in (query_ref, key_ref, value_ref)]
    for piece, field in enumerate([*fields, out_grad_ref[...]]):
        slot = 2 * (flags[2] ^ (piece // 2)) + (flags[3] ^ (piece % 2))
        for j, out_ref in enumerate(out_refs):

            @pl.when(slot == j)
            def _():
                out_ref[...] = field


def weigh(flags, turned, grad, out_grad):
    width, columns = turned.shape[0], grad.shape[2]
    piece = ((width, columns), jnp.bfloat16, (ROWS, columns), lambda i, flags: (i, 0))
    fields = [by_rows(turned, ROWS), by_rows(out_grad, ROWS)]
    for c in range(3):
        fields.append((grad, (None, *grad.shape[1:]), lambda i, flags, c=c: (c, 0, 0)))
    return streamed(weigh_kernel, width // ROWS, [flags], fields, [piece] * 4, [], 4)


def unproject_kernel(flags, grad_ref, rows_ref, w_own, w_near, w_far, keep_ref, first, second, sums_ref, weight):
    @pl.when(pl.program_id(0) == 0)
    def _():
        join_rows(flags, w_own, w_near, w_far, weight)

    total = dot(grad_ref[0], weight[0], NT)
    for c in range(1, grad_ref.shape[0]):
        total = total + dot(grad_ref[c], weight[c], NT)
    unit, unused = norm_parts(rows_ref[...].astype(jnp.float32))

    @pl.when(pl.program_id(0) == 0)
    def _():
        sums_ref[...] = jnp.zeros_like(sums_ref)

    sums_ref[0:1, :] += jnp.sum(total * unit, axis=0, keepdims=True)
    sums_ref[1:2, :] += jnp.sum(total, axis=0, keepdims=True)
    send_or_keep(total, total, first, second, keep_ref)


def unproject(flags, grad, weights, rows):
    whole, width = rows.shape
    count, unused, columns = grad.shape
    grads = (grad, (count, whole // 4, columns), lambda i, flags: (0, theirs_first(i, flags), 0))
    fields = [grads, by_rows(rows, whole // 4, theirs_first), *weights]
    scratch = [((count, width, columns), jnp.bfloat16)]
    return streamed(unproject_kernel, 4, [flags], fields, sent_and_kept(whole, width), scratch, 5, SNUG + (4 << 20))


def last_kernel(
    flags, rows_ref, resid_ref, keep_ref, block_keep, got_first, got_second, block_first, block_second, vectors, out_ref
):
    first = pl.program_id(0) == 0
    unit, scale = norm_parts(rows_ref[...].astype(jnp.float32))
    got = jnp.where(first, got_first[...], got_second[...]).astype(jnp.float32)
    inner = (keep_ref[...] + got) * vectors[0:1, :]
    mean = jnp.mean(inner, axis=-1, keepdims=True)
    slant = jnp.mean(inner * unit, axis=-1, keepdims=True)
    grad = resid_ref[...].astype(jnp.float32) + scale * (inner - mean - unit * slant)
    out_ref[0] = grad.astype(jnp.bfloat16)
    got = jnp.where(first, block_first[...], block_second[...]).astype(jnp.float32)
    out_ref[1] = (block_keep[...] + got).astype(jnp.bfloat16)


def last(flags, rows, resid, keep, block_keep, got, vectors):
    half, width = keep.shape
    size = half // 2

    def mine(i, flags):
        return flags[1] * 2 + i

    out = ((2, half, width), jnp.bfloat16, (2, size, width), lambda i, flags: (0, i, 0))
    fields = [by_rows(rows, size, mine), by_rows(resid, size, mine), by_rows(keep, size), by_rows(block_keep, size)]
    return streamed(last_kernel, 2, [flags], fields + [*got, vectors], [out], [], 3)[0]


def past_kernel(dwa_ref, hist_ref, cot_ref, grad_ref, part_ref, sums_ref):
    @pl.when(pl.program_id(0) == 0)
    def _():
        sums_ref[...] = jnp.zeros_like(sums_ref)

    grad = cot_ref[...].astype(jnp.float32)
    total = jnp.zeros_like(grad)
    for j in range(hist_ref.shape[0]):
        field = hist_ref[j].astype(jnp.float32)
        total += dwa_ref[j] * field
        grad_ref[j] = (dwa_ref[j] * grad).astype(jnp.bfloat16)
        sums_ref[j : j + 1, :] += jnp.sum(field * grad, axis=0, keepdims=True)
    part_ref[...] = total


def past(dwa, history, cot):
    count, rows, width = history.shape
    layers = pl.BlockSpec((count, ROWS, width), lambda i: (0, i, 0))
    tokens = pl.BlockSpec((ROWS, width), lambda i: (i, 0))
    return pl.pallas_call(
        past_kernel,
        grid=(rows // ROWS,),
        in_specs=[pl.BlockSpec(memory_space=pltpu.SMEM), layers, tokens],
        out_specs=[layers, tokens, whole_spec((8, width))],
        out_shape=[
            jax.ShapeDtypeStruct(history.shape, jnp.bfloat16),
            jax.ShapeDtypeStruct((rows, width), jnp.float32),
            jax.ShapeDtypeStruct((8, width), jnp.float32),
        ],
        compiler_params=pltpu.CompilerParams(vmem_limit_bytes=ROOM),
        cost_estimate=lasting(3),
    )(dwa, history, cot)


def present_kernel(flags, weight_ref, part_ref, own_ref, got_ref, out_ref, grad_ref):
    here = jnp.where(flags[0] == 1, own_ref[1], got_ref[1]).astype(jnp.float32)
    out_ref[...] = (part_ref[...] + weight_ref[weight_ref.shape[0] - 1] * here).astype(jnp.bfloat16)
    grad_ref[...] = jnp.where(flags[0] == 1, own_ref[0], got_ref[0])


def present(flags, weight, part, own, got):
    rows, width = part.shape
    both = (2, ROWS, width), lambda i, *scalars: (0, i, 0)
    out = ((rows, width), jnp.bfloat16, (ROWS, width), lambda i, *scalars: (i, 0))
    fields = [by_rows(part, ROWS), (own, *both), (got, *both)]
    return streamed(present_kernel, rows // ROWS, [flags, weight], fields, [out] * 2, [], 2, SNUG)


def place_kernel(flags, here_ref, there_ref, qkv_ref, out_ref, up_ref, down_ref):
    near, far = flags[1], flags[2]
    part = out_ref.shape[1]
    for k in range(2):
        for c in range(2):
            field = jnp.where(near == c, here_ref[k ^ far], there_ref[k ^ far]).astype(jnp.float32)
            if 2 * k + c < 3:
                qkv_ref[2 * k + c] = field[:, :part]
            else:
                out_ref[...] = field[:, :part]
            for half in range(2):
                at = (2 * half + k) * part
                (up_ref, down_ref)[c][:, at : at + part] = field[:, (1 + half) * part : (2 + half) * part]


def place(flags, here, there):
    rows, part = here.shape[1], here.shape[2] // 3
    outs = [((3, rows, part), jnp.float32), ((rows, part), jnp.float32)]
    outs += [((rows, 4 * part), jnp.float32)] * 2
    return streamed(place_kernel, 1, [flags], [here, there], outs, [], 3, SNUG)


AXES = ("tp", "dp", "far", "near")


def moves(chosen, move):
    sizes = [lax.axis_size(name) for name in AXES]
    places = [place for place in itertools.product(*map(range, sizes)) if chosen(*place)]
    index = lambda place: functools.reduce(lambda at, step: at * step[0] + step[1], zip(sizes, place), 0)
    return [(index(place), index(move(*place))) for place in places]


def away(t, d, k, c):
    return t != c


def anyone(t, d, k, c):
    return True


def swap_diagonal(field):
    return lax.ppermute(field, AXES, moves(away, lambda t, d, k, c: (c, d, k, t)))


def send_to_owner(field, other_far, other_tp):
    return lax.ppermute(
        field,
        AXES,
        moves(
            away if not other_far and not other_tp else anyone,
            lambda t, d, k, c: (c, d, k ^ other_far, t ^ other_tp),
        ),
    )


def swap_far_away(field):
    return lax.ppermute(field, AXES, moves(away, lambda t, d, k, c: (t, d, 1 - k, c)))


def swap_far(field):
    return lax.ppermute(field, "far", [(0, 1), (1, 0)])


def swap_near(field):
    return lax.ppermute(field, "near", [(0, 1), (1, 0)])


def after(field, *others):
    return lax.optimization_barrier((field, *others))[0]


def ordered(own, other, first, axis=0):
    return jnp.where(
        first, jnp.concatenate([own, other], axis=axis), jnp.concatenate([other, own], axis=axis)
    )


def part_of(field, index, axis):
    size = field.shape[axis] // 2
    return lax.dynamic_slice_in_dim(field, index * size, size, axis)


def add(*fields):
    return sum(field.astype(jnp.float32) for field in fields).astype(jnp.bfloat16)


def scatter_plane(pieces):
    return lax.psum_scatter(pieces, ("tp", "far"), scatter_dimension=0, tiled=True)[0]


def scatter_rows(piece):
    return lax.psum_scatter(piece, "dp", scatter_dimension=0, tiled=True)


def move_rows(block):
    dps = lax.axis_size("dp")
    if dps > 8:
        return [scatter_rows(block)]
    block = block.reshape(dps, block.shape[0] // dps, block.shape[1])
    place = lax.axis_index("dp")
    moved = [lax.dynamic_index_in_dim(block, place, 0, keepdims=False)]
    for step in range(1, dps):
        sent = lax.dynamic_index_in_dim(block, lax.rem(place + step, dps), 0, keepdims=False)
        moved.append(lax.ppermute(sent, "dp", [(d, (d + step) % dps) for d in range(dps)]))
    return moved


def sum_over(field, name):
    size = lax.axis_size(name)
    bit = 1
    while bit < size:
        field = field + lax.ppermute(field, name, [(d, d ^ bit) for d in range(size)])
        bit *= 2
    return field


def local(
    layer_input,
    history,
    cotangent,
    lengths,
    dwa_weights,
    gain_one,
    bias_one,
    w_qkv,
    w_out,
    gain_two,
    bias_two,
    w_up,
    w_down,
):
    rows = layer_input.shape[1]
    whole = rows * lax.axis_size("tp")
    hist_count = history.shape[0]
    part, far, near = lax.axis_index("tp"), lax.axis_index("far"), lax.axis_index("near")
    same = near == part
    flags = jnp.stack([same.astype(jnp.int32), near, far, part])

    input_got = swap_diagonal(layer_input[0])
    qkv_near = swap_diagonal(part_of(w_qkv, far, 1))
    qkv_far = swap_far_away(qkv_near)
    early_got = jnp.concatenate([part_of(w_up, 0, 1), part_of(w_down, 0, 0)], axis=0)
    late_got = jnp.concatenate([part_of(w_up, 1, 1), part_of(w_down, 1, 0)], axis=0)
    last_own = jnp.concatenate([w_out, cotangent[0]], axis=0)
    vectors = jnp.stack([gain_one, bias_one, gain_two, bias_two])

    own_lengths = jnp.where(same, lengths, swap_near(lengths))[0]
    seq_owner, token_place = positions(own_lengths, whole)
    lane = jnp.arange(LANES, dtype=jnp.int32)
    member = seq_owner[:, None] == lane[None, :]
    apart = jnp.where(member | (lane >= lengths.shape[1])[None, :], 0.0, NEG_FILL).astype(jnp.bfloat16)
    member = member.astype(jnp.bfloat16)
    half_dim = HEAD_DIM // 2
    frequency = jnp.exp((lane % half_dim).astype(jnp.float32) * (-math.log(10000.0) / half_dim))
    angles = token_place.astype(jnp.float32)[:, None] * frequency[None, :]
    cos_table = jnp.cos(angles)
    sin_table = jnp.sin(angles) * jnp.where(lane % HEAD_DIM < half_dim, -1.0, 1.0)[None, :]
    grad_history, past_sum, sums_past = past(dwa_weights, history[:, 0], cotangent[0])

    input_half = jnp.where(same, layer_input[0], input_got)
    layer_rows = ordered(input_half, swap_near(input_half), near == 0)
    layer_rows, vectors, past_sum, cos_table, sin_table, apart, member = lax.optimization_barrier(
        (layer_rows, vectors, past_sum, cos_table, sin_table, apart, member)
    )
    early_got = swap_diagonal(after(early_got, input_got))
    last_got = swap_diagonal(after(last_own, input_got))
    projected, norm_one_t = project(
        flags, layer_rows, vectors, cos_table, sin_table, w_qkv, qkv_near, qkv_far
    )
    mixed, logs = attend(apart, member, projected, LONGEST)
    late_got = swap_diagonal(after(late_got, mixed))
    last_got = jnp.where(same, last_own, after(last_got, mixed))
    weight_out = last_got[: w_out.shape[0]]
    attn = jnp.dot(mixed, weight_out, preferred_element_type=jnp.float32).astype(jnp.bfloat16)
    attn_got = swap_near(attn)
    cot_half = last_got[w_out.shape[0] :]
    scalars = [flags, dwa_weights]
    fields = [layer_rows, attn, attn_got, cot_half, swap_near(cot_half), vectors]
    *kept, back, act_early, down_early, early_pieces = feed(True, scalars, fields, w_up, w_down, early_got)
    early_sum = scatter_plane(after(early_pieces, late_got))
    back, act_late, down_late, *late_owned = feed(
        False, [flags], [*kept, back], w_up, w_down, late_got
    )
    late_moved = [send_to_owner(late_owned[j], j // 2, j % 2) for j in range(4)]
    grad_down = kept[2]
    fields = [layer_rows, attn, attn_got, grad_down, back, swap_near(back)]
    grad_attn, grad_mixed, grad_out, sums_two = middle(flags, fields, mixed, vectors, last_got)
    grad_qkv = attend_back(
        apart, member, cos_table, sin_table, projected, grad_mixed, mixed, logs, LONGEST
    )
    grad_qkv, *late_moved = lax.optimization_barrier((grad_qkv, *late_moved))
    owned = weigh(flags, norm_one_t, grad_qkv, grad_out)
    moved = [send_to_owner(owned[j], j // 2, j % 2) for j in range(4)]
    early_sum = scatter_rows(after(early_sum, grad_qkv))
    late_sum = scatter_rows(add(jnp.where(same, late_owned[0], after(late_moved[0], owned[0])), *late_moved[1:]))
    keep, *send, sums_one = unproject(
        flags, after(grad_qkv, owned[0]), (w_qkv, qkv_near, qkv_far), layer_rows
    )
    block_keep, *block_send, sums_now = lower(
        flags, act_early, act_late, down_early, down_late, layer_rows, attn, attn_got, after(grad_down, keep)
    )
    sent = [*send, *block_send]
    keep, block_keep, *arrived = lax.optimization_barrier((keep, block_keep, *sent, *moved))
    sent, moved = arrived[:4], arrived[4:]
    attn_one = add(jnp.where(same, owned[0], moved[0]), *moved[1:])
    attn_moved = move_rows(attn_one)
    got = [swap_near(field) for field in sent]
    ours = last(flags, layer_rows, grad_attn, after(keep, attn_one), block_keep, got, vectors)
    early_sum = after(early_sum, attn_one)
    early_got = swap_diagonal(early_sum)
    small = jnp.concatenate([sums_one[:2], sums_two[:2], sums_now[:1], sums_past[:hist_count]], axis=0)
    small = after(small, ours)
    for name in ("tp", "far"):
        small = sum_over(small, name)
    theirs = swap_diagonal(ours)
    small, late_sum, early_sum, early_got, *attn_moved = lax.optimization_barrier(
        (small, late_sum, early_sum, early_got, *attn_moved)
    )
    for name in ("near", "dp"):
        small = sum_over(small, name)
    attn_sum = add(*attn_moved)
    blocks = jnp.concatenate([attn_sum, jnp.where(same, early_sum, early_got), late_sum], axis=1)
    here = after(jnp.stack([blocks, swap_far(blocks)]), small)
    output, grad_input = present(flags, dwa_weights, past_sum, ours, theirs)
    grad_w_qkv, grad_w_out, grad_w_up, grad_w_down = place(flags, here, swap_near(here))

    return (
        output[None],
        grad_input[None],
        grad_history[:, None],
        jnp.sum(jnp.concatenate([small[5:], small[4:5] / dwa_weights[hist_count]], axis=0), axis=1),
        small[0],
        small[1],
        grad_w_qkv,
        grad_w_out.T,
        small[2],
        small[3],
        grad_w_up,
        grad_w_down.T,
    )


def positions(seq_lengths, token_count):
    seq_ends = jnp.cumsum(seq_lengths)
    seq_starts = seq_ends - seq_lengths
    token_index = jnp.arange(token_count, dtype=jnp.int32)
    seq_owner = jnp.sum((token_index[:, None] >= seq_ends[None, :]).astype(jnp.int32), axis=1)
    picked = (
        seq_owner[:, None] == jnp.arange(seq_lengths.shape[0], dtype=jnp.int32)[None, :]
    ).astype(jnp.int32)
    seq_begin = jnp.sum(picked * seq_starts[None, :], axis=1)
    return (seq_owner, token_index - seq_begin)


def solution(mesh):
    tps, dps, reps = (mesh.shape[name] for name in ("tp", "dp", "rep"))
    split = Mesh(mesh.devices.reshape(tps, dps, reps // 2, 2), AXES)
    in_specs = (
        P(("dp", "far", "near"), "tp", None),
        P(None, ("dp", "far", "near"), "tp", None),
        P(("dp", "far", "near"), "tp", None),
        P(("dp", "far", "near"), None),
        P(),
        P(),
        P(),
        P(None, None, "tp"),
        P("tp", None),
        P(),
        P(),
        P(None, "tp"),
        P("tp", None),
    )
    out_specs = (
        P(("dp", "far", "near"), "tp", None),
        P(("dp", "far", "near"), "tp", None),
        P(None, ("dp", "far", "near"), "tp", None),
        P(),
        P(),
        P(),
        P(None, "dp", "tp"),
        P("tp", "dp"),
        P(),
        P(),
        P("dp", "tp"),
        P("tp", "dp"),
    )
    return jax.shard_map(local, mesh=split, in_specs=in_specs, out_specs=out_specs, check_vma=False)
```

```python
import functools
import itertools
import math

import jax
import jax.numpy as jnp
from jax import lax
from jax.experimental import pallas as pl
from jax.experimental.pallas import tpu as pltpu
from jax.sharding import Mesh, PartitionSpec as P

HEAD_DIM = 64
LONGEST = 512
NEG_FILL = -1e30
NORM_EPS = 1e-05
RATE = 3e6
ROOM = 60 << 20
SNUG = 18 << 20


def lasting(microseconds):
    return pl.CostEstimate(flops=0, transcendentals=0, bytes_accessed=int(microseconds * RATE))


BLOCK = 256
LANES = 128
NT = (((1,), (1,)), ((), ()))


def dot(a, b, dims=(((1,), (0,)), ((), ()))):
    return lax.dot_general(a, b, dims, preferred_element_type=jnp.float32)


def spans(whole, reach):
    back = -(-(reach - 1) // BLOCK)
    runs = []
    for i in range(whole // BLOCK):
        count = min(i, back) + 1
        if runs and runs[-1][2] == count:
            runs[-1][1] = i + 1
        else:
            runs.append([i, i + 1, count])
    return runs


def each_block(whole, reach, body):
    for first, last, count in spans(whole, reach):

        def step(i, carry, count=count):
            body(i, i + 1 - count, count)
            return carry

        lax.fori_loop(first, last, step, 0)


def block_at(i, count=1):
    return pl.ds(pl.multiple_of(i * BLOCK, BLOCK), count * BLOCK)


def head_query(q_ref, apart_ref, i, head):
    lane = lax.broadcasted_iota(jnp.int32, (BLOCK, LANES), 1) // HEAD_DIM
    query = q_ref[block_at(i), :] * (HEAD_DIM**-0.5)
    query = jnp.where(lane == head, query, jnp.zeros_like(query))
    return query, jnp.concatenate([query, apart_ref[block_at(i), :]], axis=1)


def attend_kernel(reach, apart_ref, member_ref, q_ref, k_ref, v_ref, out_ref, logs_ref, keys):
    whole = q_ref.shape[0]
    lane = lax.broadcasted_iota(jnp.int32, (BLOCK, LANES), 1) // HEAD_DIM
    keys[:, :LANES] = k_ref[...]
    keys[:, LANES:] = member_ref[...]

    def one(i, first, count, head):
        unused, query = head_query(q_ref, apart_ref, i, head)
        own = dot(query, keys[block_at(i), :], NT)
        key_at = lax.broadcasted_iota(jnp.int32, own.shape, 1)
        query_at = lax.broadcasted_iota(jnp.int32, own.shape, 0)
        scores = jnp.where(key_at <= query_at, own, NEG_FILL)
        if count > 1:
            scores = jnp.concatenate([dot(query, keys[block_at(first, count - 1), :], NT), scores], axis=1)
        row_max = jnp.max(scores, axis=1, keepdims=True)
        exponent = jnp.exp(scores - row_max)
        row_sum = jnp.sum(exponent, axis=1, keepdims=True)
        mixed = dot(exponent.astype(jnp.bfloat16), v_ref[block_at(first, count), :]) * (1.0 / row_sum)
        return mixed, row_max + jnp.log(row_sum)

    def body(i, first, count):
        mixed, logs = zip(*[one(i, first, count, head) for head in range(2)])
        out_ref[block_at(i), :] = jnp.where(lane == 0, *mixed).astype(out_ref.dtype)
        turned = jnp.where(lane == 0, *logs).T
        for head in range(2):
            logs_ref[head : head + 1, block_at(i)] = turned[head * HEAD_DIM : head * HEAD_DIM + 1]

    each_block(whole, reach, body)


def attend(apart, member, projected, reach):
    count, whole, width = projected.shape

    def block(c):
        return pl.BlockSpec((None, whole, LANES), lambda p: (c, 0, p))

    table = pl.BlockSpec((whole, LANES), lambda p: (0, 0))
    return pl.pallas_call(
        functools.partial(attend_kernel, reach),
        grid=(width // LANES,),
        in_specs=[table, table, block(0), block(1), block(2)],
        out_specs=[
            pl.BlockSpec((whole, LANES), lambda p: (0, p)),
            pl.BlockSpec((None, 8, whole), lambda p: (p, 0, 0)),
        ],
        out_shape=[
            jax.ShapeDtypeStruct((whole, width), jnp.bfloat16),
            jax.ShapeDtypeStruct((width // LANES, 8, whole), jnp.float32),
        ],
        scratch_shapes=[pltpu.VMEM((whole, 2 * LANES), jnp.bfloat16)],
        compiler_params=pltpu.CompilerParams(vmem_limit_bytes=ROOM),
        cost_estimate=lasting(12),
    )(apart, member, projected, projected, projected)


def turn_back(field, cos, sin):
    half = HEAD_DIM // 2
    lane = lax.broadcasted_iota(jnp.int32, field.shape, 1) % HEAD_DIM
    crossed = jnp.where(lane < half, pltpu.roll(field, LANES - half, 1), pltpu.roll(field, half, 1))
    return field * cos - crossed * sin


def attend_back_kernel(
    reach, apart_ref, member_ref, cos_ref, sin_ref, q_ref, k_ref, v_ref, g_ref, mixed_ref, logs_ref, out_ref,
    keys, keys_t, key_acc, value_acc
):
    whole = q_ref.shape[0]
    lane = lax.broadcasted_iota(jnp.int32, (BLOCK, LANES), 1) // HEAD_DIM
    keys[:, :LANES] = k_ref[...]
    keys[:, LANES:] = member_ref[...]
    keys_t[...] = k_ref[...].astype(jnp.float32).T.astype(jnp.bfloat16)
    key_acc[...] = jnp.zeros_like(key_acc)
    value_acc[...] = jnp.zeros_like(value_acc)

    def one(i, first, count, head):
        span = block_at(first, count)
        plain, query = head_query(q_ref, apart_ref, i, head)
        grad = g_ref[block_at(i), :]
        grad = jnp.where(lane == head, grad, jnp.zeros_like(grad))
        own = dot(keys[block_at(i), :], query, NT)
        key_at = lax.broadcasted_iota(jnp.int32, own.shape, 0)
        query_at = lax.broadcasted_iota(jnp.int32, own.shape, 1)
        scores = jnp.where(key_at <= query_at, own, NEG_FILL)
        if count > 1:
            scores = jnp.concatenate([dot(keys[block_at(first, count - 1), :], query, NT), scores], axis=0)
        probs = jnp.exp(scores - logs_ref[head : head + 1, block_at(i)])
        grad_values = dot(probs.astype(jnp.bfloat16), grad)
        product = grad.astype(jnp.float32) * mixed_ref[block_at(i), :].astype(jnp.float32)
        high = product.astype(jnp.bfloat16)
        ones = jnp.ones((8, LANES), jnp.bfloat16)
        row_dot = dot(ones, high, NT) + dot(ones, (product - high.astype(jnp.float32)).astype(jnp.bfloat16), NT)
        grad_scores = (probs * (dot(v_ref[span, :], grad, NT) - row_dot[:1])).astype(jnp.bfloat16)
        here = dot(keys_t[:, span], grad_scores)
        return grad_values, dot(grad_scores, plain), here

    def body(i, first, count):
        span, at = block_at(first, count), block_at(i)
        values, keys_, queries = zip(*[one(i, first, count, head) for head in range(2)])
        value_acc[span, :] += values[0] + values[1]
        key_acc[span, :] += keys_[0] + keys_[1]
        row = lax.broadcasted_iota(jnp.int32, queries[0].shape, 0) // HEAD_DIM
        both = jnp.where(row == 0, *queries).T * (HEAD_DIM**-0.5)
        out_ref[0, at, :] = turn_back(both, cos_ref[at, :], sin_ref[at, :]).astype(out_ref.dtype)

    each_block(whole, reach, body)

    def finish(i, carry):
        at = block_at(i)
        out_ref[1, at, :] = turn_back(key_acc[at, :], cos_ref[at, :], sin_ref[at, :]).astype(out_ref.dtype)
        out_ref[2, at, :] = value_acc[at, :].astype(out_ref.dtype)
        return carry

    lax.fori_loop(0, whole // BLOCK, finish, 0)


def attend_back(apart, member, cos, sin, projected, grad_mixed, mixed, logs, reach):
    count, whole, width = projected.shape

    def block(c):
        return pl.BlockSpec((None, whole, LANES), lambda p: (c, 0, p))

    table = pl.BlockSpec((whole, LANES), lambda p: (0, 0))
    return pl.pallas_call(
        functools.partial(attend_back_kernel, reach),
        grid=(width // LANES,),
        in_specs=[table] * 4
        + [block(0), block(1), block(2)]
        + [pl.BlockSpec((whole, LANES), lambda p: (0, p))] * 2
        + [pl.BlockSpec((None, 8, whole), lambda p: (p, 0, 0))],
        out_specs=pl.BlockSpec((count, whole, LANES), lambda p: (0, 0, p)),
        out_shape=jax.ShapeDtypeStruct((count, whole, width), jnp.bfloat16),
        scratch_shapes=[
            pltpu.VMEM((whole, 2 * LANES), jnp.bfloat16),
            pltpu.VMEM((LANES, whole), jnp.bfloat16),
            pltpu.VMEM((whole, LANES), jnp.float32),
            pltpu.VMEM((whole, LANES), jnp.float32),
        ],
        compiler_params=pltpu.CompilerParams(vmem_limit_bytes=ROOM),
        cost_estimate=lasting(22),
    )(apart, member, cos, sin, projected, projected, projected, grad_mixed, mixed, logs)


ROWS = 256


def norm_parts(field):
    centered = field - jnp.mean(field, axis=-1, keepdims=True)
    scale = lax.rsqrt(jnp.mean(centered * centered, axis=-1, keepdims=True) + NORM_EPS)
    return centered * scale, scale


def wide(ref, at):
    return ref[at, :].astype(jnp.float32)


def row_blocks(count, body):
    def step(i, carry):
        body(i, pl.ds(pl.multiple_of(i * ROWS, ROWS), ROWS))
        return carry

    lax.fori_loop(0, count // ROWS, step, 0)


TALL = 512


def streamed(kernel, steps, scalars, fields, outs, scratch, microseconds, room=ROOM):
    def spec(shape, block=None, at=None):
        if block is None:
            return pl.BlockSpec(shape, lambda i, *scalars: (0,) * len(shape))
        return pl.BlockSpec(block, at)

    fields = [field if isinstance(field, tuple) else (field,) for field in fields]
    return pl.pallas_call(
        kernel,
        grid_spec=pltpu.PrefetchScalarGridSpec(
            num_scalar_prefetch=len(scalars),
            grid=(steps,),
            in_specs=[spec(field[0].shape, *field[1:]) for field in fields],
            out_specs=[spec(out[0], *out[2:]) for out in outs],
            scratch_shapes=[pltpu.VMEM(shape, dtype) for shape, dtype in scratch],
        ),
        out_shape=[jax.ShapeDtypeStruct(*out[:2]) for out in outs],
        compiler_params=pltpu.CompilerParams(vmem_limit_bytes=room),
        cost_estimate=lasting(microseconds),
    )(*scalars, *[field[0] for field in fields])


def by_rows(field, rows, shift=None):
    if shift is None:
        return field, (rows, field.shape[1]), lambda i, *scalars: (i, 0)
    return field, (rows, field.shape[1]), lambda i, *scalars: (shift(i, *scalars), 0)


def whole_spec(shape):
    return pl.BlockSpec(shape, lambda *at: (0,) * len(shape))


def turn(field, cos, sin):
    half = HEAD_DIM // 2
    lane = lax.broadcasted_iota(jnp.int32, field.shape, 1) % HEAD_DIM
    crossed = jnp.where(lane < half, pltpu.roll(field, LANES - half, 1), pltpu.roll(field, half, 1))
    return field * cos + crossed * sin


def join_rows(flags, own, near, far, out):
    half = near.shape[1]
    for index, got in ((flags[2], near), (1 - flags[2], far)):
        at = pl.ds(pl.multiple_of(index * half, half), half)
        out[:, at, :] = jnp.where(flags[0] == 1, own[:, at, :], got[...])


def project_kernel(flags, rows_ref, cos_ref, sin_ref, vectors, w_own, w_near, w_far, out_ref, turned_ref, weight_ref):
    @pl.when(pl.program_id(0) == 0)
    def _():
        join_rows(flags, w_own, w_near, w_far, weight_ref)

    unit, unused = norm_parts(rows_ref[...].astype(jnp.float32))
    norm = unit * vectors[0:1, :] + vectors[1:2, :]
    turned_ref[...] = norm.T.astype(jnp.bfloat16)
    norm = norm.astype(jnp.bfloat16)
    for c in range(weight_ref.shape[0]):
        field = dot(norm, weight_ref[c])
        if c == 2:
            out_ref[c] = field.astype(jnp.bfloat16)
        else:
            for p in range(field.shape[1] // LANES):
                lanes = slice(p * LANES, (p + 1) * LANES)
                out_ref[c, :, lanes] = turn(field[:, lanes], cos_ref[...], sin_ref[...]).astype(jnp.bfloat16)


def project(flags, rows, vectors, cos, sin, w_own, w_near, w_far):
    whole, width = rows.shape
    count, unused, columns = w_own.shape
    low = jnp.bfloat16
    return streamed(
        project_kernel,
        whole // ROWS,
        [flags],
        [by_rows(rows, ROWS), by_rows(cos, ROWS), by_rows(sin, ROWS), vectors, w_own, w_near, w_far],
        [
            ((count, whole, columns), low, (count, ROWS, columns), lambda i, flags: (0, i, 0)),
            ((width, whole), low, (width, ROWS), lambda i, flags: (0, i)),
        ],
        [(w_own.shape, low)],
        8,
    )


def gelu_both(up):
    root = math.sqrt(2.0 / math.pi)
    square = up * up
    bent = jnp.tanh(root * up * (1.0 + 0.044715 * square))
    half = 0.5 * (1.0 + bent)
    slope = half + 0.5 * up * (1.0 - bent * bent) * (root * (1.0 + 3.0 * 0.044715 * square))
    return up * half, slope


def feed_kernel(early, *refs):
    if early:
        flags, weight_ref, rows_ref, own_ref, got_ref, cot_here, cot_there, vectors, up_own, down_own, got = refs[:11]
        norm, norm_t, grad, grad_t, resid_ref, back_ref, act_ref, down_ref, pieces = refs[11:20]
    else:
        flags, norm, norm_t, grad, grad_t, back_early, up_own, down_own, got = refs[:9]
        back_ref, act_ref, down_ref, *pieces = refs[9:16]
    up_got, down_got = got.at[: norm.shape[1]], got.at[norm.shape[1] :]
    up_w, up_sum, down_sum = refs[-3:]
    part = up_w.shape[1] // 2
    step, last = pl.program_id(0), pl.num_programs(0) - 1

    @pl.when(step == 0)
    def _():
        up_w[...] = jnp.where(flags[0] == 1, up_own[...], up_got[...])
        down_ref[...] = jnp.where(flags[0] == 1, down_own[...], down_got[...])

    if early:

        def head(i, at):
            resid = wide(rows_ref, at) + wide(own_ref, at) + wide(got_ref, at)
            resid_ref[at, :] = resid.astype(jnp.bfloat16)
            unit, unused = norm_parts(resid)
            field = unit * vectors[2:3, :] + vectors[3:4, :]
            norm[at, :] = field.astype(jnp.bfloat16)
            norm_t[:, at] = field.T.astype(jnp.bfloat16)
            cot = jnp.where(flags[1] == step, cot_here[at, :], cot_there[at, :])
            field = cot.astype(jnp.float32) * weight_ref[weight_ref.shape[0] - 1]
            grad[at, :] = field.astype(jnp.bfloat16)
            grad_t[:, at] = field.T.astype(jnp.bfloat16)

        row_blocks(norm.shape[0], head)
    value, rise = gelu_both(dot(norm[...], up_w[...]))
    act_ref[...] = value.astype(jnp.bfloat16)
    slope = (dot(grad[...], down_ref[...], NT) * rise).astype(jnp.bfloat16)
    back = dot(slope, up_w[...], NT)
    if not early:
        back = back + back_early[...].astype(jnp.float32)
    back_ref[...] = back.astype(jnp.bfloat16)

    def store(p, at, low):
        if early:
            pieces[p, at, :] = low
            return
        slot = 2 * (flags[2] ^ (p % 2)) + (flags[3] ^ (p // 2))
        for j, piece in enumerate(pieces):

            @pl.when(slot == j)
            def _():
                piece[at, :] = low

    def grads(i, at):
        fields = (dot(norm_t[at, :], slope), dot(grad_t[at, :], act_ref[...]))
        for k, (field, total) in enumerate(zip(fields, (up_sum, down_sum))):

            @pl.when(step == 0)
            def _():
                total[at, :] = field

            @pl.when(step == last)
            def _():
                low = (total[at, :] + field).astype(jnp.bfloat16)
                for p in range(2):
                    store(2 * k + p, at, low[:, p * part : (p + 1) * part])

    row_blocks(norm_t.shape[0], grads)


def feed(early, scalars, fields, w_up, w_down, got):
    whole, width = fields[0].shape
    hidden = w_up.shape[1] // 2
    rows = whole // 2
    half = 0 if early else 1
    low = jnp.bfloat16

    def across(i, *scalars):
        return (0, i)

    tokens = ((whole, width), low, (rows, width), lambda i, *scalars: (i, 0))
    turned = ((width, whole), low, (width, rows), across)
    if early:
        operands = [by_rows(field, rows) for field in fields[:3]] + [*fields[3:]]
        outs = [tokens, turned, tokens, turned, tokens]
        pieces = [((4, width, hidden // 2), low)]
    else:
        operands = [by_rows(fields[0], rows), (fields[1], (width, rows), across)]
        operands += [by_rows(fields[2], rows), (fields[3], (width, rows), across), by_rows(fields[4], rows)]
        outs = []
        pieces = [((width, hidden // 2), low)] * 4
    operands += [
        (w_up, (width, hidden), lambda i, *scalars: (0, half)),
        (w_down, (hidden, width), lambda i, *scalars: (half, 0)),
        got,
    ]
    outs += [tokens, ((whole, hidden), low, (rows, hidden), lambda i, *scalars: (i, 0)), ((hidden, width), low)]
    sums = ((width, hidden), jnp.float32)
    return streamed(
        functools.partial(feed_kernel, early), 2, scalars, operands, outs + pieces, [((width, hidden), low), sums, sums], 17
    )


def lower_kernel(
    flags, act_early, act_late, resid_ref, cot_ref, early_ref, late_ref, keep_ref, first, second, sums_ref
):
    step = pl.program_id(0)
    total = dot(act_early[...], early_ref[...]) + dot(act_late[...], late_ref[...])
    cot = cot_ref[...].astype(jnp.float32)

    @pl.when(step == 0)
    def _():
        sums_ref[...] = jnp.zeros_like(sums_ref)

    mine = jnp.where(step < pl.num_programs(0) // 2, 0.0, 1.0)
    block = total + mine * resid_ref[...].astype(jnp.float32)
    send_or_keep(block, block, first, second, keep_ref)
    sums_ref[0:1, :] += jnp.sum(block * cot, axis=0, keepdims=True)


def send_or_keep(sent, kept, first, second, keep_ref):
    step = pl.program_id(0)
    for j, ref in enumerate((first, second)):

        @pl.when(step == j)
        def _():
            ref[...] = sent.astype(ref.dtype)

    @pl.when(step >= 2)
    def _():
        keep_ref[...] = kept.astype(keep_ref.dtype)


def theirs_first(i, flags, *more):
    return lax.rem((1 - flags[1]) * 2 + i, 4)


def sent_and_kept(whole, width):
    rows = whole // 4
    keep = ((2 * rows, width), jnp.bfloat16, (rows, width), lambda i, *scalars: (jnp.maximum(i - 2, 0), 0))
    send = ((rows, width), jnp.bfloat16)
    return [keep, send, send, ((8, width), jnp.float32)]


def lower(flags, act_early, act_late, down_early, down_late, resid, cot):
    whole, width = resid.shape
    fields = [by_rows(field, whole // 4, theirs_first) for field in (act_early, act_late, resid, cot)]
    return streamed(
        lower_kernel, 4, [flags], fields + [down_early, down_late], sent_and_kept(whole, width), [], 6, SNUG
    )


def middle_kernel(
    flags, resid_ref, cot_ref, back_own, back_got, mixed_ref,
    vectors, w_ref, grad_ref, gmixed_ref, gout_ref, sums_ref, gout,
):
    step, last = pl.program_id(0), pl.num_programs(0) - 1
    unit, scale = norm_parts(resid_ref[...].astype(jnp.float32))
    back = sum(ref[...].astype(jnp.float32) for ref in (back_own, back_got))
    inner = back * vectors[2:3, :]
    mean = jnp.mean(inner, axis=-1, keepdims=True)
    slant = jnp.mean(inner * unit, axis=-1, keepdims=True)
    grad = cot_ref[...].astype(jnp.float32) + scale * (inner - mean - unit * slant)
    low = grad.astype(jnp.bfloat16)
    grad_ref[...] = low
    gmixed_ref[...] = dot(low, w_ref[...], NT).astype(jnp.bfloat16)
    part = dot(grad.T.astype(jnp.bfloat16), mixed_ref[...])

    @pl.when(step == 0)
    def _():
        gout[...] = part
        sums_ref[...] = jnp.zeros_like(sums_ref)

    @pl.when(step > 0)
    def _():
        gout[...] += part

    @pl.when(step == last)
    def _():
        gout_ref[...] = gout[...].astype(jnp.bfloat16)

    @pl.when(step // ((last + 1) // 2) == flags[1])
    def _():
        sums_ref[0:1, :] += jnp.sum(back * unit, axis=0, keepdims=True)
        sums_ref[1:2, :] += jnp.sum(back, axis=0, keepdims=True)


def middle(flags, fields, mixed, vectors, bundle):
    whole, width = fields[0].shape
    columns = mixed.shape[1]
    low = jnp.bfloat16
    in_order = lambda i, *scalars: (i, 0)
    return streamed(
        middle_kernel,
        whole // ROWS,
        [flags],
        [by_rows(field, ROWS) for field in (*fields, mixed)]
        + [vectors, (bundle, (columns, width), lambda i, *scalars: (0, 0))],
        [
            ((whole, width), low, (ROWS, width), in_order),
            ((whole, columns), low, (ROWS, columns), in_order),
            ((width, columns), low),
            ((8, width), jnp.float32),
        ],
        [((width, columns), jnp.float32)],
        8,
    )


def weigh_kernel(flags, turned_ref, out_grad_ref, query_ref, key_ref, value_ref, *out_refs):
    rows = turned_ref[...]
    fields = [dot(rows, ref[...]).astype(jnp.bfloat16) for ref in (query_ref, key_ref, value_ref)]
    for piece, field in enumerate([*fields, out_grad_ref[...]]):
        slot = 2 * (flags[2] ^ (piece // 2)) + (flags[3] ^ (piece % 2))
        for j, out_ref in enumerate(out_refs):

            @pl.when(slot == j)
            def _():
                out_ref[...] = field


def weigh(flags, turned, grad, out_grad):
    width, columns = turned.shape[0], grad.shape[2]
    piece = ((width, columns), jnp.bfloat16, (ROWS, columns), lambda i, flags: (i, 0))
    fields = [by_rows(turned, ROWS), by_rows(out_grad, ROWS)]
    for c in range(3):
        fields.append((grad, (None, *grad.shape[1:]), lambda i, flags, c=c: (c, 0, 0)))
    return streamed(weigh_kernel, width // ROWS, [flags], fields, [piece] * 4, [], 4)


def unproject_kernel(flags, grad_ref, rows_ref, w_own, w_near, w_far, keep_ref, first, second, sums_ref, weight):
    @pl.when(pl.program_id(0) == 0)
    def _():
        join_rows(flags, w_own, w_near, w_far, weight)

    total = dot(grad_ref[0], weight[0], NT)
    for c in range(1, grad_ref.shape[0]):
        total = total + dot(grad_ref[c], weight[c], NT)
    unit, unused = norm_parts(rows_ref[...].astype(jnp.float32))

    @pl.when(pl.program_id(0) == 0)
    def _():
        sums_ref[...] = jnp.zeros_like(sums_ref)

    sums_ref[0:1, :] += jnp.sum(total * unit, axis=0, keepdims=True)
    sums_ref[1:2, :] += jnp.sum(total, axis=0, keepdims=True)
    send_or_keep(total, total, first, second, keep_ref)


def unproject(flags, grad, weights, rows):
    whole, width = rows.shape
    count, unused, columns = grad.shape
    grads = (grad, (count, whole // 4, columns), lambda i, flags: (0, theirs_first(i, flags), 0))
    fields = [grads, by_rows(rows, whole // 4, theirs_first), *weights]
    scratch = [((count, width, columns), jnp.bfloat16)]
    return streamed(unproject_kernel, 4, [flags], fields, sent_and_kept(whole, width), scratch, 5, SNUG + (4 << 20))


def last_kernel(
    flags, rows_ref, resid_ref, keep_ref, block_keep, got_first, got_second, block_first, block_second, vectors, out_ref
):
    first = pl.program_id(0) == 0
    unit, scale = norm_parts(rows_ref[...].astype(jnp.float32))
    got = jnp.where(first, got_first[...], got_second[...]).astype(jnp.float32)
    inner = (keep_ref[...].astype(jnp.float32) + got) * vectors[0:1, :]
    mean = jnp.mean(inner, axis=-1, keepdims=True)
    slant = jnp.mean(inner * unit, axis=-1, keepdims=True)
    grad = resid_ref[...].astype(jnp.float32) + scale * (inner - mean - unit * slant)
    out_ref[0] = grad.astype(jnp.bfloat16)
    got = jnp.where(first, block_first[...], block_second[...]).astype(jnp.float32)
    out_ref[1] = (block_keep[...].astype(jnp.float32) + got).astype(jnp.bfloat16)


def last(flags, rows, resid, keep, block_keep, got, vectors):
    half, width = keep.shape
    size = half // 2

    def mine(i, flags):
        return flags[1] * 2 + i

    out = ((2, half, width), jnp.bfloat16, (2, size, width), lambda i, flags: (0, i, 0))
    fields = [by_rows(rows, size, mine), by_rows(resid, size, mine), by_rows(keep, size), by_rows(block_keep, size)]
    return streamed(last_kernel, 2, [flags], fields + [*got, vectors], [out], [], 3)[0]


def past_kernel(dwa_ref, hist_ref, cot_ref, grad_ref, part_ref, sums_ref):
    @pl.when(pl.program_id(0) == 0)
    def _():
        sums_ref[...] = jnp.zeros_like(sums_ref)

    grad = cot_ref[...].astype(jnp.float32)
    total = jnp.zeros_like(grad)
    for j in range(hist_ref.shape[0]):
        field = hist_ref[j].astype(jnp.float32)
        total += dwa_ref[j] * field
        grad_ref[j] = (dwa_ref[j] * grad).astype(jnp.bfloat16)
        sums_ref[j : j + 1, :] += jnp.sum(field * grad, axis=0, keepdims=True)
    part_ref[...] = total


def past(dwa, history, cot):
    count, rows, width = history.shape
    layers = pl.BlockSpec((count, ROWS, width), lambda i: (0, i, 0))
    tokens = pl.BlockSpec((ROWS, width), lambda i: (i, 0))
    return pl.pallas_call(
        past_kernel,
        grid=(rows // ROWS,),
        in_specs=[pl.BlockSpec(memory_space=pltpu.SMEM), layers, tokens],
        out_specs=[layers, tokens, whole_spec((8, width))],
        out_shape=[
            jax.ShapeDtypeStruct(history.shape, jnp.bfloat16),
            jax.ShapeDtypeStruct((rows, width), jnp.float32),
            jax.ShapeDtypeStruct((8, width), jnp.float32),
        ],
        compiler_params=pltpu.CompilerParams(vmem_limit_bytes=ROOM),
        cost_estimate=lasting(3),
    )(dwa, history, cot)


def present_kernel(flags, weight_ref, part_ref, own_ref, got_ref, out_ref, grad_ref):
    here = jnp.where(flags[0] == 1, own_ref[1], got_ref[1]).astype(jnp.float32)
    out_ref[...] = (part_ref[...] + weight_ref[weight_ref.shape[0] - 1] * here).astype(jnp.bfloat16)
    grad_ref[...] = jnp.where(flags[0] == 1, own_ref[0], got_ref[0])


def present(flags, weight, part, own, got):
    rows, width = part.shape
    both = (2, ROWS, width), lambda i, *scalars: (0, i, 0)
    out = ((rows, width), jnp.bfloat16, (ROWS, width), lambda i, *scalars: (i, 0))
    fields = [by_rows(part, ROWS), (own, *both), (got, *both)]
    return streamed(present_kernel, rows // ROWS, [flags, weight], fields, [out] * 2, [], 2, SNUG)


def place_kernel(flags, here_ref, there_ref, qkv_ref, out_ref, up_ref, down_ref):
    near, far = flags[1], flags[2]
    part = out_ref.shape[1]
    for k in range(2):
        for c in range(2):
            field = jnp.where(near == c, here_ref[k ^ far], there_ref[k ^ far]).astype(jnp.float32)
            if 2 * k + c < 3:
                qkv_ref[2 * k + c] = field[:, :part]
            else:
                out_ref[...] = field[:, :part]
            for half in range(2):
                at = (2 * half + k) * part
                (up_ref, down_ref)[c][:, at : at + part] = field[:, (1 + half) * part : (2 + half) * part]


def place(flags, here, there):
    rows, part = here.shape[1], here.shape[2] // 3
    outs = [((3, rows, part), jnp.float32), ((rows, part), jnp.float32)]
    outs += [((rows, 4 * part), jnp.float32)] * 2
    return streamed(place_kernel, 1, [flags], [here, there], outs, [], 3, SNUG)


AXES = ("tp", "dp", "far", "near")


def moves(chosen, move):
    sizes = [lax.axis_size(name) for name in AXES]
    places = [place for place in itertools.product(*map(range, sizes)) if chosen(*place)]
    index = lambda place: functools.reduce(lambda at, step: at * step[0] + step[1], zip(sizes, place), 0)
    return [(index(place), index(move(*place))) for place in places]


def away(t, d, k, c):
    return t != c


def anyone(t, d, k, c):
    return True


def swap_diagonal(field):
    return lax.ppermute(field, AXES, moves(away, lambda t, d, k, c: (c, d, k, t)))


def send_to_owner(field, other_far, other_tp):
    return lax.ppermute(
        field,
        AXES,
        moves(
            away if not other_far and not other_tp else anyone,
            lambda t, d, k, c: (c, d, k ^ other_far, t ^ other_tp),
        ),
    )


def swap_far_away(field):
    return lax.ppermute(field, AXES, moves(away, lambda t, d, k, c: (t, d, 1 - k, c)))


def swap_far(field):
    return lax.ppermute(field, "far", [(0, 1), (1, 0)])


def swap_near(field):
    return lax.ppermute(field, "near", [(0, 1), (1, 0)])


def after(field, *others):
    return lax.optimization_barrier((field, *others))[0]


def ordered(own, other, first, axis=0):
    return jnp.where(
        first, jnp.concatenate([own, other], axis=axis), jnp.concatenate([other, own], axis=axis)
    )


def part_of(field, index, axis):
    size = field.shape[axis] // 2
    return lax.dynamic_slice_in_dim(field, index * size, size, axis)


def add(*fields):
    return sum(field.astype(jnp.float32) for field in fields).astype(jnp.bfloat16)


def scatter_plane(pieces):
    return lax.psum_scatter(pieces, ("tp", "far"), scatter_dimension=0, tiled=True)[0]


def scatter_rows(piece):
    return lax.psum_scatter(piece, "dp", scatter_dimension=0, tiled=True)


def move_rows(block):
    dps = lax.axis_size("dp")
    if dps > 8:
        return [scatter_rows(block)]
    block = block.reshape(dps, block.shape[0] // dps, block.shape[1])
    place = lax.axis_index("dp")
    moved = [lax.dynamic_index_in_dim(block, place, 0, keepdims=False)]
    for step in range(1, dps):
        sent = lax.dynamic_index_in_dim(block, lax.rem(place + step, dps), 0, keepdims=False)
        moved.append(lax.ppermute(sent, "dp", [(d, (d + step) % dps) for d in range(dps)]))
    return moved


def sum_over(field, name):
    size = lax.axis_size(name)
    bit = 1
    while bit < size:
        field = field + lax.ppermute(field, name, [(d, d ^ bit) for d in range(size)])
        bit *= 2
    return field


def local(
    layer_input,
    history,
    cotangent,
    lengths,
    dwa_weights,
    gain_one,
    bias_one,
    w_qkv,
    w_out,
    gain_two,
    bias_two,
    w_up,
    w_down,
):
    rows = layer_input.shape[1]
    whole = rows * lax.axis_size("tp")
    hist_count = history.shape[0]
    part, far, near = lax.axis_index("tp"), lax.axis_index("far"), lax.axis_index("near")
    same = near == part
    flags = jnp.stack([same.astype(jnp.int32), near, far, part])

    input_got = swap_diagonal(layer_input[0])
    qkv_near = swap_diagonal(part_of(w_qkv, far, 1))
    qkv_far = swap_far_away(qkv_near)
    early_got = jnp.concatenate([part_of(w_up, 0, 1), part_of(w_down, 0, 0)], axis=0)
    late_got = jnp.concatenate([part_of(w_up, 1, 1), part_of(w_down, 1, 0)], axis=0)
    last_own = jnp.concatenate([w_out, cotangent[0]], axis=0)
    vectors = jnp.stack([gain_one, bias_one, gain_two, bias_two])

    own_lengths = jnp.where(same, lengths, swap_near(lengths))[0]
    seq_owner, token_place = positions(own_lengths, whole)
    lane = jnp.arange(LANES, dtype=jnp.int32)
    member = seq_owner[:, None] == lane[None, :]
    apart = jnp.where(member | (lane >= lengths.shape[1])[None, :], 0.0, NEG_FILL).astype(jnp.bfloat16)
    member = member.astype(jnp.bfloat16)
    half_dim = HEAD_DIM // 2
    frequency = jnp.exp((lane % half_dim).astype(jnp.float32) * (-math.log(10000.0) / half_dim))
    angles = token_place.astype(jnp.float32)[:, None] * frequency[None, :]
    cos_table = jnp.cos(angles)
    sin_table = jnp.sin(angles) * jnp.where(lane % HEAD_DIM < half_dim, -1.0, 1.0)[None, :]
    grad_history, past_sum, sums_past = past(dwa_weights, history[:, 0], cotangent[0])

    input_half = jnp.where(same, layer_input[0], input_got)
    layer_rows = ordered(input_half, swap_near(input_half), near == 0)
    layer_rows, vectors, past_sum, cos_table, sin_table, apart, member = lax.optimization_barrier(
        (layer_rows, vectors, past_sum, cos_table, sin_table, apart, member)
    )
    early_got = swap_diagonal(after(early_got, input_got))
    last_got = swap_diagonal(after(last_own, input_got))
    projected, norm_one_t = project(
        flags, layer_rows, vectors, cos_table, sin_table, w_qkv, qkv_near, qkv_far
    )
    mixed, logs = attend(apart, member, projected, LONGEST)
    late_got = swap_diagonal(after(late_got, mixed))
    last_got = jnp.where(same, last_own, after(last_got, mixed))
    weight_out = last_got[: w_out.shape[0]]
    attn = jnp.dot(mixed, weight_out, preferred_element_type=jnp.float32).astype(jnp.bfloat16)
    attn_got = swap_near(attn)
    cot_half = last_got[w_out.shape[0] :]
    scalars = [flags, dwa_weights]
    fields = [layer_rows, attn, attn_got, cot_half, swap_near(cot_half), vectors]
    *kept, resid, back, act_early, down_early, early_pieces = feed(True, scalars, fields, w_up, w_down, early_got)
    early_sum = scatter_plane(after(early_pieces, late_got))
    back, act_late, down_late, *late_owned = feed(
        False, [flags], [*kept, back], w_up, w_down, late_got
    )
    late_moved = [send_to_owner(late_owned[j], j // 2, j % 2) for j in range(4)]
    grad_down = kept[2]
    fields = [resid, grad_down, back, swap_near(back)]
    grad_attn, grad_mixed, grad_out, sums_two = middle(flags, fields, mixed, vectors, last_got)
    grad_qkv = attend_back(
        apart, member, cos_table, sin_table, projected, grad_mixed, mixed, logs, LONGEST
    )
    grad_qkv, *late_moved = lax.optimization_barrier((grad_qkv, *late_moved))
    owned = weigh(flags, norm_one_t, grad_qkv, grad_out)
    moved = [send_to_owner(owned[j], j // 2, j % 2) for j in range(4)]
    early_sum = scatter_rows(after(early_sum, grad_qkv))
    late_sum = scatter_rows(add(jnp.where(same, late_owned[0], after(late_moved[0], owned[0])), *late_moved[1:]))
    keep, *send, sums_one = unproject(
        flags, after(grad_qkv, owned[0]), (w_qkv, qkv_near, qkv_far), layer_rows
    )
    block_keep, *block_send, sums_now = lower(
        flags, act_early, act_late, down_early, down_late, resid, after(grad_down, keep)
    )
    sent = [*send, *block_send]
    keep, block_keep, *arrived = lax.optimization_barrier((keep, block_keep, *sent, *moved))
    sent, moved = arrived[:4], arrived[4:]
    attn_one = add(jnp.where(same, owned[0], moved[0]), *moved[1:])
    attn_moved = move_rows(attn_one)
    got = [swap_near(field) for field in sent]
    ours = last(flags, layer_rows, grad_attn, after(keep, attn_one), block_keep, got, vectors)
    early_sum = after(early_sum, attn_one)
    early_got = swap_diagonal(early_sum)
    small = jnp.concatenate([sums_one[:2], sums_two[:2], sums_now[:1], sums_past[:hist_count]], axis=0)
    small = after(small, ours)
    for name in ("tp", "far"):
        small = sum_over(small, name)
    theirs = swap_diagonal(ours)
    small, late_sum, early_sum, early_got, *attn_moved = lax.optimization_barrier(
        (small, late_sum, early_sum, early_got, *attn_moved)
    )
    for name in ("near", "dp"):
        small = sum_over(small, name)
    attn_sum = add(*attn_moved)
    blocks = jnp.concatenate([attn_sum, jnp.where(same, early_sum, early_got), late_sum], axis=1)
    here = after(jnp.stack([blocks, swap_far(blocks)]), small)
    output, grad_input = present(flags, dwa_weights, past_sum, ours, theirs)
    grad_w_qkv, grad_w_out, grad_w_up, grad_w_down = place(flags, here, swap_near(here))

    return (
        output[None],
        grad_input[None],
        grad_history[:, None],
        jnp.sum(jnp.concatenate([small[5:], small[4:5] / dwa_weights[hist_count]], axis=0), axis=1),
        small[0],
        small[1],
        grad_w_qkv,
        grad_w_out.T,
        small[2],
        small[3],
        grad_w_up,
        grad_w_down.T,
    )


def positions(seq_lengths, token_count):
    seq_ends = jnp.cumsum(seq_lengths)
    seq_starts = seq_ends - seq_lengths
    token_index = jnp.arange(token_count, dtype=jnp.int32)
    seq_owner = jnp.sum((token_index[:, None] >= seq_ends[None, :]).astype(jnp.int32), axis=1)
    picked = (
        seq_owner[:, None] == jnp.arange(seq_lengths.shape[0], dtype=jnp.int32)[None, :]
    ).astype(jnp.int32)
    seq_begin = jnp.sum(picked * seq_starts[None, :], axis=1)
    return (seq_owner, token_index - seq_begin)


def solution(mesh):
    tps, dps, reps = (mesh.shape[name] for name in ("tp", "dp", "rep"))
    split = Mesh(mesh.devices.reshape(tps, dps, reps // 2, 2), AXES)
    in_specs = (
        P(("dp", "far", "near"), "tp", None),
        P(None, ("dp", "far", "near"), "tp", None),
        P(("dp", "far", "near"), "tp", None),
        P(("dp", "far", "near"), None),
        P(),
        P(),
        P(),
        P(None, None, "tp"),
        P("tp", None),
        P(),
        P(),
        P(None, "tp"),
        P("tp", None),
    )
    out_specs = (
        P(("dp", "far", "near"), "tp", None),
        P(("dp", "far", "near"), "tp", None),
        P(None, ("dp", "far", "near"), "tp", None),
        P(),
        P(),
        P(),
        P(None, "dp", "tp"),
        P("tp", "dp"),
        P(),
        P(),
        P("dp", "tp"),
        P("tp", "dp"),
    )
    return jax.shard_map(local, mesh=split, in_specs=in_specs, out_specs=out_specs, check_vma=False)
```

```python
import functools
import itertools
import math

import jax
import jax.numpy as jnp
from jax import lax
from jax.experimental import pallas as pl
from jax.experimental.pallas import tpu as pltpu
from jax.sharding import Mesh, PartitionSpec as P

HEAD_DIM = 64
LONGEST = 512
NEG_FILL = -1e30
NORM_EPS = 1e-05
RATE = 3e6
ROOM = 60 << 20
SNUG = 18 << 20


def lasting(microseconds):
    return pl.CostEstimate(flops=0, transcendentals=0, bytes_accessed=int(microseconds * RATE))


BLOCK = 256
LANES = 128
NT = (((1,), (1,)), ((), ()))


def dot(a, b, dims=(((1,), (0,)), ((), ()))):
    return lax.dot_general(a, b, dims, preferred_element_type=jnp.float32)


def spans(whole, reach):
    back = -(-(reach - 1) // BLOCK)
    runs = []
    for i in range(whole // BLOCK):
        count = min(i, back) + 1
        if runs and runs[-1][2] == count:
            runs[-1][1] = i + 1
        else:
            runs.append([i, i + 1, count])
    return runs


def each_block(whole, reach, body):
    for first, last, count in spans(whole, reach):

        def step(i, carry, count=count):
            body(i, i + 1 - count, count)
            return carry

        lax.fori_loop(first, last, step, 0)


def block_at(i, count=1):
    return pl.ds(pl.multiple_of(i * BLOCK, BLOCK), count * BLOCK)


def head_query(q_ref, apart_ref, i, head):
    lane = lax.broadcasted_iota(jnp.int32, (BLOCK, LANES), 1) // HEAD_DIM
    query = q_ref[block_at(i), :] * (HEAD_DIM**-0.5)
    query = jnp.where(lane == head, query, jnp.zeros_like(query))
    return query, jnp.concatenate([query, apart_ref[block_at(i), :]], axis=1)


def attend_kernel(reach, apart_ref, member_ref, q_ref, k_ref, v_ref, out_ref, logs_ref, keys):
    whole = q_ref.shape[0]
    lane = lax.broadcasted_iota(jnp.int32, (BLOCK, LANES), 1) // HEAD_DIM
    keys[:, :LANES] = k_ref[...]
    keys[:, LANES:] = member_ref[...]

    def one(i, first, count, head):
        unused, query = head_query(q_ref, apart_ref, i, head)
        own = dot(query, keys[block_at(i), :], NT)
        key_at = lax.broadcasted_iota(jnp.int32, own.shape, 1)
        query_at = lax.broadcasted_iota(jnp.int32, own.shape, 0)
        scores = jnp.where(key_at <= query_at, own, NEG_FILL)
        if count > 1:
            scores = jnp.concatenate([dot(query, keys[block_at(first, count - 1), :], NT), scores], axis=1)
        row_max = jnp.max(scores, axis=1, keepdims=True)
        exponent = jnp.exp(scores - row_max)
        row_sum = jnp.sum(exponent, axis=1, keepdims=True)
        mixed = dot(exponent.astype(jnp.bfloat16), v_ref[block_at(first, count), :]) * (1.0 / row_sum)
        return mixed, row_max + jnp.log(row_sum)

    def body(i, first, count):
        mixed, logs = zip(*[one(i, first, count, head) for head in range(2)])
        out_ref[block_at(i), :] = jnp.where(lane == 0, *mixed).astype(out_ref.dtype)
        turned = jnp.where(lane == 0, *logs).T
        for head in range(2):
            logs_ref[head : head + 1, block_at(i)] = turned[head * HEAD_DIM : head * HEAD_DIM + 1]

    each_block(whole, reach, body)


def attend(apart, member, projected, reach):
    count, whole, width = projected.shape

    def block(c):
        return pl.BlockSpec((None, whole, LANES), lambda p: (c, 0, p))

    table = pl.BlockSpec((whole, LANES), lambda p: (0, 0))
    return pl.pallas_call(
        functools.partial(attend_kernel, reach),
        grid=(width // LANES,),
        in_specs=[table, table, block(0), block(1), block(2)],
        out_specs=[
            pl.BlockSpec((whole, LANES), lambda p: (0, p)),
            pl.BlockSpec((None, 8, whole), lambda p: (p, 0, 0)),
        ],
        out_shape=[
            jax.ShapeDtypeStruct((whole, width), jnp.bfloat16),
            jax.ShapeDtypeStruct((width // LANES, 8, whole), jnp.float32),
        ],
        scratch_shapes=[pltpu.VMEM((whole, 2 * LANES), jnp.bfloat16)],
        compiler_params=pltpu.CompilerParams(vmem_limit_bytes=ROOM),
        cost_estimate=lasting(12),
    )(apart, member, projected, projected, projected)


def turn_back(field, cos, sin):
    half = HEAD_DIM // 2
    lane = lax.broadcasted_iota(jnp.int32, field.shape, 1) % HEAD_DIM
    crossed = jnp.where(lane < half, pltpu.roll(field, LANES - half, 1), pltpu.roll(field, half, 1))
    return field * cos - crossed * sin


def attend_back_kernel(
    reach, apart_ref, member_ref, cos_ref, sin_ref, q_ref, k_ref, v_ref, g_ref, mixed_ref, logs_ref, out_ref,
    keys, keys_t, key_acc, value_acc
):
    whole = q_ref.shape[0]
    lane = lax.broadcasted_iota(jnp.int32, (BLOCK, LANES), 1) // HEAD_DIM
    keys[:, :LANES] = k_ref[...]
    keys[:, LANES:] = member_ref[...]
    keys_t[...] = k_ref[...].astype(jnp.float32).T.astype(jnp.bfloat16)
    key_acc[...] = jnp.zeros_like(key_acc)
    value_acc[...] = jnp.zeros_like(value_acc)

    def one(i, first, count, head):
        span = block_at(first, count)
        plain, query = head_query(q_ref, apart_ref, i, head)
        grad = g_ref[block_at(i), :]
        grad = jnp.where(lane == head, grad, jnp.zeros_like(grad))
        own = dot(keys[block_at(i), :], query, NT)
        key_at = lax.broadcasted_iota(jnp.int32, own.shape, 0)
        query_at = lax.broadcasted_iota(jnp.int32, own.shape, 1)
        scores = jnp.where(key_at <= query_at, own, NEG_FILL)
        if count > 1:
            scores = jnp.concatenate([dot(keys[block_at(first, count - 1), :], query, NT), scores], axis=0)
        probs = jnp.exp(scores - logs_ref[head : head + 1, block_at(i)])
        grad_values = dot(probs.astype(jnp.bfloat16), grad)
        product = grad.astype(jnp.float32) * mixed_ref[block_at(i), :].astype(jnp.float32)
        high = product.astype(jnp.bfloat16)
        ones = jnp.ones((8, LANES), jnp.bfloat16)
        row_dot = dot(ones, high, NT) + dot(ones, (product - high.astype(jnp.float32)).astype(jnp.bfloat16), NT)
        grad_scores = (probs * (dot(v_ref[span, :], grad, NT) - row_dot[:1])).astype(jnp.bfloat16)
        here = dot(keys_t[:, span], grad_scores)
        return grad_values, dot(grad_scores, plain), here

    def body(i, first, count):
        span, at = block_at(first, count), block_at(i)
        values, keys_, queries = zip(*[one(i, first, count, head) for head in range(2)])
        value_acc[span, :] += values[0] + values[1]
        key_acc[span, :] += keys_[0] + keys_[1]
        row = lax.broadcasted_iota(jnp.int32, queries[0].shape, 0) // HEAD_DIM
        both = jnp.where(row == 0, *queries).T * (HEAD_DIM**-0.5)
        out_ref[0, at, :] = turn_back(both, cos_ref[at, :], sin_ref[at, :]).astype(out_ref.dtype)

    each_block(whole, reach, body)

    def finish(i, carry):
        at = block_at(i)
        out_ref[1, at, :] = turn_back(key_acc[at, :], cos_ref[at, :], sin_ref[at, :]).astype(out_ref.dtype)
        out_ref[2, at, :] = value_acc[at, :].astype(out_ref.dtype)
        return carry

    lax.fori_loop(0, whole // BLOCK, finish, 0)


def attend_back(apart, member, cos, sin, projected, grad_mixed, mixed, logs, reach):
    count, whole, width = projected.shape

    def block(c):
        return pl.BlockSpec((None, whole, LANES), lambda p: (c, 0, p))

    table = pl.BlockSpec((whole, LANES), lambda p: (0, 0))
    return pl.pallas_call(
        functools.partial(attend_back_kernel, reach),
        grid=(width // LANES,),
        in_specs=[table] * 4
        + [block(0), block(1), block(2)]
        + [pl.BlockSpec((whole, LANES), lambda p: (0, p))] * 2
        + [pl.BlockSpec((None, 8, whole), lambda p: (p, 0, 0))],
        out_specs=pl.BlockSpec((count, whole, LANES), lambda p: (0, 0, p)),
        out_shape=jax.ShapeDtypeStruct((count, whole, width), jnp.bfloat16),
        scratch_shapes=[
            pltpu.VMEM((whole, 2 * LANES), jnp.bfloat16),
            pltpu.VMEM((LANES, whole), jnp.bfloat16),
            pltpu.VMEM((whole, LANES), jnp.float32),
            pltpu.VMEM((whole, LANES), jnp.float32),
        ],
        compiler_params=pltpu.CompilerParams(vmem_limit_bytes=ROOM),
        cost_estimate=lasting(22),
    )(apart, member, cos, sin, projected, projected, projected, grad_mixed, mixed, logs)


ROWS = 256


def norm_parts(field):
    centered = field - jnp.mean(field, axis=-1, keepdims=True)
    scale = lax.rsqrt(jnp.mean(centered * centered, axis=-1, keepdims=True) + NORM_EPS)
    return centered * scale, scale


def wide(ref, at):
    return ref[at, :].astype(jnp.float32)


def row_blocks(count, body):
    def step(i, carry):
        body(i, pl.ds(pl.multiple_of(i * ROWS, ROWS), ROWS))
        return carry

    lax.fori_loop(0, count // ROWS, step, 0)


TALL = 512


def streamed(kernel, steps, scalars, fields, outs, scratch, microseconds, room=ROOM):
    def spec(shape, block=None, at=None):
        if block is None:
            return pl.BlockSpec(shape, lambda i, *scalars: (0,) * len(shape))
        return pl.BlockSpec(block, at)

    fields = [field if isinstance(field, tuple) else (field,) for field in fields]
    return pl.pallas_call(
        kernel,
        grid_spec=pltpu.PrefetchScalarGridSpec(
            num_scalar_prefetch=len(scalars),
            grid=(steps,),
            in_specs=[spec(field[0].shape, *field[1:]) for field in fields],
            out_specs=[spec(out[0], *out[2:]) for out in outs],
            scratch_shapes=[pltpu.VMEM(shape, dtype) for shape, dtype in scratch],
        ),
        out_shape=[jax.ShapeDtypeStruct(*out[:2]) for out in outs],
        compiler_params=pltpu.CompilerParams(vmem_limit_bytes=room),
        cost_estimate=lasting(microseconds),
    )(*scalars, *[field[0] for field in fields])


def by_rows(field, rows, shift=None):
    if shift is None:
        return field, (rows, field.shape[1]), lambda i, *scalars: (i, 0)
    return field, (rows, field.shape[1]), lambda i, *scalars: (shift(i, *scalars), 0)


def whole_spec(shape):
    return pl.BlockSpec(shape, lambda *at: (0,) * len(shape))


def turn(field, cos, sin):
    half = HEAD_DIM // 2
    lane = lax.broadcasted_iota(jnp.int32, field.shape, 1) % HEAD_DIM
    crossed = jnp.where(lane < half, pltpu.roll(field, LANES - half, 1), pltpu.roll(field, half, 1))
    return field * cos + crossed * sin


def join_rows(flags, own, near, far, out):
    half = near.shape[1]
    for index, got in ((flags[2], near), (1 - flags[2], far)):
        at = pl.ds(pl.multiple_of(index * half, half), half)
        out[:, at, :] = jnp.where(flags[0] == 1, own[:, at, :], got[...])


def project_kernel(flags, rows_ref, cos_ref, sin_ref, vectors, w_own, w_near, w_far, out_ref, turned_ref, weight_ref):
    @pl.when(pl.program_id(0) == 0)
    def _():
        join_rows(flags, w_own, w_near, w_far, weight_ref)

    unit, unused = norm_parts(rows_ref[...].astype(jnp.float32))
    norm = unit * vectors[0:1, :] + vectors[1:2, :]
    turned_ref[...] = norm.T.astype(jnp.bfloat16)
    norm = norm.astype(jnp.bfloat16)
    for c in range(weight_ref.shape[0]):
        field = dot(norm, weight_ref[c])
        if c == 2:
            out_ref[c] = field.astype(jnp.bfloat16)
        else:
            for p in range(field.shape[1] // LANES):
                lanes = slice(p * LANES, (p + 1) * LANES)
                out_ref[c, :, lanes] = turn(field[:, lanes], cos_ref[...], sin_ref[...]).astype(jnp.bfloat16)


def project(flags, rows, vectors, cos, sin, w_own, w_near, w_far):
    whole, width = rows.shape
    count, unused, columns = w_own.shape
    low = jnp.bfloat16
    return streamed(
        project_kernel,
        whole // ROWS,
        [flags],
        [by_rows(rows, ROWS), by_rows(cos, ROWS), by_rows(sin, ROWS), vectors, w_own, w_near, w_far],
        [
            ((count, whole, columns), low, (count, ROWS, columns), lambda i, flags: (0, i, 0)),
            ((width, whole), low, (width, ROWS), lambda i, flags: (0, i)),
        ],
        [(w_own.shape, low)],
        8,
    )


def gelu_both(up):
    root = math.sqrt(2.0 / math.pi)
    square = up * up
    bent = jnp.tanh(root * up * (1.0 + 0.044715 * square))
    half = 0.5 * (1.0 + bent)
    slope = half + 0.5 * up * (1.0 - bent * bent) * (root * (1.0 + 3.0 * 0.044715 * square))
    return up * half, slope


def feed_kernel(early, *refs):
    if early:
        flags, weight_ref, rows_ref, own_ref, got_ref, cot_here, cot_there, vectors, up_own, down_own, got = refs[:11]
        norm, norm_t, grad, grad_t, resid_ref, back_ref, act_ref, down_ref, pieces = refs[11:20]
    else:
        flags, norm, norm_t, grad, grad_t, back_early, up_own, down_own, got = refs[:9]
        back_ref, act_ref, down_ref, *pieces = refs[9:16]
    up_got, down_got = got.at[: norm.shape[1]], got.at[norm.shape[1] :]
    up_w, up_sum, down_sum = refs[-3:]
    part = up_w.shape[1] // 2
    step, last = pl.program_id(0), pl.num_programs(0) - 1

    @pl.when(step == 0)
    def _():
        up_w[...] = jnp.where(flags[0] == 1, up_own[...], up_got[...])
        down_ref[...] = jnp.where(flags[0] == 1, down_own[...], down_got[...])

    if early:

        def head(i, at):
            resid = wide(rows_ref, at) + wide(own_ref, at) + wide(got_ref, at)
            resid_ref[at, :] = resid.astype(jnp.bfloat16)
            unit, unused = norm_parts(resid)
            field = unit * vectors[2:3, :] + vectors[3:4, :]
            norm[at, :] = field.astype(jnp.bfloat16)
            norm_t[:, at] = field.T.astype(jnp.bfloat16)
            cot = jnp.where(flags[1] == step, cot_here[at, :], cot_there[at, :])
            field = cot.astype(jnp.float32) * weight_ref[weight_ref.shape[0] - 1]
            grad[at, :] = field.astype(jnp.bfloat16)
            grad_t[:, at] = field.T.astype(jnp.bfloat16)

        row_blocks(norm.shape[0], head)
    value, rise = gelu_both(dot(norm[...], up_w[...]))
    act_ref[...] = value.astype(jnp.bfloat16)
    slope = (dot(grad[...], down_ref[...], NT) * rise).astype(jnp.bfloat16)
    back = dot(slope, up_w[...], NT)
    if not early:
        back = back + back_early[...].astype(jnp.float32)
    back_ref[...] = back.astype(jnp.bfloat16)

    def store(p, at, low):
        if early:
            pieces[p, at, :] = low
            return
        slot = 2 * (flags[2] ^ (p % 2)) + (flags[3] ^ (p // 2))
        for j, piece in enumerate(pieces):

            @pl.when(slot == j)
            def _():
                piece[at, :] = low

    def grads(i, at):
        fields = (dot(norm_t[at, :], slope), dot(grad_t[at, :], act_ref[...]))
        for k, (field, total) in enumerate(zip(fields, (up_sum, down_sum))):

            @pl.when(step == 0)
            def _():
                total[at, :] = field

            @pl.when(step == last)
            def _():
                low = (total[at, :] + field).astype(jnp.bfloat16)
                for p in range(2):
                    store(2 * k + p, at, low[:, p * part : (p + 1) * part])

    row_blocks(norm_t.shape[0], grads)


def feed(early, scalars, fields, w_up, w_down, got):
    whole, width = fields[0].shape
    hidden = w_up.shape[1] // 2
    rows = whole // 2
    half = 0 if early else 1
    low = jnp.bfloat16

    def across(i, *scalars):
        return (0, i)

    tokens = ((whole, width), low, (rows, width), lambda i, *scalars: (i, 0))
    turned = ((width, whole), low, (width, rows), across)
    if early:
        operands = [by_rows(field, rows) for field in fields[:3]] + [*fields[3:]]
        outs = [tokens, turned, tokens, turned, tokens]
        pieces = [((4, width, hidden // 2), low)]
    else:
        operands = [by_rows(fields[0], rows), (fields[1], (width, rows), across)]
        operands += [by_rows(fields[2], rows), (fields[3], (width, rows), across), by_rows(fields[4], rows)]
        outs = []
        pieces = [((width, hidden // 2), low)] * 4
    operands += [
        (w_up, (width, hidden), lambda i, *scalars: (0, half)),
        (w_down, (hidden, width), lambda i, *scalars: (half, 0)),
        got,
    ]
    outs += [tokens, ((whole, hidden), low, (rows, hidden), lambda i, *scalars: (i, 0)), ((hidden, width), low)]
    sums = ((width, hidden), jnp.float32)
    return streamed(
        functools.partial(feed_kernel, early), 2, scalars, operands, outs + pieces, [((width, hidden), low), sums, sums], 17
    )


def lower_kernel(
    flags, act_early, act_late, resid_ref, cot_ref, early_ref, late_ref, keep_ref, first, second, sums_ref
):
    step = pl.program_id(0)
    total = dot(act_early[...], early_ref[...]) + dot(act_late[...], late_ref[...])
    cot = cot_ref[...].astype(jnp.float32)

    @pl.when(step == 0)
    def _():
        sums_ref[...] = jnp.zeros_like(sums_ref)

    mine = jnp.where(step < pl.num_programs(0) // 2, 0.0, 1.0)
    block = total + mine * resid_ref[...].astype(jnp.float32)
    send_or_keep(block, block, first, second, keep_ref)
    sums_ref[0:1, :] += jnp.sum(block * cot, axis=0, keepdims=True)


def send_or_keep(sent, kept, first, second, keep_ref):
    step = pl.program_id(0)
    for j, ref in enumerate((first, second)):

        @pl.when(step == j)
        def _():
            ref[...] = sent.astype(ref.dtype)

    @pl.when(step >= 2)
    def _():
        keep_ref[...] = kept.astype(keep_ref.dtype)


def theirs_first(i, flags, *more):
    return lax.rem((1 - flags[1]) * 2 + i, 4)


def sent_and_kept(whole, width):
    rows = whole // 4
    keep = ((2 * rows, width), jnp.bfloat16, (rows, width), lambda i, *scalars: (jnp.maximum(i - 2, 0), 0))
    send = ((rows, width), jnp.bfloat16)
    return [keep, send, send, ((8, width), jnp.float32)]


def lower(flags, act_early, act_late, down_early, down_late, resid, cot):
    whole, width = resid.shape
    fields = [by_rows(field, whole // 4, theirs_first) for field in (act_early, act_late, resid, cot)]
    return streamed(
        lower_kernel, 4, [flags], fields + [down_early, down_late], sent_and_kept(whole, width), [], 6, SNUG
    )


def middle_kernel(
    flags, resid_ref, cot_ref, back_own, back_got, mixed_ref,
    vectors, w_ref, grad_ref, gmixed_ref, gout_ref, sums_ref, gout,
):
    step, last = pl.program_id(0), pl.num_programs(0) - 1
    unit, scale = norm_parts(resid_ref[...].astype(jnp.float32))
    back = sum(ref[...].astype(jnp.float32) for ref in (back_own, back_got))
    inner = back * vectors[2:3, :]
    mean = jnp.mean(inner, axis=-1, keepdims=True)
    slant = jnp.mean(inner * unit, axis=-1, keepdims=True)
    grad = cot_ref[...].astype(jnp.float32) + scale * (inner - mean - unit * slant)
    low = grad.astype(jnp.bfloat16)
    grad_ref[...] = low
    gmixed_ref[...] = dot(low, w_ref[...], NT).astype(jnp.bfloat16)
    part = dot(grad.T.astype(jnp.bfloat16), mixed_ref[...])

    @pl.when(step == 0)
    def _():
        gout[...] = part
        sums_ref[...] = jnp.zeros_like(sums_ref)

    @pl.when(step > 0)
    def _():
        gout[...] += part

    @pl.when(step == last)
    def _():
        gout_ref[...] = gout[...].astype(jnp.bfloat16)

    @pl.when(step // ((last + 1) // 2) == flags[1])
    def _():
        sums_ref[0:1, :] += jnp.sum(back * unit, axis=0, keepdims=True)
        sums_ref[1:2, :] += jnp.sum(back, axis=0, keepdims=True)


def middle(flags, fields, mixed, vectors, bundle):
    whole, width = fields[0].shape
    columns = mixed.shape[1]
    low = jnp.bfloat16
    in_order = lambda i, *scalars: (i, 0)
    return streamed(
        middle_kernel,
        whole // ROWS,
        [flags],
        [by_rows(field, ROWS) for field in (*fields, mixed)]
        + [vectors, (bundle, (columns, width), lambda i, *scalars: (0, 0))],
        [
            ((whole, width), low, (ROWS, width), in_order),
            ((whole, columns), low, (ROWS, columns), in_order),
            ((width, columns), low),
            ((8, width), jnp.float32),
        ],
        [((width, columns), jnp.float32)],
        8,
    )


def weigh_kernel(flags, turned_ref, out_grad_ref, query_ref, key_ref, value_ref, *out_refs):
    rows = turned_ref[...]
    fields = [dot(rows, ref[...]).astype(jnp.bfloat16) for ref in (query_ref, key_ref, value_ref)]
    for piece, field in enumerate([*fields, out_grad_ref[...]]):
        slot = 2 * (flags[2] ^ (piece // 2)) + (flags[3] ^ (piece % 2))
        for j, out_ref in enumerate(out_refs):

            @pl.when(slot == j)
            def _():
                out_ref[...] = field


def weigh(flags, turned, grad, out_grad):
    width, columns = turned.shape[0], grad.shape[2]
    piece = ((width, columns), jnp.bfloat16, (ROWS, columns), lambda i, flags: (i, 0))
    fields = [by_rows(turned, ROWS), by_rows(out_grad, ROWS)]
    for c in range(3):
        fields.append((grad, (None, *grad.shape[1:]), lambda i, flags, c=c: (c, 0, 0)))
    return streamed(weigh_kernel, width // ROWS, [flags], fields, [piece] * 4, [], 4)


def unproject_kernel(flags, grad_ref, rows_ref, w_own, w_near, w_far, keep_ref, first, second, sums_ref, weight):
    @pl.when(pl.program_id(0) == 0)
    def _():
        join_rows(flags, w_own, w_near, w_far, weight)

    total = dot(grad_ref[0], weight[0], NT)
    for c in range(1, grad_ref.shape[0]):
        total = total + dot(grad_ref[c], weight[c], NT)
    unit, unused = norm_parts(rows_ref[...].astype(jnp.float32))

    @pl.when(pl.program_id(0) == 0)
    def _():
        sums_ref[...] = jnp.zeros_like(sums_ref)

    sums_ref[0:1, :] += jnp.sum(total * unit, axis=0, keepdims=True)
    sums_ref[1:2, :] += jnp.sum(total, axis=0, keepdims=True)
    send_or_keep(total, total, first, second, keep_ref)


def unproject(flags, grad, weights, rows):
    whole, width = rows.shape
    count, unused, columns = grad.shape
    grads = (grad, (count, whole // 4, columns), lambda i, flags: (0, theirs_first(i, flags), 0))
    fields = [grads, by_rows(rows, whole // 4, theirs_first), *weights]
    scratch = [((count, width, columns), jnp.bfloat16)]
    return streamed(unproject_kernel, 4, [flags], fields, sent_and_kept(whole, width), scratch, 5, SNUG + (4 << 20))


def last_kernel(
    flags, rows_ref, resid_ref, keep_ref, block_keep, got_first, got_second, block_first, block_second, vectors, out_ref
):
    first = pl.program_id(0) == 0
    unit, scale = norm_parts(rows_ref[...].astype(jnp.float32))
    got = jnp.where(first, got_first[...], got_second[...]).astype(jnp.float32)
    inner = (keep_ref[...].astype(jnp.float32) + got) * vectors[0:1, :]
    mean = jnp.mean(inner, axis=-1, keepdims=True)
    slant = jnp.mean(inner * unit, axis=-1, keepdims=True)
    grad = resid_ref[...].astype(jnp.float32) + scale * (inner - mean - unit * slant)
    out_ref[0] = grad.astype(jnp.bfloat16)
    got = jnp.where(first, block_first[...], block_second[...]).astype(jnp.float32)
    out_ref[1] = (block_keep[...].astype(jnp.float32) + got).astype(jnp.bfloat16)


def last(flags, rows, resid, keep, block_keep, got, vectors):
    half, width = keep.shape
    size = half // 2

    def mine(i, flags):
        return flags[1] * 2 + i

    out = ((2, half, width), jnp.bfloat16, (2, size, width), lambda i, flags: (0, i, 0))
    fields = [by_rows(rows, size, mine), by_rows(resid, size, mine), by_rows(keep, size), by_rows(block_keep, size)]
    return streamed(last_kernel, 2, [flags], fields + [*got, vectors], [out], [], 3)[0]


def past_kernel(dwa_ref, hist_ref, cot_ref, grad_ref, part_ref, sums_ref):
    @pl.when(pl.program_id(0) == 0)
    def _():
        sums_ref[...] = jnp.zeros_like(sums_ref)

    grad = cot_ref[...].astype(jnp.float32)
    total = jnp.zeros_like(grad)
    for j in range(hist_ref.shape[0]):
        field = hist_ref[j].astype(jnp.float32)
        total += dwa_ref[j] * field
        grad_ref[j] = (dwa_ref[j] * grad).astype(jnp.bfloat16)
        sums_ref[j : j + 1, :] += jnp.sum(field * grad, axis=0, keepdims=True)
    part_ref[...] = total


def past(dwa, history, cot):
    count, rows, width = history.shape
    layers = pl.BlockSpec((count, ROWS, width), lambda i: (0, i, 0))
    tokens = pl.BlockSpec((ROWS, width), lambda i: (i, 0))
    return pl.pallas_call(
        past_kernel,
        grid=(rows // ROWS,),
        in_specs=[pl.BlockSpec(memory_space=pltpu.SMEM), layers, tokens],
        out_specs=[layers, tokens, whole_spec((8, width))],
        out_shape=[
            jax.ShapeDtypeStruct(history.shape, jnp.bfloat16),
            jax.ShapeDtypeStruct((rows, width), jnp.float32),
            jax.ShapeDtypeStruct((8, width), jnp.float32),
        ],
        compiler_params=pltpu.CompilerParams(vmem_limit_bytes=ROOM),
        cost_estimate=lasting(3),
    )(dwa, history, cot)


def present_kernel(flags, weight_ref, part_ref, own_ref, got_ref, out_ref, grad_ref):
    here = jnp.where(flags[0] == 1, own_ref[1], got_ref[1]).astype(jnp.float32)
    out_ref[...] = (part_ref[...] + weight_ref[weight_ref.shape[0] - 1] * here).astype(jnp.bfloat16)
    grad_ref[...] = jnp.where(flags[0] == 1, own_ref[0], got_ref[0])


def present(flags, weight, part, own, got):
    rows, width = part.shape
    both = (2, ROWS, width), lambda i, *scalars: (0, i, 0)
    out = ((rows, width), jnp.bfloat16, (ROWS, width), lambda i, *scalars: (i, 0))
    fields = [by_rows(part, ROWS), (own, *both), (got, *both)]
    return streamed(present_kernel, rows // ROWS, [flags, weight], fields, [out] * 2, [], 2, SNUG)


def blocks_kernel(flags, early_own, early_got, late_ref, *refs):
    parts, out_ref = refs[:-1], refs[-1]
    part = late_ref.shape[1]
    total = sum(ref[...].astype(jnp.float32) for ref in parts)
    out_ref[:, :part] = total.astype(jnp.bfloat16)
    out_ref[:, part : 2 * part] = jnp.where(flags[0] == 1, early_own[...], early_got[...])
    out_ref[:, 2 * part :] = late_ref[...]


def blocks_of(flags, early_own, early_got, late, parts):
    rows, part = late.shape
    out = ((rows, 3 * part), jnp.bfloat16)
    return streamed(blocks_kernel, 1, [flags], [early_own, early_got, late, *parts], [out], [], 1, SNUG)[0]


def place_kernel(flags, here_ref, there_ref, qkv_ref, out_ref, up_ref, down_ref):
    near, far = flags[1], flags[2]
    part = out_ref.shape[1]
    for k in range(2):
        for c in range(2):
            field = jnp.where(near == c, here_ref[k ^ far], there_ref[k ^ far]).astype(jnp.float32)
            if 2 * k + c < 3:
                qkv_ref[2 * k + c] = field[:, :part]
            else:
                out_ref[...] = field[:, :part]
            for half in range(2):
                at = (2 * half + k) * part
                (up_ref, down_ref)[c][:, at : at + part] = field[:, (1 + half) * part : (2 + half) * part]


def place(flags, here, there):
    rows, part = here.shape[1], here.shape[2] // 3
    outs = [((3, rows, part), jnp.float32), ((rows, part), jnp.float32)]
    outs += [((rows, 4 * part), jnp.float32)] * 2
    return streamed(place_kernel, 1, [flags], [here, there], outs, [], 3, SNUG)


AXES = ("tp", "dp", "far", "near")


def moves(chosen, move):
    sizes = [lax.axis_size(name) for name in AXES]
    places = [place for place in itertools.product(*map(range, sizes)) if chosen(*place)]
    index = lambda place: functools.reduce(lambda at, step: at * step[0] + step[1], zip(sizes, place), 0)
    return [(index(place), index(move(*place))) for place in places]


def away(t, d, k, c):
    return t != c


def anyone(t, d, k, c):
    return True


def swap_diagonal(field):
    return lax.ppermute(field, AXES, moves(away, lambda t, d, k, c: (c, d, k, t)))


def send_to_owner(field, other_far, other_tp):
    return lax.ppermute(
        field,
        AXES,
        moves(
            away if not other_far and not other_tp else anyone,
            lambda t, d, k, c: (c, d, k ^ other_far, t ^ other_tp),
        ),
    )


def swap_far_away(field):
    return lax.ppermute(field, AXES, moves(away, lambda t, d, k, c: (t, d, 1 - k, c)))


def swap_far(field):
    return lax.ppermute(field, "far", [(0, 1), (1, 0)])


def swap_near(field):
    return lax.ppermute(field, "near", [(0, 1), (1, 0)])


def after(field, *others):
    return lax.optimization_barrier((field, *others))[0]


def ordered(own, other, first, axis=0):
    return jnp.where(
        first, jnp.concatenate([own, other], axis=axis), jnp.concatenate([other, own], axis=axis)
    )


def part_of(field, index, axis):
    size = field.shape[axis] // 2
    return lax.dynamic_slice_in_dim(field, index * size, size, axis)


def add(*fields):
    return sum(field.astype(jnp.float32) for field in fields).astype(jnp.bfloat16)


def scatter_plane(pieces):
    return lax.psum_scatter(pieces, ("tp", "far"), scatter_dimension=0, tiled=True)[0]


def scatter_rows(piece):
    return lax.psum_scatter(piece, "dp", scatter_dimension=0, tiled=True)


def move_rows(block):
    dps = lax.axis_size("dp")
    if dps > 8:
        return [scatter_rows(block)]
    block = block.reshape(dps, block.shape[0] // dps, block.shape[1])
    place = lax.axis_index("dp")
    moved = [lax.dynamic_index_in_dim(block, place, 0, keepdims=False)]
    for step in range(1, dps):
        sent = lax.dynamic_index_in_dim(block, lax.rem(place + step, dps), 0, keepdims=False)
        moved.append(lax.ppermute(sent, "dp", [(d, (d + step) % dps) for d in range(dps)]))
    return moved


def sum_over(field, name):
    size = lax.axis_size(name)
    bit = 1
    while bit < size:
        field = field + lax.ppermute(field, name, [(d, d ^ bit) for d in range(size)])
        bit *= 2
    return field


def local(
    layer_input,
    history,
    cotangent,
    lengths,
    dwa_weights,
    gain_one,
    bias_one,
    w_qkv,
    w_out,
    gain_two,
    bias_two,
    w_up,
    w_down,
):
    rows = layer_input.shape[1]
    whole = rows * lax.axis_size("tp")
    hist_count = history.shape[0]
    part, far, near = lax.axis_index("tp"), lax.axis_index("far"), lax.axis_index("near")
    same = near == part
    flags = jnp.stack([same.astype(jnp.int32), near, far, part])

    input_got = swap_diagonal(layer_input[0])
    qkv_near = swap_diagonal(part_of(w_qkv, far, 1))
    qkv_far = swap_far_away(qkv_near)
    early_got = jnp.concatenate([part_of(w_up, 0, 1), part_of(w_down, 0, 0)], axis=0)
    late_got = jnp.concatenate([part_of(w_up, 1, 1), part_of(w_down, 1, 0)], axis=0)
    last_own = jnp.concatenate([w_out, cotangent[0]], axis=0)
    vectors = jnp.stack([gain_one, bias_one, gain_two, bias_two])

    own_lengths = jnp.where(same, lengths, swap_near(lengths))[0]
    seq_owner, token_place = positions(own_lengths, whole)
    lane = jnp.arange(LANES, dtype=jnp.int32)
    member = seq_owner[:, None] == lane[None, :]
    apart = jnp.where(member | (lane >= lengths.shape[1])[None, :], 0.0, NEG_FILL).astype(jnp.bfloat16)
    member = member.astype(jnp.bfloat16)
    half_dim = HEAD_DIM // 2
    frequency = jnp.exp((lane % half_dim).astype(jnp.float32) * (-math.log(10000.0) / half_dim))
    angles = token_place.astype(jnp.float32)[:, None] * frequency[None, :]
    cos_table = jnp.cos(angles)
    sin_table = jnp.sin(angles) * jnp.where(lane % HEAD_DIM < half_dim, -1.0, 1.0)[None, :]
    grad_history, past_sum, sums_past = past(dwa_weights, history[:, 0], cotangent[0])

    input_half = jnp.where(same, layer_input[0], input_got)
    layer_rows = ordered(input_half, swap_near(input_half), near == 0)
    layer_rows, vectors, past_sum, cos_table, sin_table, apart, member = lax.optimization_barrier(
        (layer_rows, vectors, past_sum, cos_table, sin_table, apart, member)
    )
    early_got = swap_diagonal(after(early_got, input_got))
    last_got = swap_diagonal(after(last_own, input_got))
    projected, norm_one_t = project(
        flags, layer_rows, vectors, cos_table, sin_table, w_qkv, qkv_near, qkv_far
    )
    mixed, logs = attend(apart, member, projected, LONGEST)
    late_got = swap_diagonal(after(late_got, mixed))
    last_got = jnp.where(same, last_own, after(last_got, mixed))
    weight_out = last_got[: w_out.shape[0]]
    attn = jnp.dot(mixed, weight_out, preferred_element_type=jnp.float32).astype(jnp.bfloat16)
    attn_got = swap_near(attn)
    cot_half = last_got[w_out.shape[0] :]
    scalars = [flags, dwa_weights]
    fields = [layer_rows, attn, attn_got, cot_half, swap_near(cot_half), vectors]
    *kept, resid, back, act_early, down_early, early_pieces = feed(True, scalars, fields, w_up, w_down, early_got)
    early_sum = scatter_plane(after(early_pieces, late_got))
    back, act_late, down_late, *late_owned = feed(
        False, [flags], [*kept, back], w_up, w_down, late_got
    )
    late_moved = [send_to_owner(late_owned[j], j // 2, j % 2) for j in range(4)]
    grad_down = kept[2]
    fields = [resid, grad_down, back, swap_near(back)]
    grad_attn, grad_mixed, grad_out, sums_two = middle(flags, fields, mixed, vectors, last_got)
    grad_qkv = attend_back(
        apart, member, cos_table, sin_table, projected, grad_mixed, mixed, logs, LONGEST
    )
    grad_qkv, *late_moved = lax.optimization_barrier((grad_qkv, *late_moved))
    owned = weigh(flags, norm_one_t, grad_qkv, grad_out)
    moved = [send_to_owner(owned[j], j // 2, j % 2) for j in range(4)]
    early_sum = scatter_rows(after(early_sum, grad_qkv))
    late_sum = scatter_rows(add(jnp.where(same, late_owned[0], after(late_moved[0], owned[0])), *late_moved[1:]))
    keep, *send, sums_one = unproject(
        flags, after(grad_qkv, owned[0]), (w_qkv, qkv_near, qkv_far), layer_rows
    )
    block_keep, *block_send, sums_now = lower(
        flags, act_early, act_late, down_early, down_late, resid, after(grad_down, keep)
    )
    sent = [*send, *block_send]
    keep, block_keep, *arrived = lax.optimization_barrier((keep, block_keep, *sent, *moved))
    sent, moved = arrived[:4], arrived[4:]
    attn_one = add(jnp.where(same, owned[0], moved[0]), *moved[1:])
    attn_moved = move_rows(attn_one)
    got = [swap_near(field) for field in sent]
    ours = last(flags, layer_rows, grad_attn, after(keep, attn_one), block_keep, got, vectors)
    early_sum = after(early_sum, attn_one)
    early_got = swap_diagonal(early_sum)
    small = jnp.concatenate([sums_one[:2], sums_two[:2], sums_now[:1], sums_past[:hist_count]], axis=0)
    small = after(small, ours)
    for name in ("tp", "far"):
        small = sum_over(small, name)
    theirs = swap_diagonal(ours)
    small, late_sum, early_sum, early_got, *attn_moved = lax.optimization_barrier(
        (small, late_sum, early_sum, early_got, *attn_moved)
    )
    for name in ("near", "dp"):
        small = sum_over(small, name)
    blocks = blocks_of(flags, early_sum, early_got, late_sum, attn_moved)
    here = after(jnp.stack([blocks, swap_far(blocks)]), small)
    grad_w_qkv, grad_w_out, grad_w_up, grad_w_down = place(flags, here, swap_near(here))
    output, grad_input = present(flags, dwa_weights, past_sum, ours, after(theirs, grad_w_up))

    return (
        output[None],
        grad_input[None],
        grad_history[:, None],
        jnp.sum(jnp.concatenate([small[5:], small[4:5] / dwa_weights[hist_count]], axis=0), axis=1),
        small[0],
        small[1],
        grad_w_qkv,
        grad_w_out.T,
        small[2],
        small[3],
        grad_w_up,
        grad_w_down.T,
    )


def positions(seq_lengths, token_count):
    seq_ends = jnp.cumsum(seq_lengths)
    seq_starts = seq_ends - seq_lengths
    token_index = jnp.arange(token_count, dtype=jnp.int32)
    seq_owner = jnp.sum((token_index[:, None] >= seq_ends[None, :]).astype(jnp.int32), axis=1)
    picked = (
        seq_owner[:, None] == jnp.arange(seq_lengths.shape[0], dtype=jnp.int32)[None, :]
    ).astype(jnp.int32)
    seq_begin = jnp.sum(picked * seq_starts[None, :], axis=1)
    return (seq_owner, token_index - seq_begin)


def solution(mesh):
    tps, dps, reps = (mesh.shape[name] for name in ("tp", "dp", "rep"))
    split = Mesh(mesh.devices.reshape(tps, dps, reps // 2, 2), AXES)
    in_specs = (
        P(("dp", "far", "near"), "tp", None),
        P(None, ("dp", "far", "near"), "tp", None),
        P(("dp", "far", "near"), "tp", None),
        P(("dp", "far", "near"), None),
        P(),
        P(),
        P(),
        P(None, None, "tp"),
        P("tp", None),
        P(),
        P(),
        P(None, "tp"),
        P("tp", None),
    )
    out_specs = (
        P(("dp", "far", "near"), "tp", None),
        P(("dp", "far", "near"), "tp", None),
        P(None, ("dp", "far", "near"), "tp", None),
        P(),
        P(),
        P(),
        P(None, "dp", "tp"),
        P("tp", "dp"),
        P(),
        P(),
        P("dp", "tp"),
        P("tp", "dp"),
    )
    return jax.shard_map(local, mesh=split, in_specs=in_specs, out_specs=out_specs, check_vma=False)
```

```python
import functools
import itertools
import math

import jax
import jax.numpy as jnp
from jax import lax
from jax.experimental import pallas as pl
from jax.experimental.pallas import tpu as pltpu
from jax.sharding import Mesh, PartitionSpec as P

HEAD_DIM = 64
LONGEST = 512
NEG_FILL = -1e30
NORM_EPS = 1e-05
RATE = 3e6
ROOM = 60 << 20
SNUG = 18 << 20


def lasting(microseconds):
    return pl.CostEstimate(flops=0, transcendentals=0, bytes_accessed=int(microseconds * RATE))


BLOCK = 256
LANES = 128
NT = (((1,), (1,)), ((), ()))


def dot(a, b, dims=(((1,), (0,)), ((), ()))):
    return lax.dot_general(a, b, dims, preferred_element_type=jnp.float32)


def spans(whole, reach):
    back = -(-(reach - 1) // BLOCK)
    runs = []
    for i in range(whole // BLOCK):
        count = min(i, back) + 1
        if runs and runs[-1][2] == count:
            runs[-1][1] = i + 1
        else:
            runs.append([i, i + 1, count])
    return runs


def each_block(whole, reach, body):
    for first, last, count in spans(whole, reach):

        def step(i, carry, count=count):
            body(i, i + 1 - count, count)
            return carry

        lax.fori_loop(first, last, step, 0)


def block_at(i, count=1):
    return pl.ds(pl.multiple_of(i * BLOCK, BLOCK), count * BLOCK)


def head_query(q_ref, apart_ref, i, head):
    lane = lax.broadcasted_iota(jnp.int32, (BLOCK, LANES), 1) // HEAD_DIM
    query = q_ref[block_at(i), :] * (HEAD_DIM**-0.5)
    query = jnp.where(lane == head, query, jnp.zeros_like(query))
    return query, jnp.concatenate([query, apart_ref[block_at(i), :]], axis=1)


def attend_kernel(reach, apart_ref, member_ref, q_ref, k_ref, v_ref, out_ref, logs_ref, keys):
    whole = q_ref.shape[0]
    lane = lax.broadcasted_iota(jnp.int32, (BLOCK, LANES), 1) // HEAD_DIM
    keys[:, :LANES] = k_ref[...]
    keys[:, LANES:] = member_ref[...]

    def one(i, first, count, head):
        unused, query = head_query(q_ref, apart_ref, i, head)
        own = dot(query, keys[block_at(i), :], NT)
        key_at = lax.broadcasted_iota(jnp.int32, own.shape, 1)
        query_at = lax.broadcasted_iota(jnp.int32, own.shape, 0)
        scores = jnp.where(key_at <= query_at, own, NEG_FILL)
        if count > 1:
            scores = jnp.concatenate([dot(query, keys[block_at(first, count - 1), :], NT), scores], axis=1)
        row_max = jnp.max(scores, axis=1, keepdims=True)
        exponent = jnp.exp(scores - row_max)
        row_sum = jnp.sum(exponent, axis=1, keepdims=True)
        mixed = dot(exponent.astype(jnp.bfloat16), v_ref[block_at(first, count), :]) * (1.0 / row_sum)
        return mixed, row_max + jnp.log(row_sum)

    def body(i, first, count):
        mixed, logs = zip(*[one(i, first, count, head) for head in range(2)])
        out_ref[block_at(i), :] = jnp.where(lane == 0, *mixed).astype(out_ref.dtype)
        turned = jnp.where(lane == 0, *logs).T
        for head in range(2):
            logs_ref[head : head + 1, block_at(i)] = turned[head * HEAD_DIM : head * HEAD_DIM + 1]

    each_block(whole, reach, body)


def attend(apart, member, projected, reach):
    count, whole, width = projected.shape

    def block(c):
        return pl.BlockSpec((None, whole, LANES), lambda p: (c, 0, p))

    table = pl.BlockSpec((whole, LANES), lambda p: (0, 0))
    return pl.pallas_call(
        functools.partial(attend_kernel, reach),
        grid=(width // LANES,),
        in_specs=[table, table, block(0), block(1), block(2)],
        out_specs=[
            pl.BlockSpec((whole, LANES), lambda p: (0, p)),
            pl.BlockSpec((None, 8, whole), lambda p: (p, 0, 0)),
        ],
        out_shape=[
            jax.ShapeDtypeStruct((whole, width), jnp.bfloat16),
            jax.ShapeDtypeStruct((width // LANES, 8, whole), jnp.float32),
        ],
        scratch_shapes=[pltpu.VMEM((whole, 2 * LANES), jnp.bfloat16)],
        compiler_params=pltpu.CompilerParams(vmem_limit_bytes=ROOM),
        cost_estimate=lasting(12),
    )(apart, member, projected, projected, projected)


def turn_back(field, cos, sin):
    half = HEAD_DIM // 2
    lane = lax.broadcasted_iota(jnp.int32, field.shape, 1) % HEAD_DIM
    crossed = jnp.where(lane < half, pltpu.roll(field, LANES - half, 1), pltpu.roll(field, half, 1))
    return field * cos - crossed * sin


def attend_back_kernel(
    reach, apart_ref, member_ref, cos_ref, sin_ref, q_ref, k_ref, v_ref, g_ref, mixed_ref, logs_ref, out_ref,
    keys, keys_t, key_acc, value_acc
):
    whole = q_ref.shape[0]
    lane = lax.broadcasted_iota(jnp.int32, (BLOCK, LANES), 1) // HEAD_DIM
    keys[:, :LANES] = k_ref[...]
    keys[:, LANES:] = member_ref[...]
    keys_t[...] = k_ref[...].astype(jnp.float32).T.astype(jnp.bfloat16)
    key_acc[...] = jnp.zeros_like(key_acc)
    value_acc[...] = jnp.zeros_like(value_acc)

    def one(i, first, count, head):
        span = block_at(first, count)
        plain, query = head_query(q_ref, apart_ref, i, head)
        grad = g_ref[block_at(i), :]
        grad = jnp.where(lane == head, grad, jnp.zeros_like(grad))
        own = dot(keys[block_at(i), :], query, NT)
        key_at = lax.broadcasted_iota(jnp.int32, own.shape, 0)
        query_at = lax.broadcasted_iota(jnp.int32, own.shape, 1)
        scores = jnp.where(key_at <= query_at, own, NEG_FILL)
        if count > 1:
            scores = jnp.concatenate([dot(keys[block_at(first, count - 1), :], query, NT), scores], axis=0)
        probs = jnp.exp(scores - logs_ref[head : head + 1, block_at(i)])
        grad_values = dot(probs.astype(jnp.bfloat16), grad)
        product = grad.astype(jnp.float32) * mixed_ref[block_at(i), :].astype(jnp.float32)
        high = product.astype(jnp.bfloat16)
        ones = jnp.ones((8, LANES), jnp.bfloat16)
        row_dot = dot(ones, high, NT) + dot(ones, (product - high.astype(jnp.float32)).astype(jnp.bfloat16), NT)
        grad_scores = (probs * (dot(v_ref[span, :], grad, NT) - row_dot[:1])).astype(jnp.bfloat16)
        here = dot(keys_t[:, span], grad_scores)
        return grad_values, dot(grad_scores, plain), here

    def body(i, first, count):
        span, at = block_at(first, count), block_at(i)
        values, keys_, queries = zip(*[one(i, first, count, head) for head in range(2)])
        value_acc[span, :] += values[0] + values[1]
        key_acc[span, :] += keys_[0] + keys_[1]
        row = lax.broadcasted_iota(jnp.int32, queries[0].shape, 0) // HEAD_DIM
        both = jnp.where(row == 0, *queries).T * (HEAD_DIM**-0.5)
        out_ref[0, at, :] = turn_back(both, cos_ref[at, :], sin_ref[at, :]).astype(out_ref.dtype)

    each_block(whole, reach, body)

    def finish(i, carry):
        at = block_at(i)
        out_ref[1, at, :] = turn_back(key_acc[at, :], cos_ref[at, :], sin_ref[at, :]).astype(out_ref.dtype)
        out_ref[2, at, :] = value_acc[at, :].astype(out_ref.dtype)
        return carry

    lax.fori_loop(0, whole // BLOCK, finish, 0)


def attend_back(apart, member, cos, sin, projected, grad_mixed, mixed, logs, reach):
    count, whole, width = projected.shape

    def block(c):
        return pl.BlockSpec((None, whole, LANES), lambda p: (c, 0, p))

    table = pl.BlockSpec((whole, LANES), lambda p: (0, 0))
    return pl.pallas_call(
        functools.partial(attend_back_kernel, reach),
        grid=(width // LANES,),
        in_specs=[table] * 4
        + [block(0), block(1), block(2)]
        + [pl.BlockSpec((whole, LANES), lambda p: (0, p))] * 2
        + [pl.BlockSpec((None, 8, whole), lambda p: (p, 0, 0))],
        out_specs=pl.BlockSpec((count, whole, LANES), lambda p: (0, 0, p)),
        out_shape=jax.ShapeDtypeStruct((count, whole, width), jnp.bfloat16),
        scratch_shapes=[
            pltpu.VMEM((whole, 2 * LANES), jnp.bfloat16),
            pltpu.VMEM((LANES, whole), jnp.bfloat16),
            pltpu.VMEM((whole, LANES), jnp.float32),
            pltpu.VMEM((whole, LANES), jnp.float32),
        ],
        compiler_params=pltpu.CompilerParams(vmem_limit_bytes=ROOM),
        cost_estimate=lasting(22),
    )(apart, member, cos, sin, projected, projected, projected, grad_mixed, mixed, logs)


ROWS = 256


def norm_parts(field):
    centered = field - jnp.mean(field, axis=-1, keepdims=True)
    scale = lax.rsqrt(jnp.mean(centered * centered, axis=-1, keepdims=True) + NORM_EPS)
    return centered * scale, scale


def wide(ref, at):
    return ref[at, :].astype(jnp.float32)


def row_blocks(count, body):
    def step(i, carry):
        body(i, pl.ds(pl.multiple_of(i * ROWS, ROWS), ROWS))
        return carry

    lax.fori_loop(0, count // ROWS, step, 0)


TALL = 512


def streamed(kernel, steps, scalars, fields, outs, scratch, microseconds, room=ROOM):
    def spec(shape, block=None, at=None):
        if block is None:
            return pl.BlockSpec(shape, lambda i, *scalars: (0,) * len(shape))
        return pl.BlockSpec(block, at)

    fields = [field if isinstance(field, tuple) else (field,) for field in fields]
    return pl.pallas_call(
        kernel,
        grid_spec=pltpu.PrefetchScalarGridSpec(
            num_scalar_prefetch=len(scalars),
            grid=(steps,),
            in_specs=[spec(field[0].shape, *field[1:]) for field in fields],
            out_specs=[spec(out[0], *out[2:]) for out in outs],
            scratch_shapes=[pltpu.VMEM(shape, dtype) for shape, dtype in scratch],
        ),
        out_shape=[jax.ShapeDtypeStruct(*out[:2]) for out in outs],
        compiler_params=pltpu.CompilerParams(vmem_limit_bytes=room),
        cost_estimate=lasting(microseconds),
    )(*scalars, *[field[0] for field in fields])


def by_rows(field, rows, shift=None):
    if shift is None:
        return field, (rows, field.shape[1]), lambda i, *scalars: (i, 0)
    return field, (rows, field.shape[1]), lambda i, *scalars: (shift(i, *scalars), 0)


def whole_spec(shape):
    return pl.BlockSpec(shape, lambda *at: (0,) * len(shape))


def turn(field, cos, sin):
    half = HEAD_DIM // 2
    lane = lax.broadcasted_iota(jnp.int32, field.shape, 1) % HEAD_DIM
    crossed = jnp.where(lane < half, pltpu.roll(field, LANES - half, 1), pltpu.roll(field, half, 1))
    return field * cos + crossed * sin


def join_rows(flags, own, near, far, out):
    half = near.shape[1]
    for index, got in ((flags[2], near), (1 - flags[2], far)):
        at = pl.ds(pl.multiple_of(index * half, half), half)
        out[:, at, :] = jnp.where(flags[0] == 1, own[:, at, :], got[...])


def project_kernel(flags, rows_ref, cos_ref, sin_ref, vectors, w_own, w_near, w_far, out_ref, turned_ref, weight_ref):
    @pl.when(pl.program_id(0) == 0)
    def _():
        join_rows(flags, w_own, w_near, w_far, weight_ref)

    unit, unused = norm_parts(rows_ref[...].astype(jnp.float32))
    norm = unit * vectors[0:1, :] + vectors[1:2, :]
    turned_ref[...] = norm.T.astype(jnp.bfloat16)
    norm = norm.astype(jnp.bfloat16)
    for c in range(weight_ref.shape[0]):
        field = dot(norm, weight_ref[c])
        if c == 2:
            out_ref[c] = field.astype(jnp.bfloat16)
        else:
            for p in range(field.shape[1] // LANES):
                lanes = slice(p * LANES, (p + 1) * LANES)
                out_ref[c, :, lanes] = turn(field[:, lanes], cos_ref[...], sin_ref[...]).astype(jnp.bfloat16)


def project(flags, rows, vectors, cos, sin, w_own, w_near, w_far):
    whole, width = rows.shape
    count, unused, columns = w_own.shape
    low = jnp.bfloat16
    return streamed(
        project_kernel,
        whole // ROWS,
        [flags],
        [by_rows(rows, ROWS), by_rows(cos, ROWS), by_rows(sin, ROWS), vectors, w_own, w_near, w_far],
        [
            ((count, whole, columns), low, (count, ROWS, columns), lambda i, flags: (0, i, 0)),
            ((width, whole), low, (width, ROWS), lambda i, flags: (0, i)),
        ],
        [(w_own.shape, low)],
        8,
    )


def gelu_both(up):
    root = math.sqrt(2.0 / math.pi)
    square = up * up
    bent = jnp.tanh(root * up * (1.0 + 0.044715 * square))
    half = 0.5 * (1.0 + bent)
    slope = half + 0.5 * up * (1.0 - bent * bent) * (root * (1.0 + 3.0 * 0.044715 * square))
    return up * half, slope


def feed_kernel(early, *refs):
    if early:
        flags, weight_ref, rows_ref, own_ref, got_ref, cot_here, cot_there, vectors, up_own, down_own, got = refs[:11]
        norm, norm_t, grad, grad_t, resid_ref, back_ref, act_ref, down_ref, pieces = refs[11:20]
    else:
        flags, norm, norm_t, grad, grad_t, back_early, up_own, down_own, got = refs[:9]
        back_ref, act_ref, down_ref, *pieces = refs[9:16]
    up_got, down_got = got.at[: norm.shape[1]], got.at[norm.shape[1] :]
    up_w, up_sum, down_sum = refs[-3:]
    part = up_w.shape[1] // 2
    step, last = pl.program_id(0), pl.num_programs(0) - 1

    @pl.when(step == 0)
    def _():
        up_w[...] = jnp.where(flags[0] == 1, up_own[...], up_got[...])
        down_ref[...] = jnp.where(flags[0] == 1, down_own[...], down_got[...])

    if early:

        def head(i, at):
            resid = wide(rows_ref, at) + wide(own_ref, at) + wide(got_ref, at)
            resid_ref[at, :] = resid.astype(jnp.bfloat16)
            unit, unused = norm_parts(resid)
            field = unit * vectors[2:3, :] + vectors[3:4, :]
            norm[at, :] = field.astype(jnp.bfloat16)
            norm_t[:, at] = field.T.astype(jnp.bfloat16)
            cot = jnp.where(flags[1] == step, cot_here[at, :], cot_there[at, :])
            field = cot.astype(jnp.float32) * weight_ref[weight_ref.shape[0] - 1]
            grad[at, :] = field.astype(jnp.bfloat16)
            grad_t[:, at] = field.T.astype(jnp.bfloat16)

        row_blocks(norm.shape[0], head)
    value, rise = gelu_both(dot(norm[...], up_w[...]))
    act_ref[...] = value.astype(jnp.bfloat16)
    slope = (dot(grad[...], down_ref[...], NT) * rise).astype(jnp.bfloat16)
    back = dot(slope, up_w[...], NT)
    if not early:
        back = back + back_early[...].astype(jnp.float32)
    back_ref[...] = back.astype(jnp.bfloat16)

    def store(p, at, low):
        if early:
            pieces[p, at, :] = low
            return
        slot = 2 * (flags[2] ^ (p % 2)) + (flags[3] ^ (p // 2))
        for j, piece in enumerate(pieces):

            @pl.when(slot == j)
            def _():
                piece[at, :] = low

    def grads(i, at):
        fields = (dot(norm_t[at, :], slope), dot(grad_t[at, :], act_ref[...]))
        for k, (field, total) in enumerate(zip(fields, (up_sum, down_sum))):

            @pl.when(step == 0)
            def _():
                total[at, :] = field

            @pl.when(step == last)
            def _():
                low = (total[at, :] + field).astype(jnp.bfloat16)
                for p in range(2):
                    store(2 * k + p, at, low[:, p * part : (p + 1) * part])

    row_blocks(norm_t.shape[0], grads)


def feed(early, scalars, fields, w_up, w_down, got):
    whole, width = fields[0].shape
    hidden = w_up.shape[1] // 2
    rows = whole // 2
    half = 0 if early else 1
    low = jnp.bfloat16

    def across(i, *scalars):
        return (0, i)

    tokens = ((whole, width), low, (rows, width), lambda i, *scalars: (i, 0))
    turned = ((width, whole), low, (width, rows), across)
    if early:
        operands = [by_rows(field, rows) for field in fields[:3]] + [*fields[3:]]
        outs = [tokens, turned, tokens, turned, tokens]
        pieces = [((4, width, hidden // 2), low)]
    else:
        operands = [by_rows(fields[0], rows), (fields[1], (width, rows), across)]
        operands += [by_rows(fields[2], rows), (fields[3], (width, rows), across), by_rows(fields[4], rows)]
        outs = []
        pieces = [((width, hidden // 2), low)] * 4
    operands += [
        (w_up, (width, hidden), lambda i, *scalars: (0, half)),
        (w_down, (hidden, width), lambda i, *scalars: (half, 0)),
        got,
    ]
    outs += [tokens, ((whole, hidden), low, (rows, hidden), lambda i, *scalars: (i, 0)), ((hidden, width), low)]
    sums = ((width, hidden), jnp.float32)
    return streamed(
        functools.partial(feed_kernel, early), 2, scalars, operands, outs + pieces, [((width, hidden), low), sums, sums], 17
    )


def lower_kernel(
    flags, act_early, act_late, resid_ref, cot_ref, early_ref, late_ref, keep_ref, first, second, sums_ref
):
    step = pl.program_id(0)
    total = dot(act_early[...], early_ref[...]) + dot(act_late[...], late_ref[...])
    cot = cot_ref[...].astype(jnp.float32)

    @pl.when(step == 0)
    def _():
        sums_ref[...] = jnp.zeros_like(sums_ref)

    mine = jnp.where(step < pl.num_programs(0) // 2, 0.0, 1.0)
    block = total + mine * resid_ref[...].astype(jnp.float32)
    send_or_keep(block, block, first, second, keep_ref)
    sums_ref[0:1, :] += jnp.sum(block * cot, axis=0, keepdims=True)


def send_or_keep(sent, kept, first, second, keep_ref):
    step = pl.program_id(0)
    for j, ref in enumerate((first, second)):

        @pl.when(step == j)
        def _():
            ref[...] = sent.astype(ref.dtype)

    @pl.when(step >= 2)
    def _():
        keep_ref[...] = kept.astype(keep_ref.dtype)


def theirs_first(i, flags, *more):
    return lax.rem((1 - flags[1]) * 2 + i, 4)


def sent_and_kept(whole, width):
    rows = whole // 4
    keep = ((2 * rows, width), jnp.bfloat16, (rows, width), lambda i, *scalars: (jnp.maximum(i - 2, 0), 0))
    send = ((rows, width), jnp.bfloat16)
    return [keep, send, send, ((8, width), jnp.float32)]


def lower(flags, act_early, act_late, down_early, down_late, resid, cot):
    whole, width = resid.shape
    fields = [by_rows(field, whole // 4, theirs_first) for field in (act_early, act_late, resid, cot)]
    return streamed(
        lower_kernel, 4, [flags], fields + [down_early, down_late], sent_and_kept(whole, width), [], 6, SNUG
    )


def middle_kernel(
    flags, resid_ref, cot_ref, back_own, back_got, mixed_ref,
    vectors, w_ref, grad_ref, gmixed_ref, gout_ref, sums_ref, gout,
):
    step, last = pl.program_id(0), pl.num_programs(0) - 1
    unit, scale = norm_parts(resid_ref[...].astype(jnp.float32))
    back = sum(ref[...].astype(jnp.float32) for ref in (back_own, back_got))
    inner = back * vectors[2:3, :]
    mean = jnp.mean(inner, axis=-1, keepdims=True)
    slant = jnp.mean(inner * unit, axis=-1, keepdims=True)
    grad = cot_ref[...].astype(jnp.float32) + scale * (inner - mean - unit * slant)
    low = grad.astype(jnp.bfloat16)
    grad_ref[...] = low
    gmixed_ref[...] = dot(low, w_ref[...], NT).astype(jnp.bfloat16)
    part = dot(grad.T.astype(jnp.bfloat16), mixed_ref[...])

    @pl.when(step == 0)
    def _():
        gout[...] = part
        sums_ref[...] = jnp.zeros_like(sums_ref)

    @pl.when(step > 0)
    def _():
        gout[...] += part

    @pl.when(step == last)
    def _():
        gout_ref[...] = gout[...].astype(jnp.bfloat16)

    @pl.when(step // ((last + 1) // 2) == flags[1])
    def _():
        sums_ref[0:1, :] += jnp.sum(back * unit, axis=0, keepdims=True)
        sums_ref[1:2, :] += jnp.sum(back, axis=0, keepdims=True)


def middle(flags, fields, mixed, vectors, bundle):
    whole, width = fields[0].shape
    columns = mixed.shape[1]
    low = jnp.bfloat16
    in_order = lambda i, *scalars: (i, 0)
    return streamed(
        middle_kernel,
        whole // ROWS,
        [flags],
        [by_rows(field, ROWS) for field in (*fields, mixed)]
        + [vectors, (bundle, (columns, width), lambda i, *scalars: (0, 0))],
        [
            ((whole, width), low, (ROWS, width), in_order),
            ((whole, columns), low, (ROWS, columns), in_order),
            ((width, columns), low),
            ((8, width), jnp.float32),
        ],
        [((width, columns), jnp.float32)],
        8,
    )


def weigh_kernel(flags, turned_ref, out_grad_ref, query_ref, key_ref, value_ref, *out_refs):
    rows = turned_ref[...]
    fields = [dot(rows, ref[...]).astype(jnp.bfloat16) for ref in (query_ref, key_ref, value_ref)]
    for piece, field in enumerate([*fields, out_grad_ref[...]]):
        slot = 2 * (flags[2] ^ (piece // 2)) + (flags[3] ^ (piece % 2))
        for j, out_ref in enumerate(out_refs):

            @pl.when(slot == j)
            def _():
                out_ref[...] = field


def weigh(flags, turned, grad, out_grad):
    width, columns = turned.shape[0], grad.shape[2]
    piece = ((width, columns), jnp.bfloat16, (ROWS, columns), lambda i, flags: (i, 0))
    fields = [by_rows(turned, ROWS), by_rows(out_grad, ROWS)]
    for c in range(3):
        fields.append((grad, (None, *grad.shape[1:]), lambda i, flags, c=c: (c, 0, 0)))
    return streamed(weigh_kernel, width // ROWS, [flags], fields, [piece] * 4, [], 4)


def unproject_kernel(flags, grad_ref, rows_ref, w_own, w_near, w_far, keep_ref, first, second, sums_ref, weight):
    @pl.when(pl.program_id(0) == 0)
    def _():
        join_rows(flags, w_own, w_near, w_far, weight)

    total = dot(grad_ref[0], weight[0], NT)
    for c in range(1, grad_ref.shape[0]):
        total = total + dot(grad_ref[c], weight[c], NT)
    unit, unused = norm_parts(rows_ref[...].astype(jnp.float32))

    @pl.when(pl.program_id(0) == 0)
    def _():
        sums_ref[...] = jnp.zeros_like(sums_ref)

    sums_ref[0:1, :] += jnp.sum(total * unit, axis=0, keepdims=True)
    sums_ref[1:2, :] += jnp.sum(total, axis=0, keepdims=True)
    send_or_keep(total, total, first, second, keep_ref)


def unproject(flags, grad, weights, rows):
    whole, width = rows.shape
    count, unused, columns = grad.shape
    grads = (grad, (count, whole // 4, columns), lambda i, flags: (0, theirs_first(i, flags), 0))
    fields = [grads, by_rows(rows, whole // 4, theirs_first), *weights]
    scratch = [((count, width, columns), jnp.bfloat16)]
    return streamed(unproject_kernel, 4, [flags], fields, sent_and_kept(whole, width), scratch, 5, SNUG + (4 << 20))


def last_kernel(
    flags, rows_ref, resid_ref, keep_ref, block_keep, got_first, got_second, block_first, block_second, vectors, out_ref
):
    first = pl.program_id(0) == 0
    unit, scale = norm_parts(rows_ref[...].astype(jnp.float32))
    got = jnp.where(first, got_first[...], got_second[...]).astype(jnp.float32)
    inner = (keep_ref[...].astype(jnp.float32) + got) * vectors[0:1, :]
    mean = jnp.mean(inner, axis=-1, keepdims=True)
    slant = jnp.mean(inner * unit, axis=-1, keepdims=True)
    grad = resid_ref[...].astype(jnp.float32) + scale * (inner - mean - unit * slant)
    out_ref[0] = grad.astype(jnp.bfloat16)
    got = jnp.where(first, block_first[...], block_second[...]).astype(jnp.float32)
    out_ref[1] = (block_keep[...].astype(jnp.float32) + got).astype(jnp.bfloat16)


def last(flags, rows, resid, keep, block_keep, got, vectors):
    half, width = keep.shape
    size = half // 2

    def mine(i, flags):
        return flags[1] * 2 + i

    out = ((2, half, width), jnp.bfloat16, (2, size, width), lambda i, flags: (0, i, 0))
    fields = [by_rows(rows, size, mine), by_rows(resid, size, mine), by_rows(keep, size), by_rows(block_keep, size)]
    return streamed(last_kernel, 2, [flags], fields + [*got, vectors], [out], [], 3)[0]


def past_kernel(dwa_ref, hist_ref, cot_ref, grad_ref, part_ref, sums_ref):
    @pl.when(pl.program_id(0) == 0)
    def _():
        sums_ref[...] = jnp.zeros_like(sums_ref)

    grad = cot_ref[...].astype(jnp.float32)
    total = jnp.zeros_like(grad)
    for j in range(hist_ref.shape[0]):
        field = hist_ref[j].astype(jnp.float32)
        total += dwa_ref[j] * field
        grad_ref[j] = (dwa_ref[j] * grad).astype(jnp.bfloat16)
        sums_ref[j : j + 1, :] += jnp.sum(field * grad, axis=0, keepdims=True)
    part_ref[...] = total


def past(dwa, history, cot):
    count, rows, width = history.shape
    layers = pl.BlockSpec((count, ROWS, width), lambda i: (0, i, 0))
    tokens = pl.BlockSpec((ROWS, width), lambda i: (i, 0))
    return pl.pallas_call(
        past_kernel,
        grid=(rows // ROWS,),
        in_specs=[pl.BlockSpec(memory_space=pltpu.SMEM), layers, tokens],
        out_specs=[layers, tokens, whole_spec((8, width))],
        out_shape=[
            jax.ShapeDtypeStruct(history.shape, jnp.bfloat16),
            jax.ShapeDtypeStruct((rows, width), jnp.float32),
            jax.ShapeDtypeStruct((8, width), jnp.float32),
        ],
        compiler_params=pltpu.CompilerParams(vmem_limit_bytes=ROOM),
        cost_estimate=lasting(3),
    )(dwa, history, cot)


def present_kernel(flags, weight_ref, part_ref, own_ref, got_ref, out_ref, grad_ref):
    here = jnp.where(flags[0] == 1, own_ref[1], got_ref[1]).astype(jnp.float32)
    out_ref[...] = (part_ref[...] + weight_ref[weight_ref.shape[0] - 1] * here).astype(jnp.bfloat16)
    grad_ref[...] = jnp.where(flags[0] == 1, own_ref[0], got_ref[0])


def present(flags, weight, part, own, got):
    rows, width = part.shape
    both = (2, ROWS, width), lambda i, *scalars: (0, i, 0)
    out = ((rows, width), jnp.bfloat16, (ROWS, width), lambda i, *scalars: (i, 0))
    fields = [by_rows(part, ROWS), (own, *both), (got, *both)]
    return streamed(present_kernel, rows // ROWS, [flags, weight], fields, [out] * 2, [], 2, SNUG)


def blocks_kernel(flags, early_own, early_got, late_ref, *refs):
    parts, out_ref = refs[:-1], refs[-1]
    part = late_ref.shape[1]
    total = sum(ref[...].astype(jnp.float32) for ref in parts)
    out_ref[:, :part] = total.astype(jnp.bfloat16)
    out_ref[:, part : 2 * part] = jnp.where(flags[0] == 1, early_own[...], early_got[...])
    out_ref[:, 2 * part :] = late_ref[...]


def blocks_of(flags, early_own, early_got, late, parts):
    rows, part = late.shape
    out = ((rows, 3 * part), jnp.bfloat16)
    return streamed(blocks_kernel, 1, [flags], [early_own, early_got, late, *parts], [out], [], 1, SNUG)[0]


def deal_kernel(flags, place_ref, own_ref, *refs):
    moved, outs, total = refs[:4], refs[4:-1], refs[-1]
    first = jnp.where(flags[0] == 1, own_ref[...], moved[0][...]).astype(jnp.float32)
    total[...] = (first + sum(ref[...].astype(jnp.float32) for ref in moved[1:])).astype(jnp.bfloat16)
    rows = outs[0].shape[0]
    for step, out_ref in enumerate(outs):
        at = lax.rem(place_ref[0] + step, len(outs)) * rows
        out_ref[...] = total[pl.ds(pl.multiple_of(at, rows), rows), :]


def deal(flags, own, moved, dps):
    depth, columns = own.shape
    place = lax.axis_index("dp")[None].astype(jnp.int32)
    outs = [((depth // dps, columns), jnp.bfloat16)] * dps
    return streamed(deal_kernel, 1, [flags, place], [own, *moved], outs, [(own.shape, jnp.bfloat16)], 1, SNUG)


def place_kernel(flags, here_ref, there_ref, qkv_ref, out_ref, up_ref, down_ref):
    near, far = flags[1], flags[2]
    part = out_ref.shape[1]
    for k in range(2):
        for c in range(2):
            field = jnp.where(near == c, here_ref[k ^ far], there_ref[k ^ far]).astype(jnp.float32)
            if 2 * k + c < 3:
                qkv_ref[2 * k + c] = field[:, :part]
            else:
                out_ref[...] = field[:, :part]
            for half in range(2):
                at = (2 * half + k) * part
                (up_ref, down_ref)[c][:, at : at + part] = field[:, (1 + half) * part : (2 + half) * part]


def place(flags, here, there):
    rows, part = here.shape[1], here.shape[2] // 3
    outs = [((3, rows, part), jnp.float32), ((rows, part), jnp.float32)]
    outs += [((rows, 4 * part), jnp.float32)] * 2
    return streamed(place_kernel, 1, [flags], [here, there], outs, [], 3, SNUG)


AXES = ("tp", "dp", "far", "near")


def moves(chosen, move):
    sizes = [lax.axis_size(name) for name in AXES]
    places = [place for place in itertools.product(*map(range, sizes)) if chosen(*place)]
    index = lambda place: functools.reduce(lambda at, step: at * step[0] + step[1], zip(sizes, place), 0)
    return [(index(place), index(move(*place))) for place in places]


def away(t, d, k, c):
    return t != c


def anyone(t, d, k, c):
    return True


def swap_diagonal(field):
    return lax.ppermute(field, AXES, moves(away, lambda t, d, k, c: (c, d, k, t)))


def send_to_owner(field, other_far, other_tp):
    return lax.ppermute(
        field,
        AXES,
        moves(
            away if not other_far and not other_tp else anyone,
            lambda t, d, k, c: (c, d, k ^ other_far, t ^ other_tp),
        ),
    )


def swap_far_away(field):
    return lax.ppermute(field, AXES, moves(away, lambda t, d, k, c: (t, d, 1 - k, c)))


def swap_far(field):
    return lax.ppermute(field, "far", [(0, 1), (1, 0)])


def swap_near(field):
    return lax.ppermute(field, "near", [(0, 1), (1, 0)])


def after(field, *others):
    return lax.optimization_barrier((field, *others))[0]


def ordered(own, other, first, axis=0):
    return jnp.where(
        first, jnp.concatenate([own, other], axis=axis), jnp.concatenate([other, own], axis=axis)
    )


def part_of(field, index, axis):
    size = field.shape[axis] // 2
    return lax.dynamic_slice_in_dim(field, index * size, size, axis)


def add(*fields):
    return sum(field.astype(jnp.float32) for field in fields).astype(jnp.bfloat16)


def scatter_plane(pieces):
    return lax.psum_scatter(pieces, ("tp", "far"), scatter_dimension=0, tiled=True)[0]


def scatter_rows(piece):
    return lax.psum_scatter(piece, "dp", scatter_dimension=0, tiled=True)


def move_rows(flags, own, moved):
    dps = lax.axis_size("dp")
    if dps > 8:
        return [scatter_rows(add(jnp.where(flags[0] == 1, own, moved[0]), *moved[1:]))]
    first, *rest = deal(flags, own, moved, dps)
    return [first] + [
        lax.ppermute(field, "dp", [(d, (d + step + 1) % dps) for d in range(dps)]) for step, field in enumerate(rest)
    ]


def sum_over(field, name):
    size = lax.axis_size(name)
    bit = 1
    while bit < size:
        field = field + lax.ppermute(field, name, [(d, d ^ bit) for d in range(size)])
        bit *= 2
    return field


def local(
    layer_input,
    history,
    cotangent,
    lengths,
    dwa_weights,
    gain_one,
    bias_one,
    w_qkv,
    w_out,
    gain_two,
    bias_two,
    w_up,
    w_down,
):
    rows = layer_input.shape[1]
    whole = rows * lax.axis_size("tp")
    hist_count = history.shape[0]
    part, far, near = lax.axis_index("tp"), lax.axis_index("far"), lax.axis_index("near")
    same = near == part
    flags = jnp.stack([same.astype(jnp.int32), near, far, part])

    input_got = swap_diagonal(layer_input[0])
    qkv_near = swap_diagonal(part_of(w_qkv, far, 1))
    qkv_far = swap_far_away(qkv_near)
    early_got = jnp.concatenate([part_of(w_up, 0, 1), part_of(w_down, 0, 0)], axis=0)
    late_got = jnp.concatenate([part_of(w_up, 1, 1), part_of(w_down, 1, 0)], axis=0)
    last_own = jnp.concatenate([w_out, cotangent[0]], axis=0)
    vectors = jnp.stack([gain_one, bias_one, gain_two, bias_two])

    own_lengths = jnp.where(same, lengths, swap_near(lengths))[0]
    seq_owner, token_place = positions(own_lengths, whole)
    lane = jnp.arange(LANES, dtype=jnp.int32)
    member = seq_owner[:, None] == lane[None, :]
    apart = jnp.where(member | (lane >= lengths.shape[1])[None, :], 0.0, NEG_FILL).astype(jnp.bfloat16)
    member = member.astype(jnp.bfloat16)
    half_dim = HEAD_DIM // 2
    frequency = jnp.exp((lane % half_dim).astype(jnp.float32) * (-math.log(10000.0) / half_dim))
    angles = token_place.astype(jnp.float32)[:, None] * frequency[None, :]
    cos_table = jnp.cos(angles)
    sin_table = jnp.sin(angles) * jnp.where(lane % HEAD_DIM < half_dim, -1.0, 1.0)[None, :]
    grad_history, past_sum, sums_past = past(dwa_weights, history[:, 0], cotangent[0])

    input_half = jnp.where(same, layer_input[0], input_got)
    layer_rows = ordered(input_half, swap_near(input_half), near == 0)
    layer_rows, vectors, past_sum, cos_table, sin_table, apart, member = lax.optimization_barrier(
        (layer_rows, vectors, past_sum, cos_table, sin_table, apart, member)
    )
    early_got = swap_diagonal(after(early_got, input_got))
    last_got = swap_diagonal(after(last_own, input_got))
    projected, norm_one_t = project(
        flags, layer_rows, vectors, cos_table, sin_table, w_qkv, qkv_near, qkv_far
    )
    mixed, logs = attend(apart, member, projected, LONGEST)
    late_got = swap_diagonal(after(late_got, mixed))
    last_got = jnp.where(same, last_own, after(last_got, mixed))
    weight_out = last_got[: w_out.shape[0]]
    attn = jnp.dot(mixed, weight_out, preferred_element_type=jnp.float32).astype(jnp.bfloat16)
    attn_got = swap_near(attn)
    cot_half = last_got[w_out.shape[0] :]
    scalars = [flags, dwa_weights]
    fields = [layer_rows, attn, attn_got, cot_half, swap_near(cot_half), vectors]
    *kept, resid, back, act_early, down_early, early_pieces = feed(True, scalars, fields, w_up, w_down, early_got)
    early_sum = scatter_plane(after(early_pieces, late_got))
    back, act_late, down_late, *late_owned = feed(
        False, [flags], [*kept, back], w_up, w_down, late_got
    )
    late_moved = [send_to_owner(late_owned[j], j // 2, j % 2) for j in range(4)]
    grad_down = kept[2]
    fields = [resid, grad_down, back, swap_near(back)]
    grad_attn, grad_mixed, grad_out, sums_two = middle(flags, fields, mixed, vectors, last_got)
    grad_qkv = attend_back(
        apart, member, cos_table, sin_table, projected, grad_mixed, mixed, logs, LONGEST
    )
    grad_qkv, *late_moved = lax.optimization_barrier((grad_qkv, *late_moved))
    owned = weigh(flags, norm_one_t, grad_qkv, grad_out)
    moved = [send_to_owner(owned[j], j // 2, j % 2) for j in range(4)]
    early_sum = scatter_rows(after(early_sum, grad_qkv))
    late_sum = scatter_rows(add(jnp.where(same, late_owned[0], after(late_moved[0], owned[0])), *late_moved[1:]))
    keep, *send, sums_one = unproject(
        flags, after(grad_qkv, owned[0]), (w_qkv, qkv_near, qkv_far), layer_rows
    )
    block_keep, *block_send, sums_now = lower(
        flags, act_early, act_late, down_early, down_late, resid, after(grad_down, keep)
    )
    sent = [*send, *block_send]
    keep, block_keep, *arrived = lax.optimization_barrier((keep, block_keep, *sent, *moved))
    sent, moved = arrived[:4], arrived[4:]
    attn_moved = move_rows(flags, owned[0], moved)
    attn_one = attn_moved[0]
    got = [swap_near(field) for field in sent]
    ours = last(flags, layer_rows, grad_attn, after(keep, attn_one), block_keep, got, vectors)
    early_sum = after(early_sum, attn_one)
    early_got = swap_diagonal(early_sum)
    small = jnp.concatenate([sums_one[:2], sums_two[:2], sums_now[:1], sums_past[:hist_count]], axis=0)
    small = after(small, ours)
    for name in ("tp", "far"):
        small = sum_over(small, name)
    theirs = swap_diagonal(ours)
    small, late_sum, early_sum, early_got, *attn_moved = lax.optimization_barrier(
        (small, late_sum, early_sum, early_got, *attn_moved)
    )
    for name in ("near", "dp"):
        small = sum_over(small, name)
    blocks = blocks_of(flags, early_sum, early_got, late_sum, attn_moved)
    here = after(jnp.stack([blocks, swap_far(blocks)]), small)
    grad_w_qkv, grad_w_out, grad_w_up, grad_w_down = place(flags, here, swap_near(here))
    output, grad_input = present(flags, dwa_weights, past_sum, ours, after(theirs, grad_w_up))

    return (
        output[None],
        grad_input[None],
        grad_history[:, None],
        jnp.sum(jnp.concatenate([small[5:], small[4:5] / dwa_weights[hist_count]], axis=0), axis=1),
        small[0],
        small[1],
        grad_w_qkv,
        grad_w_out.T,
        small[2],
        small[3],
        grad_w_up,
        grad_w_down.T,
    )


def positions(seq_lengths, token_count):
    seq_ends = jnp.cumsum(seq_lengths)
    seq_starts = seq_ends - seq_lengths
    token_index = jnp.arange(token_count, dtype=jnp.int32)
    seq_owner = jnp.sum((token_index[:, None] >= seq_ends[None, :]).astype(jnp.int32), axis=1)
    picked = (
        seq_owner[:, None] == jnp.arange(seq_lengths.shape[0], dtype=jnp.int32)[None, :]
    ).astype(jnp.int32)
    seq_begin = jnp.sum(picked * seq_starts[None, :], axis=1)
    return (seq_owner, token_index - seq_begin)


def solution(mesh):
    tps, dps, reps = (mesh.shape[name] for name in ("tp", "dp", "rep"))
    split = Mesh(mesh.devices.reshape(tps, dps, reps // 2, 2), AXES)
    in_specs = (
        P(("dp", "far", "near"), "tp", None),
        P(None, ("dp", "far", "near"), "tp", None),
        P(("dp", "far", "near"), "tp", None),
        P(("dp", "far", "near"), None),
        P(),
        P(),
        P(),
        P(None, None, "tp"),
        P("tp", None),
        P(),
        P(),
        P(None, "tp"),
        P("tp", None),
    )
    out_specs = (
        P(("dp", "far", "near"), "tp", None),
        P(("dp", "far", "near"), "tp", None),
        P(None, ("dp", "far", "near"), "tp", None),
        P(),
        P(),
        P(),
        P(None, "dp", "tp"),
        P("tp", "dp"),
        P(),
        P(),
        P("dp", "tp"),
        P("tp", "dp"),
    )
    return jax.shard_map(local, mesh=split, in_specs=in_specs, out_specs=out_specs, check_vma=False)
```

```python
import functools
import itertools
import math

import jax
import jax.numpy as jnp
from jax import lax
from jax.experimental import pallas as pl
from jax.experimental.pallas import tpu as pltpu
from jax.sharding import Mesh, PartitionSpec as P

HEAD_DIM = 64
LONGEST = 512
NEG_FILL = -1e30
NORM_EPS = 1e-05
RATE = 3e6
ROOM = 60 << 20
SNUG = 18 << 20


def lasting(microseconds):
    return pl.CostEstimate(flops=0, transcendentals=0, bytes_accessed=int(microseconds * RATE))


BLOCK = 256
LANES = 128
NT = (((1,), (1,)), ((), ()))


def dot(a, b, dims=(((1,), (0,)), ((), ()))):
    return lax.dot_general(a, b, dims, preferred_element_type=jnp.float32)


def spans(whole, reach):
    back = -(-(reach - 1) // BLOCK)
    runs = []
    for i in range(whole // BLOCK):
        count = min(i, back) + 1
        if runs and runs[-1][2] == count:
            runs[-1][1] = i + 1
        else:
            runs.append([i, i + 1, count])
    return runs


def each_block(whole, reach, body):
    for first, last, count in spans(whole, reach):

        def step(i, carry, count=count):
            body(i, i + 1 - count, count)
            return carry

        lax.fori_loop(first, last, step, 0)


def block_at(i, count=1):
    return pl.ds(pl.multiple_of(i * BLOCK, BLOCK), count * BLOCK)


def head_query(q_ref, apart_ref, i, head):
    lane = lax.broadcasted_iota(jnp.int32, (BLOCK, LANES), 1) // HEAD_DIM
    query = q_ref[block_at(i), :] * (HEAD_DIM**-0.5)
    query = jnp.where(lane == head, query, jnp.zeros_like(query))
    return query, jnp.concatenate([query, apart_ref[block_at(i), :]], axis=1)


def attend_kernel(reach, apart_ref, member_ref, q_ref, k_ref, v_ref, out_ref, logs_ref, keys):
    whole = q_ref.shape[0]
    lane = lax.broadcasted_iota(jnp.int32, (BLOCK, LANES), 1) // HEAD_DIM
    keys[:, :LANES] = k_ref[...]
    keys[:, LANES:] = member_ref[...]

    def one(i, first, count, head):
        unused, query = head_query(q_ref, apart_ref, i, head)
        own = dot(query, keys[block_at(i), :], NT)
        key_at = lax.broadcasted_iota(jnp.int32, own.shape, 1)
        query_at = lax.broadcasted_iota(jnp.int32, own.shape, 0)
        scores = jnp.where(key_at <= query_at, own, NEG_FILL)
        if count > 1:
            scores = jnp.concatenate([dot(query, keys[block_at(first, count - 1), :], NT), scores], axis=1)
        row_max = jnp.max(scores, axis=1, keepdims=True)
        exponent = jnp.exp(scores - row_max)
        row_sum = jnp.sum(exponent, axis=1, keepdims=True)
        mixed = dot(exponent.astype(jnp.bfloat16), v_ref[block_at(first, count), :]) * (1.0 / row_sum)
        return mixed, row_max + jnp.log(row_sum)

    def body(i, first, count):
        mixed, logs = zip(*[one(i, first, count, head) for head in range(2)])
        out_ref[block_at(i), :] = jnp.where(lane == 0, *mixed).astype(out_ref.dtype)
        turned = jnp.where(lane == 0, *logs).T
        for head in range(2):
            logs_ref[head : head + 1, block_at(i)] = turned[head * HEAD_DIM : head * HEAD_DIM + 1]

    each_block(whole, reach, body)


def attend(apart, member, projected, reach):
    count, whole, width = projected.shape

    def block(c):
        return pl.BlockSpec((None, whole, LANES), lambda p: (c, 0, p))

    table = pl.BlockSpec((whole, LANES), lambda p: (0, 0))
    return pl.pallas_call(
        functools.partial(attend_kernel, reach),
        grid=(width // LANES,),
        in_specs=[table, table, block(0), block(1), block(2)],
        out_specs=[
            pl.BlockSpec((whole, LANES), lambda p: (0, p)),
            pl.BlockSpec((None, 8, whole), lambda p: (p, 0, 0)),
        ],
        out_shape=[
            jax.ShapeDtypeStruct((whole, width), jnp.bfloat16),
            jax.ShapeDtypeStruct((width // LANES, 8, whole), jnp.float32),
        ],
        scratch_shapes=[pltpu.VMEM((whole, 2 * LANES), jnp.bfloat16)],
        compiler_params=pltpu.CompilerParams(vmem_limit_bytes=ROOM),
        cost_estimate=lasting(12),
    )(apart, member, projected, projected, projected)


def turn_back(field, cos, sin):
    half = HEAD_DIM // 2
    lane = lax.broadcasted_iota(jnp.int32, field.shape, 1) % HEAD_DIM
    crossed = jnp.where(lane < half, pltpu.roll(field, LANES - half, 1), pltpu.roll(field, half, 1))
    return field * cos - crossed * sin


def attend_back_kernel(
    reach, apart_ref, member_ref, cos_ref, sin_ref, q_ref, k_ref, v_ref, g_ref, mixed_ref, logs_ref, out_ref,
    keys, keys_t, key_acc, value_acc
):
    whole = q_ref.shape[0]
    lane = lax.broadcasted_iota(jnp.int32, (BLOCK, LANES), 1) // HEAD_DIM
    keys[:, :LANES] = k_ref[...]
    keys[:, LANES:] = member_ref[...]
    keys_t[...] = k_ref[...].astype(jnp.float32).T.astype(jnp.bfloat16)
    key_acc[...] = jnp.zeros_like(key_acc)
    value_acc[...] = jnp.zeros_like(value_acc)

    def one(i, first, count, head):
        span = block_at(first, count)
        plain, query = head_query(q_ref, apart_ref, i, head)
        grad = g_ref[block_at(i), :]
        grad = jnp.where(lane == head, grad, jnp.zeros_like(grad))
        own = dot(keys[block_at(i), :], query, NT)
        key_at = lax.broadcasted_iota(jnp.int32, own.shape, 0)
        query_at = lax.broadcasted_iota(jnp.int32, own.shape, 1)
        scores = jnp.where(key_at <= query_at, own, NEG_FILL)
        if count > 1:
            scores = jnp.concatenate([dot(keys[block_at(first, count - 1), :], query, NT), scores], axis=0)
        probs = jnp.exp(scores - logs_ref[head : head + 1, block_at(i)])
        grad_values = dot(probs.astype(jnp.bfloat16), grad)
        product = grad.astype(jnp.float32) * mixed_ref[block_at(i), :].astype(jnp.float32)
        high = product.astype(jnp.bfloat16)
        ones = jnp.ones((8, LANES), jnp.bfloat16)
        row_dot = dot(ones, high, NT) + dot(ones, (product - high.astype(jnp.float32)).astype(jnp.bfloat16), NT)
        grad_scores = (probs * (dot(v_ref[span, :], grad, NT) - row_dot[:1])).astype(jnp.bfloat16)
        here = dot(keys_t[:, span], grad_scores)
        return grad_values, dot(grad_scores, plain), here

    def body(i, first, count):
        span, at = block_at(first, count), block_at(i)
        values, keys_, queries = zip(*[one(i, first, count, head) for head in range(2)])
        value_acc[span, :] += values[0] + values[1]
        key_acc[span, :] += keys_[0] + keys_[1]
        row = lax.broadcasted_iota(jnp.int32, queries[0].shape, 0) // HEAD_DIM
        both = jnp.where(row == 0, *queries).T * (HEAD_DIM**-0.5)
        out_ref[0, at, :] = turn_back(both, cos_ref[at, :], sin_ref[at, :]).astype(out_ref.dtype)

    each_block(whole, reach, body)

    def finish(i, carry):
        at = block_at(i)
        out_ref[1, at, :] = turn_back(key_acc[at, :], cos_ref[at, :], sin_ref[at, :]).astype(out_ref.dtype)
        out_ref[2, at, :] = value_acc[at, :].astype(out_ref.dtype)
        return carry

    lax.fori_loop(0, whole // BLOCK, finish, 0)


def attend_back(apart, member, cos, sin, projected, grad_mixed, mixed, logs, reach):
    count, whole, width = projected.shape

    def block(c):
        return pl.BlockSpec((None, whole, LANES), lambda p: (c, 0, p))

    table = pl.BlockSpec((whole, LANES), lambda p: (0, 0))
    return pl.pallas_call(
        functools.partial(attend_back_kernel, reach),
        grid=(width // LANES,),
        in_specs=[table] * 4
        + [block(0), block(1), block(2)]
        + [pl.BlockSpec((whole, LANES), lambda p: (0, p))] * 2
        + [pl.BlockSpec((None, 8, whole), lambda p: (p, 0, 0))],
        out_specs=pl.BlockSpec((count, whole, LANES), lambda p: (0, 0, p)),
        out_shape=jax.ShapeDtypeStruct((count, whole, width), jnp.bfloat16),
        scratch_shapes=[
            pltpu.VMEM((whole, 2 * LANES), jnp.bfloat16),
            pltpu.VMEM((LANES, whole), jnp.bfloat16),
            pltpu.VMEM((whole, LANES), jnp.float32),
            pltpu.VMEM((whole, LANES), jnp.float32),
        ],
        compiler_params=pltpu.CompilerParams(vmem_limit_bytes=ROOM),
        cost_estimate=lasting(22),
    )(apart, member, cos, sin, projected, projected, projected, grad_mixed, mixed, logs)


ROWS = 256


def norm_parts(field):
    centered = field - jnp.mean(field, axis=-1, keepdims=True)
    scale = lax.rsqrt(jnp.mean(centered * centered, axis=-1, keepdims=True) + NORM_EPS)
    return centered * scale, scale


def wide(ref, at):
    return ref[at, :].astype(jnp.float32)


def row_blocks(count, body):
    def step(i, carry):
        body(i, pl.ds(pl.multiple_of(i * ROWS, ROWS), ROWS))
        return carry

    lax.fori_loop(0, count // ROWS, step, 0)


TALL = 512


def streamed(kernel, steps, scalars, fields, outs, scratch, microseconds, room=ROOM):
    def spec(shape, block=None, at=None):
        if block is None:
            return pl.BlockSpec(shape, lambda i, *scalars: (0,) * len(shape))
        return pl.BlockSpec(block, at)

    fields = [field if isinstance(field, tuple) else (field,) for field in fields]
    return pl.pallas_call(
        kernel,
        grid_spec=pltpu.PrefetchScalarGridSpec(
            num_scalar_prefetch=len(scalars),
            grid=(steps,),
            in_specs=[spec(field[0].shape, *field[1:]) for field in fields],
            out_specs=[spec(out[0], *out[2:]) for out in outs],
            scratch_shapes=[pltpu.VMEM(shape, dtype) for shape, dtype in scratch],
        ),
        out_shape=[jax.ShapeDtypeStruct(*out[:2]) for out in outs],
        compiler_params=pltpu.CompilerParams(vmem_limit_bytes=room),
        cost_estimate=lasting(microseconds),
    )(*scalars, *[field[0] for field in fields])


def by_rows(field, rows, shift=None):
    if shift is None:
        return field, (rows, field.shape[1]), lambda i, *scalars: (i, 0)
    return field, (rows, field.shape[1]), lambda i, *scalars: (shift(i, *scalars), 0)


def whole_spec(shape):
    return pl.BlockSpec(shape, lambda *at: (0,) * len(shape))


def turn(field, cos, sin):
    half = HEAD_DIM // 2
    lane = lax.broadcasted_iota(jnp.int32, field.shape, 1) % HEAD_DIM
    crossed = jnp.where(lane < half, pltpu.roll(field, LANES - half, 1), pltpu.roll(field, half, 1))
    return field * cos + crossed * sin


def join_rows(flags, own, near, far, out):
    half = near.shape[1]
    for index, got in ((flags[2], near), (1 - flags[2], far)):
        at = pl.ds(pl.multiple_of(index * half, half), half)
        out[:, at, :] = jnp.where(flags[0] == 1, own[:, at, :], got[...])


def project_kernel(flags, rows_ref, cos_ref, sin_ref, vectors, w_own, w_near, w_far, out_ref, turned_ref, weight_ref):
    @pl.when(pl.program_id(0) == 0)
    def _():
        join_rows(flags, w_own, w_near, w_far, weight_ref)

    unit, unused = norm_parts(rows_ref[...].astype(jnp.float32))
    norm = unit * vectors[0:1, :] + vectors[1:2, :]
    turned_ref[...] = norm.T.astype(jnp.bfloat16)
    norm = norm.astype(jnp.bfloat16)
    for c in range(weight_ref.shape[0]):
        field = dot(norm, weight_ref[c])
        if c == 2:
            out_ref[c] = field.astype(jnp.bfloat16)
        else:
            for p in range(field.shape[1] // LANES):
                lanes = slice(p * LANES, (p + 1) * LANES)
                out_ref[c, :, lanes] = turn(field[:, lanes], cos_ref[...], sin_ref[...]).astype(jnp.bfloat16)


def project(flags, rows, vectors, cos, sin, w_own, w_near, w_far):
    whole, width = rows.shape
    count, unused, columns = w_own.shape
    low = jnp.bfloat16
    return streamed(
        project_kernel,
        whole // ROWS,
        [flags],
        [by_rows(rows, ROWS), by_rows(cos, ROWS), by_rows(sin, ROWS), vectors, w_own, w_near, w_far],
        [
            ((count, whole, columns), low, (count, ROWS, columns), lambda i, flags: (0, i, 0)),
            ((width, whole), low, (width, ROWS), lambda i, flags: (0, i)),
        ],
        [(w_own.shape, low)],
        8,
    )


def gelu_both(up):
    root = math.sqrt(2.0 / math.pi)
    square = up * up
    bent = jnp.tanh(root * up * (1.0 + 0.044715 * square))
    half = 0.5 * (1.0 + bent)
    slope = half + 0.5 * up * (1.0 - bent * bent) * (root * (1.0 + 3.0 * 0.044715 * square))
    return up * half, slope


def feed_kernel(early, *refs):
    if early:
        flags, weight_ref, rows_ref, own_ref, got_ref, cot_here, cot_there, vectors, up_own, down_own, got = refs[:11]
        norm, norm_t, grad, grad_t, resid_ref, back_ref, act_ref, down_ref, pieces = refs[11:20]
    else:
        flags, norm, norm_t, grad, grad_t, back_early, up_own, down_own, got = refs[:9]
        back_ref, act_ref, down_ref, *pieces = refs[9:16]
    up_got, down_got = got.at[: norm.shape[1]], got.at[norm.shape[1] :]
    up_w, up_sum, down_sum = refs[-3:]
    part = up_w.shape[1] // 2
    step, last = pl.program_id(0), pl.num_programs(0) - 1

    @pl.when(step == 0)
    def _():
        up_w[...] = jnp.where(flags[0] == 1, up_own[...], up_got[...])
        down_ref[...] = jnp.where(flags[0] == 1, down_own[...], down_got[...])

    if early:

        def head(i, at):
            resid = wide(rows_ref, at) + wide(own_ref, at) + wide(got_ref, at)
            resid_ref[at, :] = resid.astype(jnp.bfloat16)
            unit, unused = norm_parts(resid)
            field = unit * vectors[2:3, :] + vectors[3:4, :]
            norm[at, :] = field.astype(jnp.bfloat16)
            norm_t[:, at] = field.T.astype(jnp.bfloat16)
            cot = jnp.where(flags[1] == step, cot_here[at, :], cot_there[at, :])
            field = cot.astype(jnp.float32) * weight_ref[weight_ref.shape[0] - 1]
            grad[at, :] = field.astype(jnp.bfloat16)
            grad_t[:, at] = field.T.astype(jnp.bfloat16)

        row_blocks(norm.shape[0], head)
    value, rise = gelu_both(dot(norm[...], up_w[...]))
    act_ref[...] = value.astype(jnp.bfloat16)
    slope = (dot(grad[...], down_ref[...], NT) * rise).astype(jnp.bfloat16)
    back = dot(slope, up_w[...], NT)
    if not early:
        back = back + back_early[...].astype(jnp.float32)
    back_ref[...] = back.astype(jnp.bfloat16)

    def store(p, at, low):
        if early:
            pieces[p, at, :] = low
            return
        slot = 2 * (flags[2] ^ (p % 2)) + (flags[3] ^ (p // 2))
        for j, piece in enumerate(pieces):

            @pl.when(slot == j)
            def _():
                piece[at, :] = low

    def grads(i, at):
        fields = (dot(norm_t[at, :], slope), dot(grad_t[at, :], act_ref[...]))
        for k, (field, total) in enumerate(zip(fields, (up_sum, down_sum))):

            @pl.when(step == 0)
            def _():
                total[at, :] = field

            @pl.when(step == last)
            def _():
                low = (total[at, :] + field).astype(jnp.bfloat16)
                for p in range(2):
                    store(2 * k + p, at, low[:, p * part : (p + 1) * part])

    row_blocks(norm_t.shape[0], grads)


def feed(early, scalars, fields, w_up, w_down, got):
    whole, width = fields[0].shape
    hidden = w_up.shape[1] // 2
    rows = whole // 2
    half = 0 if early else 1
    low = jnp.bfloat16

    def across(i, *scalars):
        return (0, i)

    tokens = ((whole, width), low, (rows, width), lambda i, *scalars: (i, 0))
    turned = ((width, whole), low, (width, rows), across)
    if early:
        operands = [by_rows(field, rows) for field in fields[:3]] + [*fields[3:]]
        outs = [tokens, turned, tokens, turned, tokens]
        pieces = [((4, width, hidden // 2), low)]
    else:
        operands = [by_rows(fields[0], rows), (fields[1], (width, rows), across)]
        operands += [by_rows(fields[2], rows), (fields[3], (width, rows), across), by_rows(fields[4], rows)]
        outs = []
        pieces = [((width, hidden // 2), low)] * 4
    operands += [
        (w_up, (width, hidden), lambda i, *scalars: (0, half)),
        (w_down, (hidden, width), lambda i, *scalars: (half, 0)),
        got,
    ]
    outs += [tokens, ((whole, hidden), low, (rows, hidden), lambda i, *scalars: (i, 0)), ((hidden, width), low)]
    sums = ((width, hidden), jnp.float32)
    return streamed(
        functools.partial(feed_kernel, early), 2, scalars, operands, outs + pieces, [((width, hidden), low), sums, sums], 17
    )


def lower_kernel(
    flags, act_early, act_late, resid_ref, cot_ref, early_ref, late_ref, keep_ref, first, second, sums_ref
):
    step = pl.program_id(0)
    total = dot(act_early[...], early_ref[...]) + dot(act_late[...], late_ref[...])
    cot = cot_ref[...].astype(jnp.float32)

    @pl.when(step == 0)
    def _():
        sums_ref[...] = jnp.zeros_like(sums_ref)

    mine = jnp.where(step < pl.num_programs(0) // 2, 0.0, 1.0)
    block = total + mine * resid_ref[...].astype(jnp.float32)
    send_or_keep(block, block, first, second, keep_ref)
    sums_ref[0:1, :] += jnp.sum(block * cot, axis=0, keepdims=True)


def send_or_keep(sent, kept, first, second, keep_ref):
    step = pl.program_id(0)
    for j, ref in enumerate((first, second)):

        @pl.when(step == j)
        def _():
            ref[...] = sent.astype(ref.dtype)

    @pl.when(step >= 2)
    def _():
        keep_ref[...] = kept.astype(keep_ref.dtype)


def theirs_first(i, flags, *more):
    return lax.rem((1 - flags[1]) * 2 + i, 4)


def sent_and_kept(whole, width):
    rows = whole // 4
    keep = ((2 * rows, width), jnp.bfloat16, (rows, width), lambda i, *scalars: (jnp.maximum(i - 2, 0), 0))
    send = ((rows, width), jnp.bfloat16)
    return [keep, send, send, ((8, width), jnp.float32)]


def lower(flags, act_early, act_late, down_early, down_late, resid, cot):
    whole, width = resid.shape
    fields = [by_rows(field, whole // 4, theirs_first) for field in (act_early, act_late, resid, cot)]
    return streamed(
        lower_kernel, 4, [flags], fields + [down_early, down_late], sent_and_kept(whole, width), [], 6, SNUG
    )


def middle_kernel(
    flags, resid_ref, cot_ref, back_own, back_got, mixed_ref,
    vectors, w_ref, grad_ref, gmixed_ref, gout_ref, sums_ref, gout,
):
    step, last = pl.program_id(0), pl.num_programs(0) - 1
    unit, scale = norm_parts(resid_ref[...].astype(jnp.float32))
    back = sum(ref[...].astype(jnp.float32) for ref in (back_own, back_got))
    inner = back * vectors[2:3, :]
    mean = jnp.mean(inner, axis=-1, keepdims=True)
    slant = jnp.mean(inner * unit, axis=-1, keepdims=True)
    grad = cot_ref[...].astype(jnp.float32) + scale * (inner - mean - unit * slant)
    low = grad.astype(jnp.bfloat16)
    grad_ref[...] = low
    gmixed_ref[...] = dot(low, w_ref[...], NT).astype(jnp.bfloat16)
    part = dot(grad.T.astype(jnp.bfloat16), mixed_ref[...])

    @pl.when(step == 0)
    def _():
        gout[...] = part
        sums_ref[...] = jnp.zeros_like(sums_ref)

    @pl.when(step > 0)
    def _():
        gout[...] += part

    @pl.when(step == last)
    def _():
        gout_ref[...] = gout[...].astype(jnp.bfloat16)

    @pl.when(step // ((last + 1) // 2) == flags[1])
    def _():
        sums_ref[0:1, :] += jnp.sum(back * unit, axis=0, keepdims=True)
        sums_ref[1:2, :] += jnp.sum(back, axis=0, keepdims=True)


def middle(flags, fields, mixed, vectors, bundle):
    whole, width = fields[0].shape
    columns = mixed.shape[1]
    low = jnp.bfloat16
    in_order = lambda i, *scalars: (i, 0)
    return streamed(
        middle_kernel,
        whole // ROWS,
        [flags],
        [by_rows(field, ROWS) for field in (*fields, mixed)]
        + [vectors, (bundle, (columns, width), lambda i, *scalars: (0, 0))],
        [
            ((whole, width), low, (ROWS, width), in_order),
            ((whole, columns), low, (ROWS, columns), in_order),
            ((width, columns), low),
            ((8, width), jnp.float32),
        ],
        [((width, columns), jnp.float32)],
        8,
        40 << 20,
    )


def weigh_kernel(flags, turned_ref, out_grad_ref, query_ref, key_ref, value_ref, *out_refs):
    rows = turned_ref[...]
    fields = [dot(rows, ref[...]).astype(jnp.bfloat16) for ref in (query_ref, key_ref, value_ref)]
    for piece, field in enumerate([*fields, out_grad_ref[...]]):
        slot = 2 * (flags[2] ^ (piece // 2)) + (flags[3] ^ (piece % 2))
        for j, out_ref in enumerate(out_refs):

            @pl.when(slot == j)
            def _():
                out_ref[...] = field


def weigh(flags, turned, grad, out_grad):
    width, columns = turned.shape[0], grad.shape[2]
    piece = ((width, columns), jnp.bfloat16, (ROWS, columns), lambda i, flags: (i, 0))
    fields = [by_rows(turned, ROWS), by_rows(out_grad, ROWS)]
    for c in range(3):
        fields.append((grad, (None, *grad.shape[1:]), lambda i, flags, c=c: (c, 0, 0)))
    return streamed(weigh_kernel, width // ROWS, [flags], fields, [piece] * 4, [], 4)


def unproject_kernel(flags, grad_ref, rows_ref, w_own, w_near, w_far, keep_ref, first, second, sums_ref, weight):
    @pl.when(pl.program_id(0) == 0)
    def _():
        join_rows(flags, w_own, w_near, w_far, weight)

    total = dot(grad_ref[0], weight[0], NT)
    for c in range(1, grad_ref.shape[0]):
        total = total + dot(grad_ref[c], weight[c], NT)
    unit, unused = norm_parts(rows_ref[...].astype(jnp.float32))

    @pl.when(pl.program_id(0) == 0)
    def _():
        sums_ref[...] = jnp.zeros_like(sums_ref)

    sums_ref[0:1, :] += jnp.sum(total * unit, axis=0, keepdims=True)
    sums_ref[1:2, :] += jnp.sum(total, axis=0, keepdims=True)
    send_or_keep(total, total, first, second, keep_ref)


def unproject(flags, grad, weights, rows):
    whole, width = rows.shape
    count, unused, columns = grad.shape
    grads = (grad, (count, whole // 4, columns), lambda i, flags: (0, theirs_first(i, flags), 0))
    fields = [grads, by_rows(rows, whole // 4, theirs_first), *weights]
    scratch = [((count, width, columns), jnp.bfloat16)]
    return streamed(unproject_kernel, 4, [flags], fields, sent_and_kept(whole, width), scratch, 5, SNUG + (4 << 20))


def last_kernel(
    flags, rows_ref, resid_ref, keep_ref, block_keep, got_first, got_second, block_first, block_second, vectors, out_ref
):
    first = pl.program_id(0) == 0
    unit, scale = norm_parts(rows_ref[...].astype(jnp.float32))
    got = jnp.where(first, got_first[...], got_second[...]).astype(jnp.float32)
    inner = (keep_ref[...].astype(jnp.float32) + got) * vectors[0:1, :]
    mean = jnp.mean(inner, axis=-1, keepdims=True)
    slant = jnp.mean(inner * unit, axis=-1, keepdims=True)
    grad = resid_ref[...].astype(jnp.float32) + scale * (inner - mean - unit * slant)
    out_ref[0] = grad.astype(jnp.bfloat16)
    got = jnp.where(first, block_first[...], block_second[...]).astype(jnp.float32)
    out_ref[1] = (block_keep[...].astype(jnp.float32) + got).astype(jnp.bfloat16)


def last(flags, rows, resid, keep, block_keep, got, vectors):
    half, width = keep.shape
    size = half // 2

    def mine(i, flags):
        return flags[1] * 2 + i

    out = ((2, half, width), jnp.bfloat16, (2, size, width), lambda i, flags: (0, i, 0))
    fields = [by_rows(rows, size, mine), by_rows(resid, size, mine), by_rows(keep, size), by_rows(block_keep, size)]
    return streamed(last_kernel, 2, [flags], fields + [*got, vectors], [out], [], 3)[0]


def past_kernel(dwa_ref, hist_ref, cot_ref, grad_ref, part_ref, sums_ref):
    @pl.when(pl.program_id(0) == 0)
    def _():
        sums_ref[...] = jnp.zeros_like(sums_ref)

    grad = cot_ref[...].astype(jnp.float32)
    total = jnp.zeros_like(grad)
    for j in range(hist_ref.shape[0]):
        field = hist_ref[j].astype(jnp.float32)
        total += dwa_ref[j] * field
        grad_ref[j] = (dwa_ref[j] * grad).astype(jnp.bfloat16)
        sums_ref[j : j + 1, :] += jnp.sum(field * grad, axis=0, keepdims=True)
    part_ref[...] = total


def past(dwa, history, cot):
    count, rows, width = history.shape
    layers = pl.BlockSpec((count, ROWS, width), lambda i: (0, i, 0))
    tokens = pl.BlockSpec((ROWS, width), lambda i: (i, 0))
    return pl.pallas_call(
        past_kernel,
        grid=(rows // ROWS,),
        in_specs=[pl.BlockSpec(memory_space=pltpu.SMEM), layers, tokens],
        out_specs=[layers, tokens, whole_spec((8, width))],
        out_shape=[
            jax.ShapeDtypeStruct(history.shape, jnp.bfloat16),
            jax.ShapeDtypeStruct((rows, width), jnp.float32),
            jax.ShapeDtypeStruct((8, width), jnp.float32),
        ],
        compiler_params=pltpu.CompilerParams(vmem_limit_bytes=ROOM),
        cost_estimate=lasting(3),
    )(dwa, history, cot)


def present_kernel(flags, weight_ref, part_ref, own_ref, got_ref, out_ref, grad_ref):
    here = jnp.where(flags[0] == 1, own_ref[1], got_ref[1]).astype(jnp.float32)
    out_ref[...] = (part_ref[...] + weight_ref[weight_ref.shape[0] - 1] * here).astype(jnp.bfloat16)
    grad_ref[...] = jnp.where(flags[0] == 1, own_ref[0], got_ref[0])


def present(flags, weight, part, own, got):
    rows, width = part.shape
    both = (2, ROWS, width), lambda i, *scalars: (0, i, 0)
    out = ((rows, width), jnp.bfloat16, (ROWS, width), lambda i, *scalars: (i, 0))
    fields = [by_rows(part, ROWS), (own, *both), (got, *both)]
    return streamed(present_kernel, rows // ROWS, [flags, weight], fields, [out] * 2, [], 2, SNUG)


def blocks_kernel(flags, early_own, early_got, late_ref, *refs):
    parts, out_ref = refs[:-1], refs[-1]
    part = late_ref.shape[1]
    total = sum(ref[...].astype(jnp.float32) for ref in parts)
    out_ref[:, :part] = total.astype(jnp.bfloat16)
    out_ref[:, part : 2 * part] = jnp.where(flags[0] == 1, early_own[...], early_got[...])
    out_ref[:, 2 * part :] = late_ref[...]


def blocks_of(flags, early_own, early_got, late, parts):
    rows, part = late.shape
    out = ((rows, 3 * part), jnp.bfloat16)
    return streamed(blocks_kernel, 1, [flags], [early_own, early_got, late, *parts], [out], [], 1, SNUG)[0]


def place_kernel(flags, here_ref, there_ref, qkv_ref, out_ref, up_ref, down_ref):
    near, far = flags[1], flags[2]
    part = out_ref.shape[1]
    for k in range(2):
        for c in range(2):
            field = jnp.where(near == c, here_ref[k ^ far], there_ref[k ^ far]).astype(jnp.float32)
            if 2 * k + c < 3:
                qkv_ref[2 * k + c] = field[:, :part]
            else:
                out_ref[...] = field[:, :part]
            for half in range(2):
                at = (2 * half + k) * part
                (up_ref, down_ref)[c][:, at : at + part] = field[:, (1 + half) * part : (2 + half) * part]


def place(flags, here, there):
    rows, part = here.shape[1], here.shape[2] // 3
    outs = [((3, rows, part), jnp.float32), ((rows, part), jnp.float32)]
    outs += [((rows, 4 * part), jnp.float32)] * 2
    return streamed(place_kernel, 1, [flags], [here, there], outs, [], 3, SNUG)


AXES = ("tp", "dp", "far", "near")


def moves(chosen, move):
    sizes = [lax.axis_size(name) for name in AXES]
    places = [place for place in itertools.product(*map(range, sizes)) if chosen(*place)]
    index = lambda place: functools.reduce(lambda at, step: at * step[0] + step[1], zip(sizes, place), 0)
    return [(index(place), index(move(*place))) for place in places]


def away(t, d, k, c):
    return t != c


def anyone(t, d, k, c):
    return True


def swap_diagonal(field):
    return lax.ppermute(field, AXES, moves(away, lambda t, d, k, c: (c, d, k, t)))


def send_to_owner(field, other_far, other_tp):
    return lax.ppermute(
        field,
        AXES,
        moves(
            away if not other_far and not other_tp else anyone,
            lambda t, d, k, c: (c, d, k ^ other_far, t ^ other_tp),
        ),
    )


def swap_far_away(field):
    return lax.ppermute(field, AXES, moves(away, lambda t, d, k, c: (t, d, 1 - k, c)))


def swap_far(field):
    return lax.ppermute(field, "far", [(0, 1), (1, 0)])


def swap_near(field):
    return lax.ppermute(field, "near", [(0, 1), (1, 0)])


def after(field, *others):
    return lax.optimization_barrier((field, *others))[0]


def ordered(own, other, first, axis=0):
    return jnp.where(
        first, jnp.concatenate([own, other], axis=axis), jnp.concatenate([other, own], axis=axis)
    )


def part_of(field, index, axis):
    size = field.shape[axis] // 2
    return lax.dynamic_slice_in_dim(field, index * size, size, axis)


def add(*fields):
    return sum(field.astype(jnp.float32) for field in fields).astype(jnp.bfloat16)


def scatter_plane(pieces):
    return lax.psum_scatter(pieces, ("tp", "far"), scatter_dimension=0, tiled=True)[0]


def scatter_rows(piece):
    return lax.psum_scatter(piece, "dp", scatter_dimension=0, tiled=True)


def move_rows(block):
    dps = lax.axis_size("dp")
    if dps > 8:
        return [scatter_rows(block)]
    block = block.reshape(dps, block.shape[0] // dps, block.shape[1])
    place = lax.axis_index("dp")
    moved = [lax.dynamic_index_in_dim(block, place, 0, keepdims=False)]
    for step in range(1, dps):
        sent = lax.dynamic_index_in_dim(block, lax.rem(place + step, dps), 0, keepdims=False)
        moved.append(lax.ppermute(sent, "dp", [(d, (d + step) % dps) for d in range(dps)]))
    return moved


def sum_over(field, name):
    size = lax.axis_size(name)
    bit = 1
    while bit < size:
        field = field + lax.ppermute(field, name, [(d, d ^ bit) for d in range(size)])
        bit *= 2
    return field


def local(
    layer_input,
    history,
    cotangent,
    lengths,
    dwa_weights,
    gain_one,
    bias_one,
    w_qkv,
    w_out,
    gain_two,
    bias_two,
    w_up,
    w_down,
):
    rows = layer_input.shape[1]
    whole = rows * lax.axis_size("tp")
    hist_count = history.shape[0]
    part, far, near = lax.axis_index("tp"), lax.axis_index("far"), lax.axis_index("near")
    same = near == part
    flags = jnp.stack([same.astype(jnp.int32), near, far, part])

    input_got = swap_diagonal(layer_input[0])
    qkv_near = swap_diagonal(part_of(w_qkv, far, 1))
    qkv_far = swap_far_away(qkv_near)
    early_got = jnp.concatenate([part_of(w_up, 0, 1), part_of(w_down, 0, 0)], axis=0)
    late_got = jnp.concatenate([part_of(w_up, 1, 1), part_of(w_down, 1, 0)], axis=0)
    last_own = jnp.concatenate([w_out, cotangent[0]], axis=0)
    vectors = jnp.stack([gain_one, bias_one, gain_two, bias_two])

    own_lengths = jnp.where(same, lengths, swap_near(lengths))[0]
    seq_owner, token_place = positions(own_lengths, whole)
    lane = jnp.arange(LANES, dtype=jnp.int32)
    member = seq_owner[:, None] == lane[None, :]
    apart = jnp.where(member | (lane >= lengths.shape[1])[None, :], 0.0, NEG_FILL).astype(jnp.bfloat16)
    member = member.astype(jnp.bfloat16)
    half_dim = HEAD_DIM // 2
    frequency = jnp.exp((lane % half_dim).astype(jnp.float32) * (-math.log(10000.0) / half_dim))
    angles = token_place.astype(jnp.float32)[:, None] * frequency[None, :]
    cos_table = jnp.cos(angles)
    sin_table = jnp.sin(angles) * jnp.where(lane % HEAD_DIM < half_dim, -1.0, 1.0)[None, :]
    grad_history, past_sum, sums_past = past(dwa_weights, history[:, 0], cotangent[0])

    input_half = jnp.where(same, layer_input[0], input_got)
    layer_rows = ordered(input_half, swap_near(input_half), near == 0)
    layer_rows, vectors, past_sum, cos_table, sin_table, apart, member = lax.optimization_barrier(
        (layer_rows, vectors, past_sum, cos_table, sin_table, apart, member)
    )
    early_got = swap_diagonal(after(early_got, input_got))
    last_got = swap_diagonal(after(last_own, input_got))
    projected, norm_one_t = project(
        flags, layer_rows, vectors, cos_table, sin_table, w_qkv, qkv_near, qkv_far
    )
    mixed, logs = attend(apart, member, projected, LONGEST)
    late_got = swap_diagonal(after(late_got, mixed))
    last_got = jnp.where(same, last_own, after(last_got, mixed))
    weight_out = last_got[: w_out.shape[0]]
    attn = jnp.dot(mixed, weight_out, preferred_element_type=jnp.float32).astype(jnp.bfloat16)
    attn_got = swap_near(attn)
    cot_half = last_got[w_out.shape[0] :]
    scalars = [flags, dwa_weights]
    fields = [layer_rows, attn, attn_got, cot_half, swap_near(cot_half), vectors]
    *kept, resid, back, act_early, down_early, early_pieces = feed(True, scalars, fields, w_up, w_down, early_got)
    early_sum = scatter_plane(after(early_pieces, late_got))
    back, act_late, down_late, *late_owned = feed(
        False, [flags], [*kept, back], w_up, w_down, late_got
    )
    late_moved = [send_to_owner(late_owned[j], j // 2, j % 2) for j in range(4)]
    grad_down = kept[2]
    fields = [resid, grad_down, back, swap_near(back)]
    grad_attn, grad_mixed, grad_out, sums_two = middle(flags, fields, mixed, vectors, last_got)
    grad_qkv = attend_back(
        apart, member, cos_table, sin_table, projected, grad_mixed, mixed, logs, LONGEST
    )
    grad_qkv, *late_moved = lax.optimization_barrier((grad_qkv, *late_moved))
    owned = weigh(flags, norm_one_t, grad_qkv, grad_out)
    moved = [send_to_owner(owned[j], j // 2, j % 2) for j in range(4)]
    early_sum = scatter_rows(after(early_sum, grad_qkv))
    late_sum = scatter_rows(add(jnp.where(same, late_owned[0], after(late_moved[0], owned[0])), *late_moved[1:]))
    keep, *send, sums_one = unproject(
        flags, after(grad_qkv, owned[0]), (w_qkv, qkv_near, qkv_far), layer_rows
    )
    block_keep, *block_send, sums_now = lower(
        flags, act_early, act_late, down_early, down_late, resid, after(grad_down, keep)
    )
    sent = [*send, *block_send]
    keep, block_keep, *arrived = lax.optimization_barrier((keep, block_keep, *sent, *moved))
    sent, moved = arrived[:4], arrived[4:]
    attn_one = add(jnp.where(same, owned[0], moved[0]), *moved[1:])
    attn_moved = move_rows(attn_one)
    got = [swap_near(field) for field in sent]
    ours = last(flags, layer_rows, grad_attn, after(keep, attn_one), block_keep, got, vectors)
    early_sum = after(early_sum, attn_one)
    early_got = swap_diagonal(early_sum)
    small = jnp.concatenate([sums_one[:2], sums_two[:2], sums_now[:1], sums_past[:hist_count]], axis=0)
    small = after(small, ours)
    for name in ("tp", "far"):
        small = sum_over(small, name)
    theirs = swap_diagonal(ours)
    small, late_sum, early_sum, early_got, *attn_moved = lax.optimization_barrier(
        (small, late_sum, early_sum, early_got, *attn_moved)
    )
    for name in ("near", "dp"):
        small = sum_over(small, name)
    blocks = blocks_of(flags, early_sum, early_got, late_sum, attn_moved)
    here = after(jnp.stack([blocks, swap_far(blocks)]), small)
    grad_w_qkv, grad_w_out, grad_w_up, grad_w_down = place(flags, here, swap_near(here))
    output, grad_input = present(flags, dwa_weights, past_sum, ours, after(theirs, grad_w_up))

    return (
        output[None],
        grad_input[None],
        grad_history[:, None],
        jnp.sum(jnp.concatenate([small[5:], small[4:5] / dwa_weights[hist_count]], axis=0), axis=1),
        small[0],
        small[1],
        grad_w_qkv,
        grad_w_out.T,
        small[2],
        small[3],
        grad_w_up,
        grad_w_down.T,
    )


def positions(seq_lengths, token_count):
    seq_ends = jnp.cumsum(seq_lengths)
    seq_starts = seq_ends - seq_lengths
    token_index = jnp.arange(token_count, dtype=jnp.int32)
    seq_owner = jnp.sum((token_index[:, None] >= seq_ends[None, :]).astype(jnp.int32), axis=1)
    picked = (
        seq_owner[:, None] == jnp.arange(seq_lengths.shape[0], dtype=jnp.int32)[None, :]
    ).astype(jnp.int32)
    seq_begin = jnp.sum(picked * seq_starts[None, :], axis=1)
    return (seq_owner, token_index - seq_begin)


def solution(mesh):
    tps, dps, reps = (mesh.shape[name] for name in ("tp", "dp", "rep"))
    split = Mesh(mesh.devices.reshape(tps, dps, reps // 2, 2), AXES)
    in_specs = (
        P(("dp", "far", "near"), "tp", None),
        P(None, ("dp", "far", "near"), "tp", None),
        P(("dp", "far", "near"), "tp", None),
        P(("dp", "far", "near"), None),
        P(),
        P(),
        P(),
        P(None, None, "tp"),
        P("tp", None),
        P(),
        P(),
        P(None, "tp"),
        P("tp", None),
    )
    out_specs = (
        P(("dp", "far", "near"), "tp", None),
        P(("dp", "far", "near"), "tp", None),
        P(None, ("dp", "far", "near"), "tp", None),
        P(),
        P(),
        P(),
        P(None, "dp", "tp"),
        P("tp", "dp"),
        P(),
        P(),
        P("dp", "tp"),
        P("tp", "dp"),
    )
    return jax.shard_map(local, mesh=split, in_specs=in_specs, out_specs=out_specs, check_vma=False)
```
